32 devices in a mesh: dp: 8 (over z, y), tile: 4 (over x, core).
Axes of the slice: x: 2, y: 2, z: 4, core: 2. Of those that a mesh axis runs over, the one named last changes fastest.
Arguments:
- tokens: bfloat16 [8, 4096, 768], P('dp', 'tile'), may hold values from -6 to 6
- cotangent: bfloat16 [8, 4096, 768], P('dp', 'tile'), may hold values from -6 to 6
- counts: int32 [8, 4], P('dp', 'tile'), may hold values from 1 to 1024, as said below
- master: float32 [192, 192, 192], P('dp')
- slot_block: int32 [192], replicated, may hold values from 0 to 191, as said below
- groups: int32 [192], P('dp'), may hold values from 0 to 15
- first_moment: float32 [192, 192, 192], P('dp')
- second_moment: float32 [192, 192, 192], P('dp'), as said below
- left_basis: float32 [192, 192, 192], P('dp')
- right_basis: float32 [192, 192, 192], P('dp')
- vec_params: float32 [12, 768], replicated
- vec_first: float32 [12, 768], replicated
- vec_second: float32 [12, 768], replicated, as said below
Outputs:
- output: bfloat16 [8, 4096, 768], P('dp', 'tile')
- input_grad: float32 [8, 4096, 768], P('dp', 'tile')
- weight_grads: float32 [192, 192, 192], P('dp')
- first_out: float32 [192, 192, 192], P('dp')
- second_out: float32 [192, 192, 192], P('dp')
- master_out: float32 [192, 192, 192], P('dp')
- master_copy: bfloat16 [192, 192, 192], P('dp')
- vector_grads: float32 [12, 768], replicated
- vec_first_out: float32 [12, 768], replicated
- vec_second_out: float32 [12, 768], replicated
- vec_out: float32 [12, 768], replicated
The draws below stay inside these ranges and needn't reach their ends.
Inputs may be any that keep to these rules, and one draw needn't show every extreme that they name: `counts`: every tile of every image keeps at least one patch; some image keeps all 1024 slots of some tile. `slot_block`: a permutation of the blocks. `second_moment`: positive. `vec_second`: positive.
All inputs are finite; a program needn't handle non-finite values.
Results may differ from the reference program's by a relative error of at most 0.011.
The reference program's roundings to bfloat16 on the way count: a program that leaves them out, or rounds other values in their place, can miss the bound.
Values may be sent and summed in bfloat16 or wider, within the bound.
A program may use at most 320 MiB of HBM per device.

```python
import math
import jax
import jax.numpy as jnp
from jax import lax

D = 768
H = 12
FF = 3072
IMG_DEV = 1
SLOTS = 1024
BLK = 192
NGRP = 16
STEP = 10
IMAGES = 8
LENGTH = 4096
TOKENS = 32768
NBLK = 192
VROWS = 12
N_DP = 8
N_TILE = 4


def slot_order(key):
    return jax.random.permutation(jax.random.fold_in(key, 17), NBLK).astype(jnp.int32)


def kind_edges():
    per_row = D // BLK
    edge_qkv = per_row * (3 * D // BLK)
    edge_out = edge_qkv + per_row * per_row
    edge_up = edge_out + per_row * (FF // BLK)
    return (edge_qkv, edge_out, edge_up)


def grad_scale(slot_perm):
    edge_qkv, edge_out, edge_up = kind_edges()
    factor = jnp.where(slot_perm < edge_out, 0.3, 0.5)
    return factor * math.sqrt(0.5 * TOKENS)


def draw_slot_block(key, part):
    return slot_order(key)


def draw_counts(key, part):
    image_idx = lax.broadcasted_iota(jnp.int32, (IMAGES, N_TILE), 0)
    tile_idx = lax.broadcasted_iota(jnp.int32, (IMAGES, N_TILE), 1)
    top_count = SLOTS // 3 + (SLOTS - SLOTS // 3) * image_idx // max(IMAGES - 1, 1)
    low_bound = jnp.maximum(2 * top_count // 3, 1)
    count_span = top_count - low_bound + 1
    raw_ints = jax.random.randint(jax.random.fold_in(key, 53), (IMAGES, N_TILE), 0, 1 << 20)
    drawn = low_bound + raw_ints % count_span
    corner = jnp.logical_and(image_idx == IMAGES - 1, tile_idx == 0)
    return jnp.where(corner, SLOTS, drawn).astype(jnp.int32)


def draw_master(key, part):
    slot_perm = slot_order(key)
    edge_qkv, edge_out, edge_up = kind_edges()
    base_scale = jnp.where(slot_perm < edge_qkv, 1.0 / math.sqrt(D), jnp.where(slot_perm < edge_out, 4.0 / math.sqrt(D), jnp.where(slot_perm < edge_up, 1.0 / math.sqrt(D), 1.5 / math.sqrt(FF))))
    slot_place = jnp.arange(NBLK, dtype=jnp.float32) / max(NBLK - 1, 1)
    rise_factor = 0.6 + 1.2 * slot_place
    noise_draw = jnp.clip(jax.random.normal(jax.random.fold_in(key, 23), (NBLK, BLK, BLK), jnp.float32), -4.0, 4.0)
    return noise_draw * (base_scale * rise_factor)[:, None, None]


def draw_first_moment(key, part):
    scale_rows = grad_scale(slot_order(key))
    noise_draw = jnp.clip(jax.random.normal(jax.random.fold_in(key, 29), (NBLK, BLK, BLK), jnp.float32), -3.0, 3.0)
    return noise_draw * scale_rows[:, None, None]


def draw_second_moment(key, part):
    scale_rows = grad_scale(slot_order(key))
    block_factor = jnp.exp(jax.random.uniform(jax.random.fold_in(key, 31), (NBLK,), jnp.float32, 0.0, math.log(4.0)))
    entry_factor = jnp.exp(jax.random.uniform(jax.random.fold_in(key, 37), (NBLK, BLK, BLK), jnp.float32, math.log(0.5), math.log(2.0)))
    return entry_factor * (scale_rows * scale_rows * block_factor)[:, None, None]


def basis_draw(key, salt):
    sub_key = jax.random.fold_in(key, salt)
    noise_draw = jnp.clip(jax.random.normal(sub_key, (NBLK, BLK, BLK), jnp.float32), -4.0, 4.0) * 0.35
    return jnp.eye(BLK, dtype=jnp.float32)[None] + noise_draw / math.sqrt(BLK)


def draw_left_basis(key, part):
    return basis_draw(key, 41)


def draw_right_basis(key, part):
    return basis_draw(key, 43)


def draw_vec_params(key, part):
    sub_key = jax.random.fold_in(key, 59)
    noise_draw = jnp.clip(jax.random.normal(sub_key, (VROWS, D), jnp.float32), -4.0, 4.0)
    row_idx = lax.broadcasted_iota(jnp.int32, (VROWS, D), 0)
    is_gain = jnp.logical_or(row_idx == 0, row_idx == 2)
    return jnp.where(is_gain, 1.0 + 0.15 * noise_draw, 0.3 * noise_draw)


def vector_scale():
    return 0.7 * math.sqrt(0.5 * TOKENS)


def draw_vec_first(key, part):
    noise_draw = jnp.clip(jax.random.normal(jax.random.fold_in(key, 61), (VROWS, D), jnp.float32), -3.0, 3.0)
    return noise_draw * vector_scale()


def draw_vec_second(key, part):
    entry_factor = jnp.exp(jax.random.uniform(jax.random.fold_in(key, 67), (VROWS, D), jnp.float32, math.log(0.5), math.log(8.0)))
    return entry_factor * (vector_scale() * vector_scale())


def place_ends(result, own_key, smallest, top_value):
    extent = result.shape
    index_at = [jax.random.randint(jax.random.fold_in(own_key, axis), (), 0, extent[axis]) for axis in range(len(extent))]
    result = result.at[tuple(index_at)].set(smallest)
    longest = extent.index(max(extent))
    index_at[longest] = (index_at[longest] + 1) % extent[longest]
    return result.at[tuple(index_at)].set(top_value)


def levels(own_key, shape, split, low, top_value):
    loudness, own = 1.0, jax.random.fold_in(own_key, 6)
    for dim, blocks in split:
        heights = jnp.exp(jax.random.uniform(jax.random.fold_in(own, dim), (blocks,), jnp.float32, low / len(split), top_value / len(split)))
        loudness = loudness * jnp.repeat(heights, shape[dim] // blocks).reshape([-1 if axis == dim else 1 for axis in range(len(shape))])
    return loudness


def gaussian(stream_key, dims, scale, reach, split=(), kind=jnp.bfloat16):
    array = jax.random.normal(stream_key, dims, jnp.float32) * scale
    if len(split) > 0:
        array = levels(stream_key, dims, split, -0.22, 0.18) * array
    return jnp.clip(array, min=-reach, max=reach).astype(kind)


def setup_inputs(seed: int = 0) -> dict:
    streams_of = jax.random.split(jax.random.key(seed), 14)
    return {
        "tokens": gaussian(streams_of[0], (IMAGES, LENGTH, D), 1.0, 6.0, ((0, 8), (1, 4))),
        "cotangent": gaussian(streams_of[1], (IMAGES, LENGTH, D), 1.0, 6.0, ((0, 8), (1, 4))),
        "counts": draw_counts(jax.random.fold_in(streams_of[13], 71), 0),
        "master": draw_master(jax.random.fold_in(streams_of[13], 71), 0),
        "slot_block": draw_slot_block(jax.random.fold_in(streams_of[13], 71), 0),
        "groups": place_ends(jax.random.randint(streams_of[5], (NBLK,), 0, NGRP), jax.random.fold_in(streams_of[5], 1), 0, NGRP - 1).astype(jnp.int32),
        "first_moment": draw_first_moment(jax.random.fold_in(streams_of[13], 71), 0),
        "second_moment": draw_second_moment(jax.random.fold_in(streams_of[13], 71), 0),
        "left_basis": draw_left_basis(jax.random.fold_in(streams_of[13], 71), 0),
        "right_basis": draw_right_basis(jax.random.fold_in(streams_of[13], 71), 0),
        "vec_params": draw_vec_params(jax.random.fold_in(streams_of[13], 71), 0),
        "vec_first": draw_vec_first(jax.random.fold_in(streams_of[13], 71), 0),
        "vec_second": draw_vec_second(jax.random.fold_in(streams_of[13], 71), 0),
    }


EPS_NORM = 1e-06
BETA_ONE = 0.5
BETA_TWO = 0.5
ADAM_EPS = 1e-08
RATE_BLOCK = 0.3
RATE_VECTOR = 0.2
NEG_FILL = -1000000000.0
HIGHEST_PREC = lax.Precision.HIGHEST

@jax.custom_vjp
def low(v):
    return lax.optimization_barrier(v.astype(jnp.bfloat16)).astype(jnp.float32)

@jax.custom_vjp
def low_back(v):
    return v

def low_keep(v):
    return (low(v), None)

def low_pass(kept, grad):
    return (grad,)

def back_keep(v):
    return (v, None)

def back_low(kept, grad):
    return (low(grad),)
low.defvjp(low_keep, low_pass)
low_back.defvjp(back_keep, back_low)

def layer_norm(row_data, gain_vec, shift_vec):
    row_mean = lax.optimization_barrier(jnp.mean(row_data, axis=-1, keepdims=True))
    centred = row_data - row_mean
    inv_std = lax.rsqrt(lax.optimization_barrier(jnp.mean(centred * centred, axis=-1, keepdims=True)) + EPS_NORM)
    return centred * inv_std * gain_vec + shift_vec

def from_blocks(blocks, row_count, col_count):
    return blocks.reshape(row_count // BLK, col_count // BLK, BLK, BLK).transpose(0, 2, 1, 3).reshape(row_count, col_count)

def to_blocks(matrix):
    row_count, col_count = matrix.shape
    return matrix.reshape(row_count // BLK, BLK, col_count // BLK, BLK).transpose(0, 2, 1, 3).reshape(-1, BLK, BLK)

def attention(queries, key_rows, value_rows, valid_keys):
    image_count, query_len, model_width = queries.shape
    head_size = model_width // H

    def head_major(array_in):
        return array_in.reshape(image_count, array_in.shape[1], H, head_size).transpose(2, 0, 1, 3)

    @jax.checkpoint
    def one_head(parts):
        query_head, key_head, value_head = parts
        raw_scores = jnp.einsum('nqd,nkd->nqk', query_head, key_head, precision=HIGHEST_PREC)
        scores = low_back(raw_scores * (1.0 / math.sqrt(head_size)))
        scores = jnp.where(valid_keys[:, None, :], scores, NEG_FILL)
        row_top = lax.optimization_barrier(jnp.max(scores, axis=-1, keepdims=True))
        shifted_exp = jnp.exp(scores - row_top)
        prob_rows = low(shifted_exp / lax.optimization_barrier(jnp.sum(shifted_exp, axis=-1, keepdims=True)))
        return jnp.einsum('nqk,nkd->nqd', prob_rows, value_head, precision=HIGHEST_PREC)
    attended = lax.map(one_head, (head_major(queries), head_major(key_rows), head_major(value_rows)))
    return attended.transpose(1, 2, 0, 3).reshape(image_count, query_len, model_width)

def forward(token_rows, valid_keys, weight_set):
    w_qkv, w_out, w_up, w_down, vec_params = weight_set
    image_count, seq_len, model_width = token_rows.shape
    flat_rows = token_rows.reshape(-1, model_width)
    zero_row = jnp.zeros((model_width,), jnp.float32)
    bias_qkv = jnp.concatenate([vec_params[4], zero_row, vec_params[5]])
    act_one = low(layer_norm(flat_rows, vec_params[0], vec_params[1]))
    qkv_rows = low(low_back(jnp.dot(act_one, w_qkv, precision=HIGHEST_PREC) + bias_qkv))
    qkv_rows = qkv_rows.reshape(image_count, seq_len, 3 * model_width)
    attn_out = attention(qkv_rows[:, :, :model_width], qkv_rows[:, :, model_width:2 * model_width], qkv_rows[:, :, 2 * model_width:], valid_keys)
    attn_low = low(low_back(attn_out)).reshape(-1, model_width)
    residual = flat_rows + low_back(jnp.dot(attn_low, w_out, precision=HIGHEST_PREC) + vec_params[6])
    act_two = low(layer_norm(residual, vec_params[2], vec_params[3]))
    pre_act = low_back(jnp.dot(act_two, w_up, precision=HIGHEST_PREC) + vec_params[8:].reshape(-1))
    hidden = low(jax.nn.gelu(pre_act, approximate=False))
    branch = low_back(jnp.dot(hidden, w_down, precision=HIGHEST_PREC) + vec_params[7])
    live_rows = valid_keys.reshape(-1, 1).astype(jnp.float32)
    return (live_rows * (residual + branch)).reshape(image_count, seq_len, model_width)

def reference(tokens, cotangent, counts, master, slot_block, groups, first_moment, second_moment, left_basis, right_basis, vec_params, vec_first, vec_second):
    block_count = master.shape[0]
    inverse = jnp.zeros((block_count,), jnp.int32).at[slot_block].set(jnp.arange(block_count, dtype=jnp.int32))
    canonical = low(master)[inverse]
    per_row = D // BLK
    edge_qkv = per_row * (3 * D // BLK)
    edge_out = edge_qkv + per_row * per_row
    edge_up = edge_out + per_row * (FF // BLK)
    weight_set = (from_blocks(canonical[:edge_qkv], D, 3 * D), from_blocks(canonical[edge_qkv:edge_out], D, D), from_blocks(canonical[edge_out:edge_up], D, FF), from_blocks(canonical[edge_up:], FF, D), vec_params)
    token_groups = tokens.astype(jnp.float32).reshape(N_DP, IMG_DEV, LENGTH, D)
    cotan_groups = cotangent.astype(jnp.float32).reshape(N_DP, IMG_DEV, LENGTH, D)
    count_groups = counts.reshape(N_DP, IMG_DEV, N_TILE)
    slot_index = jnp.arange(LENGTH, dtype=jnp.int32) % SLOTS

    def one_group(grad_total, group_item):
        token_rows, cotan_rows, count_rows = group_item
        valid_keys = slot_index[None, :] < jnp.repeat(count_rows, SLOTS, axis=1)

        def forward_fn(rows_in, weights_in):
            return forward(rows_in, valid_keys, weights_in)
        layer_out, pullback = jax.vjp(forward_fn, token_rows, weight_set)
        grad_rows, grad_weights = pullback(cotan_rows)
        return (jax.tree.map(jnp.add, grad_total, grad_weights), (layer_out.astype(jnp.bfloat16), grad_rows))
    zero_set = jax.tree.map(jnp.zeros_like, weight_set)
    grad_set, (group_outs, group_grads) = lax.scan(one_group, zero_set, (token_groups, cotan_groups, count_groups))
    output = group_outs.reshape(IMAGES, LENGTH, D)
    input_grad = group_grads.reshape(IMAGES, LENGTH, D)
    grad_qkv, grad_out, grad_up, grad_down, vector_grads = grad_set
    canonical_grads = jnp.concatenate([to_blocks(grad_qkv), to_blocks(grad_out), to_blocks(grad_up), to_blocks(grad_down)], axis=0)
    weight_grads = canonical_grads[slot_block]
    rotated = jnp.einsum('bji,bjk->bik', left_basis, weight_grads, precision=HIGHEST_PREC)
    rotated = jnp.einsum('bik,bkl->bil', rotated, right_basis, precision=HIGHEST_PREC)
    first_out = BETA_ONE * first_moment + (1.0 - BETA_ONE) * rotated
    second_out = BETA_TWO * second_moment + (1.0 - BETA_TWO) * rotated * rotated
    update_rot = first_out / (1.0 - BETA_ONE ** STEP) / (jnp.sqrt(second_out / (1.0 - BETA_TWO ** STEP)) + ADAM_EPS)
    update = jnp.einsum('bij,bjk->bik', left_basis, update_rot, precision=HIGHEST_PREC)
    update = jnp.einsum('bik,blk->bil', update, right_basis, precision=HIGHEST_PREC)
    group_hot = (groups[:, None] == jnp.arange(NGRP, dtype=jnp.int32)[None, :]).astype(jnp.float32)
    weight_sq = lax.optimization_barrier(jnp.sum(master * master, axis=(1, 2)))
    update_sq = lax.optimization_barrier(jnp.sum(update * update, axis=(1, 2)))
    group_weight = lax.optimization_barrier(jnp.sum(group_hot * weight_sq[:, None], axis=0))
    group_update = lax.optimization_barrier(jnp.sum(group_hot * update_sq[:, None], axis=0))
    own_weight = lax.optimization_barrier(jnp.sum(group_hot * group_weight[None, :], axis=1))
    own_update = lax.optimization_barrier(jnp.sum(group_hot * group_update[None, :], axis=1))
    block_rate = RATE_BLOCK * jnp.sqrt(own_weight) / (jnp.sqrt(own_update) + 1e-06)
    master_out = master - block_rate[:, None, None] * update
    master_copy = master_out.astype(jnp.bfloat16)
    vec_first_out = BETA_ONE * vec_first + (1.0 - BETA_ONE) * vector_grads
    vec_second_out = BETA_TWO * vec_second + (1.0 - BETA_TWO) * vector_grads * vector_grads
    vec_update = vec_first_out / (1.0 - BETA_ONE ** STEP) / (jnp.sqrt(vec_second_out / (1.0 - BETA_TWO ** STEP)) + ADAM_EPS)
    vec_out = vec_params - RATE_VECTOR * vec_update
    return (output, input_grad, weight_grads, first_out, second_out, master_out, master_copy, vector_grads, vec_first_out, vec_second_out, vec_out)
```

```python
import functools
import math

import jax
import jax.numpy as jnp
from jax import lax
from jax.experimental import pallas as pl
from jax.experimental.pallas import tpu as pltpu
from jax.sharding import PartitionSpec as P

f32 = jnp.float32
bf = jnp.bfloat16
MESH = pl.DeviceIdType.MESH

def where_am_i():
    dp=lax.axis_index("dp"); t=lax.axis_index("tile")
    return dp//2, dp%2, t//2, t%2

def dev(z,y,x,c):
    return (z*2+y, x*2+c)

def rcopy(src,dst,ss,rs,to):
    return pltpu.make_async_remote_copy(src_ref=src,dst_ref=dst,send_sem=ss,recv_sem=rs,device_id=to,device_id_type=MESH)

def gather_kernel(own_w,own_tok,own_cnt,all_w,all_tok,all_cnt,
                  zs,zr,ys,yr,xs,xr,cs,cr,fs,fr,ts,tr,ns,nr,ls):
    z,y,x,c=where_am_i()
    per=own_w.shape[0]
    part=per//12
    def a_of(shard,xx,cc): return all_w.at[pl.ds(shard*per+(xx*2+cc)*part,part)]
    def b_of(shard,cc): return all_w.at[pl.ds(shard*per+4*part+cc*4*part,4*part)]
    own_a=own_w.at[pl.ds((x*2+c)*part,part)]
    own_b=own_w.at[pl.ds(4*part+c*4*part,4*part)]
    me=z*2+y
    core=dev(z,y,x,1-c); across=dev(z,y,1-x,c); beside=dev(z,1-y,x,c)
    up=dev(jnp.minimum(z+1,3),y,x,c); down=dev(jnp.maximum(z-1,0),y,x,c)
    def src(shard,own):
        return (own_a,own_b) if own else (a_of(shard,x,c),b_of(shard,c))
    def z_copies(zz,own,go_up):
        shard=zz*2+y
        a,b=src(shard,own)
        d=(z-zz) if go_up else (zz-z)
        k=0 if go_up else 1
        to=up if go_up else down
        return (rcopy(a,a_of(shard,x,c),zs.at[k,d,0],zr.at[k,d,0],to),rcopy(b,b_of(shard,c),zs.at[k,d,1],zr.at[k,d,1],to))
    def z_arrivals(zz,k,dist):
        shard=zz*2+y
        a,b=a_of(shard,x,c),b_of(shard,c)
        return (rcopy(a,a,zs.at[k,dist-1,0],zr.at[k,dist-1,0],up),rcopy(b,b,zs.at[k,dist-1,1],zr.at[k,dist-1,1],up))
    def y_copies(zz,own):
        shard=zz*2+y
        a,b=src(shard,own)
        return (rcopy(a,a_of(shard,x,c),ys.at[zz,0],yr.at[zz,0],beside),rcopy(b,b_of(shard,c),ys.at[zz,1],yr.at[zz,1],beside))
    def y_arrivals(zz):
        shard=zz*2+(1-y)
        a,b=a_of(shard,x,c),b_of(shard,c)
        return (rcopy(a,a,ys.at[zz,0],yr.at[zz,0],beside),rcopy(b,b,ys.at[zz,1],yr.at[zz,1],beside))
    def x_copy(shard,own):
        return rcopy(src(shard,own)[0],a_of(shard,x,c),xs.at[shard],xr.at[shard],across)
    def x_arrival(shard):
        a=a_of(shard,1-x,c)
        return rcopy(a,a,xs.at[shard],xr.at[shard],across)
    def c_copies(shard,own):
        a,b=src(shard,own)
        return (rcopy(a,a_of(shard,x,c),cs.at[shard,0],cr.at[shard,0],core),rcopy(b,b_of(shard,c),cs.at[shard,1],cr.at[shard,1],core))
    def c_arrivals(shard):
        a,b=a_of(shard,x,1-c),b_of(shard,1-c)
        return (rcopy(a,a,cs.at[shard,0],cr.at[shard,0],core),rcopy(b,b,cs.at[shard,1],cr.at[shard,1],core))
    def f_copy(shard):
        a=a_of(shard,1-x,c)
        return rcopy(a,a,fs.at[shard],fr.at[shard],core)
    def f_arrival(shard):
        a=a_of(shard,1-x,1-c)
        return rcopy(a,a,fs.at[shard],fr.at[shard],core)
    def start(cps):
        for cp in (cps if isinstance(cps,tuple) else (cps,)): cp.start()
    def got(cps):
        for cp in (cps if isinstance(cps,tuple) else (cps,)): cp.wait_recv()
    def sent(cps):
        for cp in (cps if isinstance(cps,tuple) else (cps,)): cp.wait_send()
    tile=x*2+c
    tok_x=rcopy(own_tok,all_tok.at[tile],ts.at[0],tr.at[0],across)
    tok_c=rcopy(own_tok,all_tok.at[tile],ts.at[1],tr.at[1],core)
    far=all_tok.at[(1-x)*2+c]
    tok_f=rcopy(far,far,ts.at[2],tr.at[2],core)
    near=all_tok.at[x*2+1-c]
    diag=all_tok.at[(1-x)*2+1-c]
    cnts=[rcopy(own_cnt,all_cnt.at[tile],ns.at[i],nr.at[i],to) for i,to in enumerate((across,core,dev(z,y,1-x,1-c)))]
    cnt_in=[rcopy(r,r,ns.at[i],nr.at[i],core) for i,r in enumerate((all_cnt.at[(1-x)*2+c],all_cnt.at[x*2+1-c],all_cnt.at[(1-x)*2+1-c]))]
    local=(pltpu.make_async_copy(own_w,all_w.at[pl.ds(me*per,per)],ls.at[0]),
           pltpu.make_async_copy(own_tok,all_tok.at[tile],ls.at[1]),pltpu.make_async_copy(own_cnt,all_cnt.at[tile],ls.at[2]))
    @pl.when(z<3)
    def _(): start(z_copies(z,True,True))
    @pl.when(z>0)
    def _(): start(z_copies(z,True,False))
    start(y_copies(z,True)); start(tok_x); start(tok_c)
    for cp in cnts: cp.start()
    for cp in local: cp.start()
    def from_line(k,dist):
        zz=z-dist if k==0 else z+dist
        there=(zz>=0) if k==0 else (zz<=3)
        @pl.when(there)
        def _():
            got(z_arrivals(zz,k,dist))
            @pl.when((z<3) if k==0 else (z>0))
            def _(): start(z_copies(zz,False,k==0))
            start(y_copies(zz,False)); start(x_copy(zz*2+y,False)); start(c_copies(zz*2+y,False))
    def from_beside(zz):
        got(y_arrivals(zz))
        s=zz*2+1-y
        start(x_copy(s,False)); start(c_copies(s,False))
    def guarded(f,dist):
        @pl.when(z-dist>=0)
        def _(): f(z-dist)
        @pl.when(z+dist<=3)
        def _(): f(z+dist)
    def from_across(shard):
        got(x_arrival(shard)); start(f_copy(shard))
    from_line(0,1); from_line(1,1)
    from_beside(z)
    from_line(0,2); from_line(1,2)
    guarded(from_beside,1); guarded(lambda zz: from_across(zz*2+y),1); from_across(z*2+1-y)
    from_line(0,3); from_line(1,3)
    got(tok_x); tok_f.start()
    guarded(from_beside,2); guarded(lambda zz: from_across(zz*2+y),2); guarded(lambda zz: from_across(zz*2+1-y),1)
    guarded(from_beside,3); guarded(lambda zz: from_across(zz*2+y),3); guarded(lambda zz: from_across(zz*2+1-y),2)
    guarded(lambda zz: from_across(zz*2+1-y),3)
    def drain(s,_):
        @pl.when(s!=me)
        def _():
            got(c_arrivals(s)); got(f_arrival(s)); sent(c_copies(s,False)); sent(f_copy(s)); sent(x_copy(s,False))
        return 0
    lax.fori_loop(0,8,drain,0)
    def drain_y(zz,_):
        sent(y_copies(zz,False)); return 0
    lax.fori_loop(0,4,drain_y,0)
    for dist in range(4):
        @pl.when(jnp.logical_and(z<3,z-dist>=0))
        def _(): sent(z_copies(z-dist,False,True))
        @pl.when(jnp.logical_and(z>0,z+dist<=3))
        def _(): sent(z_copies(z+dist,False,False))
    rcopy(near,near,ts.at[1],tr.at[1],core).wait_recv()
    rcopy(diag,diag,ts.at[2],tr.at[2],core).wait_recv()
    tok_x.wait_send(); tok_c.wait_send(); tok_f.wait_send()
    for cp in cnts: cp.wait_send()
    for cp in cnt_in: cp.wait_recv()
    for cp in local: cp.wait()

def gather_all(own_w,own_tok,own_cnt):
    DS=pltpu.SemaphoreType.DMA
    hbm=pl.BlockSpec(memory_space=pl.ANY)
    return pl.pallas_call(gather_kernel,
        out_shape=[jax.ShapeDtypeStruct((8*own_w.shape[0],)+own_w.shape[1:],bf),jax.ShapeDtypeStruct((4,)+own_tok.shape,bf),jax.ShapeDtypeStruct((4,)+own_cnt.shape,own_cnt.dtype)],
        in_specs=[hbm]*3,out_specs=[hbm]*3,
        scratch_shapes=[DS((2,4,2)),DS((2,4,2)),DS((4,2)),DS((4,2)),DS((8,)),DS((8,)),DS((8,2)),DS((8,2)),DS((8,)),DS((8,)),DS((3,)),DS((3,)),DS((3,)),DS((3,)),DS((3,))],
        compiler_params=pltpu.CompilerParams(has_side_effects=True),name="gather_weights_tokens")(own_w,own_tok,own_cnt)

def exchange_kernel(a_ref,o_ref,ss,rs,ls):
    dp=lax.axis_index("dp"); t=lax.axis_index("tile")
    n=a_ref.shape[0]
    own=pltpu.make_async_copy(a_ref.at[t],o_ref.at[t],ls.at[0])
    cps=[]
    for k in range(n-1,0,-1):
        p=(t+k)%n
        cp=rcopy(a_ref.at[p],o_ref.at[t],ss.at[k],rs.at[k],(dp,p)); cp.start(); cps.append(cp)
    own.start()
    for k in range(1,n):
        q=(t-k+n)%n
        rcopy(o_ref.at[q],o_ref.at[q],ss.at[k],rs.at[k],(dp,q)).wait_recv()
    for cp in cps: cp.wait_send()
    own.wait()

def exchange(a):
    DS=pltpu.SemaphoreType.DMA
    n=a.shape[0]
    hbm=pl.BlockSpec(memory_space=pl.ANY)
    return pl.pallas_call(exchange_kernel,out_shape=jax.ShapeDtypeStruct(a.shape,a.dtype),in_specs=[hbm],out_specs=hbm,
        scratch_shapes=[DS((n,)),DS((n,)),DS((1,))],compiler_params=pltpu.CompilerParams(has_side_effects=True),name="exchange_over_tile")(a)

def tile_sum_kernel(a_ref,o_ref,cbuf,xsend,xbuf,ss,rs):
    z,y,x,c=where_am_i()
    rows=a_ref.shape[1]; nch=ss.shape[1]; ch=rows//nch
    core=dev(z,y,x,1-c); across=dev(z,y,1-x,c)
    def c_copy(k,j):
        xx=(1-x) if k==0 else x
        sl=pl.ds(j*ch,ch)
        return rcopy(a_ref.at[xx*2+1-c,sl],cbuf.at[k,sl],ss.at[k,j],rs.at[k,j],core)
    def x_copy(j):
        sl=pl.ds(j*ch,ch)
        return rcopy(xsend.at[sl],xbuf.at[sl],ss.at[2,j],rs.at[2,j],across)
    for k in range(2):
        for j in range(nch): c_copy(k,j).start()
    def first(j,_):
        c_copy(0,j).wait_recv()
        sl=pl.ds(j*ch,ch)
        xsend[sl]=(a_ref[(1-x)*2+c,sl].astype(f32)+cbuf[0,sl].astype(f32)).astype(bf)
        x_copy(j).start()
        return 0
    lax.fori_loop(0,nch,first,0)
    def second(j,_):
        c_copy(1,j).wait_recv()
        x_copy(j).wait_recv()
        sl=pl.ds(j*ch,ch)
        o_ref[sl]=a_ref[x*2+c,sl].astype(f32)+cbuf[1,sl].astype(f32)+xbuf[sl].astype(f32)
        return 0
    lax.fori_loop(0,nch,second,0)
    def done(j,_):
        c_copy(0,j).wait_send(); c_copy(1,j).wait_send(); x_copy(j).wait_send()
        return 0
    lax.fori_loop(0,nch,done,0)

def tile_sum(a,nch=8):
    DS=pltpu.SemaphoreType.DMA
    n,rows,cols=a.shape
    vm=pl.BlockSpec(memory_space=pltpu.VMEM)
    return pl.pallas_call(tile_sum_kernel,out_shape=jax.ShapeDtypeStruct((rows,cols),f32),in_specs=[vm],out_specs=vm,
        scratch_shapes=[pltpu.VMEM((2,rows,cols),bf),pltpu.VMEM((rows,cols),bf),pltpu.VMEM((rows,cols),bf),DS((3,nch)),DS((3,nch))],
        compiler_params=pltpu.CompilerParams(has_side_effects=True,vmem_limit_bytes=40<<20),name="sum_rows_over_tile")(a)

def grad_sum_kernel(a_ref,o_ref,mine,xb0,yb0,zin,xb1,yb1,zin1,zin2,yb2,xb2,cs,cr,ss,rs,zs,zr,fs,fr):
    z,y,x,c=where_am_i()
    core=dev(z,y,x,1-c); across=dev(z,y,1-x,c); beside=dev(z,1-y,x,c)
    up=dev(jnp.minimum(z+1,3),y,x,c); down=dev(jnp.maximum(z-1,0),y,x,c)
    other=(1-c)*12; own=c*12
    def c_copy(p,d):
        return rcopy(a_ref.at[d,pl.ds(other+p*4,4)],mine.at[p,d],cs.at[p,d],cr.at[p,d],core)
    order=(2,0,1)
    def go(p):
        def s(d,_):
            c_copy(p,d).start(); return 0
        lax.fori_loop(0,8,s,0)
    for p in order: go(p)
    def add_own(p):
        def s(d,_):
            c_copy(p,d).wait_recv()
            for b in range(4):
                mine[p,d,b]=(mine[p,d,b].astype(f32)+a_ref[d,own+p*4+b].astype(f32)).astype(bf)
            return 0
        lax.fori_loop(0,8,s,0)
    def add(dst,src):
        n=dst.shape[0]
        for i in range(n): dst[i]=(dst[i].astype(f32)+src[i].astype(f32)).astype(bf)
    def line(buf_of,inbox,sem):
        def cp(tz,go_down):
            k=1 if go_down else 0
            return rcopy(buf_of(tz),inbox.at[k,tz],zs.at[sem,k,tz],zr.at[sem,k,tz],down if go_down else up)
        def arrive(tz,go_down):
            k=1 if go_down else 0
            return rcopy(inbox.at[k,tz],inbox.at[k,tz],zs.at[sem,k,tz],zr.at[sem,k,tz],down)
        return cp,arrive
    def line_start(cp):
        for tz in (0,1,2):
            @pl.when(z==3)
            def _(): cp(tz,True).start()
        for tz in (3,2,1):
            @pl.when(z==0)
            def _(): cp(tz,False).start()
    def line_pass(cp,arrive,buf_of,inbox,addf):
        for tz in (0,1,2):
            @pl.when(jnp.logical_and(z<3,z>tz))
            def _():
                arrive(tz,True).wait_recv(); addf(buf_of(tz),inbox.at[1,tz]); cp(tz,True).start()
            u=3-tz
            @pl.when(jnp.logical_and(z>0,z<u))
            def _():
                arrive(u,False).wait_recv(); addf(buf_of(u),inbox.at[0,u]); cp(u,False).start()
    def line_end(cp,arrive,buf_of,inbox,addf):
        @pl.when(z<3)
        def _():
            arrive(z,True).wait_recv(); addf(buf_of(z),inbox.at[1,z])
        @pl.when(z>0)
        def _():
            arrive(z,False).wait_recv(); addf(buf_of(z),inbox.at[0,z])
    def line_sent(cp):
        for tz in (0,1,2):
            @pl.when(z>tz)
            def _(): cp(tz,True).wait_send()
            @pl.when(z<3-tz)
            def _(): cp(3-tz,False).wait_send()
    def add2(dst,src):
        for i in range(2):
            for j in range(4): dst[i,j]=(dst[i,j].astype(f32)+src[i,j].astype(f32)).astype(bf)
    p2_of=lambda tz: mine.at[2,pl.ds(tz*2,2)]
    cp2,ar2=line(p2_of,zin,0)
    add_own(2); line_start(cp2)
    def x0(d): return rcopy(mine.at[0,d,pl.ds((1-x)*2,2)],xb0.at[d],ss.at[0,d],rs.at[0,d],across)
    def s0(d,_):
        c_copy(0,d).wait_recv()
        for b in range(4):
            mine[0,d,b]=(mine[0,d,b].astype(f32)+a_ref[d,own+b].astype(f32)).astype(bf)
        x0(d).start()
        return 0
    lax.fori_loop(0,8,s0,0)
    def y1(zz): return rcopy(mine.at[1,zz*2+1-y],yb0.at[zz],ss.at[1,zz],rs.at[1,zz],beside)
    add_own(1)
    for zz in range(4): y1(zz).start()
    line_pass(cp2,ar2,p2_of,zin,add2)
    def p0(zz,yy): return mine.at[0,zz*2+yy,pl.ds(x*2,2)]
    def y0(zz): return rcopy(p0(zz,1-y),yb1.at[zz],ss.at[2,zz],rs.at[2,zz],beside)
    for zz in range(4):
        for yy in range(2):
            d=zz*2+yy
            x0(d).wait_recv(); add(p0(zz,yy),xb0.at[d])
        y0(zz).start()
    def p1(zz): return mine.at[1,zz*2+y]
    def x1(zz): return rcopy(mine.at[1,zz*2+y,pl.ds((1-x)*2,2)],xb1.at[zz],ss.at[3,zz],rs.at[3,zz],across)
    for zz in range(4):
        y1(zz).wait_recv(); add(p1(zz),yb0.at[zz]); x1(zz).start()
    line_end(cp2,ar2,p2_of,zin,add2)
    y2=rcopy(mine.at[2,z*2+1-y],yb2,ss.at[4,0],rs.at[4,0],beside)
    y2.start()
    q0=lambda tz: mine.at[0,tz*2+y,pl.ds(x*2,2)]
    cp0,ar0=line(q0,zin1,1)
    for zz in range(4):
        y0(zz).wait_recv(); add(q0(zz),yb1.at[zz])
    line_start(cp0)
    q1=lambda tz: mine.at[1,tz*2+y,pl.ds(x*2,2)]
    cp1,ar1=line(q1,zin2,2)
    for zz in range(4):
        x1(zz).wait_recv(); add(q1(zz),xb1.at[zz])
    line_start(cp1)
    y2.wait_recv(); add(mine.at[2,z*2+y],yb2)
    x2=rcopy(mine.at[2,z*2+y,pl.ds((1-x)*2,2)],xb2,ss.at[5,0],rs.at[5,0],across)
    x2.start()
    line_pass(cp0,ar0,q0,zin1,add)
    line_pass(cp1,ar1,q1,zin2,add)
    x2.wait_recv()
    me=z*2+y
    add(mine.at[2,me,pl.ds(x*2,2)],xb2)
    def place(xx,cc,p): return o_ref.at[pl.ds(cc*12+p*4+xx*2,2)]
    targets=((1-x,c),(x,1-c),(1-x,1-c))
    def f_copy(i,p):
        xx,cc=targets[i]
        return rcopy(mine.at[p,me,pl.ds(x*2,2)],place(x,c,p),fs.at[i,p],fr.at[i,p],dev(z,y,xx,cc))
    def f_arrive(i,p):
        xx,cc=targets[i]
        r=place(xx,cc,p)
        return rcopy(r,r,fs.at[i,p],fr.at[i,p],core)
    def finish(p):
        o_ref[pl.ds(own+p*4+x*2,2)]=mine[p,me,pl.ds(x*2,2)]
        for i in (2,0,1): f_copy(i,p).start()
    finish(2)
    line_end(cp0,ar0,q0,zin1,add); finish(0)
    line_end(cp1,ar1,q1,zin2,add); finish(1)
    for p in range(3):
        for i in range(3): f_arrive(i,p).wait_recv()
    for p in range(3):
        for i in range(3): f_copy(i,p).wait_send()
    def drain(d,_):
        for p in range(3): c_copy(p,d).wait_send()
        x0(d).wait_send()
        return 0
    lax.fori_loop(0,8,drain,0)
    for zz in range(4):
        y1(zz).wait_send(); y0(zz).wait_send(); x1(zz).wait_send()
    y2.wait_send(); x2.wait_send()
    line_sent(cp2); line_sent(cp0); line_sent(cp1)

def grad_sum(a):
    DS=pltpu.SemaphoreType.DMA
    R=a.shape[2]
    vm=pl.BlockSpec(memory_space=pltpu.VMEM)
    V=lambda *s: pltpu.VMEM(s+(R,128),bf)
    return pl.pallas_call(grad_sum_kernel,out_shape=jax.ShapeDtypeStruct((24,R,128),bf),in_specs=[vm],out_specs=vm,
        scratch_shapes=[V(3,8,4),V(8,2),V(4,4),V(2,4,2,4),V(4,2),V(4,2),V(2,4,2),V(2,4,2),V(4),V(2),
            DS((3,8)),DS((3,8)),DS((6,8)),DS((6,8)),DS((3,2,4)),DS((3,2,4)),DS((3,3)),DS((3,3))],
        compiler_params=pltpu.CompilerParams(has_side_effects=True,vmem_limit_bytes=56<<20),name="sum_gradients")(a)


H = 12
NGRP = 16
STEP = 10
EPS_NORM = 1e-06
BETA_ONE = 0.5
BETA_TWO = 0.5
ADAM_EPS = 1e-08
RATE_BLOCK = 0.3
RATE_VECTOR = 0.2
NEG_RAW = -8.0e9
HEAD = 64
SCALE = 1.0 / math.sqrt(HEAD)
EXP2 = SCALE * math.log2(math.e)
HIGHEST_PREC = lax.Precision.HIGHEST
NN = (((1,), (0,)), ((), ()))
NT = (((1,), (1,)), ((), ()))
TN = (((0,), (0,)), ((), ()))


def mm(a, b, dims=NN):
    return lax.dot_general(a, b, dims, preferred_element_type=f32)


def vmem_spec():
    return pl.BlockSpec(memory_space=pltpu.VMEM)


def smem_spec():
    return pl.BlockSpec(memory_space=pltpu.SMEM)


def any_spec():
    return pl.BlockSpec(memory_space=pl.ANY)


def params(mib=48):
    return pltpu.CompilerParams(vmem_limit_bytes=mib << 20)


def pack(block):
    half = block.shape[0] // 2
    return block[:, :128], jnp.concatenate([block[:half, 128:], block[half:, 128:]], axis=1)


def unpack(top, tail):
    return jnp.concatenate([top, jnp.concatenate([tail[:, :64], tail[:, 64:]], axis=0)], axis=1)


def pack_kernel(m_ref, p_ref, s_ref):
    m = m_ref[0]
    top, tail = pack(m)
    p_ref[0, :192] = top.astype(bf)
    p_ref[0, 192:] = tail.astype(bf)
    s_ref[0] = jnp.full((8, 128), jnp.sum(m * m), f32)


def pack_master(master):
    n = master.shape[0]
    return pl.pallas_call(
        pack_kernel,
        grid=(n,),
        in_specs=[pl.BlockSpec((1, 192, 192), lambda i: (i, 0, 0))],
        out_specs=[pl.BlockSpec((1, 288, 128), lambda i: (i, 0, 0)), pl.BlockSpec((1, 8, 128), lambda i: (i, 0, 0))],
        out_shape=[jax.ShapeDtypeStruct((n, 288, 128), bf), jax.ShapeDtypeStruct((n, 8, 128), f32)],
        name="pack_master",
    )(master)


def assemble_kernel(inv_ref, tile_ref, w_ref, qkv_ref, out_ref, up_ref, down_ref, buf, sems):
    t = tile_ref[0]
    def where(i):
        own = (i // 3) * 12 + (i % 3) * 4 + t
        return inv_ref[jnp.where(i < 12, own, i + 36)]

    def copy(i):
        return pltpu.make_async_copy(w_ref.at[where(i)], buf.at[i], sems.at[i])

    def start(i, _):
        copy(i).start()
        return 0

    lax.fori_loop(0, 156, start, 0)

    def block(i):
        copy(i).wait()
        return unpack(buf[i, :192], buf[i, 192:])

    for r in range(4):
        qkv_ref[r * 192 : (r + 1) * 192, :] = jnp.concatenate([block(r * 3 + k) for k in range(3)], axis=1)

    def place(dst, first, pairs):
        def body(j, _):
            i = first + 2 * j
            r = pl.multiple_of((j // pairs) * 192, 64)
            col = pl.multiple_of((j % pairs) * 384, 128)
            dst[pl.ds(r, 192), pl.ds(col, 384)] = jnp.concatenate([block(i), block(i + 1)], axis=1)
            return 0

        return body

    lax.fori_loop(0, 8, place(out_ref, 12, 2), 0)
    lax.fori_loop(0, 32, place(up_ref, 28, 8), 0)
    lax.fori_loop(0, 32, place(down_ref, 92, 2), 0)


def assemble(inv, tile, w):
    shapes = [(768, 576), (768, 768), (768, 3072), (3072, 768)]
    return pl.pallas_call(
        assemble_kernel,
        in_specs=[smem_spec(), smem_spec(), any_spec()],
        out_specs=[vmem_spec()] * 4,
        out_shape=[jax.ShapeDtypeStruct(s, bf) for s in shapes],
        scratch_shapes=[pltpu.VMEM((156, 288, 128), bf), pltpu.SemaphoreType.DMA((156,))],
        compiler_params=params(40),
        name="assemble_weights",
    )(inv, tile, w)


def qkv_kernel(src_ref, cnt_ref, x0, x1, x2, x3, w_ref, gain_ref, shift_ref, bq_ref, bv_ref, a_ref, q_ref, qt_ref, k_ref, kt_ref, v_ref, vt_ref):
    i = pl.program_id(0)
    x = jnp.concatenate([r[...] for r in (x0, x1, x2, x3)], axis=0).astype(f32)
    mean = jnp.mean(x, axis=-1, keepdims=True)
    cen = x - mean
    inv_std = lax.rsqrt(jnp.mean(cen * cen, axis=-1, keepdims=True) + EPS_NORM)
    a = (cen * inv_std * gain_ref[...] + shift_ref[...]).astype(bf)
    a_ref[...] = a
    qkv = mm(a, w_ref[...])
    q = (qkv[:, :192] + bq_ref[...]).astype(bf).astype(f32)
    k = qkv[:, 192:384].astype(bf).astype(f32)
    v = (qkv[:, 384:] + bv_ref[...]).astype(bf).astype(f32)
    row = lax.broadcasted_iota(jnp.int32, (128, 64), 0)
    lane = lax.broadcasted_iota(jnp.int32, (512, 64), 1)
    masked = jnp.concatenate(
        [jnp.where(row < cnt_ref[4 * i + b], 0.0, NEG_RAW) for b in range(4)], axis=0
    )
    ones = jnp.where(lane < 4, 1.0, 0.0)
    k_tail = jnp.where(lane == 0, masked, ones)
    v_tail = jnp.where(lane < 3, 1.0, 0.0)
    zero = jnp.zeros((512, 64), f32)
    sub = lax.broadcasted_iota(jnp.int32, (64, 512), 0)
    t_tail = jnp.where(sub < 1, 1.0, 0.0)
    qt, kt, vt = q.T, k.T, v.T
    for h in range(3):
        s = slice(h * 64, (h + 1) * 64)
        q_ref[h] = jnp.concatenate([q[:, s], zero], axis=1).astype(bf)
        k_ref[h] = jnp.concatenate([k[:, s], k_tail], axis=1).astype(bf)
        v_ref[h] = jnp.concatenate([v[:, s], v_tail], axis=1).astype(bf)
        qt_ref[h] = jnp.concatenate([qt[s], t_tail], axis=0).astype(bf)
        kt_ref[h] = kt[s].astype(bf)
        vt_ref[h] = jnp.concatenate([vt[s], t_tail[:16]], axis=0).astype(bf)


def qkv_forward(src, cnt, tokens, w, gain, shift, bq, bv):
    n = tokens.shape[0]
    rows = [pl.BlockSpec((128, 768), lambda i, s, c, k=k: (s[4 * i + k], 0)) for k in range(4)]
    row = lambda i, s, c: (0, 0)
    spec = pltpu.PrefetchScalarGridSpec(
        num_scalar_prefetch=2,
        grid=(n // 512,),
        in_specs=rows
        + [pl.BlockSpec((768, 576), row), pl.BlockSpec((1, 768), row), pl.BlockSpec((1, 768), row), pl.BlockSpec((1, 192), row), pl.BlockSpec((1, 192), row)],
        out_specs=[
            pl.BlockSpec((512, 768), lambda i, s, c: (i, 0)),
            pl.BlockSpec((3, 512, 128), lambda i, s, c: (0, i, 0)),
            pl.BlockSpec((3, 128, 512), lambda i, s, c: (0, 0, i)),
            pl.BlockSpec((3, 512, 128), lambda i, s, c: (0, i, 0)),
            pl.BlockSpec((3, 64, 512), lambda i, s, c: (0, 0, i)),
            pl.BlockSpec((3, 512, 128), lambda i, s, c: (0, i, 0)),
            pl.BlockSpec((3, 80, 512), lambda i, s, c: (0, 0, i)),
        ],
    )
    shapes = [(n, 768), (3, n, 128), (3, 128, n), (3, n, 128), (3, 64, n), (3, n, 128), (3, 80, n)]
    return pl.pallas_call(
        qkv_kernel,
        grid_spec=spec,
        out_shape=[jax.ShapeDtypeStruct(s, bf) for s in shapes],
        compiler_params=params(40),
        name="norm_and_qkv",
    )(src, cnt, tokens, tokens, tokens, tokens, w, gain, shift, bq, bv)


def split3(v):
    a = v.astype(bf).astype(f32)
    b = (v - a).astype(bf).astype(f32)
    return a, b, v - a - b


def attend_kernel(bq, n_ref, k_ref, qt_ref, vt_ref, ot_ref, qb_ref):
    live = n_ref[0]
    qi = pl.program_id(1)

    @pl.when(qi * bq < live * 128)
    def _():
        qt = qt_ref[0]

        def block(start, size, carry):
            top, acc = carry
            s = mm(k_ref[0, pl.ds(start, size), :], qt) * EXP2
            new = jnp.maximum(top, jnp.max(s, axis=0, keepdims=True))
            p = jnp.exp2(s - new).astype(bf)
            acc = acc * jnp.exp2(top - new) + mm(vt_ref[0, :, pl.ds(start, size)], p)
            return new, acc

        def step(j, carry):
            return block(pl.multiple_of(j * 1024, 1024), 1024, carry)

        def rest(j, carry):
            return block(pl.multiple_of(j * 256, 256), 256, carry)

        pairs = (live + 1) // 2
        carry = (jnp.full((1, bq), -3e38, f32), jnp.zeros((80, bq), f32))
        carry = lax.fori_loop(0, pairs // 4, step, carry)
        top, acc = lax.fori_loop((pairs // 4) * 4, pairs, rest, carry)
        total = acc[64:65]
        ot_ref[0] = acc[:64] / total
        a, b, c = split3((top + jnp.log2(total)) * (-1.0 / EXP2))
        row = lax.broadcasted_iota(jnp.int32, (64, bq), 0)
        tail = jnp.where(row == 0, 1.0, jnp.where(row == 1, a, jnp.where(row == 2, b, jnp.where(row == 3, c, 0.0))))
        qb_ref[0, :64] = qt[:64]
        qb_ref[0, 64:] = tail.astype(bf)


def attend(live, k, qt, vt, bq=1024):
    n = k.shape[1]
    spec = pltpu.PrefetchScalarGridSpec(
        num_scalar_prefetch=1,
        grid=(3, n // bq),
        in_specs=[
            pl.BlockSpec((1, n, 128), lambda h, i, s: (h, 0, 0)),
            pl.BlockSpec((1, 128, bq), lambda h, i, s: (h, 0, i)),
            pl.BlockSpec((1, 80, n), lambda h, i, s: (h, 0, 0)),
        ],
        out_specs=[pl.BlockSpec((1, 64, bq), lambda h, i, s: (h, 0, i)), pl.BlockSpec((1, 128, bq), lambda h, i, s: (h, 0, i))],
    )
    return pl.pallas_call(
        functools.partial(attend_kernel, bq),
        grid_spec=spec,
        out_shape=[jax.ShapeDtypeStruct((3, 64, n), f32), jax.ShapeDtypeStruct((3, 128, n), bf)],
        compiler_params=params(48),
        name="attention_forward",
    )(live, k, qt, vt)


def spread_kernel(src_ref, n_ref, ot_ref, o_ref):
    live = n_ref[0]
    per = o_ref.shape[2] // 128

    def step(b, _):
        g = src_ref[b]
        lanes = pl.ds(pl.multiple_of(b * 128, 128), 128)
        to = pl.ds(pl.multiple_of((g % per) * 128, 128), 128)

        @pl.when(b < live)
        def _():
            for h in range(3):
                o_ref[g // per, h * 64 : (h + 1) * 64, to] = ot_ref[h, :, lanes].astype(bf)

        @pl.when(b >= live)
        def _():
            o_ref[g // per, :, to] = jnp.zeros((192, 128), bf)

        return 0

    lax.fori_loop(0, ot_ref.shape[2] // 128, step, 0)


def spread(src, live, ot, tiles):
    n = ot.shape[2]
    return pl.pallas_call(
        spread_kernel,
        in_specs=[smem_spec(), smem_spec(), vmem_spec()],
        out_specs=vmem_spec(),
        out_shape=jax.ShapeDtypeStruct((tiles, 192, n // tiles), bf),
        compiler_params=params(24),
        name="spread_attended",
    )(src, live, ot)


def collect_kernel(src_ref, n_ref, g_ref, ot_ref, dt_ref, d_ref):
    live = n_ref[0]
    per = g_ref.shape[2] // 128
    row = lax.broadcasted_iota(jnp.int32, (64, 128), 0)

    def step(b, _):
        g = src_ref[b]
        to = pl.ds(pl.multiple_of(b * 128, 128), 128)
        lanes = pl.ds(pl.multiple_of((g % per) * 128, 128), 128)

        @pl.when(b < live)
        def _():
            for h in range(3):
                d = g_ref[g // per, h * 64 : (h + 1) * 64, lanes].astype(f32)
                delta = jnp.sum(d * ot_ref[h, :, to], axis=0, keepdims=True)
                x, y, z = split3(-delta)
                tail = jnp.where(row == 0, x, jnp.where(row == 1, y, jnp.where(row == 2, z, 0.0)))
                both = jnp.concatenate([d, tail], axis=0)
                dt_ref[h, :, to] = both.astype(bf)
                d_ref[h, to, :] = jnp.concatenate([d, jnp.zeros_like(d)], axis=0).T.astype(bf)

        @pl.when(b >= live)
        def _():
            dt_ref[:, :, to] = jnp.zeros((3, 128, 128), bf)
            d_ref[:, to, :] = jnp.zeros((3, 128, 128), bf)

        return 0

    lax.fori_loop(0, ot_ref.shape[2] // 128, step, 0)


def collect(src, live, grad, ot):
    n = ot.shape[2]
    return pl.pallas_call(
        collect_kernel,
        in_specs=[smem_spec(), smem_spec(), vmem_spec(), vmem_spec()],
        out_specs=[vmem_spec()] * 2,
        out_shape=[jax.ShapeDtypeStruct((3, 128, n), bf), jax.ShapeDtypeStruct((3, n, 128), bf)],
        compiler_params=params(32),
        name="collect_attended_grad",
    )(src, live, grad, ot)


def attend_back_kernel(bq, bk, n_ref, k_ref, kt_ref, v_ref, qb_ref, q_ref, dt_ref, d_ref, dq_ref, dk_ref, dv_ref):
    live = n_ref[0]
    j = pl.program_id(1)

    @pl.when(j == 0)
    def _():
        dq_ref[...] = jnp.zeros_like(dq_ref)

    @pl.when(j * bk < live * 128)
    def _():
        k, v, kt = k_ref[0], v_ref[0], kt_ref[0]

        def block(start, size, carry):
            dk, dv = carry
            lanes = pl.ds(start, size)
            p = jnp.exp2(mm(k, qb_ref[0, :, lanes]) * EXP2)
            ds = (p * mm(v, dt_ref[0, :, lanes])).astype(bf)
            dv = dv + mm(p.astype(bf), d_ref[0, lanes, :])
            dk = dk + mm(ds, q_ref[0, lanes, :])
            dq_ref[0, :, lanes] += mm(kt, ds)
            return dk, dv

        def step(i, carry):
            return block(pl.multiple_of(i * bq, bq), bq, carry)

        def rest(i, carry):
            return block(pl.multiple_of(i * 256, 256), 256, carry)

        pairs = (live + 1) // 2
        full = pairs * 256 // bq
        zero = jnp.zeros((bk, 128), f32)
        carry = lax.fori_loop(0, full, step, (zero, zero))
        dk, dv = lax.fori_loop(full * bq // 256, pairs, rest, carry)
        dk_ref[0] = (dk * SCALE).astype(bf)
        dv_ref[0] = dv.astype(bf)


def attend_back(live, k, kt, v, qb, q, dt, d, bq=1024, bk=512):
    n = k.shape[1]
    whole_t = lambda h, j, s: (h, 0, 0)
    spec = pltpu.PrefetchScalarGridSpec(
        num_scalar_prefetch=1,
        grid=(3, n // bk),
        in_specs=[
            pl.BlockSpec((1, bk, 128), lambda h, j, s: (h, j, 0)),
            pl.BlockSpec((1, 64, bk), lambda h, j, s: (h, 0, j)),
            pl.BlockSpec((1, bk, 128), lambda h, j, s: (h, j, 0)),
            pl.BlockSpec((1, 128, n), whole_t),
            pl.BlockSpec((1, n, 128), whole_t),
            pl.BlockSpec((1, 128, n), whole_t),
            pl.BlockSpec((1, n, 128), whole_t),
        ],
        out_specs=[
            pl.BlockSpec((1, 64, n), whole_t),
            pl.BlockSpec((1, bk, 128), lambda h, j, s: (h, j, 0)),
            pl.BlockSpec((1, bk, 128), lambda h, j, s: (h, j, 0)),
        ],
    )
    return pl.pallas_call(
        functools.partial(attend_back_kernel, bq, bk),
        grid_spec=spec,
        out_shape=[jax.ShapeDtypeStruct((3, 64, n), f32), jax.ShapeDtypeStruct((3, n, 128), bf), jax.ShapeDtypeStruct((3, n, 128), bf)],
        compiler_params=params(48),
        name="attention_backward",
    )(live, k, kt, v, qb, q, dt, d)


def qkv_back_kernel(src_ref, n_ref, dq_ref, dk_ref, dv_ref, a_ref, w_ref, g_ref, gw_ref, gb_ref, acc, sums, rows, sems):
    i = pl.program_id(0)
    live = n_ref[0]

    @pl.when(i == 0)
    def _():
        acc[...] = jnp.zeros_like(acc)
        sums[...] = jnp.zeros_like(sums)

    @pl.when(4 * i < live)
    def _():
        dq = jnp.concatenate([dq_ref[h] for h in range(3)], axis=0).T * SCALE
        g = jnp.concatenate(
            [dq] + [dk_ref[h][:, :64].astype(f32) for h in range(3)] + [dv_ref[h][:, :64].astype(f32) for h in range(3)], axis=1
        ).astype(bf)
        acc[...] += mm(a_ref[...], g, TN)
        sums[...] += jnp.broadcast_to(jnp.sum(g.astype(f32), axis=0, keepdims=True), sums.shape)
        rows[...] = mm(g, w_ref[...], NT).astype(bf)

    @pl.when(4 * i >= live)
    def _():
        rows[...] = jnp.zeros_like(rows)

    copies = [
        pltpu.make_async_copy(rows.at[pl.ds(b * 128, 128)], g_ref.at[pl.ds(pl.multiple_of(src_ref[4 * i + b] * 128, 128), 128)], sems.at[b])
        for b in range(4)
    ]
    for copy in copies:
        copy.start()
    for copy in copies:
        copy.wait()

    @pl.when(i == pl.num_programs(0) - 1)
    def _():
        for r in range(4):
            for c in range(3):
                top, tail = pack(acc[r * 192 : (r + 1) * 192, c * 192 : (c + 1) * 192])
                gw_ref[r * 3 + c, :192] = top.astype(bf)
                gw_ref[r * 3 + c, 192:] = tail.astype(bf)
        gb_ref[...] = sums[...]


def qkv_backward(src, live, dq, dk, dv, a, w):
    n = a.shape[0]
    spec = pltpu.PrefetchScalarGridSpec(
        num_scalar_prefetch=2,
        grid=(n // 512,),
        in_specs=[
            pl.BlockSpec((3, 64, 512), lambda i, s, c: (0, 0, i)),
            pl.BlockSpec((3, 512, 128), lambda i, s, c: (0, i, 0)),
            pl.BlockSpec((3, 512, 128), lambda i, s, c: (0, i, 0)),
            pl.BlockSpec((512, 768), lambda i, s, c: (i, 0)),
            pl.BlockSpec((768, 576), lambda i, s, c: (0, 0)),
        ],
        out_specs=[any_spec(), pl.BlockSpec((12, 288, 128), lambda i, s, c: (0, 0, 0)), pl.BlockSpec((8, 576), lambda i, s, c: (0, 0))],
        scratch_shapes=[pltpu.VMEM((768, 576), f32), pltpu.VMEM((8, 576), f32), pltpu.VMEM((512, 768), bf), pltpu.SemaphoreType.DMA((4,))],
    )
    return pl.pallas_call(
        qkv_back_kernel,
        grid_spec=spec,
        out_shape=[jax.ShapeDtypeStruct((n, 768), bf), jax.ShapeDtypeStruct((12, 288, 128), bf), jax.ShapeDtypeStruct((8, 576), f32)],
        compiler_params=params(32),
        name="qkv_backward",
    )(src, live, dq, dk, dv, a, w)


def slots_kernel(inv_ref, tile_ref, qkv_ref, out_ref, up_ref, down_ref, s_ref):
    t = tile_ref[0]

    def clear(c, _):
        s_ref[inv_ref[c]] = jnp.zeros((288, 128), bf)
        return 0

    lax.fori_loop(0, 48, clear, 0)

    def own(i, _):
        s_ref[inv_ref[(i // 3) * 12 + (i % 3) * 4 + t]] = qkv_ref[i]
        return 0

    lax.fori_loop(0, 12, own, 0)

    def put(src, first, pairs):
        def body(j, _):
            r = pl.multiple_of((j // pairs) * 192, 64)
            col = pl.multiple_of((j % pairs) * 384, 128)
            two = src[pl.ds(r, 192), pl.ds(col, 384)]
            for b in range(2):
                top, tail = pack(two[:, b * 192 : (b + 1) * 192])
                slot = inv_ref[first + 2 * j + b]
                s_ref[slot, :192] = top.astype(bf)
                s_ref[slot, 192:] = tail.astype(bf)
            return 0

        return body

    lax.fori_loop(0, 8, put(out_ref, 48, 2), 0)
    lax.fori_loop(0, 32, put(up_ref, 64, 8), 0)
    lax.fori_loop(0, 32, put(down_ref, 128, 2), 0)


def to_slots(inv, tile, gqkv, gout, gup, gdown):
    return pl.pallas_call(
        slots_kernel,
        in_specs=[smem_spec(), smem_spec()] + [vmem_spec()] * 4,
        out_specs=vmem_spec(),
        out_shape=jax.ShapeDtypeStruct((192, 288, 128), bf),
        compiler_params=params(48),
        name="gradients_to_slots",
    )(inv, tile, gqkv, gout, gup, gdown)


def adam_kernel(g_ref, m1_ref, m2_ref, l_ref, r_ref, g_out, m1_out, m2_out, u_out, s_out):
    dot = functools.partial(lax.dot_general, preferred_element_type=f32, precision=HIGHEST_PREC)
    grad = unpack(g_ref[0, :192].astype(f32), g_ref[0, 192:].astype(f32))
    left, right = l_ref[0], r_ref[0]
    rot = dot(dot(left, grad, TN), right, NN)
    first = BETA_ONE * m1_ref[0] + (1.0 - BETA_ONE) * rot
    second = BETA_TWO * m2_ref[0] + (1.0 - BETA_TWO) * rot * rot
    upd = (first / (1.0 - BETA_ONE**STEP)) / (jnp.sqrt(second / (1.0 - BETA_TWO**STEP)) + ADAM_EPS)
    upd = dot(dot(left, upd, NN), right, NT)
    g_out[0] = grad
    m1_out[0] = first
    m2_out[0] = second
    u_out[0] = upd
    s_out[0] = jnp.full((8, 128), jnp.sum(upd * upd), f32)


def adam(grads, first, second, left, right):
    n = grads.shape[0]
    big = pl.BlockSpec((1, 192, 192), lambda i: (i, 0, 0))
    return pl.pallas_call(
        adam_kernel,
        grid=(n,),
        in_specs=[pl.BlockSpec((1, 288, 128), lambda i: (i, 0, 0))] + [big] * 4,
        out_specs=[big] * 4 + [pl.BlockSpec((1, 8, 128), lambda i: (i, 0, 0))],
        out_shape=[jax.ShapeDtypeStruct((n, 192, 192), f32)] * 4 + [jax.ShapeDtypeStruct((n, 8, 128), f32)],
        compiler_params=params(32),
        name="rotated_adam",
    )(grads, first, second, left, right)


def norm_forward(row_data, gain_vec, shift_vec):
    row_mean = jnp.mean(row_data, axis=-1, keepdims=True)
    centred = row_data - row_mean
    inv_std = lax.rsqrt(jnp.mean(centred * centred, axis=-1, keepdims=True) + EPS_NORM)
    normed = centred * inv_std
    return (normed * gain_vec + shift_vec, normed, inv_std)


def norm_back(grad_out, normed, inv_std, gain_vec):
    grad_normed = grad_out * gain_vec
    return inv_std * (
        grad_normed
        - jnp.mean(grad_normed, axis=-1, keepdims=True)
        - normed * jnp.mean(grad_normed * normed, axis=-1, keepdims=True)
    )


def middle(row_input, cotangent, live_rows, o_t, w_out, w_up, w_down, vec_params):
    bias_up = vec_params[8:].reshape(-1)
    residual = row_input + mm(o_t, w_out, TN) + vec_params[6]
    normed_mid, normed_two, inv_std_two = norm_forward(residual, vec_params[2], vec_params[3])
    act_two = normed_mid.astype(bf)
    pre_act = mm(act_two, w_up) + bias_up
    hidden_f, gelu_pull = jax.vjp(lambda v: jax.nn.gelu(v, approximate=False), pre_act)
    hidden = hidden_f.astype(bf)
    output = (live_rows * (residual + mm(hidden, w_down) + vec_params[7])).astype(bf)
    grad_y = cotangent * live_rows
    gm = grad_y.astype(bf)
    grad_down = mm(hidden, gm, TN).astype(bf)
    grad_pre = gelu_pull(mm(gm, w_down, NT))[0].astype(bf)
    grad_up = mm(act_two, grad_pre, TN).astype(bf)
    grad_mid = mm(grad_pre, w_up, NT)
    grad_resid = grad_y + norm_back(grad_mid, normed_two, inv_std_two, vec_params[2])
    gb = grad_resid.astype(bf)
    grad_out = mm(o_t, gb).astype(bf)
    go_t = mm(w_out, gb, NT).astype(bf)
    sums = [
        jnp.sum(grad_mid * normed_two, axis=0),
        jnp.sum(grad_mid, axis=0),
        jnp.sum(gb.astype(f32), axis=0),
        jnp.sum(gm.astype(f32), axis=0),
        jnp.sum(grad_pre.astype(f32), axis=0).reshape(-1, row_input.shape[1]),
    ]
    return output, grad_resid, go_t, grad_out, grad_up, grad_down, sums


def block_plan(counts, slot_count):
    tiles = counts.shape[0]
    per = slot_count // 128
    j = lax.broadcasted_iota(jnp.int32, (tiles, per), 1)
    kept = jnp.clip(counts[:, None] - j * 128, 0, 128).reshape(-1)
    full = (kept > 0).astype(jnp.int32)
    index = jnp.arange(tiles * per, dtype=jnp.int32)
    before = (index[None, :] < index[:, None]).astype(jnp.int32)
    ahead = jnp.sum(before * full[None, :], axis=1)
    live = jnp.sum(full)
    place = jnp.where(full > 0, ahead, live + index - ahead)
    hot = (place[None, :] == index[:, None]).astype(jnp.int32)
    return jnp.sum(hot * index[None, :], axis=1), jnp.sum(hot * kept[None, :], axis=1), live.reshape(1)


def make_body(tuned):
    def body(tokens, cotangent, counts, master, slot_block, groups, first_moment, second_moment, left_basis, right_basis, vec_params, vec_first, vec_second):
        slot_count, width = tokens.shape[1:]
        per_owner = master.shape[0]
        tile = lax.axis_index("tile")
        packed, weight_sq = pack_master(master)
        own_tokens = tokens.reshape(slot_count, width)
        count_tile = jnp.broadcast_to(counts.reshape(1, 1), (8, 128))
        if tuned:
            blocks, token_all, count_all = gather_all(packed, own_tokens, count_tile)
        else:
            blocks = lax.all_gather(packed, "dp", axis=0, tiled=True)
            token_all = lax.all_gather(own_tokens, "tile", axis=0)
            count_all = lax.all_gather(count_tile, "tile", axis=0)
        tiles = token_all.shape[0]
        block_count = blocks.shape[0]
        src, cnt, live = block_plan(count_all[:, 0, 0], slot_count)
        index = jnp.arange(block_count, dtype=jnp.int32)
        inverse = jnp.sum((slot_block[None, :] == index[:, None]).astype(jnp.int32) * index[None, :], axis=1)
        tile_one = tile.astype(jnp.int32).reshape(1)
        w_qkv, w_out, w_up, w_down = assemble(inverse, tile_one, blocks)
        own = width // tiles
        bias = lambda row: lax.dynamic_slice(vec_params[row : row + 1], (0, tile * own), (1, own))
        a1, q, qt, k, kt, v, vt = qkv_forward(
            src, cnt, token_all.reshape(-1, width), w_qkv, vec_params[0:1], vec_params[1:2], bias(4), bias(5)
        )
        ot, qb = attend(live, k, qt, vt)
        o_t = exchange(spread(src, live, ot, tiles)).reshape(width, slot_count)

        row_input = own_tokens.astype(f32)
        slot_index = lax.broadcasted_iota(jnp.int32, (slot_count, 1), 0)
        live_rows = (slot_index < counts[0, 0]).astype(f32)
        output, grad_resid, go_t, grad_out, grad_up, grad_down, sums = middle(
            row_input, cotangent.reshape(slot_count, width).astype(f32), live_rows, o_t, w_out, w_up, w_down, vec_params
        )
        go = exchange(go_t.reshape(tiles, own, slot_count))
        dt, d = collect(src, live, go, ot)
        dq, dk, dv = attend_back(live, k, kt, v, qb, q, dt, d)
        g_part, gw_qkv, qkv_sums = qkv_backward(src, live, dq, dk, dv, a1, w_qkv)
        g_part = g_part.reshape(tiles, slot_count, width)
        slot_grads = to_slots(inverse, tile_one, gw_qkv, grad_out, grad_up, grad_down)
        if tuned:
            g1 = tile_sum(g_part)
            grads = grad_sum(slot_grads.reshape(-1, per_owner, 288, 128))
        else:
            g1 = lax.psum_scatter(g_part.astype(f32), "tile", scatter_dimension=0, tiled=False)
            grads = lax.psum(lax.psum_scatter(slot_grads.astype(f32), "dp", scatter_dimension=0, tiled=True), "tile").astype(bf)
        _, normed_one, inv_std_one = norm_forward(row_input, vec_params[0], vec_params[1])
        input_grad = grad_resid + norm_back(g1, normed_one, inv_std_one, vec_params[0])
        zero = jnp.zeros((width,), f32)
        at_own = lambda s: lax.dynamic_update_slice(zero, s, (tile * own,))
        rows = jnp.stack(
            [jnp.sum(g1 * normed_one, axis=0), jnp.sum(g1, axis=0), sums[0], sums[1], at_own(qkv_sums[0, :own]), at_own(qkv_sums[0, 2 * own :]), sums[2], sums[3]],
            axis=0,
        )
        vector_grads = lax.psum(jnp.concatenate([rows, sums[4]], axis=0), ("dp", "tile"))

        weight_grads, first_out, second_out, update, update_sq = adam(grads, first_moment, second_moment, left_basis, right_basis)
        group_hot = (groups[:, None] == jnp.arange(NGRP, dtype=jnp.int32)[None, :]).astype(f32)
        both = jnp.stack([weight_sq[:, 0, 0], update_sq[:, 0, 0]], axis=0)
        group_both = lax.psum(jnp.sum(group_hot[None] * both[:, :, None], axis=1), "dp")
        own_both = jnp.sum(group_hot[None] * group_both[:, None, :], axis=2)
        block_rate = RATE_BLOCK * jnp.sqrt(own_both[0]) / (jnp.sqrt(own_both[1]) + 1e-06)
        master_out = master - block_rate[:, None, None] * update
        vec_first_out = BETA_ONE * vec_first + (1.0 - BETA_ONE) * vector_grads
        vec_second_out = BETA_TWO * vec_second + (1.0 - BETA_TWO) * vector_grads * vector_grads
        vec_update = (vec_first_out / (1.0 - BETA_ONE**STEP)) / (jnp.sqrt(vec_second_out / (1.0 - BETA_TWO**STEP)) + ADAM_EPS)
        return (
            output.reshape(1, slot_count, width),
            input_grad.reshape(1, slot_count, width),
            weight_grads,
            first_out,
            second_out,
            master_out,
            master_out.astype(bf),
            vector_grads,
            vec_first_out,
            vec_second_out,
            vec_params - RATE_VECTOR * vec_update,
        )

    return body


def solution(mesh):
    tuned = (mesh.shape["dp"], mesh.shape["tile"]) == (8, 4)
    rows, blocks = P("dp", "tile", None), P("dp", None, None)
    return jax.shard_map(
        make_body(tuned),
        mesh=mesh,
        in_specs=(rows, rows, P("dp", "tile"), blocks, P(), P("dp"), blocks, blocks, blocks, blocks, P(), P(), P()),
        out_specs=(rows, rows, blocks, blocks, blocks, blocks, blocks, P(), P(), P(), P()),
        check_vma=False,
    )
```

```python
import functools
import math

import jax
import jax.numpy as jnp
from jax import lax
from jax.experimental import pallas as pl
from jax.experimental.pallas import tpu as pltpu
from jax.sharding import PartitionSpec as P

f32 = jnp.float32
bf = jnp.bfloat16
MESH = pl.DeviceIdType.MESH

def where_am_i():
    dp=lax.axis_index("dp"); t=lax.axis_index("tile")
    return dp//2, dp%2, t//2, t%2

def dev(z,y,x,c):
    return (z*2+y, x*2+c)

def rcopy(src,dst,ss,rs,to):
    return pltpu.make_async_remote_copy(src_ref=src,dst_ref=dst,send_sem=ss,recv_sem=rs,device_id=to,device_id_type=MESH)

def gather_kernel(own_w,own_tok,own_cnt,all_w,all_tok,all_cnt,
                  zs,zr,ys,yr,xs,xr,cs,cr,fs,fr,ts,tr,ns,nr,ls):
    z,y,x,c=where_am_i()
    per=own_w.shape[0]
    part=per//12
    def a_of(shard,xx,cc): return all_w.at[pl.ds(shard*per+(xx*2+cc)*part,part)]
    def b_of(shard,cc): return all_w.at[pl.ds(shard*per+4*part+cc*4*part,4*part)]
    own_a=own_w.at[pl.ds((x*2+c)*part,part)]
    own_b=own_w.at[pl.ds(4*part+c*4*part,4*part)]
    me=z*2+y
    core=dev(z,y,x,1-c); across=dev(z,y,1-x,c); beside=dev(z,1-y,x,c)
    up=dev(jnp.minimum(z+1,3),y,x,c); down=dev(jnp.maximum(z-1,0),y,x,c)
    def src(shard,own):
        return (own_a,own_b) if own else (a_of(shard,x,c),b_of(shard,c))
    def z_copies(zz,own,go_up):
        shard=zz*2+y
        a,b=src(shard,own)
        d=(z-zz) if go_up else (zz-z)
        k=0 if go_up else 1
        to=up if go_up else down
        return (rcopy(a,a_of(shard,x,c),zs.at[k,d,0],zr.at[k,d,0],to),rcopy(b,b_of(shard,c),zs.at[k,d,1],zr.at[k,d,1],to))
    def z_arrivals(zz,k,dist):
        shard=zz*2+y
        a,b=a_of(shard,x,c),b_of(shard,c)
        return (rcopy(a,a,zs.at[k,dist-1,0],zr.at[k,dist-1,0],up),rcopy(b,b,zs.at[k,dist-1,1],zr.at[k,dist-1,1],up))
    def y_copies(zz,own):
        shard=zz*2+y
        a,b=src(shard,own)
        return (rcopy(a,a_of(shard,x,c),ys.at[zz,0],yr.at[zz,0],beside),rcopy(b,b_of(shard,c),ys.at[zz,1],yr.at[zz,1],beside))
    def y_arrivals(zz):
        shard=zz*2+(1-y)
        a,b=a_of(shard,x,c),b_of(shard,c)
        return (rcopy(a,a,ys.at[zz,0],yr.at[zz,0],beside),rcopy(b,b,ys.at[zz,1],yr.at[zz,1],beside))
    def x_copy(shard,own):
        return rcopy(src(shard,own)[0],a_of(shard,x,c),xs.at[shard],xr.at[shard],across)
    def x_arrival(shard):
        a=a_of(shard,1-x,c)
        return rcopy(a,a,xs.at[shard],xr.at[shard],across)
    def c_copies(shard,own):
        a,b=src(shard,own)
        return (rcopy(a,a_of(shard,x,c),cs.at[shard,0],cr.at[shard,0],core),rcopy(b,b_of(shard,c),cs.at[shard,1],cr.at[shard,1],core))
    def c_arrivals(shard):
        a,b=a_of(shard,x,1-c),b_of(shard,1-c)
        return (rcopy(a,a,cs.at[shard,0],cr.at[shard,0],core),rcopy(b,b,cs.at[shard,1],cr.at[shard,1],core))
    def f_copy(shard):
        a=a_of(shard,1-x,c)
        return rcopy(a,a,fs.at[shard],fr.at[shard],core)
    def f_arrival(shard):
        a=a_of(shard,1-x,1-c)
        return rcopy(a,a,fs.at[shard],fr.at[shard],core)
    def start(cps):
        for cp in (cps if isinstance(cps,tuple) else (cps,)): cp.start()
    def got(cps):
        for cp in (cps if isinstance(cps,tuple) else (cps,)): cp.wait_recv()
    def sent(cps):
        for cp in (cps if isinstance(cps,tuple) else (cps,)): cp.wait_send()
    tile=x*2+c
    tok_x=rcopy(own_tok,all_tok.at[tile],ts.at[0],tr.at[0],across)
    tok_c=rcopy(own_tok,all_tok.at[tile],ts.at[1],tr.at[1],core)
    far=all_tok.at[(1-x)*2+c]
    tok_f=rcopy(far,far,ts.at[2],tr.at[2],core)
    near=all_tok.at[x*2+1-c]
    diag=all_tok.at[(1-x)*2+1-c]
    cnts=[rcopy(own_cnt,all_cnt.at[tile],ns.at[i],nr.at[i],to) for i,to in enumerate((across,core,dev(z,y,1-x,1-c)))]
    cnt_in=[rcopy(r,r,ns.at[i],nr.at[i],core) for i,r in enumerate((all_cnt.at[(1-x)*2+c],all_cnt.at[x*2+1-c],all_cnt.at[(1-x)*2+1-c]))]
    local=(pltpu.make_async_copy(own_w,all_w.at[pl.ds(me*per,per)],ls.at[0]),
           pltpu.make_async_copy(own_tok,all_tok.at[tile],ls.at[1]),pltpu.make_async_copy(own_cnt,all_cnt.at[tile],ls.at[2]))
    @pl.when(z<3)
    def _(): start(z_copies(z,True,True))
    @pl.when(z>0)
    def _(): start(z_copies(z,True,False))
    start(y_copies(z,True)); start(tok_x); start(tok_c)
    for cp in cnts: cp.start()
    for cp in local: cp.start()
    def from_line(k,dist):
        zz=z-dist if k==0 else z+dist
        there=(zz>=0) if k==0 else (zz<=3)
        @pl.when(there)
        def _():
            got(z_arrivals(zz,k,dist))
            @pl.when((z<3) if k==0 else (z>0))
            def _(): start(z_copies(zz,False,k==0))
            start(y_copies(zz,False)); start(x_copy(zz*2+y,False)); start(c_copies(zz*2+y,False))
    def from_beside(zz):
        got(y_arrivals(zz))
        s=zz*2+1-y
        start(x_copy(s,False)); start(c_copies(s,False))
    def guarded(f,dist):
        @pl.when(z-dist>=0)
        def _(): f(z-dist)
        @pl.when(z+dist<=3)
        def _(): f(z+dist)
    def from_across(shard):
        got(x_arrival(shard)); start(f_copy(shard))
    from_line(0,1); from_line(1,1)
    from_beside(z)
    from_line(0,2); from_line(1,2)
    guarded(from_beside,1); guarded(lambda zz: from_across(zz*2+y),1); from_across(z*2+1-y)
    from_line(0,3); from_line(1,3)
    got(tok_x); tok_f.start()
    guarded(from_beside,2); guarded(lambda zz: from_across(zz*2+y),2); guarded(lambda zz: from_across(zz*2+1-y),1)
    guarded(from_beside,3); guarded(lambda zz: from_across(zz*2+y),3); guarded(lambda zz: from_across(zz*2+1-y),2)
    guarded(lambda zz: from_across(zz*2+1-y),3)
    def drain(s,_):
        @pl.when(s!=me)
        def _():
            got(c_arrivals(s)); got(f_arrival(s)); sent(c_copies(s,False)); sent(f_copy(s)); sent(x_copy(s,False))
        return 0
    lax.fori_loop(0,8,drain,0)
    def drain_y(zz,_):
        sent(y_copies(zz,False)); return 0
    lax.fori_loop(0,4,drain_y,0)
    for dist in range(4):
        @pl.when(jnp.logical_and(z<3,z-dist>=0))
        def _(): sent(z_copies(z-dist,False,True))
        @pl.when(jnp.logical_and(z>0,z+dist<=3))
        def _(): sent(z_copies(z+dist,False,False))
    rcopy(near,near,ts.at[1],tr.at[1],core).wait_recv()
    rcopy(diag,diag,ts.at[2],tr.at[2],core).wait_recv()
    tok_x.wait_send(); tok_c.wait_send(); tok_f.wait_send()
    for cp in cnts: cp.wait_send()
    for cp in cnt_in: cp.wait_recv()
    for cp in local: cp.wait()

def gather_all(own_w,own_tok,own_cnt):
    DS=pltpu.SemaphoreType.DMA
    hbm=pl.BlockSpec(memory_space=pl.ANY)
    return pl.pallas_call(gather_kernel,
        out_shape=[jax.ShapeDtypeStruct((8*own_w.shape[0],)+own_w.shape[1:],bf),jax.ShapeDtypeStruct((4,)+own_tok.shape,bf),jax.ShapeDtypeStruct((4,)+own_cnt.shape,own_cnt.dtype)],
        in_specs=[pl.BlockSpec(memory_space=pltpu.VMEM)]*3,out_specs=[hbm]*3,
        scratch_shapes=[DS((2,4,2)),DS((2,4,2)),DS((4,2)),DS((4,2)),DS((8,)),DS((8,)),DS((8,2)),DS((8,2)),DS((8,)),DS((8,)),DS((3,)),DS((3,)),DS((3,)),DS((3,)),DS((3,))],
        compiler_params=pltpu.CompilerParams(has_side_effects=True,vmem_limit_bytes=16<<20),name="gather_weights_tokens")(own_w,own_tok,own_cnt)

def exchange_kernel(a_ref,o_ref,ss,rs):
    dp=lax.axis_index("dp"); t=lax.axis_index("tile")
    n=a_ref.shape[0]
    def out(k):
        p=(t+k)%n
        return rcopy(a_ref.at[p],o_ref.at[t],ss.at[k],rs.at[k],(dp,p))
    def arrive(k):
        q=(t-k+n)%n
        return rcopy(o_ref.at[q],o_ref.at[q],ss.at[k],rs.at[k],(dp,q))
    for k in range(n-1,0,-1): out(k).start()
    o_ref[t]=a_ref[t]
    for k in range(1,n): arrive(k).wait_recv()
    for k in range(1,n): out(k).wait_send()

def exchange(a):
    DS=pltpu.SemaphoreType.DMA
    n=a.shape[0]
    vm=pl.BlockSpec(memory_space=pltpu.VMEM)
    return pl.pallas_call(exchange_kernel,out_shape=jax.ShapeDtypeStruct(a.shape,a.dtype),in_specs=[vm],out_specs=vm,
        scratch_shapes=[DS((n,)),DS((n,))],compiler_params=pltpu.CompilerParams(has_side_effects=True,vmem_limit_bytes=16<<20),name="exchange_over_tile")(a)

def totals_kernel(v_ref,g_ref,vo_ref,go_ref,vt,vd,gd,ts,tr,ds,dr,gs,gr):
    dp=lax.axis_index("dp"); t=lax.axis_index("tile")
    nt,nd=vt.shape[0],vd.shape[0]
    def g_copy(k):
        p=(dp+k)%nd
        return rcopy(gd.at[dp],gd.at[dp],gs.at[k],gr.at[k],(p,t))
    def g_arrive(k):
        q=(dp-k+nd)%nd
        return rcopy(gd.at[q],gd.at[q],gs.at[k],gr.at[k],(q,t))
    def t_copy(k):
        p=(t+k)%nt
        return rcopy(vt.at[t],vt.at[t],ts.at[k],tr.at[k],(dp,p))
    def t_arrive(k):
        q=(t-k+nt)%nt
        return rcopy(vt.at[q],vt.at[q],ts.at[k],tr.at[k],(dp,q))
    def d_copy(k):
        p=(dp+k)%nd
        return rcopy(vd.at[dp],vd.at[dp],ds.at[k],dr.at[k],(p,t))
    def d_arrive(k):
        q=(dp-k+nd)%nd
        return rcopy(vd.at[q],vd.at[q],ds.at[k],dr.at[k],(q,t))
    def loop(n,f):
        def s(k,_):
            f(k); return 0
        lax.fori_loop(1,n,s,0)
    vt[t]=v_ref[...]
    gd[dp]=g_ref[...]
    loop(nt,lambda k: t_copy(k).start())
    loop(nd,lambda k: g_copy(k).start())
    loop(nt,lambda k: t_arrive(k).wait_recv())
    acc=vt[0]
    for i in range(1,nt): acc=acc+vt[i]
    vd[dp]=acc
    loop(nd,lambda k: d_copy(k).start())
    loop(nd,lambda k: g_arrive(k).wait_recv())
    acc=gd[0]
    for i in range(1,nd): acc=acc+gd[i]
    go_ref[...]=acc
    loop(nd,lambda k: d_arrive(k).wait_recv())
    acc=vd[0]
    for i in range(1,nd): acc=acc+vd[i]
    vo_ref[...]=acc
    loop(nt,lambda k: t_copy(k).wait_send())
    loop(nd,lambda k: g_copy(k).wait_send())
    loop(nd,lambda k: d_copy(k).wait_send())

def totals(v,g,nd,nt):
    DS=pltpu.SemaphoreType.DMA
    vm=pl.BlockSpec(memory_space=pltpu.VMEM)
    return pl.pallas_call(totals_kernel,out_shape=[jax.ShapeDtypeStruct(v.shape,f32),jax.ShapeDtypeStruct(g.shape,f32)],in_specs=[vm]*2,out_specs=[vm]*2,
        scratch_shapes=[pltpu.VMEM((nt,)+v.shape,f32),pltpu.VMEM((nd,)+v.shape,f32),pltpu.VMEM((nd,)+g.shape,f32),DS((nt,)),DS((nt,)),DS((nd,)),DS((nd,)),DS((nd,)),DS((nd,))],
        compiler_params=pltpu.CompilerParams(has_side_effects=True,vmem_limit_bytes=16<<20),name="sum_small")(v,g)

def grad_sum_kernel(a_ref,o_ref,mine,xb0,yb0,zin,xb1,yb1,zin1,zin2,yb2,xb2,cs,cr,ss,rs,zs,zr,fs,fr):
    z,y,x,c=where_am_i()
    core=dev(z,y,x,1-c); across=dev(z,y,1-x,c); beside=dev(z,1-y,x,c)
    up=dev(jnp.minimum(z+1,3),y,x,c); down=dev(jnp.maximum(z-1,0),y,x,c)
    other=(1-c)*12; own=c*12
    def c_copy(p,d):
        return rcopy(a_ref.at[d,pl.ds(other+p*4,4)],mine.at[p,d],cs.at[p,d],cr.at[p,d],core)
    order=(2,0,1)
    def go(p):
        def s(d,_):
            c_copy(p,d).start(); return 0
        lax.fori_loop(0,8,s,0)
    for p in order: go(p)
    def add_own(p):
        def s(d,_):
            c_copy(p,d).wait_recv()
            for b in range(4):
                mine[p,d,b]=(mine[p,d,b].astype(f32)+a_ref[d,own+p*4+b].astype(f32)).astype(bf)
            return 0
        lax.fori_loop(0,8,s,0)
    def add(dst,src):
        n=dst.shape[0]
        for i in range(n): dst[i]=(dst[i].astype(f32)+src[i].astype(f32)).astype(bf)
    def line(buf_of,inbox,sem):
        def cp(tz,go_down):
            k=1 if go_down else 0
            return rcopy(buf_of(tz),inbox.at[k,tz],zs.at[sem,k,tz],zr.at[sem,k,tz],down if go_down else up)
        def arrive(tz,go_down):
            k=1 if go_down else 0
            return rcopy(inbox.at[k,tz],inbox.at[k,tz],zs.at[sem,k,tz],zr.at[sem,k,tz],down)
        return cp,arrive
    def line_start(cp):
        for tz in (0,1,2):
            @pl.when(z==3)
            def _(): cp(tz,True).start()
        for tz in (3,2,1):
            @pl.when(z==0)
            def _(): cp(tz,False).start()
    def line_pass(cp,arrive,buf_of,inbox,addf):
        for tz in (0,1,2):
            @pl.when(jnp.logical_and(z<3,z>tz))
            def _():
                arrive(tz,True).wait_recv(); addf(buf_of(tz),inbox.at[1,tz]); cp(tz,True).start()
            u=3-tz
            @pl.when(jnp.logical_and(z>0,z<u))
            def _():
                arrive(u,False).wait_recv(); addf(buf_of(u),inbox.at[0,u]); cp(u,False).start()
    def line_end(cp,arrive,buf_of,inbox,addf):
        @pl.when(z<3)
        def _():
            arrive(z,True).wait_recv(); addf(buf_of(z),inbox.at[1,z])
        @pl.when(z>0)
        def _():
            arrive(z,False).wait_recv(); addf(buf_of(z),inbox.at[0,z])
    def line_sent(cp):
        for tz in (0,1,2):
            @pl.when(z>tz)
            def _(): cp(tz,True).wait_send()
            @pl.when(z<3-tz)
            def _(): cp(3-tz,False).wait_send()
    def add2(dst,src):
        for i in range(2):
            for j in range(4): dst[i,j]=(dst[i,j].astype(f32)+src[i,j].astype(f32)).astype(bf)
    p2_of=lambda tz: mine.at[2,pl.ds(tz*2,2)]
    cp2,ar2=line(p2_of,zin,0)
    add_own(2); line_start(cp2)
    def x0(d): return rcopy(mine.at[0,d,pl.ds((1-x)*2,2)],xb0.at[d],ss.at[0,d],rs.at[0,d],across)
    def s0(d,_):
        c_copy(0,d).wait_recv()
        for b in range(4):
            mine[0,d,b]=(mine[0,d,b].astype(f32)+a_ref[d,own+b].astype(f32)).astype(bf)
        x0(d).start()
        return 0
    lax.fori_loop(0,8,s0,0)
    def y1(zz): return rcopy(mine.at[1,zz*2+1-y],yb0.at[zz],ss.at[1,zz],rs.at[1,zz],beside)
    add_own(1)
    for zz in range(4): y1(zz).start()
    line_pass(cp2,ar2,p2_of,zin,add2)
    def p0(zz,yy): return mine.at[0,zz*2+yy,pl.ds(x*2,2)]
    def y0(zz): return rcopy(p0(zz,1-y),yb1.at[zz],ss.at[2,zz],rs.at[2,zz],beside)
    for zz in range(4):
        for yy in range(2):
            d=zz*2+yy
            x0(d).wait_recv(); add(p0(zz,yy),xb0.at[d])
        y0(zz).start()
    def p1(zz): return mine.at[1,zz*2+y]
    def x1(zz): return rcopy(mine.at[1,zz*2+y,pl.ds((1-x)*2,2)],xb1.at[zz],ss.at[3,zz],rs.at[3,zz],across)
    for zz in range(4):
        y1(zz).wait_recv(); add(p1(zz),yb0.at[zz]); x1(zz).start()
    line_end(cp2,ar2,p2_of,zin,add2)
    y2=rcopy(mine.at[2,z*2+1-y],yb2,ss.at[4,0],rs.at[4,0],beside)
    y2.start()
    q0=lambda tz: mine.at[0,tz*2+y,pl.ds(x*2,2)]
    cp0,ar0=line(q0,zin1,1)
    for zz in range(4):
        y0(zz).wait_recv(); add(q0(zz),yb1.at[zz])
    line_start(cp0)
    q1=lambda tz: mine.at[1,tz*2+y,pl.ds(x*2,2)]
    cp1,ar1=line(q1,zin2,2)
    for zz in range(4):
        x1(zz).wait_recv(); add(q1(zz),xb1.at[zz])
    line_start(cp1)
    y2.wait_recv(); add(mine.at[2,z*2+y],yb2)
    x2=rcopy(mine.at[2,z*2+y,pl.ds((1-x)*2,2)],xb2,ss.at[5,0],rs.at[5,0],across)
    x2.start()
    line_pass(cp0,ar0,q0,zin1,add)
    line_pass(cp1,ar1,q1,zin2,add)
    x2.wait_recv()
    me=z*2+y
    add(mine.at[2,me,pl.ds(x*2,2)],xb2)
    def place(xx,cc,p): return o_ref.at[pl.ds(cc*12+p*4+xx*2,2)]
    def f_copy(i,p):
        if i==2: return rcopy(place(1-x,c,p),place(1-x,c,p),fs.at[2,p],fr.at[2,p],core)
        return rcopy(mine.at[p,me,pl.ds(x*2,2)],place(x,c,p),fs.at[i,p],fr.at[i,p],across if i==0 else core)
    def f_arrive(i,p):
        r=(place(1-x,c,p),place(x,1-c,p),place(1-x,1-c,p))[i]
        return rcopy(r,r,fs.at[i,p],fr.at[i,p],core)
    def finish(p):
        o_ref[pl.ds(own+p*4+x*2,2)]=mine[p,me,pl.ds(x*2,2)]
        for i in range(2): f_copy(i,p).start()
    finish(2)
    line_end(cp0,ar0,q0,zin1,add); finish(0)
    line_end(cp1,ar1,q1,zin2,add); finish(1)
    for p in (2,0,1):
        f_arrive(0,p).wait_recv(); f_copy(2,p).start()
    for p in range(3):
        f_arrive(1,p).wait_recv(); f_arrive(2,p).wait_recv()
    for p in range(3):
        for i in range(3): f_copy(i,p).wait_send()
    def drain(d,_):
        for p in range(3): c_copy(p,d).wait_send()
        x0(d).wait_send()
        return 0
    lax.fori_loop(0,8,drain,0)
    for zz in range(4):
        y1(zz).wait_send(); y0(zz).wait_send(); x1(zz).wait_send()
    y2.wait_send(); x2.wait_send()
    line_sent(cp2); line_sent(cp0); line_sent(cp1)

def grad_sum(a):
    DS=pltpu.SemaphoreType.DMA
    R=a.shape[2]
    vm=pl.BlockSpec(memory_space=pltpu.VMEM)
    V=lambda *s: pltpu.VMEM(s+(R,128),bf)
    return pl.pallas_call(grad_sum_kernel,out_shape=jax.ShapeDtypeStruct((24,R,128),bf),in_specs=[vm],out_specs=vm,
        scratch_shapes=[V(3,8,4),V(8,2),V(4,4),V(2,4,2,4),V(4,2),V(4,2),V(2,4,2),V(2,4,2),V(4),V(2),
            DS((3,8)),DS((3,8)),DS((6,8)),DS((6,8)),DS((3,2,4)),DS((3,2,4)),DS((3,3)),DS((3,3))],
        cost_estimate=pl.CostEstimate(flops=10**7,bytes_accessed=200*10**6,transcendentals=0),
        compiler_params=pltpu.CompilerParams(has_side_effects=True,vmem_limit_bytes=56<<20),name="sum_gradients")(a)


H = 12
NGRP = 16
STEP = 10
EPS_NORM = 1e-06
BETA_ONE = 0.5
BETA_TWO = 0.5
ADAM_EPS = 1e-08
RATE_BLOCK = 0.3
RATE_VECTOR = 0.2
NEG_RAW = -8.0e9
HEAD = 64
SCALE = 1.0 / math.sqrt(HEAD)
EXP2 = SCALE * math.log2(math.e)
NN = (((1,), (0,)), ((), ()))
NT = (((1,), (1,)), ((), ()))
TN = (((0,), (0,)), ((), ()))


def mm(a, b, dims=NN):
    return lax.dot_general(a, b, dims, preferred_element_type=f32)


def vmem_spec():
    return pl.BlockSpec(memory_space=pltpu.VMEM)


def smem_spec():
    return pl.BlockSpec(memory_space=pltpu.SMEM)


def any_spec():
    return pl.BlockSpec(memory_space=pl.ANY)


def params(mib=48):
    return pltpu.CompilerParams(vmem_limit_bytes=mib << 20)


def pack(block):
    half = block.shape[0] // 2
    return block[:, :128], jnp.concatenate([block[:half, 128:], block[half:, 128:]], axis=1)


def unpack(top, tail):
    return jnp.concatenate([top, jnp.concatenate([tail[:, :64], tail[:, 64:]], axis=0)], axis=1)


def group_of(n):
    return 4 if n % 4 == 0 else 3 if n % 3 == 0 else 1


def pack_kernel(m_ref, p_ref, s_ref):
    for b in range(m_ref.shape[0]):
        m = m_ref[b]
        top, tail = pack(m)
        p_ref[b, :192] = top.astype(bf)
        p_ref[b, 192:] = tail.astype(bf)
        s_ref[b] = jnp.full((8, 128), jnp.sum(m * m), f32)


def pack_master(master):
    n = master.shape[0]
    g = group_of(n)
    at = lambda i: (i, 0, 0)
    return pl.pallas_call(
        pack_kernel,
        grid=(n // g,),
        in_specs=[pl.BlockSpec((g, 192, 192), at)],
        out_specs=[pl.BlockSpec((g, 288, 128), at), pl.BlockSpec((g, 8, 128), at)],
        out_shape=[jax.ShapeDtypeStruct((n, 288, 128), bf), jax.ShapeDtypeStruct((n, 8, 128), f32)],
        name="pack_master",
    )(master)


def assemble_kernel(inv_ref, tile_ref, w_ref, qkv_ref, out_ref, up_ref, down_ref, buf, sems):
    t = tile_ref[0]
    def where(i):
        own = (i // 3) * 12 + (i % 3) * 4 + t
        return inv_ref[jnp.where(i < 12, own, i + 36)]

    def copy(i):
        return pltpu.make_async_copy(w_ref.at[where(i)], buf.at[i], sems.at[i])

    def start(i, _):
        copy(i).start()
        return 0

    lax.fori_loop(0, 156, start, 0)

    def block(i):
        copy(i).wait()
        return unpack(buf[i, :192], buf[i, 192:])

    for r in range(4):
        qkv_ref[r * 192 : (r + 1) * 192, :] = jnp.concatenate([block(r * 3 + k) for k in range(3)], axis=1)

    def place(dst, first, pairs):
        def body(j, _):
            i = first + 2 * j
            r = pl.multiple_of((j // pairs) * 192, 64)
            col = pl.multiple_of((j % pairs) * 384, 128)
            dst[pl.ds(r, 192), pl.ds(col, 384)] = jnp.concatenate([block(i), block(i + 1)], axis=1)
            return 0

        return body

    lax.fori_loop(0, 8, place(out_ref, 12, 2), 0)
    lax.fori_loop(0, 32, place(up_ref, 28, 8), 0)
    lax.fori_loop(0, 32, place(down_ref, 92, 2), 0)


def assemble(inv, tile, w):
    shapes = [(768, 576), (768, 768), (768, 3072), (3072, 768)]
    return pl.pallas_call(
        assemble_kernel,
        in_specs=[smem_spec(), smem_spec(), any_spec()],
        out_specs=[vmem_spec()] * 4,
        out_shape=[jax.ShapeDtypeStruct(s, bf) for s in shapes],
        scratch_shapes=[pltpu.VMEM((156, 288, 128), bf), pltpu.SemaphoreType.DMA((156,))],
        compiler_params=params(40),
        name="assemble_weights",
    )(inv, tile, w)


def qkv_kernel(src_ref, cnt_ref, x0, x1, x2, x3, w_ref, gain_ref, shift_ref, bq_ref, bv_ref, a_ref, q_ref, qt_ref, k_ref, kt_ref, v_ref, vt_ref):
    i = pl.program_id(0)
    x = jnp.concatenate([r[...] for r in (x0, x1, x2, x3)], axis=0).astype(f32)
    mean = jnp.mean(x, axis=-1, keepdims=True)
    cen = x - mean
    inv_std = lax.rsqrt(jnp.mean(cen * cen, axis=-1, keepdims=True) + EPS_NORM)
    a = (cen * inv_std * gain_ref[...] + shift_ref[...]).astype(bf)
    a_ref[...] = a
    qkv = mm(a, w_ref[...])
    q = (qkv[:, :192] + bq_ref[...]).astype(bf).astype(f32)
    k = qkv[:, 192:384].astype(bf).astype(f32)
    v = (qkv[:, 384:] + bv_ref[...]).astype(bf).astype(f32)
    row = lax.broadcasted_iota(jnp.int32, (128, 64), 0)
    lane = lax.broadcasted_iota(jnp.int32, (512, 64), 1)
    masked = jnp.concatenate(
        [jnp.where(row < cnt_ref[4 * i + b], 0.0, NEG_RAW) for b in range(4)], axis=0
    )
    ones = jnp.where(lane < 4, 1.0, 0.0)
    k_tail = jnp.where(lane == 0, masked, ones)
    v_tail = jnp.where(lane < 3, 1.0, 0.0)
    zero = jnp.zeros((512, 64), f32)
    sub = lax.broadcasted_iota(jnp.int32, (64, 512), 0)
    t_tail = jnp.where(sub < 1, 1.0, 0.0)
    qt, kt, vt = q.T, k.T, v.T
    for h in range(3):
        s = slice(h * 64, (h + 1) * 64)
        q_ref[h] = jnp.concatenate([q[:, s], zero], axis=1).astype(bf)
        k_ref[h] = jnp.concatenate([k[:, s], k_tail], axis=1).astype(bf)
        v_ref[h] = jnp.concatenate([v[:, s], v_tail], axis=1).astype(bf)
        qt_ref[h] = jnp.concatenate([qt[s], t_tail], axis=0).astype(bf)
        kt_ref[h] = kt[s].astype(bf)
        vt_ref[h] = jnp.concatenate([vt[s], t_tail[:16]], axis=0).astype(bf)


def qkv_forward(src, cnt, tokens, w, gain, shift, bq, bv):
    n = tokens.shape[0]
    rows = [pl.BlockSpec((128, 768), lambda i, s, c, k=k: (s[4 * i + k], 0)) for k in range(4)]
    row = lambda i, s, c: (0, 0)
    spec = pltpu.PrefetchScalarGridSpec(
        num_scalar_prefetch=2,
        grid=(n // 512,),
        in_specs=rows
        + [pl.BlockSpec((768, 576), row), pl.BlockSpec((1, 768), row), pl.BlockSpec((1, 768), row), pl.BlockSpec((1, 192), row), pl.BlockSpec((1, 192), row)],
        out_specs=[
            pl.BlockSpec((512, 768), lambda i, s, c: (i, 0)),
            pl.BlockSpec((3, 512, 128), lambda i, s, c: (0, i, 0)),
            pl.BlockSpec((3, 128, 512), lambda i, s, c: (0, 0, i)),
            pl.BlockSpec((3, 512, 128), lambda i, s, c: (0, i, 0)),
            pl.BlockSpec((3, 64, 512), lambda i, s, c: (0, 0, i)),
            pl.BlockSpec((3, 512, 128), lambda i, s, c: (0, i, 0)),
            pl.BlockSpec((3, 80, 512), lambda i, s, c: (0, 0, i)),
        ],
    )
    shapes = [(n, 768), (3, n, 128), (3, 128, n), (3, n, 128), (3, 64, n), (3, n, 128), (3, 80, n)]
    return pl.pallas_call(
        qkv_kernel,
        grid_spec=spec,
        out_shape=[jax.ShapeDtypeStruct(s, bf) for s in shapes],
        compiler_params=params(40),
        name="norm_and_qkv",
    )(src, cnt, tokens, tokens, tokens, tokens, w, gain, shift, bq, bv)


def split3(v):
    a = v.astype(bf).astype(f32)
    b = (v - a).astype(bf).astype(f32)
    return a, b, v - a - b


def attend_kernel(bq, n_ref, k_ref, qt_ref, vt_ref, ot_ref, qb_ref):
    live = n_ref[0]
    qi = pl.program_id(1)

    @pl.when(qi * bq < live * 128)
    def _():
        qt = qt_ref[0]

        def block(start, size, carry):
            top, acc = carry
            s = mm(k_ref[0, pl.ds(start, size), :], qt) * EXP2
            new = jnp.maximum(top, jnp.max(s, axis=0, keepdims=True))
            p = jnp.exp2(s - new).astype(bf)
            acc = acc * jnp.exp2(top - new) + mm(vt_ref[0, :, pl.ds(start, size)], p)
            return new, acc

        def step(j, carry):
            return block(pl.multiple_of(j * 1024, 1024), 1024, carry)

        def rest(j, carry):
            return block(pl.multiple_of(j * 256, 256), 256, carry)

        pairs = (live + 1) // 2
        carry = (jnp.full((1, bq), -3e38, f32), jnp.zeros((80, bq), f32))
        carry = lax.fori_loop(0, pairs // 4, step, carry)
        top, acc = lax.fori_loop((pairs // 4) * 4, pairs, rest, carry)
        total = acc[64:65]
        ot_ref[0] = acc[:64] / total
        a, b, c = split3((top + jnp.log2(total)) * (-1.0 / EXP2))
        row = lax.broadcasted_iota(jnp.int32, (64, bq), 0)
        tail = jnp.where(row == 0, 1.0, jnp.where(row == 1, a, jnp.where(row == 2, b, jnp.where(row == 3, c, 0.0))))
        qb_ref[0, :64] = qt[:64]
        qb_ref[0, 64:] = tail.astype(bf)


def attend(live, k, qt, vt, bq=1024):
    n = k.shape[1]
    spec = pltpu.PrefetchScalarGridSpec(
        num_scalar_prefetch=1,
        grid=(3, n // bq),
        in_specs=[
            pl.BlockSpec((1, n, 128), lambda h, i, s: (h, 0, 0)),
            pl.BlockSpec((1, 128, bq), lambda h, i, s: (h, 0, i)),
            pl.BlockSpec((1, 80, n), lambda h, i, s: (h, 0, 0)),
        ],
        out_specs=[pl.BlockSpec((1, 64, bq), lambda h, i, s: (h, 0, i)), pl.BlockSpec((1, 128, bq), lambda h, i, s: (h, 0, i))],
    )
    return pl.pallas_call(
        functools.partial(attend_kernel, bq),
        grid_spec=spec,
        out_shape=[jax.ShapeDtypeStruct((3, 64, n), f32), jax.ShapeDtypeStruct((3, 128, n), bf)],
        compiler_params=params(48),
        name="attention_forward",
    )(live, k, qt, vt)


def spread_kernel(src_ref, n_ref, ot_ref, o_ref):
    live = n_ref[0]
    per = o_ref.shape[2] // 128

    def step(b, _):
        g = src_ref[b]
        lanes = pl.ds(pl.multiple_of(b * 128, 128), 128)
        to = pl.ds(pl.multiple_of((g % per) * 128, 128), 128)

        @pl.when(b < live)
        def _():
            for h in range(3):
                o_ref[g // per, h * 64 : (h + 1) * 64, to] = ot_ref[h, :, lanes].astype(bf)

        @pl.when(b >= live)
        def _():
            o_ref[g // per, :, to] = jnp.zeros((192, 128), bf)

        return 0

    lax.fori_loop(0, ot_ref.shape[2] // 128, step, 0)


def spread(src, live, ot, tiles):
    n = ot.shape[2]
    return pl.pallas_call(
        spread_kernel,
        in_specs=[smem_spec(), smem_spec(), vmem_spec()],
        out_specs=vmem_spec(),
        out_shape=jax.ShapeDtypeStruct((tiles, 192, n // tiles), bf),
        compiler_params=params(24),
        name="spread_attended",
    )(src, live, ot)


def collect_kernel(src_ref, n_ref, g_ref, ot_ref, dt_ref, d_ref):
    live = n_ref[0]
    per = g_ref.shape[2] // 128
    row = lax.broadcasted_iota(jnp.int32, (64, 128), 0)

    def step(b, _):
        g = src_ref[b]
        to = pl.ds(pl.multiple_of(b * 128, 128), 128)
        lanes = pl.ds(pl.multiple_of((g % per) * 128, 128), 128)

        @pl.when(b < live)
        def _():
            for h in range(3):
                d = g_ref[g // per, h * 64 : (h + 1) * 64, lanes].astype(f32)
                delta = jnp.sum(d * ot_ref[h, :, to], axis=0, keepdims=True)
                x, y, z = split3(-delta)
                tail = jnp.where(row == 0, x, jnp.where(row == 1, y, jnp.where(row == 2, z, 0.0)))
                both = jnp.concatenate([d, tail], axis=0)
                dt_ref[h, :, to] = both.astype(bf)
                d_ref[h, to, :] = jnp.concatenate([d, jnp.zeros_like(d)], axis=0).T.astype(bf)

        @pl.when(b >= live)
        def _():
            dt_ref[:, :, to] = jnp.zeros((3, 128, 128), bf)
            d_ref[:, to, :] = jnp.zeros((3, 128, 128), bf)

        return 0

    lax.fori_loop(0, ot_ref.shape[2] // 128, step, 0)


def collect(src, live, grad, ot):
    n = ot.shape[2]
    return pl.pallas_call(
        collect_kernel,
        in_specs=[smem_spec(), smem_spec(), vmem_spec(), vmem_spec()],
        out_specs=[vmem_spec()] * 2,
        out_shape=[jax.ShapeDtypeStruct((3, 128, n), bf), jax.ShapeDtypeStruct((3, n, 128), bf)],
        compiler_params=params(32),
        name="collect_attended_grad",
    )(src, live, grad, ot)


def attend_back_kernel(bq, bk, n_ref, k_ref, kt_ref, v_ref, qb_ref, q_ref, dt_ref, d_ref, dq_ref, dk_ref, dv_ref):
    live = n_ref[0]
    j = pl.program_id(1)

    @pl.when(j == 0)
    def _():
        dq_ref[...] = jnp.zeros_like(dq_ref)

    @pl.when(j * bk < live * 128)
    def _():
        k, v, kt = k_ref[0], v_ref[0], kt_ref[0]

        def block(start, size, carry):
            dk, dv = carry
            lanes = pl.ds(start, size)
            p = jnp.exp2(mm(k, qb_ref[0, :, lanes]) * EXP2)
            ds = (p * mm(v, dt_ref[0, :, lanes])).astype(bf)
            dv = dv + mm(p.astype(bf), d_ref[0, lanes, :])
            dk = dk + mm(ds, q_ref[0, lanes, :])
            dq_ref[0, :, lanes] += mm(kt, ds)
            return dk, dv

        def step(i, carry):
            return block(pl.multiple_of(i * bq, bq), bq, carry)

        def rest(i, carry):
            return block(pl.multiple_of(i * 256, 256), 256, carry)

        pairs = (live + 1) // 2
        full = pairs * 256 // bq
        zero = jnp.zeros((bk, 128), f32)
        carry = lax.fori_loop(0, full, step, (zero, zero))
        dk, dv = lax.fori_loop(full * bq // 256, pairs, rest, carry)
        dk_ref[0] = (dk * SCALE).astype(bf)
        dv_ref[0] = dv.astype(bf)


def attend_back(live, k, kt, v, qb, q, dt, d, bq=1024, bk=512):
    n = k.shape[1]
    whole_t = lambda h, j, s: (h, 0, 0)
    spec = pltpu.PrefetchScalarGridSpec(
        num_scalar_prefetch=1,
        grid=(3, n // bk),
        in_specs=[
            pl.BlockSpec((1, bk, 128), lambda h, j, s: (h, j, 0)),
            pl.BlockSpec((1, 64, bk), lambda h, j, s: (h, 0, j)),
            pl.BlockSpec((1, bk, 128), lambda h, j, s: (h, j, 0)),
            pl.BlockSpec((1, 128, n), whole_t),
            pl.BlockSpec((1, n, 128), whole_t),
            pl.BlockSpec((1, 128, n), whole_t),
            pl.BlockSpec((1, n, 128), whole_t),
        ],
        out_specs=[
            pl.BlockSpec((1, 64, n), whole_t),
            pl.BlockSpec((1, bk, 128), lambda h, j, s: (h, j, 0)),
            pl.BlockSpec((1, bk, 128), lambda h, j, s: (h, j, 0)),
        ],
    )
    return pl.pallas_call(
        functools.partial(attend_back_kernel, bq, bk),
        grid_spec=spec,
        out_shape=[jax.ShapeDtypeStruct((3, 64, n), f32), jax.ShapeDtypeStruct((3, n, 128), bf), jax.ShapeDtypeStruct((3, n, 128), bf)],
        compiler_params=params(48),
        name="attention_backward",
    )(live, k, kt, v, qb, q, dt, d)


def qkv_back_kernel(src_ref, n_ref, dq_ref, dk_ref, dv_ref, a_ref, w_ref, g_ref, gw_ref, gb_ref, acc, sums, rows, sems):
    i = pl.program_id(0)
    live = n_ref[0]

    @pl.when(i == 0)
    def _():
        acc[...] = jnp.zeros_like(acc)
        sums[...] = jnp.zeros_like(sums)

    @pl.when(4 * i < live)
    def _():
        dq = jnp.concatenate([dq_ref[h] for h in range(3)], axis=0).T * SCALE
        g = jnp.concatenate(
            [dq] + [dk_ref[h][:, :64].astype(f32) for h in range(3)] + [dv_ref[h][:, :64].astype(f32) for h in range(3)], axis=1
        ).astype(bf)
        acc[...] += mm(a_ref[...], g, TN)
        sums[...] += jnp.broadcast_to(jnp.sum(g.astype(f32), axis=0, keepdims=True), sums.shape)
        rows[...] = mm(g, w_ref[...], NT).astype(bf)

    @pl.when(4 * i >= live)
    def _():
        rows[...] = jnp.zeros_like(rows)

    copies = [
        pltpu.make_async_copy(rows.at[pl.ds(b * 128, 128)], g_ref.at[pl.ds(pl.multiple_of(src_ref[4 * i + b] * 128, 128), 128)], sems.at[b])
        for b in range(4)
    ]
    for copy in copies:
        copy.start()
    for copy in copies:
        copy.wait()

    @pl.when(i == pl.num_programs(0) - 1)
    def _():
        for r in range(4):
            for c in range(3):
                top, tail = pack(acc[r * 192 : (r + 1) * 192, c * 192 : (c + 1) * 192])
                gw_ref[r * 3 + c, :192] = top.astype(bf)
                gw_ref[r * 3 + c, 192:] = tail.astype(bf)
        gb_ref[...] = sums[...]


def qkv_backward(src, live, dq, dk, dv, a, w):
    n = a.shape[0]
    spec = pltpu.PrefetchScalarGridSpec(
        num_scalar_prefetch=2,
        grid=(n // 512,),
        in_specs=[
            pl.BlockSpec((3, 64, 512), lambda i, s, c: (0, 0, i)),
            pl.BlockSpec((3, 512, 128), lambda i, s, c: (0, i, 0)),
            pl.BlockSpec((3, 512, 128), lambda i, s, c: (0, i, 0)),
            pl.BlockSpec((512, 768), lambda i, s, c: (i, 0)),
            pl.BlockSpec((768, 576), lambda i, s, c: (0, 0)),
        ],
        out_specs=[any_spec(), pl.BlockSpec((12, 288, 128), lambda i, s, c: (0, 0, 0)), pl.BlockSpec((8, 576), lambda i, s, c: (0, 0))],
        scratch_shapes=[pltpu.VMEM((768, 576), f32), pltpu.VMEM((8, 576), f32), pltpu.VMEM((512, 768), bf), pltpu.SemaphoreType.DMA((4,))],
    )
    return pl.pallas_call(
        qkv_back_kernel,
        grid_spec=spec,
        out_shape=[jax.ShapeDtypeStruct((n, 768), bf), jax.ShapeDtypeStruct((12, 288, 128), bf), jax.ShapeDtypeStruct((8, 576), f32)],
        compiler_params=params(32),
        name="qkv_backward",
    )(src, live, dq, dk, dv, a, w)


def slots_kernel(inv_ref, tile_ref, qkv_ref, out_ref, up_ref, down_ref, s_ref):
    t = tile_ref[0]

    def clear(c, _):
        s_ref[inv_ref[c]] = jnp.zeros((288, 128), bf)
        return 0

    lax.fori_loop(0, 48, clear, 0)

    def own(i, _):
        s_ref[inv_ref[(i // 3) * 12 + (i % 3) * 4 + t]] = qkv_ref[i]
        return 0

    lax.fori_loop(0, 12, own, 0)

    def put(src, first, pairs):
        def body(j, _):
            r = pl.multiple_of((j // pairs) * 192, 64)
            col = pl.multiple_of((j % pairs) * 384, 128)
            two = src[pl.ds(r, 192), pl.ds(col, 384)]
            for b in range(2):
                top, tail = pack(two[:, b * 192 : (b + 1) * 192])
                slot = inv_ref[first + 2 * j + b]
                s_ref[slot, :192] = top.astype(bf)
                s_ref[slot, 192:] = tail.astype(bf)
            return 0

        return body

    lax.fori_loop(0, 8, put(out_ref, 48, 2), 0)
    lax.fori_loop(0, 32, put(up_ref, 64, 8), 0)
    lax.fori_loop(0, 32, put(down_ref, 128, 2), 0)


def to_slots(inv, tile, gqkv, gout, gup, gdown):
    return pl.pallas_call(
        slots_kernel,
        in_specs=[smem_spec(), smem_spec()] + [vmem_spec()] * 4,
        out_specs=vmem_spec(),
        out_shape=jax.ShapeDtypeStruct((192, 288, 128), bf),
        compiler_params=params(48),
        name="gradients_to_slots",
    )(inv, tile, gqkv, gout, gup, gdown)


def split2(v):
    hi = v.astype(bf)
    return hi, (v - hi.astype(f32)).astype(bf)


def mm3(a, b, dims):
    return mm(a[0], b[0], dims) + (mm(a[0], b[1], dims) + mm(a[1], b[0], dims))


def adam_kernel(g_ref, m1_ref, m2_ref, l_ref, r_ref, g_out, m1_out, m2_out, u_out, s_out):
    for b in range(g_ref.shape[0]):
        grad = unpack(g_ref[b, :192].astype(f32), g_ref[b, 192:].astype(f32))
        left, right = split2(l_ref[b]), split2(r_ref[b])
        low = grad.astype(bf)
        rot = mm3(split2(mm(left[0], low, TN) + mm(left[1], low, TN)), right, NN)
        first = BETA_ONE * m1_ref[b] + (1.0 - BETA_ONE) * rot
        second = BETA_TWO * m2_ref[b] + (1.0 - BETA_TWO) * rot * rot
        upd = (first / (1.0 - BETA_ONE**STEP)) / (jnp.sqrt(second / (1.0 - BETA_TWO**STEP)) + ADAM_EPS)
        upd = mm3(split2(mm3(left, split2(upd), NN)), right, NT)
        g_out[b] = grad
        m1_out[b] = first
        m2_out[b] = second
        u_out[b] = upd
        s_out[b] = jnp.full((8, 128), jnp.sum(upd * upd), f32)


def adam(grads, first, second, left, right):
    n = grads.shape[0]
    g = group_of(n)
    at = lambda i: (i, 0, 0)
    big = pl.BlockSpec((g, 192, 192), at)
    return pl.pallas_call(
        adam_kernel,
        grid=(n // g,),
        in_specs=[pl.BlockSpec((g, 288, 128), at)] + [big] * 4,
        out_specs=[big] * 4 + [pl.BlockSpec((g, 8, 128), at)],
        out_shape=[jax.ShapeDtypeStruct((n, 192, 192), f32)] * 4 + [jax.ShapeDtypeStruct((n, 8, 128), f32)],
        compiler_params=params(40),
        name="rotated_adam",
    )(grads, first, second, left, right)


def norm_forward(row_data, gain_vec, shift_vec):
    row_mean = jnp.mean(row_data, axis=-1, keepdims=True)
    centred = row_data - row_mean
    inv_std = lax.rsqrt(jnp.mean(centred * centred, axis=-1, keepdims=True) + EPS_NORM)
    normed = centred * inv_std
    return (normed * gain_vec + shift_vec, normed, inv_std)


def norm_back(grad_out, normed, inv_std, gain_vec):
    grad_normed = grad_out * gain_vec
    return inv_std * (
        grad_normed
        - jnp.mean(grad_normed, axis=-1, keepdims=True)
        - normed * jnp.mean(grad_normed * normed, axis=-1, keepdims=True)
    )


def middle(row_input, cotangent, live_rows, o_t, w_out, w_up, w_down, vec_params):
    bias_up = vec_params[8:].reshape(-1)
    residual = row_input + mm(o_t, w_out, TN) + vec_params[6]
    normed_mid, normed_two, inv_std_two = norm_forward(residual, vec_params[2], vec_params[3])
    act_two = normed_mid.astype(bf)
    pre_act = mm(act_two, w_up) + bias_up
    hidden_f, gelu_pull = jax.vjp(lambda v: jax.nn.gelu(v, approximate=False), pre_act)
    hidden = hidden_f.astype(bf)
    output = (live_rows * (residual + mm(hidden, w_down) + vec_params[7])).astype(bf)
    grad_y = cotangent * live_rows
    gm = grad_y.astype(bf)
    grad_down = mm(hidden, gm, TN).astype(bf)
    grad_pre = gelu_pull(mm(gm, w_down, NT))[0].astype(bf)
    grad_up = mm(act_two, grad_pre, TN).astype(bf)
    grad_mid = mm(grad_pre, w_up, NT)
    grad_resid = grad_y + norm_back(grad_mid, normed_two, inv_std_two, vec_params[2])
    gb = grad_resid.astype(bf)
    grad_out = mm(o_t, gb).astype(bf)
    go_t = mm(w_out, gb, NT).astype(bf)
    sums = [
        jnp.sum(grad_mid * normed_two, axis=0),
        jnp.sum(grad_mid, axis=0),
        jnp.sum(gb.astype(f32), axis=0),
        jnp.sum(gm.astype(f32), axis=0),
        jnp.sum(grad_pre.astype(f32), axis=0).reshape(-1, row_input.shape[1]),
    ]
    return output, grad_resid, go_t, grad_out, grad_up, grad_down, sums


def block_plan(counts, slot_count):
    tiles = counts.shape[0]
    per = slot_count // 128
    j = lax.broadcasted_iota(jnp.int32, (tiles, per), 1)
    kept = jnp.clip(counts[:, None] - j * 128, 0, 128).reshape(-1)
    full = (kept > 0).astype(jnp.int32)
    index = jnp.arange(tiles * per, dtype=jnp.int32)
    before = (index[None, :] < index[:, None]).astype(jnp.int32)
    ahead = jnp.sum(before * full[None, :], axis=1)
    live = jnp.sum(full)
    place = jnp.where(full > 0, ahead, live + index - ahead)
    hot = (place[None, :] == index[:, None]).astype(jnp.int32)
    return jnp.sum(hot * index[None, :], axis=1), jnp.sum(hot * kept[None, :], axis=1), live.reshape(1)


def make_body(tuned):
    def body(tokens, cotangent, counts, master, slot_block, groups, first_moment, second_moment, left_basis, right_basis, vec_params, vec_first, vec_second):
        slot_count, width = tokens.shape[1:]
        per_owner = master.shape[0]
        tile = lax.axis_index("tile")
        packed, weight_sq = pack_master(master)
        own_tokens = tokens.reshape(slot_count, width)
        count_tile = jnp.broadcast_to(counts.reshape(1, 1), (8, 128))
        if tuned:
            blocks, token_all, count_all = gather_all(packed, own_tokens, count_tile)
        else:
            blocks = lax.all_gather(packed, "dp", axis=0, tiled=True)
            token_all = lax.all_gather(own_tokens, "tile", axis=0)
            count_all = lax.all_gather(count_tile, "tile", axis=0)
        tiles = token_all.shape[0]
        block_count = blocks.shape[0]
        src, cnt, live = block_plan(count_all[:, 0, 0], slot_count)
        index = jnp.arange(block_count, dtype=jnp.int32)
        inverse = jnp.sum((slot_block[None, :] == index[:, None]).astype(jnp.int32) * index[None, :], axis=1)
        tile_one = tile.astype(jnp.int32).reshape(1)
        w_qkv, w_out, w_up, w_down = assemble(inverse, tile_one, blocks)
        own = width // tiles
        bias = lambda row: lax.dynamic_slice(vec_params[row : row + 1], (0, tile * own), (1, own))
        a1, q, qt, k, kt, v, vt = qkv_forward(
            src, cnt, token_all.reshape(-1, width), w_qkv, vec_params[0:1], vec_params[1:2], bias(4), bias(5)
        )
        ot, qb = attend(live, k, qt, vt)
        o_t = exchange(spread(src, live, ot, tiles)).reshape(width, slot_count)

        row_input = own_tokens.astype(f32)
        slot_index = lax.broadcasted_iota(jnp.int32, (slot_count, 1), 0)
        live_rows = (slot_index < counts[0, 0]).astype(f32)
        output, grad_resid, go_t, grad_out, grad_up, grad_down, sums = middle(
            row_input, cotangent.reshape(slot_count, width).astype(f32), live_rows, o_t, w_out, w_up, w_down, vec_params
        )
        go = exchange(go_t.reshape(tiles, own, slot_count))
        dt, d = collect(src, live, go, ot)
        dq, dk, dv = attend_back(live, k, kt, v, qb, q, dt, d)
        g_part, gw_qkv, qkv_sums = qkv_backward(src, live, dq, dk, dv, a1, w_qkv)
        g_part = g_part.reshape(tiles, slot_count, width)
        slot_grads = to_slots(inverse, tile_one, gw_qkv, grad_out, grad_up, grad_down)
        if tuned:
            g1 = lax.psum_scatter(g_part, "tile", scatter_dimension=0, tiled=False).astype(f32)
            grads = grad_sum(slot_grads.reshape(-1, per_owner, 288, 128))
        else:
            g1 = lax.psum_scatter(g_part.astype(f32), "tile", scatter_dimension=0, tiled=False)
            grads = lax.psum(lax.psum_scatter(slot_grads.astype(f32), "dp", scatter_dimension=0, tiled=True), "tile").astype(bf)
        _, normed_one, inv_std_one = norm_forward(row_input, vec_params[0], vec_params[1])
        input_grad = grad_resid + norm_back(g1, normed_one, inv_std_one, vec_params[0])
        zero = jnp.zeros((width,), f32)
        at_own = lambda s: lax.dynamic_update_slice(zero, s, (tile * own,))
        rows = jnp.stack(
            [jnp.sum(g1 * normed_one, axis=0), jnp.sum(g1, axis=0), sums[0], sums[1], at_own(qkv_sums[0, :own]), at_own(qkv_sums[0, 2 * own :]), sums[2], sums[3]],
            axis=0,
        )
        vector_part = jnp.concatenate([rows, sums[4]], axis=0)

        weight_grads, first_out, second_out, update, update_sq = adam(grads, first_moment, second_moment, left_basis, right_basis)
        group_hot = (groups[:, None] == jnp.arange(NGRP, dtype=jnp.int32)[None, :]).astype(f32)
        both = jnp.stack([weight_sq[:, 0, 0], update_sq[:, 0, 0]], axis=0)
        group_part = jnp.pad(jnp.sum(group_hot[None] * both[:, :, None], axis=1), ((0, 6), (0, 128 - NGRP)))
        vector_grads, group_both = totals(vector_part, group_part, block_count // per_owner, tiles)
        own_both = jnp.sum(group_hot[None] * group_both[:2, None, :NGRP], axis=2)
        block_rate = RATE_BLOCK * jnp.sqrt(own_both[0]) / (jnp.sqrt(own_both[1]) + 1e-06)
        master_out = master - block_rate[:, None, None] * update
        vec_first_out = BETA_ONE * vec_first + (1.0 - BETA_ONE) * vector_grads
        vec_second_out = BETA_TWO * vec_second + (1.0 - BETA_TWO) * vector_grads * vector_grads
        vec_update = (vec_first_out / (1.0 - BETA_ONE**STEP)) / (jnp.sqrt(vec_second_out / (1.0 - BETA_TWO**STEP)) + ADAM_EPS)
        return (
            output.reshape(1, slot_count, width),
            input_grad.reshape(1, slot_count, width),
            weight_grads,
            first_out,
            second_out,
            master_out,
            master_out.astype(bf),
            vector_grads,
            vec_first_out,
            vec_second_out,
            vec_params - RATE_VECTOR * vec_update,
        )

    return body


def solution(mesh):
    tuned = (mesh.shape["dp"], mesh.shape["tile"]) == (8, 4)
    rows, blocks = P("dp", "tile", None), P("dp", None, None)
    return jax.shard_map(
        make_body(tuned),
        mesh=mesh,
        in_specs=(rows, rows, P("dp", "tile"), blocks, P(), P("dp"), blocks, blocks, blocks, blocks, P(), P(), P()),
        out_specs=(rows, rows, blocks, blocks, blocks, blocks, blocks, P(), P(), P(), P()),
        check_vma=False,
    )
```

```python
import functools
import math

import jax
import jax.numpy as jnp
from jax import lax
from jax.experimental import pallas as pl
from jax.experimental.pallas import tpu as pltpu
from jax.sharding import PartitionSpec as P

f32 = jnp.float32
bf = jnp.bfloat16
MESH = pl.DeviceIdType.MESH

def where_am_i():
    dp=lax.axis_index("dp"); t=lax.axis_index("tile")
    return dp//2, dp%2, t//2, t%2

def dev(z,y,x,c):
    return (z*2+y, x*2+c)

def rcopy(src,dst,ss,rs,to):
    return pltpu.make_async_remote_copy(src_ref=src,dst_ref=dst,send_sem=ss,recv_sem=rs,device_id=to,device_id_type=MESH)

def gather_kernel(own_w,own_tok,own_cnt,all_w,all_tok,all_cnt,
                  zs,zr,ys,yr,xs,xr,cs,cr,fs,fr,ts,tr,ns,nr,ls):
    z,y,x,c=where_am_i()
    per=own_w.shape[0]
    part=per//12
    def a_of(shard,xx,cc): return all_w.at[pl.ds(shard*per+(xx*2+cc)*part,part)]
    def b_of(shard,cc): return all_w.at[pl.ds(shard*per+4*part+cc*4*part,4*part)]
    own_a=own_w.at[pl.ds((x*2+c)*part,part)]
    own_b=own_w.at[pl.ds(4*part+c*4*part,4*part)]
    me=z*2+y
    core=dev(z,y,x,1-c); across=dev(z,y,1-x,c); beside=dev(z,1-y,x,c)
    up=dev(jnp.minimum(z+1,3),y,x,c); down=dev(jnp.maximum(z-1,0),y,x,c)
    def src(shard,own):
        return (own_a,own_b) if own else (a_of(shard,x,c),b_of(shard,c))
    def z_copies(zz,own,go_up):
        shard=zz*2+y
        a,b=src(shard,own)
        d=(z-zz) if go_up else (zz-z)
        k=0 if go_up else 1
        to=up if go_up else down
        return (rcopy(a,a_of(shard,x,c),zs.at[k,d,0],zr.at[k,d,0],to),rcopy(b,b_of(shard,c),zs.at[k,d,1],zr.at[k,d,1],to))
    def z_arrivals(zz,k,dist):
        shard=zz*2+y
        a,b=a_of(shard,x,c),b_of(shard,c)
        return (rcopy(a,a,zs.at[k,dist-1,0],zr.at[k,dist-1,0],up),rcopy(b,b,zs.at[k,dist-1,1],zr.at[k,dist-1,1],up))
    def y_copies(zz,own):
        shard=zz*2+y
        a,b=src(shard,own)
        return (rcopy(a,a_of(shard,x,c),ys.at[zz,0],yr.at[zz,0],beside),rcopy(b,b_of(shard,c),ys.at[zz,1],yr.at[zz,1],beside))
    def y_arrivals(zz):
        shard=zz*2+(1-y)
        a,b=a_of(shard,x,c),b_of(shard,c)
        return (rcopy(a,a,ys.at[zz,0],yr.at[zz,0],beside),rcopy(b,b,ys.at[zz,1],yr.at[zz,1],beside))
    def x_copy(shard,own):
        return rcopy(src(shard,own)[0],a_of(shard,x,c),xs.at[shard],xr.at[shard],across)
    def x_arrival(shard):
        a=a_of(shard,1-x,c)
        return rcopy(a,a,xs.at[shard],xr.at[shard],across)
    def c_copies(shard,own):
        a,b=src(shard,own)
        return (rcopy(a,a_of(shard,x,c),cs.at[shard,0],cr.at[shard,0],core),rcopy(b,b_of(shard,c),cs.at[shard,1],cr.at[shard,1],core))
    def c_arrivals(shard):
        a,b=a_of(shard,x,1-c),b_of(shard,1-c)
        return (rcopy(a,a,cs.at[shard,0],cr.at[shard,0],core),rcopy(b,b,cs.at[shard,1],cr.at[shard,1],core))
    def f_copy(shard):
        a=a_of(shard,1-x,c)
        return rcopy(a,a,fs.at[shard],fr.at[shard],core)
    def f_arrival(shard):
        a=a_of(shard,1-x,1-c)
        return rcopy(a,a,fs.at[shard],fr.at[shard],core)
    def start(cps):
        for cp in (cps if isinstance(cps,tuple) else (cps,)): cp.start()
    def got(cps):
        for cp in (cps if isinstance(cps,tuple) else (cps,)): cp.wait_recv()
    def sent(cps):
        for cp in (cps if isinstance(cps,tuple) else (cps,)): cp.wait_send()
    tile=x*2+c
    tok_x=rcopy(own_tok,all_tok.at[tile],ts.at[0],tr.at[0],across)
    tok_c=rcopy(own_tok,all_tok.at[tile],ts.at[1],tr.at[1],core)
    far=all_tok.at[(1-x)*2+c]
    tok_f=rcopy(far,far,ts.at[2],tr.at[2],core)
    near=all_tok.at[x*2+1-c]
    diag=all_tok.at[(1-x)*2+1-c]
    cnts=[rcopy(own_cnt,all_cnt.at[tile],ns.at[i],nr.at[i],to) for i,to in enumerate((across,core,dev(z,y,1-x,1-c)))]
    cnt_in=[rcopy(r,r,ns.at[i],nr.at[i],core) for i,r in enumerate((all_cnt.at[(1-x)*2+c],all_cnt.at[x*2+1-c],all_cnt.at[(1-x)*2+1-c]))]
    local=(pltpu.make_async_copy(own_w,all_w.at[pl.ds(me*per,per)],ls.at[0]),
           pltpu.make_async_copy(own_tok,all_tok.at[tile],ls.at[1]),pltpu.make_async_copy(own_cnt,all_cnt.at[tile],ls.at[2]))
    @pl.when(z<3)
    def _(): start(z_copies(z,True,True))
    @pl.when(z>0)
    def _(): start(z_copies(z,True,False))
    start(y_copies(z,True)); start(tok_x); start(tok_c)
    for cp in cnts: cp.start()
    for cp in local: cp.start()
    def from_line(k,dist):
        zz=z-dist if k==0 else z+dist
        there=(zz>=0) if k==0 else (zz<=3)
        @pl.when(there)
        def _():
            got(z_arrivals(zz,k,dist))
            @pl.when((z<3) if k==0 else (z>0))
            def _(): start(z_copies(zz,False,k==0))
            start(y_copies(zz,False)); start(x_copy(zz*2+y,False)); start(c_copies(zz*2+y,False))
    def from_beside(zz):
        got(y_arrivals(zz))
        s=zz*2+1-y
        start(x_copy(s,False)); start(c_copies(s,False))
    def guarded(f,dist):
        @pl.when(z-dist>=0)
        def _(): f(z-dist)
        @pl.when(z+dist<=3)
        def _(): f(z+dist)
    def from_across(shard):
        got(x_arrival(shard)); start(f_copy(shard))
    from_line(0,1); from_line(1,1)
    from_beside(z)
    from_line(0,2); from_line(1,2)
    guarded(from_beside,1); guarded(lambda zz: from_across(zz*2+y),1); from_across(z*2+1-y)
    from_line(0,3); from_line(1,3)
    got(tok_x); tok_f.start()
    guarded(from_beside,2); guarded(lambda zz: from_across(zz*2+y),2); guarded(lambda zz: from_across(zz*2+1-y),1)
    guarded(from_beside,3); guarded(lambda zz: from_across(zz*2+y),3); guarded(lambda zz: from_across(zz*2+1-y),2)
    guarded(lambda zz: from_across(zz*2+1-y),3)
    def drain(s,_):
        @pl.when(s!=me)
        def _():
            got(c_arrivals(s)); got(f_arrival(s)); sent(c_copies(s,False)); sent(f_copy(s)); sent(x_copy(s,False))
        return 0
    lax.fori_loop(0,8,drain,0)
    def drain_y(zz,_):
        sent(y_copies(zz,False)); return 0
    lax.fori_loop(0,4,drain_y,0)
    for dist in range(4):
        @pl.when(jnp.logical_and(z<3,z-dist>=0))
        def _(): sent(z_copies(z-dist,False,True))
        @pl.when(jnp.logical_and(z>0,z+dist<=3))
        def _(): sent(z_copies(z+dist,False,False))
    rcopy(near,near,ts.at[1],tr.at[1],core).wait_recv()
    rcopy(diag,diag,ts.at[2],tr.at[2],core).wait_recv()
    tok_x.wait_send(); tok_c.wait_send(); tok_f.wait_send()
    for cp in cnts: cp.wait_send()
    for cp in cnt_in: cp.wait_recv()
    for cp in local: cp.wait()

def gather_all(own_w,own_tok,own_cnt):
    DS=pltpu.SemaphoreType.DMA
    hbm=pl.BlockSpec(memory_space=pl.ANY)
    return pl.pallas_call(gather_kernel,
        out_shape=[jax.ShapeDtypeStruct((8*own_w.shape[0],)+own_w.shape[1:],bf),jax.ShapeDtypeStruct((4,)+own_tok.shape,bf),jax.ShapeDtypeStruct((4,)+own_cnt.shape,own_cnt.dtype)],
        in_specs=[pl.BlockSpec(memory_space=pltpu.VMEM)]*3,out_specs=[hbm]*3,
        scratch_shapes=[DS((2,4,2)),DS((2,4,2)),DS((4,2)),DS((4,2)),DS((8,)),DS((8,)),DS((8,2)),DS((8,2)),DS((8,)),DS((8,)),DS((3,)),DS((3,)),DS((3,)),DS((3,)),DS((3,))],
        compiler_params=pltpu.CompilerParams(has_side_effects=True,vmem_limit_bytes=16<<20),name="gather_weights_tokens")(own_w,own_tok,own_cnt)

def exchange_kernel(a_ref,o_ref,ss,rs):
    dp=lax.axis_index("dp"); t=lax.axis_index("tile")
    n=a_ref.shape[0]
    def out(k):
        p=(t+k)%n
        return rcopy(a_ref.at[p],o_ref.at[t],ss.at[k],rs.at[k],(dp,p))
    def arrive(k):
        q=(t-k+n)%n
        return rcopy(o_ref.at[q],o_ref.at[q],ss.at[k],rs.at[k],(dp,q))
    for k in range(n-1,0,-1): out(k).start()
    o_ref[t]=a_ref[t]
    for k in range(1,n): arrive(k).wait_recv()
    for k in range(1,n): out(k).wait_send()

def exchange(a):
    DS=pltpu.SemaphoreType.DMA
    n=a.shape[0]
    vm=pl.BlockSpec(memory_space=pltpu.VMEM)
    return pl.pallas_call(exchange_kernel,out_shape=jax.ShapeDtypeStruct(a.shape,a.dtype),in_specs=[vm],out_specs=vm,
        scratch_shapes=[DS((n,)),DS((n,))],compiler_params=pltpu.CompilerParams(has_side_effects=True,vmem_limit_bytes=16<<20),name="exchange_over_tile")(a)

def totals_kernel(v_ref,g_ref,vo_ref,go_ref,vt,vd,gd,ts,tr,ds,dr,gs,gr):
    dp=lax.axis_index("dp"); t=lax.axis_index("tile")
    nt,nd=vt.shape[0],vd.shape[0]
    def g_copy(k):
        p=(dp+k)%nd
        return rcopy(gd.at[dp],gd.at[dp],gs.at[k],gr.at[k],(p,t))
    def g_arrive(k):
        q=(dp-k+nd)%nd
        return rcopy(gd.at[q],gd.at[q],gs.at[k],gr.at[k],(q,t))
    def t_copy(k):
        p=(t+k)%nt
        return rcopy(vt.at[t],vt.at[t],ts.at[k],tr.at[k],(dp,p))
    def t_arrive(k):
        q=(t-k+nt)%nt
        return rcopy(vt.at[q],vt.at[q],ts.at[k],tr.at[k],(dp,q))
    def d_copy(k):
        p=(dp+k)%nd
        return rcopy(vd.at[dp],vd.at[dp],ds.at[k],dr.at[k],(p,t))
    def d_arrive(k):
        q=(dp-k+nd)%nd
        return rcopy(vd.at[q],vd.at[q],ds.at[k],dr.at[k],(q,t))
    def loop(n,f):
        def s(k,_):
            f(k); return 0
        lax.fori_loop(1,n,s,0)
    vt[t]=v_ref[...]
    gd[dp]=g_ref[...]
    loop(nt,lambda k: t_copy(k).start())
    loop(nd,lambda k: g_copy(k).start())
    loop(nt,lambda k: t_arrive(k).wait_recv())
    acc=vt[0]
    for i in range(1,nt): acc=acc+vt[i]
    vd[dp]=acc
    loop(nd,lambda k: d_copy(k).start())
    loop(nd,lambda k: g_arrive(k).wait_recv())
    acc=gd[0]
    for i in range(1,nd): acc=acc+gd[i]
    go_ref[...]=acc
    loop(nd,lambda k: d_arrive(k).wait_recv())
    acc=vd[0]
    for i in range(1,nd): acc=acc+vd[i]
    vo_ref[...]=acc
    loop(nt,lambda k: t_copy(k).wait_send())
    loop(nd,lambda k: g_copy(k).wait_send())
    loop(nd,lambda k: d_copy(k).wait_send())

def totals(v,g,nd,nt):
    DS=pltpu.SemaphoreType.DMA
    vm=pl.BlockSpec(memory_space=pltpu.VMEM)
    return pl.pallas_call(totals_kernel,out_shape=[jax.ShapeDtypeStruct(v.shape,f32),jax.ShapeDtypeStruct(g.shape,f32)],in_specs=[vm]*2,out_specs=[vm]*2,
        scratch_shapes=[pltpu.VMEM((nt,)+v.shape,f32),pltpu.VMEM((nd,)+v.shape,f32),pltpu.VMEM((nd,)+g.shape,f32),DS((nt,)),DS((nt,)),DS((nd,)),DS((nd,)),DS((nd,)),DS((nd,))],
        compiler_params=pltpu.CompilerParams(has_side_effects=True,vmem_limit_bytes=16<<20),name="sum_small")(v,g)

def grad_sum_kernel(a_ref,o_ref,mine,xb0,yb0,zin,xb1,yb1,zin1,zin2,yb2,xb2,cs,cr,ss,rs,zs,zr,fs,fr):
    z,y,x,c=where_am_i()
    core=dev(z,y,x,1-c); across=dev(z,y,1-x,c); beside=dev(z,1-y,x,c)
    up=dev(jnp.minimum(z+1,3),y,x,c); down=dev(jnp.maximum(z-1,0),y,x,c)
    other=(1-c)*12; own=c*12
    def c_copy(p,d):
        return rcopy(a_ref.at[d,pl.ds(other+p*4,4)],mine.at[p,d],cs.at[p,d],cr.at[p,d],core)
    order=(2,0,1)
    def go(p):
        def s(d,_):
            c_copy(p,d).start(); return 0
        lax.fori_loop(0,8,s,0)
    for p in order: go(p)
    def add_own(p):
        def s(d,_):
            c_copy(p,d).wait_recv()
            for b in range(4):
                mine[p,d,b]=(mine[p,d,b].astype(f32)+a_ref[d,own+p*4+b].astype(f32)).astype(bf)
            return 0
        lax.fori_loop(0,8,s,0)
    def add(dst,src):
        n=dst.shape[0]
        for i in range(n): dst[i]=(dst[i].astype(f32)+src[i].astype(f32)).astype(bf)
    def line(buf_of,inbox,sem):
        def cp(tz,go_down):
            k=1 if go_down else 0
            return rcopy(buf_of(tz),inbox.at[k,tz],zs.at[sem,k,tz],zr.at[sem,k,tz],down if go_down else up)
        def arrive(tz,go_down):
            k=1 if go_down else 0
            return rcopy(inbox.at[k,tz],inbox.at[k,tz],zs.at[sem,k,tz],zr.at[sem,k,tz],down)
        return cp,arrive
    def line_start(cp):
        @pl.when(z==3)
        def _(): cp(0,True).start()
        @pl.when(z==0)
        def _(): cp(3,False).start()
    def line_pass(cp,arrive,buf_of,inbox,addf):
        for tz in (0,1):
            @pl.when(z==3)
            def _():
                cp(tz,True).wait_send(); cp(tz+1,True).start()
            @pl.when(z==0)
            def _():
                cp(3-tz,False).wait_send(); cp(2-tz,False).start()
        for tz in (0,1,2):
            @pl.when(jnp.logical_and(z<3,z>tz))
            def _():
                arrive(tz,True).wait_recv(); addf(buf_of(tz),inbox.at[1,tz]); cp(tz,True).start()
            u=3-tz
            @pl.when(jnp.logical_and(z>0,z<u))
            def _():
                arrive(u,False).wait_recv(); addf(buf_of(u),inbox.at[0,u]); cp(u,False).start()
    def line_end(cp,arrive,buf_of,inbox,addf):
        @pl.when(z<3)
        def _():
            arrive(z,True).wait_recv(); addf(buf_of(z),inbox.at[1,z])
        @pl.when(z>0)
        def _():
            arrive(z,False).wait_recv(); addf(buf_of(z),inbox.at[0,z])
    def line_sent(cp):
        @pl.when(z==3)
        def _(): cp(2,True).wait_send()
        @pl.when(z==0)
        def _(): cp(1,False).wait_send()
        for tz in (0,1,2):
            @pl.when(jnp.logical_and(z<3,z>tz))
            def _(): cp(tz,True).wait_send()
            @pl.when(jnp.logical_and(z>0,z<3-tz))
            def _(): cp(3-tz,False).wait_send()
    def add2(dst,src):
        for i in range(2):
            for j in range(4): dst[i,j]=(dst[i,j].astype(f32)+src[i,j].astype(f32)).astype(bf)
    p2_of=lambda tz: mine.at[2,pl.ds(tz*2,2)]
    cp2,ar2=line(p2_of,zin,0)
    add_own(2); line_start(cp2)
    def x0(d): return rcopy(mine.at[0,d,pl.ds((1-x)*2,2)],xb0.at[d],ss.at[0,d],rs.at[0,d],across)
    def s0(d,_):
        c_copy(0,d).wait_recv()
        for b in range(4):
            mine[0,d,b]=(mine[0,d,b].astype(f32)+a_ref[d,own+b].astype(f32)).astype(bf)
        x0(d).start()
        return 0
    lax.fori_loop(0,8,s0,0)
    def y1(zz): return rcopy(mine.at[1,zz*2+1-y],yb0.at[zz],ss.at[1,zz],rs.at[1,zz],beside)
    add_own(1)
    for zz in range(4): y1(zz).start()
    line_pass(cp2,ar2,p2_of,zin,add2)
    def p0(zz,yy): return mine.at[0,zz*2+yy,pl.ds(x*2,2)]
    def y0(zz): return rcopy(p0(zz,1-y),yb1.at[zz],ss.at[2,zz],rs.at[2,zz],beside)
    for zz in range(4):
        for yy in range(2):
            d=zz*2+yy
            x0(d).wait_recv(); add(p0(zz,yy),xb0.at[d])
        y0(zz).start()
    def p1(zz): return mine.at[1,zz*2+y]
    def x1(zz): return rcopy(mine.at[1,zz*2+y,pl.ds((1-x)*2,2)],xb1.at[zz],ss.at[3,zz],rs.at[3,zz],across)
    for zz in range(4):
        y1(zz).wait_recv(); add(p1(zz),yb0.at[zz]); x1(zz).start()
    q0=lambda tz: mine.at[0,tz*2+y,pl.ds(x*2,2)]
    cp0,ar0=line(q0,zin1,1)
    q1=lambda tz: mine.at[1,tz*2+y,pl.ds(x*2,2)]
    cp1,ar1=line(q1,zin2,2)
    for zz in range(4):
        y0(zz).wait_recv(); add(q0(zz),yb1.at[zz])
    line_start(cp0)
    line_end(cp2,ar2,p2_of,zin,add2)
    y2=rcopy(mine.at[2,z*2+1-y],yb2,ss.at[4,0],rs.at[4,0],beside)
    y2.start()
    for zz in range(4):
        x1(zz).wait_recv(); add(q1(zz),xb1.at[zz])
    line_start(cp1)
    line_pass(cp0,ar0,q0,zin1,add)
    y2.wait_recv(); add(mine.at[2,z*2+y],yb2)
    x2=rcopy(mine.at[2,z*2+y,pl.ds((1-x)*2,2)],xb2,ss.at[5,0],rs.at[5,0],across)
    x2.start()
    line_pass(cp1,ar1,q1,zin2,add)
    x2.wait_recv()
    me=z*2+y
    add(mine.at[2,me,pl.ds(x*2,2)],xb2)
    def place(xx,cc,p): return o_ref.at[pl.ds(cc*12+p*4+xx*2,2)]
    def f_copy(i,p):
        if i==2: return rcopy(place(1-x,c,p),place(1-x,c,p),fs.at[2,p],fr.at[2,p],core)
        return rcopy(mine.at[p,me,pl.ds(x*2,2)],place(x,c,p),fs.at[i,p],fr.at[i,p],across if i==0 else core)
    def f_arrive(i,p):
        r=(place(1-x,c,p),place(x,1-c,p),place(1-x,1-c,p))[i]
        return rcopy(r,r,fs.at[i,p],fr.at[i,p],core)
    def finish(p):
        o_ref[pl.ds(own+p*4+x*2,2)]=mine[p,me,pl.ds(x*2,2)]
        for i in range(2): f_copy(i,p).start()
    finish(2)
    line_end(cp0,ar0,q0,zin1,add); finish(0)
    line_end(cp1,ar1,q1,zin2,add); finish(1)
    for p in (2,0,1):
        f_arrive(0,p).wait_recv(); f_copy(2,p).start()
    for p in range(3):
        f_arrive(1,p).wait_recv(); f_arrive(2,p).wait_recv()
    for p in range(3):
        for i in range(3): f_copy(i,p).wait_send()
    def drain(d,_):
        for p in range(3): c_copy(p,d).wait_send()
        x0(d).wait_send()
        return 0
    lax.fori_loop(0,8,drain,0)
    for zz in range(4):
        y1(zz).wait_send(); y0(zz).wait_send(); x1(zz).wait_send()
    y2.wait_send(); x2.wait_send()
    line_sent(cp2); line_sent(cp0); line_sent(cp1)

def grad_sum(a):
    DS=pltpu.SemaphoreType.DMA
    R=a.shape[2]
    vm=pl.BlockSpec(memory_space=pltpu.VMEM)
    V=lambda *s: pltpu.VMEM(s+(R,128),bf)
    return pl.pallas_call(grad_sum_kernel,out_shape=jax.ShapeDtypeStruct((24,R,128),bf),in_specs=[vm],out_specs=vm,
        scratch_shapes=[V(3,8,4),V(8,2),V(4,4),V(2,4,2,4),V(4,2),V(4,2),V(2,4,2),V(2,4,2),V(4),V(2),
            DS((3,8)),DS((3,8)),DS((6,8)),DS((6,8)),DS((3,2,4)),DS((3,2,4)),DS((3,3)),DS((3,3))],
        cost_estimate=pl.CostEstimate(flops=10**7,bytes_accessed=200*10**6,transcendentals=0),
        compiler_params=pltpu.CompilerParams(has_side_effects=True,vmem_limit_bytes=56<<20),name="sum_gradients")(a)


H = 12
NGRP = 16
STEP = 10
EPS_NORM = 1e-06
BETA_ONE = 0.5
BETA_TWO = 0.5
ADAM_EPS = 1e-08
RATE_BLOCK = 0.3
RATE_VECTOR = 0.2
NEG_RAW = -8.0e9
HEAD = 64
SCALE = 1.0 / math.sqrt(HEAD)
EXP2 = SCALE * math.log2(math.e)
NN = (((1,), (0,)), ((), ()))
NT = (((1,), (1,)), ((), ()))
TN = (((0,), (0,)), ((), ()))


def mm(a, b, dims=NN):
    return lax.dot_general(a, b, dims, preferred_element_type=f32)


def vmem_spec():
    return pl.BlockSpec(memory_space=pltpu.VMEM)


def smem_spec():
    return pl.BlockSpec(memory_space=pltpu.SMEM)


def any_spec():
    return pl.BlockSpec(memory_space=pl.ANY)


def params(mib=48):
    return pltpu.CompilerParams(vmem_limit_bytes=mib << 20)


def pack(block, odd):
    half = block.shape[0] // 2
    left, right = block[:, :64], block[:, 128:]
    even_tail = jnp.concatenate([right[:half], right[half:]], axis=1)
    odd_tail = jnp.concatenate([left[half:], left[:half]], axis=1)
    return jnp.where(odd, block[:, 64:], block[:, :128]), jnp.where(odd, odd_tail, even_tail)


def unpack(top, tail, odd):
    first, second = tail[:, :64], tail[:, 64:]
    even = jnp.concatenate([top, jnp.concatenate([first, second], axis=0)], axis=1)
    return jnp.where(odd, jnp.concatenate([jnp.concatenate([second, first], axis=0), top], axis=1), even)


def turn(v):
    return jnp.concatenate([v[:, 64:], v[:, :64]], axis=1)


def group_of(n):
    return 4 if n % 4 == 0 else 3 if n % 3 == 0 else 1


def pack_kernel(odd_ref, m_ref, p_ref, s_ref):
    g = m_ref.shape[0]
    for b in range(g):
        m = m_ref[b]
        top, tail = pack(m, odd_ref[pl.program_id(0) * g + b] == 1)
        p_ref[b, :192] = top.astype(bf)
        p_ref[b, 192:] = tail.astype(bf)
        s_ref[b] = jnp.full((8, 128), jnp.sum(m * m), f32)


def pack_master(odd, master):
    n = master.shape[0]
    g = group_of(n)
    at = lambda i, s: (i, 0, 0)
    spec = pltpu.PrefetchScalarGridSpec(
        num_scalar_prefetch=1,
        grid=(n // g,),
        in_specs=[pl.BlockSpec((g, 192, 192), at)],
        out_specs=[pl.BlockSpec((g, 288, 128), at), pl.BlockSpec((g, 8, 128), at)],
    )
    return pl.pallas_call(
        pack_kernel,
        grid_spec=spec,
        out_shape=[jax.ShapeDtypeStruct((n, 288, 128), bf), jax.ShapeDtypeStruct((n, 8, 128), f32)],
        compiler_params=params(16),
        name="pack_master",
    )(odd, master)


def qkv_kernel(src_ref, cnt_ref, at_ref, x0, x1, x2, x3, blk_ref, gain_ref, shift_ref, bq_ref, bv_ref, a_ref, q_ref, qt_ref, k_ref, kt_ref, v_ref, vt_ref, w_ref, buf, sems):
    i = pl.program_id(0)

    @pl.when(i == 0)
    def _():
        copies = [pltpu.make_async_copy(blk_ref.at[at_ref[j]], buf.at[j], sems.at[j]) for j in range(12)]
        for copy in copies:
            copy.start()
        odd = at_ref[12] == 1
        for r in range(4):
            parts = []
            for c in range(3):
                copies[r * 3 + c].wait()
                p = buf[r * 3 + c].astype(f32)
                parts.append(unpack(p[:192], p[192:], odd))
            w_ref[r * 192 : (r + 1) * 192, :] = jnp.concatenate(parts, axis=1).astype(bf)

    x = jnp.concatenate([r[...] for r in (x0, x1, x2, x3)], axis=0).astype(f32)
    mean = jnp.mean(x, axis=-1, keepdims=True)
    cen = x - mean
    inv_std = lax.rsqrt(jnp.mean(cen * cen, axis=-1, keepdims=True) + EPS_NORM)
    a = (cen * inv_std * gain_ref[...] + shift_ref[...]).astype(bf)
    a_ref[...] = a
    qkv = mm(a, w_ref[...])
    q = (qkv[:, :192] + bq_ref[...]).astype(bf).astype(f32)
    k = qkv[:, 192:384].astype(bf).astype(f32)
    v = (qkv[:, 384:] + bv_ref[...]).astype(bf).astype(f32)
    row = lax.broadcasted_iota(jnp.int32, (128, 64), 0)
    lane = lax.broadcasted_iota(jnp.int32, (512, 64), 1)
    masked = jnp.concatenate(
        [jnp.where(row < cnt_ref[4 * i + b], 0.0, NEG_RAW) for b in range(4)], axis=0
    )
    ones = jnp.where(lane < 4, 1.0, 0.0)
    k_tail = jnp.where(lane == 0, masked, ones)
    v_tail = jnp.where(lane < 3, 1.0, 0.0)
    zero = jnp.zeros((512, 64), f32)
    sub = lax.broadcasted_iota(jnp.int32, (64, 512), 0)
    t_tail = jnp.where(sub < 1, 1.0, 0.0)
    qt, kt, vt = q.T, k.T, v.T
    for h in range(3):
        s = slice(h * 64, (h + 1) * 64)
        q_ref[h] = jnp.concatenate([q[:, s], zero], axis=1).astype(bf)
        k_ref[h] = jnp.concatenate([k[:, s], k_tail], axis=1).astype(bf)
        v_ref[h] = jnp.concatenate([v[:, s], v_tail], axis=1).astype(bf)
        qt_ref[h] = jnp.concatenate([qt[s], t_tail], axis=0).astype(bf)
        kt_ref[h] = kt[s].astype(bf)
        vt_ref[h] = jnp.concatenate([vt[s], t_tail[:16]], axis=0).astype(bf)


def qkv_forward(src, cnt, own_at, tokens, blocks, gain, shift, bq, bv):
    n = tokens.shape[0]
    rows = [pl.BlockSpec((128, 768), lambda i, s, c, o, k=k: (s[4 * i + k], 0)) for k in range(4)]
    row = lambda i, s, c, o: (0, 0)
    spec = pltpu.PrefetchScalarGridSpec(
        num_scalar_prefetch=3,
        grid=(n // 512,),
        in_specs=rows
        + [any_spec(), pl.BlockSpec((1, 768), row), pl.BlockSpec((1, 768), row), pl.BlockSpec((1, 192), row), pl.BlockSpec((1, 192), row)],
        out_specs=[
            pl.BlockSpec((512, 768), lambda i, s, c, o: (i, 0)),
            pl.BlockSpec((3, 512, 128), lambda i, s, c, o: (0, i, 0)),
            pl.BlockSpec((3, 128, 512), lambda i, s, c, o: (0, 0, i)),
            pl.BlockSpec((3, 512, 128), lambda i, s, c, o: (0, i, 0)),
            pl.BlockSpec((3, 64, 512), lambda i, s, c, o: (0, 0, i)),
            pl.BlockSpec((3, 512, 128), lambda i, s, c, o: (0, i, 0)),
            pl.BlockSpec((3, 80, 512), lambda i, s, c, o: (0, 0, i)),
            pl.BlockSpec((768, 576), row),
        ],
        scratch_shapes=[pltpu.VMEM((12, 288, 128), bf), pltpu.SemaphoreType.DMA((12,))],
    )
    shapes = [(n, 768), (3, n, 128), (3, 128, n), (3, n, 128), (3, 64, n), (3, n, 128), (3, 80, n), (768, 576)]
    return pl.pallas_call(
        qkv_kernel,
        grid_spec=spec,
        out_shape=[jax.ShapeDtypeStruct(s, bf) for s in shapes],
        compiler_params=params(40),
        name="norm_and_qkv",
    )(src, cnt, own_at, tokens, tokens, tokens, tokens, blocks, gain, shift, bq, bv)


def split3(v):
    a = v.astype(bf).astype(f32)
    b = (v - a).astype(bf).astype(f32)
    return a, b, v - a - b


def attend_kernel(bq, n_ref, k_ref, qt_ref, vt_ref, ot_ref, qb_ref):
    live = n_ref[0]
    qi = pl.program_id(1)

    @pl.when(qi * bq < live * 128)
    def _():
        qt = qt_ref[0]

        def block(start, size, carry):
            top, acc = carry
            s = mm(k_ref[0, pl.ds(start, size), :], qt) * EXP2
            new = jnp.maximum(top, jnp.max(s, axis=0, keepdims=True))
            p = jnp.exp2(s - new).astype(bf)
            acc = acc * jnp.exp2(top - new) + mm(vt_ref[0, :, pl.ds(start, size)], p)
            return new, acc

        def step(j, carry):
            return block(pl.multiple_of(j * 1024, 1024), 1024, carry)

        def rest(j, carry):
            return block(pl.multiple_of(j * 256, 256), 256, carry)

        pairs = (live + 1) // 2
        carry = (jnp.full((1, bq), -3e38, f32), jnp.zeros((80, bq), f32))
        carry = lax.fori_loop(0, pairs // 4, step, carry)
        top, acc = lax.fori_loop((pairs // 4) * 4, pairs, rest, carry)
        total = acc[64:65]
        ot_ref[0] = acc[:64] / total
        a, b, c = split3((top + jnp.log2(total)) * (-1.0 / EXP2))
        row = lax.broadcasted_iota(jnp.int32, (64, bq), 0)
        tail = jnp.where(row == 0, 1.0, jnp.where(row == 1, a, jnp.where(row == 2, b, jnp.where(row == 3, c, 0.0))))
        qb_ref[0, :64] = qt[:64]
        qb_ref[0, 64:] = tail.astype(bf)


def attend(live, k, qt, vt, bq=1024):
    n = k.shape[1]
    spec = pltpu.PrefetchScalarGridSpec(
        num_scalar_prefetch=1,
        grid=(3, n // bq),
        in_specs=[
            pl.BlockSpec((1, n, 128), lambda h, i, s: (h, 0, 0)),
            pl.BlockSpec((1, 128, bq), lambda h, i, s: (h, 0, i)),
            pl.BlockSpec((1, 80, n), lambda h, i, s: (h, 0, 0)),
        ],
        out_specs=[pl.BlockSpec((1, 64, bq), lambda h, i, s: (h, 0, i)), pl.BlockSpec((1, 128, bq), lambda h, i, s: (h, 0, i))],
    )
    return pl.pallas_call(
        functools.partial(attend_kernel, bq),
        grid_spec=spec,
        out_shape=[jax.ShapeDtypeStruct((3, 64, n), f32), jax.ShapeDtypeStruct((3, 128, n), bf)],
        compiler_params=params(48),
        name="attention_forward",
    )(live, k, qt, vt)


def spread_kernel(src_ref, n_ref, ot_ref, o_ref):
    live = n_ref[0]
    per = o_ref.shape[2] // 128

    def step(b, _):
        g = src_ref[b]
        lanes = pl.ds(pl.multiple_of(b * 128, 128), 128)
        to = pl.ds(pl.multiple_of((g % per) * 128, 128), 128)

        @pl.when(b < live)
        def _():
            for h in range(3):
                o_ref[g // per, h * 64 : (h + 1) * 64, to] = ot_ref[h, :, lanes].astype(bf)

        @pl.when(b >= live)
        def _():
            o_ref[g // per, :, to] = jnp.zeros((192, 128), bf)

        return 0

    lax.fori_loop(0, ot_ref.shape[2] // 128, step, 0)


def spread(src, live, ot, tiles):
    n = ot.shape[2]
    return pl.pallas_call(
        spread_kernel,
        in_specs=[smem_spec(), smem_spec(), vmem_spec()],
        out_specs=vmem_spec(),
        out_shape=jax.ShapeDtypeStruct((tiles, 192, n // tiles), bf),
        compiler_params=params(24),
        name="spread_attended",
    )(src, live, ot)


def collect_kernel(src_ref, n_ref, g_ref, ot_ref, dt_ref, d_ref):
    live = n_ref[0]
    per = g_ref.shape[2] // 128
    row = lax.broadcasted_iota(jnp.int32, (64, 128), 0)

    def step(b, _):
        g = src_ref[b]
        to = pl.ds(pl.multiple_of(b * 128, 128), 128)
        lanes = pl.ds(pl.multiple_of((g % per) * 128, 128), 128)

        @pl.when(b < live)
        def _():
            for h in range(3):
                d = g_ref[g // per, h * 64 : (h + 1) * 64, lanes].astype(f32)
                delta = jnp.sum(d * ot_ref[h, :, to], axis=0, keepdims=True)
                x, y, z = split3(-delta)
                tail = jnp.where(row == 0, x, jnp.where(row == 1, y, jnp.where(row == 2, z, 0.0)))
                both = jnp.concatenate([d, tail], axis=0)
                dt_ref[h, :, to] = both.astype(bf)
                d_ref[h, to, :] = jnp.concatenate([d, jnp.zeros_like(d)], axis=0).T.astype(bf)

        @pl.when(b >= live)
        def _():
            dt_ref[:, :, to] = jnp.zeros((3, 128, 128), bf)
            d_ref[:, to, :] = jnp.zeros((3, 128, 128), bf)

        return 0

    lax.fori_loop(0, ot_ref.shape[2] // 128, step, 0)


def collect(src, live, grad, ot):
    n = ot.shape[2]
    return pl.pallas_call(
        collect_kernel,
        in_specs=[smem_spec(), smem_spec(), vmem_spec(), vmem_spec()],
        out_specs=[vmem_spec()] * 2,
        out_shape=[jax.ShapeDtypeStruct((3, 128, n), bf), jax.ShapeDtypeStruct((3, n, 128), bf)],
        compiler_params=params(32),
        name="collect_attended_grad",
    )(src, live, grad, ot)


def attend_back_kernel(bq, bk, n_ref, k_ref, kt_ref, v_ref, qb_ref, q_ref, dt_ref, d_ref, dq_ref, dk_ref, dv_ref):
    live = n_ref[0]
    j = pl.program_id(1)

    @pl.when(j == 0)
    def _():
        dq_ref[...] = jnp.zeros_like(dq_ref)

    @pl.when(j * bk < live * 128)
    def _():
        k, v, kt = k_ref[0], v_ref[0], kt_ref[0]

        def block(start, size, carry):
            dk, dv = carry
            lanes = pl.ds(start, size)
            p = jnp.exp2(mm(k, qb_ref[0, :, lanes]) * EXP2)
            ds = (p * mm(v, dt_ref[0, :, lanes])).astype(bf)
            dv = dv + mm(p.astype(bf), d_ref[0, lanes, :])
            dk = dk + mm(ds, q_ref[0, lanes, :])
            dq_ref[0, :, lanes] += mm(kt, ds)
            return dk, dv

        def step(i, carry):
            return block(pl.multiple_of(i * bq, bq), bq, carry)

        def rest(i, carry):
            return block(pl.multiple_of(i * 256, 256), 256, carry)

        pairs = (live + 1) // 2
        full = pairs * 256 // bq
        zero = jnp.zeros((bk, 128), f32)
        carry = lax.fori_loop(0, full, step, (zero, zero))
        dk, dv = lax.fori_loop(full * bq // 256, pairs, rest, carry)
        dk_ref[0] = (dk * SCALE).astype(bf)
        dv_ref[0] = dv.astype(bf)


def attend_back(live, k, kt, v, qb, q, dt, d, bq=1024, bk=512):
    n = k.shape[1]
    whole_t = lambda h, j, s: (h, 0, 0)
    spec = pltpu.PrefetchScalarGridSpec(
        num_scalar_prefetch=1,
        grid=(3, n // bk),
        in_specs=[
            pl.BlockSpec((1, bk, 128), lambda h, j, s: (h, j, 0)),
            pl.BlockSpec((1, 64, bk), lambda h, j, s: (h, 0, j)),
            pl.BlockSpec((1, bk, 128), lambda h, j, s: (h, j, 0)),
            pl.BlockSpec((1, 128, n), whole_t),
            pl.BlockSpec((1, n, 128), whole_t),
            pl.BlockSpec((1, 128, n), whole_t),
            pl.BlockSpec((1, n, 128), whole_t),
        ],
        out_specs=[
            pl.BlockSpec((1, 64, n), whole_t),
            pl.BlockSpec((1, bk, 128), lambda h, j, s: (h, j, 0)),
            pl.BlockSpec((1, bk, 128), lambda h, j, s: (h, j, 0)),
        ],
    )
    return pl.pallas_call(
        functools.partial(attend_back_kernel, bq, bk),
        grid_spec=spec,
        out_shape=[jax.ShapeDtypeStruct((3, 64, n), f32), jax.ShapeDtypeStruct((3, n, 128), bf), jax.ShapeDtypeStruct((3, n, 128), bf)],
        compiler_params=params(48),
        name="attention_backward",
    )(live, k, kt, v, qb, q, dt, d)


def qkv_back_kernel(src_ref, n_ref, at_ref, dq_ref, dk_ref, dv_ref, a_ref, w_ref, s_in, g_ref, s_ref, gb_ref, acc, sums, rows, packed, sems, psems):
    i = pl.program_id(0)
    live = n_ref[0]

    @pl.when(i == 0)
    def _():
        acc[...] = jnp.zeros_like(acc)
        sums[...] = jnp.zeros_like(sums)

    @pl.when(4 * i < live)
    def _():
        dq = jnp.concatenate([dq_ref[h] for h in range(3)], axis=0).T * SCALE
        g = jnp.concatenate(
            [dq] + [dk_ref[h][:, :64].astype(f32) for h in range(3)] + [dv_ref[h][:, :64].astype(f32) for h in range(3)], axis=1
        ).astype(bf)
        acc[...] += mm(a_ref[...], g, TN)
        sums[...] += jnp.broadcast_to(jnp.sum(g.astype(f32), axis=0, keepdims=True), sums.shape)
        rows[...] = mm(g, w_ref[...], NT).astype(bf)

    @pl.when(4 * i >= live)
    def _():
        rows[...] = jnp.zeros_like(rows)

    copies = [
        pltpu.make_async_copy(rows.at[pl.ds(b * 128, 128)], g_ref.at[pl.ds(pl.multiple_of(src_ref[4 * i + b] * 128, 128), 128)], sems.at[b])
        for b in range(4)
    ]
    for copy in copies:
        copy.start()
    for copy in copies:
        copy.wait()

    @pl.when(i == pl.num_programs(0) - 1)
    def _():
        out = []
        for r in range(4):
            for c in range(3):
                j = r * 3 + c
                top, tail = pack(acc[r * 192 : (r + 1) * 192, c * 192 : (c + 1) * 192], at_ref[12] == 1)
                packed[j, :192] = top.astype(bf)
                packed[j, 192:] = tail.astype(bf)
                out.append(pltpu.make_async_copy(packed.at[j], s_ref.at[at_ref[j]], psems.at[j]))
                out[-1].start()
        gb_ref[...] = sums[...]
        for copy in out:
            copy.wait()


def qkv_backward(src, live, own_at, dq, dk, dv, a, w, slots):
    n = a.shape[0]
    spec = pltpu.PrefetchScalarGridSpec(
        num_scalar_prefetch=3,
        grid=(n // 512,),
        in_specs=[
            pl.BlockSpec((3, 64, 512), lambda i, s, c, o: (0, 0, i)),
            pl.BlockSpec((3, 512, 128), lambda i, s, c, o: (0, i, 0)),
            pl.BlockSpec((3, 512, 128), lambda i, s, c, o: (0, i, 0)),
            pl.BlockSpec((512, 768), lambda i, s, c, o: (i, 0)),
            pl.BlockSpec((768, 576), lambda i, s, c, o: (0, 0)),
            any_spec(),
        ],
        out_specs=[any_spec(), any_spec(), pl.BlockSpec((8, 576), lambda i, s, c, o: (0, 0))],
        scratch_shapes=[
            pltpu.VMEM((768, 576), f32),
            pltpu.VMEM((8, 576), f32),
            pltpu.VMEM((512, 768), bf),
            pltpu.VMEM((12, 288, 128), bf),
            pltpu.SemaphoreType.DMA((4,)),
            pltpu.SemaphoreType.DMA((12,)),
        ],
    )
    return pl.pallas_call(
        qkv_back_kernel,
        grid_spec=spec,
        out_shape=[jax.ShapeDtypeStruct((n, 768), bf), jax.ShapeDtypeStruct(slots.shape, bf), jax.ShapeDtypeStruct((8, 576), f32)],
        input_output_aliases={8: 1},
        compiler_params=params(32),
        name="qkv_backward",
    )(src, live, own_at, dq, dk, dv, a, w, slots)


def gelu_parts(z):
    cdf = 0.5 + 0.5 * lax.erf(z * math.sqrt(0.5))
    return z * cdf, cdf + z * (jnp.exp2(z * z * (-0.5 * math.log2(math.e))) * (1.0 / math.sqrt(2.0 * math.pi)))


def column_sum(v):
    return jnp.sum(v, axis=0, keepdims=True)


def middle_kernel(inv_ref, cnt_ref, blk_ref, o_ref, x_ref, c_ref, vp_ref, bu_ref, y_ref, gr_ref, go_ref, s_ref, vs_ref, us_ref,
                  w_out, w_up, w_down, tails, u_s, gz_s, a2_s, gm_s, gb_s, o_s, ring, zero, tsem, isem, osem, zsem):
    i = pl.program_id(0)
    rows = x_ref.shape[0]
    r0 = pl.multiple_of(i * rows, rows)
    kinds = ((w_out, 48, 2, 4), (w_up, 64, 8, 4), (w_down, 128, 2, 16))

    def zero_copy(j):
        return pltpu.make_async_copy(zero, s_ref.at[inv_ref[j]], zsem.at[j])

    @pl.when(i == 0)
    def _():
        vs_ref[...] = jnp.zeros_like(vs_ref)
        us_ref[...] = jnp.zeros_like(us_ref)
        zero[...] = jnp.zeros_like(zero)

        def pair(w, first, pairs):
            def copies(j):
                r = pl.multiple_of((j // pairs) * 192, 64)
                col = pl.multiple_of((j % pairs) * 384, 128)
                out = []
                for b, off in ((0, 0), (1, 256)):
                    at = first + 2 * j + b
                    slot = inv_ref[at]
                    out.append(pltpu.make_async_copy(blk_ref.at[slot, pl.ds(0, 192)], w.at[pl.ds(r, 192), pl.ds(col + off, 128)], tsem.at[at - 48]))
                    out.append(pltpu.make_async_copy(blk_ref.at[slot, pl.ds(192, 96)], tails.at[at - 48], isem.at[at - 48]))
                return out, r, col

            def start(j, _):
                for copy in copies(j)[0]:
                    copy.start()
                return 0

            def join(j, _):
                got, r, col = copies(j)
                for copy in got:
                    copy.wait()
                even = tails[first + 2 * j - 48].astype(f32)
                odd = tails[first + 2 * j - 47].astype(f32)
                lane = lax.broadcasted_iota(jnp.int32, even.shape, 1) < 64
                w[pl.ds(r, 96), pl.ds(col + 128, 128)] = jnp.where(lane, even, odd).astype(bf)
                w[pl.ds(r + 96, 96), pl.ds(col + 128, 128)] = turn(jnp.where(lane, odd, even)).astype(bf)
                return 0

            return start, join

        todo = [(pair(w, first, pairs), pairs * high) for w, first, pairs, high in kinds]
        for (start, _), n in todo:
            lax.fori_loop(0, n, start, 0)

        def clear(j, _):
            zero_copy(j).start()
            return 0

        lax.fori_loop(0, 48, clear, 0)
        for (_, join), n in todo:
            lax.fori_loop(0, n, join, 0)

    vp = vp_ref[...]
    row = r0 + lax.broadcasted_iota(jnp.int32, (rows, 1), 0)
    live = jnp.where(row < cnt_ref[0], 1.0, 0.0)
    o_t = jnp.concatenate([o_ref[t] for t in range(4)], axis=0)
    o_s[:, pl.ds(r0, rows)] = o_t
    res = x_ref[...].astype(f32) + mm(o_t, w_out[...], TN) + vp[6:7]
    cen = res - jnp.mean(res, axis=-1, keepdims=True)
    inv_std = lax.rsqrt(jnp.mean(cen * cen, axis=-1, keepdims=True) + EPS_NORM)
    normed = cen * inv_std
    a2 = (normed * vp[2:3] + vp[3:4]).astype(bf)
    gy = c_ref[...].astype(f32) * live
    gm = gy.astype(bf)
    a2_s[pl.ds(r0, rows), :] = a2
    gm_s[pl.ds(r0, rows), :] = gm
    branch = jnp.zeros((rows, 768), f32)
    g2 = jnp.zeros((rows, 768), f32)
    for j in range(4):
        cols = slice(j * 768, (j + 1) * 768)
        u, slope = gelu_parts(mm(a2, w_up[:, cols]) + bu_ref[:, cols])
        u = u.astype(bf)
        u_s[pl.ds(r0, rows), cols] = u
        branch = branch + mm(u, w_down[cols, :])
        gz = (mm(gm, w_down[cols, :], NT) * slope).astype(bf)
        gz_s[pl.ds(r0, rows), cols] = gz
        us_ref[:, cols] += jnp.broadcast_to(column_sum(gz.astype(f32)), (8, 768))
        g2 = g2 + mm(gz, w_up[:, cols], NT)
    y_ref[...] = (live * (res + branch + vp[7:8])).astype(bf)
    d2 = g2 * vp[2:3]
    gr = gy + inv_std * (d2 - jnp.mean(d2, axis=-1, keepdims=True) - normed * jnp.mean(d2 * normed, axis=-1, keepdims=True))
    gr_ref[...] = gr
    gb = gr.astype(bf)
    gb_s[pl.ds(r0, rows), :] = gb
    vs_ref[0:1, :] += column_sum(g2 * normed)
    vs_ref[1:2, :] += column_sum(g2)
    vs_ref[2:3, :] += column_sum(gb.astype(f32))
    vs_ref[3:4, :] += column_sum(gm.astype(f32))
    go = mm(w_out[...], gb, NT).astype(bf)
    for t in range(4):
        go_ref[t] = go[t * 192 : (t + 1) * 192]

    @pl.when(i == pl.num_programs(0) - 1)
    def _():
        def out_copy(k, at):
            return pltpu.make_async_copy(ring.at[k], s_ref.at[inv_ref[at]], osem.at[k])

        def send(n, g, first, pairs, high, low):
            half = (n % 2) * 8

            def put(r, b):
                return first + (high + r) * 2 * pairs + 2 * low + b

            for r in range(4):
                part = g[r * 192 : (r + 1) * 192]
                mid = part[:, 128:256]
                upper, lower = mid[:96], turn(mid[96:])
                lane = lax.broadcasted_iota(jnp.int32, upper.shape, 1) < 64
                for b, top, tail in ((0, part[:, :128], jnp.where(lane, upper, lower)), (1, part[:, 256:], jnp.where(lane, lower, upper))):
                    k = half + 2 * r + b

                    @pl.when(n >= 2)
                    def _():
                        out_copy(k, 0).wait()

                    ring[k, :192] = top.astype(bf)
                    ring[k, 192:] = tail.astype(bf)
                    out_copy(k, put(r, b)).start()

        def lanes(j):
            return pl.ds(pl.multiple_of(j * 384, 128), 384)

        def grad_out(n, _):
            send(n, mm(o_s[...], gb_s[:, lanes(n)]), 48, 2, 0, n)
            return 0

        def grad_up(n, _):
            send(n, mm(a2_s[...], gz_s[:, lanes(n)], TN), 64, 8, 0, n)
            return 0

        def grad_down(n, _):
            high = n // 2
            send(n, mm(u_s[:, pl.ds(pl.multiple_of(high * 768, 128), 768)], gm_s[:, lanes(n % 2)], TN), 128, 2, high * 4, n % 2)
            return 0

        def drain():
            for k in range(16):
                out_copy(k, 0).wait()

        for f, n in ((grad_out, 2), (grad_up, 8), (grad_down, 8)):
            lax.fori_loop(0, n, f, 0)
            drain()

        def cleared(j, _):
            zero_copy(j).wait()
            return 0

        lax.fori_loop(0, 48, cleared, 0)


def middle(inv, count, blocks, o_t, tokens, cotangent, vec_params, bias_up, rows=256):
    n, width = tokens.shape
    hidden = bias_up.shape[1]
    row = lambda i, s, c: (i, 0)
    fixed = lambda i, s, c: (0, 0)
    col = lambda i, s, c: (0, 0, i)
    V, DS = pltpu.VMEM, pltpu.SemaphoreType.DMA
    spec = pltpu.PrefetchScalarGridSpec(
        num_scalar_prefetch=2,
        grid=(n // rows,),
        in_specs=[any_spec(), pl.BlockSpec((4, 192, rows), col), pl.BlockSpec((rows, width), row), pl.BlockSpec((rows, width), row),
                  pl.BlockSpec((12, width), fixed), pl.BlockSpec((1, hidden), fixed)],
        out_specs=[pl.BlockSpec((rows, width), row), pl.BlockSpec((rows, width), row), pl.BlockSpec((4, 192, rows), col), any_spec(),
                   pl.BlockSpec((8, width), fixed), pl.BlockSpec((8, hidden), fixed)],
        scratch_shapes=[V((768, 768), bf), V((768, 3072), bf), V((3072, 768), bf), V((144, 96, 128), bf), V((n, 3072), bf), V((n, 3072), bf),
                        V((n, 768), bf), V((n, 768), bf), V((n, 768), bf), V((768, n), bf), V((16, 288, 128), bf), V((288, 128), bf),
                        DS((144,)), DS((144,)), DS((16,)), DS((48,))],
    )
    return pl.pallas_call(
        middle_kernel,
        grid_spec=spec,
        out_shape=[jax.ShapeDtypeStruct((n, width), bf), jax.ShapeDtypeStruct((n, width), f32), jax.ShapeDtypeStruct((4, 192, n), bf),
                   jax.ShapeDtypeStruct(blocks.shape, bf), jax.ShapeDtypeStruct((8, width), f32), jax.ShapeDtypeStruct((8, hidden), f32)],
        compiler_params=params(60),
        name="projection_and_mlp",
    )(inv, count, blocks, o_t, tokens, cotangent, vec_params, bias_up)


def split2(v):
    hi = v.astype(bf)
    return hi, (v - hi.astype(f32)).astype(bf)


def mm3(a, b, dims):
    return mm(a[0], b[0], dims) + (mm(a[0], b[1], dims) + mm(a[1], b[0], dims))


def adam_kernel(odd_ref, g_ref, m1_ref, m2_ref, l_ref, r_ref, g_out, m1_out, m2_out, u_out, s_out):
    for b in range(g_ref.shape[0]):
        grad = unpack(g_ref[b, :192].astype(f32), g_ref[b, 192:].astype(f32), odd_ref[pl.program_id(0) * g_ref.shape[0] + b] == 1)
        left, right = split2(l_ref[b]), split2(r_ref[b])
        low = grad.astype(bf)
        rot = mm3(split2(mm(left[0], low, TN) + mm(left[1], low, TN)), right, NN)
        first = BETA_ONE * m1_ref[b] + (1.0 - BETA_ONE) * rot
        second = BETA_TWO * m2_ref[b] + (1.0 - BETA_TWO) * rot * rot
        upd = (first / (1.0 - BETA_ONE**STEP)) / (jnp.sqrt(second / (1.0 - BETA_TWO**STEP)) + ADAM_EPS)
        upd = mm3(split2(mm3(left, split2(upd), NN)), right, NT)
        g_out[b] = grad
        m1_out[b] = first
        m2_out[b] = second
        u_out[b] = upd
        s_out[b] = jnp.full((8, 128), jnp.sum(upd * upd), f32)


def adam(odd, grads, first, second, left, right):
    n = grads.shape[0]
    g = group_of(n)
    at = lambda i, s: (i, 0, 0)
    big = pl.BlockSpec((g, 192, 192), at)
    spec = pltpu.PrefetchScalarGridSpec(
        num_scalar_prefetch=1,
        grid=(n // g,),
        in_specs=[pl.BlockSpec((g, 288, 128), at)] + [big] * 4,
        out_specs=[big] * 4 + [pl.BlockSpec((g, 8, 128), at)],
    )
    return pl.pallas_call(
        adam_kernel,
        grid_spec=spec,
        out_shape=[jax.ShapeDtypeStruct((n, 192, 192), f32)] * 4 + [jax.ShapeDtypeStruct((n, 8, 128), f32)],
        compiler_params=params(40),
        name="rotated_adam",
    )(odd, grads, first, second, left, right)


def norm_forward(row_data, gain_vec, shift_vec):
    row_mean = jnp.mean(row_data, axis=-1, keepdims=True)
    centred = row_data - row_mean
    inv_std = lax.rsqrt(jnp.mean(centred * centred, axis=-1, keepdims=True) + EPS_NORM)
    normed = centred * inv_std
    return (normed * gain_vec + shift_vec, normed, inv_std)


def norm_back(grad_out, normed, inv_std, gain_vec):
    grad_normed = grad_out * gain_vec
    return inv_std * (
        grad_normed
        - jnp.mean(grad_normed, axis=-1, keepdims=True)
        - normed * jnp.mean(grad_normed * normed, axis=-1, keepdims=True)
    )


def block_plan(counts, slot_count):
    tiles = counts.shape[0]
    per = slot_count // 128
    j = lax.broadcasted_iota(jnp.int32, (tiles, per), 1)
    kept = jnp.clip(counts[:, None] - j * 128, 0, 128).reshape(-1)
    full = (kept > 0).astype(jnp.int32)
    index = jnp.arange(tiles * per, dtype=jnp.int32)
    before = (index[None, :] < index[:, None]).astype(jnp.int32)
    ahead = jnp.sum(before * full[None, :], axis=1)
    live = jnp.sum(full)
    place = jnp.where(full > 0, ahead, live + index - ahead)
    hot = (place[None, :] == index[:, None]).astype(jnp.int32)
    return jnp.sum(hot * index[None, :], axis=1), jnp.sum(hot * kept[None, :], axis=1), live.reshape(1)


def make_body(tuned):
    def body(tokens, cotangent, counts, master, slot_block, groups, first_moment, second_moment, left_basis, right_basis, vec_params, vec_first, vec_second):
        slot_count, width = tokens.shape[1:]
        per_owner = master.shape[0]
        tile = lax.axis_index("tile")
        mine = lax.dynamic_slice(slot_block, (lax.axis_index("dp") * per_owner,), (per_owner,))
        odd = mine % 2
        packed, weight_sq = pack_master(odd, master)
        own_tokens = tokens.reshape(slot_count, width)
        count_tile = jnp.broadcast_to(counts.reshape(1, 1), (8, 128))
        if tuned:
            blocks, token_all, count_all = gather_all(packed, own_tokens, count_tile)
        else:
            blocks = lax.all_gather(packed, "dp", axis=0, tiled=True)
            token_all = lax.all_gather(own_tokens, "tile", axis=0)
            count_all = lax.all_gather(count_tile, "tile", axis=0)
        tiles = token_all.shape[0]
        block_count = blocks.shape[0]
        src, cnt, live = block_plan(count_all[:, 0, 0], slot_count)
        index = jnp.arange(block_count, dtype=jnp.int32)
        inverse = jnp.sum((slot_block[None, :] == index[:, None]).astype(jnp.int32) * index[None, :], axis=1)
        own_block = jnp.arange(12, dtype=jnp.int32) // 3 * 12 + jnp.arange(12, dtype=jnp.int32) % 3 * 4 + tile
        own_at = jnp.sum((slot_block[None, :] == own_block[:, None]).astype(jnp.int32) * index[None, :], axis=1)
        own_at = jnp.concatenate([own_at, tile.reshape(1) % 2])
        own = width // tiles
        bias = lambda row: lax.dynamic_slice(vec_params[row : row + 1], (0, tile * own), (1, own))
        a1, q, qt, k, kt, v, vt, w_qkv = qkv_forward(
            src, cnt, own_at, token_all.reshape(-1, width), blocks, vec_params[0:1], vec_params[1:2], bias(4), bias(5)
        )
        ot, qb = attend(live, k, qt, vt)
        o_t = exchange(spread(src, live, ot, tiles))
        output, grad_resid, go_t, slots, sums, up_sums = middle(
            inverse, counts.reshape(1), blocks, o_t, own_tokens, cotangent.reshape(slot_count, width), vec_params, vec_params[8:].reshape(1, -1)
        )
        go = exchange(go_t)
        dt, d = collect(src, live, go, ot)
        dq, dk, dv = attend_back(live, k, kt, v, qb, q, dt, d)
        g_part, slot_grads, qkv_sums = qkv_backward(src, live, own_at, dq, dk, dv, a1, w_qkv, slots)
        g_part = g_part.reshape(tiles, slot_count, width)
        if tuned:
            g1 = lax.psum_scatter(g_part, "tile", scatter_dimension=0, tiled=False).astype(f32)
            grads = grad_sum(slot_grads.reshape(-1, per_owner, 288, 128))
        else:
            g1 = lax.psum_scatter(g_part.astype(f32), "tile", scatter_dimension=0, tiled=False)
            grads = lax.psum(lax.psum_scatter(slot_grads.astype(f32), "dp", scatter_dimension=0, tiled=True), "tile").astype(bf)
        row_input = own_tokens.astype(f32)
        _, normed_one, inv_std_one = norm_forward(row_input, vec_params[0], vec_params[1])
        input_grad = grad_resid + norm_back(g1, normed_one, inv_std_one, vec_params[0])
        zero = jnp.zeros((width,), f32)
        at_own = lambda s: lax.dynamic_update_slice(zero, s, (tile * own,))
        rows = jnp.stack(
            [jnp.sum(g1 * normed_one, axis=0), jnp.sum(g1, axis=0), sums[0], sums[1], at_own(qkv_sums[0, :own]), at_own(qkv_sums[0, 2 * own :]), sums[2], sums[3]],
            axis=0,
        )
        vector_part = jnp.concatenate([rows, up_sums[0].reshape(-1, width)], axis=0)

        weight_grads, first_out, second_out, update, update_sq = adam(odd, grads, first_moment, second_moment, left_basis, right_basis)
        group_hot = (groups[:, None] == jnp.arange(NGRP, dtype=jnp.int32)[None, :]).astype(f32)
        both = jnp.stack([weight_sq[:, 0, 0], update_sq[:, 0, 0]], axis=0)
        group_part = jnp.pad(jnp.sum(group_hot[None] * both[:, :, None], axis=1), ((0, 6), (0, 128 - NGRP)))
        vector_grads, group_both = totals(vector_part, group_part, block_count // per_owner, tiles)
        own_both = jnp.sum(group_hot[None] * group_both[:2, None, :NGRP], axis=2)
        block_rate = RATE_BLOCK * jnp.sqrt(own_both[0]) / (jnp.sqrt(own_both[1]) + 1e-06)
        master_out = master - block_rate[:, None, None] * update
        vec_first_out = BETA_ONE * vec_first + (1.0 - BETA_ONE) * vector_grads
        vec_second_out = BETA_TWO * vec_second + (1.0 - BETA_TWO) * vector_grads * vector_grads
        vec_update = (vec_first_out / (1.0 - BETA_ONE**STEP)) / (jnp.sqrt(vec_second_out / (1.0 - BETA_TWO**STEP)) + ADAM_EPS)
        return (
            output.reshape(1, slot_count, width),
            input_grad.reshape(1, slot_count, width),
            weight_grads,
            first_out,
            second_out,
            master_out,
            master_out.astype(bf),
            vector_grads,
            vec_first_out,
            vec_second_out,
            vec_params - RATE_VECTOR * vec_update,
        )

    return body


def solution(mesh):
    tuned = (mesh.shape["dp"], mesh.shape["tile"]) == (8, 4)
    rows, blocks = P("dp", "tile", None), P("dp", None, None)
    return jax.shard_map(
        make_body(tuned),
        mesh=mesh,
        in_specs=(rows, rows, P("dp", "tile"), blocks, P(), P("dp"), blocks, blocks, blocks, blocks, P(), P(), P()),
        out_specs=(rows, rows, blocks, blocks, blocks, blocks, blocks, P(), P(), P(), P()),
        check_vma=False,
    )
```

```python
import functools
import math

import jax
import jax.numpy as jnp
from jax import lax
from jax.experimental import pallas as pl
from jax.experimental.pallas import tpu as pltpu
from jax.sharding import PartitionSpec as P

f32 = jnp.float32
bf = jnp.bfloat16
MESH = pl.DeviceIdType.MESH

def where_am_i():
    dp=lax.axis_index("dp"); t=lax.axis_index("tile")
    return dp//2, dp%2, t//2, t%2

def dev(z,y,x,c):
    return (z*2+y, x*2+c)

def rcopy(src,dst,ss,rs,to):
    return pltpu.make_async_remote_copy(src_ref=src,dst_ref=dst,send_sem=ss,recv_sem=rs,device_id=to,device_id_type=MESH)

def gather_kernel(own_w,own_tok,own_cnt,all_w,all_tok,all_cnt,
                  zs,zr,ys,yr,xs,xr,cs,cr,fs,fr,ts,tr,ns,nr,ls):
    z,y,x,c=where_am_i()
    per=own_w.shape[0]
    part=per//12
    def a_of(shard,xx,cc): return all_w.at[pl.ds(shard*per+(xx*2+cc)*part,part)]
    def b_of(shard,cc): return all_w.at[pl.ds(shard*per+4*part+cc*4*part,4*part)]
    own_a=own_w.at[pl.ds((x*2+c)*part,part)]
    own_b=own_w.at[pl.ds(4*part+c*4*part,4*part)]
    me=z*2+y
    core=dev(z,y,x,1-c); across=dev(z,y,1-x,c); beside=dev(z,1-y,x,c)
    up=dev(jnp.minimum(z+1,3),y,x,c); down=dev(jnp.maximum(z-1,0),y,x,c)
    def src(shard,own):
        return (own_a,own_b) if own else (a_of(shard,x,c),b_of(shard,c))
    def z_copies(zz,own,go_up):
        shard=zz*2+y
        a,b=src(shard,own)
        d=(z-zz) if go_up else (zz-z)
        k=0 if go_up else 1
        to=up if go_up else down
        return (rcopy(a,a_of(shard,x,c),zs.at[k,d,0],zr.at[k,d,0],to),rcopy(b,b_of(shard,c),zs.at[k,d,1],zr.at[k,d,1],to))
    def z_arrivals(zz,k,dist):
        shard=zz*2+y
        a,b=a_of(shard,x,c),b_of(shard,c)
        return (rcopy(a,a,zs.at[k,dist-1,0],zr.at[k,dist-1,0],up),rcopy(b,b,zs.at[k,dist-1,1],zr.at[k,dist-1,1],up))
    def y_copies(zz,own):
        shard=zz*2+y
        a,b=src(shard,own)
        return (rcopy(a,a_of(shard,x,c),ys.at[zz,0],yr.at[zz,0],beside),rcopy(b,b_of(shard,c),ys.at[zz,1],yr.at[zz,1],beside))
    def y_arrivals(zz):
        shard=zz*2+(1-y)
        a,b=a_of(shard,x,c),b_of(shard,c)
        return (rcopy(a,a,ys.at[zz,0],yr.at[zz,0],beside),rcopy(b,b,ys.at[zz,1],yr.at[zz,1],beside))
    def x_copy(shard,own):
        return rcopy(src(shard,own)[0],a_of(shard,x,c),xs.at[shard],xr.at[shard],across)
    def x_arrival(shard):
        a=a_of(shard,1-x,c)
        return rcopy(a,a,xs.at[shard],xr.at[shard],across)
    def c_copies(shard,own):
        a,b=src(shard,own)
        return (rcopy(a,a_of(shard,x,c),cs.at[shard,0],cr.at[shard,0],core),rcopy(b,b_of(shard,c),cs.at[shard,1],cr.at[shard,1],core))
    def c_arrivals(shard):
        a,b=a_of(shard,x,1-c),b_of(shard,1-c)
        return (rcopy(a,a,cs.at[shard,0],cr.at[shard,0],core),rcopy(b,b,cs.at[shard,1],cr.at[shard,1],core))
    def f_copy(shard):
        a=a_of(shard,1-x,c)
        return rcopy(a,a,fs.at[shard],fr.at[shard],core)
    def f_arrival(shard):
        a=a_of(shard,1-x,1-c)
        return rcopy(a,a,fs.at[shard],fr.at[shard],core)
    def start(cps):
        for cp in (cps if isinstance(cps,tuple) else (cps,)): cp.start()
    def got(cps):
        for cp in (cps if isinstance(cps,tuple) else (cps,)): cp.wait_recv()
    def sent(cps):
        for cp in (cps if isinstance(cps,tuple) else (cps,)): cp.wait_send()
    tile=x*2+c
    tok_x=rcopy(own_tok,all_tok.at[tile],ts.at[0],tr.at[0],across)
    tok_c=rcopy(own_tok,all_tok.at[tile],ts.at[1],tr.at[1],core)
    far=all_tok.at[(1-x)*2+c]
    tok_f=rcopy(far,far,ts.at[2],tr.at[2],core)
    near=all_tok.at[x*2+1-c]
    diag=all_tok.at[(1-x)*2+1-c]
    cnts=[rcopy(own_cnt,all_cnt.at[tile],ns.at[i],nr.at[i],to) for i,to in enumerate((across,core,dev(z,y,1-x,1-c)))]
    cnt_in=[rcopy(r,r,ns.at[i],nr.at[i],core) for i,r in enumerate((all_cnt.at[(1-x)*2+c],all_cnt.at[x*2+1-c],all_cnt.at[(1-x)*2+1-c]))]
    local=(pltpu.make_async_copy(own_w,all_w.at[pl.ds(me*per,per)],ls.at[0]),
           pltpu.make_async_copy(own_tok,all_tok.at[tile],ls.at[1]),pltpu.make_async_copy(own_cnt,all_cnt.at[tile],ls.at[2]))
    @pl.when(z<3)
    def _(): start(z_copies(z,True,True))
    @pl.when(z>0)
    def _(): start(z_copies(z,True,False))
    start(y_copies(z,True)); start(tok_x); start(tok_c)
    for cp in cnts: cp.start()
    for cp in local: cp.start()
    def from_line(k,dist):
        zz=z-dist if k==0 else z+dist
        there=(zz>=0) if k==0 else (zz<=3)
        @pl.when(there)
        def _():
            got(z_arrivals(zz,k,dist))
            @pl.when((z<3) if k==0 else (z>0))
            def _(): start(z_copies(zz,False,k==0))
            start(y_copies(zz,False)); start(x_copy(zz*2+y,False)); start(c_copies(zz*2+y,False))
    def from_beside(zz):
        got(y_arrivals(zz))
        s=zz*2+1-y
        start(x_copy(s,False)); start(c_copies(s,False))
    def guarded(f,dist):
        @pl.when(z-dist>=0)
        def _(): f(z-dist)
        @pl.when(z+dist<=3)
        def _(): f(z+dist)
    def from_across(shard):
        got(x_arrival(shard)); start(f_copy(shard))
    from_line(0,1); from_line(1,1)
    from_beside(z)
    from_line(0,2); from_line(1,2)
    guarded(from_beside,1); guarded(lambda zz: from_across(zz*2+y),1); from_across(z*2+1-y)
    from_line(0,3); from_line(1,3)
    got(tok_x); tok_f.start()
    guarded(from_beside,2); guarded(lambda zz: from_across(zz*2+y),2); guarded(lambda zz: from_across(zz*2+1-y),1)
    guarded(from_beside,3); guarded(lambda zz: from_across(zz*2+y),3); guarded(lambda zz: from_across(zz*2+1-y),2)
    guarded(lambda zz: from_across(zz*2+1-y),3)
    def drain(s,_):
        @pl.when(s!=me)
        def _():
            got(c_arrivals(s)); got(f_arrival(s)); sent(c_copies(s,False)); sent(f_copy(s)); sent(x_copy(s,False))
        return 0
    lax.fori_loop(0,8,drain,0)
    def drain_y(zz,_):
        sent(y_copies(zz,False)); return 0
    lax.fori_loop(0,4,drain_y,0)
    for dist in range(4):
        @pl.when(jnp.logical_and(z<3,z-dist>=0))
        def _(): sent(z_copies(z-dist,False,True))
        @pl.when(jnp.logical_and(z>0,z+dist<=3))
        def _(): sent(z_copies(z+dist,False,False))
    rcopy(near,near,ts.at[1],tr.at[1],core).wait_recv()
    rcopy(diag,diag,ts.at[2],tr.at[2],core).wait_recv()
    tok_x.wait_send(); tok_c.wait_send(); tok_f.wait_send()
    for cp in cnts: cp.wait_send()
    for cp in cnt_in: cp.wait_recv()
    for cp in local: cp.wait()

def gather_all(own_w,own_tok,own_cnt):
    DS=pltpu.SemaphoreType.DMA
    hbm=pl.BlockSpec(memory_space=pl.ANY)
    return pl.pallas_call(gather_kernel,
        out_shape=[jax.ShapeDtypeStruct((8*own_w.shape[0],)+own_w.shape[1:],bf),jax.ShapeDtypeStruct((4,)+own_tok.shape,bf),jax.ShapeDtypeStruct((4,)+own_cnt.shape,own_cnt.dtype)],
        in_specs=[pl.BlockSpec(memory_space=pltpu.VMEM)]*3,out_specs=[hbm]*3,
        scratch_shapes=[DS((2,4,2)),DS((2,4,2)),DS((4,2)),DS((4,2)),DS((8,)),DS((8,)),DS((8,2)),DS((8,2)),DS((8,)),DS((8,)),DS((3,)),DS((3,)),DS((3,)),DS((3,)),DS((3,))],
        compiler_params=pltpu.CompilerParams(has_side_effects=True,vmem_limit_bytes=60<<20),name="gather_weights_tokens")(own_w,own_tok,own_cnt)

def exchange_kernel(a_ref,o_ref,ss,rs):
    dp=lax.axis_index("dp"); t=lax.axis_index("tile")
    n=a_ref.shape[0]
    def out(k):
        p=(t+k)%n
        return rcopy(a_ref.at[p],o_ref.at[t],ss.at[k],rs.at[k],(dp,p))
    def arrive(k):
        q=(t-k+n)%n
        return rcopy(o_ref.at[q],o_ref.at[q],ss.at[k],rs.at[k],(dp,q))
    for k in range(n-1,0,-1): out(k).start()
    o_ref[t]=a_ref[t]
    for k in range(1,n): arrive(k).wait_recv()
    for k in range(1,n): out(k).wait_send()

def exchange(a):
    DS=pltpu.SemaphoreType.DMA
    n=a.shape[0]
    vm=pl.BlockSpec(memory_space=pltpu.VMEM)
    return pl.pallas_call(exchange_kernel,out_shape=jax.ShapeDtypeStruct(a.shape,a.dtype),in_specs=[vm],out_specs=vm,
        scratch_shapes=[DS((n,)),DS((n,))],compiler_params=pltpu.CompilerParams(has_side_effects=True,vmem_limit_bytes=60<<20),name="exchange_over_tile")(a)

def totals_kernel(v_ref,g_ref,vo_ref,go_ref,vt,vd,gd,ts,tr,ds,dr,gs,gr):
    dp=lax.axis_index("dp"); t=lax.axis_index("tile")
    nt,nd=vt.shape[0],vd.shape[0]
    def g_copy(k):
        p=(dp+k)%nd
        return rcopy(gd.at[dp],gd.at[dp],gs.at[k],gr.at[k],(p,t))
    def g_arrive(k):
        q=(dp-k+nd)%nd
        return rcopy(gd.at[q],gd.at[q],gs.at[k],gr.at[k],(q,t))
    def t_copy(k):
        p=(t+k)%nt
        return rcopy(vt.at[t],vt.at[t],ts.at[k],tr.at[k],(dp,p))
    def t_arrive(k):
        q=(t-k+nt)%nt
        return rcopy(vt.at[q],vt.at[q],ts.at[k],tr.at[k],(dp,q))
    def d_copy(k):
        p=(dp+k)%nd
        return rcopy(vd.at[dp],vd.at[dp],ds.at[k],dr.at[k],(p,t))
    def d_arrive(k):
        q=(dp-k+nd)%nd
        return rcopy(vd.at[q],vd.at[q],ds.at[k],dr.at[k],(q,t))
    def loop(n,f):
        def s(k,_):
            f(k); return 0
        lax.fori_loop(1,n,s,0)
    vt[t]=v_ref[...]
    gd[dp]=g_ref[...]
    loop(nt,lambda k: t_copy(k).start())
    loop(nd,lambda k: g_copy(k).start())
    loop(nt,lambda k: t_arrive(k).wait_recv())
    acc=vt[0]
    for i in range(1,nt): acc=acc+vt[i]
    vd[dp]=acc
    loop(nd,lambda k: d_copy(k).start())
    loop(nd,lambda k: g_arrive(k).wait_recv())
    acc=gd[0]
    for i in range(1,nd): acc=acc+gd[i]
    go_ref[...]=acc
    loop(nd,lambda k: d_arrive(k).wait_recv())
    acc=vd[0]
    for i in range(1,nd): acc=acc+vd[i]
    vo_ref[...]=acc
    loop(nt,lambda k: t_copy(k).wait_send())
    loop(nd,lambda k: g_copy(k).wait_send())
    loop(nd,lambda k: d_copy(k).wait_send())

def totals(v,g,nd,nt):
    DS=pltpu.SemaphoreType.DMA
    vm=pl.BlockSpec(memory_space=pltpu.VMEM)
    return pl.pallas_call(totals_kernel,out_shape=[jax.ShapeDtypeStruct(v.shape,f32),jax.ShapeDtypeStruct(g.shape,f32)],in_specs=[vm]*2,out_specs=[vm]*2,
        scratch_shapes=[pltpu.VMEM((nt,)+v.shape,f32),pltpu.VMEM((nd,)+v.shape,f32),pltpu.VMEM((nd,)+g.shape,f32),DS((nt,)),DS((nt,)),DS((nd,)),DS((nd,)),DS((nd,)),DS((nd,))],
        compiler_params=pltpu.CompilerParams(has_side_effects=True,vmem_limit_bytes=60<<20),name="sum_small")(v,g)

def grad_sum_kernel(a_ref,o_ref,mine,xb0,yb0,zin,xb1,yb1,zin1,zin2,yb2,xb2,cs,cr,ss,rs,zs,zr,fs,fr):
    z,y,x,c=where_am_i()
    core=dev(z,y,x,1-c); across=dev(z,y,1-x,c); beside=dev(z,1-y,x,c)
    up=dev(jnp.minimum(z+1,3),y,x,c); down=dev(jnp.maximum(z-1,0),y,x,c)
    other=(1-c)*12; own=c*12
    def c_copy(p,d):
        return rcopy(a_ref.at[d,pl.ds(other+p*4,4)],mine.at[p,d],cs.at[p,d],cr.at[p,d],core)
    order=(2,0,1)
    def go(p):
        def s(d,_):
            c_copy(p,d).start(); return 0
        lax.fori_loop(0,8,s,0)
    for p in order: go(p)
    def add_own(p):
        def s(d,_):
            c_copy(p,d).wait_recv()
            for b in range(4):
                mine[p,d,b]=(mine[p,d,b].astype(f32)+a_ref[d,own+p*4+b].astype(f32)).astype(bf)
            return 0
        lax.fori_loop(0,8,s,0)
    def add(dst,src):
        n=dst.shape[0]
        for i in range(n): dst[i]=(dst[i].astype(f32)+src[i].astype(f32)).astype(bf)
    def line(buf_of,inbox,sem):
        def cp(tz,go_down):
            k=1 if go_down else 0
            return rcopy(buf_of(tz),inbox.at[k,tz],zs.at[sem,k,tz],zr.at[sem,k,tz],down if go_down else up)
        def arrive(tz,go_down):
            k=1 if go_down else 0
            return rcopy(inbox.at[k,tz],inbox.at[k,tz],zs.at[sem,k,tz],zr.at[sem,k,tz],down)
        return cp,arrive
    def line_start(cp):
        @pl.when(z==3)
        def _(): cp(0,True).start()
        @pl.when(z==0)
        def _(): cp(3,False).start()
    def line_pass(cp,arrive,buf_of,inbox,addf):
        for tz in (0,1):
            @pl.when(z==3)
            def _():
                cp(tz,True).wait_send(); cp(tz+1,True).start()
            @pl.when(z==0)
            def _():
                cp(3-tz,False).wait_send(); cp(2-tz,False).start()
        for tz in (0,1,2):
            @pl.when(jnp.logical_and(z<3,z>tz))
            def _():
                arrive(tz,True).wait_recv(); addf(buf_of(tz),inbox.at[1,tz]); cp(tz,True).start()
            u=3-tz
            @pl.when(jnp.logical_and(z>0,z<u))
            def _():
                arrive(u,False).wait_recv(); addf(buf_of(u),inbox.at[0,u]); cp(u,False).start()
    def line_end(cp,arrive,buf_of,inbox,addf):
        @pl.when(z<3)
        def _():
            arrive(z,True).wait_recv(); addf(buf_of(z),inbox.at[1,z])
        @pl.when(z>0)
        def _():
            arrive(z,False).wait_recv(); addf(buf_of(z),inbox.at[0,z])
    def line_sent(cp):
        @pl.when(z==3)
        def _(): cp(2,True).wait_send()
        @pl.when(z==0)
        def _(): cp(1,False).wait_send()
        for tz in (0,1,2):
            @pl.when(jnp.logical_and(z<3,z>tz))
            def _(): cp(tz,True).wait_send()
            @pl.when(jnp.logical_and(z>0,z<3-tz))
            def _(): cp(3-tz,False).wait_send()
    def add2(dst,src):
        for i in range(2):
            for j in range(4): dst[i,j]=(dst[i,j].astype(f32)+src[i,j].astype(f32)).astype(bf)
    p2_of=lambda tz: mine.at[2,pl.ds(tz*2,2)]
    cp2,ar2=line(p2_of,zin,0)
    add_own(2); line_start(cp2)
    def x0(d): return rcopy(mine.at[0,d,pl.ds((1-x)*2,2)],xb0.at[d],ss.at[0,d],rs.at[0,d],across)
    def s0(d,_):
        c_copy(0,d).wait_recv()
        for b in range(4):
            mine[0,d,b]=(mine[0,d,b].astype(f32)+a_ref[d,own+b].astype(f32)).astype(bf)
        x0(d).start()
        return 0
    lax.fori_loop(0,8,s0,0)
    def y1(zz): return rcopy(mine.at[1,zz*2+1-y],yb0.at[zz],ss.at[1,zz],rs.at[1,zz],beside)
    add_own(1)
    for zz in range(4): y1(zz).start()
    line_pass(cp2,ar2,p2_of,zin,add2)
    def p0(zz,yy): return mine.at[0,zz*2+yy,pl.ds(x*2,2)]
    def y0(zz): return rcopy(p0(zz,1-y),yb1.at[zz],ss.at[2,zz],rs.at[2,zz],beside)
    for zz in range(4):
        for yy in range(2):
            d=zz*2+yy
            x0(d).wait_recv(); add(p0(zz,yy),xb0.at[d])
        y0(zz).start()
    def p1(zz): return mine.at[1,zz*2+y]
    def x1(zz): return rcopy(mine.at[1,zz*2+y,pl.ds((1-x)*2,2)],xb1.at[zz],ss.at[3,zz],rs.at[3,zz],across)
    for zz in range(4):
        y1(zz).wait_recv(); add(p1(zz),yb0.at[zz]); x1(zz).start()
    q0=lambda tz: mine.at[0,tz*2+y,pl.ds(x*2,2)]
    cp0,ar0=line(q0,zin1,1)
    q1=lambda tz: mine.at[1,tz*2+y,pl.ds(x*2,2)]
    cp1,ar1=line(q1,zin2,2)
    for zz in range(4):
        y0(zz).wait_recv(); add(q0(zz),yb1.at[zz])
    line_start(cp0)
    line_end(cp2,ar2,p2_of,zin,add2)
    y2=rcopy(mine.at[2,z*2+1-y],yb2,ss.at[4,0],rs.at[4,0],beside)
    y2.start()
    for zz in range(4):
        x1(zz).wait_recv(); add(q1(zz),xb1.at[zz])
    line_start(cp1)
    line_pass(cp0,ar0,q0,zin1,add)
    y2.wait_recv(); add(mine.at[2,z*2+y],yb2)
    x2=rcopy(mine.at[2,z*2+y,pl.ds((1-x)*2,2)],xb2,ss.at[5,0],rs.at[5,0],across)
    x2.start()
    line_pass(cp1,ar1,q1,zin2,add)
    x2.wait_recv()
    me=z*2+y
    add(mine.at[2,me,pl.ds(x*2,2)],xb2)
    def place(xx,cc,p): return o_ref.at[pl.ds(cc*12+p*4+xx*2,2)]
    def f_copy(i,p):
        if i==2: return rcopy(place(1-x,c,p),place(1-x,c,p),fs.at[2,p],fr.at[2,p],core)
        return rcopy(mine.at[p,me,pl.ds(x*2,2)],place(x,c,p),fs.at[i,p],fr.at[i,p],across if i==0 else core)
    def f_arrive(i,p):
        r=(place(1-x,c,p),place(x,1-c,p),place(1-x,1-c,p))[i]
        return rcopy(r,r,fs.at[i,p],fr.at[i,p],core)
    def finish(p):
        o_ref[pl.ds(own+p*4+x*2,2)]=mine[p,me,pl.ds(x*2,2)]
        for i in range(2): f_copy(i,p).start()
    finish(2)
    line_end(cp0,ar0,q0,zin1,add); finish(0)
    line_end(cp1,ar1,q1,zin2,add); finish(1)
    for p in (2,0,1):
        f_arrive(0,p).wait_recv(); f_copy(2,p).start()
    for p in range(3):
        f_arrive(1,p).wait_recv(); f_arrive(2,p).wait_recv()
    for p in range(3):
        for i in range(3): f_copy(i,p).wait_send()
    def drain(d,_):
        for p in range(3): c_copy(p,d).wait_send()
        x0(d).wait_send()
        return 0
    lax.fori_loop(0,8,drain,0)
    for zz in range(4):
        y1(zz).wait_send(); y0(zz).wait_send(); x1(zz).wait_send()
    y2.wait_send(); x2.wait_send()
    line_sent(cp2); line_sent(cp0); line_sent(cp1)

def grad_sum(a):
    DS=pltpu.SemaphoreType.DMA
    R=a.shape[2]
    vm=pl.BlockSpec(memory_space=pltpu.VMEM)
    V=lambda *s: pltpu.VMEM(s+(R,128),bf)
    return pl.pallas_call(grad_sum_kernel,out_shape=jax.ShapeDtypeStruct((24,R,128),bf),in_specs=[vm],out_specs=vm,
        scratch_shapes=[V(3,8,4),V(8,2),V(4,4),V(2,4,2,4),V(4,2),V(4,2),V(2,4,2),V(2,4,2),V(4),V(2),
            DS((3,8)),DS((3,8)),DS((6,8)),DS((6,8)),DS((3,2,4)),DS((3,2,4)),DS((3,3)),DS((3,3))],
        cost_estimate=pl.CostEstimate(flops=10**7,bytes_accessed=200*10**6,transcendentals=0),
        compiler_params=pltpu.CompilerParams(has_side_effects=True,vmem_limit_bytes=60<<20),name="sum_gradients")(a)


H = 12
NGRP = 16
STEP = 10
EPS_NORM = 1e-06
BETA_ONE = 0.5
BETA_TWO = 0.5
ADAM_EPS = 1e-08
RATE_BLOCK = 0.3
RATE_VECTOR = 0.2
NEG_RAW = -8.0e9
HEAD = 64
SCALE = 1.0 / math.sqrt(HEAD)
EXP2 = SCALE * math.log2(math.e)
NN = (((1,), (0,)), ((), ()))
NT = (((1,), (1,)), ((), ()))
TN = (((0,), (0,)), ((), ()))


def mm(a, b, dims=NN):
    return lax.dot_general(a, b, dims, preferred_element_type=f32)


def column_sum(v):
    return jnp.sum(v, axis=0, keepdims=True)


def vmem_spec():
    return pl.BlockSpec(memory_space=pltpu.VMEM)


def smem_spec():
    return pl.BlockSpec(memory_space=pltpu.SMEM)


def any_spec():
    return pl.BlockSpec(memory_space=pl.ANY)


def params(mib=60):
    return pltpu.CompilerParams(vmem_limit_bytes=mib << 20)


def pack(block, odd):
    half = block.shape[0] // 2
    left, right = block[:, :64], block[:, 128:]
    even_tail = jnp.concatenate([right[:half], right[half:]], axis=1)
    odd_tail = jnp.concatenate([left[half:], left[:half]], axis=1)
    return jnp.where(odd, block[:, 64:], block[:, :128]), jnp.where(odd, odd_tail, even_tail)


def unpack(top, tail, odd):
    first, second = tail[:, :64], tail[:, 64:]
    even = jnp.concatenate([top, jnp.concatenate([first, second], axis=0)], axis=1)
    return jnp.where(odd, jnp.concatenate([jnp.concatenate([second, first], axis=0), top], axis=1), even)


def turn(v):
    return jnp.concatenate([v[:, 64:], v[:, :64]], axis=1)


def group_of(n):
    return 4 if n % 4 == 0 else 3 if n % 3 == 0 else 1


def pack_kernel(odd_ref, m_ref, p_ref, s_ref):
    g = m_ref.shape[0]
    for b in range(g):
        m = m_ref[b]
        top, tail = pack(m, odd_ref[pl.program_id(0) * g + b] == 1)
        p_ref[b, :192] = top.astype(bf)
        p_ref[b, 192:] = tail.astype(bf)
        s_ref[b] = jnp.full((8, 128), jnp.sum(m * m), f32)


def pack_master(odd, master):
    n = master.shape[0]
    g = group_of(n)
    at = lambda i, s: (i, 0, 0)
    spec = pltpu.PrefetchScalarGridSpec(
        num_scalar_prefetch=1,
        grid=(n // g,),
        in_specs=[pl.BlockSpec((g, 192, 192), at)],
        out_specs=[pl.BlockSpec((g, 288, 128), at), pl.BlockSpec((g, 8, 128), at)],
    )
    return pl.pallas_call(
        pack_kernel,
        grid_spec=spec,
        out_shape=[jax.ShapeDtypeStruct((n, 288, 128), bf), jax.ShapeDtypeStruct((n, 8, 128), f32)],
        compiler_params=params(),
        name="pack_master",
    )(odd, master)


def qkv_kernel(src_ref, cnt_ref, at_ref, x0, x1, x2, x3, blk_ref, gain_ref, shift_ref, bq_ref, bv_ref, a_ref, q_ref, qt_ref, k_ref, kt_ref, v_ref, vt_ref, w_ref, st_ref, buf, sems):
    i = pl.program_id(0)

    @pl.when(i == 0)
    def _():
        copies = [pltpu.make_async_copy(blk_ref.at[at_ref[j]], buf.at[j], sems.at[j]) for j in range(12)]
        for copy in copies:
            copy.start()
        odd = at_ref[12] == 1
        for r in range(4):
            parts = []
            for c in range(3):
                copies[r * 3 + c].wait()
                p = buf[r * 3 + c].astype(f32)
                parts.append(unpack(p[:192], p[192:], odd))
            w_ref[r * 192 : (r + 1) * 192, :] = jnp.concatenate(parts, axis=1).astype(bf)

    x = jnp.concatenate([r[...] for r in (x0, x1, x2, x3)], axis=0).astype(f32)
    mean = jnp.mean(x, axis=-1, keepdims=True)
    cen = x - mean
    inv_std = lax.rsqrt(jnp.mean(cen * cen, axis=-1, keepdims=True) + EPS_NORM)
    a = (cen * inv_std * gain_ref[...] + shift_ref[...]).astype(bf)
    a_ref[...] = a
    qkv = mm(a, w_ref[...])
    q = (qkv[:, :192] + bq_ref[...]).astype(bf).astype(f32)
    k = qkv[:, 192:384].astype(bf).astype(f32)
    v = (qkv[:, 384:] + bv_ref[...]).astype(bf).astype(f32)
    row = lax.broadcasted_iota(jnp.int32, (128, 64), 0)
    lane = lax.broadcasted_iota(jnp.int32, (512, 64), 1)
    masked = jnp.concatenate(
        [jnp.where(row < cnt_ref[4 * i + b], 0.0, NEG_RAW) for b in range(4)], axis=0
    )
    ones = jnp.where(lane < 4, 1.0, 0.0)
    k_tail = jnp.where(lane == 0, masked, ones)
    v_tail = jnp.where(lane < 3, 1.0, 0.0)
    zero = jnp.zeros((512, 64), f32)
    sub = lax.broadcasted_iota(jnp.int32, (64, 512), 0)
    t_tail = jnp.where(sub < 1, 1.0, 0.0)
    qt, kt, vt = q.T, k.T, v.T
    longest = lambda a: jnp.max(jnp.concatenate([column_sum(a[h * 64 : (h + 1) * 64] ** 2) for h in range(3)], axis=0))
    st_ref[0] = jnp.where(lax.broadcasted_iota(jnp.int32, (8, 128), 0) == 0, longest(qt), longest(kt))
    for h in range(3):
        s = slice(h * 64, (h + 1) * 64)
        q_ref[h] = jnp.concatenate([q[:, s], zero], axis=1).astype(bf)
        k_ref[h] = jnp.concatenate([k[:, s], k_tail], axis=1).astype(bf)
        v_ref[h] = jnp.concatenate([v[:, s], v_tail], axis=1).astype(bf)
        qt_ref[h] = jnp.concatenate([qt[s], t_tail], axis=0).astype(bf)
        kt_ref[h] = kt[s].astype(bf)
        vt_ref[h] = jnp.concatenate([vt[s], t_tail[:16]], axis=0).astype(bf)


def qkv_forward(src, cnt, own_at, tokens, blocks, gain, shift, bq, bv):
    n = tokens.shape[0]
    rows = [pl.BlockSpec((128, 768), lambda i, s, c, o, k=k: (s[4 * i + k], 0)) for k in range(4)]
    row = lambda i, s, c, o: (0, 0)
    spec = pltpu.PrefetchScalarGridSpec(
        num_scalar_prefetch=3,
        grid=(n // 512,),
        in_specs=rows
        + [any_spec(), pl.BlockSpec((1, 768), row), pl.BlockSpec((1, 768), row), pl.BlockSpec((1, 192), row), pl.BlockSpec((1, 192), row)],
        out_specs=[
            pl.BlockSpec((512, 768), lambda i, s, c, o: (i, 0)),
            pl.BlockSpec((3, 512, 128), lambda i, s, c, o: (0, i, 0)),
            pl.BlockSpec((3, 128, 512), lambda i, s, c, o: (0, 0, i)),
            pl.BlockSpec((3, 512, 128), lambda i, s, c, o: (0, i, 0)),
            pl.BlockSpec((3, 64, 512), lambda i, s, c, o: (0, 0, i)),
            pl.BlockSpec((3, 512, 128), lambda i, s, c, o: (0, i, 0)),
            pl.BlockSpec((3, 80, 512), lambda i, s, c, o: (0, 0, i)),
            pl.BlockSpec((768, 576), row),
            pl.BlockSpec((1, 8, 128), lambda i, s, c, o: (i, 0, 0)),
        ],
        scratch_shapes=[pltpu.VMEM((12, 288, 128), bf), pltpu.SemaphoreType.DMA((12,))],
    )
    shapes = [(n, 768), (3, n, 128), (3, 128, n), (3, n, 128), (3, 64, n), (3, n, 128), (3, 80, n), (768, 576)]
    return pl.pallas_call(
        qkv_kernel,
        grid_spec=spec,
        out_shape=[jax.ShapeDtypeStruct(s, bf) for s in shapes] + [jax.ShapeDtypeStruct((n // 512, 8, 128), f32)],
        compiler_params=params(),
        name="norm_and_qkv",
    )(src, cnt, own_at, tokens, tokens, tokens, tokens, blocks, gain, shift, bq, bv)


def split3(v):
    a = v.astype(bf).astype(f32)
    b = (v - a).astype(bf).astype(f32)
    return a, b, v - a - b


def in_steps(units, sizes, body, carry):
    at = 0
    for size in sizes:
        count = (units - at) // size
        carry = lax.fori_loop(0, count, lambda i, c, at=at, size=size: body(at + i * size, size, c), carry)
        at = at + count * size
    return carry


def attend_kernel(bq, n_ref, k_ref, qt_ref, vt_ref, ot_ref, qb_ref):
    live = n_ref[0]
    qi = pl.program_id(1)
    units = (live + 3) // 4

    def finish(top, acc):
        total = acc[64:65]
        ot_ref[0] = acc[:64] / total
        a, b, c = split3((top + jnp.log2(total)) * (-1.0 / EXP2))
        row = lax.broadcasted_iota(jnp.int32, (64, bq), 0)
        tail = jnp.where(row == 0, 1.0, jnp.where(row == 1, a, jnp.where(row == 2, b, jnp.where(row == 3, c, 0.0))))
        qb_ref[0, :64] = qt_ref[0, :64]
        qb_ref[0, 64:] = tail.astype(bf)

    def keys(u, size):
        return pl.ds(pl.multiple_of(u * 512, 512), size * 512)

    @pl.when(jnp.logical_and(qi * bq < live * 128, n_ref[1] == 1))
    def _():
        qt = qt_ref[0]

        def body(u, size, acc):
            for part in range(size):
                at = keys(u + part, 1)
                p = jnp.exp2(mm(k_ref[0, at, :], qt) * EXP2).astype(bf)
                acc = acc + mm(vt_ref[0, :, at], p)
            return acc

        finish(0.0, in_steps(units, (4, 2, 1), body, jnp.zeros((80, bq), f32)))

    @pl.when(jnp.logical_and(qi * bq < live * 128, n_ref[1] == 0))
    def _():
        qt = qt_ref[0]

        def body(u, size, carry):
            top, acc = carry
            s = mm(k_ref[0, keys(u, size), :], qt) * EXP2
            new = jnp.maximum(top, jnp.max(s, axis=0, keepdims=True))
            p = jnp.exp2(s - new).astype(bf)
            return new, acc * jnp.exp2(top - new) + mm(vt_ref[0, :, keys(u, size)], p)

        finish(*in_steps(units, (2, 1), body, (jnp.full((1, bq), -3e38, f32), jnp.zeros((80, bq), f32))))


def attend(live, k, qt, vt, bq=1024):
    n = k.shape[1]
    spec = pltpu.PrefetchScalarGridSpec(
        num_scalar_prefetch=1,
        grid=(3, n // bq),
        in_specs=[
            pl.BlockSpec((1, n, 128), lambda h, i, s: (h, 0, 0)),
            pl.BlockSpec((1, 128, bq), lambda h, i, s: (h, 0, i)),
            pl.BlockSpec((1, 80, n), lambda h, i, s: (h, 0, 0)),
        ],
        out_specs=[pl.BlockSpec((1, 64, bq), lambda h, i, s: (h, 0, i)), pl.BlockSpec((1, 128, bq), lambda h, i, s: (h, 0, i))],
    )
    return pl.pallas_call(
        functools.partial(attend_kernel, bq),
        grid_spec=spec,
        out_shape=[jax.ShapeDtypeStruct((3, 64, n), f32), jax.ShapeDtypeStruct((3, 128, n), bf)],
        compiler_params=params(),
        name="attention_forward",
    )(live, k, qt, vt)


def spread_kernel(src_ref, n_ref, ot_ref, o_ref):
    live = n_ref[0]
    per = o_ref.shape[2] // 128

    def step(b, _):
        g = src_ref[b]
        lanes = pl.ds(pl.multiple_of(b * 128, 128), 128)
        to = pl.ds(pl.multiple_of((g % per) * 128, 128), 128)

        @pl.when(b < live)
        def _():
            for h in range(3):
                o_ref[g // per, h * 64 : (h + 1) * 64, to] = ot_ref[h, :, lanes].astype(bf)

        @pl.when(b >= live)
        def _():
            o_ref[g // per, :, to] = jnp.zeros((192, 128), bf)

        return 0

    lax.fori_loop(0, ot_ref.shape[2] // 128, step, 0)


def spread(src, live, ot, tiles):
    n = ot.shape[2]
    return pl.pallas_call(
        spread_kernel,
        in_specs=[smem_spec(), smem_spec(), vmem_spec()],
        out_specs=vmem_spec(),
        out_shape=jax.ShapeDtypeStruct((tiles, 192, n // tiles), bf),
        compiler_params=params(),
        name="spread_attended",
    )(src, live, ot)


def collect_kernel(src_ref, n_ref, g_ref, ot_ref, dt_ref, d_ref):
    live = n_ref[0]
    per = g_ref.shape[2] // 128
    row = lax.broadcasted_iota(jnp.int32, (64, 128), 0)

    def step(b, _):
        g = src_ref[b]
        to = pl.ds(pl.multiple_of(b * 128, 128), 128)
        lanes = pl.ds(pl.multiple_of((g % per) * 128, 128), 128)

        @pl.when(b < live)
        def _():
            for h in range(3):
                d = g_ref[g // per, h * 64 : (h + 1) * 64, lanes].astype(f32)
                delta = jnp.sum(d * ot_ref[h, :, to], axis=0, keepdims=True)
                x, y, z = split3(-delta)
                tail = jnp.where(row == 0, x, jnp.where(row == 1, y, jnp.where(row == 2, z, 0.0)))
                both = jnp.concatenate([d, tail], axis=0)
                dt_ref[h, :, to] = both.astype(bf)
                d_ref[h, to, :] = jnp.concatenate([d, jnp.zeros_like(d)], axis=0).T.astype(bf)

        @pl.when(b >= live)
        def _():
            dt_ref[:, :, to] = jnp.zeros((3, 128, 128), bf)
            d_ref[:, to, :] = jnp.zeros((3, 128, 128), bf)

        return 0

    lax.fori_loop(0, ot_ref.shape[2] // 128, step, 0)


def collect(src, live, grad, ot):
    n = ot.shape[2]
    return pl.pallas_call(
        collect_kernel,
        in_specs=[smem_spec(), smem_spec(), vmem_spec(), vmem_spec()],
        out_specs=[vmem_spec()] * 2,
        out_shape=[jax.ShapeDtypeStruct((3, 128, n), bf), jax.ShapeDtypeStruct((3, n, 128), bf)],
        compiler_params=params(),
        name="collect_attended_grad",
    )(src, live, grad, ot)


def attend_back_kernel(bk, n_ref, k_ref, kt_ref, v_ref, qb_ref, q_ref, dt_ref, d_ref, dq_ref, dk_ref, dv_ref):
    live = n_ref[0]
    j = pl.program_id(1)

    @pl.when(j == 0)
    def _():
        dq_ref[...] = jnp.zeros_like(dq_ref)

    @pl.when(j * bk < live * 128)
    def _():
        k, v, kt = k_ref[0], v_ref[0], kt_ref[0]

        def body(u, size, carry):
            dk, dv = carry

            def lanes(part):
                return pl.ds(pl.multiple_of((u * 2 + part) * 256, 256), 256)

            def products(part):
                return mm(k, qb_ref[0, :, lanes(part)]), mm(v, dt_ref[0, :, lanes(part)])

            s, dp = products(0)
            for part in range(2 * size):
                ahead = products(part + 1) if part + 1 < 2 * size else None
                p = jnp.exp2(s * EXP2)
                ds = (p * dp).astype(bf)
                dv = dv + mm(p.astype(bf), d_ref[0, lanes(part), :])
                dk = dk + mm(ds, q_ref[0, lanes(part), :])
                dq_ref[0, :, lanes(part)] += mm(kt, ds)
                s, dp = ahead or (s, dp)
            return dk, dv

        zero = jnp.zeros((bk, 128), f32)
        dk, dv = in_steps((live + 3) // 4, (4, 2, 1), body, (zero, zero))
        dk_ref[0] = (dk * SCALE).astype(bf)
        dv_ref[0] = dv.astype(bf)


def attend_back(live, k, kt, v, qb, q, dt, d, bk=512):
    n = k.shape[1]
    whole_t = lambda h, j, s: (h, 0, 0)
    spec = pltpu.PrefetchScalarGridSpec(
        num_scalar_prefetch=1,
        grid=(3, n // bk),
        in_specs=[
            pl.BlockSpec((1, bk, 128), lambda h, j, s: (h, j, 0)),
            pl.BlockSpec((1, 64, bk), lambda h, j, s: (h, 0, j)),
            pl.BlockSpec((1, bk, 128), lambda h, j, s: (h, j, 0)),
            pl.BlockSpec((1, 128, n), whole_t),
            pl.BlockSpec((1, n, 128), whole_t),
            pl.BlockSpec((1, 128, n), whole_t),
            pl.BlockSpec((1, n, 128), whole_t),
        ],
        out_specs=[
            pl.BlockSpec((1, 64, n), whole_t),
            pl.BlockSpec((1, bk, 128), lambda h, j, s: (h, j, 0)),
            pl.BlockSpec((1, bk, 128), lambda h, j, s: (h, j, 0)),
        ],
    )
    return pl.pallas_call(
        functools.partial(attend_back_kernel, bk),
        grid_spec=spec,
        out_shape=[jax.ShapeDtypeStruct((3, 64, n), f32), jax.ShapeDtypeStruct((3, n, 128), bf), jax.ShapeDtypeStruct((3, n, 128), bf)],
        compiler_params=params(),
        name="attention_backward",
    )(live, k, kt, v, qb, q, dt, d)


def qkv_back_kernel(src_ref, n_ref, at_ref, dq_ref, dk_ref, dv_ref, a_ref, w_ref, s_in, g_ref, s_ref, gb_ref, acc, sums, rows, packed, sems, psems):
    i = pl.program_id(0)
    live = n_ref[0]

    @pl.when(i == 0)
    def _():
        acc[...] = jnp.zeros_like(acc)
        sums[...] = jnp.zeros_like(sums)

    @pl.when(4 * i < live)
    def _():
        dq = jnp.concatenate([dq_ref[h] for h in range(3)], axis=0).T * SCALE
        g = jnp.concatenate(
            [dq] + [dk_ref[h][:, :64].astype(f32) for h in range(3)] + [dv_ref[h][:, :64].astype(f32) for h in range(3)], axis=1
        ).astype(bf)
        acc[...] += mm(a_ref[...], g, TN)
        sums[...] += jnp.broadcast_to(jnp.sum(g.astype(f32), axis=0, keepdims=True), sums.shape)
        rows[...] = mm(g, w_ref[...], NT).astype(bf)

    @pl.when(4 * i >= live)
    def _():
        rows[...] = jnp.zeros_like(rows)

    copies = [
        pltpu.make_async_copy(rows.at[pl.ds(b * 128, 128)], g_ref.at[pl.ds(pl.multiple_of(src_ref[4 * i + b] * 128, 128), 128)], sems.at[b])
        for b in range(4)
    ]
    for copy in copies:
        copy.start()
    for copy in copies:
        copy.wait()

    @pl.when(i == pl.num_programs(0) - 1)
    def _():
        out = []
        for r in range(4):
            for c in range(3):
                j = r * 3 + c
                top, tail = pack(acc[r * 192 : (r + 1) * 192, c * 192 : (c + 1) * 192], at_ref[12] == 1)
                packed[j, :192] = top.astype(bf)
                packed[j, 192:] = tail.astype(bf)
                out.append(pltpu.make_async_copy(packed.at[j], s_ref.at[at_ref[j]], psems.at[j]))
                out[-1].start()
        gb_ref[...] = sums[...]
        for copy in out:
            copy.wait()


def qkv_backward(src, live, own_at, dq, dk, dv, a, w, slots):
    n = a.shape[0]
    spec = pltpu.PrefetchScalarGridSpec(
        num_scalar_prefetch=3,
        grid=(n // 512,),
        in_specs=[
            pl.BlockSpec((3, 64, 512), lambda i, s, c, o: (0, 0, i)),
            pl.BlockSpec((3, 512, 128), lambda i, s, c, o: (0, i, 0)),
            pl.BlockSpec((3, 512, 128), lambda i, s, c, o: (0, i, 0)),
            pl.BlockSpec((512, 768), lambda i, s, c, o: (i, 0)),
            pl.BlockSpec((768, 576), lambda i, s, c, o: (0, 0)),
            any_spec(),
        ],
        out_specs=[any_spec(), any_spec(), pl.BlockSpec((8, 576), lambda i, s, c, o: (0, 0))],
        scratch_shapes=[
            pltpu.VMEM((768, 576), f32),
            pltpu.VMEM((8, 576), f32),
            pltpu.VMEM((512, 768), bf),
            pltpu.VMEM((12, 288, 128), bf),
            pltpu.SemaphoreType.DMA((4,)),
            pltpu.SemaphoreType.DMA((12,)),
        ],
    )
    return pl.pallas_call(
        qkv_back_kernel,
        grid_spec=spec,
        out_shape=[jax.ShapeDtypeStruct((n, 768), bf), jax.ShapeDtypeStruct(slots.shape, bf), jax.ShapeDtypeStruct((8, 576), f32)],
        input_output_aliases={8: 1},
        compiler_params=params(),
        name="qkv_backward",
    )(src, live, own_at, dq, dk, dv, a, w, slots)


def gelu_parts(z):
    cdf = 0.5 + 0.5 * lax.erf(z * math.sqrt(0.5))
    return z * cdf, cdf + z * (jnp.exp2(z * z * (-0.5 * math.log2(math.e))) * (1.0 / math.sqrt(2.0 * math.pi)))


def middle_kernel(inv_ref, cnt_ref, blk_ref, o_ref, x_ref, c_ref, vp_ref, bu_ref, y_ref, gr_ref, go_ref, s_ref, vs_ref, us_ref,
                  w_out, w_up, w_down, tails, u_s, gz_s, a2_s, gm_s, gb_s, o_s, ring, zero, tsem, isem, osem, zsem):
    i = pl.program_id(0)
    rows = x_ref.shape[0]
    r0 = pl.multiple_of(i * rows, rows)
    kinds = ((w_out, 48, 2, 4), (w_up, 64, 8, 4), (w_down, 128, 2, 16))

    def zero_copy(j):
        return pltpu.make_async_copy(zero, s_ref.at[inv_ref[j]], zsem.at[j])

    @pl.when(i == 0)
    def _():
        vs_ref[...] = jnp.zeros_like(vs_ref)
        us_ref[...] = jnp.zeros_like(us_ref)
        zero[...] = jnp.zeros_like(zero)

        def pair(w, first, pairs):
            def copies(j):
                r = pl.multiple_of((j // pairs) * 192, 64)
                col = pl.multiple_of((j % pairs) * 384, 128)
                out = []
                for b, off in ((0, 0), (1, 256)):
                    at = first + 2 * j + b
                    slot = inv_ref[at]
                    out.append(pltpu.make_async_copy(blk_ref.at[slot, pl.ds(0, 192)], w.at[pl.ds(r, 192), pl.ds(col + off, 128)], tsem.at[at - 48]))
                    out.append(pltpu.make_async_copy(blk_ref.at[slot, pl.ds(192, 96)], tails.at[at - 48], isem.at[at - 48]))
                return out, r, col

            def start(j, _):
                for copy in copies(j)[0]:
                    copy.start()
                return 0

            def join(j, _):
                got, r, col = copies(j)
                for copy in got:
                    copy.wait()
                even = tails[first + 2 * j - 48].astype(f32)
                odd = tails[first + 2 * j - 47].astype(f32)
                lane = lax.broadcasted_iota(jnp.int32, even.shape, 1) < 64
                w[pl.ds(r, 96), pl.ds(col + 128, 128)] = jnp.where(lane, even, odd).astype(bf)
                w[pl.ds(r + 96, 96), pl.ds(col + 128, 128)] = turn(jnp.where(lane, odd, even)).astype(bf)
                return 0

            return start, join

        todo = [(pair(w, first, pairs), pairs * high) for w, first, pairs, high in kinds]
        for (start, _), n in todo:
            lax.fori_loop(0, n, start, 0)

        def clear(j, _):
            zero_copy(j).start()
            return 0

        lax.fori_loop(0, 48, clear, 0)
        for (_, join), n in todo:
            lax.fori_loop(0, n, join, 0)

    vp = vp_ref[...]
    row = r0 + lax.broadcasted_iota(jnp.int32, (rows, 1), 0)
    live = jnp.where(row < cnt_ref[0], 1.0, 0.0)
    o_t = jnp.concatenate([o_ref[t] for t in range(4)], axis=0)
    o_s[:, pl.ds(r0, rows)] = o_t
    res = x_ref[...].astype(f32) + mm(o_t, w_out[...], TN) + vp[6:7]
    cen = res - jnp.mean(res, axis=-1, keepdims=True)
    inv_std = lax.rsqrt(jnp.mean(cen * cen, axis=-1, keepdims=True) + EPS_NORM)
    normed = cen * inv_std
    a2 = (normed * vp[2:3] + vp[3:4]).astype(bf)
    gy = c_ref[...].astype(f32) * live
    gm = gy.astype(bf)
    a2_s[pl.ds(r0, rows), :] = a2
    gm_s[pl.ds(r0, rows), :] = gm
    branch = jnp.zeros((rows, 768), f32)
    g2 = jnp.zeros((rows, 768), f32)
    for j in range(4):
        cols = slice(j * 768, (j + 1) * 768)
        u, slope = gelu_parts(mm(a2, w_up[:, cols]) + bu_ref[:, cols])
        u = u.astype(bf)
        u_s[pl.ds(r0, rows), cols] = u
        branch = branch + mm(u, w_down[cols, :])
        gz = (mm(gm, w_down[cols, :], NT) * slope).astype(bf)
        gz_s[pl.ds(r0, rows), cols] = gz
        us_ref[:, cols] += jnp.broadcast_to(column_sum(gz.astype(f32)), (8, 768))
        g2 = g2 + mm(gz, w_up[:, cols], NT)
    y_ref[...] = (live * (res + branch + vp[7:8])).astype(bf)
    d2 = g2 * vp[2:3]
    gr = gy + inv_std * (d2 - jnp.mean(d2, axis=-1, keepdims=True) - normed * jnp.mean(d2 * normed, axis=-1, keepdims=True))
    gr_ref[...] = gr
    gb = gr.astype(bf)
    gb_s[pl.ds(r0, rows), :] = gb
    vs_ref[0:1, :] += column_sum(g2 * normed)
    vs_ref[1:2, :] += column_sum(g2)
    vs_ref[2:3, :] += column_sum(gb.astype(f32))
    vs_ref[3:4, :] += column_sum(gm.astype(f32))
    go = mm(w_out[...], gb, NT).astype(bf)
    for t in range(4):
        go_ref[t] = go[t * 192 : (t + 1) * 192]

    @pl.when(i == pl.num_programs(0) - 1)
    def _():
        def out_copy(k, at):
            return pltpu.make_async_copy(ring.at[k], s_ref.at[inv_ref[at]], osem.at[k])

        def send(n, g, first, pairs, high, low):
            half = (n % 2) * 8

            def put(r, b):
                return first + (high + r) * 2 * pairs + 2 * low + b

            for r in range(4):
                part = g[r * 192 : (r + 1) * 192]
                mid = part[:, 128:256]
                upper, lower = mid[:96], turn(mid[96:])
                lane = lax.broadcasted_iota(jnp.int32, upper.shape, 1) < 64
                for b, top, tail in ((0, part[:, :128], jnp.where(lane, upper, lower)), (1, part[:, 256:], jnp.where(lane, lower, upper))):
                    k = half + 2 * r + b

                    @pl.when(n >= 2)
                    def _():
                        out_copy(k, 0).wait()

                    ring[k, :192] = top.astype(bf)
                    ring[k, 192:] = tail.astype(bf)
                    out_copy(k, put(r, b)).start()

        def lanes(j):
            return pl.ds(pl.multiple_of(j * 384, 128), 384)

        def grad_out(n, _):
            send(n, mm(o_s[...], gb_s[:, lanes(n)]), 48, 2, 0, n)
            return 0

        def grad_up(n, _):
            send(n, mm(a2_s[...], gz_s[:, lanes(n)], TN), 64, 8, 0, n)
            return 0

        def grad_down(n, _):
            high = n // 2
            send(n, mm(u_s[:, pl.ds(pl.multiple_of(high * 768, 128), 768)], gm_s[:, lanes(n % 2)], TN), 128, 2, high * 4, n % 2)
            return 0

        def drain():
            for k in range(16):
                out_copy(k, 0).wait()

        for f, n in ((grad_out, 2), (grad_up, 8), (grad_down, 8)):
            lax.fori_loop(0, n, f, 0)
            drain()

        def cleared(j, _):
            zero_copy(j).wait()
            return 0

        lax.fori_loop(0, 48, cleared, 0)


def middle(inv, count, blocks, o_t, tokens, cotangent, vec_params, bias_up, rows=256):
    n, width = tokens.shape
    hidden = bias_up.shape[1]
    row = lambda i, s, c: (i, 0)
    fixed = lambda i, s, c: (0, 0)
    col = lambda i, s, c: (0, 0, i)
    V, DS = pltpu.VMEM, pltpu.SemaphoreType.DMA
    spec = pltpu.PrefetchScalarGridSpec(
        num_scalar_prefetch=2,
        grid=(n // rows,),
        in_specs=[any_spec(), pl.BlockSpec((4, 192, rows), col), pl.BlockSpec((rows, width), row), pl.BlockSpec((rows, width), row),
                  pl.BlockSpec((12, width), fixed), pl.BlockSpec((1, hidden), fixed)],
        out_specs=[pl.BlockSpec((rows, width), row), pl.BlockSpec((rows, width), row), pl.BlockSpec((4, 192, rows), col), any_spec(),
                   pl.BlockSpec((8, width), fixed), pl.BlockSpec((8, hidden), fixed)],
        scratch_shapes=[V((768, 768), bf), V((768, 3072), bf), V((3072, 768), bf), V((144, 96, 128), bf), V((n, 3072), bf), V((n, 3072), bf),
                        V((n, 768), bf), V((n, 768), bf), V((n, 768), bf), V((768, n), bf), V((16, 288, 128), bf), V((288, 128), bf),
                        DS((144,)), DS((144,)), DS((16,)), DS((48,))],
    )
    return pl.pallas_call(
        middle_kernel,
        grid_spec=spec,
        out_shape=[jax.ShapeDtypeStruct((n, width), bf), jax.ShapeDtypeStruct((n, width), f32), jax.ShapeDtypeStruct((4, 192, n), bf),
                   jax.ShapeDtypeStruct(blocks.shape, bf), jax.ShapeDtypeStruct((8, width), f32), jax.ShapeDtypeStruct((8, hidden), f32)],
        compiler_params=params(),
        name="projection_and_mlp",
    )(inv, count, blocks, o_t, tokens, cotangent, vec_params, bias_up)


def split2(v):
    hi = v.astype(bf)
    return hi, (v - hi.astype(f32)).astype(bf)


def mm3(a, b, dims):
    return mm(a[0], b[0], dims) + (mm(a[0], b[1], dims) + mm(a[1], b[0], dims))


def adam_kernel(odd_ref, g_ref, m1_ref, m2_ref, l_ref, r_ref, g_out, m1_out, m2_out, u_out, s_out):
    for b in range(g_ref.shape[0]):
        grad = unpack(g_ref[b, :192].astype(f32), g_ref[b, 192:].astype(f32), odd_ref[pl.program_id(0) * g_ref.shape[0] + b] == 1)
        left, right = split2(l_ref[b]), split2(r_ref[b])
        low = grad.astype(bf)
        rot = mm3(split2(mm(left[0], low, TN) + mm(left[1], low, TN)), right, NN)
        first = BETA_ONE * m1_ref[b] + (1.0 - BETA_ONE) * rot
        second = BETA_TWO * m2_ref[b] + (1.0 - BETA_TWO) * rot * rot
        upd = (first / (1.0 - BETA_ONE**STEP)) / (jnp.sqrt(second / (1.0 - BETA_TWO**STEP)) + ADAM_EPS)
        upd = mm3(split2(mm3(left, split2(upd), NN)), right, NT)
        g_out[b] = grad
        m1_out[b] = first
        m2_out[b] = second
        u_out[b] = upd
        s_out[b] = jnp.full((8, 128), jnp.sum(upd * upd), f32)


def adam(odd, grads, first, second, left, right):
    n = grads.shape[0]
    g = group_of(n)
    at = lambda i, s: (i, 0, 0)
    big = pl.BlockSpec((g, 192, 192), at)
    spec = pltpu.PrefetchScalarGridSpec(
        num_scalar_prefetch=1,
        grid=(n // g,),
        in_specs=[pl.BlockSpec((g, 288, 128), at)] + [big] * 4,
        out_specs=[big] * 4 + [pl.BlockSpec((g, 8, 128), at)],
    )
    return pl.pallas_call(
        adam_kernel,
        grid_spec=spec,
        out_shape=[jax.ShapeDtypeStruct((n, 192, 192), f32)] * 4 + [jax.ShapeDtypeStruct((n, 8, 128), f32)],
        compiler_params=params(),
        name="rotated_adam",
    )(odd, grads, first, second, left, right)


def norm_forward(row_data, gain_vec, shift_vec):
    row_mean = jnp.mean(row_data, axis=-1, keepdims=True)
    centred = row_data - row_mean
    inv_std = lax.rsqrt(jnp.mean(centred * centred, axis=-1, keepdims=True) + EPS_NORM)
    normed = centred * inv_std
    return (normed * gain_vec + shift_vec, normed, inv_std)


def norm_back(grad_out, normed, inv_std, gain_vec):
    grad_normed = grad_out * gain_vec
    return inv_std * (
        grad_normed
        - jnp.mean(grad_normed, axis=-1, keepdims=True)
        - normed * jnp.mean(grad_normed * normed, axis=-1, keepdims=True)
    )


def block_plan(counts, slot_count):
    tiles = counts.shape[0]
    per = slot_count // 128
    j = lax.broadcasted_iota(jnp.int32, (tiles, per), 1)
    kept = jnp.clip(counts[:, None] - j * 128, 0, 128).reshape(-1)
    full = (kept > 0).astype(jnp.int32)
    index = jnp.arange(tiles * per, dtype=jnp.int32)
    before = (index[None, :] < index[:, None]).astype(jnp.int32)
    ahead = jnp.sum(before * full[None, :], axis=1)
    live = jnp.sum(full)
    place = jnp.where(full > 0, ahead, live + index - ahead)
    hot = (place[None, :] == index[:, None]).astype(jnp.int32)
    return jnp.sum(hot * index[None, :], axis=1), jnp.sum(hot * kept[None, :], axis=1), live.reshape(1)


def make_body(tuned):
    def body(tokens, cotangent, counts, master, slot_block, groups, first_moment, second_moment, left_basis, right_basis, vec_params, vec_first, vec_second):
        slot_count, width = tokens.shape[1:]
        per_owner = master.shape[0]
        tile = lax.axis_index("tile")
        mine = lax.dynamic_slice(slot_block, (lax.axis_index("dp") * per_owner,), (per_owner,))
        odd = mine % 2
        packed, weight_sq = pack_master(odd, master)
        own_tokens = tokens.reshape(slot_count, width)
        count_tile = jnp.broadcast_to(counts.reshape(1, 1), (8, 128))
        if tuned:
            blocks, token_all, count_all = gather_all(packed, own_tokens, count_tile)
        else:
            blocks = lax.all_gather(packed, "dp", axis=0, tiled=True)
            token_all = lax.all_gather(own_tokens, "tile", axis=0)
            count_all = lax.all_gather(count_tile, "tile", axis=0)
        tiles = token_all.shape[0]
        block_count = blocks.shape[0]
        src, cnt, live = block_plan(count_all[:, 0, 0], slot_count)
        index = jnp.arange(block_count, dtype=jnp.int32)
        inverse = jnp.sum((slot_block[None, :] == index[:, None]).astype(jnp.int32) * index[None, :], axis=1)
        own_block = jnp.arange(12, dtype=jnp.int32) // 3 * 12 + jnp.arange(12, dtype=jnp.int32) % 3 * 4 + tile
        own_at = jnp.sum((slot_block[None, :] == own_block[:, None]).astype(jnp.int32) * index[None, :], axis=1)
        own_at = jnp.concatenate([own_at, tile.reshape(1) % 2])
        own = width // tiles
        bias = lambda row: lax.dynamic_slice(vec_params[row : row + 1], (0, tile * own), (1, own))
        a1, q, qt, k, kt, v, vt, w_qkv, lengths = qkv_forward(
            src, cnt, own_at, token_all.reshape(-1, width), blocks, vec_params[0:1], vec_params[1:2], bias(4), bias(5)
        )
        mild = jnp.sqrt(jnp.max(lengths[:, 0, 0])) * jnp.sqrt(jnp.max(lengths[:, 1, 0])) * EXP2 <= 60.0
        live = jnp.concatenate([live, mild.astype(jnp.int32).reshape(1)])
        ot, qb = attend(live, k, qt, vt)
        o_t = exchange(spread(src, live, ot, tiles))
        output, grad_resid, go_t, slots, sums, up_sums = middle(
            inverse, counts.reshape(1), blocks, o_t, own_tokens, cotangent.reshape(slot_count, width), vec_params, vec_params[8:].reshape(1, -1)
        )
        go = exchange(go_t)
        dt, d = collect(src, live, go, ot)
        dq, dk, dv = attend_back(live, k, kt, v, qb, q, dt, d)
        g_part, slot_grads, qkv_sums = qkv_backward(src, live, own_at, dq, dk, dv, a1, w_qkv, slots)
        g_part = g_part.reshape(tiles, slot_count, width)
        if tuned:
            g1 = lax.psum_scatter(g_part, "tile", scatter_dimension=0, tiled=False).astype(f32)
            grads = grad_sum(slot_grads.reshape(-1, per_owner, 288, 128))
        else:
            g1 = lax.psum_scatter(g_part.astype(f32), "tile", scatter_dimension=0, tiled=False)
            grads = lax.psum(lax.psum_scatter(slot_grads.astype(f32), "dp", scatter_dimension=0, tiled=True), "tile").astype(bf)
        row_input = own_tokens.astype(f32)
        _, normed_one, inv_std_one = norm_forward(row_input, vec_params[0], vec_params[1])
        input_grad = grad_resid + norm_back(g1, normed_one, inv_std_one, vec_params[0])
        zero = jnp.zeros((width,), f32)
        at_own = lambda s: lax.dynamic_update_slice(zero, s, (tile * own,))
        rows = jnp.stack(
            [jnp.sum(g1 * normed_one, axis=0), jnp.sum(g1, axis=0), sums[0], sums[1], at_own(qkv_sums[0, :own]), at_own(qkv_sums[0, 2 * own :]), sums[2], sums[3]],
            axis=0,
        )
        vector_part = jnp.concatenate([rows, up_sums[0].reshape(-1, width)], axis=0)

        weight_grads, first_out, second_out, update, update_sq = adam(odd, grads, first_moment, second_moment, left_basis, right_basis)
        group_hot = (groups[:, None] == jnp.arange(NGRP, dtype=jnp.int32)[None, :]).astype(f32)
        both = jnp.stack([weight_sq[:, 0, 0], update_sq[:, 0, 0]], axis=0)
        group_part = jnp.pad(jnp.sum(group_hot[None] * both[:, :, None], axis=1), ((0, 6), (0, 128 - NGRP)))
        vector_grads, group_both = totals(vector_part, group_part, block_count // per_owner, tiles)
        own_both = jnp.sum(group_hot[None] * group_both[:2, None, :NGRP], axis=2)
        block_rate = RATE_BLOCK * jnp.sqrt(own_both[0]) / (jnp.sqrt(own_both[1]) + 1e-06)
        master_out = master - block_rate[:, None, None] * update
        vec_first_out = BETA_ONE * vec_first + (1.0 - BETA_ONE) * vector_grads
        vec_second_out = BETA_TWO * vec_second + (1.0 - BETA_TWO) * vector_grads * vector_grads
        vec_update = (vec_first_out / (1.0 - BETA_ONE**STEP)) / (jnp.sqrt(vec_second_out / (1.0 - BETA_TWO**STEP)) + ADAM_EPS)
        return (
            output.reshape(1, slot_count, width),
            input_grad.reshape(1, slot_count, width),
            weight_grads,
            first_out,
            second_out,
            master_out,
            master_out.astype(bf),
            vector_grads,
            vec_first_out,
            vec_second_out,
            vec_params - RATE_VECTOR * vec_update,
        )

    return body


def solution(mesh):
    tuned = (mesh.shape["dp"], mesh.shape["tile"]) == (8, 4)
    rows, blocks = P("dp", "tile", None), P("dp", None, None)
    return jax.shard_map(
        make_body(tuned),
        mesh=mesh,
        in_specs=(rows, rows, P("dp", "tile"), blocks, P(), P("dp"), blocks, blocks, blocks, blocks, P(), P(), P()),
        out_specs=(rows, rows, blocks, blocks, blocks, blocks, blocks, P(), P(), P(), P()),
        check_vma=False,
    )
```

```python
import functools
import math

import jax
import jax.numpy as jnp
from jax import lax
from jax.experimental import pallas as pl
from jax.experimental.pallas import tpu as pltpu
from jax.sharding import PartitionSpec as P

f32 = jnp.float32
bf = jnp.bfloat16
MESH = pl.DeviceIdType.MESH

def where_am_i():
    dp=lax.axis_index("dp"); t=lax.axis_index("tile")
    return dp//2, dp%2, t//2, t%2

def dev(z,y,x,c):
    return (z*2+y, x*2+c)

def rcopy(src,dst,ss,rs,to):
    return pltpu.make_async_remote_copy(src_ref=src,dst_ref=dst,send_sem=ss,recv_sem=rs,device_id=to,device_id_type=MESH)

def gather_kernel(own_w,own_tok,own_cnt,all_w,all_tok,all_cnt,
                  zs,zr,ys,yr,xs,xr,cs,cr,fs,fr,ts,tr,ns,nr,ls):
    z,y,x,c=where_am_i()
    per=own_w.shape[0]
    part=per//12
    def a_of(shard,xx,cc): return all_w.at[pl.ds(shard*per+(xx*2+cc)*part,part)]
    def b_of(shard,cc): return all_w.at[pl.ds(shard*per+4*part+cc*4*part,4*part)]
    own_a=own_w.at[pl.ds((x*2+c)*part,part)]
    own_b=own_w.at[pl.ds(4*part+c*4*part,4*part)]
    me=z*2+y
    core=dev(z,y,x,1-c); across=dev(z,y,1-x,c); beside=dev(z,1-y,x,c)
    up=dev(jnp.minimum(z+1,3),y,x,c); down=dev(jnp.maximum(z-1,0),y,x,c)
    def src(shard,own):
        return (own_a,own_b) if own else (a_of(shard,x,c),b_of(shard,c))
    def z_copies(zz,own,go_up):
        shard=zz*2+y
        a,b=src(shard,own)
        d=(z-zz) if go_up else (zz-z)
        k=0 if go_up else 1
        to=up if go_up else down
        return (rcopy(a,a_of(shard,x,c),zs.at[k,d,0],zr.at[k,d,0],to),rcopy(b,b_of(shard,c),zs.at[k,d,1],zr.at[k,d,1],to))
    def z_arrivals(zz,k,dist):
        shard=zz*2+y
        a,b=a_of(shard,x,c),b_of(shard,c)
        return (rcopy(a,a,zs.at[k,dist-1,0],zr.at[k,dist-1,0],up),rcopy(b,b,zs.at[k,dist-1,1],zr.at[k,dist-1,1],up))
    def y_copies(zz,own):
        shard=zz*2+y
        a,b=src(shard,own)
        return (rcopy(a,a_of(shard,x,c),ys.at[zz,0],yr.at[zz,0],beside),rcopy(b,b_of(shard,c),ys.at[zz,1],yr.at[zz,1],beside))
    def y_arrivals(zz):
        shard=zz*2+(1-y)
        a,b=a_of(shard,x,c),b_of(shard,c)
        return (rcopy(a,a,ys.at[zz,0],yr.at[zz,0],beside),rcopy(b,b,ys.at[zz,1],yr.at[zz,1],beside))
    def x_copy(shard,own):
        return rcopy(src(shard,own)[0],a_of(shard,x,c),xs.at[shard],xr.at[shard],across)
    def x_arrival(shard):
        a=a_of(shard,1-x,c)
        return rcopy(a,a,xs.at[shard],xr.at[shard],across)
    def c_copies(shard,own):
        a,b=src(shard,own)
        return (rcopy(a,a_of(shard,x,c),cs.at[shard,0],cr.at[shard,0],core),rcopy(b,b_of(shard,c),cs.at[shard,1],cr.at[shard,1],core))
    def c_arrivals(shard):
        a,b=a_of(shard,x,1-c),b_of(shard,1-c)
        return (rcopy(a,a,cs.at[shard,0],cr.at[shard,0],core),rcopy(b,b,cs.at[shard,1],cr.at[shard,1],core))
    def f_copy(shard):
        a=a_of(shard,1-x,c)
        return rcopy(a,a,fs.at[shard],fr.at[shard],core)
    def f_arrival(shard):
        a=a_of(shard,1-x,1-c)
        return rcopy(a,a,fs.at[shard],fr.at[shard],core)
    def start(cps):
        for cp in (cps if isinstance(cps,tuple) else (cps,)): cp.start()
    def got(cps):
        for cp in (cps if isinstance(cps,tuple) else (cps,)): cp.wait_recv()
    def sent(cps):
        for cp in (cps if isinstance(cps,tuple) else (cps,)): cp.wait_send()
    tile=x*2+c
    tok_x=rcopy(own_tok,all_tok.at[tile],ts.at[0],tr.at[0],across)
    tok_c=rcopy(own_tok,all_tok.at[tile],ts.at[1],tr.at[1],core)
    far=all_tok.at[(1-x)*2+c]
    tok_f=rcopy(far,far,ts.at[2],tr.at[2],core)
    near=all_tok.at[x*2+1-c]
    diag=all_tok.at[(1-x)*2+1-c]
    cnts=[rcopy(own_cnt,all_cnt.at[tile],ns.at[i],nr.at[i],to) for i,to in enumerate((across,core,dev(z,y,1-x,1-c)))]
    cnt_in=[rcopy(r,r,ns.at[i],nr.at[i],core) for i,r in enumerate((all_cnt.at[(1-x)*2+c],all_cnt.at[x*2+1-c],all_cnt.at[(1-x)*2+1-c]))]
    local=(pltpu.make_async_copy(own_w,all_w.at[pl.ds(me*per,per)],ls.at[0]),
           pltpu.make_async_copy(own_tok,all_tok.at[tile],ls.at[1]),pltpu.make_async_copy(own_cnt,all_cnt.at[tile],ls.at[2]))
    @pl.when(z<3)
    def _(): start(z_copies(z,True,True))
    @pl.when(z>0)
    def _(): start(z_copies(z,True,False))
    start(y_copies(z,True)); start(tok_x); start(tok_c)
    for cp in cnts: cp.start()
    for cp in local: cp.start()
    def from_line(k,dist):
        zz=z-dist if k==0 else z+dist
        there=(zz>=0) if k==0 else (zz<=3)
        @pl.when(there)
        def _():
            got(z_arrivals(zz,k,dist))
            @pl.when((z<3) if k==0 else (z>0))
            def _(): start(z_copies(zz,False,k==0))
            start(y_copies(zz,False)); start(x_copy(zz*2+y,False)); start(c_copies(zz*2+y,False))
    def from_beside(zz):
        got(y_arrivals(zz))
        s=zz*2+1-y
        start(x_copy(s,False)); start(c_copies(s,False))
    def guarded(f,dist):
        @pl.when(z-dist>=0)
        def _(): f(z-dist)
        @pl.when(z+dist<=3)
        def _(): f(z+dist)
    def from_across(shard):
        got(x_arrival(shard)); start(f_copy(shard))
    from_line(0,1); from_line(1,1)
    from_beside(z)
    from_line(0,2); from_line(1,2)
    guarded(from_beside,1); guarded(lambda zz: from_across(zz*2+y),1); from_across(z*2+1-y)
    from_line(0,3); from_line(1,3)
    got(tok_x); tok_f.start()
    guarded(from_beside,2); guarded(lambda zz: from_across(zz*2+y),2); guarded(lambda zz: from_across(zz*2+1-y),1)
    guarded(from_beside,3); guarded(lambda zz: from_across(zz*2+y),3); guarded(lambda zz: from_across(zz*2+1-y),2)
    guarded(lambda zz: from_across(zz*2+1-y),3)
    def drain(s,_):
        @pl.when(s!=me)
        def _():
            got(c_arrivals(s)); got(f_arrival(s)); sent(c_copies(s,False)); sent(f_copy(s)); sent(x_copy(s,False))
        return 0
    lax.fori_loop(0,8,drain,0)
    def drain_y(zz,_):
        sent(y_copies(zz,False)); return 0
    lax.fori_loop(0,4,drain_y,0)
    for dist in range(4):
        @pl.when(jnp.logical_and(z<3,z-dist>=0))
        def _(): sent(z_copies(z-dist,False,True))
        @pl.when(jnp.logical_and(z>0,z+dist<=3))
        def _(): sent(z_copies(z+dist,False,False))
    rcopy(near,near,ts.at[1],tr.at[1],core).wait_recv()
    rcopy(diag,diag,ts.at[2],tr.at[2],core).wait_recv()
    tok_x.wait_send(); tok_c.wait_send(); tok_f.wait_send()
    for cp in cnts: cp.wait_send()
    for cp in cnt_in: cp.wait_recv()
    for cp in local: cp.wait()

def gather_all(own_w,own_tok,own_cnt):
    DS=pltpu.SemaphoreType.DMA
    hbm=pl.BlockSpec(memory_space=pl.ANY)
    return pl.pallas_call(gather_kernel,
        out_shape=[jax.ShapeDtypeStruct((8*own_w.shape[0],)+own_w.shape[1:],bf),jax.ShapeDtypeStruct((4,)+own_tok.shape,bf),jax.ShapeDtypeStruct((4,)+own_cnt.shape,own_cnt.dtype)],
        in_specs=[pl.BlockSpec(memory_space=pltpu.VMEM)]*3,out_specs=[hbm]*3,
        scratch_shapes=[DS((2,4,2)),DS((2,4,2)),DS((4,2)),DS((4,2)),DS((8,)),DS((8,)),DS((8,2)),DS((8,2)),DS((8,)),DS((8,)),DS((3,)),DS((3,)),DS((3,)),DS((3,)),DS((3,))],
        compiler_params=pltpu.CompilerParams(has_side_effects=True,vmem_limit_bytes=60<<20),name="gather_weights_tokens")(own_w,own_tok,own_cnt)

def totals_kernel(v_ref,g_ref,vo_ref,go_ref,vt,vd,gd,ts,tr,ds,dr,gs,gr):
    dp=lax.axis_index("dp"); t=lax.axis_index("tile")
    nt,nd=vt.shape[0],vd.shape[0]
    def g_copy(k):
        p=(dp+k)%nd
        return rcopy(gd.at[dp],gd.at[dp],gs.at[k],gr.at[k],(p,t))
    def g_arrive(k):
        q=(dp-k+nd)%nd
        return rcopy(gd.at[q],gd.at[q],gs.at[k],gr.at[k],(q,t))
    def t_copy(k):
        p=(t+k)%nt
        return rcopy(vt.at[t],vt.at[t],ts.at[k],tr.at[k],(dp,p))
    def t_arrive(k):
        q=(t-k+nt)%nt
        return rcopy(vt.at[q],vt.at[q],ts.at[k],tr.at[k],(dp,q))
    def d_copy(k):
        p=(dp+k)%nd
        return rcopy(vd.at[dp],vd.at[dp],ds.at[k],dr.at[k],(p,t))
    def d_arrive(k):
        q=(dp-k+nd)%nd
        return rcopy(vd.at[q],vd.at[q],ds.at[k],dr.at[k],(q,t))
    def loop(n,f):
        def s(k,_):
            f(k); return 0
        lax.fori_loop(1,n,s,0)
    vt[t]=v_ref[...]
    gd[dp]=g_ref[...]
    loop(nt,lambda k: t_copy(k).start())
    loop(nd,lambda k: g_copy(k).start())
    loop(nt,lambda k: t_arrive(k).wait_recv())
    acc=vt[0]
    for i in range(1,nt): acc=acc+vt[i]
    vd[dp]=acc
    loop(nd,lambda k: d_copy(k).start())
    loop(nd,lambda k: g_arrive(k).wait_recv())
    acc=gd[0]
    for i in range(1,nd): acc=acc+gd[i]
    go_ref[...]=acc
    loop(nd,lambda k: d_arrive(k).wait_recv())
    acc=vd[0]
    for i in range(1,nd): acc=acc+vd[i]
    vo_ref[...]=acc
    loop(nt,lambda k: t_copy(k).wait_send())
    loop(nd,lambda k: g_copy(k).wait_send())
    loop(nd,lambda k: d_copy(k).wait_send())

def totals(v,g,nd,nt):
    DS=pltpu.SemaphoreType.DMA
    vm=pl.BlockSpec(memory_space=pltpu.VMEM)
    return pl.pallas_call(totals_kernel,out_shape=[jax.ShapeDtypeStruct(v.shape,f32),jax.ShapeDtypeStruct(g.shape,f32)],in_specs=[vm]*2,out_specs=[vm]*2,
        scratch_shapes=[pltpu.VMEM((nt,)+v.shape,f32),pltpu.VMEM((nd,)+v.shape,f32),pltpu.VMEM((nd,)+g.shape,f32),DS((nt,)),DS((nt,)),DS((nd,)),DS((nd,)),DS((nd,)),DS((nd,))],
        compiler_params=pltpu.CompilerParams(has_side_effects=True,vmem_limit_bytes=60<<20),name="sum_small")(v,g)

def grad_sum_kernel(a_ref,o_ref,mine,xb0,yb0,zin,xb1,yb1,zin1,zin2,yb2,xb2,cs,cr,ss,rs,zs,zr,fs,fr):
    z,y,x,c=where_am_i()
    core=dev(z,y,x,1-c); across=dev(z,y,1-x,c); beside=dev(z,1-y,x,c)
    up=dev(jnp.minimum(z+1,3),y,x,c); down=dev(jnp.maximum(z-1,0),y,x,c)
    other=(1-c)*12; own=c*12
    def c_copy(p,d):
        return rcopy(a_ref.at[d,pl.ds(other+p*4,4)],mine.at[p,d],cs.at[p,d],cr.at[p,d],core)
    order=(2,0,1)
    def go(p):
        def s(d,_):
            c_copy(p,d).start(); return 0
        lax.fori_loop(0,8,s,0)
    for p in order: go(p)
    def add_own(p):
        def s(d,_):
            c_copy(p,d).wait_recv()
            for b in range(4):
                mine[p,d,b]=(mine[p,d,b].astype(f32)+a_ref[d,own+p*4+b].astype(f32)).astype(bf)
            return 0
        lax.fori_loop(0,8,s,0)
    def add(dst,src):
        n=dst.shape[0]
        for i in range(n): dst[i]=(dst[i].astype(f32)+src[i].astype(f32)).astype(bf)
    def line(buf_of,inbox,sem):
        def cp(tz,go_down):
            k=1 if go_down else 0
            return rcopy(buf_of(tz),inbox.at[k,tz],zs.at[sem,k,tz],zr.at[sem,k,tz],down if go_down else up)
        def arrive(tz,go_down):
            k=1 if go_down else 0
            return rcopy(inbox.at[k,tz],inbox.at[k,tz],zs.at[sem,k,tz],zr.at[sem,k,tz],down)
        return cp,arrive
    def line_start(cp):
        @pl.when(z==3)
        def _(): cp(0,True).start()
        @pl.when(z==0)
        def _(): cp(3,False).start()
    def line_pass(cp,arrive,buf_of,inbox,addf):
        for tz in (0,1):
            @pl.when(z==3)
            def _():
                cp(tz,True).wait_send(); cp(tz+1,True).start()
            @pl.when(z==0)
            def _():
                cp(3-tz,False).wait_send(); cp(2-tz,False).start()
        for tz in (0,1,2):
            @pl.when(jnp.logical_and(z<3,z>tz))
            def _():
                arrive(tz,True).wait_recv(); addf(buf_of(tz),inbox.at[1,tz]); cp(tz,True).start()
            u=3-tz
            @pl.when(jnp.logical_and(z>0,z<u))
            def _():
                arrive(u,False).wait_recv(); addf(buf_of(u),inbox.at[0,u]); cp(u,False).start()
    def line_end(cp,arrive,buf_of,inbox,addf):
        @pl.when(z<3)
        def _():
            arrive(z,True).wait_recv(); addf(buf_of(z),inbox.at[1,z])
        @pl.when(z>0)
        def _():
            arrive(z,False).wait_recv(); addf(buf_of(z),inbox.at[0,z])
    def line_sent(cp):
        @pl.when(z==3)
        def _(): cp(2,True).wait_send()
        @pl.when(z==0)
        def _(): cp(1,False).wait_send()
        for tz in (0,1,2):
            @pl.when(jnp.logical_and(z<3,z>tz))
            def _(): cp(tz,True).wait_send()
            @pl.when(jnp.logical_and(z>0,z<3-tz))
            def _(): cp(3-tz,False).wait_send()
    def add2(dst,src):
        for i in range(2):
            for j in range(4): dst[i,j]=(dst[i,j].astype(f32)+src[i,j].astype(f32)).astype(bf)
    p2_of=lambda tz: mine.at[2,pl.ds(tz*2,2)]
    cp2,ar2=line(p2_of,zin,0)
    add_own(2); line_start(cp2)
    def x0(d): return rcopy(mine.at[0,d,pl.ds((1-x)*2,2)],xb0.at[d],ss.at[0,d],rs.at[0,d],across)
    def s0(d,_):
        c_copy(0,d).wait_recv()
        for b in range(4):
            mine[0,d,b]=(mine[0,d,b].astype(f32)+a_ref[d,own+b].astype(f32)).astype(bf)
        x0(d).start()
        return 0
    lax.fori_loop(0,8,s0,0)
    def y1(zz): return rcopy(mine.at[1,zz*2+1-y],yb0.at[zz],ss.at[1,zz],rs.at[1,zz],beside)
    add_own(1)
    for zz in range(4): y1(zz).start()
    line_pass(cp2,ar2,p2_of,zin,add2)
    def p0(zz,yy): return mine.at[0,zz*2+yy,pl.ds(x*2,2)]
    def y0(zz): return rcopy(p0(zz,1-y),yb1.at[zz],ss.at[2,zz],rs.at[2,zz],beside)
    for zz in range(4):
        for yy in range(2):
            d=zz*2+yy
            x0(d).wait_recv(); add(p0(zz,yy),xb0.at[d])
        y0(zz).start()
    def p1(zz): return mine.at[1,zz*2+y]
    def x1(zz): return rcopy(mine.at[1,zz*2+y,pl.ds((1-x)*2,2)],xb1.at[zz],ss.at[3,zz],rs.at[3,zz],across)
    for zz in range(4):
        y1(zz).wait_recv(); add(p1(zz),yb0.at[zz]); x1(zz).start()
    q0=lambda tz: mine.at[0,tz*2+y,pl.ds(x*2,2)]
    cp0,ar0=line(q0,zin1,1)
    q1=lambda tz: mine.at[1,tz*2+y,pl.ds(x*2,2)]
    cp1,ar1=line(q1,zin2,2)
    for zz in range(4):
        y0(zz).wait_recv(); add(q0(zz),yb1.at[zz])
    line_start(cp0)
    line_end(cp2,ar2,p2_of,zin,add2)
    y2=rcopy(mine.at[2,z*2+1-y],yb2,ss.at[4,0],rs.at[4,0],beside)
    y2.start()
    for zz in range(4):
        x1(zz).wait_recv(); add(q1(zz),xb1.at[zz])
    line_start(cp1)
    line_pass(cp0,ar0,q0,zin1,add)
    y2.wait_recv(); add(mine.at[2,z*2+y],yb2)
    x2=rcopy(mine.at[2,z*2+y,pl.ds((1-x)*2,2)],xb2,ss.at[5,0],rs.at[5,0],across)
    x2.start()
    line_pass(cp1,ar1,q1,zin2,add)
    x2.wait_recv()
    me=z*2+y
    add(mine.at[2,me,pl.ds(x*2,2)],xb2)
    def place(xx,cc,p): return o_ref.at[pl.ds(cc*12+p*4+xx*2,2)]
    def f_copy(i,p):
        if i==2: return rcopy(place(1-x,c,p),place(1-x,c,p),fs.at[2,p],fr.at[2,p],core)
        return rcopy(mine.at[p,me,pl.ds(x*2,2)],place(x,c,p),fs.at[i,p],fr.at[i,p],across if i==0 else core)
    def f_arrive(i,p):
        r=(place(1-x,c,p),place(x,1-c,p),place(1-x,1-c,p))[i]
        return rcopy(r,r,fs.at[i,p],fr.at[i,p],core)
    def finish(p):
        o_ref[pl.ds(own+p*4+x*2,2)]=mine[p,me,pl.ds(x*2,2)]
        for i in range(2): f_copy(i,p).start()
    finish(2)
    line_end(cp0,ar0,q0,zin1,add); finish(0)
    line_end(cp1,ar1,q1,zin2,add); finish(1)
    for p in (2,0,1):
        f_arrive(0,p).wait_recv(); f_copy(2,p).start()
    for p in range(3):
        f_arrive(1,p).wait_recv(); f_arrive(2,p).wait_recv()
    for p in range(3):
        for i in range(3): f_copy(i,p).wait_send()
    def drain(d,_):
        for p in range(3): c_copy(p,d).wait_send()
        x0(d).wait_send()
        return 0
    lax.fori_loop(0,8,drain,0)
    for zz in range(4):
        y1(zz).wait_send(); y0(zz).wait_send(); x1(zz).wait_send()
    y2.wait_send(); x2.wait_send()
    line_sent(cp2); line_sent(cp0); line_sent(cp1)

def grad_sum(a):
    DS=pltpu.SemaphoreType.DMA
    R=a.shape[2]
    vm=pl.BlockSpec(memory_space=pltpu.VMEM)
    V=lambda *s: pltpu.VMEM(s+(R,128),bf)
    return pl.pallas_call(grad_sum_kernel,out_shape=jax.ShapeDtypeStruct((24,R,128),bf),in_specs=[vm],out_specs=vm,
        scratch_shapes=[V(3,8,4),V(8,2),V(4,4),V(2,4,2,4),V(4,2),V(4,2),V(2,4,2),V(2,4,2),V(4),V(2),
            DS((3,8)),DS((3,8)),DS((6,8)),DS((6,8)),DS((3,2,4)),DS((3,2,4)),DS((3,3)),DS((3,3))],
        cost_estimate=pl.CostEstimate(flops=10**7,bytes_accessed=200*10**6,transcendentals=0),
        compiler_params=pltpu.CompilerParams(has_side_effects=True,vmem_limit_bytes=60<<20),name="sum_gradients")(a)


H = 12
NGRP = 16
STEP = 10
EPS_NORM = 1e-06
BETA_ONE = 0.5
BETA_TWO = 0.5
ADAM_EPS = 1e-08
RATE_BLOCK = 0.3
RATE_VECTOR = 0.2
NEG_RAW = -8.0e9
HEAD = 64
SCALE = 1.0 / math.sqrt(HEAD)
EXP2 = SCALE * math.log2(math.e)
NN = (((1,), (0,)), ((), ()))
NT = (((1,), (1,)), ((), ()))
TN = (((0,), (0,)), ((), ()))


def mm(a, b, dims=NN):
    return lax.dot_general(a, b, dims, preferred_element_type=f32)


def column_sum(v):
    return jnp.sum(v, axis=0, keepdims=True)


def vmem_spec():
    return pl.BlockSpec(memory_space=pltpu.VMEM)


def smem_spec():
    return pl.BlockSpec(memory_space=pltpu.SMEM)


def any_spec():
    return pl.BlockSpec(memory_space=pl.ANY)


def params(mib=60):
    return pltpu.CompilerParams(vmem_limit_bytes=mib << 20)


def pack(block, odd):
    half = block.shape[0] // 2
    left, right = block[:, :64], block[:, 128:]
    even_tail = jnp.concatenate([right[:half], right[half:]], axis=1)
    odd_tail = jnp.concatenate([left[half:], left[:half]], axis=1)
    return jnp.where(odd, block[:, 64:], block[:, :128]), jnp.where(odd, odd_tail, even_tail)


def unpack(top, tail, odd):
    first, second = tail[:, :64], tail[:, 64:]
    even = jnp.concatenate([top, jnp.concatenate([first, second], axis=0)], axis=1)
    return jnp.where(odd, jnp.concatenate([jnp.concatenate([second, first], axis=0), top], axis=1), even)


def turn(v):
    return jnp.concatenate([v[:, 64:], v[:, :64]], axis=1)


def group_of(n):
    return 4 if n % 4 == 0 else 3 if n % 3 == 0 else 1


def pack_kernel(odd_ref, m_ref, p_ref, s_ref):
    g = m_ref.shape[0]
    for b in range(g):
        m = m_ref[b]
        top, tail = pack(m, odd_ref[pl.program_id(0) * g + b] == 1)
        p_ref[b, :192] = top.astype(bf)
        p_ref[b, 192:] = tail.astype(bf)
        s_ref[b] = jnp.full((8, 128), jnp.sum(m * m), f32)


def pack_master(odd, master):
    n = master.shape[0]
    g = group_of(n)
    at = lambda i, s: (i, 0, 0)
    spec = pltpu.PrefetchScalarGridSpec(
        num_scalar_prefetch=1,
        grid=(n // g,),
        in_specs=[pl.BlockSpec((g, 192, 192), at)],
        out_specs=[pl.BlockSpec((g, 288, 128), at), pl.BlockSpec((g, 8, 128), at)],
    )
    return pl.pallas_call(
        pack_kernel,
        grid_spec=spec,
        out_shape=[jax.ShapeDtypeStruct((n, 288, 128), bf), jax.ShapeDtypeStruct((n, 8, 128), f32)],
        compiler_params=params(),
        name="pack_master",
    )(odd, master)


def qkv_kernel(src_ref, cnt_ref, at_ref, x0, x1, x2, x3, blk_ref, gain_ref, shift_ref, bq_ref, bv_ref, a_ref, q_ref, qt_ref, k_ref, kt_ref, v_ref, vt_ref, w_ref, st_ref, buf, sems):
    i = pl.program_id(0)

    @pl.when(i == 0)
    def _():
        copies = [pltpu.make_async_copy(blk_ref.at[at_ref[j]], buf.at[j], sems.at[j]) for j in range(12)]
        for copy in copies:
            copy.start()
        odd = at_ref[12] == 1
        for r in range(4):
            parts = []
            for c in range(3):
                copies[r * 3 + c].wait()
                p = buf[r * 3 + c].astype(f32)
                parts.append(unpack(p[:192], p[192:], odd))
            w_ref[r * 192 : (r + 1) * 192, :] = jnp.concatenate(parts, axis=1).astype(bf)

    x = jnp.concatenate([r[...] for r in (x0, x1, x2, x3)], axis=0).astype(f32)
    mean = jnp.mean(x, axis=-1, keepdims=True)
    cen = x - mean
    inv_std = lax.rsqrt(jnp.mean(cen * cen, axis=-1, keepdims=True) + EPS_NORM)
    a = (cen * inv_std * gain_ref[...] + shift_ref[...]).astype(bf)
    a_ref[...] = a
    qkv = mm(a, w_ref[...])
    q = (qkv[:, :192] + bq_ref[...]).astype(bf).astype(f32)
    k = qkv[:, 192:384].astype(bf).astype(f32)
    v = (qkv[:, 384:] + bv_ref[...]).astype(bf).astype(f32)
    row = lax.broadcasted_iota(jnp.int32, (128, 64), 0)
    lane = lax.broadcasted_iota(jnp.int32, (512, 64), 1)
    masked = jnp.concatenate(
        [jnp.where(row < cnt_ref[4 * i + b], 0.0, NEG_RAW) for b in range(4)], axis=0
    )
    ones = jnp.where(lane < 4, 1.0, 0.0)
    k_tail = jnp.where(lane == 0, masked, ones)
    v_tail = jnp.where(lane < 3, 1.0, 0.0)
    zero = jnp.zeros((512, 64), f32)
    sub = lax.broadcasted_iota(jnp.int32, (64, 512), 0)
    t_tail = jnp.where(sub < 1, 1.0, 0.0)
    qt, kt, vt = q.T, k.T, v.T
    longest = lambda a: jnp.max(jnp.concatenate([column_sum(a[h * 64 : (h + 1) * 64] ** 2) for h in range(3)], axis=0))
    st_ref[0] = jnp.where(lax.broadcasted_iota(jnp.int32, (8, 128), 0) == 0, longest(qt), longest(kt))
    for h in range(3):
        s = slice(h * 64, (h + 1) * 64)
        q_ref[h] = jnp.concatenate([q[:, s], zero], axis=1).astype(bf)
        k_ref[h] = jnp.concatenate([k[:, s], k_tail], axis=1).astype(bf)
        v_ref[h] = jnp.concatenate([v[:, s], v_tail], axis=1).astype(bf)
        qt_ref[h] = jnp.concatenate([qt[s], t_tail], axis=0).astype(bf)
        kt_ref[h] = kt[s].astype(bf)
        vt_ref[h] = jnp.concatenate([vt[s], t_tail[:16]], axis=0).astype(bf)


def qkv_forward(src, cnt, own_at, tokens, blocks, gain, shift, bq, bv):
    n = tokens.shape[0]
    rows = [pl.BlockSpec((128, 768), lambda i, s, c, o, k=k: (s[4 * i + k], 0)) for k in range(4)]
    row = lambda i, s, c, o: (0, 0)
    spec = pltpu.PrefetchScalarGridSpec(
        num_scalar_prefetch=3,
        grid=(n // 512,),
        in_specs=rows
        + [any_spec(), pl.BlockSpec((1, 768), row), pl.BlockSpec((1, 768), row), pl.BlockSpec((1, 192), row), pl.BlockSpec((1, 192), row)],
        out_specs=[
            pl.BlockSpec((512, 768), lambda i, s, c, o: (i, 0)),
            pl.BlockSpec((3, 512, 128), lambda i, s, c, o: (0, i, 0)),
            pl.BlockSpec((3, 128, 512), lambda i, s, c, o: (0, 0, i)),
            pl.BlockSpec((3, 512, 128), lambda i, s, c, o: (0, i, 0)),
            pl.BlockSpec((3, 64, 512), lambda i, s, c, o: (0, 0, i)),
            pl.BlockSpec((3, 512, 128), lambda i, s, c, o: (0, i, 0)),
            pl.BlockSpec((3, 80, 512), lambda i, s, c, o: (0, 0, i)),
            pl.BlockSpec((768, 576), row),
            pl.BlockSpec((1, 8, 128), lambda i, s, c, o: (i, 0, 0)),
        ],
        scratch_shapes=[pltpu.VMEM((12, 288, 128), bf), pltpu.SemaphoreType.DMA((12,))],
    )
    shapes = [(n, 768), (3, n, 128), (3, 128, n), (3, n, 128), (3, 64, n), (3, n, 128), (3, 80, n), (768, 576)]
    return pl.pallas_call(
        qkv_kernel,
        grid_spec=spec,
        out_shape=[jax.ShapeDtypeStruct(s, bf) for s in shapes] + [jax.ShapeDtypeStruct((n // 512, 8, 128), f32)],
        compiler_params=params(),
        name="norm_and_qkv",
    )(src, cnt, own_at, tokens, tokens, tokens, tokens, blocks, gain, shift, bq, bv)


def split3(v):
    a = v.astype(bf).astype(f32)
    b = (v - a).astype(bf).astype(f32)
    return a, b, v - a - b


def in_steps(units, sizes, body, carry):
    at = 0
    for size in sizes:
        count = (units - at) // size
        carry = lax.fori_loop(0, count, lambda i, c, at=at, size=size: body(at + i * size, size, c), carry)
        at = at + count * size
    return carry


def attend_kernel(bq, n_ref, k_ref, qt_ref, vt_ref, ot_ref, qb_ref, p_ref, rt_ref):
    live = n_ref[0]
    qi = pl.program_id(1)
    units = (live + 3) // 4

    def finish(top, acc):
        total = acc[64:65]
        ot_ref[0] = acc[:64] / total
        rt_ref[0] = 1.0 / total
        a, b, c = split3((top + jnp.log2(total)) * (-1.0 / EXP2))
        row = lax.broadcasted_iota(jnp.int32, (64, bq), 0)
        tail = jnp.where(row == 0, 1.0, jnp.where(row == 1, a, jnp.where(row == 2, b, jnp.where(row == 3, c, 0.0))))
        qb_ref[0, :64] = qt_ref[0, :64]
        qb_ref[0, 64:] = tail.astype(bf)

    def keys(u, size):
        return pl.ds(pl.multiple_of(u * 512, 512), size * 512)

    @pl.when(jnp.logical_and(qi * bq < live * 128, n_ref[1] == 1))
    def _():
        qt = qt_ref[0]

        def body(u, size, acc):
            for part in range(size):
                at = keys(u + part, 1)
                p = jnp.exp2(mm(k_ref[0, at, :], qt) * EXP2).astype(bf)
                p_ref[0, at, :] = p
                acc = acc + mm(vt_ref[0, :, at], p)
            return acc

        finish(0.0, in_steps(units, (4, 2, 1), body, jnp.zeros((80, bq), f32)))

    @pl.when(jnp.logical_and(qi * bq < live * 128, n_ref[1] == 0))
    def _():
        qt = qt_ref[0]

        def body(u, size, carry):
            top, acc = carry
            s = mm(k_ref[0, keys(u, size), :], qt) * EXP2
            new = jnp.maximum(top, jnp.max(s, axis=0, keepdims=True))
            p = jnp.exp2(s - new).astype(bf)
            return new, acc * jnp.exp2(top - new) + mm(vt_ref[0, :, keys(u, size)], p)

        finish(*in_steps(units, (2, 1), body, (jnp.full((1, bq), -3e38, f32), jnp.zeros((80, bq), f32))))


def attend(live, k, qt, vt, bq=1024):
    n = k.shape[1]
    spec = pltpu.PrefetchScalarGridSpec(
        num_scalar_prefetch=1,
        grid=(3, n // bq),
        in_specs=[
            pl.BlockSpec((1, n, 128), lambda h, i, s: (h, 0, 0)),
            pl.BlockSpec((1, 128, bq), lambda h, i, s: (h, 0, i)),
            pl.BlockSpec((1, 80, n), lambda h, i, s: (h, 0, 0)),
        ],
        out_specs=[
            pl.BlockSpec((1, 64, bq), lambda h, i, s: (h, 0, i)),
            pl.BlockSpec((1, 128, bq), lambda h, i, s: (h, 0, i)),
            pl.BlockSpec((1, n, bq), lambda h, i, s: (h, 0, i)),
            pl.BlockSpec((1, 1, bq), lambda h, i, s: (h, 0, i)),
        ],
    )
    return pl.pallas_call(
        functools.partial(attend_kernel, bq),
        grid_spec=spec,
        out_shape=[
            jax.ShapeDtypeStruct((3, 64, n), f32),
            jax.ShapeDtypeStruct((3, 128, n), bf),
            jax.ShapeDtypeStruct((3, n, n), bf),
            jax.ShapeDtypeStruct((3, 1, n), f32),
        ],
        compiler_params=params(),
        name="attention_forward",
    )(live, k, qt, vt)


def spread_kernel(src_ref, n_ref, t_ref, ot_ref, *o_refs):
    live, t, tiles = n_ref[0], t_ref[0], len(o_refs)
    per = o_refs[0].shape[1] // 128

    def step(b, _):
        g = src_ref[b]
        lanes = pl.ds(pl.multiple_of(b * 128, 128), 128)
        to = pl.ds(pl.multiple_of((g % per) * 128, 128), 128)
        for k in range(tiles):
            here = (g // per - t + tiles) % tiles == k

            @pl.when(jnp.logical_and(here, b < live))
            def _():
                for h in range(3):
                    o_refs[k][h * 64 : (h + 1) * 64, to] = ot_ref[h, :, lanes].astype(bf)

            @pl.when(jnp.logical_and(here, b >= live))
            def _():
                o_refs[k][:, to] = jnp.zeros((192, 128), bf)

        return 0

    lax.fori_loop(0, ot_ref.shape[2] // 128, step, 0)


def spread(src, live, tile, ot, tiles):
    n = ot.shape[2]
    return pl.pallas_call(
        spread_kernel,
        in_specs=[smem_spec()] * 3 + [vmem_spec()],
        out_specs=[vmem_spec()] * tiles,
        out_shape=[jax.ShapeDtypeStruct((192, n // tiles), bf)] * tiles,
        compiler_params=params(),
        name="spread_attended",
    )(src, live, tile, ot)


def collect_kernel(src_ref, n_ref, t_ref, ot_ref, rt_ref, *refs):
    g_refs, (dt_ref, d_ref) = refs[:-2], refs[-2:]
    live, t, tiles = n_ref[0], t_ref[0], len(g_refs)
    mild = n_ref[1] == 1
    per = g_refs[0].shape[1] // 128
    row = lax.broadcasted_iota(jnp.int32, (64, 128), 0)

    def step(b, _):
        g = src_ref[b]
        to = pl.ds(pl.multiple_of(b * 128, 128), 128)
        lanes = pl.ds(pl.multiple_of((g % per) * 128, 128), 128)
        for k in range(tiles):

            @pl.when(jnp.logical_and((t - g // per + tiles) % tiles == k, b < live))
            def _():
                for h in range(3):
                    scale = jnp.where(mild, rt_ref[h, :, to], 1.0)
                    d = (g_refs[k][h * 64 : (h + 1) * 64, lanes].astype(f32) * scale).astype(bf).astype(f32)
                    x, y, z = split3(-jnp.sum(d * ot_ref[h, :, to], axis=0, keepdims=True))
                    tail = jnp.where(row == 0, x, jnp.where(row == 1, y, jnp.where(row == 2, z, 0.0)))
                    dt_ref[h, :, to] = jnp.concatenate([d, tail], axis=0).astype(bf)
                    d_ref[h, to, :] = jnp.concatenate([d, jnp.zeros_like(d)], axis=0).T.astype(bf)

        @pl.when(b >= live)
        def _():
            dt_ref[:, :, to] = jnp.zeros((3, 128, 128), bf)
            d_ref[:, to, :] = jnp.zeros((3, 128, 128), bf)

        return 0

    lax.fori_loop(0, ot_ref.shape[2] // 128, step, 0)


def collect(src, live, tile, grads, ot, rt):
    n = ot.shape[2]
    return pl.pallas_call(
        collect_kernel,
        in_specs=[smem_spec()] * 3 + [vmem_spec()] * (2 + len(grads)),
        out_specs=[vmem_spec()] * 2,
        out_shape=[jax.ShapeDtypeStruct((3, 128, n), bf), jax.ShapeDtypeStruct((3, n, 128), bf)],
        compiler_params=params(),
        name="collect_attended_grad",
    )(src, live, tile, ot, rt, *grads)


def attend_back_kernel(bk, n_ref, p_ref, k_ref, kt_ref, v_ref, qb_ref, q_ref, dt_ref, d_ref, dq_ref, dk_ref, dv_ref):
    live = n_ref[0]
    j = pl.program_id(1)

    @pl.when(j == 0)
    def _():
        dq_ref[...] = jnp.zeros_like(dq_ref)

    @pl.when(j * bk < live * 128)
    def _():
        k, v, kt = k_ref[0], v_ref[0], kt_ref[0]

        def lanes(u, part):
            return pl.ds(pl.multiple_of((u * 2 + part) * 256, 256), 256)

        def kept(u, size, carry):
            dk, dv = carry
            dp = mm(v, dt_ref[0, :, lanes(u, 0)])
            for part in range(2 * size):
                at = lanes(u, part)
                ahead = mm(v, dt_ref[0, :, lanes(u, part + 1)]) if part + 1 < 2 * size else None
                p = p_ref[0, :, at]
                ds = (p.astype(f32) * dp).astype(bf)
                dv = dv + mm(p, d_ref[0, at, :])
                dk = dk + mm(ds, q_ref[0, at, :])
                dq_ref[0, :, at] += mm(kt, ds)
                dp = dp if ahead is None else ahead
            return dk, dv

        def again(u, size, carry):
            dk, dv = carry
            for part in range(2 * size):
                at = lanes(u, part)
                p = jnp.exp2(mm(k, qb_ref[0, :, at]) * EXP2)
                ds = (p * mm(v, dt_ref[0, :, at])).astype(bf)
                dv = dv + mm(p.astype(bf), d_ref[0, at, :])
                dk = dk + mm(ds, q_ref[0, at, :])
                dq_ref[0, :, at] += mm(kt, ds)
            return dk, dv

        units = (live + 3) // 4
        zero = jnp.zeros((bk, 128), f32)
        dk, dv = lax.cond(
            n_ref[1] == 1,
            lambda: in_steps(units, (4, 2, 1), kept, (zero, zero)),
            lambda: in_steps(units, (2, 1), again, (zero, zero)),
        )
        dk_ref[0] = (dk * SCALE).astype(bf)
        dv_ref[0] = dv.astype(bf)


def attend_back(live, p, k, kt, v, qb, q, dt, d, bk=512):
    n = k.shape[1]
    whole_t = lambda h, j, s: (h, 0, 0)
    spec = pltpu.PrefetchScalarGridSpec(
        num_scalar_prefetch=1,
        grid=(3, n // bk),
        in_specs=[
            pl.BlockSpec((1, bk, n), lambda h, j, s: (h, j, 0)),
            pl.BlockSpec((1, bk, 128), lambda h, j, s: (h, j, 0)),
            pl.BlockSpec((1, 64, bk), lambda h, j, s: (h, 0, j)),
            pl.BlockSpec((1, bk, 128), lambda h, j, s: (h, j, 0)),
            pl.BlockSpec((1, 128, n), whole_t),
            pl.BlockSpec((1, n, 128), whole_t),
            pl.BlockSpec((1, 128, n), whole_t),
            pl.BlockSpec((1, n, 128), whole_t),
        ],
        out_specs=[
            pl.BlockSpec((1, 64, n), whole_t),
            pl.BlockSpec((1, bk, 128), lambda h, j, s: (h, j, 0)),
            pl.BlockSpec((1, bk, 128), lambda h, j, s: (h, j, 0)),
        ],
    )
    return pl.pallas_call(
        functools.partial(attend_back_kernel, bk),
        grid_spec=spec,
        out_shape=[jax.ShapeDtypeStruct((3, 64, n), f32), jax.ShapeDtypeStruct((3, n, 128), bf), jax.ShapeDtypeStruct((3, n, 128), bf)],
        compiler_params=params(),
        name="attention_backward",
    )(live, p, k, kt, v, qb, q, dt, d)


def qkv_back_kernel(src_ref, n_ref, at_ref, dq_ref, dk_ref, dv_ref, a_ref, w_ref, s_in, g_ref, s_ref, gb_ref, acc, sums, rows, packed, sems, psems):
    i = pl.program_id(0)
    live = n_ref[0]

    @pl.when(i == 0)
    def _():
        acc[...] = jnp.zeros_like(acc)
        sums[...] = jnp.zeros_like(sums)

    @pl.when(4 * i < live)
    def _():
        dq = jnp.concatenate([dq_ref[h] for h in range(3)], axis=0).T * SCALE
        g = jnp.concatenate(
            [dq] + [dk_ref[h][:, :64].astype(f32) for h in range(3)] + [dv_ref[h][:, :64].astype(f32) for h in range(3)], axis=1
        ).astype(bf)
        acc[...] += mm(a_ref[...], g, TN)
        sums[...] += jnp.broadcast_to(jnp.sum(g.astype(f32), axis=0, keepdims=True), sums.shape)
        rows[...] = mm(g, w_ref[...], NT).astype(bf)

    @pl.when(4 * i >= live)
    def _():
        rows[...] = jnp.zeros_like(rows)

    copies = [
        pltpu.make_async_copy(rows.at[pl.ds(b * 128, 128)], g_ref.at[pl.ds(pl.multiple_of(src_ref[4 * i + b] * 128, 128), 128)], sems.at[b])
        for b in range(4)
    ]
    for copy in copies:
        copy.start()
    for copy in copies:
        copy.wait()

    @pl.when(i == pl.num_programs(0) - 1)
    def _():
        out = []
        for r in range(4):
            for c in range(3):
                j = r * 3 + c
                top, tail = pack(acc[r * 192 : (r + 1) * 192, c * 192 : (c + 1) * 192], at_ref[12] == 1)
                packed[j, :192] = top.astype(bf)
                packed[j, 192:] = tail.astype(bf)
                out.append(pltpu.make_async_copy(packed.at[j], s_ref.at[at_ref[j]], psems.at[j]))
                out[-1].start()
        gb_ref[...] = sums[...]
        for copy in out:
            copy.wait()


def qkv_backward(src, live, own_at, dq, dk, dv, a, w, slots):
    n = a.shape[0]
    spec = pltpu.PrefetchScalarGridSpec(
        num_scalar_prefetch=3,
        grid=(n // 512,),
        in_specs=[
            pl.BlockSpec((3, 64, 512), lambda i, s, c, o: (0, 0, i)),
            pl.BlockSpec((3, 512, 128), lambda i, s, c, o: (0, i, 0)),
            pl.BlockSpec((3, 512, 128), lambda i, s, c, o: (0, i, 0)),
            pl.BlockSpec((512, 768), lambda i, s, c, o: (i, 0)),
            pl.BlockSpec((768, 576), lambda i, s, c, o: (0, 0)),
            any_spec(),
        ],
        out_specs=[any_spec(), any_spec(), pl.BlockSpec((8, 576), lambda i, s, c, o: (0, 0))],
        scratch_shapes=[
            pltpu.VMEM((768, 576), f32),
            pltpu.VMEM((8, 576), f32),
            pltpu.VMEM((512, 768), bf),
            pltpu.VMEM((12, 288, 128), bf),
            pltpu.SemaphoreType.DMA((4,)),
            pltpu.SemaphoreType.DMA((12,)),
        ],
    )
    return pl.pallas_call(
        qkv_back_kernel,
        grid_spec=spec,
        out_shape=[jax.ShapeDtypeStruct((n, 768), bf), jax.ShapeDtypeStruct(slots.shape, bf), jax.ShapeDtypeStruct((8, 576), f32)],
        input_output_aliases={8: 1},
        compiler_params=params(),
        name="qkv_backward",
    )(src, live, own_at, dq, dk, dv, a, w, slots)


def gelu_parts(z):
    cdf = 0.5 + 0.5 * lax.erf(z * math.sqrt(0.5))
    return z * cdf, cdf + z * (jnp.exp2(z * z * (-0.5 * math.log2(math.e))) * (1.0 / math.sqrt(2.0 * math.pi)))


def middle_kernel(inv_ref, cnt_ref, t_ref, blk_ref, o0, o1, o2, o3, x_ref, c_ref, vp_ref, bu_ref, y_ref, gr_ref, g0, g1, g2_ref, g3,
                  u_s, gz_s, a2_s, gm_s, gb_s, o_s, vs_ref, us_ref, w_out, w_up, w_down, tails, tsem, isem):
    i = pl.program_id(0)
    rows = x_ref.shape[0]
    r0 = i * rows
    kinds = ((w_out, 48, 2, 4), (w_up, 64, 8, 4), (w_down, 128, 2, 16))

    @pl.when(i == 0)
    def _():
        vs_ref[...] = jnp.zeros_like(vs_ref)
        us_ref[...] = jnp.zeros_like(us_ref)

        def pair(w, first, pairs):
            def copies(j):
                r = pl.multiple_of((j // pairs) * 192, 64)
                col = pl.multiple_of((j % pairs) * 384, 128)
                out = []
                for b, off in ((0, 0), (1, 256)):
                    at = first + 2 * j + b
                    slot = inv_ref[at]
                    out.append(pltpu.make_async_copy(blk_ref.at[slot, pl.ds(0, 192)], w.at[pl.ds(r, 192), pl.ds(col + off, 128)], tsem.at[at - 48]))
                    out.append(pltpu.make_async_copy(blk_ref.at[slot, pl.ds(192, 96)], tails.at[at - 48], isem.at[at - 48]))
                return out, r, col

            def start(j, _):
                for copy in copies(j)[0]:
                    copy.start()
                return 0

            def join(j, _):
                got, r, col = copies(j)
                for copy in got:
                    copy.wait()
                even = tails[first + 2 * j - 48].astype(f32)
                odd = tails[first + 2 * j - 47].astype(f32)
                lane = lax.broadcasted_iota(jnp.int32, even.shape, 1) < 64
                w[pl.ds(r, 96), pl.ds(col + 128, 128)] = jnp.where(lane, even, odd).astype(bf)
                w[pl.ds(r + 96, 96), pl.ds(col + 128, 128)] = turn(jnp.where(lane, odd, even)).astype(bf)
                return 0

            return start, join

        todo = [(pair(w, first, pairs), pairs * high) for w, first, pairs, high in kinds]
        for (start, _), n in todo:
            lax.fori_loop(0, n, start, 0)

        for (_, join), n in todo:
            lax.fori_loop(0, n, join, 0)

    vp = vp_ref[...]
    row = r0 + lax.broadcasted_iota(jnp.int32, (rows, 1), 0)
    live = jnp.where(row < cnt_ref[0], 1.0, 0.0)
    t = t_ref[0]
    for k, ref in enumerate((o0, o1, o2, o3)):
        o_s[pl.ds(pl.multiple_of(((t - k + 4) % 4) * 192, 64), 192), :] = ref[...]
    o_t = o_s[...]
    res = x_ref[...].astype(f32) + mm(o_t, w_out[...], TN) + vp[6:7]
    cen = res - jnp.mean(res, axis=-1, keepdims=True)
    inv_std = lax.rsqrt(jnp.mean(cen * cen, axis=-1, keepdims=True) + EPS_NORM)
    normed = cen * inv_std
    a2 = (normed * vp[2:3] + vp[3:4]).astype(bf)
    gy = c_ref[...].astype(f32) * live
    gm = gy.astype(bf)
    a2_s[...] = a2
    gm_s[...] = gm
    branch = jnp.zeros((rows, 768), f32)
    g2 = jnp.zeros((rows, 768), f32)
    for j in range(4):
        cols = slice(j * 768, (j + 1) * 768)
        u, slope = gelu_parts(mm(a2, w_up[:, cols]) + bu_ref[:, cols])
        u = u.astype(bf)
        u_s[:, cols] = u
        branch = branch + mm(u, w_down[cols, :])
        gz = (mm(gm, w_down[cols, :], NT) * slope).astype(bf)
        gz_s[:, cols] = gz
        us_ref[:, cols] += jnp.broadcast_to(column_sum(gz.astype(f32)), (8, 768))
        g2 = g2 + mm(gz, w_up[:, cols], NT)
    y_ref[...] = (live * (res + branch + vp[7:8])).astype(bf)
    d2 = g2 * vp[2:3]
    gr = gy + inv_std * (d2 - jnp.mean(d2, axis=-1, keepdims=True) - normed * jnp.mean(d2 * normed, axis=-1, keepdims=True))
    gr_ref[...] = gr
    gb = gr.astype(bf)
    gb_s[...] = gb
    vs_ref[0:1, :] += column_sum(g2 * normed)
    vs_ref[1:2, :] += column_sum(g2)
    vs_ref[2:3, :] += column_sum(gb.astype(f32))
    vs_ref[3:4, :] += column_sum(gm.astype(f32))
    for k, ref in enumerate((g0, g1, g2_ref, g3)):
        ref[...] = mm(w_out[pl.ds(pl.multiple_of(((t + k) % 4) * 192, 64), 192), :], gb, NT).astype(bf)


def weight_grad_kernel(inv_ref, o_in, gb_in, a2_in, gz_in, u_in, gm_in, s_ref, o_s, gb_s, a2_s, gz_s, u_s, gm_s, ring, zero, lsem, osem, zsem):
    def zero_copy(j):
        return pltpu.make_async_copy(zero, s_ref.at[inv_ref[j]], zsem.at[j])

    loads = [pltpu.make_async_copy(a, b, lsem.at[j]) for j, (a, b) in enumerate(
        ((o_in, o_s), (gb_in, gb_s), (a2_in, a2_s), (gz_in, gz_s), (gm_in, gm_s), (u_in, u_s)))]
    for load in loads:
        load.start()
    zero[...] = jnp.zeros_like(zero)

    def clear(j, _):
        zero_copy(j).start()
        return 0

    lax.fori_loop(0, 48, clear, 0)
    def out_copy(k, at):
        return pltpu.make_async_copy(ring.at[k], s_ref.at[inv_ref[at]], osem.at[k])

    def send(n, g, first, pairs, high, low):
        half = (n % 2) * 8

        def put(r, b):
            return first + (high + r) * 2 * pairs + 2 * low + b

        for r in range(4):
            part = g[r * 192 : (r + 1) * 192]
            mid = part[:, 128:256]
            upper, lower = mid[:96], turn(mid[96:])
            lane = lax.broadcasted_iota(jnp.int32, upper.shape, 1) < 64
            for b, top, tail in ((0, part[:, :128], jnp.where(lane, upper, lower)), (1, part[:, 256:], jnp.where(lane, lower, upper))):
                k = half + 2 * r + b

                @pl.when(n >= 2)
                def _():
                    out_copy(k, 0).wait()

                ring[k, :192] = top.astype(bf)
                ring[k, 192:] = tail.astype(bf)
                out_copy(k, put(r, b)).start()

    def lanes(j):
        return pl.ds(pl.multiple_of(j * 384, 128), 384)

    def grad_out(n, _):
        send(n, mm(o_s[...], gb_s[:, lanes(n)]), 48, 2, 0, n)
        return 0

    def grad_up(n, _):
        send(n, mm(a2_s[...], gz_s[:, lanes(n)], TN), 64, 8, 0, n)
        return 0

    def grad_down(n, _):
        high = n // 2
        send(n, mm(u_s[:, pl.ds(pl.multiple_of(high * 768, 128), 768)], gm_s[:, lanes(n % 2)], TN), 128, 2, high * 4, n % 2)
        return 0

    def drain():
        for k in range(16):
            out_copy(k, 0).wait()

    for f, n, first in ((grad_out, 2, 0), (grad_up, 8, 2), (grad_down, 8, 4)):
        loads[first].wait()
        loads[first + 1].wait()
        lax.fori_loop(0, n, f, 0)
        drain()

    def cleared(j, _):
        zero_copy(j).wait()
        return 0

    lax.fori_loop(0, 48, cleared, 0)


def middle(inv, count, tile, blocks, o_parts, tokens, cotangent, vec_params, bias_up, rows=256):
    n, width = tokens.shape
    hidden = bias_up.shape[1]
    row = lambda i, s, c, t: (i, 0)
    fixed = lambda i, s, c, t: (0, 0)
    col = lambda i, s, c, t: (0, i)
    V, DS = pltpu.VMEM, pltpu.SemaphoreType.DMA
    narrow, wide, part = pl.BlockSpec((rows, width), row), pl.BlockSpec((rows, hidden), row), pl.BlockSpec((192, rows), col)
    spec = pltpu.PrefetchScalarGridSpec(
        num_scalar_prefetch=3,
        grid=(n // rows,),
        in_specs=[any_spec()] + [part] * 4 + [narrow, narrow, pl.BlockSpec((12, width), fixed), pl.BlockSpec((1, hidden), fixed)],
        out_specs=[narrow, narrow] + [part] * 4 + [wide, wide, narrow, narrow, narrow, pl.BlockSpec((width, rows), col),
                   pl.BlockSpec((8, width), fixed), pl.BlockSpec((8, hidden), fixed)],
        scratch_shapes=[V((768, 768), bf), V((768, 3072), bf), V((3072, 768), bf), V((144, 96, 128), bf), DS((144,)), DS((144,))],
    )
    S = jax.ShapeDtypeStruct
    return pl.pallas_call(
        middle_kernel,
        grid_spec=spec,
        out_shape=[S((n, width), bf), S((n, width), f32)] + [S((192, n), bf)] * 4 + [S((n, hidden), bf)] * 2 + [S((n, width), bf)] * 3
        + [S((width, n), bf), S((8, width), f32), S((8, hidden), f32)],
        compiler_params=params(),
        name="projection_and_mlp",
    )(inv, count, tile, blocks, *o_parts, tokens, cotangent, vec_params, bias_up)


def weight_grads_to_slots(inv, block_count, o_t, gb, a2, gz, u, gm):
    V, DS = pltpu.VMEM, pltpu.SemaphoreType.DMA
    arrays = (o_t, gb, a2, gz, u, gm)
    return pl.pallas_call(
        weight_grad_kernel,
        in_specs=[smem_spec()] + [any_spec()] * 6,
        out_specs=any_spec(),
        out_shape=jax.ShapeDtypeStruct((block_count, 288, 128), bf),
        scratch_shapes=[V(a.shape, bf) for a in arrays] + [V((16, 288, 128), bf), V((288, 128), bf), DS((6,)), DS((16,)), DS((48,))],
        cost_estimate=pl.CostEstimate(flops=6 * 10**10, bytes_accessed=32 * 10**6, transcendentals=0),
        compiler_params=params(),
        name="mlp_weight_gradients",
    )(inv, *arrays)


def split2(v):
    hi = v.astype(bf)
    return hi, (v - hi.astype(f32)).astype(bf)


def mm3(a, b, dims):
    return mm(a[0], b[0], dims) + (mm(a[0], b[1], dims) + mm(a[1], b[0], dims))


def adam_kernel(odd_ref, g_ref, m1_ref, m2_ref, l_ref, r_ref, g_out, m1_out, m2_out, u_out, s_out):
    for b in range(g_ref.shape[0]):
        grad = unpack(g_ref[b, :192].astype(f32), g_ref[b, 192:].astype(f32), odd_ref[pl.program_id(0) * g_ref.shape[0] + b] == 1)
        left, right = split2(l_ref[b]), split2(r_ref[b])
        low = grad.astype(bf)
        rot = mm3(split2(mm(left[0], low, TN) + mm(left[1], low, TN)), right, NN)
        first = BETA_ONE * m1_ref[b] + (1.0 - BETA_ONE) * rot
        second = BETA_TWO * m2_ref[b] + (1.0 - BETA_TWO) * rot * rot
        upd = (first / (1.0 - BETA_ONE**STEP)) / (jnp.sqrt(second / (1.0 - BETA_TWO**STEP)) + ADAM_EPS)
        upd = mm3(split2(mm3(left, split2(upd), NN)), right, NT)
        g_out[b] = grad
        m1_out[b] = first
        m2_out[b] = second
        u_out[b] = upd
        s_out[b] = jnp.full((8, 128), jnp.sum(upd * upd), f32)


def adam(odd, grads, first, second, left, right):
    n = grads.shape[0]
    g = group_of(n)
    at = lambda i, s: (i, 0, 0)
    big = pl.BlockSpec((g, 192, 192), at)
    spec = pltpu.PrefetchScalarGridSpec(
        num_scalar_prefetch=1,
        grid=(n // g,),
        in_specs=[pl.BlockSpec((g, 288, 128), at)] + [big] * 4,
        out_specs=[big] * 4 + [pl.BlockSpec((g, 8, 128), at)],
    )
    return pl.pallas_call(
        adam_kernel,
        grid_spec=spec,
        out_shape=[jax.ShapeDtypeStruct((n, 192, 192), f32)] * 4 + [jax.ShapeDtypeStruct((n, 8, 128), f32)],
        compiler_params=params(),
        name="rotated_adam",
    )(odd, grads, first, second, left, right)


def norm_forward(row_data, gain_vec, shift_vec):
    row_mean = jnp.mean(row_data, axis=-1, keepdims=True)
    centred = row_data - row_mean
    inv_std = lax.rsqrt(jnp.mean(centred * centred, axis=-1, keepdims=True) + EPS_NORM)
    normed = centred * inv_std
    return (normed * gain_vec + shift_vec, normed, inv_std)


def norm_back(grad_out, normed, inv_std, gain_vec):
    grad_normed = grad_out * gain_vec
    return inv_std * (
        grad_normed
        - jnp.mean(grad_normed, axis=-1, keepdims=True)
        - normed * jnp.mean(grad_normed * normed, axis=-1, keepdims=True)
    )


def block_plan(counts, slot_count):
    tiles = counts.shape[0]
    per = slot_count // 128
    j = lax.broadcasted_iota(jnp.int32, (tiles, per), 1)
    kept = jnp.clip(counts[:, None] - j * 128, 0, 128).reshape(-1)
    full = (kept > 0).astype(jnp.int32)
    index = jnp.arange(tiles * per, dtype=jnp.int32)
    before = (index[None, :] < index[:, None]).astype(jnp.int32)
    ahead = jnp.sum(before * full[None, :], axis=1)
    live = jnp.sum(full)
    place = jnp.where(full > 0, ahead, live + index - ahead)
    hot = (place[None, :] == index[:, None]).astype(jnp.int32)
    return jnp.sum(hot * index[None, :], axis=1), jnp.sum(hot * kept[None, :], axis=1), live.reshape(1)


def make_body(tuned):
    def body(tokens, cotangent, counts, master, slot_block, groups, first_moment, second_moment, left_basis, right_basis, vec_params, vec_first, vec_second):
        slot_count, width = tokens.shape[1:]
        per_owner = master.shape[0]
        tile = lax.axis_index("tile")
        mine = lax.dynamic_slice(slot_block, (lax.axis_index("dp") * per_owner,), (per_owner,))
        odd = mine % 2
        packed, weight_sq = pack_master(odd, master)
        own_tokens = tokens.reshape(slot_count, width)
        count_tile = jnp.broadcast_to(counts.reshape(1, 1), (8, 128))
        if tuned:
            blocks, token_all, count_all = gather_all(packed, own_tokens, count_tile)
        else:
            blocks = lax.all_gather(packed, "dp", axis=0, tiled=True)
            token_all = lax.all_gather(own_tokens, "tile", axis=0)
            count_all = lax.all_gather(count_tile, "tile", axis=0)
        tiles = token_all.shape[0]
        block_count = blocks.shape[0]
        src, cnt, live = block_plan(count_all[:, 0, 0], slot_count)
        index = jnp.arange(block_count, dtype=jnp.int32)
        inverse = jnp.sum((slot_block[None, :] == index[:, None]).astype(jnp.int32) * index[None, :], axis=1)
        own_block = jnp.arange(12, dtype=jnp.int32) // 3 * 12 + jnp.arange(12, dtype=jnp.int32) % 3 * 4 + tile
        own_at = jnp.sum((slot_block[None, :] == own_block[:, None]).astype(jnp.int32) * index[None, :], axis=1)
        own_at = jnp.concatenate([own_at, tile.reshape(1) % 2])
        own = width // tiles
        bias = lambda row: lax.dynamic_slice(vec_params[row : row + 1], (0, tile * own), (1, own))
        a1, q, qt, k, kt, v, vt, w_qkv, lengths = qkv_forward(
            src, cnt, own_at, token_all.reshape(-1, width), blocks, vec_params[0:1], vec_params[1:2], bias(4), bias(5)
        )
        mild = jnp.sqrt(jnp.max(lengths[:, 0, 0])) * jnp.sqrt(jnp.max(lengths[:, 1, 0])) * EXP2 <= 60.0
        live = jnp.concatenate([live, mild.astype(jnp.int32).reshape(1)])
        ot, qb, p, rt = attend(live, k, qt, vt)

        def shift(parts):
            return [parts[0]] + [lax.ppermute(parts[j], "tile", [(s, (s + j) % tiles) for s in range(tiles)]) for j in range(1, tiles)]

        tile_one = tile.astype(jnp.int32).reshape(1)
        o_parts = shift(spread(src, live, tile_one, ot, tiles))
        output, grad_resid, *rest = middle(
            inverse, counts.reshape(1), tile_one, blocks, o_parts, own_tokens, cotangent.reshape(slot_count, width), vec_params, vec_params[8:].reshape(1, -1)
        )
        go_parts, (u, gz, a2, gm, gb, o_t, sums, up_sums) = rest[:tiles], rest[tiles:]
        go_parts = shift(go_parts)
        slots = weight_grads_to_slots(inverse, block_count, o_t, gb, a2, gz, u, gm)
        dt, d = collect(src, live, tile_one, go_parts, ot, rt)
        dq, dk, dv = attend_back(live, p, k, kt, v, qb, q, dt, d)
        g_part, slot_grads, qkv_sums = qkv_backward(src, live, own_at, dq, dk, dv, a1, w_qkv, slots)
        g_part = g_part.reshape(tiles, slot_count, width)
        if tuned:
            g1 = lax.psum_scatter(g_part, "tile", scatter_dimension=0, tiled=False).astype(f32)
            grads = grad_sum(slot_grads.reshape(-1, per_owner, 288, 128))
        else:
            g1 = lax.psum_scatter(g_part.astype(f32), "tile", scatter_dimension=0, tiled=False)
            grads = lax.psum(lax.psum_scatter(slot_grads.astype(f32), "dp", scatter_dimension=0, tiled=True), "tile").astype(bf)
        row_input = own_tokens.astype(f32)
        _, normed_one, inv_std_one = norm_forward(row_input, vec_params[0], vec_params[1])
        input_grad = grad_resid + norm_back(g1, normed_one, inv_std_one, vec_params[0])
        zero = jnp.zeros((width,), f32)
        at_own = lambda s: lax.dynamic_update_slice(zero, s, (tile * own,))
        rows = jnp.stack(
            [jnp.sum(g1 * normed_one, axis=0), jnp.sum(g1, axis=0), sums[0], sums[1], at_own(qkv_sums[0, :own]), at_own(qkv_sums[0, 2 * own :]), sums[2], sums[3]],
            axis=0,
        )
        vector_part = jnp.concatenate([rows, up_sums[0].reshape(-1, width)], axis=0)

        weight_grads, first_out, second_out, update, update_sq = adam(odd, grads, first_moment, second_moment, left_basis, right_basis)
        group_hot = (groups[:, None] == jnp.arange(NGRP, dtype=jnp.int32)[None, :]).astype(f32)
        both = jnp.stack([weight_sq[:, 0, 0], update_sq[:, 0, 0]], axis=0)
        group_part = jnp.pad(jnp.sum(group_hot[None] * both[:, :, None], axis=1), ((0, 6), (0, 128 - NGRP)))
        vector_grads, group_both = totals(vector_part, group_part, block_count // per_owner, tiles)
        own_both = jnp.sum(group_hot[None] * group_both[:2, None, :NGRP], axis=2)
        block_rate = RATE_BLOCK * jnp.sqrt(own_both[0]) / (jnp.sqrt(own_both[1]) + 1e-06)
        master_out = master - block_rate[:, None, None] * update
        vec_first_out = BETA_ONE * vec_first + (1.0 - BETA_ONE) * vector_grads
        vec_second_out = BETA_TWO * vec_second + (1.0 - BETA_TWO) * vector_grads * vector_grads
        vec_update = (vec_first_out / (1.0 - BETA_ONE**STEP)) / (jnp.sqrt(vec_second_out / (1.0 - BETA_TWO**STEP)) + ADAM_EPS)
        return (
            output.reshape(1, slot_count, width),
            input_grad.reshape(1, slot_count, width),
            weight_grads,
            first_out,
            second_out,
            master_out,
            master_out.astype(bf),
            vector_grads,
            vec_first_out,
            vec_second_out,
            vec_params - RATE_VECTOR * vec_update,
        )

    return body


def solution(mesh):
    tuned = (mesh.shape["dp"], mesh.shape["tile"]) == (8, 4)
    rows, blocks = P("dp", "tile", None), P("dp", None, None)
    return jax.shard_map(
        make_body(tuned),
        mesh=mesh,
        in_specs=(rows, rows, P("dp", "tile"), blocks, P(), P("dp"), blocks, blocks, blocks, blocks, P(), P(), P()),
        out_specs=(rows, rows, blocks, blocks, blocks, blocks, blocks, P(), P(), P(), P()),
        check_vma=False,
    )
```

```python
import functools
import math

import jax
import jax.numpy as jnp
from jax import lax
from jax.experimental import pallas as pl
from jax.experimental.pallas import tpu as pltpu
from jax.sharding import PartitionSpec as P

f32 = jnp.float32
bf = jnp.bfloat16
MESH = pl.DeviceIdType.MESH

def where_am_i():
    dp=lax.axis_index("dp"); t=lax.axis_index("tile")
    return dp//2, dp%2, t//2, t%2

def dev(z,y,x,c):
    return (z*2+y, x*2+c)

def rcopy(src,dst,ss,rs,to):
    return pltpu.make_async_remote_copy(src_ref=src,dst_ref=dst,send_sem=ss,recv_sem=rs,device_id=to,device_id_type=MESH)

def gather_kernel(own_w,own_tok,own_cnt,all_w,all_tok,all_cnt,
                  zs,zr,ys,yr,xs,xr,cs,cr,fs,fr,ts,tr,ns,nr,ls):
    z,y,x,c=where_am_i()
    per=own_w.shape[0]
    part=per//12
    def a_of(shard,xx,cc): return all_w.at[pl.ds(shard*per+(xx*2+cc)*part,part)]
    def b_of(shard,cc): return all_w.at[pl.ds(shard*per+4*part+cc*4*part,4*part)]
    own_a=own_w.at[pl.ds((x*2+c)*part,part)]
    own_b=own_w.at[pl.ds(4*part+c*4*part,4*part)]
    me=z*2+y
    core=dev(z,y,x,1-c); across=dev(z,y,1-x,c); beside=dev(z,1-y,x,c)
    up=dev(jnp.minimum(z+1,3),y,x,c); down=dev(jnp.maximum(z-1,0),y,x,c)
    def src(shard,own):
        return (own_a,own_b) if own else (a_of(shard,x,c),b_of(shard,c))
    def z_copies(zz,own,go_up):
        shard=zz*2+y
        a,b=src(shard,own)
        d=(z-zz) if go_up else (zz-z)
        k=0 if go_up else 1
        to=up if go_up else down
        return (rcopy(a,a_of(shard,x,c),zs.at[k,d,0],zr.at[k,d,0],to),rcopy(b,b_of(shard,c),zs.at[k,d,1],zr.at[k,d,1],to))
    def z_arrivals(zz,k,dist):
        shard=zz*2+y
        a,b=a_of(shard,x,c),b_of(shard,c)
        return (rcopy(a,a,zs.at[k,dist-1,0],zr.at[k,dist-1,0],up),rcopy(b,b,zs.at[k,dist-1,1],zr.at[k,dist-1,1],up))
    def y_copies(zz,own):
        shard=zz*2+y
        a,b=src(shard,own)
        return (rcopy(a,a_of(shard,x,c),ys.at[zz,0],yr.at[zz,0],beside),rcopy(b,b_of(shard,c),ys.at[zz,1],yr.at[zz,1],beside))
    def y_arrivals(zz):
        shard=zz*2+(1-y)
        a,b=a_of(shard,x,c),b_of(shard,c)
        return (rcopy(a,a,ys.at[zz,0],yr.at[zz,0],beside),rcopy(b,b,ys.at[zz,1],yr.at[zz,1],beside))
    def x_copy(shard,own):
        return rcopy(src(shard,own)[0],a_of(shard,x,c),xs.at[shard],xr.at[shard],across)
    def x_arrival(shard):
        a=a_of(shard,1-x,c)
        return rcopy(a,a,xs.at[shard],xr.at[shard],across)
    def c_copies(shard,own):
        a,b=src(shard,own)
        return (rcopy(a,a_of(shard,x,c),cs.at[shard,0],cr.at[shard,0],core),rcopy(b,b_of(shard,c),cs.at[shard,1],cr.at[shard,1],core))
    def c_arrivals(shard):
        a,b=a_of(shard,x,1-c),b_of(shard,1-c)
        return (rcopy(a,a,cs.at[shard,0],cr.at[shard,0],core),rcopy(b,b,cs.at[shard,1],cr.at[shard,1],core))
    def f_copy(shard):
        a=a_of(shard,1-x,c)
        return rcopy(a,a,fs.at[shard],fr.at[shard],core)
    def f_arrival(shard):
        a=a_of(shard,1-x,1-c)
        return rcopy(a,a,fs.at[shard],fr.at[shard],core)
    def start(cps):
        for cp in (cps if isinstance(cps,tuple) else (cps,)): cp.start()
    def got(cps):
        for cp in (cps if isinstance(cps,tuple) else (cps,)): cp.wait_recv()
    def sent(cps):
        for cp in (cps if isinstance(cps,tuple) else (cps,)): cp.wait_send()
    tile=x*2+c
    tok_x=rcopy(own_tok,all_tok.at[tile],ts.at[0],tr.at[0],across)
    tok_c=rcopy(own_tok,all_tok.at[tile],ts.at[1],tr.at[1],core)
    far=all_tok.at[(1-x)*2+c]
    tok_f=rcopy(far,far,ts.at[2],tr.at[2],core)
    near=all_tok.at[x*2+1-c]
    diag=all_tok.at[(1-x)*2+1-c]
    cnts=[rcopy(own_cnt,all_cnt.at[tile],ns.at[i],nr.at[i],to) for i,to in enumerate((across,core,dev(z,y,1-x,1-c)))]
    cnt_in=[rcopy(r,r,ns.at[i],nr.at[i],core) for i,r in enumerate((all_cnt.at[(1-x)*2+c],all_cnt.at[x*2+1-c],all_cnt.at[(1-x)*2+1-c]))]
    local=(pltpu.make_async_copy(own_w,all_w.at[pl.ds(me*per,per)],ls.at[0]),
           pltpu.make_async_copy(own_tok,all_tok.at[tile],ls.at[1]),pltpu.make_async_copy(own_cnt,all_cnt.at[tile],ls.at[2]))
    @pl.when(z<3)
    def _(): start(z_copies(z,True,True))
    @pl.when(z>0)
    def _(): start(z_copies(z,True,False))
    start(y_copies(z,True)); start(tok_x); start(tok_c)
    for cp in cnts: cp.start()
    for cp in local: cp.start()
    def from_line(k,dist):
        zz=z-dist if k==0 else z+dist
        there=(zz>=0) if k==0 else (zz<=3)
        @pl.when(there)
        def _():
            got(z_arrivals(zz,k,dist))
            @pl.when((z<3) if k==0 else (z>0))
            def _(): start(z_copies(zz,False,k==0))
            start(y_copies(zz,False)); start(x_copy(zz*2+y,False)); start(c_copies(zz*2+y,False))
    def from_beside(zz):
        got(y_arrivals(zz))
        s=zz*2+1-y
        start(x_copy(s,False)); start(c_copies(s,False))
    def guarded(f,dist):
        @pl.when(z-dist>=0)
        def _(): f(z-dist)
        @pl.when(z+dist<=3)
        def _(): f(z+dist)
    def from_across(shard):
        got(x_arrival(shard)); start(f_copy(shard))
    from_line(0,1); from_line(1,1)
    from_beside(z)
    from_line(0,2); from_line(1,2)
    guarded(from_beside,1); guarded(lambda zz: from_across(zz*2+y),1); from_across(z*2+1-y)
    from_line(0,3); from_line(1,3)
    got(tok_x); tok_f.start()
    guarded(from_beside,2); guarded(lambda zz: from_across(zz*2+y),2); guarded(lambda zz: from_across(zz*2+1-y),1)
    guarded(from_beside,3); guarded(lambda zz: from_across(zz*2+y),3); guarded(lambda zz: from_across(zz*2+1-y),2)
    guarded(lambda zz: from_across(zz*2+1-y),3)
    def drain(s,_):
        @pl.when(s!=me)
        def _():
            got(c_arrivals(s)); got(f_arrival(s)); sent(c_copies(s,False)); sent(f_copy(s)); sent(x_copy(s,False))
        return 0
    lax.fori_loop(0,8,drain,0)
    def drain_y(zz,_):
        sent(y_copies(zz,False)); return 0
    lax.fori_loop(0,4,drain_y,0)
    for dist in range(4):
        @pl.when(jnp.logical_and(z<3,z-dist>=0))
        def _(): sent(z_copies(z-dist,False,True))
        @pl.when(jnp.logical_and(z>0,z+dist<=3))
        def _(): sent(z_copies(z+dist,False,False))
    rcopy(near,near,ts.at[1],tr.at[1],core).wait_recv()
    rcopy(diag,diag,ts.at[2],tr.at[2],core).wait_recv()
    tok_x.wait_send(); tok_c.wait_send(); tok_f.wait_send()
    for cp in cnts: cp.wait_send()
    for cp in cnt_in: cp.wait_recv()
    for cp in local: cp.wait()

def gather_all(own_w,own_tok,own_cnt):
    DS=pltpu.SemaphoreType.DMA
    hbm=pl.BlockSpec(memory_space=pl.ANY)
    return pl.pallas_call(gather_kernel,
        out_shape=[jax.ShapeDtypeStruct((8*own_w.shape[0],)+own_w.shape[1:],bf),jax.ShapeDtypeStruct((4,)+own_tok.shape,bf),jax.ShapeDtypeStruct((4,)+own_cnt.shape,own_cnt.dtype)],
        in_specs=[pl.BlockSpec(memory_space=pltpu.VMEM)]*3,out_specs=[hbm]*3,
        scratch_shapes=[DS((2,4,2)),DS((2,4,2)),DS((4,2)),DS((4,2)),DS((8,)),DS((8,)),DS((8,2)),DS((8,2)),DS((8,)),DS((8,)),DS((3,)),DS((3,)),DS((3,)),DS((3,)),DS((3,))],
        compiler_params=pltpu.CompilerParams(has_side_effects=True,vmem_limit_bytes=60<<20),name="gather_weights_tokens")(own_w,own_tok,own_cnt)

def group_sum_kernel(g_ref,o_ref,gd,gs,gr):
    dp=lax.axis_index("dp"); t=lax.axis_index("tile")
    nd=gd.shape[0]
    def copy(k):
        return rcopy(gd.at[dp],gd.at[dp],gs.at[k],gr.at[k],((dp+k)%nd,t))
    def arrive(k):
        q=(dp-k+nd)%nd
        return rcopy(gd.at[q],gd.at[q],gs.at[k],gr.at[k],(q,t))
    def loop(f):
        def s(k,_):
            f(k); return 0
        lax.fori_loop(1,nd,s,0)
    gd[dp]=g_ref[...]
    loop(lambda k: copy(k).start())
    loop(lambda k: arrive(k).wait_recv())
    acc=gd[0]
    for i in range(1,nd): acc=acc+gd[i]
    o_ref[...]=acc
    loop(lambda k: copy(k).wait_send())

def group_sum(g,nd):
    DS=pltpu.SemaphoreType.DMA
    vm=pl.BlockSpec(memory_space=pltpu.VMEM)
    return pl.pallas_call(group_sum_kernel,out_shape=jax.ShapeDtypeStruct(g.shape,f32),in_specs=[vm],out_specs=vm,
        scratch_shapes=[pltpu.VMEM((nd,)+g.shape,f32),DS((nd,)),DS((nd,))],
        compiler_params=pltpu.CompilerParams(has_side_effects=True,vmem_limit_bytes=60<<20),name="sum_groups")(g)

def last_sums_kernel(l_ref,k0,k1,k2,r0,r1,r2,v_ref,early,late,vo_ref,lr,vt,vd,ls,lrs,ps,pr,xs,xr,cs,cr,fs,fr,es,er,ts,tr,ds,dr):
    z,y,x,c=where_am_i()
    dp=lax.axis_index("dp"); t=lax.axis_index("tile")
    core=dev(z,y,x,1-c); across=dev(z,y,1-x,c)
    def loop(f,first=0,n=8):
        def s(k,_):
            f(k); return 0
        lax.fori_loop(first,n,s,0)
    def l_copy(k):
        p=(dp+k)%8
        return rcopy(l_ref.at[pl.ds(p*3,3)],lr.at[dp],ls.at[k],lrs.at[k],(p,t))
    def l_arrive(k):
        q=(dp-k+8)%8
        return rcopy(lr.at[q],lr.at[q],ls.at[k],lrs.at[k],(q,t))
    loop(lambda k: l_copy(k).start(),1)
    def t_copy(k): return rcopy(vt.at[t],vt.at[t],ts.at[k],tr.at[k],(dp,(t+k)%4))
    def t_arrive(k):
        q=(t-k+4)%4
        return rcopy(vt.at[q],vt.at[q],ts.at[k],tr.at[k],(dp,q))
    def d_copy(k): return rcopy(vd.at[dp],vd.at[dp],ds.at[k],dr.at[k],((dp+k)%8,t))
    def d_arrive(k):
        q=(dp-k+8)%8
        return rcopy(vd.at[q],vd.at[q],ds.at[k],dr.at[k],(q,t))
    vt[t]=v_ref[...]
    loop(lambda k: t_copy(k).start(),1,4)
    def place(xx,cc,p): return early.at[pl.ds(cc*12+p*4+xx*2,2)]
    for p,(kept,came) in enumerate(((k0,r0),(k1,r1),(k2,r2))):
        early[pl.ds(c*12+p*4+x*2,2)]=(kept[...].astype(f32)+came[...].astype(f32)).astype(bf)
    def e_copy(i,p):
        r=place(1-x,c,p) if i==2 else place(x,c,p)
        return rcopy(r,r,es.at[i,p],er.at[i,p],across if i==0 else core)
    def e_arrive(i,p):
        r=(place(1-x,c,p),place(x,1-c,p),place(1-x,1-c,p))[i]
        return rcopy(r,r,es.at[i,p],er.at[i,p],core)
    for p in range(3):
        e_copy(0,p).start(); e_copy(1,p).start()
    lr[dp]=l_ref[pl.ds(dp*3,3)]
    loop(lambda k: t_arrive(k).wait_recv(),1,4)
    vd[dp]=vt[0]+vt[1]+vt[2]+vt[3]
    loop(lambda k: d_copy(k).start(),1)
    loop(lambda k: l_arrive(k).wait_recv(),1)
    for i in range(3):
        acc=lr[0,i].astype(f32)
        for q in range(1,8): acc=acc+lr[q,i].astype(f32)
        late[t,dp*3+i]=acc.astype(bf)
    def piece(tt,q): return late.at[tt,pl.ds(q*3,3)]
    def p_copy(k): return rcopy(piece(t,dp),piece(t,dp),ps.at[k],pr.at[k],((dp+k)%8,t))
    def p_arrive(k):
        q=(dp-k+8)%8
        return rcopy(piece(t,q),piece(t,q),ps.at[k],pr.at[k],(q,t))
    def x_copy(q): return rcopy(piece(t,q),piece(t,q),xs.at[q],xr.at[q],across)
    def x_arrive(q): return rcopy(piece((1-x)*2+c,q),piece((1-x)*2+c,q),xs.at[q],xr.at[q],across)
    def c_copy(q): return rcopy(piece(t,q),piece(t,q),cs.at[q],cr.at[q],core)
    def c_arrive(q): return rcopy(piece(x*2+1-c,q),piece(x*2+1-c,q),cs.at[q],cr.at[q],core)
    def f_copy(q): return rcopy(piece((1-x)*2+c,q),piece((1-x)*2+c,q),fs.at[q],fr.at[q],core)
    def f_arrive(q): return rcopy(piece((1-x)*2+1-c,q),piece((1-x)*2+1-c,q),fs.at[q],fr.at[q],core)
    loop(lambda k: p_copy(k).start(),1)
    x_copy(dp).start(); c_copy(dp).start()
    for p in range(3):
        e_arrive(0,p).wait_recv(); e_copy(2,p).start()
    def onward(k):
        q=(dp-k+8)%8
        p_arrive(k).wait_recv(); x_copy(q).start(); c_copy(q).start()
    loop(onward,1)
    loop(lambda k: d_arrive(k).wait_recv(),1)
    acc=vd[0]
    for i in range(1,8): acc=acc+vd[i]
    vo_ref[...]=acc
    def over(k):
        q=(dp-k+8)%8
        x_arrive(q).wait_recv(); f_copy(q).start()
    loop(over)
    def drain(q):
        c_arrive(q).wait_recv(); f_arrive(q).wait_recv()
        x_copy(q).wait_send(); c_copy(q).wait_send(); f_copy(q).wait_send()
    loop(drain)
    def sent(k):
        l_copy(k).wait_send(); p_copy(k).wait_send(); d_copy(k).wait_send()
    loop(sent,1)
    loop(lambda k: t_copy(k).wait_send(),1,4)
    for p in range(3):
        e_arrive(1,p).wait_recv(); e_arrive(2,p).wait_recv()
        for i in range(3): e_copy(i,p).wait_send()

def last_sums(own,kept,came,v):
    DS=pltpu.SemaphoreType.DMA
    vm=pl.BlockSpec(memory_space=pltpu.VMEM)
    V=pltpu.VMEM
    S=jax.ShapeDtypeStruct
    early,late,total=pl.pallas_call(last_sums_kernel,out_shape=[S((24,288,128),bf),S((4,24,144,128),bf),S(v.shape,f32)],in_specs=[vm]*8,out_specs=[vm]*3,
        scratch_shapes=[V((8,3,144,128),bf),V((4,)+v.shape,f32),V((8,)+v.shape,f32)]+[DS((8,))]*10+[DS((3,3))]*2+[DS((4,))]*2+[DS((8,))]*2,
        cost_estimate=pl.CostEstimate(flops=10**7,bytes_accessed=150*10**6,transcendentals=0),
        compiler_params=pltpu.CompilerParams(has_side_effects=True,vmem_limit_bytes=60<<20),name="last_gradient_sums")(own.reshape(24,144,128),*kept,*came,v)
    return early,late.reshape(48,288,128),total


H = 12
NGRP = 16
STEP = 10
EPS_NORM = 1e-06
BETA_ONE = 0.5
BETA_TWO = 0.5
ADAM_EPS = 1e-08
RATE_BLOCK = 0.3
RATE_VECTOR = 0.2
NEG_RAW = -8.0e9
HEAD = 64
SCALE = 1.0 / math.sqrt(HEAD)
EXP2 = SCALE * math.log2(math.e)
NN = (((1,), (0,)), ((), ()))
NT = (((1,), (1,)), ((), ()))
TN = (((0,), (0,)), ((), ()))


def mm(a, b, dims=NN):
    return lax.dot_general(a, b, dims, preferred_element_type=f32)


def column_sum(v):
    return jnp.sum(v, axis=0, keepdims=True)


def vmem_spec():
    return pl.BlockSpec(memory_space=pltpu.VMEM)


def smem_spec():
    return pl.BlockSpec(memory_space=pltpu.SMEM)


def any_spec():
    return pl.BlockSpec(memory_space=pl.ANY)


def params(mib=60):
    return pltpu.CompilerParams(vmem_limit_bytes=mib << 20)


def pack(block, odd):
    half = block.shape[0] // 2
    left, right = block[:, :64], block[:, 128:]
    even_tail = jnp.concatenate([right[:half], right[half:]], axis=1)
    odd_tail = jnp.concatenate([left[half:], left[:half]], axis=1)
    return jnp.where(odd, block[:, 64:], block[:, :128]), jnp.where(odd, odd_tail, even_tail)


def unpack(top, tail, odd):
    first, second = tail[:, :64], tail[:, 64:]
    even = jnp.concatenate([top, jnp.concatenate([first, second], axis=0)], axis=1)
    return jnp.where(odd, jnp.concatenate([jnp.concatenate([second, first], axis=0), top], axis=1), even)


def turn(v):
    return jnp.concatenate([v[:, 64:], v[:, :64]], axis=1)


def group_of(n):
    return 4 if n % 4 == 0 else 3 if n % 3 == 0 else 1


def pack_kernel(odd_ref, m_ref, p_ref, s_ref):
    g = m_ref.shape[0]
    for b in range(g):
        m = m_ref[b]
        top, tail = pack(m, odd_ref[pl.program_id(0) * g + b] == 1)
        p_ref[b, :192] = top.astype(bf)
        p_ref[b, 192:] = tail.astype(bf)
        s_ref[b] = jnp.full((8, 128), jnp.sum(m * m), f32)


def pack_master(odd, master):
    n = master.shape[0]
    g = group_of(n)
    at = lambda i, s: (i, 0, 0)
    spec = pltpu.PrefetchScalarGridSpec(
        num_scalar_prefetch=1,
        grid=(n // g,),
        in_specs=[pl.BlockSpec((g, 192, 192), at)],
        out_specs=[pl.BlockSpec((g, 288, 128), at), pl.BlockSpec((g, 8, 128), at)],
    )
    return pl.pallas_call(
        pack_kernel,
        grid_spec=spec,
        out_shape=[jax.ShapeDtypeStruct((n, 288, 128), bf), jax.ShapeDtypeStruct((n, 8, 128), f32)],
        compiler_params=params(),
        name="pack_master",
    )(odd, master)


def qkv_kernel(src_ref, cnt_ref, at_ref, x0, x1, x2, x3, blk_ref, gain_ref, shift_ref, bq_ref, bv_ref, a_ref, q_ref, qt_ref, k_ref, kt_ref, v_ref, vt_ref, w_ref, st_ref, buf, sems):
    i = pl.program_id(0)

    @pl.when(i == 0)
    def _():
        copies = [pltpu.make_async_copy(blk_ref.at[at_ref[j]], buf.at[j], sems.at[j]) for j in range(12)]
        for copy in copies:
            copy.start()
        odd = at_ref[12] == 1
        for r in range(4):
            parts = []
            for c in range(3):
                copies[r * 3 + c].wait()
                p = buf[r * 3 + c].astype(f32)
                parts.append(unpack(p[:192], p[192:], odd))
            w_ref[r * 192 : (r + 1) * 192, :] = jnp.concatenate(parts, axis=1).astype(bf)

    x = jnp.concatenate([r[...] for r in (x0, x1, x2, x3)], axis=0).astype(f32)
    mean = jnp.mean(x, axis=-1, keepdims=True)
    cen = x - mean
    inv_std = lax.rsqrt(jnp.mean(cen * cen, axis=-1, keepdims=True) + EPS_NORM)
    a = (cen * inv_std * gain_ref[...] + shift_ref[...]).astype(bf)
    a_ref[...] = a
    qkv = mm(a, w_ref[...])
    q = (qkv[:, :192] + bq_ref[...]).astype(bf).astype(f32)
    k = qkv[:, 192:384].astype(bf).astype(f32)
    v = (qkv[:, 384:] + bv_ref[...]).astype(bf).astype(f32)
    row = lax.broadcasted_iota(jnp.int32, (128, 64), 0)
    lane = lax.broadcasted_iota(jnp.int32, (512, 64), 1)
    masked = jnp.concatenate(
        [jnp.where(row < cnt_ref[4 * i + b], 0.0, NEG_RAW) for b in range(4)], axis=0
    )
    ones = jnp.where(lane < 4, 1.0, 0.0)
    k_tail = jnp.where(lane == 0, masked, ones)
    v_tail = jnp.where(lane < 3, 1.0, 0.0)
    zero = jnp.zeros((512, 64), f32)
    sub = lax.broadcasted_iota(jnp.int32, (64, 512), 0)
    t_tail = jnp.where(sub < 1, 1.0, 0.0)
    qt, kt, vt = q.T, k.T, v.T
    longest = lambda a: jnp.max(jnp.concatenate([column_sum(a[h * 64 : (h + 1) * 64] ** 2) for h in range(3)], axis=0))
    st_ref[0] = jnp.where(lax.broadcasted_iota(jnp.int32, (8, 128), 0) == 0, longest(qt), longest(kt))
    for h in range(3):
        s = slice(h * 64, (h + 1) * 64)
        q_ref[h] = jnp.concatenate([q[:, s], zero], axis=1).astype(bf)
        k_ref[h] = jnp.concatenate([k[:, s], k_tail], axis=1).astype(bf)
        v_ref[h] = jnp.concatenate([v[:, s], v_tail], axis=1).astype(bf)
        qt_ref[h] = jnp.concatenate([qt[s], t_tail], axis=0).astype(bf)
        kt_ref[h] = kt[s].astype(bf)
        vt_ref[h] = jnp.concatenate([vt[s], t_tail[:16]], axis=0).astype(bf)


def qkv_forward(src, cnt, own_at, tokens, blocks, gain, shift, bq, bv):
    n = tokens.shape[0]
    rows = [pl.BlockSpec((128, 768), lambda i, s, c, o, k=k: (s[4 * i + k], 0)) for k in range(4)]
    row = lambda i, s, c, o: (0, 0)
    spec = pltpu.PrefetchScalarGridSpec(
        num_scalar_prefetch=3,
        grid=(n // 512,),
        in_specs=rows
        + [any_spec(), pl.BlockSpec((1, 768), row), pl.BlockSpec((1, 768), row), pl.BlockSpec((1, 192), row), pl.BlockSpec((1, 192), row)],
        out_specs=[
            pl.BlockSpec((512, 768), lambda i, s, c, o: (i, 0)),
            pl.BlockSpec((3, 512, 128), lambda i, s, c, o: (0, i, 0)),
            pl.BlockSpec((3, 128, 512), lambda i, s, c, o: (0, 0, i)),
            pl.BlockSpec((3, 512, 128), lambda i, s, c, o: (0, i, 0)),
            pl.BlockSpec((3, 64, 512), lambda i, s, c, o: (0, 0, i)),
            pl.BlockSpec((3, 512, 128), lambda i, s, c, o: (0, i, 0)),
            pl.BlockSpec((3, 80, 512), lambda i, s, c, o: (0, 0, i)),
            pl.BlockSpec((768, 576), row),
            pl.BlockSpec((1, 8, 128), lambda i, s, c, o: (i, 0, 0)),
        ],
        scratch_shapes=[pltpu.VMEM((12, 288, 128), bf), pltpu.SemaphoreType.DMA((12,))],
    )
    shapes = [(n, 768), (3, n, 128), (3, 128, n), (3, n, 128), (3, 64, n), (3, n, 128), (3, 80, n), (768, 576)]
    return pl.pallas_call(
        qkv_kernel,
        grid_spec=spec,
        out_shape=[jax.ShapeDtypeStruct(s, bf) for s in shapes] + [jax.ShapeDtypeStruct((n // 512, 8, 128), f32)],
        compiler_params=params(),
        name="norm_and_qkv",
    )(src, cnt, own_at, tokens, tokens, tokens, tokens, blocks, gain, shift, bq, bv)


def split3(v):
    a = v.astype(bf).astype(f32)
    b = (v - a).astype(bf).astype(f32)
    return a, b, v - a - b


def in_steps(units, sizes, body, carry):
    at = 0
    for size in sizes:
        count = (units - at) // size
        carry = lax.fori_loop(0, count, lambda i, c, at=at, size=size: body(at + i * size, size, c), carry)
        at = at + count * size
    return carry


def attend_kernel(bq, n_ref, k_ref, qt_ref, vt_ref, ot_ref, qb_ref, p_ref, rt_ref):
    live = n_ref[0]
    qi = pl.program_id(1)
    units = (live + 3) // 4

    def finish(top, acc):
        total = acc[64:65]
        ot_ref[0] = acc[:64] / total
        rt_ref[0] = 1.0 / total
        a, b, c = split3((top + jnp.log2(total)) * (-1.0 / EXP2))
        row = lax.broadcasted_iota(jnp.int32, (64, bq), 0)
        tail = jnp.where(row == 0, 1.0, jnp.where(row == 1, a, jnp.where(row == 2, b, jnp.where(row == 3, c, 0.0))))
        qb_ref[0, :64] = qt_ref[0, :64]
        qb_ref[0, 64:] = tail.astype(bf)

    def keys(u, size):
        return pl.ds(pl.multiple_of(u * 512, 512), size * 512)

    @pl.when(jnp.logical_and(qi * bq < live * 128, n_ref[1] == 1))
    def _():
        qt = qt_ref[0]

        def body(u, size, acc):
            for part in range(size):
                at = keys(u + part, 1)
                p = jnp.exp2(mm(k_ref[0, at, :], qt) * EXP2).astype(bf)
                p_ref[0, at, :] = p
                acc = acc + mm(vt_ref[0, :, at], p)
            return acc

        finish(0.0, in_steps(units, (4, 2, 1), body, jnp.zeros((80, bq), f32)))

    @pl.when(jnp.logical_and(qi * bq < live * 128, n_ref[1] == 0))
    def _():
        qt = qt_ref[0]

        def body(u, size, carry):
            top, acc = carry
            s = mm(k_ref[0, keys(u, size), :], qt) * EXP2
            new = jnp.maximum(top, jnp.max(s, axis=0, keepdims=True))
            p = jnp.exp2(s - new).astype(bf)
            return new, acc * jnp.exp2(top - new) + mm(vt_ref[0, :, keys(u, size)], p)

        finish(*in_steps(units, (2, 1), body, (jnp.full((1, bq), -3e38, f32), jnp.zeros((80, bq), f32))))


def attend(live, k, qt, vt, bq=1024):
    n = k.shape[1]
    spec = pltpu.PrefetchScalarGridSpec(
        num_scalar_prefetch=1,
        grid=(3, n // bq),
        in_specs=[
            pl.BlockSpec((1, n, 128), lambda h, i, s: (h, 0, 0)),
            pl.BlockSpec((1, 128, bq), lambda h, i, s: (h, 0, i)),
            pl.BlockSpec((1, 80, n), lambda h, i, s: (h, 0, 0)),
        ],
        out_specs=[
            pl.BlockSpec((1, 64, bq), lambda h, i, s: (h, 0, i)),
            pl.BlockSpec((1, 128, bq), lambda h, i, s: (h, 0, i)),
            pl.BlockSpec((1, n, bq), lambda h, i, s: (h, 0, i)),
            pl.BlockSpec((1, 1, bq), lambda h, i, s: (h, 0, i)),
        ],
    )
    return pl.pallas_call(
        functools.partial(attend_kernel, bq),
        grid_spec=spec,
        out_shape=[
            jax.ShapeDtypeStruct((3, 64, n), f32),
            jax.ShapeDtypeStruct((3, 128, n), bf),
            jax.ShapeDtypeStruct((3, n, n), bf),
            jax.ShapeDtypeStruct((3, 1, n), f32),
        ],
        compiler_params=params(),
        name="attention_forward",
    )(live, k, qt, vt)


def spread_kernel(src_ref, n_ref, t_ref, ot_ref, *o_refs):
    live, t, tiles = n_ref[0], t_ref[0], len(o_refs)
    per = o_refs[0].shape[1] // 128

    def step(b, _):
        g = src_ref[b]
        lanes = pl.ds(pl.multiple_of(b * 128, 128), 128)
        to = pl.ds(pl.multiple_of((g % per) * 128, 128), 128)
        for k in range(tiles):
            here = (g // per - t + tiles) % tiles == k

            @pl.when(jnp.logical_and(here, b < live))
            def _():
                for h in range(3):
                    o_refs[k][h * 64 : (h + 1) * 64, to] = ot_ref[h, :, lanes].astype(bf)

            @pl.when(jnp.logical_and(here, b >= live))
            def _():
                o_refs[k][:, to] = jnp.zeros((192, 128), bf)

        return 0

    lax.fori_loop(0, ot_ref.shape[2] // 128, step, 0)


def spread(src, live, tile, ot, tiles):
    n = ot.shape[2]
    return pl.pallas_call(
        spread_kernel,
        in_specs=[smem_spec()] * 3 + [vmem_spec()],
        out_specs=[vmem_spec()] * tiles,
        out_shape=[jax.ShapeDtypeStruct((192, n // tiles), bf)] * tiles,
        compiler_params=params(),
        name="spread_attended",
    )(src, live, tile, ot)


def collect_kernel(src_ref, n_ref, t_ref, ot_ref, rt_ref, *refs):
    g_refs, (dt_ref, d_ref) = refs[:-2], refs[-2:]
    live, t, tiles = n_ref[0], t_ref[0], len(g_refs)
    mild = n_ref[1] == 1
    per = g_refs[0].shape[1] // 128
    row = lax.broadcasted_iota(jnp.int32, (64, 128), 0)

    def step(b, _):
        g = src_ref[b]
        to = pl.ds(pl.multiple_of(b * 128, 128), 128)
        lanes = pl.ds(pl.multiple_of((g % per) * 128, 128), 128)
        for k in range(tiles):

            @pl.when(jnp.logical_and((t - g // per + tiles) % tiles == k, b < live))
            def _():
                for h in range(3):
                    scale = jnp.where(mild, rt_ref[h, :, to], 1.0)
                    d = (g_refs[k][h * 64 : (h + 1) * 64, lanes].astype(f32) * scale).astype(bf).astype(f32)
                    x, y, z = split3(-jnp.sum(d * ot_ref[h, :, to], axis=0, keepdims=True))
                    tail = jnp.where(row == 0, x, jnp.where(row == 1, y, jnp.where(row == 2, z, 0.0)))
                    dt_ref[h, :, to] = jnp.concatenate([d, tail], axis=0).astype(bf)
                    d_ref[h, to, :] = jnp.concatenate([d, jnp.zeros_like(d)], axis=0).T.astype(bf)

        @pl.when(b >= live)
        def _():
            dt_ref[:, :, to] = jnp.zeros((3, 128, 128), bf)
            d_ref[:, to, :] = jnp.zeros((3, 128, 128), bf)

        return 0

    lax.fori_loop(0, ot_ref.shape[2] // 128, step, 0)


def collect(src, live, tile, grads, ot, rt):
    n = ot.shape[2]
    return pl.pallas_call(
        collect_kernel,
        in_specs=[smem_spec()] * 3 + [vmem_spec()] * (2 + len(grads)),
        out_specs=[vmem_spec()] * 2,
        out_shape=[jax.ShapeDtypeStruct((3, 128, n), bf), jax.ShapeDtypeStruct((3, n, 128), bf)],
        compiler_params=params(),
        name="collect_attended_grad",
    )(src, live, tile, ot, rt, *grads)


def attend_back_kernel(bk, n_ref, p_ref, k_ref, kt_ref, v_ref, qb_ref, q_ref, dt_ref, d_ref, dq_ref, dk_ref, dv_ref):
    live = n_ref[0]
    j = pl.program_id(0)

    @pl.when(j == 0)
    def _():
        dq_ref[...] = jnp.zeros_like(dq_ref)

    @pl.when(j * bk < live * 128)
    def _():
        k, v, kt = k_ref[0], v_ref[0], kt_ref[0]

        def lanes(u, part):
            return pl.ds(pl.multiple_of((u * 2 + part) * 256, 256), 256)

        def kept(u, size, carry):
            dk, dv = carry
            dp = mm(v, dt_ref[0, :, lanes(u, 0)])
            for part in range(2 * size):
                at = lanes(u, part)
                ahead = mm(v, dt_ref[0, :, lanes(u, part + 1)]) if part + 1 < 2 * size else None
                p = p_ref[0, :, at]
                ds = (p.astype(f32) * dp).astype(bf)
                dv = dv + mm(p, d_ref[0, at, :])
                dk = dk + mm(ds, q_ref[0, at, :])
                dq_ref[0, :, at] += mm(kt, ds)
                dp = dp if ahead is None else ahead
            return dk, dv

        def again(u, size, carry):
            dk, dv = carry
            for part in range(2 * size):
                at = lanes(u, part)
                p = jnp.exp2(mm(k, qb_ref[0, :, at]) * EXP2)
                ds = (p * mm(v, dt_ref[0, :, at])).astype(bf)
                dv = dv + mm(p.astype(bf), d_ref[0, at, :])
                dk = dk + mm(ds, q_ref[0, at, :])
                dq_ref[0, :, at] += mm(kt, ds)
            return dk, dv

        units = (live + 3) // 4
        zero = jnp.zeros((bk, 128), f32)
        dk, dv = lax.cond(
            n_ref[1] == 1,
            lambda: in_steps(units, (4, 2, 1), kept, (zero, zero)),
            lambda: in_steps(units, (2, 1), again, (zero, zero)),
        )
        dk_ref[0] = (dk * SCALE).astype(bf)
        dv_ref[0] = dv.astype(bf)


def attend_back(head, live, p, k, kt, v, qb, q, dt, d, bk=512):
    n = k.shape[1]
    whole_t = lambda j, s: (head, 0, 0)
    rows = lambda j, s: (head, j, 0)
    spec = pltpu.PrefetchScalarGridSpec(
        num_scalar_prefetch=1,
        grid=(n // bk,),
        in_specs=[
            pl.BlockSpec((1, bk, n), rows),
            pl.BlockSpec((1, bk, 128), rows),
            pl.BlockSpec((1, 64, bk), lambda j, s: (head, 0, j)),
            pl.BlockSpec((1, bk, 128), rows),
            pl.BlockSpec((1, 128, n), whole_t),
            pl.BlockSpec((1, n, 128), whole_t),
            pl.BlockSpec((1, 128, n), whole_t),
            pl.BlockSpec((1, n, 128), whole_t),
        ],
        out_specs=[
            pl.BlockSpec((1, 64, n), lambda j, s: (0, 0, 0)),
            pl.BlockSpec((1, bk, 128), lambda j, s: (0, j, 0)),
            pl.BlockSpec((1, bk, 128), lambda j, s: (0, j, 0)),
        ],
    )
    return pl.pallas_call(
        functools.partial(attend_back_kernel, bk),
        grid_spec=spec,
        out_shape=[jax.ShapeDtypeStruct((1, 64, n), f32), jax.ShapeDtypeStruct((1, n, 128), bf), jax.ShapeDtypeStruct((1, n, 128), bf)],
        cost_estimate=pl.CostEstimate(flops=4 * 10**10, bytes_accessed=50 * 10**6, transcendentals=0),
        compiler_params=params(),
        name="attention_backward",
    )(live, p, k, kt, v, qb, q, dt, d)


def qkv_back_kernel(src_ref, n_ref, odd_ref, x0, x1, x2, x3, gain_ref, a_ref, w_ref, *refs):
    grads, (g_ref, gw_ref, gb_ref, vs_ref, acc, sums, rows, sems) = refs[:9], refs[9:]
    dqs, dks, dvs = grads[0::3], grads[1::3], grads[2::3]
    i = pl.program_id(0)
    live = n_ref[0]

    @pl.when(i == 0)
    def _():
        acc[...] = jnp.zeros_like(acc)
        sums[...] = jnp.zeros_like(sums)
        vs_ref[...] = jnp.zeros_like(vs_ref)

    @pl.when(4 * i < live)
    def _():
        dq = jnp.concatenate([r[0] for r in dqs], axis=0).T * SCALE
        g = jnp.concatenate([dq] + [r[0][:, :64].astype(f32) for r in dks] + [r[0][:, :64].astype(f32) for r in dvs], axis=1).astype(bf)
        acc[...] += mm(a_ref[...], g, TN)
        sums[...] += jnp.broadcast_to(column_sum(g.astype(f32)), sums.shape)
        g1 = mm(g, w_ref[...], NT)
        rows[...] = g1.astype(bf)
        x = jnp.concatenate([r[...] for r in (x0, x1, x2, x3)], axis=0).astype(f32)
        cen = x - jnp.mean(x, axis=-1, keepdims=True)
        normed = cen * lax.rsqrt(jnp.mean(cen * cen, axis=-1, keepdims=True) + EPS_NORM)
        vs_ref[0:1, :] += column_sum(g1 * normed)
        vs_ref[1:2, :] += column_sum(g1)

    @pl.when(4 * i >= live)
    def _():
        rows[...] = jnp.zeros_like(rows)

    copies = [
        pltpu.make_async_copy(rows.at[pl.ds(b * 128, 128)], g_ref.at[pl.ds(pl.multiple_of(src_ref[4 * i + b] * 128, 128), 128)], sems.at[b])
        for b in range(4)
    ]
    for copy in copies:
        copy.start()
    for copy in copies:
        copy.wait()

    @pl.when(i == pl.num_programs(0) - 1)
    def _():
        for r in range(4):
            for c in range(3):
                top, tail = pack(acc[r * 192 : (r + 1) * 192, c * 192 : (c + 1) * 192], odd_ref[0] == 1)
                gw_ref[r * 3 + c, :192] = top.astype(bf)
                gw_ref[r * 3 + c, 192:] = tail.astype(bf)
        gb_ref[...] = sums[...]


def qkv_backward(src, live, odd, tokens, gain, a, w, grads):
    n = a.shape[0]
    fixed = lambda i, s, c, o: (0, 0)
    row = lambda i, s, c, o: (0, i, 0)
    spec = pltpu.PrefetchScalarGridSpec(
        num_scalar_prefetch=3,
        grid=(n // 512,),
        in_specs=[pl.BlockSpec((128, 768), lambda i, s, c, o, k=k: (s[4 * i + k], 0)) for k in range(4)]
        + [pl.BlockSpec((1, 768), fixed), pl.BlockSpec((512, 768), lambda i, s, c, o: (i, 0)), pl.BlockSpec((768, 576), fixed)]
        + [pl.BlockSpec((1, 64, 512), lambda i, s, c, o: (0, 0, i)), pl.BlockSpec((1, 512, 128), row), pl.BlockSpec((1, 512, 128), row)] * 3,
        out_specs=[any_spec(), pl.BlockSpec((12, 288, 128), lambda i, s, c, o: (0, 0, 0)), pl.BlockSpec((8, 576), fixed), pl.BlockSpec((8, 768), fixed)],
        scratch_shapes=[pltpu.VMEM((768, 576), f32), pltpu.VMEM((8, 576), f32), pltpu.VMEM((512, 768), bf), pltpu.SemaphoreType.DMA((4,))],
    )
    S = jax.ShapeDtypeStruct
    return pl.pallas_call(
        qkv_back_kernel,
        grid_spec=spec,
        out_shape=[S((n, 768), bf), S((12, 288, 128), bf), S((8, 576), f32), S((8, 768), f32)],
        cost_estimate=pl.CostEstimate(flops=3 * 10**10, bytes_accessed=40 * 10**6, transcendentals=0),
        compiler_params=params(),
        name="qkv_backward",
    )(src, live, odd, tokens, tokens, tokens, tokens, gain, a, w, *grads)


def gelu_parts(z):
    cdf = 0.5 + 0.5 * lax.erf(z * math.sqrt(0.5))
    return z * cdf, cdf + z * (jnp.exp2(z * z * (-0.5 * math.log2(math.e))) * (1.0 / math.sqrt(2.0 * math.pi)))


def middle_kernel(inv_ref, cnt_ref, t_ref, blk_ref, o0, o1, o2, o3, x_ref, c_ref, vp_ref, bu_ref, y_ref, gr_ref, g0, g1, g2_ref, g3,
                  u_s, gz_s, a2_s, gm_s, gb_s, o_s, vs_ref, us_ref, w_out, w_up, w_down, tails, tsem, isem):
    i = pl.program_id(0)
    rows = x_ref.shape[0]
    r0 = i * rows
    kinds = ((w_out, 48, 2, 4), (w_up, 64, 8, 4), (w_down, 128, 2, 16))

    @pl.when(i == 0)
    def _():
        vs_ref[...] = jnp.zeros_like(vs_ref)
        us_ref[...] = jnp.zeros_like(us_ref)

        def pair(w, first, pairs):
            def copies(j):
                r = pl.multiple_of((j // pairs) * 192, 64)
                col = pl.multiple_of((j % pairs) * 384, 128)
                out = []
                for b, off in ((0, 0), (1, 256)):
                    at = first + 2 * j + b
                    slot = inv_ref[at]
                    out.append(pltpu.make_async_copy(blk_ref.at[slot, pl.ds(0, 192)], w.at[pl.ds(r, 192), pl.ds(col + off, 128)], tsem.at[at - 48]))
                    out.append(pltpu.make_async_copy(blk_ref.at[slot, pl.ds(192, 96)], tails.at[at - 48], isem.at[at - 48]))
                return out, r, col

            def start(j, _):
                for copy in copies(j)[0]:
                    copy.start()
                return 0

            def join(j, _):
                got, r, col = copies(j)
                for copy in got:
                    copy.wait()
                even = tails[first + 2 * j - 48].astype(f32)
                odd = tails[first + 2 * j - 47].astype(f32)
                lane = lax.broadcasted_iota(jnp.int32, even.shape, 1) < 64
                w[pl.ds(r, 96), pl.ds(col + 128, 128)] = jnp.where(lane, even, odd).astype(bf)
                w[pl.ds(r + 96, 96), pl.ds(col + 128, 128)] = turn(jnp.where(lane, odd, even)).astype(bf)
                return 0

            return start, join

        todo = [(pair(w, first, pairs), pairs * high) for w, first, pairs, high in kinds]
        for (start, _), n in todo:
            lax.fori_loop(0, n, start, 0)

        for (_, join), n in todo:
            lax.fori_loop(0, n, join, 0)

    vp = vp_ref[...]
    row = r0 + lax.broadcasted_iota(jnp.int32, (rows, 1), 0)
    live = jnp.where(row < cnt_ref[0], 1.0, 0.0)
    t = t_ref[0]
    for k, ref in enumerate((o0, o1, o2, o3)):
        o_s[pl.ds(pl.multiple_of(((t - k + 4) % 4) * 192, 64), 192), :] = ref[...]
    o_t = o_s[...]
    res = x_ref[...].astype(f32) + mm(o_t, w_out[...], TN) + vp[6:7]
    cen = res - jnp.mean(res, axis=-1, keepdims=True)
    inv_std = lax.rsqrt(jnp.mean(cen * cen, axis=-1, keepdims=True) + EPS_NORM)
    normed = cen * inv_std
    a2 = (normed * vp[2:3] + vp[3:4]).astype(bf)
    gy = c_ref[...].astype(f32) * live
    gm = gy.astype(bf)
    a2_s[...] = a2
    gm_s[...] = gm
    branch = jnp.zeros((rows, 768), f32)
    g2 = jnp.zeros((rows, 768), f32)
    for j in range(4):
        cols = slice(j * 768, (j + 1) * 768)
        u, slope = gelu_parts(mm(a2, w_up[:, cols]) + bu_ref[:, cols])
        u = u.astype(bf)
        u_s[:, cols] = u
        branch = branch + mm(u, w_down[cols, :])
        gz = (mm(gm, w_down[cols, :], NT) * slope).astype(bf)
        gz_s[:, cols] = gz
        us_ref[:, cols] += jnp.broadcast_to(column_sum(gz.astype(f32)), (8, 768))
        g2 = g2 + mm(gz, w_up[:, cols], NT)
    y_ref[...] = (live * (res + branch + vp[7:8])).astype(bf)
    d2 = g2 * vp[2:3]
    gr = gy + inv_std * (d2 - jnp.mean(d2, axis=-1, keepdims=True) - normed * jnp.mean(d2 * normed, axis=-1, keepdims=True))
    gr_ref[...] = gr
    gb = gr.astype(bf)
    gb_s[...] = gb
    vs_ref[0:1, :] += column_sum(g2 * normed)
    vs_ref[1:2, :] += column_sum(g2)
    vs_ref[2:3, :] += column_sum(gb.astype(f32))
    vs_ref[3:4, :] += column_sum(gm.astype(f32))
    for k, ref in enumerate((g0, g1, g2_ref, g3)):
        ref[...] = mm(w_out[pl.ds(pl.multiple_of(((t + k) % 4) * 192, 64), 192), :], gb, NT).astype(bf)


def weight_grad_kernel(outs, pos_ref, o_in, gb_in, a2_in, gz_in, u_in, gm_in, *refs):
    s_refs, (o_s, gb_s, a2_s, gz_s, u_s, gm_s, ring, zero, lsem, osem, zsem) = refs[:outs], refs[outs:]
    each = s_refs[0].shape[0]

    def to_slot(block, at, sem):
        for o in range(outs):

            @pl.when(at // each == o)
            def _():
                pltpu.make_async_copy(block, s_refs[o].at[at % each], sem).start()

    def landed(block, sem):
        pltpu.make_async_copy(block, s_refs[0].at[0], sem).wait()

    loads = [pltpu.make_async_copy(a, b, lsem.at[j]) for j, (a, b) in enumerate(
        ((o_in, o_s), (gb_in, gb_s), (a2_in, a2_s), (gz_in, gz_s), (gm_in, gm_s), (u_in, u_s)))]
    for load in loads:
        load.start()
    zero[...] = jnp.zeros_like(zero)

    def clear(j, _):
        to_slot(zero, pos_ref[j], zsem.at[j])
        return 0

    lax.fori_loop(0, 48, clear, 0)
    def send(n, g, first, pairs, high, low):
        half = (n % 2) * 8

        def put(r, b):
            return first + (high + r) * 2 * pairs + 2 * low + b

        for r in range(4):
            part = g[r * 192 : (r + 1) * 192]
            mid = part[:, 128:256]
            upper, lower = mid[:96], turn(mid[96:])
            lane = lax.broadcasted_iota(jnp.int32, upper.shape, 1) < 64
            for b, top, tail in ((0, part[:, :128], jnp.where(lane, upper, lower)), (1, part[:, 256:], jnp.where(lane, lower, upper))):
                k = half + 2 * r + b

                @pl.when(n >= 2)
                def _():
                    landed(ring.at[k], osem.at[k])

                ring[k, :192] = top.astype(bf)
                ring[k, 192:] = tail.astype(bf)
                to_slot(ring.at[k], pos_ref[put(r, b)], osem.at[k])

    def lanes(j):
        return pl.ds(pl.multiple_of(j * 384, 128), 384)

    def grad_out(n, _):
        send(n, mm(o_s[...], gb_s[:, lanes(n)]), 48, 2, 0, n)
        return 0

    def grad_up(n, _):
        send(n, mm(a2_s[...], gz_s[:, lanes(n)], TN), 64, 8, 0, n)
        return 0

    def grad_down(n, _):
        high = n // 2
        send(n, mm(u_s[:, pl.ds(pl.multiple_of(high * 768, 128), 768)], gm_s[:, lanes(n % 2)], TN), 128, 2, high * 4, n % 2)
        return 0

    def drain():
        for k in range(16):
            landed(ring.at[k], osem.at[k])

    for f, n, first in ((grad_out, 2, 0), (grad_up, 8, 2), (grad_down, 8, 4)):
        loads[first].wait()
        loads[first + 1].wait()
        lax.fori_loop(0, n, f, 0)
        drain()

    def cleared(j, _):
        landed(zero, zsem.at[j])
        return 0

    lax.fori_loop(0, 48, cleared, 0)


def middle(inv, count, tile, blocks, o_parts, tokens, cotangent, vec_params, bias_up, rows=256):
    n, width = tokens.shape
    hidden = bias_up.shape[1]
    row = lambda i, s, c, t: (i, 0)
    fixed = lambda i, s, c, t: (0, 0)
    col = lambda i, s, c, t: (0, i)
    V, DS = pltpu.VMEM, pltpu.SemaphoreType.DMA
    narrow, wide, part = pl.BlockSpec((rows, width), row), pl.BlockSpec((rows, hidden), row), pl.BlockSpec((192, rows), col)
    spec = pltpu.PrefetchScalarGridSpec(
        num_scalar_prefetch=3,
        grid=(n // rows,),
        in_specs=[any_spec()] + [part] * 4 + [narrow, narrow, pl.BlockSpec((12, width), fixed), pl.BlockSpec((1, hidden), fixed)],
        out_specs=[narrow, narrow] + [part] * 4 + [wide, wide, narrow, narrow, narrow, pl.BlockSpec((width, rows), col),
                   pl.BlockSpec((8, width), fixed), pl.BlockSpec((8, hidden), fixed)],
        scratch_shapes=[V((768, 768), bf), V((768, 3072), bf), V((3072, 768), bf), V((144, 96, 128), bf), DS((144,)), DS((144,))],
    )
    S = jax.ShapeDtypeStruct
    return pl.pallas_call(
        middle_kernel,
        grid_spec=spec,
        out_shape=[S((n, width), bf), S((n, width), f32)] + [S((192, n), bf)] * 4 + [S((n, hidden), bf)] * 2 + [S((n, width), bf)] * 3
        + [S((width, n), bf), S((8, width), f32), S((8, hidden), f32)],
        compiler_params=params(),
        name="projection_and_mlp",
    )(inv, count, tile, blocks, *o_parts, tokens, cotangent, vec_params, bias_up)


def weight_grads_to_slots(pos, outs, block_count, o_t, gb, a2, gz, u, gm):
    V, DS = pltpu.VMEM, pltpu.SemaphoreType.DMA
    arrays = (o_t, gb, a2, gz, u, gm)
    return pl.pallas_call(
        functools.partial(weight_grad_kernel, outs),
        in_specs=[smem_spec()] + [any_spec()] * 6,
        out_specs=[any_spec()] * outs,
        out_shape=[jax.ShapeDtypeStruct((block_count // outs, 288, 128), bf)] * outs,
        scratch_shapes=[V(a.shape, bf) for a in arrays] + [V((16, 288, 128), bf), V((288, 128), bf), DS((6,)), DS((16,)), DS((48,))],
        cost_estimate=pl.CostEstimate(flops=6 * 10**10, bytes_accessed=32 * 10**6, transcendentals=0),
        compiler_params=params(),
        name="mlp_weight_gradients",
    )(pos, *arrays)


def fold_kernel(bits_ref, *refs):
    n = len(refs) // 6 * 4
    ins, outs = refs[:n], refs[n:]
    for j, out in enumerate(outs):
        out[...] = (ins[2 * j][...].astype(f32) + ins[2 * j + 1][...].astype(f32)).astype(bf)


def fold(bits, kept, came):
    half = {96: 16}.get(kept[0][0].shape[0], kept[0][0].shape[0] // 2)
    g = min(half, 4)
    specs, args = [], []
    for p in range(len(kept)):
        for side in (1, 0):
            for array, first in (kept[p], came[p]):
                at = lambda i, b, p=p, side=side, first=first: (first // g + (b[p] * (1 - 2 * side) + side) * (half // g) + i, 0, 0)
                specs.append(pl.BlockSpec((g, 288, 128), at))
                args.append(array)
    count = 2 * len(kept)
    out = pl.pallas_call(
        fold_kernel,
        grid_spec=pltpu.PrefetchScalarGridSpec(
            num_scalar_prefetch=1,
            grid=(half // g,),
            in_specs=specs,
            out_specs=[pl.BlockSpec((g, 288, 128), lambda i, b: (i, 0, 0))] * count,
        ),
        out_shape=[jax.ShapeDtypeStruct((half, 288, 128), bf)] * count,
        compiler_params=params(),
        name="add_gradients",
    )(bits, *args)
    return out[0::2], out[1::2]


def split2(v):
    hi = v.astype(bf)
    return hi, (v - hi.astype(f32)).astype(bf)


def mm3(a, b, dims):
    return mm(a[0], b[0], dims) + (mm(a[0], b[1], dims) + mm(a[1], b[0], dims))


def adam_kernel(odd_ref, from_ref, g_ref, late_ref, m1_ref, m2_ref, l_ref, r_ref, g_out, m1_out, m2_out, u_out, s_out):
    for b in range(g_ref.shape[0]):
        slot = pl.program_id(0) * g_ref.shape[0] + b
        place = from_ref[slot]
        part = jnp.where(place >= 0, late_ref[jnp.maximum(place, 0)].astype(f32), g_ref[b].astype(f32))
        grad = unpack(part[:192], part[192:], odd_ref[slot] == 1)
        left, right = split2(l_ref[b]), split2(r_ref[b])
        low = grad.astype(bf)
        rot = mm3(split2(mm(left[0], low, TN) + mm(left[1], low, TN)), right, NN)
        first = BETA_ONE * m1_ref[b] + (1.0 - BETA_ONE) * rot
        second = BETA_TWO * m2_ref[b] + (1.0 - BETA_TWO) * rot * rot
        upd = (first / (1.0 - BETA_ONE**STEP)) / (jnp.sqrt(second / (1.0 - BETA_TWO**STEP)) + ADAM_EPS)
        upd = mm3(split2(mm3(left, split2(upd), NN)), right, NT)
        g_out[b] = grad
        m1_out[b] = first
        m2_out[b] = second
        u_out[b] = upd
        s_out[b] = jnp.full((8, 128), jnp.sum(upd * upd), f32)


def adam(odd, late_at, grads, late, first, second, left, right):
    n = grads.shape[0]
    g = group_of(n)
    at = lambda i, s, f: (i, 0, 0)
    big = pl.BlockSpec((g, 192, 192), at)
    spec = pltpu.PrefetchScalarGridSpec(
        num_scalar_prefetch=2,
        grid=(n // g,),
        in_specs=[pl.BlockSpec((g, 288, 128), at), pl.BlockSpec(late.shape, lambda i, s, f: (0, 0, 0))] + [big] * 4,
        out_specs=[big] * 4 + [pl.BlockSpec((g, 8, 128), at)],
    )
    return pl.pallas_call(
        adam_kernel,
        grid_spec=spec,
        out_shape=[jax.ShapeDtypeStruct((n, 192, 192), f32)] * 4 + [jax.ShapeDtypeStruct((n, 8, 128), f32)],
        compiler_params=params(),
        name="rotated_adam",
    )(odd, late_at, grads, late, first, second, left, right)


def halving_places(slot, core):
    dp, r = slot // 24, slot % 24
    y, z1, z2, x, s = dp % 2, dp // 2 % 2, dp // 4, r % 4 // 2, r % 2
    portion = r % 12 // 4
    bits = [(x, y, z1), (y, z1, x), (z1, x, y)]
    inside = sum(jnp.where(portion == p, (b[0] * 4 + b[1] * 2 + b[2]) * 4, 0) for p, b in enumerate(bits)) + z2 * 2 + s
    return jnp.where(r // 12 == core, 0, 96) + portion * 32 + inside


def norm_forward(row_data, gain_vec, shift_vec):
    row_mean = jnp.mean(row_data, axis=-1, keepdims=True)
    centred = row_data - row_mean
    inv_std = lax.rsqrt(jnp.mean(centred * centred, axis=-1, keepdims=True) + EPS_NORM)
    normed = centred * inv_std
    return (normed * gain_vec + shift_vec, normed, inv_std)


def norm_back(grad_out, normed, inv_std, gain_vec):
    grad_normed = grad_out * gain_vec
    return inv_std * (
        grad_normed
        - jnp.mean(grad_normed, axis=-1, keepdims=True)
        - normed * jnp.mean(grad_normed * normed, axis=-1, keepdims=True)
    )


def block_plan(counts, slot_count):
    tiles = counts.shape[0]
    per = slot_count // 128
    j = lax.broadcasted_iota(jnp.int32, (tiles, per), 1)
    kept = jnp.clip(counts[:, None] - j * 128, 0, 128).reshape(-1)
    full = (kept > 0).astype(jnp.int32)
    index = jnp.arange(tiles * per, dtype=jnp.int32)
    before = (index[None, :] < index[:, None]).astype(jnp.int32)
    ahead = jnp.sum(before * full[None, :], axis=1)
    live = jnp.sum(full)
    place = jnp.where(full > 0, ahead, live + index - ahead)
    hot = (place[None, :] == index[:, None]).astype(jnp.int32)
    return jnp.sum(hot * index[None, :], axis=1), jnp.sum(hot * kept[None, :], axis=1), live.reshape(1)


def make_body(tuned):
    def body(tokens, cotangent, counts, master, slot_block, groups, first_moment, second_moment, left_basis, right_basis, vec_params, vec_first, vec_second):
        slot_count, width = tokens.shape[1:]
        per_owner = master.shape[0]
        tile = lax.axis_index("tile")
        mine = lax.dynamic_slice(slot_block, (lax.axis_index("dp") * per_owner,), (per_owner,))
        odd = mine % 2
        packed, weight_sq = pack_master(odd, master)
        own_tokens = tokens.reshape(slot_count, width)
        count_tile = jnp.broadcast_to(counts.reshape(1, 1), (8, 128))
        if tuned:
            blocks, token_all, count_all = gather_all(packed, own_tokens, count_tile)
        else:
            blocks = lax.all_gather(packed, "dp", axis=0, tiled=True)
            token_all = lax.all_gather(own_tokens, "tile", axis=0)
            count_all = lax.all_gather(count_tile, "tile", axis=0)
        tiles = token_all.shape[0]
        block_count = blocks.shape[0]
        src, cnt, live = block_plan(count_all[:, 0, 0], slot_count)
        index = jnp.arange(block_count, dtype=jnp.int32)
        inverse = jnp.sum((slot_block[None, :] == index[:, None]).astype(jnp.int32) * index[None, :], axis=1)
        own_block = jnp.arange(12, dtype=jnp.int32) // 3 * 12 + jnp.arange(12, dtype=jnp.int32) % 3 * 4 + tile
        own_at = jnp.sum((slot_block[None, :] == own_block[:, None]).astype(jnp.int32) * index[None, :], axis=1)
        own_at = jnp.concatenate([own_at, tile.reshape(1) % 2])
        own = width // tiles
        bias = lambda row: lax.dynamic_slice(vec_params[row : row + 1], (0, tile * own), (1, own))
        a1, q, qt, k, kt, v, vt, w_qkv, lengths = qkv_forward(
            src, cnt, own_at, token_all.reshape(-1, width), blocks, vec_params[0:1], vec_params[1:2], bias(4), bias(5)
        )
        mild = jnp.sqrt(jnp.max(lengths[:, 0, 0])) * jnp.sqrt(jnp.max(lengths[:, 1, 0])) * EXP2 <= 60.0
        live = jnp.concatenate([live, mild.astype(jnp.int32).reshape(1)])
        ot, qb, p, rt = attend(live, k, qt, vt)

        def shift(parts):
            return [parts[0]] + [lax.ppermute(parts[j], "tile", [(s, (s + j) % tiles) for s in range(tiles)]) for j in range(1, tiles)]

        tile_one = tile.astype(jnp.int32).reshape(1)
        o_parts = shift(spread(src, live, tile_one, ot, tiles))
        output, grad_resid, *rest = middle(
            inverse, counts.reshape(1), tile_one, blocks, o_parts, own_tokens, cotangent.reshape(slot_count, width), vec_params, vec_params[8:].reshape(1, -1)
        )
        go_parts, (u, gz, a2, gm, gb, o_t, sums, up_sums) = rest[:tiles], rest[tiles:]
        go_parts = shift(go_parts)
        head_grads = []

        def back(head, dt):
            head_grads.extend(attend_back(head, live, p, k, kt, v, qb, q, dt, d))

        if tuned:
            dp = lax.axis_index("dp")
            x, y, z1, z2 = tile // 2, dp % 2, dp // 2 % 2, dp // 4
            flip = lambda array, axis, bit: lax.ppermute(array, axis, [(s, s ^ bit) for s in range(8 if axis == "dp" else 4)])
            turns = [[(x, "tile", 2), (y, "dp", 1), (z1, "dp", 2)][j:] + [(x, "tile", 2), (y, "dp", 1), (z1, "dp", 2)][:j] for j in range(3)]
            turns.append([(z2, "dp", 4)] * 3)
            keep, send = weight_grads_to_slots(halving_places(inverse, tile % 2), 2, block_count, o_t, gb, a2, gz, u, gm)
            send, go_parts = lax.optimization_barrier((send, go_parts))
            came = flip(send, "tile", 1)
            dt, d = collect(src, live, tile_one, go_parts, ot, rt)
            dt, came = lax.optimization_barrier((dt, came))
            kept, came = [(keep, 32 * j) for j in range(3)], [(came, 32 * j) for j in range(3)]
            for j, turn_of in enumerate(turns):
                bits = jnp.stack([bit for bit, _, _ in turn_of]).astype(jnp.int32)
                sends, kept = fold(bits, kept, came)
                if j < 3:
                    dt, sends = lax.optimization_barrier((dt, sends))
                    came = [flip(array, axis, bit) for array, (_, axis, bit) in zip(sends, turn_of)]
                    back(j, dt)
                    head_grads[-3], came = lax.optimization_barrier((head_grads[-3], came))
                    kept, came = [(a, 0) for a in kept], [(a, 0) for a in came]
                else:
                    head_grads[-3], sends = lax.optimization_barrier((head_grads[-3], sends))
                    came = [flip(array, axis, bit) for array, (_, axis, bit) in zip(sends, turn_of)]
        else:
            slots = weight_grads_to_slots(inverse, 1, block_count, o_t, gb, a2, gz, u, gm)[0]
            dt, d = collect(src, live, tile_one, go_parts, ot, rt)
            for head in range(3):
                back(head, dt)
        g_part, gw_qkv, qkv_sums, norm_sums = qkv_backward(
            src, live, tile_one % 2, token_all.reshape(-1, width), vec_params[0:1], a1, w_qkv, head_grads
        )
        g_part = g_part.reshape(tiles, slot_count, width)
        if tuned:
            g_part, came = lax.optimization_barrier((g_part, came))
        zero = jnp.zeros((width,), f32)
        at_own = lambda s: lax.dynamic_update_slice(zero, s, (tile * own,))
        vector_part = jnp.concatenate(
            [norm_sums[0:2], sums[0:2], at_own(qkv_sums[0, :own])[None], at_own(qkv_sums[0, 2 * own :])[None], sums[2:4], up_sums[0].reshape(-1, width)], axis=0
        )
        g1 = lax.psum_scatter(g_part, "tile", scatter_dimension=0, tiled=False)
        if tuned:
            early, late, vector_grads = last_sums(gw_qkv, kept, came, vector_part)
        else:
            early = lax.psum(lax.psum_scatter(slots.astype(f32), "dp", scatter_dimension=0, tiled=True), "tile").astype(bf)
            late = lax.all_gather(lax.psum(gw_qkv.astype(f32), "dp").astype(bf), "tile", axis=0, tiled=True)
            vector_grads = lax.psum(vector_part, ("dp", "tile"))
        row_input = own_tokens.astype(f32)
        _, normed_one, inv_std_one = norm_forward(row_input, vec_params[0], vec_params[1])
        input_grad = grad_resid + norm_back(g1.astype(f32), normed_one, inv_std_one, vec_params[0])
        late_at = jnp.where(mine < 48, mine % 4 * 12 + mine // 12 * 3 + mine % 12 // 4, -1)
        weight_grads, first_out, second_out, update, update_sq = adam(odd, late_at, early, late, first_moment, second_moment, left_basis, right_basis)
        group_hot = (groups[:, None] == jnp.arange(NGRP, dtype=jnp.int32)[None, :]).astype(f32)
        both = jnp.stack([weight_sq[:, 0, 0], update_sq[:, 0, 0]], axis=0)
        group_part = jnp.pad(jnp.sum(group_hot[None] * both[:, :, None], axis=1), ((0, 6), (0, 128 - NGRP)))
        group_both = group_sum(group_part, block_count // per_owner)
        own_both = jnp.sum(group_hot[None] * group_both[:2, None, :NGRP], axis=2)
        block_rate = RATE_BLOCK * jnp.sqrt(own_both[0]) / (jnp.sqrt(own_both[1]) + 1e-06)
        master_out = master - block_rate[:, None, None] * update
        vec_first_out = BETA_ONE * vec_first + (1.0 - BETA_ONE) * vector_grads
        vec_second_out = BETA_TWO * vec_second + (1.0 - BETA_TWO) * vector_grads * vector_grads
        vec_update = (vec_first_out / (1.0 - BETA_ONE**STEP)) / (jnp.sqrt(vec_second_out / (1.0 - BETA_TWO**STEP)) + ADAM_EPS)
        return (
            output.reshape(1, slot_count, width),
            input_grad.reshape(1, slot_count, width),
            weight_grads,
            first_out,
            second_out,
            master_out,
            master_out.astype(bf),
            vector_grads,
            vec_first_out,
            vec_second_out,
            vec_params - RATE_VECTOR * vec_update,
        )

    return body


def solution(mesh):
    tuned = (mesh.shape["dp"], mesh.shape["tile"]) == (8, 4)
    rows, blocks = P("dp", "tile", None), P("dp", None, None)
    return jax.shard_map(
        make_body(tuned),
        mesh=mesh,
        in_specs=(rows, rows, P("dp", "tile"), blocks, P(), P("dp"), blocks, blocks, blocks, blocks, P(), P(), P()),
        out_specs=(rows, rows, blocks, blocks, blocks, blocks, blocks, P(), P(), P(), P()),
        check_vma=False,
    )
```

```python
import functools
import math

import jax
import jax.numpy as jnp
from jax import lax
from jax.experimental import pallas as pl
from jax.experimental.pallas import tpu as pltpu
from jax.sharding import PartitionSpec as P

f32 = jnp.float32
bf = jnp.bfloat16
MESH = pl.DeviceIdType.MESH

def where_am_i():
    dp=lax.axis_index("dp"); t=lax.axis_index("tile")
    return dp//2, dp%2, t//2, t%2

def dev(z,y,x,c):
    return (z*2+y, x*2+c)

def rcopy(src,dst,ss,rs,to):
    return pltpu.make_async_remote_copy(src_ref=src,dst_ref=dst,send_sem=ss,recv_sem=rs,device_id=to,device_id_type=MESH)

def gather_kernel(own_w,own_tok,own_cnt,all_w,all_tok,all_cnt,
                  zs,zr,ys,yr,xs,xr,cs,cr,fs,fr,ts,tr,ns,nr,ls):
    z,y,x,c=where_am_i()
    per=own_w.shape[0]
    part=per//12
    def a_of(shard,xx,cc): return all_w.at[pl.ds(shard*per+(xx*2+cc)*part,part)]
    def b_of(shard,cc): return all_w.at[pl.ds(shard*per+4*part+cc*4*part,4*part)]
    own_a=own_w.at[pl.ds((x*2+c)*part,part)]
    own_b=own_w.at[pl.ds(4*part+c*4*part,4*part)]
    me=z*2+y
    core=dev(z,y,x,1-c); across=dev(z,y,1-x,c); beside=dev(z,1-y,x,c)
    up=dev(jnp.minimum(z+1,3),y,x,c); down=dev(jnp.maximum(z-1,0),y,x,c)
    def src(shard,own):
        return (own_a,own_b) if own else (a_of(shard,x,c),b_of(shard,c))
    def z_copies(zz,own,go_up):
        shard=zz*2+y
        a,b=src(shard,own)
        d=(z-zz) if go_up else (zz-z)
        k=0 if go_up else 1
        to=up if go_up else down
        return (rcopy(a,a_of(shard,x,c),zs.at[k,d,0],zr.at[k,d,0],to),rcopy(b,b_of(shard,c),zs.at[k,d,1],zr.at[k,d,1],to))
    def z_arrivals(zz,k,dist):
        shard=zz*2+y
        a,b=a_of(shard,x,c),b_of(shard,c)
        return (rcopy(a,a,zs.at[k,dist-1,0],zr.at[k,dist-1,0],up),rcopy(b,b,zs.at[k,dist-1,1],zr.at[k,dist-1,1],up))
    def y_copies(zz,own):
        shard=zz*2+y
        a,b=src(shard,own)
        return (rcopy(a,a_of(shard,x,c),ys.at[zz,0],yr.at[zz,0],beside),rcopy(b,b_of(shard,c),ys.at[zz,1],yr.at[zz,1],beside))
    def y_arrivals(zz):
        shard=zz*2+(1-y)
        a,b=a_of(shard,x,c),b_of(shard,c)
        return (rcopy(a,a,ys.at[zz,0],yr.at[zz,0],beside),rcopy(b,b,ys.at[zz,1],yr.at[zz,1],beside))
    def x_copy(shard,own):
        return rcopy(src(shard,own)[0],a_of(shard,x,c),xs.at[shard],xr.at[shard],across)
    def x_arrival(shard):
        a=a_of(shard,1-x,c)
        return rcopy(a,a,xs.at[shard],xr.at[shard],across)
    def c_copies(shard,own):
        a,b=src(shard,own)
        return (rcopy(a,a_of(shard,x,c),cs.at[shard,0],cr.at[shard,0],core),rcopy(b,b_of(shard,c),cs.at[shard,1],cr.at[shard,1],core))
    def c_arrivals(shard):
        a,b=a_of(shard,x,1-c),b_of(shard,1-c)
        return (rcopy(a,a,cs.at[shard,0],cr.at[shard,0],core),rcopy(b,b,cs.at[shard,1],cr.at[shard,1],core))
    def f_copy(shard):
        a=a_of(shard,1-x,c)
        return rcopy(a,a,fs.at[shard],fr.at[shard],core)
    def f_arrival(shard):
        a=a_of(shard,1-x,1-c)
        return rcopy(a,a,fs.at[shard],fr.at[shard],core)
    def start(cps):
        for cp in (cps if isinstance(cps,tuple) else (cps,)): cp.start()
    def got(cps):
        for cp in (cps if isinstance(cps,tuple) else (cps,)): cp.wait_recv()
    def sent(cps):
        for cp in (cps if isinstance(cps,tuple) else (cps,)): cp.wait_send()
    tile=x*2+c
    tok_x=rcopy(own_tok,all_tok.at[tile],ts.at[0],tr.at[0],across)
    tok_c=rcopy(own_tok,all_tok.at[tile],ts.at[1],tr.at[1],core)
    far=all_tok.at[(1-x)*2+c]
    tok_f=rcopy(far,far,ts.at[2],tr.at[2],core)
    near=all_tok.at[x*2+1-c]
    diag=all_tok.at[(1-x)*2+1-c]
    cnts=[rcopy(own_cnt,all_cnt.at[tile],ns.at[i],nr.at[i],to) for i,to in enumerate((across,core,dev(z,y,1-x,1-c)))]
    cnt_in=[rcopy(r,r,ns.at[i],nr.at[i],core) for i,r in enumerate((all_cnt.at[(1-x)*2+c],all_cnt.at[x*2+1-c],all_cnt.at[(1-x)*2+1-c]))]
    local=(pltpu.make_async_copy(own_w,all_w.at[pl.ds(me*per,per)],ls.at[0]),
           pltpu.make_async_copy(own_tok,all_tok.at[tile],ls.at[1]),pltpu.make_async_copy(own_cnt,all_cnt.at[tile],ls.at[2]))
    @pl.when(z<3)
    def _(): start(z_copies(z,True,True))
    @pl.when(z>0)
    def _(): start(z_copies(z,True,False))
    start(y_copies(z,True)); start(tok_x); start(tok_c)
    for cp in cnts: cp.start()
    for cp in local: cp.start()
    def from_line(k,dist):
        zz=z-dist if k==0 else z+dist
        there=(zz>=0) if k==0 else (zz<=3)
        @pl.when(there)
        def _():
            got(z_arrivals(zz,k,dist))
            @pl.when((z<3) if k==0 else (z>0))
            def _(): start(z_copies(zz,False,k==0))
            start(y_copies(zz,False)); start(x_copy(zz*2+y,False)); start(c_copies(zz*2+y,False))
    def from_beside(zz):
        got(y_arrivals(zz))
        s=zz*2+1-y
        start(x_copy(s,False)); start(c_copies(s,False))
    def guarded(f,dist):
        @pl.when(z-dist>=0)
        def _(): f(z-dist)
        @pl.when(z+dist<=3)
        def _(): f(z+dist)
    def from_across(shard):
        got(x_arrival(shard)); start(f_copy(shard))
    from_line(0,1); from_line(1,1)
    from_beside(z)
    from_line(0,2); from_line(1,2)
    guarded(from_beside,1); guarded(lambda zz: from_across(zz*2+y),1); from_across(z*2+1-y)
    from_line(0,3); from_line(1,3)
    got(tok_x); tok_f.start()
    guarded(from_beside,2); guarded(lambda zz: from_across(zz*2+y),2); guarded(lambda zz: from_across(zz*2+1-y),1)
    guarded(from_beside,3); guarded(lambda zz: from_across(zz*2+y),3); guarded(lambda zz: from_across(zz*2+1-y),2)
    guarded(lambda zz: from_across(zz*2+1-y),3)
    def drain(s,_):
        @pl.when(s!=me)
        def _():
            got(c_arrivals(s)); got(f_arrival(s)); sent(c_copies(s,False)); sent(f_copy(s)); sent(x_copy(s,False))
        return 0
    lax.fori_loop(0,8,drain,0)
    def drain_y(zz,_):
        sent(y_copies(zz,False)); return 0
    lax.fori_loop(0,4,drain_y,0)
    for dist in range(4):
        @pl.when(jnp.logical_and(z<3,z-dist>=0))
        def _(): sent(z_copies(z-dist,False,True))
        @pl.when(jnp.logical_and(z>0,z+dist<=3))
        def _(): sent(z_copies(z+dist,False,False))
    rcopy(near,near,ts.at[1],tr.at[1],core).wait_recv()
    rcopy(diag,diag,ts.at[2],tr.at[2],core).wait_recv()
    tok_x.wait_send(); tok_c.wait_send(); tok_f.wait_send()
    for cp in cnts: cp.wait_send()
    for cp in cnt_in: cp.wait_recv()
    for cp in local: cp.wait()

def gather_all(own_w,own_tok,own_cnt):
    DS=pltpu.SemaphoreType.DMA
    hbm=pl.BlockSpec(memory_space=pl.ANY)
    return pl.pallas_call(gather_kernel,
        out_shape=[jax.ShapeDtypeStruct((8*own_w.shape[0],)+own_w.shape[1:],bf),jax.ShapeDtypeStruct((4,)+own_tok.shape,bf),jax.ShapeDtypeStruct((4,)+own_cnt.shape,own_cnt.dtype)],
        in_specs=[pl.BlockSpec(memory_space=pltpu.VMEM)]*3,out_specs=[hbm]*3,
        scratch_shapes=[DS((2,4,2)),DS((2,4,2)),DS((4,2)),DS((4,2)),DS((8,)),DS((8,)),DS((8,2)),DS((8,2)),DS((8,)),DS((8,)),DS((3,)),DS((3,)),DS((3,)),DS((3,)),DS((3,))],
        compiler_params=pltpu.CompilerParams(has_side_effects=True,vmem_limit_bytes=60<<20),name="gather_weights_tokens")(own_w,own_tok,own_cnt)

def group_sum_kernel(g_ref,o_ref,gd,gs,gr):
    dp=lax.axis_index("dp"); t=lax.axis_index("tile")
    nd=gd.shape[0]
    def copy(k):
        return rcopy(gd.at[dp],gd.at[dp],gs.at[k],gr.at[k],((dp+k)%nd,t))
    def arrive(k):
        q=(dp-k+nd)%nd
        return rcopy(gd.at[q],gd.at[q],gs.at[k],gr.at[k],(q,t))
    def loop(f):
        def s(k,_):
            f(k); return 0
        lax.fori_loop(1,nd,s,0)
    gd[dp]=g_ref[...]
    loop(lambda k: copy(k).start())
    loop(lambda k: arrive(k).wait_recv())
    acc=gd[0]
    for i in range(1,nd): acc=acc+gd[i]
    o_ref[...]=acc
    loop(lambda k: copy(k).wait_send())

def group_sum(g,nd):
    DS=pltpu.SemaphoreType.DMA
    vm=pl.BlockSpec(memory_space=pltpu.VMEM)
    return pl.pallas_call(group_sum_kernel,out_shape=jax.ShapeDtypeStruct(g.shape,f32),in_specs=[vm],out_specs=vm,
        scratch_shapes=[pltpu.VMEM((nd,)+g.shape,f32),DS((nd,)),DS((nd,))],
        compiler_params=pltpu.CompilerParams(has_side_effects=True,vmem_limit_bytes=60<<20),name="sum_groups")(g)

def last_sums_kernel(l_ref,mine,over,v_ref,early,late,vo_ref,lr,vt,vd,ls,lrs,ps,pr,xs,xr,cs,cr,fs,fr,es,er,ts,tr,ds,dr):
    z,y,x,c=where_am_i()
    dp=lax.axis_index("dp"); t=lax.axis_index("tile")
    core=dev(z,y,x,1-c); across=dev(z,y,1-x,c)
    def loop(f,first=0,n=8):
        def s(k,_):
            f(k); return 0
        lax.fori_loop(first,n,s,0)
    def l_copy(k):
        p=(dp+k)%8
        return rcopy(l_ref.at[pl.ds(p*3,3)],lr.at[dp],ls.at[k],lrs.at[k],(p,t))
    def l_arrive(k):
        q=(dp-k+8)%8
        return rcopy(lr.at[q],lr.at[q],ls.at[k],lrs.at[k],(q,t))
    loop(lambda k: l_copy(k).start(),1)
    def t_copy(k): return rcopy(vt.at[t],vt.at[t],ts.at[k],tr.at[k],(dp,(t+k)%4))
    def t_arrive(k):
        q=(t-k+4)%4
        return rcopy(vt.at[q],vt.at[q],ts.at[k],tr.at[k],(dp,q))
    def d_copy(k): return rcopy(vd.at[dp],vd.at[dp],ds.at[k],dr.at[k],((dp+k)%8,t))
    def d_arrive(k):
        q=(dp-k+8)%8
        return rcopy(vd.at[q],vd.at[q],ds.at[k],dr.at[k],(q,t))
    vt[t]=v_ref[...]
    loop(lambda k: t_copy(k).start(),1,4)
    def place(xx,cc,p): return early.at[pl.ds(cc*12+p*6+xx*3,3)]
    for p in range(2):
        early[pl.ds(c*12+p*6+x*3,3)]=mine[pl.ds(p*3,3)]
        early[pl.ds(c*12+p*6+(1-x)*3,3)]=over[pl.ds(p*3,3)]
    def e_copy(i,p): return rcopy(place(i,c,p),place(i,c,p),es.at[i,p],er.at[i,p],core)
    def e_arrive(i,p): return rcopy(place(i,1-c,p),place(i,1-c,p),es.at[i,p],er.at[i,p],core)
    for p in range(2):
        e_copy(0,p).start(); e_copy(1,p).start()
    lr[dp]=l_ref[pl.ds(dp*3,3)]
    loop(lambda k: t_arrive(k).wait_recv(),1,4)
    vd[dp]=vt[0]+vt[1]+vt[2]+vt[3]
    loop(lambda k: d_copy(k).start(),1)
    loop(lambda k: l_arrive(k).wait_recv(),1)
    for i in range(3):
        acc=lr[0,i].astype(f32)
        for q in range(1,8): acc=acc+lr[q,i].astype(f32)
        late[t,dp*3+i]=acc.astype(bf)
    def piece(tt,q): return late.at[tt,pl.ds(q*3,3)]
    def p_copy(k): return rcopy(piece(t,dp),piece(t,dp),ps.at[k],pr.at[k],((dp+k)%8,t))
    def p_arrive(k):
        q=(dp-k+8)%8
        return rcopy(piece(t,q),piece(t,q),ps.at[k],pr.at[k],(q,t))
    def x_copy(q): return rcopy(piece(t,q),piece(t,q),xs.at[q],xr.at[q],across)
    def x_arrive(q): return rcopy(piece((1-x)*2+c,q),piece((1-x)*2+c,q),xs.at[q],xr.at[q],across)
    def c_copy(q): return rcopy(piece(t,q),piece(t,q),cs.at[q],cr.at[q],core)
    def c_arrive(q): return rcopy(piece(x*2+1-c,q),piece(x*2+1-c,q),cs.at[q],cr.at[q],core)
    def f_copy(q): return rcopy(piece((1-x)*2+c,q),piece((1-x)*2+c,q),fs.at[q],fr.at[q],core)
    def f_arrive(q): return rcopy(piece((1-x)*2+1-c,q),piece((1-x)*2+1-c,q),fs.at[q],fr.at[q],core)
    loop(lambda k: p_copy(k).start(),1)
    x_copy(dp).start(); c_copy(dp).start()
    def onward(k):
        q=(dp-k+8)%8
        p_arrive(k).wait_recv(); x_copy(q).start(); c_copy(q).start()
    loop(onward,1)
    loop(lambda k: d_arrive(k).wait_recv(),1)
    acc=vd[0]
    for i in range(1,8): acc=acc+vd[i]
    vo_ref[...]=acc
    def from_across(k):
        q=(dp-k+8)%8
        x_arrive(q).wait_recv(); f_copy(q).start()
    loop(from_across)
    def drain(q):
        c_arrive(q).wait_recv(); f_arrive(q).wait_recv()
        x_copy(q).wait_send(); c_copy(q).wait_send(); f_copy(q).wait_send()
    loop(drain)
    def sent(k):
        l_copy(k).wait_send(); p_copy(k).wait_send(); d_copy(k).wait_send()
    loop(sent,1)
    loop(lambda k: t_copy(k).wait_send(),1,4)
    for p in range(2):
        for i in range(2):
            e_arrive(i,p).wait_recv(); e_copy(i,p).wait_send()

def last_sums(own,mine,over,v):
    DS=pltpu.SemaphoreType.DMA
    vm=pl.BlockSpec(memory_space=pltpu.VMEM)
    V=pltpu.VMEM
    S=jax.ShapeDtypeStruct
    early,late,total=pl.pallas_call(last_sums_kernel,out_shape=[S((24,288,128),bf),S((4,24,144,128),bf),S(v.shape,f32)],in_specs=[vm]*4,out_specs=[vm]*3,
        scratch_shapes=[V((8,3,144,128),bf),V((4,)+v.shape,f32),V((8,)+v.shape,f32)]+[DS((8,))]*10+[DS((2,2))]*2+[DS((4,))]*2+[DS((8,))]*2,
        cost_estimate=pl.CostEstimate(flops=10**7,bytes_accessed=150*10**6,transcendentals=0),
        compiler_params=pltpu.CompilerParams(has_side_effects=True,vmem_limit_bytes=60<<20),name="last_gradient_sums")(own.reshape(24,144,128),mine,over,v)
    return early,late.reshape(48,288,128),total


H = 12
NGRP = 16
STEP = 10
EPS_NORM = 1e-06
BETA_ONE = 0.5
BETA_TWO = 0.5
ADAM_EPS = 1e-08
RATE_BLOCK = 0.3
RATE_VECTOR = 0.2
NEG_RAW = -8.0e9
HEAD = 64
SCALE = 1.0 / math.sqrt(HEAD)
EXP2 = SCALE * math.log2(math.e)
NN = (((1,), (0,)), ((), ()))
NT = (((1,), (1,)), ((), ()))
TN = (((0,), (0,)), ((), ()))


def mm(a, b, dims=NN):
    return lax.dot_general(a, b, dims, preferred_element_type=f32)


def column_sum(v):
    return jnp.sum(v, axis=0, keepdims=True)


def vmem_spec():
    return pl.BlockSpec(memory_space=pltpu.VMEM)


def smem_spec():
    return pl.BlockSpec(memory_space=pltpu.SMEM)


def any_spec():
    return pl.BlockSpec(memory_space=pl.ANY)


def params(mib=60):
    return pltpu.CompilerParams(vmem_limit_bytes=mib << 20)


def pack(block, odd):
    half = block.shape[0] // 2
    left, right = block[:, :64], block[:, 128:]
    even_tail = jnp.concatenate([right[:half], right[half:]], axis=1)
    odd_tail = jnp.concatenate([left[half:], left[:half]], axis=1)
    return jnp.where(odd, block[:, 64:], block[:, :128]), jnp.where(odd, odd_tail, even_tail)


def unpack(top, tail, odd):
    first, second = tail[:, :64], tail[:, 64:]
    even = jnp.concatenate([top, jnp.concatenate([first, second], axis=0)], axis=1)
    return jnp.where(odd, jnp.concatenate([jnp.concatenate([second, first], axis=0), top], axis=1), even)


def turn(v):
    return jnp.concatenate([v[:, 64:], v[:, :64]], axis=1)


def group_of(n):
    return 4 if n % 4 == 0 else 3 if n % 3 == 0 else 1


def pack_kernel(odd_ref, m_ref, p_ref, s_ref):
    g = m_ref.shape[0]
    for b in range(g):
        m = m_ref[b]
        top, tail = pack(m, odd_ref[pl.program_id(0) * g + b] == 1)
        p_ref[b, :192] = top.astype(bf)
        p_ref[b, 192:] = tail.astype(bf)
        s_ref[b] = jnp.full((8, 128), jnp.sum(m * m), f32)


def pack_master(odd, master):
    n = master.shape[0]
    g = group_of(n)
    at = lambda i, s: (i, 0, 0)
    spec = pltpu.PrefetchScalarGridSpec(
        num_scalar_prefetch=1,
        grid=(n // g,),
        in_specs=[pl.BlockSpec((g, 192, 192), at)],
        out_specs=[pl.BlockSpec((g, 288, 128), at), pl.BlockSpec((g, 8, 128), at)],
    )
    return pl.pallas_call(
        pack_kernel,
        grid_spec=spec,
        out_shape=[jax.ShapeDtypeStruct((n, 288, 128), bf), jax.ShapeDtypeStruct((n, 8, 128), f32)],
        compiler_params=params(),
        name="pack_master",
    )(odd, master)


def qkv_kernel(src_ref, cnt_ref, at_ref, x0, x1, x2, x3, blk_ref, gain_ref, shift_ref, bq_ref, bv_ref, a_ref, q_ref, qt_ref, k_ref, kt_ref, v_ref, vt_ref, w_ref, st_ref, buf, sems):
    i = pl.program_id(0)

    @pl.when(i == 0)
    def _():
        copies = [pltpu.make_async_copy(blk_ref.at[at_ref[j]], buf.at[j], sems.at[j]) for j in range(12)]
        for copy in copies:
            copy.start()
        odd = at_ref[12] == 1
        for r in range(4):
            parts = []
            for c in range(3):
                copies[r * 3 + c].wait()
                p = buf[r * 3 + c].astype(f32)
                parts.append(unpack(p[:192], p[192:], odd))
            w_ref[r * 192 : (r + 1) * 192, :] = jnp.concatenate(parts, axis=1).astype(bf)

    x = jnp.concatenate([r[...] for r in (x0, x1, x2, x3)], axis=0).astype(f32)
    mean = jnp.mean(x, axis=-1, keepdims=True)
    cen = x - mean
    inv_std = lax.rsqrt(jnp.mean(cen * cen, axis=-1, keepdims=True) + EPS_NORM)
    a = (cen * inv_std * gain_ref[...] + shift_ref[...]).astype(bf)
    a_ref[...] = a
    qkv = mm(a, w_ref[...])
    q = (qkv[:, :192] + bq_ref[...]).astype(bf).astype(f32)
    k = qkv[:, 192:384].astype(bf).astype(f32)
    v = (qkv[:, 384:] + bv_ref[...]).astype(bf).astype(f32)
    row = lax.broadcasted_iota(jnp.int32, (128, 64), 0)
    lane = lax.broadcasted_iota(jnp.int32, (512, 64), 1)
    masked = jnp.concatenate(
        [jnp.where(row < cnt_ref[4 * i + b], 0.0, NEG_RAW) for b in range(4)], axis=0
    )
    ones = jnp.where(lane < 4, 1.0, 0.0)
    k_tail = jnp.where(lane == 0, masked, ones)
    v_tail = jnp.where(lane < 3, 1.0, 0.0)
    zero = jnp.zeros((512, 64), f32)
    sub = lax.broadcasted_iota(jnp.int32, (64, 512), 0)
    t_tail = jnp.where(sub < 1, 1.0, 0.0)
    qt, kt, vt = q.T, k.T, v.T
    longest = lambda a: jnp.max(jnp.concatenate([column_sum(a[h * 64 : (h + 1) * 64] ** 2) for h in range(3)], axis=0))
    st_ref[0] = jnp.where(lax.broadcasted_iota(jnp.int32, (8, 128), 0) == 0, longest(qt), longest(kt))
    for h in range(3):
        s = slice(h * 64, (h + 1) * 64)
        q_ref[h] = jnp.concatenate([q[:, s], zero], axis=1).astype(bf)
        k_ref[h] = jnp.concatenate([k[:, s], k_tail], axis=1).astype(bf)
        v_ref[h] = jnp.concatenate([v[:, s], v_tail], axis=1).astype(bf)
        qt_ref[h] = jnp.concatenate([qt[s], t_tail], axis=0).astype(bf)
        kt_ref[h] = kt[s].astype(bf)
        vt_ref[h] = jnp.concatenate([vt[s], t_tail[:16]], axis=0).astype(bf)


def qkv_forward(src, cnt, own_at, tokens, blocks, gain, shift, bq, bv):
    n = tokens.shape[0]
    rows = [pl.BlockSpec((128, 768), lambda i, s, c, o, k=k: (s[4 * i + k], 0)) for k in range(4)]
    row = lambda i, s, c, o: (0, 0)
    spec = pltpu.PrefetchScalarGridSpec(
        num_scalar_prefetch=3,
        grid=(n // 512,),
        in_specs=rows
        + [any_spec(), pl.BlockSpec((1, 768), row), pl.BlockSpec((1, 768), row), pl.BlockSpec((1, 192), row), pl.BlockSpec((1, 192), row)],
        out_specs=[
            pl.BlockSpec((512, 768), lambda i, s, c, o: (i, 0)),
            pl.BlockSpec((3, 512, 128), lambda i, s, c, o: (0, i, 0)),
            pl.BlockSpec((3, 128, 512), lambda i, s, c, o: (0, 0, i)),
            pl.BlockSpec((3, 512, 128), lambda i, s, c, o: (0, i, 0)),
            pl.BlockSpec((3, 64, 512), lambda i, s, c, o: (0, 0, i)),
            pl.BlockSpec((3, 512, 128), lambda i, s, c, o: (0, i, 0)),
            pl.BlockSpec((3, 80, 512), lambda i, s, c, o: (0, 0, i)),
            pl.BlockSpec((768, 576), row),
            pl.BlockSpec((1, 8, 128), lambda i, s, c, o: (i, 0, 0)),
        ],
        scratch_shapes=[pltpu.VMEM((12, 288, 128), bf), pltpu.SemaphoreType.DMA((12,))],
    )
    shapes = [(n, 768), (3, n, 128), (3, 128, n), (3, n, 128), (3, 64, n), (3, n, 128), (3, 80, n), (768, 576)]
    return pl.pallas_call(
        qkv_kernel,
        grid_spec=spec,
        out_shape=[jax.ShapeDtypeStruct(s, bf) for s in shapes] + [jax.ShapeDtypeStruct((n // 512, 8, 128), f32)],
        compiler_params=params(),
        name="norm_and_qkv",
    )(src, cnt, own_at, tokens, tokens, tokens, tokens, blocks, gain, shift, bq, bv)


def split3(v):
    a = v.astype(bf).astype(f32)
    b = (v - a).astype(bf).astype(f32)
    return a, b, v - a - b


def in_steps(units, sizes, body, carry):
    at = 0
    for size in sizes:
        count = (units - at) // size
        carry = lax.fori_loop(0, count, lambda i, c, at=at, size=size: body(at + i * size, size, c), carry)
        at = at + count * size
    return carry


def attend_kernel(bq, n_ref, k_ref, qt_ref, vt_ref, ot_ref, qb_ref, p_ref, rt_ref):
    live = n_ref[0]
    qi = pl.program_id(1)
    units = (live + 3) // 4

    def finish(top, acc):
        total = acc[64:65]
        ot_ref[0] = acc[:64] / total
        rt_ref[0] = 1.0 / total
        a, b, c = split3((top + jnp.log2(total)) * (-1.0 / EXP2))
        row = lax.broadcasted_iota(jnp.int32, (64, bq), 0)
        tail = jnp.where(row == 0, 1.0, jnp.where(row == 1, a, jnp.where(row == 2, b, jnp.where(row == 3, c, 0.0))))
        qb_ref[0, :64] = qt_ref[0, :64]
        qb_ref[0, 64:] = tail.astype(bf)

    def keys(u, size):
        return pl.ds(pl.multiple_of(u * 512, 512), size * 512)

    @pl.when(jnp.logical_and(qi * bq < live * 128, n_ref[1] == 1))
    def _():
        qt = qt_ref[0]

        def body(u, size, acc):
            for part in range(size):
                at = keys(u + part, 1)
                p = jnp.exp2(mm(k_ref[0, at, :], qt) * EXP2).astype(bf)
                p_ref[0, at, :] = p
                acc = acc + mm(vt_ref[0, :, at], p)
            return acc

        finish(0.0, in_steps(units, (4, 2, 1), body, jnp.zeros((80, bq), f32)))

    @pl.when(jnp.logical_and(qi * bq < live * 128, n_ref[1] == 0))
    def _():
        qt = qt_ref[0]

        def body(u, size, carry):
            top, acc = carry
            s = mm(k_ref[0, keys(u, size), :], qt) * EXP2
            new = jnp.maximum(top, jnp.max(s, axis=0, keepdims=True))
            p = jnp.exp2(s - new).astype(bf)
            return new, acc * jnp.exp2(top - new) + mm(vt_ref[0, :, keys(u, size)], p)

        finish(*in_steps(units, (2, 1), body, (jnp.full((1, bq), -3e38, f32), jnp.zeros((80, bq), f32))))


def attend(live, k, qt, vt, bq=1024):
    n = k.shape[1]
    spec = pltpu.PrefetchScalarGridSpec(
        num_scalar_prefetch=1,
        grid=(3, n // bq),
        in_specs=[
            pl.BlockSpec((1, n, 128), lambda h, i, s: (h, 0, 0)),
            pl.BlockSpec((1, 128, bq), lambda h, i, s: (h, 0, i)),
            pl.BlockSpec((1, 80, n), lambda h, i, s: (h, 0, 0)),
        ],
        out_specs=[
            pl.BlockSpec((1, 64, bq), lambda h, i, s: (h, 0, i)),
            pl.BlockSpec((1, 128, bq), lambda h, i, s: (h, 0, i)),
            pl.BlockSpec((1, n, bq), lambda h, i, s: (h, 0, i)),
            pl.BlockSpec((1, 1, bq), lambda h, i, s: (h, 0, i)),
        ],
    )
    return pl.pallas_call(
        functools.partial(attend_kernel, bq),
        grid_spec=spec,
        out_shape=[
            jax.ShapeDtypeStruct((3, 64, n), f32),
            jax.ShapeDtypeStruct((3, 128, n), bf),
            jax.ShapeDtypeStruct((3, n, n), bf),
            jax.ShapeDtypeStruct((3, 1, n), f32),
        ],
        compiler_params=params(),
        name="attention_forward",
    )(live, k, qt, vt)


def spread_kernel(src_ref, n_ref, t_ref, ot_ref, *o_refs):
    live, t, tiles = n_ref[0], t_ref[0], len(o_refs)
    per = o_refs[0].shape[1] // 128

    def step(b, _):
        g = src_ref[b]
        lanes = pl.ds(pl.multiple_of(b * 128, 128), 128)
        to = pl.ds(pl.multiple_of((g % per) * 128, 128), 128)
        for k in range(tiles):
            here = (g // per - t + tiles) % tiles == k

            @pl.when(jnp.logical_and(here, b < live))
            def _():
                for h in range(3):
                    o_refs[k][h * 64 : (h + 1) * 64, to] = ot_ref[h, :, lanes].astype(bf)

            @pl.when(jnp.logical_and(here, b >= live))
            def _():
                o_refs[k][:, to] = jnp.zeros((192, 128), bf)

        return 0

    lax.fori_loop(0, ot_ref.shape[2] // 128, step, 0)


def spread(src, live, tile, ot, tiles):
    n = ot.shape[2]
    return pl.pallas_call(
        spread_kernel,
        in_specs=[smem_spec()] * 3 + [vmem_spec()],
        out_specs=[vmem_spec()] * tiles,
        out_shape=[jax.ShapeDtypeStruct((192, n // tiles), bf)] * tiles,
        compiler_params=params(),
        name="spread_attended",
    )(src, live, tile, ot)


def collect_kernel(src_ref, n_ref, t_ref, ot_ref, rt_ref, *refs):
    g_refs, (dt_ref, d_ref) = refs[:-2], refs[-2:]
    live, t, tiles = n_ref[0], t_ref[0], len(g_refs)
    mild = n_ref[1] == 1
    per = g_refs[0].shape[1] // 128
    row = lax.broadcasted_iota(jnp.int32, (64, 128), 0)

    def step(b, _):
        g = src_ref[b]
        to = pl.ds(pl.multiple_of(b * 128, 128), 128)
        lanes = pl.ds(pl.multiple_of((g % per) * 128, 128), 128)
        for k in range(tiles):

            @pl.when(jnp.logical_and((t - g // per + tiles) % tiles == k, b < live))
            def _():
                for h in range(3):
                    scale = jnp.where(mild, rt_ref[h, :, to], 1.0)
                    d = (g_refs[k][h * 64 : (h + 1) * 64, lanes].astype(f32) * scale).astype(bf).astype(f32)
                    x, y, z = split3(-jnp.sum(d * ot_ref[h, :, to], axis=0, keepdims=True))
                    tail = jnp.where(row == 0, x, jnp.where(row == 1, y, jnp.where(row == 2, z, 0.0)))
                    dt_ref[h, :, to] = jnp.concatenate([d, tail], axis=0).astype(bf)
                    d_ref[h, to, :] = jnp.concatenate([d, jnp.zeros_like(d)], axis=0).T.astype(bf)

        @pl.when(b >= live)
        def _():
            dt_ref[:, :, to] = jnp.zeros((3, 128, 128), bf)
            d_ref[:, to, :] = jnp.zeros((3, 128, 128), bf)

        return 0

    lax.fori_loop(0, ot_ref.shape[2] // 128, step, 0)


def collect(src, live, tile, grads, ot, rt):
    n = ot.shape[2]
    return pl.pallas_call(
        collect_kernel,
        in_specs=[smem_spec()] * 3 + [vmem_spec()] * (2 + len(grads)),
        out_specs=[vmem_spec()] * 2,
        out_shape=[jax.ShapeDtypeStruct((3, 128, n), bf), jax.ShapeDtypeStruct((3, n, 128), bf)],
        compiler_params=params(),
        name="collect_attended_grad",
    )(src, live, tile, ot, rt, *grads)


def attend_back_kernel(bk, n_ref, p_ref, k_ref, kt_ref, v_ref, qb_ref, q_ref, dt_ref, d_ref, dq_ref, dk_ref, dv_ref):
    live = n_ref[0]
    j = pl.program_id(1)

    @pl.when(j == 0)
    def _():
        dq_ref[...] = jnp.zeros_like(dq_ref)

    @pl.when(j * bk < live * 128)
    def _():
        k, v, kt = k_ref[0], v_ref[0], kt_ref[0]

        def lanes(u, part):
            return pl.ds(pl.multiple_of((u * 2 + part) * 256, 256), 256)

        def kept(u, size, carry):
            dk, dv = carry
            dp = mm(v, dt_ref[0, :, lanes(u, 0)])
            for part in range(2 * size):
                at = lanes(u, part)
                ahead = mm(v, dt_ref[0, :, lanes(u, part + 1)]) if part + 1 < 2 * size else None
                p = p_ref[0, :, at]
                ds = (p.astype(f32) * dp).astype(bf)
                dv = dv + mm(p, d_ref[0, at, :])
                dk = dk + mm(ds, q_ref[0, at, :])
                dq_ref[0, :, at] += mm(kt, ds)
                dp = dp if ahead is None else ahead
            return dk, dv

        def again(u, size, carry):
            dk, dv = carry
            for part in range(2 * size):
                at = lanes(u, part)
                p = jnp.exp2(mm(k, qb_ref[0, :, at]) * EXP2)
                ds = (p * mm(v, dt_ref[0, :, at])).astype(bf)
                dv = dv + mm(p.astype(bf), d_ref[0, at, :])
                dk = dk + mm(ds, q_ref[0, at, :])
                dq_ref[0, :, at] += mm(kt, ds)
            return dk, dv

        units = (live + 3) // 4
        zero = jnp.zeros((bk, 128), f32)
        dk, dv = lax.cond(
            n_ref[1] == 1,
            lambda: in_steps(units, (4, 2, 1), kept, (zero, zero)),
            lambda: in_steps(units, (2, 1), again, (zero, zero)),
        )
        dk_ref[0] = (dk * SCALE).astype(bf)
        dv_ref[0] = dv.astype(bf)


def attend_back(first, heads, live, p, k, kt, v, qb, q, dt, d, bk=512):
    n = k.shape[1]
    whole_t = lambda h, j, s: (first + h, 0, 0)
    rows = lambda h, j, s: (first + h, j, 0)
    spec = pltpu.PrefetchScalarGridSpec(
        num_scalar_prefetch=1,
        grid=(heads, n // bk),
        in_specs=[
            pl.BlockSpec((1, bk, n), rows),
            pl.BlockSpec((1, bk, 128), rows),
            pl.BlockSpec((1, 64, bk), lambda h, j, s: (first + h, 0, j)),
            pl.BlockSpec((1, bk, 128), rows),
            pl.BlockSpec((1, 128, n), whole_t),
            pl.BlockSpec((1, n, 128), whole_t),
            pl.BlockSpec((1, 128, n), whole_t),
            pl.BlockSpec((1, n, 128), whole_t),
        ],
        out_specs=[
            pl.BlockSpec((1, 64, n), lambda h, j, s: (h, 0, 0)),
            pl.BlockSpec((1, bk, 128), lambda h, j, s: (h, j, 0)),
            pl.BlockSpec((1, bk, 128), lambda h, j, s: (h, j, 0)),
        ],
    )
    S = jax.ShapeDtypeStruct
    return pl.pallas_call(
        functools.partial(attend_back_kernel, bk),
        grid_spec=spec,
        out_shape=[S((heads, 64, n), f32), S((heads, n, 128), bf), S((heads, n, 128), bf)],
        cost_estimate=pl.CostEstimate(flops=heads * 4 * 10**10, bytes_accessed=heads * 50 * 10**6, transcendentals=0),
        compiler_params=params(),
        name="attention_backward",
    )(live, p, k, kt, v, qb, q, dt, d)


def qkv_back_kernel(given, src_ref, n_ref, odd_ref, x0, x1, x2, x3, gain_ref, a_ref, w_ref, *refs):
    grads, (ga_ref, gz_ref, gw_ref, gb_ref, vs_ref, acc, sums, rows, sems) = refs[:given], refs[given:]
    dqs, dks, dvs = [[(r, h) for r in grads[j::3] for h in range(r.shape[0])] for j in range(3)]
    early = ga_ref.shape[1] // 128
    i = pl.program_id(0)
    live = n_ref[0]

    @pl.when(i == 0)
    def _():
        acc[...] = jnp.zeros_like(acc)
        sums[...] = jnp.zeros_like(sums)
        vs_ref[...] = jnp.zeros_like(vs_ref)

    @pl.when(4 * i < live)
    def _():
        dq = jnp.concatenate([r[h] for r, h in dqs], axis=0).T * SCALE
        g = jnp.concatenate([dq] + [r[h][:, :64].astype(f32) for r, h in dks + dvs], axis=1).astype(bf)
        acc[...] += mm(a_ref[...], g, TN)
        sums[...] += jnp.broadcast_to(column_sum(g.astype(f32)), sums.shape)
        g1 = mm(g, w_ref[...], NT)
        rows[...] = g1.astype(bf)
        x = jnp.concatenate([r[...] for r in (x0, x1, x2, x3)], axis=0).astype(f32)
        cen = x - jnp.mean(x, axis=-1, keepdims=True)
        normed = cen * lax.rsqrt(jnp.mean(cen * cen, axis=-1, keepdims=True) + EPS_NORM)
        vs_ref[0:1, :] += column_sum(g1 * normed)
        vs_ref[1:2, :] += column_sum(g1)

    @pl.when(4 * i >= live)
    def _():
        rows[...] = jnp.zeros_like(rows)

    per = early + gz_ref.shape[1] // 128
    for b in range(4):
        block, at = rows.at[pl.ds(b * 128, 128)], src_ref[4 * i + b]
        t, j = at // per, at % per

        @pl.when(j < early)
        def _():
            pltpu.make_async_copy(block, ga_ref.at[t, pl.ds(pl.multiple_of(j * 128, 128), 128)], sems.at[b]).start()

        @pl.when(j >= early)
        def _():
            pltpu.make_async_copy(block, gz_ref.at[t, pl.ds(pl.multiple_of((j - early) * 128, 128), 128)], sems.at[b]).start()

    for b in range(4):
        pltpu.make_async_copy(rows.at[pl.ds(b * 128, 128)], ga_ref.at[0, pl.ds(0, 128)], sems.at[b]).wait()

    @pl.when(i == pl.num_programs(0) - 1)
    def _():
        for r in range(4):
            for c in range(3):
                top, tail = pack(acc[r * 192 : (r + 1) * 192, c * 192 : (c + 1) * 192], odd_ref[0] == 1)
                gw_ref[r * 3 + c, :192] = top.astype(bf)
                gw_ref[r * 3 + c, 192:] = tail.astype(bf)
        gb_ref[...] = sums[...]


def qkv_backward(src, live, odd, tokens, gain, a, w, grads, tiles, early):
    n = a.shape[0]
    per = n // tiles
    fixed = lambda i, s, c, o: (0, 0)
    row = lambda i, s, c, o: (0, i, 0)
    spec = pltpu.PrefetchScalarGridSpec(
        num_scalar_prefetch=3,
        grid=(n // 512,),
        in_specs=[pl.BlockSpec((128, 768), lambda i, s, c, o, k=k: (s[4 * i + k], 0)) for k in range(4)]
        + [pl.BlockSpec((1, 768), fixed), pl.BlockSpec((512, 768), lambda i, s, c, o: (i, 0)), pl.BlockSpec((768, 576), fixed)]
        + [
            pl.BlockSpec((g.shape[0], 64, 512), lambda i, s, c, o: (0, 0, i)) if g.shape[1] == 64 else pl.BlockSpec((g.shape[0], 512, 128), row)
            for g in grads
        ],
        out_specs=[any_spec(), any_spec(), pl.BlockSpec((12, 288, 128), lambda i, s, c, o: (0, 0, 0)), pl.BlockSpec((8, 576), fixed), pl.BlockSpec((8, 768), fixed)],
        scratch_shapes=[pltpu.VMEM((768, 576), f32), pltpu.VMEM((8, 576), f32), pltpu.VMEM((512, 768), bf), pltpu.SemaphoreType.DMA((4,))],
    )
    S = jax.ShapeDtypeStruct
    return pl.pallas_call(
        functools.partial(qkv_back_kernel, len(grads)),
        grid_spec=spec,
        out_shape=[S((tiles, early, 768), bf), S((tiles, per - early, 768), bf), S((12, 288, 128), bf), S((8, 576), f32), S((8, 768), f32)],
        cost_estimate=pl.CostEstimate(flops=3 * 10**10, bytes_accessed=40 * 10**6, transcendentals=0),
        compiler_params=params(),
        name="qkv_backward",
    )(src, live, odd, tokens, tokens, tokens, tokens, gain, a, w, *grads)


def gelu_parts(z):
    cdf = 0.5 + 0.5 * lax.erf(z * math.sqrt(0.5))
    return z * cdf, cdf + z * (jnp.exp2(z * z * (-0.5 * math.log2(math.e))) * (1.0 / math.sqrt(2.0 * math.pi)))


def middle_kernel(inv_ref, cnt_ref, t_ref, blk_ref, o0, o1, o2, o3, x_ref, c_ref, vp_ref, bu_ref, y_ref, gr_ref, g0, g1, g2_ref, g3,
                  u_s, gz_s, a2_s, gm_s, gb_s, o_s, vs_ref, us_ref, w_out, w_up, w_down, tails, tsem, isem):
    i = pl.program_id(0)
    rows = x_ref.shape[0]
    r0 = i * rows
    kinds = ((w_out, 48, 2, 4), (w_up, 64, 8, 4), (w_down, 128, 2, 16))

    @pl.when(i == 0)
    def _():
        vs_ref[...] = jnp.zeros_like(vs_ref)
        us_ref[...] = jnp.zeros_like(us_ref)

        def pair(w, first, pairs):
            def copies(j):
                r = pl.multiple_of((j // pairs) * 192, 64)
                col = pl.multiple_of((j % pairs) * 384, 128)
                out = []
                for b, off in ((0, 0), (1, 256)):
                    at = first + 2 * j + b
                    slot = inv_ref[at]
                    out.append(pltpu.make_async_copy(blk_ref.at[slot, pl.ds(0, 192)], w.at[pl.ds(r, 192), pl.ds(col + off, 128)], tsem.at[at - 48]))
                    out.append(pltpu.make_async_copy(blk_ref.at[slot, pl.ds(192, 96)], tails.at[at - 48], isem.at[at - 48]))
                return out, r, col

            def start(j, _):
                for copy in copies(j)[0]:
                    copy.start()
                return 0

            def join(j, _):
                got, r, col = copies(j)
                for copy in got:
                    copy.wait()
                even = tails[first + 2 * j - 48].astype(f32)
                odd = tails[first + 2 * j - 47].astype(f32)
                lane = lax.broadcasted_iota(jnp.int32, even.shape, 1) < 64
                w[pl.ds(r, 96), pl.ds(col + 128, 128)] = jnp.where(lane, even, odd).astype(bf)
                w[pl.ds(r + 96, 96), pl.ds(col + 128, 128)] = turn(jnp.where(lane, odd, even)).astype(bf)
                return 0

            return start, join

        todo = [(pair(w, first, pairs), pairs * high) for w, first, pairs, high in kinds]
        for (start, _), n in todo:
            lax.fori_loop(0, n, start, 0)

        for (_, join), n in todo:
            lax.fori_loop(0, n, join, 0)

    vp = vp_ref[...]
    row = r0 + lax.broadcasted_iota(jnp.int32, (rows, 1), 0)
    live = jnp.where(row < cnt_ref[0], 1.0, 0.0)
    t = t_ref[0]
    for k, ref in enumerate((o0, o1, o2, o3)):
        o_s[pl.ds(pl.multiple_of(((t - k + 4) % 4) * 192, 64), 192), :] = ref[...]
    o_t = o_s[...]
    res = x_ref[...].astype(f32) + mm(o_t, w_out[...], TN) + vp[6:7]
    cen = res - jnp.mean(res, axis=-1, keepdims=True)
    inv_std = lax.rsqrt(jnp.mean(cen * cen, axis=-1, keepdims=True) + EPS_NORM)
    normed = cen * inv_std
    a2 = (normed * vp[2:3] + vp[3:4]).astype(bf)
    gy = c_ref[...].astype(f32) * live
    gm = gy.astype(bf)
    a2_s[...] = a2
    gm_s[...] = gm
    branch = jnp.zeros((rows, 768), f32)
    g2 = jnp.zeros((rows, 768), f32)
    for j in range(4):
        cols = slice(j * 768, (j + 1) * 768)
        u, slope = gelu_parts(mm(a2, w_up[:, cols]) + bu_ref[:, cols])
        u = u.astype(bf)
        u_s[:, cols] = u
        branch = branch + mm(u, w_down[cols, :])
        gz = (mm(gm, w_down[cols, :], NT) * slope).astype(bf)
        gz_s[:, cols] = gz
        us_ref[:, cols] += jnp.broadcast_to(column_sum(gz.astype(f32)), (8, 768))
        g2 = g2 + mm(gz, w_up[:, cols], NT)
    y_ref[...] = (live * (res + branch + vp[7:8])).astype(bf)
    d2 = g2 * vp[2:3]
    gr = gy + inv_std * (d2 - jnp.mean(d2, axis=-1, keepdims=True) - normed * jnp.mean(d2 * normed, axis=-1, keepdims=True))
    gr_ref[...] = gr
    gb = gr.astype(bf)
    gb_s[...] = gb
    vs_ref[0:1, :] += column_sum(g2 * normed)
    vs_ref[1:2, :] += column_sum(g2)
    vs_ref[2:3, :] += column_sum(gb.astype(f32))
    vs_ref[3:4, :] += column_sum(gm.astype(f32))
    for k, ref in enumerate((g0, g1, g2_ref, g3)):
        ref[...] = mm(w_out[pl.ds(pl.multiple_of(((t + k) % 4) * 192, 64), 192), :], gb, NT).astype(bf)


def weight_grad_kernel(outs, pos_ref, o_in, gb_in, a2_in, gz_in, u_in, gm_in, *refs):
    s_refs, (o_s, gb_s, a2_s, gz_s, u_s, gm_s, ring, zero, lsem, osem, zsem) = refs[:outs], refs[outs:]
    each = s_refs[0].shape[0]

    def to_slot(block, at, sem):
        for o in range(outs):

            @pl.when(at // each == o)
            def _():
                pltpu.make_async_copy(block, s_refs[o].at[at % each], sem).start()

    def landed(block, sem):
        pltpu.make_async_copy(block, s_refs[0].at[0], sem).wait()

    loads = [pltpu.make_async_copy(a, b, lsem.at[j]) for j, (a, b) in enumerate(
        ((o_in, o_s), (gb_in, gb_s), (a2_in, a2_s), (gz_in, gz_s), (gm_in, gm_s), (u_in, u_s)))]
    for load in loads:
        load.start()
    zero[...] = jnp.zeros_like(zero)

    def clear(j, _):
        to_slot(zero, pos_ref[j], zsem.at[j])
        return 0

    lax.fori_loop(0, 48, clear, 0)
    def send(n, g, first, pairs, high, low):
        half = (n % 2) * 8

        def put(r, b):
            return first + (high + r) * 2 * pairs + 2 * low + b

        for r in range(4):
            part = g[r * 192 : (r + 1) * 192]
            mid = part[:, 128:256]
            upper, lower = mid[:96], turn(mid[96:])
            lane = lax.broadcasted_iota(jnp.int32, upper.shape, 1) < 64
            for b, top, tail in ((0, part[:, :128], jnp.where(lane, upper, lower)), (1, part[:, 256:], jnp.where(lane, lower, upper))):
                k = half + 2 * r + b

                @pl.when(n >= 2)
                def _():
                    landed(ring.at[k], osem.at[k])

                ring[k, :192] = top.astype(bf)
                ring[k, 192:] = tail.astype(bf)
                to_slot(ring.at[k], pos_ref[put(r, b)], osem.at[k])

    def lanes(j):
        return pl.ds(pl.multiple_of(j * 384, 128), 384)

    def grad_out(n, _):
        send(n, mm(o_s[...], gb_s[:, lanes(n)]), 48, 2, 0, n)
        return 0

    def grad_up(n, _):
        send(n, mm(a2_s[...], gz_s[:, lanes(n)], TN), 64, 8, 0, n)
        return 0

    def grad_down(n, _):
        high = n // 2
        send(n, mm(u_s[:, pl.ds(pl.multiple_of(high * 768, 128), 768)], gm_s[:, lanes(n % 2)], TN), 128, 2, high * 4, n % 2)
        return 0

    def drain():
        for k in range(16):
            landed(ring.at[k], osem.at[k])

    for f, n, first in ((grad_out, 2, 0), (grad_up, 8, 2), (grad_down, 8, 4)):
        loads[first].wait()
        loads[first + 1].wait()
        lax.fori_loop(0, n, f, 0)
        drain()

    def cleared(j, _):
        landed(zero, zsem.at[j])
        return 0

    lax.fori_loop(0, 48, cleared, 0)


def middle(inv, count, tile, blocks, o_parts, tokens, cotangent, vec_params, bias_up, rows=256):
    n, width = tokens.shape
    hidden = bias_up.shape[1]
    row = lambda i, s, c, t: (i, 0)
    fixed = lambda i, s, c, t: (0, 0)
    col = lambda i, s, c, t: (0, i)
    V, DS = pltpu.VMEM, pltpu.SemaphoreType.DMA
    narrow, wide, part = pl.BlockSpec((rows, width), row), pl.BlockSpec((rows, hidden), row), pl.BlockSpec((192, rows), col)
    spec = pltpu.PrefetchScalarGridSpec(
        num_scalar_prefetch=3,
        grid=(n // rows,),
        in_specs=[any_spec()] + [part] * 4 + [narrow, narrow, pl.BlockSpec((12, width), fixed), pl.BlockSpec((1, hidden), fixed)],
        out_specs=[narrow, narrow] + [part] * 4 + [wide, wide, narrow, narrow, narrow, pl.BlockSpec((width, rows), col),
                   pl.BlockSpec((8, width), fixed), pl.BlockSpec((8, hidden), fixed)],
        scratch_shapes=[V((768, 768), bf), V((768, 3072), bf), V((3072, 768), bf), V((144, 96, 128), bf), DS((144,)), DS((144,))],
    )
    S = jax.ShapeDtypeStruct
    return pl.pallas_call(
        middle_kernel,
        grid_spec=spec,
        out_shape=[S((n, width), bf), S((n, width), f32)] + [S((192, n), bf)] * 4 + [S((n, hidden), bf)] * 2 + [S((n, width), bf)] * 3
        + [S((width, n), bf), S((8, width), f32), S((8, hidden), f32)],
        compiler_params=params(),
        name="projection_and_mlp",
    )(inv, count, tile, blocks, *o_parts, tokens, cotangent, vec_params, bias_up)


def weight_grads_to_slots(pos, outs, block_count, o_t, gb, a2, gz, u, gm):
    V, DS = pltpu.VMEM, pltpu.SemaphoreType.DMA
    arrays = (o_t, gb, a2, gz, u, gm)
    return pl.pallas_call(
        functools.partial(weight_grad_kernel, outs),
        in_specs=[smem_spec()] + [any_spec()] * 6,
        out_specs=[any_spec()] * outs,
        out_shape=[jax.ShapeDtypeStruct((block_count // outs, 288, 128), bf)] * outs,
        scratch_shapes=[V(a.shape, bf) for a in arrays] + [V((16, 288, 128), bf), V((288, 128), bf), DS((6,)), DS((16,)), DS((48,))],
        cost_estimate=pl.CostEstimate(flops=6 * 10**10, bytes_accessed=32 * 10**6, transcendentals=0),
        compiler_params=params(),
        name="mlp_weight_gradients",
    )(pos, *arrays)


def quarters(b0, b1):
    return (b0 * 2 + b1, (1 - b0) * 2 + b1, b0 * 2 + 1 - b1, (1 - b0) * 2 + 1 - b1)


def add_pair_kernel(common, bits_ref, *refs):
    outs = list(refs[16:])
    for p in range(2):
        for side in range(4):
            j = 4 * p + side
            total = (refs[2 * j][...].astype(f32) + refs[2 * j + 1][...].astype(f32)).astype(bf)
            if side == common[p]:
                outs[6][p] = total
            else:
                outs[3 * p + side - (side > common[p])][...] = total


def add_pair(bits, common, keep, came):
    specs = []
    for p in range(2):
        for side in range(4):
            at = lambda i, b, p=p, side=side: (p * 12 + quarters(b[2 * p], b[2 * p + 1])[side] * 3 + i, 0, 0)
            specs += [pl.BlockSpec((4, 288, 128), at)] * 2
    S = jax.ShapeDtypeStruct
    return pl.pallas_call(
        functools.partial(add_pair_kernel, common),
        grid_spec=pltpu.PrefetchScalarGridSpec(
            num_scalar_prefetch=1,
            grid=(3,),
            in_specs=specs,
            out_specs=[pl.BlockSpec((4, 288, 128), lambda i, b: (i, 0, 0))] * 6 + [pl.BlockSpec((2, 4, 288, 128), lambda i, b: (0, i, 0, 0))],
        ),
        out_shape=[S((12, 288, 128), bf)] * 6 + [S((2, 12, 288, 128), bf)],
        compiler_params=params(),
        name="add_gradients_of_cores",
    )(bits, *[keep, came] * 8)


def add_four_kernel(common, bits_ref, *refs):
    outs = refs[7:]
    for p in range(2):
        parts = refs[3 * p : 3 * p + 3]
        for side, q in enumerate(quarters(bits_ref[2 * p], bits_ref[2 * p + 1])):
            for b in range(3):
                total = (sum(r[q * 3 + b].astype(f32) for r in parts) + refs[6][p, q * 3 + b].astype(f32)).astype(bf)
                if side == common[p]:
                    outs[6][p, b] = total
                else:
                    outs[3 * p + side - (side > common[p])][b] = total


def add_four(bits, common, parts):
    S = jax.ShapeDtypeStruct
    return pl.pallas_call(
        functools.partial(add_four_kernel, common),
        in_specs=[smem_spec()] + [vmem_spec()] * 7,
        out_specs=[vmem_spec()] * 7,
        out_shape=[S((3, 288, 128), bf)] * 6 + [S((2, 3, 288, 128), bf)],
        compiler_params=params(),
        name="add_gradients",
    )(bits, *parts)


def add_last_kernel(*refs):
    for p in range(2):
        for b in range(3):
            refs[7][3 * p + b] = (sum(r[b].astype(f32) for r in refs[3 * p : 3 * p + 3]) + refs[6][p, b].astype(f32)).astype(bf)


def add_last(parts):
    return pl.pallas_call(
        add_last_kernel,
        in_specs=[vmem_spec()] * 7,
        out_specs=vmem_spec(),
        out_shape=jax.ShapeDtypeStruct((6, 288, 128), bf),
        compiler_params=params(),
        name="add_last_gradients",
    )(*parts)


def split2(v):
    hi = v.astype(bf)
    return hi, (v - hi.astype(f32)).astype(bf)


def mm3(a, b, dims):
    return mm(a[0], b[0], dims) + (mm(a[0], b[1], dims) + mm(a[1], b[0], dims))


def adam_kernel(odd_ref, from_ref, g_ref, late_ref, m1_ref, m2_ref, l_ref, r_ref, g_out, m1_out, m2_out, u_out, s_out):
    for b in range(g_ref.shape[0]):
        slot = pl.program_id(0) * g_ref.shape[0] + b
        place = from_ref[slot]
        part = jnp.where(place >= 0, late_ref[jnp.maximum(place, 0)].astype(f32), g_ref[b].astype(f32))
        grad = unpack(part[:192], part[192:], odd_ref[slot] == 1)
        left, right = split2(l_ref[b]), split2(r_ref[b])
        low = grad.astype(bf)
        rot = mm3(split2(mm(left[0], low, TN) + mm(left[1], low, TN)), right, NN)
        first = BETA_ONE * m1_ref[b] + (1.0 - BETA_ONE) * rot
        second = BETA_TWO * m2_ref[b] + (1.0 - BETA_TWO) * rot * rot
        upd = (first / (1.0 - BETA_ONE**STEP)) / (jnp.sqrt(second / (1.0 - BETA_TWO**STEP)) + ADAM_EPS)
        upd = mm3(split2(mm3(left, split2(upd), NN)), right, NT)
        g_out[b] = grad
        m1_out[b] = first
        m2_out[b] = second
        u_out[b] = upd
        s_out[b] = jnp.full((8, 128), jnp.sum(upd * upd), f32)


def adam(odd, late_at, grads, late, first, second, left, right):
    n = grads.shape[0]
    g = group_of(n)
    at = lambda i, s, f: (i, 0, 0)
    big = pl.BlockSpec((g, 192, 192), at)
    spec = pltpu.PrefetchScalarGridSpec(
        num_scalar_prefetch=2,
        grid=(n // g,),
        in_specs=[pl.BlockSpec((g, 288, 128), at), pl.BlockSpec(late.shape, lambda i, s, f: (0, 0, 0))] + [big] * 4,
        out_specs=[big] * 4 + [pl.BlockSpec((g, 8, 128), at)],
    )
    return pl.pallas_call(
        adam_kernel,
        grid_spec=spec,
        out_shape=[jax.ShapeDtypeStruct((n, 192, 192), f32)] * 4 + [jax.ShapeDtypeStruct((n, 8, 128), f32)],
        compiler_params=params(),
        name="rotated_adam",
    )(odd, late_at, grads, late, first, second, left, right)


def halving_places(slot, core):
    dp, r = slot // 24, slot % 24
    y, z, far, x, s = dp % 2, dp // 2 % 2, dp // 4, r % 6 // 3, r % 3
    portion = r % 12 // 6
    inside = jnp.where(portion == 0, x * 8 + y * 4 + z * 2 + far, y * 8 + z * 4 + x * 2 + far)
    return jnp.where(r // 12 == core, 0, 96) + portion * 48 + inside * 3 + s


def norm_forward(row_data, gain_vec, shift_vec):
    row_mean = jnp.mean(row_data, axis=-1, keepdims=True)
    centred = row_data - row_mean
    inv_std = lax.rsqrt(jnp.mean(centred * centred, axis=-1, keepdims=True) + EPS_NORM)
    normed = centred * inv_std
    return (normed * gain_vec + shift_vec, normed, inv_std)


def norm_back(grad_out, normed, inv_std, gain_vec):
    grad_normed = grad_out * gain_vec
    return inv_std * (
        grad_normed
        - jnp.mean(grad_normed, axis=-1, keepdims=True)
        - normed * jnp.mean(grad_normed * normed, axis=-1, keepdims=True)
    )


def block_plan(counts, slot_count):
    tiles = counts.shape[0]
    per = slot_count // 128
    j = lax.broadcasted_iota(jnp.int32, (tiles, per), 1)
    kept = jnp.clip(counts[:, None] - j * 128, 0, 128).reshape(-1)
    full = (kept > 0).astype(jnp.int32)
    index = jnp.arange(tiles * per, dtype=jnp.int32)
    before = (index[None, :] < index[:, None]).astype(jnp.int32)
    ahead = jnp.sum(before * full[None, :], axis=1)
    live = jnp.sum(full)
    place = jnp.where(full > 0, ahead, live + index - ahead)
    hot = (place[None, :] == index[:, None]).astype(jnp.int32)
    return jnp.sum(hot * index[None, :], axis=1), jnp.sum(hot * kept[None, :], axis=1), live.reshape(1)


def make_body(tuned):
    def body(tokens, cotangent, counts, master, slot_block, groups, first_moment, second_moment, left_basis, right_basis, vec_params, vec_first, vec_second):
        slot_count, width = tokens.shape[1:]
        per_owner = master.shape[0]
        tile = lax.axis_index("tile")
        mine = lax.dynamic_slice(slot_block, (lax.axis_index("dp") * per_owner,), (per_owner,))
        odd = mine % 2
        packed, weight_sq = pack_master(odd, master)
        own_tokens = tokens.reshape(slot_count, width)
        count_tile = jnp.broadcast_to(counts.reshape(1, 1), (8, 128))
        if tuned:
            blocks, token_all, count_all = gather_all(packed, own_tokens, count_tile)
        else:
            blocks = lax.all_gather(packed, "dp", axis=0, tiled=True)
            token_all = lax.all_gather(own_tokens, "tile", axis=0)
            count_all = lax.all_gather(count_tile, "tile", axis=0)
        tiles = token_all.shape[0]
        block_count = blocks.shape[0]
        src, cnt, live = block_plan(count_all[:, 0, 0], slot_count)
        index = jnp.arange(block_count, dtype=jnp.int32)
        inverse = jnp.sum((slot_block[None, :] == index[:, None]).astype(jnp.int32) * index[None, :], axis=1)
        own_block = jnp.arange(12, dtype=jnp.int32) // 3 * 12 + jnp.arange(12, dtype=jnp.int32) % 3 * 4 + tile
        own_at = jnp.sum((slot_block[None, :] == own_block[:, None]).astype(jnp.int32) * index[None, :], axis=1)
        own_at = jnp.concatenate([own_at, tile.reshape(1) % 2])
        own = width // tiles
        bias = lambda row: lax.dynamic_slice(vec_params[row : row + 1], (0, tile * own), (1, own))
        a1, q, qt, k, kt, v, vt, w_qkv, lengths = qkv_forward(
            src, cnt, own_at, token_all.reshape(-1, width), blocks, vec_params[0:1], vec_params[1:2], bias(4), bias(5)
        )
        mild = jnp.sqrt(jnp.max(lengths[:, 0, 0])) * jnp.sqrt(jnp.max(lengths[:, 1, 0])) * EXP2 <= 60.0
        live = jnp.concatenate([live, mild.astype(jnp.int32).reshape(1)])
        ot, qb, p, rt = attend(live, k, qt, vt)

        def shift(parts):
            return [parts[0]] + [lax.ppermute(parts[j], "tile", [(s, (s + j) % tiles) for s in range(tiles)]) for j in range(1, tiles)]

        tile_one = tile.astype(jnp.int32).reshape(1)
        o_parts = shift(spread(src, live, tile_one, ot, tiles))
        output, grad_resid, *rest = middle(
            inverse, counts.reshape(1), tile_one, blocks, o_parts, own_tokens, cotangent.reshape(slot_count, width), vec_params, vec_params[8:].reshape(1, -1)
        )
        go_parts, (u, gz, a2, gm, gb, o_t, sums, up_sums) = rest[:tiles], rest[tiles:]
        go_parts = shift(go_parts)
        back = lambda first, heads, dt: list(attend_back(first, heads, live, p, k, kt, v, qb, q, dt, d))
        if tuned:
            dp = lax.axis_index("dp")
            bit = {"x": tile // 2, "y": dp % 2, "z": dp // 2 % 2, "far": dp // 4}
            mask = {"x": 2, "y": 4, "z": 8, "far": 16}

            def flip(array, *names):
                change = sum(mask[name] for name in names)
                return lax.ppermute(array, ("dp", "tile"), [(s, s ^ change) for s in range(32)])

            def three(sums, pairs, common):
                out = []
                for p, (a, b) in enumerate(pairs):
                    ways = [(), (a,), (b,), (a, b)]
                    del ways[common[p]]
                    out += [flip(sums[3 * p + j], *way) if way else sums[3 * p + j] for j, way in enumerate(ways)]
                return out + [flip(sums[6], pairs[0][common[0] - 1])]

            def bits_of(pairs):
                return jnp.stack([bit[name] for pair in pairs for name in pair]).astype(jnp.int32)

            first, second = [("x", "y"), ("y", "z")], [("z", "far"), ("x", "far")]
            keep, send = weight_grads_to_slots(halving_places(inverse, tile % 2), 2, block_count, o_t, gb, a2, gz, u, gm)
            send, go_parts = lax.optimization_barrier((send, go_parts))
            came = lax.ppermute(send, "tile", [(s, s ^ 1) for s in range(4)])
            dt, d = collect(src, live, tile_one, go_parts, ot, rt)
            dt, came = lax.optimization_barrier((dt, came))
            sums_one = add_pair(bits_of(first), (2, 1), keep, came)
            dt, sums_one = lax.optimization_barrier((dt, sums_one))
            parts = three(sums_one, first, (2, 1))
            head_grads = back(0, 2, dt)
            head_grads[0], parts = lax.optimization_barrier((head_grads[0], parts))
            sums_two = add_four(bits_of(second), (2, 2), parts)
            dt, sums_two = lax.optimization_barrier((dt, sums_two))
            parts = three(sums_two, second, (2, 2))
            head_grads += back(2, 1, dt)
            head_grads[3], parts = lax.optimization_barrier((head_grads[3], parts))
            mine_early = add_last(parts)
            head_grads[3], mine_early = lax.optimization_barrier((head_grads[3], mine_early))
            over_early = flip(mine_early, "x")
        else:
            slots = weight_grads_to_slots(inverse, 1, block_count, o_t, gb, a2, gz, u, gm)[0]
            dt, d = collect(src, live, tile_one, go_parts, ot, rt)
            head_grads = back(0, 3, dt)
        g_one, g_two, gw_qkv, qkv_sums, norm_sums = qkv_backward(
            src, live, tile_one % 2, token_all.reshape(-1, width), vec_params[0:1], a1, w_qkv, head_grads, tiles, slot_count * 3 // 8
        )
        if tuned:
            g_one, over_early = lax.optimization_barrier((g_one, over_early))
        zero = jnp.zeros((width,), f32)
        at_own = lambda s: lax.dynamic_update_slice(zero, s, (tile * own,))
        vector_part = jnp.concatenate(
            [norm_sums[0:2], sums[0:2], at_own(qkv_sums[0, :own])[None], at_own(qkv_sums[0, 2 * own :])[None], sums[2:4], up_sums[0].reshape(-1, width)], axis=0
        )
        if tuned:
            early, late, vector_grads = last_sums(gw_qkv, mine_early, over_early, vector_part)
            g_two, early = lax.optimization_barrier((g_two, early))
        else:
            early = lax.psum(lax.psum_scatter(slots.astype(f32), "dp", scatter_dimension=0, tiled=True), "tile").astype(bf)
            late = lax.all_gather(lax.psum(gw_qkv.astype(f32), "dp").astype(bf), "tile", axis=0, tiled=True)
            vector_grads = lax.psum(vector_part, ("dp", "tile"))
        g1 = jnp.concatenate([lax.psum_scatter(part, "tile", scatter_dimension=0, tiled=False) for part in (g_one, g_two)], axis=0)
        row_input = own_tokens.astype(f32)
        _, normed_one, inv_std_one = norm_forward(row_input, vec_params[0], vec_params[1])
        input_grad = grad_resid + norm_back(g1.astype(f32), normed_one, inv_std_one, vec_params[0])
        late_at = jnp.where(mine < 48, mine % 4 * 12 + mine // 12 * 3 + mine % 12 // 4, -1)
        weight_grads, first_out, second_out, update, update_sq = adam(odd, late_at, early, late, first_moment, second_moment, left_basis, right_basis)
        group_hot = (groups[:, None] == jnp.arange(NGRP, dtype=jnp.int32)[None, :]).astype(f32)
        both = jnp.stack([weight_sq[:, 0, 0], update_sq[:, 0, 0]], axis=0)
        group_part = jnp.pad(jnp.sum(group_hot[None] * both[:, :, None], axis=1), ((0, 6), (0, 128 - NGRP)))
        group_both = group_sum(group_part, block_count // per_owner)
        own_both = jnp.sum(group_hot[None] * group_both[:2, None, :NGRP], axis=2)
        block_rate = RATE_BLOCK * jnp.sqrt(own_both[0]) / (jnp.sqrt(own_both[1]) + 1e-06)
        master_out = master - block_rate[:, None, None] * update
        vec_first_out = BETA_ONE * vec_first + (1.0 - BETA_ONE) * vector_grads
        vec_second_out = BETA_TWO * vec_second + (1.0 - BETA_TWO) * vector_grads * vector_grads
        vec_update = (vec_first_out / (1.0 - BETA_ONE**STEP)) / (jnp.sqrt(vec_second_out / (1.0 - BETA_TWO**STEP)) + ADAM_EPS)
        return (
            output.reshape(1, slot_count, width),
            input_grad.reshape(1, slot_count, width),
            weight_grads,
            first_out,
            second_out,
            master_out,
            master_out.astype(bf),
            vector_grads,
            vec_first_out,
            vec_second_out,
            vec_params - RATE_VECTOR * vec_update,
        )

    return body


def solution(mesh):
    tuned = (mesh.shape["dp"], mesh.shape["tile"]) == (8, 4)
    rows, blocks = P("dp", "tile", None), P("dp", None, None)
    return jax.shard_map(
        make_body(tuned),
        mesh=mesh,
        in_specs=(rows, rows, P("dp", "tile"), blocks, P(), P("dp"), blocks, blocks, blocks, blocks, P(), P(), P()),
        out_specs=(rows, rows, blocks, blocks, blocks, blocks, blocks, P(), P(), P(), P()),
        check_vma=False,
    )
```

```python
import functools
import math

import jax
import jax.numpy as jnp
from jax import lax
from jax.experimental import pallas as pl
from jax.experimental.pallas import tpu as pltpu
from jax.sharding import PartitionSpec as P

f32 = jnp.float32
bf = jnp.bfloat16
MESH = pl.DeviceIdType.MESH

def where_am_i():
    dp=lax.axis_index("dp"); t=lax.axis_index("tile")
    return dp//2, dp%2, t//2, t%2

def dev(z,y,x,c):
    return (z*2+y, x*2+c)

def rcopy(src,dst,ss,rs,to):
    return pltpu.make_async_remote_copy(src_ref=src,dst_ref=dst,send_sem=ss,recv_sem=rs,device_id=to,device_id_type=MESH)

def gather_kernel(own_w,own_tok,own_cnt,all_w,all_tok,all_cnt,
                  zs,zr,ys,yr,xs,xr,cs,cr,fs,fr,ts,tr,ns,nr,ls):
    z,y,x,c=where_am_i()
    per=own_w.shape[0]
    part=per//12
    def a_of(shard,xx,cc): return all_w.at[pl.ds(shard*per+(xx*2+cc)*part,part)]
    def b_of(shard,cc): return all_w.at[pl.ds(shard*per+4*part+cc*4*part,4*part)]
    own_a=own_w.at[pl.ds((x*2+c)*part,part)]
    own_b=own_w.at[pl.ds(4*part+c*4*part,4*part)]
    me=z*2+y
    core=dev(z,y,x,1-c); across=dev(z,y,1-x,c); beside=dev(z,1-y,x,c)
    up=dev(jnp.minimum(z+1,3),y,x,c); down=dev(jnp.maximum(z-1,0),y,x,c)
    def src(shard,own):
        return (own_a,own_b) if own else (a_of(shard,x,c),b_of(shard,c))
    def z_copies(zz,own,go_up):
        shard=zz*2+y
        a,b=src(shard,own)
        d=(z-zz) if go_up else (zz-z)
        k=0 if go_up else 1
        to=up if go_up else down
        return (rcopy(a,a_of(shard,x,c),zs.at[k,d,0],zr.at[k,d,0],to),rcopy(b,b_of(shard,c),zs.at[k,d,1],zr.at[k,d,1],to))
    def z_arrivals(zz,k,dist):
        shard=zz*2+y
        a,b=a_of(shard,x,c),b_of(shard,c)
        return (rcopy(a,a,zs.at[k,dist-1,0],zr.at[k,dist-1,0],up),rcopy(b,b,zs.at[k,dist-1,1],zr.at[k,dist-1,1],up))
    def y_copies(zz,own):
        shard=zz*2+y
        a,b=src(shard,own)
        return (rcopy(a,a_of(shard,x,c),ys.at[zz,0],yr.at[zz,0],beside),rcopy(b,b_of(shard,c),ys.at[zz,1],yr.at[zz,1],beside))
    def y_arrivals(zz):
        shard=zz*2+(1-y)
        a,b=a_of(shard,x,c),b_of(shard,c)
        return (rcopy(a,a,ys.at[zz,0],yr.at[zz,0],beside),rcopy(b,b,ys.at[zz,1],yr.at[zz,1],beside))
    def x_copy(shard,own):
        return rcopy(src(shard,own)[0],a_of(shard,x,c),xs.at[shard],xr.at[shard],across)
    def x_arrival(shard):
        a=a_of(shard,1-x,c)
        return rcopy(a,a,xs.at[shard],xr.at[shard],across)
    def c_copies(shard,own):
        a,b=src(shard,own)
        return (rcopy(a,a_of(shard,x,c),cs.at[shard,0],cr.at[shard,0],core),rcopy(b,b_of(shard,c),cs.at[shard,1],cr.at[shard,1],core))
    def c_arrivals(shard):
        a,b=a_of(shard,x,1-c),b_of(shard,1-c)
        return (rcopy(a,a,cs.at[shard,0],cr.at[shard,0],core),rcopy(b,b,cs.at[shard,1],cr.at[shard,1],core))
    def f_copy(shard):
        a=a_of(shard,1-x,c)
        return rcopy(a,a,fs.at[shard],fr.at[shard],core)
    def f_arrival(shard):
        a=a_of(shard,1-x,1-c)
        return rcopy(a,a,fs.at[shard],fr.at[shard],core)
    def start(cps):
        for cp in (cps if isinstance(cps,tuple) else (cps,)): cp.start()
    def got(cps):
        for cp in (cps if isinstance(cps,tuple) else (cps,)): cp.wait_recv()
    def sent(cps):
        for cp in (cps if isinstance(cps,tuple) else (cps,)): cp.wait_send()
    tile=x*2+c
    tok_x=rcopy(own_tok,all_tok.at[tile],ts.at[0],tr.at[0],across)
    tok_c=rcopy(own_tok,all_tok.at[tile],ts.at[1],tr.at[1],core)
    far=all_tok.at[(1-x)*2+c]
    tok_f=rcopy(far,far,ts.at[2],tr.at[2],core)
    near=all_tok.at[x*2+1-c]
    diag=all_tok.at[(1-x)*2+1-c]
    cnts=[rcopy(own_cnt,all_cnt.at[tile],ns.at[i],nr.at[i],to) for i,to in enumerate((across,core,dev(z,y,1-x,1-c)))]
    cnt_in=[rcopy(r,r,ns.at[i],nr.at[i],core) for i,r in enumerate((all_cnt.at[(1-x)*2+c],all_cnt.at[x*2+1-c],all_cnt.at[(1-x)*2+1-c]))]
    local=(pltpu.make_async_copy(own_w,all_w.at[pl.ds(me*per,per)],ls.at[0]),
           pltpu.make_async_copy(own_tok,all_tok.at[tile],ls.at[1]),pltpu.make_async_copy(own_cnt,all_cnt.at[tile],ls.at[2]))
    @pl.when(z<3)
    def _(): start(z_copies(z,True,True))
    @pl.when(z>0)
    def _(): start(z_copies(z,True,False))
    start(y_copies(z,True)); start(tok_x); start(tok_c)
    for cp in cnts: cp.start()
    for cp in local: cp.start()
    def from_line(k,dist):
        zz=z-dist if k==0 else z+dist
        there=(zz>=0) if k==0 else (zz<=3)
        @pl.when(there)
        def _():
            got(z_arrivals(zz,k,dist))
            @pl.when((z<3) if k==0 else (z>0))
            def _(): start(z_copies(zz,False,k==0))
            start(y_copies(zz,False)); start(x_copy(zz*2+y,False)); start(c_copies(zz*2+y,False))
    def from_beside(zz):
        got(y_arrivals(zz))
        s=zz*2+1-y
        start(x_copy(s,False)); start(c_copies(s,False))
    def guarded(f,dist):
        @pl.when(z-dist>=0)
        def _(): f(z-dist)
        @pl.when(z+dist<=3)
        def _(): f(z+dist)
    def from_across(shard):
        got(x_arrival(shard)); start(f_copy(shard))
    from_line(0,1); from_line(1,1)
    from_beside(z)
    from_line(0,2); from_line(1,2)
    guarded(from_beside,1); guarded(lambda zz: from_across(zz*2+y),1); from_across(z*2+1-y)
    from_line(0,3); from_line(1,3)
    got(tok_x); tok_f.start()
    guarded(from_beside,2); guarded(lambda zz: from_across(zz*2+y),2); guarded(lambda zz: from_across(zz*2+1-y),1)
    guarded(from_beside,3); guarded(lambda zz: from_across(zz*2+y),3); guarded(lambda zz: from_across(zz*2+1-y),2)
    guarded(lambda zz: from_across(zz*2+1-y),3)
    def drain(s,_):
        @pl.when(s!=me)
        def _():
            got(c_arrivals(s)); got(f_arrival(s)); sent(c_copies(s,False)); sent(f_copy(s)); sent(x_copy(s,False))
        return 0
    lax.fori_loop(0,8,drain,0)
    def drain_y(zz,_):
        sent(y_copies(zz,False)); return 0
    lax.fori_loop(0,4,drain_y,0)
    for dist in range(4):
        @pl.when(jnp.logical_and(z<3,z-dist>=0))
        def _(): sent(z_copies(z-dist,False,True))
        @pl.when(jnp.logical_and(z>0,z+dist<=3))
        def _(): sent(z_copies(z+dist,False,False))
    rcopy(near,near,ts.at[1],tr.at[1],core).wait_recv()
    rcopy(diag,diag,ts.at[2],tr.at[2],core).wait_recv()
    tok_x.wait_send(); tok_c.wait_send(); tok_f.wait_send()
    for cp in cnts: cp.wait_send()
    for cp in cnt_in: cp.wait_recv()
    for cp in local: cp.wait()

def gather_all(own_w,own_tok,own_cnt):
    DS=pltpu.SemaphoreType.DMA
    hbm=pl.BlockSpec(memory_space=pl.ANY)
    return pl.pallas_call(gather_kernel,
        out_shape=[jax.ShapeDtypeStruct((8*own_w.shape[0],)+own_w.shape[1:],bf),jax.ShapeDtypeStruct((4,)+own_tok.shape,bf),jax.ShapeDtypeStruct((4,)+own_cnt.shape,own_cnt.dtype)],
        in_specs=[pl.BlockSpec(memory_space=pltpu.VMEM)]*3,out_specs=[hbm]*3,
        scratch_shapes=[DS((2,4,2)),DS((2,4,2)),DS((4,2)),DS((4,2)),DS((8,)),DS((8,)),DS((8,2)),DS((8,2)),DS((8,)),DS((8,)),DS((3,)),DS((3,)),DS((3,)),DS((3,)),DS((3,))],
        compiler_params=pltpu.CompilerParams(has_side_effects=True,vmem_limit_bytes=60<<20),name="gather_weights_tokens")(own_w,own_tok,own_cnt)

def group_sum_kernel(g_ref,o_ref,gd,gs,gr):
    dp=lax.axis_index("dp"); t=lax.axis_index("tile")
    nd=gd.shape[0]
    def copy(k):
        return rcopy(gd.at[dp],gd.at[dp],gs.at[k],gr.at[k],((dp+k)%nd,t))
    def arrive(k):
        q=(dp-k+nd)%nd
        return rcopy(gd.at[q],gd.at[q],gs.at[k],gr.at[k],(q,t))
    def loop(f):
        def s(k,_):
            f(k); return 0
        lax.fori_loop(1,nd,s,0)
    gd[dp]=g_ref[...]
    loop(lambda k: copy(k).start())
    loop(lambda k: arrive(k).wait_recv())
    acc=gd[0]
    for i in range(1,nd): acc=acc+gd[i]
    o_ref[...]=acc
    loop(lambda k: copy(k).wait_send())

def group_sum(g,nd):
    DS=pltpu.SemaphoreType.DMA
    vm=pl.BlockSpec(memory_space=pltpu.VMEM)
    return pl.pallas_call(group_sum_kernel,out_shape=jax.ShapeDtypeStruct(g.shape,f32),in_specs=[vm],out_specs=vm,
        scratch_shapes=[pltpu.VMEM((nd,)+g.shape,f32),DS((nd,)),DS((nd,))],
        compiler_params=pltpu.CompilerParams(has_side_effects=True,vmem_limit_bytes=60<<20),name="sum_groups")(g)

def last_sums_kernel(l_ref,mine,over,v_ref,early,late,vo_ref,yb,zb,own,vb,vd,y1s,y1r,z2s,z2r,z3s,z3r,y4s,y4r,xs,xr,cs,cr,fs,fr,es,er,ts,tr,ds,dr,us,ur):
    z,y,x,c=where_am_i()
    dp=lax.axis_index("dp"); t=lax.axis_index("tile")
    core=dev(z,y,x,1-c); across=dev(z,y,1-x,c); beside=dev(z,1-y,x,c)
    def loop(f,first,n):
        def s(k,_):
            f(k); return 0
        lax.fori_loop(first,n,s,0)
    at=lambda i: pl.ds(i*3,3)
    def y1(k):
        q=(z+k)%4
        return rcopy(l_ref.at[at((1-y)*4+q)],yb.at[q],y1s.at[q],y1r.at[q],beside)
    def z2(k):
        q=(z+k)%4
        return rcopy(own.at[q],zb.at[z],z2s.at[k],z2r.at[k],dev(q,y,x,c))
    def z2_arrive(k):
        q=(z-k+4)%4
        return rcopy(zb.at[q],zb.at[q],z2s.at[k],z2r.at[k],dev(q,y,x,c))
    for k in (2,1,3,0): y1(k).start()
    def t1(k): return rcopy(v_ref.at[(t+k)%4],vb.at[t],ts.at[k],tr.at[k],(dp,(t+k)%4))
    def t1_arrive(k):
        q=(t-k+4)%4
        return rcopy(vb.at[q],vb.at[q],ts.at[k],tr.at[k],(dp,q))
    def d_copy(k): return rcopy(vd.at[dp],vd.at[dp],ds.at[k],dr.at[k],((dp+k)%8,t))
    def d_arrive(k):
        q=(dp-k+8)%8
        return rcopy(vd.at[q],vd.at[q],ds.at[k],dr.at[k],(q,t))
    def t2(k): return rcopy(vo_ref.at[t],vo_ref.at[t],us.at[k],ur.at[k],(dp,(t+k)%4))
    def t2_arrive(k):
        q=(t-k+4)%4
        return rcopy(vo_ref.at[q],vo_ref.at[q],us.at[k],ur.at[k],(dp,q))
    loop(lambda k: t1(k).start(),1,4)
    vb[t]=v_ref[t]
    def place(xx,cc,p): return early.at[pl.ds(cc*12+p*6+xx*3,3)]
    for p in range(2):
        early[pl.ds(c*12+p*6+x*3,3)]=mine[pl.ds(p*3,3)]
        early[pl.ds(c*12+p*6+(1-x)*3,3)]=over[pl.ds(p*3,3)]
    def e_copy(i,p): return rcopy(place(i,c,p),place(i,c,p),es.at[i,p],er.at[i,p],core)
    def e_arrive(i,p): return rcopy(place(i,1-c,p),place(i,1-c,p),es.at[i,p],er.at[i,p],core)
    for p in range(2):
        e_copy(0,p).start(); e_copy(1,p).start()
    loop(lambda k: t1_arrive(k).wait_recv(),1,4)
    vd[dp]=vb[0]+vb[1]+vb[2]+vb[3]
    loop(lambda k: d_copy(k).start(),1,8)
    for k in (2,1,3,0):
        q=(z+k)%4
        y1(k).wait_recv()
        for i in range(3): own[q,i]=(l_ref[(y*4+q)*3+i].astype(f32)+yb[q,i].astype(f32)).astype(bf)
        if k: z2(k).start()
    zb[z]=own[z]
    loop(lambda k: z2_arrive(k).wait_recv(),1,4)
    for i in range(3):
        late[t,(y*4+z)*3+i]=(zb[0,i].astype(f32)+zb[1,i].astype(f32)+zb[2,i].astype(f32)+zb[3,i].astype(f32)).astype(bf)
    def piece(tt,yy,zz): return late.at[tt,at(yy*4+zz)]
    def z3(k): return rcopy(piece(t,y,z),piece(t,y,z),z3s.at[k],z3r.at[k],dev((z+k)%4,y,x,c))
    def z3_arrive(k):
        q=(z-k+4)%4
        return rcopy(piece(t,y,q),piece(t,y,q),z3s.at[k],z3r.at[k],dev(q,y,x,c))
    def y4(q): return rcopy(piece(t,y,q),piece(t,y,q),y4s.at[q],y4r.at[q],beside)
    def y4_arrive(q): return rcopy(piece(t,1-y,q),piece(t,1-y,q),y4s.at[q],y4r.at[q],beside)
    far=(1-x)*2+c
    def x_copy(yy,q): return rcopy(piece(t,yy,q),piece(t,yy,q),xs.at[yy*4+q],xr.at[yy*4+q],across)
    def x_arrive(yy,q): return rcopy(piece(far,yy,q),piece(far,yy,q),xs.at[yy*4+q],xr.at[yy*4+q],across)
    def c_copy(yy,q): return rcopy(piece(t,yy,q),piece(t,yy,q),cs.at[yy*4+q],cr.at[yy*4+q],core)
    def c_arrive(yy,q): return rcopy(piece(x*2+1-c,yy,q),piece(x*2+1-c,yy,q),cs.at[yy*4+q],cr.at[yy*4+q],core)
    def f_copy(yy,q): return rcopy(piece(far,yy,q),piece(far,yy,q),fs.at[yy*4+q],fr.at[yy*4+q],core)
    def f_arrive(yy,q):
        r=piece((1-x)*2+1-c,yy,q)
        return rcopy(r,r,fs.at[yy*4+q],fr.at[yy*4+q],core)
    for k in (1,3,2): z3(k).start()
    y4(z).start(); x_copy(y,z).start(); c_copy(y,z).start()
    def passed_on(k):
        q=(z-k+4)%4
        if k:
            z3_arrive(k).wait_recv()
            y4(q).start(); x_copy(y,q).start(); c_copy(y,q).start()
        y4_arrive(q).wait_recv()
        x_copy(1-y,q).start(); c_copy(1-y,q).start()
    for k in (0,1,3,2): passed_on(k)
    loop(lambda k: d_arrive(k).wait_recv(),1,8)
    acc=vd[0]
    for i in range(1,8): acc=acc+vd[i]
    vo_ref[t]=acc
    loop(lambda k: t2(k).start(),1,4)
    for k in (0,1,3,2):
        q=(z-k+4)%4
        for yy in (y,1-y):
            x_arrive(yy,q).wait_recv(); f_copy(yy,q).start()
    def drain(q):
        for yy in range(2):
            c_arrive(yy,q).wait_recv(); f_arrive(yy,q).wait_recv()
            x_copy(yy,q).wait_send(); c_copy(yy,q).wait_send(); f_copy(yy,q).wait_send()
        y4(q).wait_send()
        y1(q).wait_send()
    loop(drain,0,4)
    def sent(k):
        t2_arrive(k).wait_recv()
        z2(k).wait_send(); z3(k).wait_send(); t1(k).wait_send(); t2(k).wait_send()
    loop(sent,1,4)
    loop(lambda k: d_copy(k).wait_send(),1,8)
    for p in range(2):
        for i in range(2):
            e_arrive(i,p).wait_recv(); e_copy(i,p).wait_send()

def last_sums(own,mine,over,v):
    DS=pltpu.SemaphoreType.DMA
    vm=pl.BlockSpec(memory_space=pltpu.VMEM)
    V=pltpu.VMEM
    S=jax.ShapeDtypeStruct
    rows=(3,v.shape[1])
    early,late,total=pl.pallas_call(last_sums_kernel,out_shape=[S((24,288,128),bf),S((4,24,144,128),bf),S((4,)+rows,f32)],in_specs=[vm]*4,out_specs=[vm]*3,
        scratch_shapes=[V((4,3,144,128),bf)]*3+[V((4,)+rows,f32),V((8,)+rows,f32)]+[DS((4,))]*8+[DS((8,))]*6+[DS((2,2))]*2+[DS((4,))]*2+[DS((8,))]*2+[DS((4,))]*2,
        cost_estimate=pl.CostEstimate(flops=10**7,bytes_accessed=150*10**6,transcendentals=0),
        compiler_params=pltpu.CompilerParams(has_side_effects=True,vmem_limit_bytes=60<<20),name="last_gradient_sums")(own.reshape(24,144,128),mine,over,v.reshape((4,)+rows))
    return early,late.reshape(48,288,128),total.reshape(v.shape)


H = 12
NGRP = 16
STEP = 10
EPS_NORM = 1e-06
BETA_ONE = 0.5
BETA_TWO = 0.5
ADAM_EPS = 1e-08
RATE_BLOCK = 0.3
RATE_VECTOR = 0.2
NEG_RAW = -8.0e9
HEAD = 64
SCALE = 1.0 / math.sqrt(HEAD)
EXP2 = SCALE * math.log2(math.e)
NN = (((1,), (0,)), ((), ()))
NT = (((1,), (1,)), ((), ()))
TN = (((0,), (0,)), ((), ()))


def mm(a, b, dims=NN):
    return lax.dot_general(a, b, dims, preferred_element_type=f32)


def column_sum(v):
    return jnp.sum(v, axis=0, keepdims=True)


def vmem_spec():
    return pl.BlockSpec(memory_space=pltpu.VMEM)


def smem_spec():
    return pl.BlockSpec(memory_space=pltpu.SMEM)


def any_spec():
    return pl.BlockSpec(memory_space=pl.ANY)


def params(mib=60):
    return pltpu.CompilerParams(vmem_limit_bytes=mib << 20)


def pack(block, odd):
    half = block.shape[0] // 2
    left, right = block[:, :64], block[:, 128:]
    even_tail = jnp.concatenate([right[:half], right[half:]], axis=1)
    odd_tail = jnp.concatenate([left[half:], left[:half]], axis=1)
    return jnp.where(odd, block[:, 64:], block[:, :128]), jnp.where(odd, odd_tail, even_tail)


def unpack(top, tail, odd):
    first, second = tail[:, :64], tail[:, 64:]
    even = jnp.concatenate([top, jnp.concatenate([first, second], axis=0)], axis=1)
    return jnp.where(odd, jnp.concatenate([jnp.concatenate([second, first], axis=0), top], axis=1), even)


def turn(v):
    return jnp.concatenate([v[:, 64:], v[:, :64]], axis=1)


def group_of(n):
    return 4 if n % 4 == 0 else 3 if n % 3 == 0 else 1


def pack_kernel(odd_ref, m_ref, p_ref, s_ref):
    g = m_ref.shape[0]
    for b in range(g):
        m = m_ref[b]
        top, tail = pack(m, odd_ref[pl.program_id(0) * g + b] == 1)
        p_ref[b, :192] = top.astype(bf)
        p_ref[b, 192:] = tail.astype(bf)
        s_ref[b] = jnp.full((8, 128), jnp.sum(m * m), f32)


def pack_master(odd, master):
    n = master.shape[0]
    g = group_of(n)
    at = lambda i, s: (i, 0, 0)
    spec = pltpu.PrefetchScalarGridSpec(
        num_scalar_prefetch=1,
        grid=(n // g,),
        in_specs=[pl.BlockSpec((g, 192, 192), at)],
        out_specs=[pl.BlockSpec((g, 288, 128), at), pl.BlockSpec((g, 8, 128), at)],
    )
    return pl.pallas_call(
        pack_kernel,
        grid_spec=spec,
        out_shape=[jax.ShapeDtypeStruct((n, 288, 128), bf), jax.ShapeDtypeStruct((n, 8, 128), f32)],
        compiler_params=params(),
        name="pack_master",
    )(odd, master)


def qkv_kernel(src_ref, cnt_ref, at_ref, x0, x1, x2, x3, blk_ref, gain_ref, shift_ref, bq_ref, bv_ref, a_ref, q_ref, qt_ref, k_ref, kt_ref, v_ref, vt_ref, w_ref, st_ref, buf, sems):
    i = pl.program_id(0)

    @pl.when(i == 0)
    def _():
        copies = [pltpu.make_async_copy(blk_ref.at[at_ref[j]], buf.at[j], sems.at[j]) for j in range(12)]
        for copy in copies:
            copy.start()
        odd = at_ref[12] == 1
        for r in range(4):
            parts = []
            for c in range(3):
                copies[r * 3 + c].wait()
                p = buf[r * 3 + c].astype(f32)
                parts.append(unpack(p[:192], p[192:], odd))
            w_ref[r * 192 : (r + 1) * 192, :] = jnp.concatenate(parts, axis=1).astype(bf)

    x = jnp.concatenate([r[...] for r in (x0, x1, x2, x3)], axis=0).astype(f32)
    mean = jnp.mean(x, axis=-1, keepdims=True)
    cen = x - mean
    inv_std = lax.rsqrt(jnp.mean(cen * cen, axis=-1, keepdims=True) + EPS_NORM)
    a = (cen * inv_std * gain_ref[...] + shift_ref[...]).astype(bf)
    a_ref[...] = a
    qkv = mm(a, w_ref[...])
    q = (qkv[:, :192] + bq_ref[...]).astype(bf).astype(f32)
    k = qkv[:, 192:384].astype(bf).astype(f32)
    v = (qkv[:, 384:] + bv_ref[...]).astype(bf).astype(f32)
    row = lax.broadcasted_iota(jnp.int32, (128, 64), 0)
    lane = lax.broadcasted_iota(jnp.int32, (512, 64), 1)
    masked = jnp.concatenate(
        [jnp.where(row < cnt_ref[4 * i + b], 0.0, NEG_RAW) for b in range(4)], axis=0
    )
    ones = jnp.where(lane < 4, 1.0, 0.0)
    k_tail = jnp.where(lane == 0, masked, ones)
    v_tail = jnp.where(lane < 3, 1.0, 0.0)
    zero = jnp.zeros((512, 64), f32)
    sub = lax.broadcasted_iota(jnp.int32, (64, 512), 0)
    t_tail = jnp.where(sub < 1, 1.0, 0.0)
    qt, kt, vt = q.T, k.T, v.T
    longest = lambda a: jnp.max(jnp.concatenate([column_sum(a[h * 64 : (h + 1) * 64] ** 2) for h in range(3)], axis=0))
    st_ref[0] = jnp.where(lax.broadcasted_iota(jnp.int32, (8, 128), 0) == 0, longest(qt), longest(kt))
    for h in range(3):
        s = slice(h * 64, (h + 1) * 64)
        q_ref[h] = jnp.concatenate([q[:, s], zero], axis=1).astype(bf)
        k_ref[h] = jnp.concatenate([k[:, s], k_tail], axis=1).astype(bf)
        v_ref[h] = jnp.concatenate([v[:, s], v_tail], axis=1).astype(bf)
        qt_ref[h] = jnp.concatenate([qt[s], t_tail], axis=0).astype(bf)
        kt_ref[h] = kt[s].astype(bf)
        vt_ref[h] = jnp.concatenate([vt[s], t_tail[:16]], axis=0).astype(bf)


def qkv_forward(src, cnt, own_at, tokens, blocks, gain, shift, bq, bv):
    n = tokens.shape[0]
    rows = [pl.BlockSpec((128, 768), lambda i, s, c, o, k=k: (s[4 * i + k], 0)) for k in range(4)]
    row = lambda i, s, c, o: (0, 0)
    spec = pltpu.PrefetchScalarGridSpec(
        num_scalar_prefetch=3,
        grid=(n // 512,),
        in_specs=rows
        + [any_spec(), pl.BlockSpec((1, 768), row), pl.BlockSpec((1, 768), row), pl.BlockSpec((1, 192), row), pl.BlockSpec((1, 192), row)],
        out_specs=[
            pl.BlockSpec((512, 768), lambda i, s, c, o: (i, 0)),
            pl.BlockSpec((3, 512, 128), lambda i, s, c, o: (0, i, 0)),
            pl.BlockSpec((3, 128, 512), lambda i, s, c, o: (0, 0, i)),
            pl.BlockSpec((3, 512, 128), lambda i, s, c, o: (0, i, 0)),
            pl.BlockSpec((3, 64, 512), lambda i, s, c, o: (0, 0, i)),
            pl.BlockSpec((3, 512, 128), lambda i, s, c, o: (0, i, 0)),
            pl.BlockSpec((3, 80, 512), lambda i, s, c, o: (0, 0, i)),
            pl.BlockSpec((768, 576), row),
            pl.BlockSpec((1, 8, 128), lambda i, s, c, o: (i, 0, 0)),
        ],
        scratch_shapes=[pltpu.VMEM((12, 288, 128), bf), pltpu.SemaphoreType.DMA((12,))],
    )
    shapes = [(n, 768), (3, n, 128), (3, 128, n), (3, n, 128), (3, 64, n), (3, n, 128), (3, 80, n), (768, 576)]
    return pl.pallas_call(
        qkv_kernel,
        grid_spec=spec,
        out_shape=[jax.ShapeDtypeStruct(s, bf) for s in shapes] + [jax.ShapeDtypeStruct((n // 512, 8, 128), f32)],
        compiler_params=params(),
        name="norm_and_qkv",
    )(src, cnt, own_at, tokens, tokens, tokens, tokens, blocks, gain, shift, bq, bv)


def split3(v):
    a = v.astype(bf).astype(f32)
    b = (v - a).astype(bf).astype(f32)
    return a, b, v - a - b


def in_steps(units, sizes, body, carry):
    at = 0
    for size in sizes:
        count = (units - at) // size
        carry = lax.fori_loop(0, count, lambda i, c, at=at, size=size: body(at + i * size, size, c), carry)
        at = at + count * size
    return carry


def attend_kernel(bq, n_ref, k_ref, qt_ref, vt_ref, ot_ref, qb_ref, p_ref, rt_ref):
    live = n_ref[0]
    qi = pl.program_id(1)
    pairs = (live + 1) // 2

    def finish(top, acc):
        total = acc[64:65]
        ot_ref[0] = acc[:64] / total
        rt_ref[0] = 1.0 / total
        a, b, c = split3((top + jnp.log2(total)) * (-1.0 / EXP2))
        row = lax.broadcasted_iota(jnp.int32, (64, bq), 0)
        tail = jnp.where(row == 0, 1.0, jnp.where(row == 1, a, jnp.where(row == 2, b, jnp.where(row == 3, c, 0.0))))
        qb_ref[0, :64] = qt_ref[0, :64]
        qb_ref[0, 64:] = tail.astype(bf)

    def keys(u, size):
        return pl.ds(pl.multiple_of(u * 256, 256), size * 256)

    @pl.when(jnp.logical_and(qi * bq < live * 128, n_ref[1] == 1))
    def _():
        qt = qt_ref[0]

        def body(u, size, acc):
            step = min(size, 2)
            for part in range(0, size, step):
                at = keys(u + part, step)
                p = jnp.exp2(mm(k_ref[0, at, :], qt) * EXP2).astype(bf)
                p_ref[0, at, :] = p
                acc = acc + mm(vt_ref[0, :, at], p)
            return acc

        finish(0.0, in_steps(pairs, (8, 4, 2, 1), body, jnp.zeros((80, bq), f32)))

    @pl.when(jnp.logical_and(qi * bq < live * 128, n_ref[1] == 0))
    def _():
        qt = qt_ref[0]

        def body(u, size, carry):
            top, acc = carry
            s = mm(k_ref[0, keys(u, size), :], qt) * EXP2
            new = jnp.maximum(top, jnp.max(s, axis=0, keepdims=True))
            p = jnp.exp2(s - new).astype(bf)
            return new, acc * jnp.exp2(top - new) + mm(vt_ref[0, :, keys(u, size)], p)

        finish(*in_steps(pairs, (4, 2, 1), body, (jnp.full((1, bq), -3e38, f32), jnp.zeros((80, bq), f32))))


def attend(live, k, qt, vt, bq=1024):
    n = k.shape[1]
    spec = pltpu.PrefetchScalarGridSpec(
        num_scalar_prefetch=1,
        grid=(3, n // bq),
        in_specs=[
            pl.BlockSpec((1, n, 128), lambda h, i, s: (h, 0, 0)),
            pl.BlockSpec((1, 128, bq), lambda h, i, s: (h, 0, i)),
            pl.BlockSpec((1, 80, n), lambda h, i, s: (h, 0, 0)),
        ],
        out_specs=[
            pl.BlockSpec((1, 64, bq), lambda h, i, s: (h, 0, i)),
            pl.BlockSpec((1, 128, bq), lambda h, i, s: (h, 0, i)),
            pl.BlockSpec((1, n, bq), lambda h, i, s: (h, 0, i)),
            pl.BlockSpec((1, 1, bq), lambda h, i, s: (h, 0, i)),
        ],
    )
    return pl.pallas_call(
        functools.partial(attend_kernel, bq),
        grid_spec=spec,
        out_shape=[
            jax.ShapeDtypeStruct((3, 64, n), f32),
            jax.ShapeDtypeStruct((3, 128, n), bf),
            jax.ShapeDtypeStruct((3, n, n), bf),
            jax.ShapeDtypeStruct((3, 1, n), f32),
        ],
        compiler_params=params(),
        name="attention_forward",
    )(live, k, qt, vt)


def spread_kernel(src_ref, n_ref, t_ref, ot_ref, *o_refs):
    live, t, tiles = n_ref[0], t_ref[0], len(o_refs)
    per = o_refs[0].shape[1] // 128

    def step(b, _):
        g = src_ref[b]
        lanes = pl.ds(pl.multiple_of(b * 128, 128), 128)
        to = pl.ds(pl.multiple_of((g % per) * 128, 128), 128)
        for k in range(tiles):
            here = (g // per - t + tiles) % tiles == k

            @pl.when(jnp.logical_and(here, b < live))
            def _():
                for h in range(3):
                    o_refs[k][h * 64 : (h + 1) * 64, to] = ot_ref[h, :, lanes].astype(bf)

            @pl.when(jnp.logical_and(here, b >= live))
            def _():
                o_refs[k][:, to] = jnp.zeros((192, 128), bf)

        return 0

    lax.fori_loop(0, ot_ref.shape[2] // 128, step, 0)


def spread(src, live, tile, ot, tiles):
    n = ot.shape[2]
    return pl.pallas_call(
        spread_kernel,
        in_specs=[smem_spec()] * 3 + [vmem_spec()],
        out_specs=[vmem_spec()] * tiles,
        out_shape=[jax.ShapeDtypeStruct((192, n // tiles), bf)] * tiles,
        compiler_params=params(),
        name="spread_attended",
    )(src, live, tile, ot)


def collect_kernel(src_ref, n_ref, t_ref, ot_ref, rt_ref, *refs):
    g_refs, (dt_ref, d_ref) = refs[:-2], refs[-2:]
    live, t, tiles = n_ref[0], t_ref[0], len(g_refs)
    mild = n_ref[1] == 1
    per = g_refs[0].shape[1] // 128
    row = lax.broadcasted_iota(jnp.int32, (64, 128), 0)

    def step(b, _):
        g = src_ref[b]
        to = pl.ds(pl.multiple_of(b * 128, 128), 128)
        lanes = pl.ds(pl.multiple_of((g % per) * 128, 128), 128)
        for k in range(tiles):

            @pl.when(jnp.logical_and((t - g // per + tiles) % tiles == k, b < live))
            def _():
                for h in range(3):
                    scale = jnp.where(mild, rt_ref[h, :, to], 1.0)
                    d = (g_refs[k][h * 64 : (h + 1) * 64, lanes].astype(f32) * scale).astype(bf).astype(f32)
                    x, y, z = split3(-jnp.sum(d * ot_ref[h, :, to], axis=0, keepdims=True))
                    tail = jnp.where(row == 0, x, jnp.where(row == 1, y, jnp.where(row == 2, z, 0.0)))
                    dt_ref[h, :, to] = jnp.concatenate([d, tail], axis=0).astype(bf)
                    d_ref[h, to, :] = jnp.concatenate([d, jnp.zeros_like(d)], axis=0).T.astype(bf)

        @pl.when(b >= live)
        def _():
            dt_ref[:, :, to] = jnp.zeros((3, 128, 128), bf)
            d_ref[:, to, :] = jnp.zeros((3, 128, 128), bf)

        return 0

    lax.fori_loop(0, ot_ref.shape[2] // 128, step, 0)


def collect(src, live, tile, grads, ot, rt):
    n = ot.shape[2]
    return pl.pallas_call(
        collect_kernel,
        in_specs=[smem_spec()] * 3 + [vmem_spec()] * (2 + len(grads)),
        out_specs=[vmem_spec()] * 2,
        out_shape=[jax.ShapeDtypeStruct((3, 128, n), bf), jax.ShapeDtypeStruct((3, n, 128), bf)],
        compiler_params=params(),
        name="collect_attended_grad",
    )(src, live, tile, ot, rt, *grads)


def attend_back_kernel(bk, n_ref, p_ref, k_ref, kt_ref, v_ref, qb_ref, q_ref, dt_ref, d_ref, dq_ref, dk_ref, dv_ref):
    live = n_ref[0]
    j = pl.program_id(1)

    @pl.when(j == 0)
    def _():
        dq_ref[...] = jnp.zeros_like(dq_ref)

    def lanes(u):
        return pl.ds(pl.multiple_of(u * 256, 256), 256)

    pairs = (live + 1) // 2

    def over_queries(rows, sizes, body):
        zero = jnp.zeros((rows, 128), f32)
        dk, dv = in_steps(pairs, sizes, body, (zero, zero))
        dk_ref[0, :rows] = (dk * SCALE).astype(bf)
        dv_ref[0, :rows] = dv.astype(bf)

    def with_kept(rows):
        k, v, kt = k_ref[0, :rows], v_ref[0, :rows], kt_ref[0, :, :rows]

        def body(u, size, carry):
            dk, dv = carry
            dp = mm(v, dt_ref[0, :, lanes(u)])
            for part in range(size):
                at = lanes(u + part)
                ahead = mm(v, dt_ref[0, :, lanes(u + part + 1)]) if part + 1 < size else None
                p = p_ref[0, :rows, at]
                ds = (p.astype(f32) * dp).astype(bf)
                dv = dv + mm(p, d_ref[0, at, :])
                dk = dk + mm(ds, q_ref[0, at, :])
                dq_ref[0, :, at] += mm(kt, ds)
                dp = dp if ahead is None else ahead
            return dk, dv

        over_queries(rows, (8, 4, 2, 1), body)

    @pl.when(jnp.logical_and(n_ref[1] == 1, 2 * j + 2 <= pairs))
    def _():
        with_kept(bk)

    @pl.when(jnp.logical_and(n_ref[1] == 1, 2 * j + 1 == pairs))
    def _():
        dk_ref[0, bk // 2 :] = jnp.zeros((bk // 2, 128), bf)
        dv_ref[0, bk // 2 :] = jnp.zeros((bk // 2, 128), bf)
        with_kept(bk // 2)

    @pl.when(jnp.logical_and(n_ref[1] == 0, j * bk < live * 128))
    def _():
        k, v, kt = k_ref[0], v_ref[0], kt_ref[0]

        def body(u, size, carry):
            dk, dv = carry
            for part in range(size):
                at = lanes(u + part)
                p = jnp.exp2(mm(k, qb_ref[0, :, at]) * EXP2)
                ds = (p * mm(v, dt_ref[0, :, at])).astype(bf)
                dv = dv + mm(p.astype(bf), d_ref[0, at, :])
                dk = dk + mm(ds, q_ref[0, at, :])
                dq_ref[0, :, at] += mm(kt, ds)
            return dk, dv

        over_queries(bk, (4, 1), body)


def attend_back(first, heads, live, p, k, kt, v, qb, q, dt, d, bk=512):
    n = k.shape[1]
    whole_t = lambda h, j, s: (first + h, 0, 0)
    rows = lambda h, j, s: (first + h, j, 0)
    spec = pltpu.PrefetchScalarGridSpec(
        num_scalar_prefetch=1,
        grid=(heads, n // bk),
        in_specs=[
            pl.BlockSpec((1, bk, n), rows),
            pl.BlockSpec((1, bk, 128), rows),
            pl.BlockSpec((1, 64, bk), lambda h, j, s: (first + h, 0, j)),
            pl.BlockSpec((1, bk, 128), rows),
            pl.BlockSpec((1, 128, n), whole_t),
            pl.BlockSpec((1, n, 128), whole_t),
            pl.BlockSpec((1, 128, n), whole_t),
            pl.BlockSpec((1, n, 128), whole_t),
        ],
        out_specs=[
            pl.BlockSpec((1, 64, n), lambda h, j, s: (h, 0, 0)),
            pl.BlockSpec((1, bk, 128), lambda h, j, s: (h, j, 0)),
            pl.BlockSpec((1, bk, 128), lambda h, j, s: (h, j, 0)),
        ],
    )
    S = jax.ShapeDtypeStruct
    return pl.pallas_call(
        functools.partial(attend_back_kernel, bk),
        grid_spec=spec,
        out_shape=[S((heads, 64, n), f32), S((heads, n, 128), bf), S((heads, n, 128), bf)],
        cost_estimate=pl.CostEstimate(flops=heads * 4 * 10**10, bytes_accessed=heads * 50 * 10**6, transcendentals=0),
        compiler_params=params(),
        name="attention_backward",
    )(live, p, k, kt, v, qb, q, dt, d)


def qkv_back_kernel(given, src_ref, n_ref, odd_ref, x0, x1, x2, x3, gain_ref, a_ref, w_ref, *refs):
    grads, (ga_ref, gz_ref, gw_ref, gb_ref, vs_ref, acc, sums, rows, sems) = refs[:given], refs[given:]
    dqs, dks, dvs = [[(r, h) for r in grads[j::3] for h in range(r.shape[0])] for j in range(3)]
    early = ga_ref.shape[1] // 128
    i = pl.program_id(0)
    live = n_ref[0]

    @pl.when(i == 0)
    def _():
        acc[...] = jnp.zeros_like(acc)
        sums[...] = jnp.zeros_like(sums)
        vs_ref[...] = jnp.zeros_like(vs_ref)

    @pl.when(4 * i < live)
    def _():
        dq = jnp.concatenate([r[h] for r, h in dqs], axis=0).T * SCALE
        g = jnp.concatenate([dq] + [r[h][:, :64].astype(f32) for r, h in dks + dvs], axis=1).astype(bf)
        acc[...] += mm(a_ref[...], g, TN)
        sums[...] += jnp.broadcast_to(column_sum(g.astype(f32)), sums.shape)
        g1 = mm(g, w_ref[...], NT)
        rows[...] = g1.astype(bf)
        x = jnp.concatenate([r[...] for r in (x0, x1, x2, x3)], axis=0).astype(f32)
        cen = x - jnp.mean(x, axis=-1, keepdims=True)
        normed = cen * lax.rsqrt(jnp.mean(cen * cen, axis=-1, keepdims=True) + EPS_NORM)
        vs_ref[0:1, :] += column_sum(g1 * normed)
        vs_ref[1:2, :] += column_sum(g1)

    @pl.when(4 * i >= live)
    def _():
        rows[...] = jnp.zeros_like(rows)

    per = early + gz_ref.shape[1] // 128
    for b in range(4):
        block, at = rows.at[pl.ds(b * 128, 128)], src_ref[4 * i + b]
        t, j = at // per, at % per

        @pl.when(j < early)
        def _():
            pltpu.make_async_copy(block, ga_ref.at[t, pl.ds(pl.multiple_of(j * 128, 128), 128)], sems.at[b]).start()

        @pl.when(j >= early)
        def _():
            pltpu.make_async_copy(block, gz_ref.at[t, pl.ds(pl.multiple_of((j - early) * 128, 128), 128)], sems.at[b]).start()

    for b in range(4):
        pltpu.make_async_copy(rows.at[pl.ds(b * 128, 128)], ga_ref.at[0, pl.ds(0, 128)], sems.at[b]).wait()

    @pl.when(i == pl.num_programs(0) - 1)
    def _():
        for r in range(4):
            for c in range(3):
                top, tail = pack(acc[r * 192 : (r + 1) * 192, c * 192 : (c + 1) * 192], odd_ref[0] == 1)
                gw_ref[r * 3 + c, :192] = top.astype(bf)
                gw_ref[r * 3 + c, 192:] = tail.astype(bf)
        gb_ref[...] = sums[...]


def qkv_backward(src, live, odd, tokens, gain, a, w, grads, tiles, early):
    n = a.shape[0]
    per = n // tiles
    fixed = lambda i, s, c, o: (0, 0)
    row = lambda i, s, c, o: (0, i, 0)
    spec = pltpu.PrefetchScalarGridSpec(
        num_scalar_prefetch=3,
        grid=(n // 512,),
        in_specs=[pl.BlockSpec((128, 768), lambda i, s, c, o, k=k: (s[4 * i + k], 0)) for k in range(4)]
        + [pl.BlockSpec((1, 768), fixed), pl.BlockSpec((512, 768), lambda i, s, c, o: (i, 0)), pl.BlockSpec((768, 576), fixed)]
        + [
            pl.BlockSpec((g.shape[0], 64, 512), lambda i, s, c, o: (0, 0, i)) if g.shape[1] == 64 else pl.BlockSpec((g.shape[0], 512, 128), row)
            for g in grads
        ],
        out_specs=[any_spec(), any_spec(), pl.BlockSpec((12, 288, 128), lambda i, s, c, o: (0, 0, 0)), pl.BlockSpec((8, 576), fixed), pl.BlockSpec((8, 768), fixed)],
        scratch_shapes=[pltpu.VMEM((768, 576), f32), pltpu.VMEM((8, 576), f32), pltpu.VMEM((512, 768), bf), pltpu.SemaphoreType.DMA((4,))],
    )
    S = jax.ShapeDtypeStruct
    return pl.pallas_call(
        functools.partial(qkv_back_kernel, len(grads)),
        grid_spec=spec,
        out_shape=[S((tiles, early, 768), bf), S((tiles, per - early, 768), bf), S((12, 288, 128), bf), S((8, 576), f32), S((8, 768), f32)],
        cost_estimate=pl.CostEstimate(flops=3 * 10**10, bytes_accessed=40 * 10**6, transcendentals=0),
        compiler_params=params(),
        name="qkv_backward",
    )(src, live, odd, tokens, tokens, tokens, tokens, gain, a, w, *grads)


def gelu_parts(z):
    cdf = 0.5 + 0.5 * lax.erf(z * math.sqrt(0.5))
    return z * cdf, cdf + z * (jnp.exp2(z * z * (-0.5 * math.log2(math.e))) * (1.0 / math.sqrt(2.0 * math.pi)))


def middle_kernel(inv_ref, cnt_ref, t_ref, blk_ref, o0, o1, o2, o3, x_ref, c_ref, vp_ref, bu_ref, y_ref, gr_ref, g0, g1, g2_ref, g3,
                  u_s, gz_s, a2_s, gm_s, gb_s, o_s, vs_ref, us_ref, w_out, w_up, w_down, tails, tsem, isem):
    i = pl.program_id(0)
    rows = x_ref.shape[0]
    r0 = i * rows
    kinds = ((w_out, 48, 2, 4), (w_up, 64, 8, 4), (w_down, 128, 2, 16))

    @pl.when(i == 0)
    def _():
        vs_ref[...] = jnp.zeros_like(vs_ref)
        us_ref[...] = jnp.zeros_like(us_ref)

        def pair(w, first, pairs):
            def copies(j):
                r = pl.multiple_of((j // pairs) * 192, 64)
                col = pl.multiple_of((j % pairs) * 384, 128)
                out = []
                for b, off in ((0, 0), (1, 256)):
                    at = first + 2 * j + b
                    slot = inv_ref[at]
                    out.append(pltpu.make_async_copy(blk_ref.at[slot, pl.ds(0, 192)], w.at[pl.ds(r, 192), pl.ds(col + off, 128)], tsem.at[at - 48]))
                    out.append(pltpu.make_async_copy(blk_ref.at[slot, pl.ds(192, 96)], tails.at[at - 48], isem.at[at - 48]))
                return out, r, col

            def start(j, _):
                for copy in copies(j)[0]:
                    copy.start()
                return 0

            def join(j, _):
                got, r, col = copies(j)
                for copy in got:
                    copy.wait()
                even = tails[first + 2 * j - 48].astype(f32)
                odd = tails[first + 2 * j - 47].astype(f32)
                lane = lax.broadcasted_iota(jnp.int32, even.shape, 1) < 64
                w[pl.ds(r, 96), pl.ds(col + 128, 128)] = jnp.where(lane, even, odd).astype(bf)
                w[pl.ds(r + 96, 96), pl.ds(col + 128, 128)] = turn(jnp.where(lane, odd, even)).astype(bf)
                return 0

            return start, join

        todo = [(pair(w, first, pairs), pairs * high) for w, first, pairs, high in kinds]
        for (start, _), n in todo:
            lax.fori_loop(0, n, start, 0)

        for (_, join), n in todo:
            lax.fori_loop(0, n, join, 0)

    vp = vp_ref[...]
    row = r0 + lax.broadcasted_iota(jnp.int32, (rows, 1), 0)
    live = jnp.where(row < cnt_ref[0], 1.0, 0.0)
    t = t_ref[0]
    for k, ref in enumerate((o0, o1, o2, o3)):
        o_s[pl.ds(pl.multiple_of(((t - k + 4) % 4) * 192, 64), 192), :] = ref[...]
    o_t = o_s[...]
    res = x_ref[...].astype(f32) + mm(o_t, w_out[...], TN) + vp[6:7]
    cen = res - jnp.mean(res, axis=-1, keepdims=True)
    inv_std = lax.rsqrt(jnp.mean(cen * cen, axis=-1, keepdims=True) + EPS_NORM)
    normed = cen * inv_std
    a2 = (normed * vp[2:3] + vp[3:4]).astype(bf)
    gy = c_ref[...].astype(f32) * live
    gm = gy.astype(bf)
    a2_s[...] = a2
    gm_s[...] = gm
    branch = jnp.zeros((rows, 768), f32)
    g2 = jnp.zeros((rows, 768), f32)
    for j in range(4):
        cols = slice(j * 768, (j + 1) * 768)
        u, slope = gelu_parts(mm(a2, w_up[:, cols]) + bu_ref[:, cols])
        u = u.astype(bf)
        u_s[:, cols] = u
        branch = branch + mm(u, w_down[cols, :])
        gz = (mm(gm, w_down[cols, :], NT) * slope).astype(bf)
        gz_s[:, cols] = gz
        us_ref[:, cols] += jnp.broadcast_to(column_sum(gz.astype(f32)), (8, 768))
        g2 = g2 + mm(gz, w_up[:, cols], NT)
    y_ref[...] = (live * (res + branch + vp[7:8])).astype(bf)
    d2 = g2 * vp[2:3]
    gr = gy + inv_std * (d2 - jnp.mean(d2, axis=-1, keepdims=True) - normed * jnp.mean(d2 * normed, axis=-1, keepdims=True))
    gr_ref[...] = gr
    gb = gr.astype(bf)
    gb_s[...] = gb
    vs_ref[0:1, :] += column_sum(g2 * normed)
    vs_ref[1:2, :] += column_sum(g2)
    vs_ref[2:3, :] += column_sum(gb.astype(f32))
    vs_ref[3:4, :] += column_sum(gm.astype(f32))
    for k, ref in enumerate((g0, g1, g2_ref, g3)):
        ref[...] = mm(w_out[pl.ds(pl.multiple_of(((t + k) % 4) * 192, 64), 192), :], gb, NT).astype(bf)


def weight_grad_kernel(outs, pos_ref, o_in, gb_in, a2_in, gz_in, u_in, gm_in, *refs):
    s_refs, (o_s, gb_s, a2_s, gz_s, u_s, gm_s, ring, zero, lsem, osem, zsem) = refs[:outs], refs[outs:]
    each = s_refs[0].shape[0]

    def to_slot(block, at, sem):
        for o in range(outs):

            @pl.when(at // each == o)
            def _():
                pltpu.make_async_copy(block, s_refs[o].at[at % each], sem).start()

    def landed(block, sem):
        pltpu.make_async_copy(block, s_refs[0].at[0], sem).wait()

    loads = [pltpu.make_async_copy(a, b, lsem.at[j]) for j, (a, b) in enumerate(
        ((o_in, o_s), (gb_in, gb_s), (a2_in, a2_s), (gz_in, gz_s), (gm_in, gm_s), (u_in, u_s)))]
    for load in loads:
        load.start()
    zero[...] = jnp.zeros_like(zero)

    def clear(j, _):
        to_slot(zero, pos_ref[j], zsem.at[j])
        return 0

    lax.fori_loop(0, 48, clear, 0)
    def send(n, g, first, pairs, high, low):
        half = (n % 2) * 8

        def put(r, b):
            return first + (high + r) * 2 * pairs + 2 * low + b

        for r in range(4):
            part = g[r * 192 : (r + 1) * 192]
            mid = part[:, 128:256]
            upper, lower = mid[:96], turn(mid[96:])
            lane = lax.broadcasted_iota(jnp.int32, upper.shape, 1) < 64
            for b, top, tail in ((0, part[:, :128], jnp.where(lane, upper, lower)), (1, part[:, 256:], jnp.where(lane, lower, upper))):
                k = half + 2 * r + b

                @pl.when(n >= 2)
                def _():
                    landed(ring.at[k], osem.at[k])

                ring[k, :192] = top.astype(bf)
                ring[k, 192:] = tail.astype(bf)
                to_slot(ring.at[k], pos_ref[put(r, b)], osem.at[k])

    def lanes(j):
        return pl.ds(pl.multiple_of(j * 384, 128), 384)

    def grad_out(n, _):
        send(n, mm(o_s[...], gb_s[:, lanes(n)]), 48, 2, 0, n)
        return 0

    def grad_up(n, _):
        send(n, mm(a2_s[...], gz_s[:, lanes(n)], TN), 64, 8, 0, n)
        return 0

    def grad_down(n, _):
        high = n // 2
        send(n, mm(u_s[:, pl.ds(pl.multiple_of(high * 768, 128), 768)], gm_s[:, lanes(n % 2)], TN), 128, 2, high * 4, n % 2)
        return 0

    def drain():
        for k in range(16):
            landed(ring.at[k], osem.at[k])

    for f, n, first in ((grad_out, 2, 0), (grad_up, 8, 2), (grad_down, 8, 4)):
        loads[first].wait()
        loads[first + 1].wait()
        lax.fori_loop(0, n, f, 0)
        drain()

    def cleared(j, _):
        landed(zero, zsem.at[j])
        return 0

    lax.fori_loop(0, 48, cleared, 0)


def middle(inv, count, tile, blocks, o_parts, tokens, cotangent, vec_params, bias_up, rows=256):
    n, width = tokens.shape
    hidden = bias_up.shape[1]
    row = lambda i, s, c, t: (i, 0)
    fixed = lambda i, s, c, t: (0, 0)
    col = lambda i, s, c, t: (0, i)
    V, DS = pltpu.VMEM, pltpu.SemaphoreType.DMA
    narrow, wide, part = pl.BlockSpec((rows, width), row), pl.BlockSpec((rows, hidden), row), pl.BlockSpec((192, rows), col)
    spec = pltpu.PrefetchScalarGridSpec(
        num_scalar_prefetch=3,
        grid=(n // rows,),
        in_specs=[any_spec()] + [part] * 4 + [narrow, narrow, pl.BlockSpec((12, width), fixed), pl.BlockSpec((1, hidden), fixed)],
        out_specs=[narrow, narrow] + [part] * 4 + [wide, wide, narrow, narrow, narrow, pl.BlockSpec((width, rows), col),
                   pl.BlockSpec((8, width), fixed), pl.BlockSpec((8, hidden), fixed)],
        scratch_shapes=[V((768, 768), bf), V((768, 3072), bf), V((3072, 768), bf), V((144, 96, 128), bf), DS((144,)), DS((144,))],
    )
    S = jax.ShapeDtypeStruct
    return pl.pallas_call(
        middle_kernel,
        grid_spec=spec,
        out_shape=[S((n, width), bf), S((n, width), f32)] + [S((192, n), bf)] * 4 + [S((n, hidden), bf)] * 2 + [S((n, width), bf)] * 3
        + [S((width, n), bf), S((8, width), f32), S((8, hidden), f32)],
        compiler_params=params(),
        name="projection_and_mlp",
    )(inv, count, tile, blocks, *o_parts, tokens, cotangent, vec_params, bias_up)


def weight_grads_to_slots(pos, outs, block_count, o_t, gb, a2, gz, u, gm):
    V, DS = pltpu.VMEM, pltpu.SemaphoreType.DMA
    arrays = (o_t, gb, a2, gz, u, gm)
    return pl.pallas_call(
        functools.partial(weight_grad_kernel, outs),
        in_specs=[smem_spec()] + [any_spec()] * 6,
        out_specs=[any_spec()] * outs,
        out_shape=[jax.ShapeDtypeStruct((block_count // outs, 288, 128), bf)] * outs,
        scratch_shapes=[V(a.shape, bf) for a in arrays] + [V((16, 288, 128), bf), V((288, 128), bf), DS((6,)), DS((16,)), DS((48,))],
        cost_estimate=pl.CostEstimate(flops=6 * 10**10, bytes_accessed=32 * 10**6, transcendentals=0),
        compiler_params=params(),
        name="mlp_weight_gradients",
    )(pos, *arrays)


def quarters(b0, b1):
    return (b0 * 2 + b1, (1 - b0) * 2 + b1, b0 * 2 + 1 - b1, (1 - b0) * 2 + 1 - b1)


def add_pair_kernel(common, bits_ref, *refs):
    outs = list(refs[16:])
    for p in range(2):
        for side in range(4):
            j = 4 * p + side
            total = (refs[2 * j][...].astype(f32) + refs[2 * j + 1][...].astype(f32)).astype(bf)
            if side == common[p]:
                outs[6][p] = total
            else:
                outs[3 * p + side - (side > common[p])][...] = total


def add_pair(bits, common, keep, came):
    specs = []
    for p in range(2):
        for side in range(4):
            at = lambda i, b, p=p, side=side: (p * 12 + quarters(b[2 * p], b[2 * p + 1])[side] * 3 + i, 0, 0)
            specs += [pl.BlockSpec((4, 288, 128), at)] * 2
    S = jax.ShapeDtypeStruct
    return pl.pallas_call(
        functools.partial(add_pair_kernel, common),
        grid_spec=pltpu.PrefetchScalarGridSpec(
            num_scalar_prefetch=1,
            grid=(3,),
            in_specs=specs,
            out_specs=[pl.BlockSpec((4, 288, 128), lambda i, b: (i, 0, 0))] * 6 + [pl.BlockSpec((2, 4, 288, 128), lambda i, b: (0, i, 0, 0))],
        ),
        out_shape=[S((12, 288, 128), bf)] * 6 + [S((2, 12, 288, 128), bf)],
        compiler_params=params(),
        name="add_gradients_of_cores",
    )(bits, *[keep, came] * 8)


def add_four_kernel(common, bits_ref, *refs):
    outs = refs[7:]
    for p in range(2):
        parts = refs[3 * p : 3 * p + 3]
        for side, q in enumerate(quarters(bits_ref[2 * p], bits_ref[2 * p + 1])):
            for b in range(3):
                total = (sum(r[q * 3 + b].astype(f32) for r in parts) + refs[6][p, q * 3 + b].astype(f32)).astype(bf)
                if side == common[p]:
                    outs[6][p, b] = total
                else:
                    outs[3 * p + side - (side > common[p])][b] = total


def add_four(bits, common, parts):
    S = jax.ShapeDtypeStruct
    return pl.pallas_call(
        functools.partial(add_four_kernel, common),
        in_specs=[smem_spec()] + [vmem_spec()] * 7,
        out_specs=[vmem_spec()] * 7,
        out_shape=[S((3, 288, 128), bf)] * 6 + [S((2, 3, 288, 128), bf)],
        compiler_params=params(),
        name="add_gradients",
    )(bits, *parts)


def add_last_kernel(*refs):
    for p in range(2):
        for b in range(3):
            refs[7][3 * p + b] = (sum(r[b].astype(f32) for r in refs[3 * p : 3 * p + 3]) + refs[6][p, b].astype(f32)).astype(bf)


def add_last(parts):
    return pl.pallas_call(
        add_last_kernel,
        in_specs=[vmem_spec()] * 7,
        out_specs=vmem_spec(),
        out_shape=jax.ShapeDtypeStruct((6, 288, 128), bf),
        compiler_params=params(),
        name="add_last_gradients",
    )(*parts)


def split2(v):
    hi = v.astype(bf)
    return hi, (v - hi.astype(f32)).astype(bf)


def mm3(a, b, dims):
    return mm(a[0], b[0], dims) + (mm(a[0], b[1], dims) + mm(a[1], b[0], dims))


def adam_kernel(odd_ref, from_ref, g_ref, late_ref, m1_ref, m2_ref, l_ref, r_ref, g_out, m1_out, m2_out, u_out, s_out):
    for b in range(g_ref.shape[0]):
        slot = pl.program_id(0) * g_ref.shape[0] + b
        place = from_ref[slot]
        part = jnp.where(place >= 0, late_ref[jnp.maximum(place, 0)].astype(f32), g_ref[b].astype(f32))
        grad = unpack(part[:192], part[192:], odd_ref[slot] == 1)
        left, right = split2(l_ref[b]), split2(r_ref[b])
        low = grad.astype(bf)
        rot = mm3(split2(mm(left[0], low, TN) + mm(left[1], low, TN)), right, NN)
        first = BETA_ONE * m1_ref[b] + (1.0 - BETA_ONE) * rot
        second = BETA_TWO * m2_ref[b] + (1.0 - BETA_TWO) * rot * rot
        upd = (first / (1.0 - BETA_ONE**STEP)) / (jnp.sqrt(second / (1.0 - BETA_TWO**STEP)) + ADAM_EPS)
        upd = mm3(split2(mm3(left, split2(upd), NN)), right, NT)
        g_out[b] = grad
        m1_out[b] = first
        m2_out[b] = second
        u_out[b] = upd
        s_out[b] = jnp.full((8, 128), jnp.sum(upd * upd), f32)


def adam(odd, late_at, grads, late, first, second, left, right):
    n = grads.shape[0]
    g = group_of(n)
    at = lambda i, s, f: (i, 0, 0)
    big = pl.BlockSpec((g, 192, 192), at)
    spec = pltpu.PrefetchScalarGridSpec(
        num_scalar_prefetch=2,
        grid=(n // g,),
        in_specs=[pl.BlockSpec((g, 288, 128), at), pl.BlockSpec(late.shape, lambda i, s, f: (0, 0, 0))] + [big] * 4,
        out_specs=[big] * 4 + [pl.BlockSpec((g, 8, 128), at)],
    )
    return pl.pallas_call(
        adam_kernel,
        grid_spec=spec,
        out_shape=[jax.ShapeDtypeStruct((n, 192, 192), f32)] * 4 + [jax.ShapeDtypeStruct((n, 8, 128), f32)],
        compiler_params=params(),
        name="rotated_adam",
    )(odd, late_at, grads, late, first, second, left, right)


def halving_places(slot, core):
    dp, r = slot // 24, slot % 24
    y, z, far, x, s = dp % 2, dp // 2 % 2, dp // 4, r % 6 // 3, r % 3
    portion = r % 12 // 6
    inside = jnp.where(portion == 0, x * 8 + y * 4 + z * 2 + far, y * 8 + z * 4 + x * 2 + far)
    return jnp.where(r // 12 == core, 0, 96) + portion * 48 + inside * 3 + s


def norm_forward(row_data, gain_vec, shift_vec):
    row_mean = jnp.mean(row_data, axis=-1, keepdims=True)
    centred = row_data - row_mean
    inv_std = lax.rsqrt(jnp.mean(centred * centred, axis=-1, keepdims=True) + EPS_NORM)
    normed = centred * inv_std
    return (normed * gain_vec + shift_vec, normed, inv_std)


def norm_back(grad_out, normed, inv_std, gain_vec):
    grad_normed = grad_out * gain_vec
    return inv_std * (
        grad_normed
        - jnp.mean(grad_normed, axis=-1, keepdims=True)
        - normed * jnp.mean(grad_normed * normed, axis=-1, keepdims=True)
    )


def block_plan(counts, slot_count):
    tiles = counts.shape[0]
    per = slot_count // 128
    j = lax.broadcasted_iota(jnp.int32, (tiles, per), 1)
    kept = jnp.clip(counts[:, None] - j * 128, 0, 128).reshape(-1)
    full = (kept > 0).astype(jnp.int32)
    index = jnp.arange(tiles * per, dtype=jnp.int32)
    before = (index[None, :] < index[:, None]).astype(jnp.int32)
    ahead = jnp.sum(before * full[None, :], axis=1)
    live = jnp.sum(full)
    place = jnp.where(full > 0, ahead, live + index - ahead)
    hot = (place[None, :] == index[:, None]).astype(jnp.int32)
    return jnp.sum(hot * index[None, :], axis=1), jnp.sum(hot * kept[None, :], axis=1), live.reshape(1)


def make_body(tuned):
    def body(tokens, cotangent, counts, master, slot_block, groups, first_moment, second_moment, left_basis, right_basis, vec_params, vec_first, vec_second):
        slot_count, width = tokens.shape[1:]
        per_owner = master.shape[0]
        tile = lax.axis_index("tile")
        mine = lax.dynamic_slice(slot_block, (lax.axis_index("dp") * per_owner,), (per_owner,))
        odd = mine % 2
        packed, weight_sq = pack_master(odd, master)
        own_tokens = tokens.reshape(slot_count, width)
        count_tile = jnp.broadcast_to(counts.reshape(1, 1), (8, 128))
        if tuned:
            blocks, token_all, count_all = gather_all(packed, own_tokens, count_tile)
        else:
            blocks = lax.all_gather(packed, "dp", axis=0, tiled=True)
            token_all = lax.all_gather(own_tokens, "tile", axis=0)
            count_all = lax.all_gather(count_tile, "tile", axis=0)
        tiles = token_all.shape[0]
        block_count = blocks.shape[0]
        src, cnt, live = block_plan(count_all[:, 0, 0], slot_count)
        index = jnp.arange(block_count, dtype=jnp.int32)
        inverse = jnp.sum((slot_block[None, :] == index[:, None]).astype(jnp.int32) * index[None, :], axis=1)
        own_block = jnp.arange(12, dtype=jnp.int32) // 3 * 12 + jnp.arange(12, dtype=jnp.int32) % 3 * 4 + tile
        own_at = jnp.sum((slot_block[None, :] == own_block[:, None]).astype(jnp.int32) * index[None, :], axis=1)
        own_at = jnp.concatenate([own_at, tile.reshape(1) % 2])
        own = width // tiles
        bias = lambda row: lax.dynamic_slice(vec_params[row : row + 1], (0, tile * own), (1, own))
        a1, q, qt, k, kt, v, vt, w_qkv, lengths = qkv_forward(
            src, cnt, own_at, token_all.reshape(-1, width), blocks, vec_params[0:1], vec_params[1:2], bias(4), bias(5)
        )
        mild = jnp.sqrt(jnp.max(lengths[:, 0, 0])) * jnp.sqrt(jnp.max(lengths[:, 1, 0])) * EXP2 <= 60.0
        live = jnp.concatenate([live, mild.astype(jnp.int32).reshape(1)])
        ot, qb, p, rt = attend(live, k, qt, vt)

        def shift(parts):
            return [parts[0]] + [lax.ppermute(parts[j], "tile", [(s, (s + j) % tiles) for s in range(tiles)]) for j in range(1, tiles)]

        tile_one = tile.astype(jnp.int32).reshape(1)
        o_parts = shift(spread(src, live, tile_one, ot, tiles))
        output, grad_resid, *rest = middle(
            inverse, counts.reshape(1), tile_one, blocks, o_parts, own_tokens, cotangent.reshape(slot_count, width), vec_params, vec_params[8:].reshape(1, -1)
        )
        go_parts, (u, gz, a2, gm, gb, o_t, sums, up_sums) = rest[:tiles], rest[tiles:]
        go_parts = shift(go_parts)
        back = lambda first, heads, dt: list(attend_back(first, heads, live, p, k, kt, v, qb, q, dt, d))
        if tuned:
            dp = lax.axis_index("dp")
            bit = {"x": tile // 2, "y": dp % 2, "z": dp // 2 % 2, "far": dp // 4}
            mask = {"x": 2, "y": 4, "z": 8, "far": 16}

            def flip(array, *names):
                change = sum(mask[name] for name in names)
                return lax.ppermute(array, ("dp", "tile"), [(s, s ^ change) for s in range(32)])

            def three(sums, pairs, common):
                out = []
                for p, (a, b) in enumerate(pairs):
                    ways = [(), (a,), (b,), (a, b)]
                    del ways[common[p]]
                    out += [flip(sums[3 * p + j], *way) if way else sums[3 * p + j] for j, way in enumerate(ways)]
                return out + [flip(sums[6], pairs[0][common[0] - 1])]

            def bits_of(pairs):
                return jnp.stack([bit[name] for pair in pairs for name in pair]).astype(jnp.int32)

            first, second = [("x", "y"), ("y", "z")], [("z", "far"), ("x", "far")]
            keep, send = weight_grads_to_slots(halving_places(inverse, tile % 2), 2, block_count, o_t, gb, a2, gz, u, gm)
            send, go_parts = lax.optimization_barrier((send, go_parts))
            came = lax.ppermute(send, "tile", [(s, s ^ 1) for s in range(4)])
            dt, d = collect(src, live, tile_one, go_parts, ot, rt)
            dt, came = lax.optimization_barrier((dt, came))
            sums_one = add_pair(bits_of(first), (2, 1), keep, came)
            dt, sums_one = lax.optimization_barrier((dt, sums_one))
            parts = three(sums_one, first, (2, 1))
            head_grads = back(0, 2, dt)
            head_grads[0], parts = lax.optimization_barrier((head_grads[0], parts))
            sums_two = add_four(bits_of(second), (2, 2), parts)
            dt, sums_two = lax.optimization_barrier((dt, sums_two))
            parts = three(sums_two, second, (2, 2))
            head_grads += back(2, 1, dt)
            head_grads[3], parts = lax.optimization_barrier((head_grads[3], parts))
            mine_early = add_last(parts)
            head_grads[3], mine_early = lax.optimization_barrier((head_grads[3], mine_early))
            over_early = flip(mine_early, "x")
        else:
            slots = weight_grads_to_slots(inverse, 1, block_count, o_t, gb, a2, gz, u, gm)[0]
            dt, d = collect(src, live, tile_one, go_parts, ot, rt)
            head_grads = back(0, 3, dt)
        g_one, g_two, gw_qkv, qkv_sums, norm_sums = qkv_backward(
            src, live, tile_one % 2, token_all.reshape(-1, width), vec_params[0:1], a1, w_qkv, head_grads, tiles, slot_count * 3 // 8
        )
        if tuned:
            g_one, over_early = lax.optimization_barrier((g_one, over_early))
        zero = jnp.zeros((width,), f32)
        at_own = lambda s: lax.dynamic_update_slice(zero, s, (tile * own,))
        vector_part = jnp.concatenate(
            [norm_sums[0:2], sums[0:2], at_own(qkv_sums[0, :own])[None], at_own(qkv_sums[0, 2 * own :])[None], sums[2:4], up_sums[0].reshape(-1, width)], axis=0
        )
        if tuned:
            early, late, vector_grads = last_sums(gw_qkv, mine_early, over_early, vector_part)
            g_two, early = lax.optimization_barrier((g_two, early))
        else:
            early = lax.psum(lax.psum_scatter(slots.astype(f32), "dp", scatter_dimension=0, tiled=True), "tile").astype(bf)
            late = lax.all_gather(lax.psum(gw_qkv.astype(f32), "dp").astype(bf), "tile", axis=0, tiled=True)
            vector_grads = lax.psum(vector_part, ("dp", "tile"))
        g1 = jnp.concatenate([lax.psum_scatter(part, "tile", scatter_dimension=0, tiled=False) for part in (g_one, g_two)], axis=0)
        row_input = own_tokens.astype(f32)
        _, normed_one, inv_std_one = norm_forward(row_input, vec_params[0], vec_params[1])
        input_grad = grad_resid + norm_back(g1.astype(f32), normed_one, inv_std_one, vec_params[0])
        late_at = jnp.where(mine < 48, mine % 4 * 12 + mine // 12 * 3 + mine % 12 // 4, -1)
        weight_grads, first_out, second_out, update, update_sq = adam(odd, late_at, early, late, first_moment, second_moment, left_basis, right_basis)
        group_hot = (groups[:, None] == jnp.arange(NGRP, dtype=jnp.int32)[None, :]).astype(f32)
        both = jnp.stack([weight_sq[:, 0, 0], update_sq[:, 0, 0]], axis=0)
        group_part = jnp.pad(jnp.sum(group_hot[None] * both[:, :, None], axis=1), ((0, 6), (0, 128 - NGRP)))
        group_both = group_sum(group_part, block_count // per_owner)
        own_both = jnp.sum(group_hot[None] * group_both[:2, None, :NGRP], axis=2)
        block_rate = RATE_BLOCK * jnp.sqrt(own_both[0]) / (jnp.sqrt(own_both[1]) + 1e-06)
        master_out = master - block_rate[:, None, None] * update
        vec_first_out = BETA_ONE * vec_first + (1.0 - BETA_ONE) * vector_grads
        vec_second_out = BETA_TWO * vec_second + (1.0 - BETA_TWO) * vector_grads * vector_grads
        vec_update = (vec_first_out / (1.0 - BETA_ONE**STEP)) / (jnp.sqrt(vec_second_out / (1.0 - BETA_TWO**STEP)) + ADAM_EPS)
        return (
            output.reshape(1, slot_count, width),
            input_grad.reshape(1, slot_count, width),
            weight_grads,
            first_out,
            second_out,
            master_out,
            master_out.astype(bf),
            vector_grads,
            vec_first_out,
            vec_second_out,
            vec_params - RATE_VECTOR * vec_update,
        )

    return body


def solution(mesh):
    tuned = (mesh.shape["dp"], mesh.shape["tile"]) == (8, 4)
    rows, blocks = P("dp", "tile", None), P("dp", None, None)
    return jax.shard_map(
        make_body(tuned),
        mesh=mesh,
        in_specs=(rows, rows, P("dp", "tile"), blocks, P(), P("dp"), blocks, blocks, blocks, blocks, P(), P(), P()),
        out_specs=(rows, rows, blocks, blocks, blocks, blocks, blocks, P(), P(), P(), P()),
        check_vma=False,
    )
```

```python
import functools
import math

import jax
import jax.numpy as jnp
from jax import lax
from jax.experimental import pallas as pl
from jax.experimental.pallas import tpu as pltpu
from jax.sharding import PartitionSpec as P

f32 = jnp.float32
bf = jnp.bfloat16
MESH = pl.DeviceIdType.MESH

def where_am_i():
    dp=lax.axis_index("dp"); t=lax.axis_index("tile")
    return dp//2, dp%2, t//2, t%2

def dev(z,y,x,c):
    return (z*2+y, x*2+c)

def rcopy(src,dst,ss,rs,to):
    return pltpu.make_async_remote_copy(src_ref=src,dst_ref=dst,send_sem=ss,recv_sem=rs,device_id=to,device_id_type=MESH)

def gather_kernel(own_w,own_tok,own_cnt,all_w,all_tok,all_cnt,
                  zs,zr,ys,yr,xs,xr,cs,cr,fs,fr,ts,tr,ns,nr,ls):
    z,y,x,c=where_am_i()
    per=own_w.shape[0]
    part=per//12
    def a_of(shard,xx,cc): return all_w.at[pl.ds(shard*per+(xx*2+cc)*part,part)]
    def b_of(shard,cc): return all_w.at[pl.ds(shard*per+4*part+cc*4*part,4*part)]
    own_a=own_w.at[pl.ds((x*2+c)*part,part)]
    own_b=own_w.at[pl.ds(4*part+c*4*part,4*part)]
    me=z*2+y
    core=dev(z,y,x,1-c); across=dev(z,y,1-x,c); beside=dev(z,1-y,x,c)
    up=dev(jnp.minimum(z+1,3),y,x,c); down=dev(jnp.maximum(z-1,0),y,x,c)
    def src(shard,own):
        return (own_a,own_b) if own else (a_of(shard,x,c),b_of(shard,c))
    def z_copies(zz,own,go_up):
        shard=zz*2+y
        a,b=src(shard,own)
        d=(z-zz) if go_up else (zz-z)
        k=0 if go_up else 1
        to=up if go_up else down
        return (rcopy(a,a_of(shard,x,c),zs.at[k,d,0],zr.at[k,d,0],to),rcopy(b,b_of(shard,c),zs.at[k,d,1],zr.at[k,d,1],to))
    def z_arrivals(zz,k,dist):
        shard=zz*2+y
        a,b=a_of(shard,x,c),b_of(shard,c)
        return (rcopy(a,a,zs.at[k,dist-1,0],zr.at[k,dist-1,0],up),rcopy(b,b,zs.at[k,dist-1,1],zr.at[k,dist-1,1],up))
    def y_copies(zz,own):
        shard=zz*2+y
        a,b=src(shard,own)
        return (rcopy(a,a_of(shard,x,c),ys.at[zz,0],yr.at[zz,0],beside),rcopy(b,b_of(shard,c),ys.at[zz,1],yr.at[zz,1],beside))
    def y_arrivals(zz):
        shard=zz*2+(1-y)
        a,b=a_of(shard,x,c),b_of(shard,c)
        return (rcopy(a,a,ys.at[zz,0],yr.at[zz,0],beside),rcopy(b,b,ys.at[zz,1],yr.at[zz,1],beside))
    def x_copy(shard,own):
        return rcopy(src(shard,own)[0],a_of(shard,x,c),xs.at[shard],xr.at[shard],across)
    def x_arrival(shard):
        a=a_of(shard,1-x,c)
        return rcopy(a,a,xs.at[shard],xr.at[shard],across)
    def c_copies(shard,own):
        a,b=src(shard,own)
        return (rcopy(a,a_of(shard,x,c),cs.at[shard,0],cr.at[shard,0],core),rcopy(b,b_of(shard,c),cs.at[shard,1],cr.at[shard,1],core))
    def c_arrivals(shard):
        a,b=a_of(shard,x,1-c),b_of(shard,1-c)
        return (rcopy(a,a,cs.at[shard,0],cr.at[shard,0],core),rcopy(b,b,cs.at[shard,1],cr.at[shard,1],core))
    def f_copy(shard):
        a=a_of(shard,1-x,c)
        return rcopy(a,a,fs.at[shard],fr.at[shard],core)
    def f_arrival(shard):
        a=a_of(shard,1-x,1-c)
        return rcopy(a,a,fs.at[shard],fr.at[shard],core)
    def start(cps):
        for cp in (cps if isinstance(cps,tuple) else (cps,)): cp.start()
    def got(cps):
        for cp in (cps if isinstance(cps,tuple) else (cps,)): cp.wait_recv()
    def sent(cps):
        for cp in (cps if isinstance(cps,tuple) else (cps,)): cp.wait_send()
    tile=x*2+c
    tok_x=rcopy(own_tok,all_tok.at[tile],ts.at[0],tr.at[0],across)
    tok_c=rcopy(own_tok,all_tok.at[tile],ts.at[1],tr.at[1],core)
    far=all_tok.at[(1-x)*2+c]
    tok_f=rcopy(far,far,ts.at[2],tr.at[2],core)
    near=all_tok.at[x*2+1-c]
    diag=all_tok.at[(1-x)*2+1-c]
    cnts=[rcopy(own_cnt,all_cnt.at[tile],ns.at[i],nr.at[i],to) for i,to in enumerate((across,core,dev(z,y,1-x,1-c)))]
    cnt_in=[rcopy(r,r,ns.at[i],nr.at[i],core) for i,r in enumerate((all_cnt.at[(1-x)*2+c],all_cnt.at[x*2+1-c],all_cnt.at[(1-x)*2+1-c]))]
    local=(pltpu.make_async_copy(own_w,all_w.at[pl.ds(me*per,per)],ls.at[0]),
           pltpu.make_async_copy(own_tok,all_tok.at[tile],ls.at[1]),pltpu.make_async_copy(own_cnt,all_cnt.at[tile],ls.at[2]))
    @pl.when(z<3)
    def _(): start(z_copies(z,True,True))
    @pl.when(z>0)
    def _(): start(z_copies(z,True,False))
    start(y_copies(z,True)); start(tok_x); start(tok_c)
    for cp in cnts: cp.start()
    for cp in local: cp.start()
    def from_line(k,dist):
        zz=z-dist if k==0 else z+dist
        there=(zz>=0) if k==0 else (zz<=3)
        @pl.when(there)
        def _():
            got(z_arrivals(zz,k,dist))
            @pl.when((z<3) if k==0 else (z>0))
            def _(): start(z_copies(zz,False,k==0))
            start(y_copies(zz,False)); start(x_copy(zz*2+y,False)); start(c_copies(zz*2+y,False))
    def from_beside(zz):
        got(y_arrivals(zz))
        s=zz*2+1-y
        start(x_copy(s,False)); start(c_copies(s,False))
    def guarded(f,dist):
        @pl.when(z-dist>=0)
        def _(): f(z-dist)
        @pl.when(z+dist<=3)
        def _(): f(z+dist)
    def from_across(shard):
        got(x_arrival(shard)); start(f_copy(shard))
    from_line(0,1); from_line(1,1)
    from_beside(z)
    from_line(0,2); from_line(1,2)
    guarded(from_beside,1); guarded(lambda zz: from_across(zz*2+y),1); from_across(z*2+1-y)
    from_line(0,3); from_line(1,3)
    got(tok_x); tok_f.start()
    guarded(from_beside,2); guarded(lambda zz: from_across(zz*2+y),2); guarded(lambda zz: from_across(zz*2+1-y),1)
    guarded(from_beside,3); guarded(lambda zz: from_across(zz*2+y),3); guarded(lambda zz: from_across(zz*2+1-y),2)
    guarded(lambda zz: from_across(zz*2+1-y),3)
    def drain(s,_):
        @pl.when(s!=me)
        def _():
            got(c_arrivals(s)); got(f_arrival(s)); sent(c_copies(s,False)); sent(f_copy(s)); sent(x_copy(s,False))
        return 0
    lax.fori_loop(0,8,drain,0)
    def drain_y(zz,_):
        sent(y_copies(zz,False)); return 0
    lax.fori_loop(0,4,drain_y,0)
    for dist in range(4):
        @pl.when(jnp.logical_and(z<3,z-dist>=0))
        def _(): sent(z_copies(z-dist,False,True))
        @pl.when(jnp.logical_and(z>0,z+dist<=3))
        def _(): sent(z_copies(z+dist,False,False))
    rcopy(near,near,ts.at[1],tr.at[1],core).wait_recv()
    rcopy(diag,diag,ts.at[2],tr.at[2],core).wait_recv()
    tok_x.wait_send(); tok_c.wait_send(); tok_f.wait_send()
    for cp in cnts: cp.wait_send()
    for cp in cnt_in: cp.wait_recv()
    for cp in local: cp.wait()

def gather_all(own_w,own_tok,own_cnt):
    DS=pltpu.SemaphoreType.DMA
    hbm=pl.BlockSpec(memory_space=pl.ANY)
    return pl.pallas_call(gather_kernel,
        out_shape=[jax.ShapeDtypeStruct((8*own_w.shape[0],)+own_w.shape[1:],bf),jax.ShapeDtypeStruct((4,)+own_tok.shape,bf),jax.ShapeDtypeStruct((4,)+own_cnt.shape,own_cnt.dtype)],
        in_specs=[pl.BlockSpec(memory_space=pltpu.VMEM)]*3,out_specs=[hbm]*3,
        scratch_shapes=[DS((2,4,2)),DS((2,4,2)),DS((4,2)),DS((4,2)),DS((8,)),DS((8,)),DS((8,2)),DS((8,2)),DS((8,)),DS((8,)),DS((3,)),DS((3,)),DS((3,)),DS((3,)),DS((3,))],
        compiler_params=pltpu.CompilerParams(has_side_effects=True,vmem_limit_bytes=60<<20),name="gather_weights_tokens")(own_w,own_tok,own_cnt)

def finish_kernel(rate_scale,wsq_ref,usq_ref,hot_ref,m_ref,u_ref,mo_ref,mc_ref,m,u,c,gd,gs,gr,ls,os):
    dp=lax.axis_index("dp"); t=lax.axis_index("tile")
    nd=gd.shape[0]
    blocks=m.shape[0]
    loads=[pltpu.make_async_copy(m_ref,m,ls.at[0]),pltpu.make_async_copy(u_ref,u,ls.at[1])]
    def copy(k):
        return rcopy(gd.at[dp],gd.at[dp],gs.at[k],gr.at[k],((dp+k)%nd,t))
    def arrive(k):
        q=(dp-k+nd)%nd
        return rcopy(gd.at[q],gd.at[q],gs.at[k],gr.at[k],(q,t))
    def loop(f):
        def s(k,_):
            f(k); return 0
        lax.fori_loop(1,nd,s,0)
    hot=hot_ref[...]
    part=lambda sq: jnp.broadcast_to(jnp.sum(hot*sq[:,0,:],axis=0,keepdims=True),(8,128))
    gd[dp,0]=part(wsq_ref[...])
    gd[dp,1]=part(usq_ref[...])
    loop(lambda k: copy(k).start())
    for load in loads: load.start()
    loop(lambda k: arrive(k).wait_recv())
    acc=gd[0]
    for i in range(1,nd): acc=acc+gd[i]
    own=lambda a: jnp.sum(hot*a[0:1],axis=1,keepdims=True)
    rate=rate_scale*jnp.sqrt(own(acc[0]))/(jnp.sqrt(own(acc[1]))+1e-06)
    for load in loads: load.wait()
    outs=[]
    for b in range(blocks):
        new=m[b]-rate[b:b+1]*u[b]
        m[b]=new
        c[b]=new.astype(bf)
        outs+=[pltpu.make_async_copy(m.at[b],mo_ref.at[b],os.at[0,b]),pltpu.make_async_copy(c.at[b],mc_ref.at[b],os.at[1,b])]
        outs[-1].start(); outs[-2].start()
    for out in outs: out.wait()
    loop(lambda k: copy(k).wait_send())

def finish(rate_scale,wsq,usq,hot,master,update,nd):
    DS=pltpu.SemaphoreType.DMA
    vm=pl.BlockSpec(memory_space=pltpu.VMEM); hbm=pl.BlockSpec(memory_space=pl.ANY)
    V=pltpu.VMEM
    n=master.shape[0]
    return pl.pallas_call(functools.partial(finish_kernel,rate_scale),out_shape=[jax.ShapeDtypeStruct(master.shape,f32),jax.ShapeDtypeStruct(master.shape,bf)],
        in_specs=[vm]*3+[hbm]*2,out_specs=[hbm]*2,
        scratch_shapes=[V(master.shape,f32),V(master.shape,f32),V(master.shape,bf),V((nd,2,8,128),f32),DS((nd,)),DS((nd,)),DS((2,)),DS((2,n))],
        compiler_params=pltpu.CompilerParams(has_side_effects=True,vmem_limit_bytes=60<<20),name="group_rates_and_weights")(wsq,usq,hot,master,update)

def last_sums_kernel(l_ref,mine,over,v_ref,early,late,vo_ref,yb,zb,own,vb,vd,y1s,y1r,z2s,z2r,z3s,z3r,y4s,y4r,xs,xr,cs,cr,fs,fr,es,er,ts,tr,ds,dr,us,ur):
    z,y,x,c=where_am_i()
    dp=lax.axis_index("dp"); t=lax.axis_index("tile")
    core=dev(z,y,x,1-c); across=dev(z,y,1-x,c); beside=dev(z,1-y,x,c)
    def loop(f,first,n):
        def s(k,_):
            f(k); return 0
        lax.fori_loop(first,n,s,0)
    at=lambda i: pl.ds(i*3,3)
    def y1(k):
        q=(z+k)%4
        return rcopy(l_ref.at[at((1-y)*4+q)],yb.at[q],y1s.at[q],y1r.at[q],beside)
    def z2(k):
        q=(z+k)%4
        return rcopy(own.at[q],zb.at[z],z2s.at[k],z2r.at[k],dev(q,y,x,c))
    def z2_arrive(k):
        q=(z-k+4)%4
        return rcopy(zb.at[q],zb.at[q],z2s.at[k],z2r.at[k],dev(q,y,x,c))
    for k in (2,1,3,0): y1(k).start()
    def t1(k): return rcopy(v_ref.at[(t+k)%4],vb.at[t],ts.at[k],tr.at[k],(dp,(t+k)%4))
    def t1_arrive(k):
        q=(t-k+4)%4
        return rcopy(vb.at[q],vb.at[q],ts.at[k],tr.at[k],(dp,q))
    def d_copy(k): return rcopy(vd.at[dp],vd.at[dp],ds.at[k],dr.at[k],((dp+k)%8,t))
    def d_arrive(k):
        q=(dp-k+8)%8
        return rcopy(vd.at[q],vd.at[q],ds.at[k],dr.at[k],(q,t))
    def t2(k): return rcopy(vo_ref.at[t],vo_ref.at[t],us.at[k],ur.at[k],(dp,(t+k)%4))
    def t2_arrive(k):
        q=(t-k+4)%4
        return rcopy(vo_ref.at[q],vo_ref.at[q],us.at[k],ur.at[k],(dp,q))
    loop(lambda k: t1(k).start(),1,4)
    vb[t]=v_ref[t]
    def place(xx,cc,p): return early.at[pl.ds(cc*12+p*6+xx*3,3)]
    for p in range(2):
        early[pl.ds(c*12+p*6+x*3,3)]=mine[pl.ds(p*3,3)]
        early[pl.ds(c*12+p*6+(1-x)*3,3)]=over[pl.ds(p*3,3)]
    def e_copy(i,p): return rcopy(place(i,c,p),place(i,c,p),es.at[i,p],er.at[i,p],core)
    def e_arrive(i,p): return rcopy(place(i,1-c,p),place(i,1-c,p),es.at[i,p],er.at[i,p],core)
    for p in range(2):
        e_copy(0,p).start(); e_copy(1,p).start()
    loop(lambda k: t1_arrive(k).wait_recv(),1,4)
    vd[dp]=vb[0]+vb[1]+vb[2]+vb[3]
    loop(lambda k: d_copy(k).start(),1,8)
    for k in (2,1,3,0):
        q=(z+k)%4
        y1(k).wait_recv()
        for i in range(3): own[q,i]=(l_ref[(y*4+q)*3+i].astype(f32)+yb[q,i].astype(f32)).astype(bf)
        if k: z2(k).start()
    zb[z]=own[z]
    loop(lambda k: z2_arrive(k).wait_recv(),1,4)
    for i in range(3):
        late[t,(y*4+z)*3+i]=(zb[0,i].astype(f32)+zb[1,i].astype(f32)+zb[2,i].astype(f32)+zb[3,i].astype(f32)).astype(bf)
    def piece(tt,yy,zz): return late.at[tt,at(yy*4+zz)]
    def z3(k): return rcopy(piece(t,y,z),piece(t,y,z),z3s.at[k],z3r.at[k],dev((z+k)%4,y,x,c))
    def z3_arrive(k):
        q=(z-k+4)%4
        return rcopy(piece(t,y,q),piece(t,y,q),z3s.at[k],z3r.at[k],dev(q,y,x,c))
    def y4(q): return rcopy(piece(t,y,q),piece(t,y,q),y4s.at[q],y4r.at[q],beside)
    def y4_arrive(q): return rcopy(piece(t,1-y,q),piece(t,1-y,q),y4s.at[q],y4r.at[q],beside)
    far=(1-x)*2+c
    def x_copy(yy,q): return rcopy(piece(t,yy,q),piece(t,yy,q),xs.at[yy*4+q],xr.at[yy*4+q],across)
    def x_arrive(yy,q): return rcopy(piece(far,yy,q),piece(far,yy,q),xs.at[yy*4+q],xr.at[yy*4+q],across)
    def c_copy(yy,q): return rcopy(piece(t,yy,q),piece(t,yy,q),cs.at[yy*4+q],cr.at[yy*4+q],core)
    def c_arrive(yy,q): return rcopy(piece(x*2+1-c,yy,q),piece(x*2+1-c,yy,q),cs.at[yy*4+q],cr.at[yy*4+q],core)
    def f_copy(yy,q): return rcopy(piece(far,yy,q),piece(far,yy,q),fs.at[yy*4+q],fr.at[yy*4+q],core)
    def f_arrive(yy,q):
        r=piece((1-x)*2+1-c,yy,q)
        return rcopy(r,r,fs.at[yy*4+q],fr.at[yy*4+q],core)
    for k in (1,3,2): z3(k).start()
    y4(z).start(); x_copy(y,z).start(); c_copy(y,z).start()
    def passed_on(k):
        q=(z-k+4)%4
        if k:
            z3_arrive(k).wait_recv()
            y4(q).start(); x_copy(y,q).start(); c_copy(y,q).start()
        y4_arrive(q).wait_recv()
        x_copy(1-y,q).start(); c_copy(1-y,q).start()
    for k in (0,1,3,2): passed_on(k)
    loop(lambda k: d_arrive(k).wait_recv(),1,8)
    acc=vd[0]
    for i in range(1,8): acc=acc+vd[i]
    vo_ref[t]=acc
    loop(lambda k: t2(k).start(),1,4)
    for k in (0,1,3,2):
        q=(z-k+4)%4
        for yy in (y,1-y):
            x_arrive(yy,q).wait_recv(); f_copy(yy,q).start()
    def drain(q):
        for yy in range(2):
            c_arrive(yy,q).wait_recv(); f_arrive(yy,q).wait_recv()
            x_copy(yy,q).wait_send(); c_copy(yy,q).wait_send(); f_copy(yy,q).wait_send()
        y4(q).wait_send()
        y1(q).wait_send()
    loop(drain,0,4)
    def sent(k):
        t2_arrive(k).wait_recv()
        z2(k).wait_send(); z3(k).wait_send(); t1(k).wait_send(); t2(k).wait_send()
    loop(sent,1,4)
    loop(lambda k: d_copy(k).wait_send(),1,8)
    for p in range(2):
        for i in range(2):
            e_arrive(i,p).wait_recv(); e_copy(i,p).wait_send()

def last_sums(own,mine,over,v):
    DS=pltpu.SemaphoreType.DMA
    vm=pl.BlockSpec(memory_space=pltpu.VMEM)
    V=pltpu.VMEM
    S=jax.ShapeDtypeStruct
    rows=(3,v.shape[1])
    early,late,total=pl.pallas_call(last_sums_kernel,out_shape=[S((24,288,128),bf),S((4,24,144,128),bf),S((4,)+rows,f32)],in_specs=[vm]*4,out_specs=[vm]*3,
        scratch_shapes=[V((4,3,144,128),bf)]*3+[V((4,)+rows,f32),V((8,)+rows,f32)]+[DS((4,))]*8+[DS((8,))]*6+[DS((2,2))]*2+[DS((4,))]*2+[DS((8,))]*2+[DS((4,))]*2,
        cost_estimate=pl.CostEstimate(flops=10**7,bytes_accessed=150*10**6,transcendentals=0),
        compiler_params=pltpu.CompilerParams(has_side_effects=True,vmem_limit_bytes=60<<20),name="last_gradient_sums")(own.reshape(24,144,128),mine,over,v.reshape((4,)+rows))
    return early,late.reshape(48,288,128),total.reshape(v.shape)


H = 12
STEP = 10
EPS_NORM = 1e-06
BETA_ONE = 0.5
BETA_TWO = 0.5
ADAM_EPS = 1e-08
RATE_BLOCK = 0.3
RATE_VECTOR = 0.2
NEG_RAW = -8.0e9
HEAD = 64
SCALE = 1.0 / math.sqrt(HEAD)
EXP2 = SCALE * math.log2(math.e)
NN = (((1,), (0,)), ((), ()))
NT = (((1,), (1,)), ((), ()))
TN = (((0,), (0,)), ((), ()))


def mm(a, b, dims=NN):
    return lax.dot_general(a, b, dims, preferred_element_type=f32)


def column_sum(v):
    return jnp.sum(v, axis=0, keepdims=True)


def vmem_spec():
    return pl.BlockSpec(memory_space=pltpu.VMEM)


def smem_spec():
    return pl.BlockSpec(memory_space=pltpu.SMEM)


def any_spec():
    return pl.BlockSpec(memory_space=pl.ANY)


def params(mib=60):
    return pltpu.CompilerParams(vmem_limit_bytes=mib << 20)


def pack(block, odd):
    half = block.shape[0] // 2
    left, right = block[:, :64], block[:, 128:]
    even_tail = jnp.concatenate([right[:half], right[half:]], axis=1)
    odd_tail = jnp.concatenate([left[half:], left[:half]], axis=1)
    return jnp.where(odd, block[:, 64:], block[:, :128]), jnp.where(odd, odd_tail, even_tail)


def unpack(top, tail, odd):
    first, second = tail[:, :64], tail[:, 64:]
    even = jnp.concatenate([top, jnp.concatenate([first, second], axis=0)], axis=1)
    return jnp.where(odd, jnp.concatenate([jnp.concatenate([second, first], axis=0), top], axis=1), even)


def turn(v):
    return jnp.concatenate([v[:, 64:], v[:, :64]], axis=1)


def group_of(n):
    return 4 if n % 4 == 0 else 3 if n % 3 == 0 else 1


def pack_kernel(odd_ref, m_ref, p_ref, s_ref):
    g = m_ref.shape[0]
    for b in range(g):
        m = m_ref[b]
        top, tail = pack(m, odd_ref[pl.program_id(0) * g + b] == 1)
        p_ref[b, :192] = top.astype(bf)
        p_ref[b, 192:] = tail.astype(bf)
        s_ref[b] = jnp.full((8, 128), jnp.sum(m * m), f32)


def pack_master(odd, master):
    n = master.shape[0]
    g = group_of(n)
    at = lambda i, s: (i, 0, 0)
    spec = pltpu.PrefetchScalarGridSpec(
        num_scalar_prefetch=1,
        grid=(n // g,),
        in_specs=[pl.BlockSpec((g, 192, 192), at)],
        out_specs=[pl.BlockSpec((g, 288, 128), at), pl.BlockSpec((g, 8, 128), at)],
    )
    return pl.pallas_call(
        pack_kernel,
        grid_spec=spec,
        out_shape=[jax.ShapeDtypeStruct((n, 288, 128), bf), jax.ShapeDtypeStruct((n, 8, 128), f32)],
        compiler_params=params(),
        name="pack_master",
    )(odd, master)


def qkv_kernel(src_ref, cnt_ref, at_ref, x0, x1, x2, x3, blk_ref, gain_ref, shift_ref, bq_ref, bv_ref, a_ref, q_ref, qt_ref, k_ref, kt_ref, v_ref, vt_ref, w_ref, st_ref, buf, sems):
    i = pl.program_id(0)

    @pl.when(i == 0)
    def _():
        copies = [pltpu.make_async_copy(blk_ref.at[at_ref[j]], buf.at[j], sems.at[j]) for j in range(12)]
        for copy in copies:
            copy.start()
        odd = at_ref[12] == 1
        for r in range(4):
            parts = []
            for c in range(3):
                copies[r * 3 + c].wait()
                p = buf[r * 3 + c].astype(f32)
                parts.append(unpack(p[:192], p[192:], odd))
            w_ref[r * 192 : (r + 1) * 192, :] = jnp.concatenate(parts, axis=1).astype(bf)

    x = jnp.concatenate([r[...] for r in (x0, x1, x2, x3)], axis=0).astype(f32)
    mean = jnp.mean(x, axis=-1, keepdims=True)
    cen = x - mean
    inv_std = lax.rsqrt(jnp.mean(cen * cen, axis=-1, keepdims=True) + EPS_NORM)
    a = (cen * inv_std * gain_ref[...] + shift_ref[...]).astype(bf)
    a_ref[...] = a
    qkv = mm(a, w_ref[...])
    q = (qkv[:, :192] + bq_ref[...]).astype(bf).astype(f32)
    k = qkv[:, 192:384].astype(bf).astype(f32)
    v = (qkv[:, 384:] + bv_ref[...]).astype(bf).astype(f32)
    row = lax.broadcasted_iota(jnp.int32, (128, 64), 0)
    lane = lax.broadcasted_iota(jnp.int32, (512, 64), 1)
    masked = jnp.concatenate(
        [jnp.where(row < cnt_ref[4 * i + b], 0.0, NEG_RAW) for b in range(4)], axis=0
    )
    ones = jnp.where(lane < 4, 1.0, 0.0)
    k_tail = jnp.where(lane == 0, masked, ones)
    v_tail = jnp.where(lane < 3, 1.0, 0.0)
    zero = jnp.zeros((512, 64), f32)
    sub = lax.broadcasted_iota(jnp.int32, (64, 512), 0)
    t_tail = jnp.where(sub < 1, 1.0, 0.0)
    qt, kt, vt = q.T, k.T, v.T
    longest = lambda a: jnp.max(jnp.concatenate([column_sum(a[h * 64 : (h + 1) * 64] ** 2) for h in range(3)], axis=0))
    st_ref[0] = jnp.where(lax.broadcasted_iota(jnp.int32, (8, 128), 0) == 0, longest(qt), longest(kt))
    for h in range(3):
        s = slice(h * 64, (h + 1) * 64)
        q_ref[h] = jnp.concatenate([q[:, s], zero], axis=1).astype(bf)
        k_ref[h] = jnp.concatenate([k[:, s], k_tail], axis=1).astype(bf)
        v_ref[h] = jnp.concatenate([v[:, s], v_tail], axis=1).astype(bf)
        qt_ref[h] = jnp.concatenate([qt[s], t_tail], axis=0).astype(bf)
        kt_ref[h] = kt[s].astype(bf)
        vt_ref[h] = jnp.concatenate([vt[s], t_tail[:16]], axis=0).astype(bf)


def qkv_forward(src, cnt, own_at, tokens, blocks, gain, shift, bq, bv):
    n = tokens.shape[0]
    rows = [pl.BlockSpec((128, 768), lambda i, s, c, o, k=k: (s[4 * i + k], 0)) for k in range(4)]
    row = lambda i, s, c, o: (0, 0)
    spec = pltpu.PrefetchScalarGridSpec(
        num_scalar_prefetch=3,
        grid=(n // 512,),
        in_specs=rows
        + [any_spec(), pl.BlockSpec((1, 768), row), pl.BlockSpec((1, 768), row), pl.BlockSpec((1, 192), row), pl.BlockSpec((1, 192), row)],
        out_specs=[
            pl.BlockSpec((512, 768), lambda i, s, c, o: (i, 0)),
            pl.BlockSpec((3, 512, 128), lambda i, s, c, o: (0, i, 0)),
            pl.BlockSpec((3, 128, 512), lambda i, s, c, o: (0, 0, i)),
            pl.BlockSpec((3, 512, 128), lambda i, s, c, o: (0, i, 0)),
            pl.BlockSpec((3, 64, 512), lambda i, s, c, o: (0, 0, i)),
            pl.BlockSpec((3, 512, 128), lambda i, s, c, o: (0, i, 0)),
            pl.BlockSpec((3, 80, 512), lambda i, s, c, o: (0, 0, i)),
            pl.BlockSpec((768, 576), row),
            pl.BlockSpec((1, 8, 128), lambda i, s, c, o: (i, 0, 0)),
        ],
        scratch_shapes=[pltpu.VMEM((12, 288, 128), bf), pltpu.SemaphoreType.DMA((12,))],
    )
    shapes = [(n, 768), (3, n, 128), (3, 128, n), (3, n, 128), (3, 64, n), (3, n, 128), (3, 80, n), (768, 576)]
    return pl.pallas_call(
        qkv_kernel,
        grid_spec=spec,
        out_shape=[jax.ShapeDtypeStruct(s, bf) for s in shapes] + [jax.ShapeDtypeStruct((n // 512, 8, 128), f32)],
        compiler_params=params(),
        name="norm_and_qkv",
    )(src, cnt, own_at, tokens, tokens, tokens, tokens, blocks, gain, shift, bq, bv)


def split3(v):
    a = v.astype(bf).astype(f32)
    b = (v - a).astype(bf).astype(f32)
    return a, b, v - a - b


def in_steps(units, sizes, body, carry):
    at = 0
    for size in sizes:
        count = (units - at) // size
        carry = lax.fori_loop(0, count, lambda i, c, at=at, size=size: body(at + i * size, size, c), carry)
        at = at + count * size
    return carry


def attend_kernel(bq, n_ref, k_ref, qt_ref, vt_ref, ot_ref, qb_ref, p_ref, rt_ref):
    live = n_ref[0]
    qi = pl.program_id(1)
    pairs = (live + 7) // 8 * 4

    def finish(top, acc):
        total = acc[64:65]
        ot_ref[0] = acc[:64] / total
        rt_ref[0] = 1.0 / total
        a, b, c = split3((top + jnp.log2(total)) * (-1.0 / EXP2))
        row = lax.broadcasted_iota(jnp.int32, (64, bq), 0)
        tail = jnp.where(row == 0, 1.0, jnp.where(row == 1, a, jnp.where(row == 2, b, jnp.where(row == 3, c, 0.0))))
        qb_ref[0, :64] = qt_ref[0, :64]
        qb_ref[0, 64:] = tail.astype(bf)

    def keys(u, size):
        return pl.ds(pl.multiple_of(u * 256, 256), size * 256)

    @pl.when(jnp.logical_and(qi * bq < live * 128, n_ref[1] == 1))
    def _():
        qt = qt_ref[0]

        def body(u, size, acc):
            step = min(size, 2)
            for part in range(0, size, step):
                at = keys(u + part, step)
                p = jnp.exp2(mm(k_ref[0, at, :], qt) * EXP2).astype(bf)
                p_ref[0, at, :] = p
                acc = acc + mm(vt_ref[0, :, at], p)
            return acc

        finish(0.0, in_steps(pairs, (16, 8, 4), body, jnp.zeros((80, bq), f32)))

    @pl.when(jnp.logical_and(qi * bq < live * 128, n_ref[1] == 0))
    def _():
        qt = qt_ref[0]

        def body(u, size, carry):
            top, acc = carry
            s = mm(k_ref[0, keys(u, size), :], qt) * EXP2
            new = jnp.maximum(top, jnp.max(s, axis=0, keepdims=True))
            p = jnp.exp2(s - new).astype(bf)
            return new, acc * jnp.exp2(top - new) + mm(vt_ref[0, :, keys(u, size)], p)

        finish(*in_steps(pairs, (4,), body, (jnp.full((1, bq), -3e38, f32), jnp.zeros((80, bq), f32))))


def attend(live, k, qt, vt, bq=1024):
    n = k.shape[1]
    spec = pltpu.PrefetchScalarGridSpec(
        num_scalar_prefetch=1,
        grid=(3, n // bq),
        in_specs=[
            pl.BlockSpec((1, n, 128), lambda h, i, s: (h, 0, 0)),
            pl.BlockSpec((1, 128, bq), lambda h, i, s: (h, 0, i)),
            pl.BlockSpec((1, 80, n), lambda h, i, s: (h, 0, 0)),
        ],
        out_specs=[
            pl.BlockSpec((1, 64, bq), lambda h, i, s: (h, 0, i)),
            pl.BlockSpec((1, 128, bq), lambda h, i, s: (h, 0, i)),
            pl.BlockSpec((1, n, bq), lambda h, i, s: (h, 0, i)),
            pl.BlockSpec((1, 1, bq), lambda h, i, s: (h, 0, i)),
        ],
    )
    return pl.pallas_call(
        functools.partial(attend_kernel, bq),
        grid_spec=spec,
        out_shape=[
            jax.ShapeDtypeStruct((3, 64, n), f32),
            jax.ShapeDtypeStruct((3, 128, n), bf),
            jax.ShapeDtypeStruct((3, n, n), bf),
            jax.ShapeDtypeStruct((3, 1, n), f32),
        ],
        compiler_params=params(),
        name="attention_forward",
    )(live, k, qt, vt)


def spread_kernel(src_ref, n_ref, t_ref, ot_ref, *o_refs):
    live, t, tiles = n_ref[0], t_ref[0], len(o_refs)
    per = o_refs[0].shape[1] // 128

    def step(b, _):
        g = src_ref[b]
        lanes = pl.ds(pl.multiple_of(b * 128, 128), 128)
        to = pl.ds(pl.multiple_of((g % per) * 128, 128), 128)
        for k in range(tiles):
            here = (g // per - t + tiles) % tiles == k

            @pl.when(jnp.logical_and(here, b < live))
            def _():
                for h in range(3):
                    o_refs[k][h * 64 : (h + 1) * 64, to] = ot_ref[h, :, lanes].astype(bf)

            @pl.when(jnp.logical_and(here, b >= live))
            def _():
                o_refs[k][:, to] = jnp.zeros((192, 128), bf)

        return 0

    lax.fori_loop(0, ot_ref.shape[2] // 128, step, 0)


def spread(src, live, tile, ot, tiles):
    n = ot.shape[2]
    return pl.pallas_call(
        spread_kernel,
        in_specs=[smem_spec()] * 3 + [vmem_spec()],
        out_specs=[vmem_spec()] * tiles,
        out_shape=[jax.ShapeDtypeStruct((192, n // tiles), bf)] * tiles,
        compiler_params=params(),
        name="spread_attended",
    )(src, live, tile, ot)


def collect_kernel(src_ref, n_ref, t_ref, ot_ref, rt_ref, *refs):
    g_refs, (dt_ref, d_ref) = refs[:-2], refs[-2:]
    live, t, tiles = n_ref[0], t_ref[0], len(g_refs)
    mild = n_ref[1] == 1
    per = g_refs[0].shape[1] // 128
    row = lax.broadcasted_iota(jnp.int32, (64, 128), 0)

    def step(b, _):
        g = src_ref[b]
        to = pl.ds(pl.multiple_of(b * 128, 128), 128)
        lanes = pl.ds(pl.multiple_of((g % per) * 128, 128), 128)
        for k in range(tiles):

            @pl.when(jnp.logical_and((t - g // per + tiles) % tiles == k, b < live))
            def _():
                for h in range(3):
                    scale = jnp.where(mild, rt_ref[h, :, to], 1.0)
                    d = (g_refs[k][h * 64 : (h + 1) * 64, lanes].astype(f32) * scale).astype(bf).astype(f32)
                    x, y, z = split3(-jnp.sum(d * ot_ref[h, :, to], axis=0, keepdims=True))
                    tail = jnp.where(row == 0, x, jnp.where(row == 1, y, jnp.where(row == 2, z, 0.0)))
                    dt_ref[h, :, to] = jnp.concatenate([d, tail], axis=0).astype(bf)
                    d_ref[h, to, :] = jnp.concatenate([d, jnp.zeros_like(d)], axis=0).T.astype(bf)

        @pl.when(b >= live)
        def _():
            dt_ref[:, :, to] = jnp.zeros((3, 128, 128), bf)
            d_ref[:, to, :] = jnp.zeros((3, 128, 128), bf)

        return 0

    lax.fori_loop(0, ot_ref.shape[2] // 128, step, 0)


def collect(src, live, tile, grads, ot, rt):
    n = ot.shape[2]
    return pl.pallas_call(
        collect_kernel,
        in_specs=[smem_spec()] * 3 + [vmem_spec()] * (2 + len(grads)),
        out_specs=[vmem_spec()] * 2,
        out_shape=[jax.ShapeDtypeStruct((3, 128, n), bf), jax.ShapeDtypeStruct((3, n, 128), bf)],
        compiler_params=params(),
        name="collect_attended_grad",
    )(src, live, tile, ot, rt, *grads)


def attend_back_kernel(bk, n_ref, p_ref, k_ref, kt_ref, v_ref, qb_ref, q_ref, dt_ref, d_ref, dq_ref, dk_ref, dv_ref):
    live = n_ref[0]
    j = pl.program_id(1)

    @pl.when(j == 0)
    def _():
        dq_ref[...] = jnp.zeros_like(dq_ref)

    def lanes(u):
        return pl.ds(pl.multiple_of(u * 256, 256), 256)

    pairs = (live + 1) // 2

    def over_queries(rows, sizes, body):
        zero = jnp.zeros((rows, 128), f32)
        dk, dv = in_steps((live + 7) // 8 * 4, sizes, body, (zero, zero))
        dk_ref[0, :rows] = (dk * SCALE).astype(bf)
        dv_ref[0, :rows] = dv.astype(bf)

    def with_kept(rows):
        k, v, kt = k_ref[0, :rows], v_ref[0, :rows], kt_ref[0, :, :rows]

        def body(u, size, carry):
            dk, dv = carry
            dp = mm(v, dt_ref[0, :, lanes(u)])
            for part in range(size):
                at = lanes(u + part)
                ahead = mm(v, dt_ref[0, :, lanes(u + part + 1)]) if part + 1 < size else None
                p = p_ref[0, :rows, at]
                ds = (p.astype(f32) * dp).astype(bf)
                dv = dv + mm(p, d_ref[0, at, :])
                dk = dk + mm(ds, q_ref[0, at, :])
                dq_ref[0, :, at] += mm(kt, ds)
                dp = dp if ahead is None else ahead
            return dk, dv

        over_queries(rows, (16, 8, 4), body)

    @pl.when(jnp.logical_and(n_ref[1] == 1, 2 * j + 2 <= pairs))
    def _():
        with_kept(bk)

    @pl.when(jnp.logical_and(n_ref[1] == 1, 2 * j + 1 == pairs))
    def _():
        dk_ref[0, bk // 2 :] = jnp.zeros((bk // 2, 128), bf)
        dv_ref[0, bk // 2 :] = jnp.zeros((bk // 2, 128), bf)
        with_kept(bk // 2)

    @pl.when(jnp.logical_and(n_ref[1] == 0, j * bk < live * 128))
    def _():
        k, v, kt = k_ref[0], v_ref[0], kt_ref[0]

        def body(u, size, carry):
            dk, dv = carry
            for part in range(size):
                at = lanes(u + part)
                p = jnp.exp2(mm(k, qb_ref[0, :, at]) * EXP2)
                ds = (p * mm(v, dt_ref[0, :, at])).astype(bf)
                dv = dv + mm(p.astype(bf), d_ref[0, at, :])
                dk = dk + mm(ds, q_ref[0, at, :])
                dq_ref[0, :, at] += mm(kt, ds)
            return dk, dv

        over_queries(bk, (4,), body)


def attend_back(first, heads, live, p, k, kt, v, qb, q, dt, d, bk=512):
    n = k.shape[1]
    whole_t = lambda h, j, s: (first + h, 0, 0)
    rows = lambda h, j, s: (first + h, j, 0)
    spec = pltpu.PrefetchScalarGridSpec(
        num_scalar_prefetch=1,
        grid=(heads, n // bk),
        in_specs=[
            pl.BlockSpec((1, bk, n), rows),
            pl.BlockSpec((1, bk, 128), rows),
            pl.BlockSpec((1, 64, bk), lambda h, j, s: (first + h, 0, j)),
            pl.BlockSpec((1, bk, 128), rows),
            pl.BlockSpec((1, 128, n), whole_t),
            pl.BlockSpec((1, n, 128), whole_t),
            pl.BlockSpec((1, 128, n), whole_t),
            pl.BlockSpec((1, n, 128), whole_t),
        ],
        out_specs=[
            pl.BlockSpec((1, 64, n), lambda h, j, s: (h, 0, 0)),
            pl.BlockSpec((1, bk, 128), lambda h, j, s: (h, j, 0)),
            pl.BlockSpec((1, bk, 128), lambda h, j, s: (h, j, 0)),
        ],
    )
    S = jax.ShapeDtypeStruct
    return pl.pallas_call(
        functools.partial(attend_back_kernel, bk),
        grid_spec=spec,
        out_shape=[S((heads, 64, n), f32), S((heads, n, 128), bf), S((heads, n, 128), bf)],
        cost_estimate=pl.CostEstimate(flops=heads * 4 * 10**10, bytes_accessed=heads * 50 * 10**6, transcendentals=0),
        compiler_params=params(),
        name="attention_backward",
    )(live, p, k, kt, v, qb, q, dt, d)


def qkv_back_kernel(given, src_ref, n_ref, odd_ref, x0, x1, x2, x3, gain_ref, a_ref, w_ref, *refs):
    grads, (ga_ref, gz_ref, gw_ref, gb_ref, vs_ref, acc, sums, rows, sems) = refs[:given], refs[given:]
    dqs, dks, dvs = [[(r, h) for r in grads[j::3] for h in range(r.shape[0])] for j in range(3)]
    early = ga_ref.shape[1] // 128
    i = pl.program_id(0)
    live = n_ref[0]

    @pl.when(i == 0)
    def _():
        acc[...] = jnp.zeros_like(acc)
        sums[...] = jnp.zeros_like(sums)
        vs_ref[...] = jnp.zeros_like(vs_ref)

    @pl.when(4 * i < live)
    def _():
        dq = jnp.concatenate([r[h] for r, h in dqs], axis=0).T * SCALE
        g = jnp.concatenate([dq] + [r[h][:, :64].astype(f32) for r, h in dks + dvs], axis=1).astype(bf)
        acc[...] += mm(a_ref[...], g, TN)
        sums[...] += jnp.broadcast_to(column_sum(g.astype(f32)), sums.shape)
        g1 = mm(g, w_ref[...], NT)
        rows[...] = g1.astype(bf)
        x = jnp.concatenate([r[...] for r in (x0, x1, x2, x3)], axis=0).astype(f32)
        cen = x - jnp.mean(x, axis=-1, keepdims=True)
        normed = cen * lax.rsqrt(jnp.mean(cen * cen, axis=-1, keepdims=True) + EPS_NORM)
        vs_ref[0:1, :] += column_sum(g1 * normed)
        vs_ref[1:2, :] += column_sum(g1)

    @pl.when(4 * i >= live)
    def _():
        rows[...] = jnp.zeros_like(rows)

    per = early + gz_ref.shape[1] // 128
    for b in range(4):
        block, at = rows.at[pl.ds(b * 128, 128)], src_ref[4 * i + b]
        t, j = at // per, at % per

        @pl.when(j < early)
        def _():
            pltpu.make_async_copy(block, ga_ref.at[t, pl.ds(pl.multiple_of(j * 128, 128), 128)], sems.at[b]).start()

        @pl.when(j >= early)
        def _():
            pltpu.make_async_copy(block, gz_ref.at[t, pl.ds(pl.multiple_of((j - early) * 128, 128), 128)], sems.at[b]).start()

    for b in range(4):
        pltpu.make_async_copy(rows.at[pl.ds(b * 128, 128)], ga_ref.at[0, pl.ds(0, 128)], sems.at[b]).wait()

    @pl.when(i == pl.num_programs(0) - 1)
    def _():
        for r in range(4):
            for c in range(3):
                top, tail = pack(acc[r * 192 : (r + 1) * 192, c * 192 : (c + 1) * 192], odd_ref[0] == 1)
                gw_ref[r * 3 + c, :192] = top.astype(bf)
                gw_ref[r * 3 + c, 192:] = tail.astype(bf)
        gb_ref[...] = sums[...]


def qkv_backward(src, live, odd, tokens, gain, a, w, grads, tiles, early):
    n = a.shape[0]
    per = n // tiles
    fixed = lambda i, s, c, o: (0, 0)
    row = lambda i, s, c, o: (0, i, 0)
    spec = pltpu.PrefetchScalarGridSpec(
        num_scalar_prefetch=3,
        grid=(n // 512,),
        in_specs=[pl.BlockSpec((128, 768), lambda i, s, c, o, k=k: (s[4 * i + k], 0)) for k in range(4)]
        + [pl.BlockSpec((1, 768), fixed), pl.BlockSpec((512, 768), lambda i, s, c, o: (i, 0)), pl.BlockSpec((768, 576), fixed)]
        + [
            pl.BlockSpec((g.shape[0], 64, 512), lambda i, s, c, o: (0, 0, i)) if g.shape[1] == 64 else pl.BlockSpec((g.shape[0], 512, 128), row)
            for g in grads
        ],
        out_specs=[any_spec(), any_spec(), pl.BlockSpec((12, 288, 128), lambda i, s, c, o: (0, 0, 0)), pl.BlockSpec((8, 576), fixed), pl.BlockSpec((8, 768), fixed)],
        scratch_shapes=[pltpu.VMEM((768, 576), f32), pltpu.VMEM((8, 576), f32), pltpu.VMEM((512, 768), bf), pltpu.SemaphoreType.DMA((4,))],
    )
    S = jax.ShapeDtypeStruct
    return pl.pallas_call(
        functools.partial(qkv_back_kernel, len(grads)),
        grid_spec=spec,
        out_shape=[S((tiles, early, 768), bf), S((tiles, per - early, 768), bf), S((12, 288, 128), bf), S((8, 576), f32), S((8, 768), f32)],
        cost_estimate=pl.CostEstimate(flops=3 * 10**10, bytes_accessed=40 * 10**6, transcendentals=0),
        compiler_params=params(),
        name="qkv_backward",
    )(src, live, odd, tokens, tokens, tokens, tokens, gain, a, w, *grads)


def gelu_parts(z):
    cdf = 0.5 + 0.5 * lax.erf(z * math.sqrt(0.5))
    return z * cdf, cdf + z * (jnp.exp2(z * z * (-0.5 * math.log2(math.e))) * (1.0 / math.sqrt(2.0 * math.pi)))


def middle_kernel(inv_ref, cnt_ref, t_ref, blk_ref, o0, o1, o2, o3, x_ref, c_ref, vp_ref, bu_ref, y_ref, gr_ref, g0, g1, g2_ref, g3,
                  u_s, gz_s, a2_s, gm_s, gb_s, o_s, vs_ref, us_ref, w_out, w_up, w_down, tails, tsem, isem):
    i = pl.program_id(0)
    rows = x_ref.shape[0]
    r0 = i * rows
    kinds = ((w_out, 48, 2, 4), (w_up, 64, 8, 4), (w_down, 128, 2, 16))

    @pl.when(i == 0)
    def _():
        vs_ref[...] = jnp.zeros_like(vs_ref)
        us_ref[...] = jnp.zeros_like(us_ref)

        def pair(w, first, pairs):
            def copies(j):
                r = pl.multiple_of((j // pairs) * 192, 64)
                col = pl.multiple_of((j % pairs) * 384, 128)
                out = []
                for b, off in ((0, 0), (1, 256)):
                    at = first + 2 * j + b
                    slot = inv_ref[at]
                    out.append(pltpu.make_async_copy(blk_ref.at[slot, pl.ds(0, 192)], w.at[pl.ds(r, 192), pl.ds(col + off, 128)], tsem.at[at - 48]))
                    out.append(pltpu.make_async_copy(blk_ref.at[slot, pl.ds(192, 96)], tails.at[at - 48], isem.at[at - 48]))
                return out, r, col

            def start(j, _):
                for copy in copies(j)[0]:
                    copy.start()
                return 0

            def join(j, _):
                got, r, col = copies(j)
                for copy in got:
                    copy.wait()
                even = tails[first + 2 * j - 48].astype(f32)
                odd = tails[first + 2 * j - 47].astype(f32)
                lane = lax.broadcasted_iota(jnp.int32, even.shape, 1) < 64
                w[pl.ds(r, 96), pl.ds(col + 128, 128)] = jnp.where(lane, even, odd).astype(bf)
                w[pl.ds(r + 96, 96), pl.ds(col + 128, 128)] = turn(jnp.where(lane, odd, even)).astype(bf)
                return 0

            return start, join

        todo = [(pair(w, first, pairs), pairs * high) for w, first, pairs, high in kinds]
        for (start, _), n in todo:
            lax.fori_loop(0, n, start, 0)

        for (_, join), n in todo:
            lax.fori_loop(0, n, join, 0)

    vp = vp_ref[...]
    row = r0 + lax.broadcasted_iota(jnp.int32, (rows, 1), 0)
    live = jnp.where(row < cnt_ref[0], 1.0, 0.0)
    t = t_ref[0]
    for k, ref in enumerate((o0, o1, o2, o3)):
        o_s[pl.ds(pl.multiple_of(((t - k + 4) % 4) * 192, 64), 192), :] = ref[...]
    o_t = o_s[...]
    res = x_ref[...].astype(f32) + mm(o_t, w_out[...], TN) + vp[6:7]
    cen = res - jnp.mean(res, axis=-1, keepdims=True)
    inv_std = lax.rsqrt(jnp.mean(cen * cen, axis=-1, keepdims=True) + EPS_NORM)
    normed = cen * inv_std
    a2 = (normed * vp[2:3] + vp[3:4]).astype(bf)
    gy = c_ref[...].astype(f32) * live
    gm = gy.astype(bf)
    a2_s[...] = a2
    gm_s[...] = gm
    branch = jnp.zeros((rows, 768), f32)
    g2 = jnp.zeros((rows, 768), f32)
    for j in range(4):
        cols = slice(j * 768, (j + 1) * 768)
        u, slope = gelu_parts(mm(a2, w_up[:, cols]) + bu_ref[:, cols])
        u = u.astype(bf)
        u_s[:, cols] = u
        branch = branch + mm(u, w_down[cols, :])
        gz = (mm(gm, w_down[cols, :], NT) * slope).astype(bf)
        gz_s[:, cols] = gz
        us_ref[:, cols] += jnp.broadcast_to(column_sum(gz.astype(f32)), (8, 768))
        g2 = g2 + mm(gz, w_up[:, cols], NT)
    y_ref[...] = (live * (res + branch + vp[7:8])).astype(bf)
    d2 = g2 * vp[2:3]
    gr = gy + inv_std * (d2 - jnp.mean(d2, axis=-1, keepdims=True) - normed * jnp.mean(d2 * normed, axis=-1, keepdims=True))
    gr_ref[...] = gr
    gb = gr.astype(bf)
    gb_s[...] = gb
    vs_ref[0:1, :] += column_sum(g2 * normed)
    vs_ref[1:2, :] += column_sum(g2)
    vs_ref[2:3, :] += column_sum(gb.astype(f32))
    vs_ref[3:4, :] += column_sum(gm.astype(f32))
    for k, ref in enumerate((g0, g1, g2_ref, g3)):
        ref[...] = mm(w_out[pl.ds(pl.multiple_of(((t + k) % 4) * 192, 64), 192), :], gb, NT).astype(bf)


def weight_grad_kernel(outs, pos_ref, o_in, gb_in, a2_in, gz_in, u_in, gm_in, *refs):
    s_refs, (o_s, gb_s, a2_s, gz_s, u_s, gm_s, ring, zero, lsem, osem, zsem) = refs[:outs], refs[outs:]
    each = s_refs[0].shape[0]

    def to_slot(block, at, sem):
        for o in range(outs):

            @pl.when(at // each == o)
            def _():
                pltpu.make_async_copy(block, s_refs[o].at[at % each], sem).start()

    def landed(block, sem):
        pltpu.make_async_copy(block, s_refs[0].at[0], sem).wait()

    loads = [pltpu.make_async_copy(a, b, lsem.at[j]) for j, (a, b) in enumerate(
        ((o_in, o_s), (gb_in, gb_s), (a2_in, a2_s), (gz_in, gz_s), (gm_in, gm_s), (u_in, u_s)))]
    for load in loads:
        load.start()
    zero[...] = jnp.zeros_like(zero)

    def clear(j, _):
        to_slot(zero, pos_ref[j], zsem.at[j])
        return 0

    lax.fori_loop(0, 48, clear, 0)
    def send(n, g, first, pairs, high, low):
        half = (n % 2) * 8

        def put(r, b):
            return first + (high + r) * 2 * pairs + 2 * low + b

        for r in range(4):
            part = g[r * 192 : (r + 1) * 192]
            mid = part[:, 128:256]
            upper, lower = mid[:96], turn(mid[96:])
            lane = lax.broadcasted_iota(jnp.int32, upper.shape, 1) < 64
            for b, top, tail in ((0, part[:, :128], jnp.where(lane, upper, lower)), (1, part[:, 256:], jnp.where(lane, lower, upper))):
                k = half + 2 * r + b

                @pl.when(n >= 2)
                def _():
                    landed(ring.at[k], osem.at[k])

                ring[k, :192] = top.astype(bf)
                ring[k, 192:] = tail.astype(bf)
                to_slot(ring.at[k], pos_ref[put(r, b)], osem.at[k])

    def lanes(j):
        return pl.ds(pl.multiple_of(j * 384, 128), 384)

    def grad_out(n, _):
        send(n, mm(o_s[...], gb_s[:, lanes(n)]), 48, 2, 0, n)
        return 0

    def grad_up(n, _):
        send(n, mm(a2_s[...], gz_s[:, lanes(n)], TN), 64, 8, 0, n)
        return 0

    def grad_down(n, _):
        high = n // 2
        send(n, mm(u_s[:, pl.ds(pl.multiple_of(high * 768, 128), 768)], gm_s[:, lanes(n % 2)], TN), 128, 2, high * 4, n % 2)
        return 0

    def drain():
        for k in range(16):
            landed(ring.at[k], osem.at[k])

    for f, n, first in ((grad_out, 2, 0), (grad_up, 8, 2), (grad_down, 8, 4)):
        loads[first].wait()
        loads[first + 1].wait()
        lax.fori_loop(0, n, f, 0)
        drain()

    def cleared(j, _):
        landed(zero, zsem.at[j])
        return 0

    lax.fori_loop(0, 48, cleared, 0)


def middle(inv, count, tile, blocks, o_parts, tokens, cotangent, vec_params, bias_up, rows=256):
    n, width = tokens.shape
    hidden = bias_up.shape[1]
    row = lambda i, s, c, t: (i, 0)
    fixed = lambda i, s, c, t: (0, 0)
    col = lambda i, s, c, t: (0, i)
    V, DS = pltpu.VMEM, pltpu.SemaphoreType.DMA
    narrow, wide, part = pl.BlockSpec((rows, width), row), pl.BlockSpec((rows, hidden), row), pl.BlockSpec((192, rows), col)
    spec = pltpu.PrefetchScalarGridSpec(
        num_scalar_prefetch=3,
        grid=(n // rows,),
        in_specs=[any_spec()] + [part] * 4 + [narrow, narrow, pl.BlockSpec((12, width), fixed), pl.BlockSpec((1, hidden), fixed)],
        out_specs=[narrow, narrow] + [part] * 4 + [wide, wide, narrow, narrow, narrow, pl.BlockSpec((width, rows), col),
                   pl.BlockSpec((8, width), fixed), pl.BlockSpec((8, hidden), fixed)],
        scratch_shapes=[V((768, 768), bf), V((768, 3072), bf), V((3072, 768), bf), V((144, 96, 128), bf), DS((144,)), DS((144,))],
    )
    S = jax.ShapeDtypeStruct
    return pl.pallas_call(
        middle_kernel,
        grid_spec=spec,
        out_shape=[S((n, width), bf), S((n, width), f32)] + [S((192, n), bf)] * 4 + [S((n, hidden), bf)] * 2 + [S((n, width), bf)] * 3
        + [S((width, n), bf), S((8, width), f32), S((8, hidden), f32)],
        compiler_params=params(),
        name="projection_and_mlp",
    )(inv, count, tile, blocks, *o_parts, tokens, cotangent, vec_params, bias_up)


def weight_grads_to_slots(pos, outs, block_count, o_t, gb, a2, gz, u, gm):
    V, DS = pltpu.VMEM, pltpu.SemaphoreType.DMA
    arrays = (o_t, gb, a2, gz, u, gm)
    return pl.pallas_call(
        functools.partial(weight_grad_kernel, outs),
        in_specs=[smem_spec()] + [any_spec()] * 6,
        out_specs=[any_spec()] * outs,
        out_shape=[jax.ShapeDtypeStruct((block_count // outs, 288, 128), bf)] * outs,
        scratch_shapes=[V(a.shape, bf) for a in arrays] + [V((16, 288, 128), bf), V((288, 128), bf), DS((6,)), DS((16,)), DS((48,))],
        cost_estimate=pl.CostEstimate(flops=6 * 10**10, bytes_accessed=32 * 10**6, transcendentals=0),
        compiler_params=params(),
        name="mlp_weight_gradients",
    )(pos, *arrays)


def quarters(b0, b1):
    return (b0 * 2 + b1, (1 - b0) * 2 + b1, b0 * 2 + 1 - b1, (1 - b0) * 2 + 1 - b1)


def add_pair_kernel(common, bits_ref, *refs):
    outs = list(refs[16:])
    for p in range(2):
        for side in range(4):
            j = 4 * p + side
            total = (refs[2 * j][...].astype(f32) + refs[2 * j + 1][...].astype(f32)).astype(bf)
            if side == common[p]:
                outs[6][p] = total
            else:
                outs[3 * p + side - (side > common[p])][...] = total


def add_pair(bits, common, keep, came):
    specs = []
    for p in range(2):
        for side in range(4):
            at = lambda i, b, p=p, side=side: (p * 12 + quarters(b[2 * p], b[2 * p + 1])[side] * 3 + i, 0, 0)
            specs += [pl.BlockSpec((4, 288, 128), at)] * 2
    S = jax.ShapeDtypeStruct
    return pl.pallas_call(
        functools.partial(add_pair_kernel, common),
        grid_spec=pltpu.PrefetchScalarGridSpec(
            num_scalar_prefetch=1,
            grid=(3,),
            in_specs=specs,
            out_specs=[pl.BlockSpec((4, 288, 128), lambda i, b: (i, 0, 0))] * 6 + [pl.BlockSpec((2, 4, 288, 128), lambda i, b: (0, i, 0, 0))],
        ),
        out_shape=[S((12, 288, 128), bf)] * 6 + [S((2, 12, 288, 128), bf)],
        compiler_params=params(),
        name="add_gradients_of_cores",
    )(bits, *[keep, came] * 8)


def add_four_kernel(common, bits_ref, *refs):
    outs = refs[7:]
    for p in range(2):
        parts = refs[3 * p : 3 * p + 3]
        for side, q in enumerate(quarters(bits_ref[2 * p], bits_ref[2 * p + 1])):
            for b in range(3):
                total = (sum(r[q * 3 + b].astype(f32) for r in parts) + refs[6][p, q * 3 + b].astype(f32)).astype(bf)
                if side == common[p]:
                    outs[6][p, b] = total
                else:
                    outs[3 * p + side - (side > common[p])][b] = total


def add_four(bits, common, parts):
    S = jax.ShapeDtypeStruct
    return pl.pallas_call(
        functools.partial(add_four_kernel, common),
        in_specs=[smem_spec()] + [vmem_spec()] * 7,
        out_specs=[vmem_spec()] * 7,
        out_shape=[S((3, 288, 128), bf)] * 6 + [S((2, 3, 288, 128), bf)],
        compiler_params=params(),
        name="add_gradients",
    )(bits, *parts)


def add_last_kernel(*refs):
    for p in range(2):
        for b in range(3):
            refs[7][3 * p + b] = (sum(r[b].astype(f32) for r in refs[3 * p : 3 * p + 3]) + refs[6][p, b].astype(f32)).astype(bf)


def add_last(parts):
    return pl.pallas_call(
        add_last_kernel,
        in_specs=[vmem_spec()] * 7,
        out_specs=vmem_spec(),
        out_shape=jax.ShapeDtypeStruct((6, 288, 128), bf),
        compiler_params=params(),
        name="add_last_gradients",
    )(*parts)


def adam_kernel(odd_ref, from_ref, g_ref, late_ref, m1_ref, m2_ref, l_ref, r_ref, g_out, m1_out, m2_out, u_out, s_out):
    for b in range(g_ref.shape[0]):
        slot = pl.program_id(0) * g_ref.shape[0] + b
        place = from_ref[slot]
        part = jnp.where(place >= 0, late_ref[jnp.maximum(place, 0)].astype(f32), g_ref[b].astype(f32))
        grad = unpack(part[:192], part[192:], odd_ref[slot] == 1)
        left, right = l_ref[b].astype(bf), r_ref[b].astype(bf)
        rot = mm(mm(left, grad.astype(bf), TN).astype(bf), right)
        first = BETA_ONE * m1_ref[b] + (1.0 - BETA_ONE) * rot
        second = BETA_TWO * m2_ref[b] + (1.0 - BETA_TWO) * rot * rot
        upd = (first / (1.0 - BETA_ONE**STEP)) / (jnp.sqrt(second / (1.0 - BETA_TWO**STEP)) + ADAM_EPS)
        upd = mm(mm(left, upd.astype(bf)).astype(bf), right, NT)
        g_out[b] = grad
        m1_out[b] = first
        m2_out[b] = second
        u_out[b] = upd
        s_out[b] = jnp.full((8, 128), jnp.sum(upd * upd), f32)


def adam(odd, late_at, grads, late, first, second, left, right):
    n = grads.shape[0]
    g = group_of(n)
    at = lambda i, s, f: (i, 0, 0)
    big = pl.BlockSpec((g, 192, 192), at)
    spec = pltpu.PrefetchScalarGridSpec(
        num_scalar_prefetch=2,
        grid=(n // g,),
        in_specs=[pl.BlockSpec((g, 288, 128), at), pl.BlockSpec(late.shape, lambda i, s, f: (0, 0, 0))] + [big] * 4,
        out_specs=[big] * 4 + [pl.BlockSpec((g, 8, 128), at)],
    )
    return pl.pallas_call(
        adam_kernel,
        grid_spec=spec,
        out_shape=[jax.ShapeDtypeStruct((n, 192, 192), f32)] * 4 + [jax.ShapeDtypeStruct((n, 8, 128), f32)],
        compiler_params=params(),
        name="rotated_adam",
    )(odd, late_at, grads, late, first, second, left, right)


def halving_places(slot, core):
    dp, r = slot // 24, slot % 24
    y, z, far, x, s = dp % 2, dp // 2 % 2, dp // 4, r % 6 // 3, r % 3
    portion = r % 12 // 6
    inside = jnp.where(portion == 0, x * 8 + y * 4 + z * 2 + far, y * 8 + z * 4 + x * 2 + far)
    return jnp.where(r // 12 == core, 0, 96) + portion * 48 + inside * 3 + s


def norm_forward(row_data, gain_vec, shift_vec):
    row_mean = jnp.mean(row_data, axis=-1, keepdims=True)
    centred = row_data - row_mean
    inv_std = lax.rsqrt(jnp.mean(centred * centred, axis=-1, keepdims=True) + EPS_NORM)
    normed = centred * inv_std
    return (normed * gain_vec + shift_vec, normed, inv_std)


def norm_back(grad_out, normed, inv_std, gain_vec):
    grad_normed = grad_out * gain_vec
    return inv_std * (
        grad_normed
        - jnp.mean(grad_normed, axis=-1, keepdims=True)
        - normed * jnp.mean(grad_normed * normed, axis=-1, keepdims=True)
    )


def block_plan(counts, slot_count):
    tiles = counts.shape[0]
    per = slot_count // 128
    j = lax.broadcasted_iota(jnp.int32, (tiles, per), 1)
    kept = jnp.clip(counts[:, None] - j * 128, 0, 128).reshape(-1)
    full = (kept > 0).astype(jnp.int32)
    index = jnp.arange(tiles * per, dtype=jnp.int32)
    before = (index[None, :] < index[:, None]).astype(jnp.int32)
    ahead = jnp.sum(before * full[None, :], axis=1)
    live = jnp.sum(full)
    place = jnp.where(full > 0, ahead, live + index - ahead)
    hot = (place[None, :] == index[:, None]).astype(jnp.int32)
    return jnp.sum(hot * index[None, :], axis=1), jnp.sum(hot * kept[None, :], axis=1), live.reshape(1)


def make_body(tuned):
    def body(tokens, cotangent, counts, master, slot_block, groups, first_moment, second_moment, left_basis, right_basis, vec_params, vec_first, vec_second):
        slot_count, width = tokens.shape[1:]
        per_owner = master.shape[0]
        tile = lax.axis_index("tile")
        mine = lax.dynamic_slice(slot_block, (lax.axis_index("dp") * per_owner,), (per_owner,))
        odd = mine % 2
        packed, weight_sq = pack_master(odd, master)
        own_tokens = tokens.reshape(slot_count, width)
        count_tile = jnp.broadcast_to(counts.reshape(1, 1), (8, 128))
        if tuned:
            blocks, token_all, count_all = gather_all(packed, own_tokens, count_tile)
        else:
            blocks = lax.all_gather(packed, "dp", axis=0, tiled=True)
            token_all = lax.all_gather(own_tokens, "tile", axis=0)
            count_all = lax.all_gather(count_tile, "tile", axis=0)
        tiles = token_all.shape[0]
        block_count = blocks.shape[0]
        src, cnt, live = block_plan(count_all[:, 0, 0], slot_count)
        index = jnp.arange(block_count, dtype=jnp.int32)
        inverse = jnp.sum((slot_block[None, :] == index[:, None]).astype(jnp.int32) * index[None, :], axis=1)
        own_block = jnp.arange(12, dtype=jnp.int32) // 3 * 12 + jnp.arange(12, dtype=jnp.int32) % 3 * 4 + tile
        own_at = jnp.sum((slot_block[None, :] == own_block[:, None]).astype(jnp.int32) * index[None, :], axis=1)
        own_at = jnp.concatenate([own_at, tile.reshape(1) % 2])
        own = width // tiles
        bias = lambda row: lax.dynamic_slice(vec_params[row : row + 1], (0, tile * own), (1, own))
        a1, q, qt, k, kt, v, vt, w_qkv, lengths = qkv_forward(
            src, cnt, own_at, token_all.reshape(-1, width), blocks, vec_params[0:1], vec_params[1:2], bias(4), bias(5)
        )
        mild = jnp.sqrt(jnp.max(lengths[:, 0, 0])) * jnp.sqrt(jnp.max(lengths[:, 1, 0])) * EXP2 <= 60.0
        live = jnp.concatenate([live, mild.astype(jnp.int32).reshape(1)])
        ot, qb, p, rt = attend(live, k, qt, vt)

        def shift(parts):
            return [parts[0]] + [lax.ppermute(parts[j], "tile", [(s, (s + j) % tiles) for s in range(tiles)]) for j in range(1, tiles)]

        tile_one = tile.astype(jnp.int32).reshape(1)
        o_parts = shift(spread(src, live, tile_one, ot, tiles))
        output, grad_resid, *rest = middle(
            inverse, counts.reshape(1), tile_one, blocks, o_parts, own_tokens, cotangent.reshape(slot_count, width), vec_params, vec_params[8:].reshape(1, -1)
        )
        go_parts, (u, gz, a2, gm, gb, o_t, sums, up_sums) = rest[:tiles], rest[tiles:]
        go_parts = shift(go_parts)
        back = lambda first, heads, dt: list(attend_back(first, heads, live, p, k, kt, v, qb, q, dt, d))
        if tuned:
            dp = lax.axis_index("dp")
            bit = {"x": tile // 2, "y": dp % 2, "z": dp // 2 % 2, "far": dp // 4}
            mask = {"x": 2, "y": 4, "z": 8, "far": 16}

            def flip(array, *names):
                change = sum(mask[name] for name in names)
                return lax.ppermute(array, ("dp", "tile"), [(s, s ^ change) for s in range(32)])

            def three(sums, pairs, common):
                out = []
                for p, (a, b) in enumerate(pairs):
                    ways = [(), (a,), (b,), (a, b)]
                    del ways[common[p]]
                    out += [flip(sums[3 * p + j], *way) if way else sums[3 * p + j] for j, way in enumerate(ways)]
                return out + [flip(sums[6], pairs[0][common[0] - 1])]

            def bits_of(pairs):
                return jnp.stack([bit[name] for pair in pairs for name in pair]).astype(jnp.int32)

            first, second = [("x", "y"), ("y", "z")], [("z", "far"), ("x", "far")]
            keep, send = weight_grads_to_slots(halving_places(inverse, tile % 2), 2, block_count, o_t, gb, a2, gz, u, gm)
            send, go_parts = lax.optimization_barrier((send, go_parts))
            came = lax.ppermute(send, "tile", [(s, s ^ 1) for s in range(4)])
            dt, d = collect(src, live, tile_one, go_parts, ot, rt)
            dt, came = lax.optimization_barrier((dt, came))
            sums_one = add_pair(bits_of(first), (2, 1), keep, came)
            dt, sums_one = lax.optimization_barrier((dt, sums_one))
            parts = three(sums_one, first, (2, 1))
            head_grads = back(0, 2, dt)
            head_grads[0], parts = lax.optimization_barrier((head_grads[0], parts))
            sums_two = add_four(bits_of(second), (2, 2), parts)
            dt, sums_two = lax.optimization_barrier((dt, sums_two))
            parts = three(sums_two, second, (2, 2))
            head_grads += back(2, 1, dt)
            head_grads[3], parts = lax.optimization_barrier((head_grads[3], parts))
            mine_early = add_last(parts)
            head_grads[3], mine_early = lax.optimization_barrier((head_grads[3], mine_early))
            over_early = flip(mine_early, "x")
        else:
            slots = weight_grads_to_slots(inverse, 1, block_count, o_t, gb, a2, gz, u, gm)[0]
            dt, d = collect(src, live, tile_one, go_parts, ot, rt)
            head_grads = back(0, 3, dt)
        g_one, g_two, gw_qkv, qkv_sums, norm_sums = qkv_backward(
            src, live, tile_one % 2, token_all.reshape(-1, width), vec_params[0:1], a1, w_qkv, head_grads, tiles, slot_count * 3 // 8
        )
        if tuned:
            g_one, over_early = lax.optimization_barrier((g_one, over_early))
        zero = jnp.zeros((width,), f32)
        at_own = lambda s: lax.dynamic_update_slice(zero, s, (tile * own,))
        vector_part = jnp.concatenate(
            [norm_sums[0:2], sums[0:2], at_own(qkv_sums[0, :own])[None], at_own(qkv_sums[0, 2 * own :])[None], sums[2:4], up_sums[0].reshape(-1, width)], axis=0
        )
        if tuned:
            early, late, vector_grads = last_sums(gw_qkv, mine_early, over_early, vector_part)
            g_two, early = lax.optimization_barrier((g_two, early))
        else:
            early = lax.psum(lax.psum_scatter(slots.astype(f32), "dp", scatter_dimension=0, tiled=True), "tile").astype(bf)
            late = lax.all_gather(lax.psum(gw_qkv.astype(f32), "dp").astype(bf), "tile", axis=0, tiled=True)
            vector_grads = lax.psum(vector_part, ("dp", "tile"))
        g1 = jnp.concatenate([lax.psum_scatter(part, "tile", scatter_dimension=0, tiled=False) for part in (g_one, g_two)], axis=0)
        row_input = own_tokens.astype(f32)
        _, normed_one, inv_std_one = norm_forward(row_input, vec_params[0], vec_params[1])
        input_grad = grad_resid + norm_back(g1.astype(f32), normed_one, inv_std_one, vec_params[0])
        late_at = jnp.where(mine < 48, mine % 4 * 12 + mine // 12 * 3 + mine % 12 // 4, -1)
        weight_grads, first_out, second_out, update, update_sq = adam(odd, late_at, early, late, first_moment, second_moment, left_basis, right_basis)
        group_hot = (groups[:, None] == jnp.arange(128, dtype=jnp.int32)[None, :]).astype(f32)
        master_out, master_copy = finish(RATE_BLOCK, weight_sq, update_sq, group_hot, master, update, block_count // per_owner)
        vec_first_out = BETA_ONE * vec_first + (1.0 - BETA_ONE) * vector_grads
        vec_second_out = BETA_TWO * vec_second + (1.0 - BETA_TWO) * vector_grads * vector_grads
        vec_update = (vec_first_out / (1.0 - BETA_ONE**STEP)) / (jnp.sqrt(vec_second_out / (1.0 - BETA_TWO**STEP)) + ADAM_EPS)
        return (
            output.reshape(1, slot_count, width),
            input_grad.reshape(1, slot_count, width),
            weight_grads,
            first_out,
            second_out,
            master_out,
            master_copy,
            vector_grads,
            vec_first_out,
            vec_second_out,
            vec_params - RATE_VECTOR * vec_update,
        )

    return body


def solution(mesh):
    tuned = (mesh.shape["dp"], mesh.shape["tile"]) == (8, 4)
    rows, blocks = P("dp", "tile", None), P("dp", None, None)
    return jax.shard_map(
        make_body(tuned),
        mesh=mesh,
        in_specs=(rows, rows, P("dp", "tile"), blocks, P(), P("dp"), blocks, blocks, blocks, blocks, P(), P(), P()),
        out_specs=(rows, rows, blocks, blocks, blocks, blocks, blocks, P(), P(), P(), P()),
        check_vma=False,
    )
```

```python
import functools
import math

import jax
import jax.numpy as jnp
from jax import lax
from jax.experimental import pallas as pl
from jax.experimental.pallas import tpu as pltpu
from jax.sharding import PartitionSpec as P

f32 = jnp.float32
bf = jnp.bfloat16
MESH = pl.DeviceIdType.MESH

def where_am_i():
    dp=lax.axis_index("dp"); t=lax.axis_index("tile")
    return dp//2, dp%2, t//2, t%2

def dev(z,y,x,c):
    return (z*2+y, x*2+c)

def rcopy(src,dst,ss,rs,to):
    return pltpu.make_async_remote_copy(src_ref=src,dst_ref=dst,send_sem=ss,recv_sem=rs,device_id=to,device_id_type=MESH)

def gather_kernel(own_w,own_tok,own_cnt,all_w,all_tok,all_cnt,zs,zr,ys,yr,cs,cr,ts,tr,ns,nr,ls):
    z,y,x,c=where_am_i()
    per=own_w.shape[0]
    half=per//2
    def piece(shard,cc): return all_w.at[pl.ds(shard*per+cc*half,half)]
    own=own_w.at[pl.ds(c*half,half)]
    me=z*2+y
    core=dev(z,y,x,1-c); across=dev(z,y,1-x,c); beside=dev(z,1-y,x,c)
    up=dev(jnp.minimum(z+1,3),y,x,c); down=dev(jnp.maximum(z-1,0),y,x,c)
    def src(shard,first): return own if first else piece(shard,c)
    def z_copy(zz,first,go_up):
        shard=zz*2+y
        d=(z-zz) if go_up else (zz-z)
        k=0 if go_up else 1
        return rcopy(src(shard,first),piece(shard,c),zs.at[k,d],zr.at[k,d],up if go_up else down)
    def z_arrival(zz,k,dist):
        r=piece(zz*2+y,c)
        return rcopy(r,r,zs.at[k,dist-1],zr.at[k,dist-1],up)
    def y_copy(zz,first):
        shard=zz*2+y
        return rcopy(src(shard,first),piece(shard,c),ys.at[zz],yr.at[zz],beside)
    def y_arrival(zz):
        r=piece(zz*2+1-y,c)
        return rcopy(r,r,ys.at[zz],yr.at[zz],beside)
    def c_copy(shard): return rcopy(piece(shard,c),piece(shard,c),cs.at[shard],cr.at[shard],core)
    def c_arrival(shard): return rcopy(piece(shard,1-c),piece(shard,1-c),cs.at[shard],cr.at[shard],core)
    tile=x*2+c
    tok_x=rcopy(own_tok,all_tok.at[tile],ts.at[0],tr.at[0],across)
    tok_c=rcopy(own_tok,all_tok.at[tile],ts.at[1],tr.at[1],core)
    far=all_tok.at[(1-x)*2+c]
    tok_f=rcopy(far,far,ts.at[2],tr.at[2],core)
    near=all_tok.at[x*2+1-c]
    diag=all_tok.at[(1-x)*2+1-c]
    cnts=[rcopy(own_cnt,all_cnt.at[tile],ns.at[i],nr.at[i],to) for i,to in enumerate((across,core,dev(z,y,1-x,1-c)))]
    cnt_in=[rcopy(r,r,ns.at[i],nr.at[i],core) for i,r in enumerate((all_cnt.at[(1-x)*2+c],all_cnt.at[x*2+1-c],all_cnt.at[(1-x)*2+1-c]))]
    local=(pltpu.make_async_copy(own_w,all_w.at[pl.ds(me*per,per)],ls.at[0]),
           pltpu.make_async_copy(own_tok,all_tok.at[tile],ls.at[1]),pltpu.make_async_copy(own_cnt,all_cnt.at[tile],ls.at[2]))
    @pl.when(z<3)
    def _(): z_copy(z,True,True).start()
    @pl.when(z>0)
    def _(): z_copy(z,True,False).start()
    y_copy(z,True).start(); tok_x.start(); tok_c.start()
    for cp in cnts: cp.start()
    for cp in local: cp.start()
    def from_line(k,dist):
        zz=z-dist if k==0 else z+dist
        there=(zz>=0) if k==0 else (zz<=3)
        @pl.when(there)
        def _():
            z_arrival(zz,k,dist).wait_recv()
            @pl.when((z<3) if k==0 else (z>0))
            def _(): z_copy(zz,False,k==0).start()
            y_copy(zz,False).start(); c_copy(zz*2+y).start()
    def from_beside(zz):
        y_arrival(zz).wait_recv(); c_copy(zz*2+1-y).start()
    def guarded(f,dist):
        @pl.when(z-dist>=0)
        def _(): f(z-dist)
        @pl.when(z+dist<=3)
        def _(): f(z+dist)
    from_line(0,1); from_line(1,1)
    from_beside(z)
    from_line(0,2); from_line(1,2)
    guarded(from_beside,1)
    from_line(0,3); from_line(1,3)
    tok_x.wait_recv(); tok_f.start()
    guarded(from_beside,2)
    guarded(from_beside,3)
    def drain(s,_):
        @pl.when(s!=me)
        def _():
            c_arrival(s).wait_recv(); c_copy(s).wait_send()
        return 0
    lax.fori_loop(0,8,drain,0)
    def drain_y(zz,_):
        y_copy(zz,False).wait_send(); return 0
    lax.fori_loop(0,4,drain_y,0)
    for dist in range(4):
        @pl.when(jnp.logical_and(z<3,z-dist>=0))
        def _(): z_copy(z-dist,False,True).wait_send()
        @pl.when(jnp.logical_and(z>0,z+dist<=3))
        def _(): z_copy(z+dist,False,False).wait_send()
    rcopy(near,near,ts.at[1],tr.at[1],core).wait_recv()
    rcopy(diag,diag,ts.at[2],tr.at[2],core).wait_recv()
    tok_x.wait_send(); tok_c.wait_send(); tok_f.wait_send()
    for cp in cnts: cp.wait_send()
    for cp in cnt_in: cp.wait_recv()
    for cp in local: cp.wait()

def gather_all(own_w,own_tok,own_cnt):
    DS=pltpu.SemaphoreType.DMA
    hbm=pl.BlockSpec(memory_space=pl.ANY)
    return pl.pallas_call(gather_kernel,
        out_shape=[jax.ShapeDtypeStruct((8*own_w.shape[0],)+own_w.shape[1:],bf),jax.ShapeDtypeStruct((4,)+own_tok.shape,bf),jax.ShapeDtypeStruct((4,)+own_cnt.shape,own_cnt.dtype)],
        in_specs=[pl.BlockSpec(memory_space=pltpu.VMEM)]*3,out_specs=[hbm]*3,
        scratch_shapes=[DS((2,4)),DS((2,4)),DS((4,)),DS((4,)),DS((8,)),DS((8,)),DS((3,)),DS((3,)),DS((3,)),DS((3,)),DS((3,))],
        compiler_params=pltpu.CompilerParams(has_side_effects=True,vmem_limit_bytes=60<<20),name="gather_weights_tokens")(own_w,own_tok,own_cnt)

def group_sum_kernel(g_ref,o_ref,gd,gs,gr):
    dp=lax.axis_index("dp"); t=lax.axis_index("tile")
    nd=gd.shape[0]
    def copy(k):
        return rcopy(gd.at[dp],gd.at[dp],gs.at[k],gr.at[k],((dp+k)%nd,t))
    def arrive(k):
        q=(dp-k+nd)%nd
        return rcopy(gd.at[q],gd.at[q],gs.at[k],gr.at[k],(q,t))
    def loop(f):
        def s(k,_):
            f(k); return 0
        lax.fori_loop(1,nd,s,0)
    gd[dp]=g_ref[...]
    loop(lambda k: copy(k).start())
    loop(lambda k: arrive(k).wait_recv())
    acc=gd[0]
    for i in range(1,nd): acc=acc+gd[i]
    o_ref[...]=acc
    loop(lambda k: copy(k).wait_send())

def group_sum(g,nd):
    DS=pltpu.SemaphoreType.DMA
    vm=pl.BlockSpec(memory_space=pltpu.VMEM)
    return pl.pallas_call(group_sum_kernel,out_shape=jax.ShapeDtypeStruct(g.shape,f32),in_specs=[vm],out_specs=vm,
        scratch_shapes=[pltpu.VMEM((nd,)+g.shape,f32),DS((nd,)),DS((nd,))],
        compiler_params=pltpu.CompilerParams(has_side_effects=True,vmem_limit_bytes=60<<20),name="sum_groups")(g)

def last_sums_kernel(l_ref,mine,over,v_ref,early,late,vo_ref,yb,zb,own,vb,vd,y1s,y1r,z2s,z2r,z3s,z3r,y4s,y4r,xs,xr,cs,cr,fs,fr,es,er,ts,tr,ds,dr,us,ur):
    z,y,x,c=where_am_i()
    dp=lax.axis_index("dp"); t=lax.axis_index("tile")
    core=dev(z,y,x,1-c); across=dev(z,y,1-x,c); beside=dev(z,1-y,x,c)
    def loop(f,first,n):
        def s(k,_):
            f(k); return 0
        lax.fori_loop(first,n,s,0)
    at=lambda i: pl.ds(i*3,3)
    def y1(k):
        q=(z+k)%4
        return rcopy(l_ref.at[at((1-y)*4+q)],yb.at[q],y1s.at[q],y1r.at[q],beside)
    def z2(k):
        q=(z+k)%4
        return rcopy(own.at[q],zb.at[z],z2s.at[k],z2r.at[k],dev(q,y,x,c))
    def z2_arrive(k):
        q=(z-k+4)%4
        return rcopy(zb.at[q],zb.at[q],z2s.at[k],z2r.at[k],dev(q,y,x,c))
    for k in (2,1,3,0): y1(k).start()
    def t1(k): return rcopy(v_ref.at[(t+k)%4],vb.at[t],ts.at[k],tr.at[k],(dp,(t+k)%4))
    def t1_arrive(k):
        q=(t-k+4)%4
        return rcopy(vb.at[q],vb.at[q],ts.at[k],tr.at[k],(dp,q))
    def d_copy(k): return rcopy(vd.at[dp],vd.at[dp],ds.at[k],dr.at[k],((dp+k)%8,t))
    def d_arrive(k):
        q=(dp-k+8)%8
        return rcopy(vd.at[q],vd.at[q],ds.at[k],dr.at[k],(q,t))
    def t2(k): return rcopy(vo_ref.at[t],vo_ref.at[t],us.at[k],ur.at[k],(dp,(t+k)%4))
    def t2_arrive(k):
        q=(t-k+4)%4
        return rcopy(vo_ref.at[q],vo_ref.at[q],us.at[k],ur.at[k],(dp,q))
    loop(lambda k: t1(k).start(),1,4)
    vb[t]=v_ref[t]
    def place(xx,cc,p): return early.at[pl.ds(cc*12+p*6+xx*3,3)]
    for p in range(2):
        early[pl.ds(c*12+p*6+x*3,3)]=mine[pl.ds(p*3,3)]
        early[pl.ds(c*12+p*6+(1-x)*3,3)]=over[pl.ds(p*3,3)]
    def e_copy(i,p): return rcopy(place(i,c,p),place(i,c,p),es.at[i,p],er.at[i,p],core)
    def e_arrive(i,p): return rcopy(place(i,1-c,p),place(i,1-c,p),es.at[i,p],er.at[i,p],core)
    for p in range(2):
        e_copy(0,p).start(); e_copy(1,p).start()
    loop(lambda k: t1_arrive(k).wait_recv(),1,4)
    vd[dp]=vb[0]+vb[1]+vb[2]+vb[3]
    loop(lambda k: d_copy(k).start(),1,8)
    for k in (2,1,3,0):
        q=(z+k)%4
        y1(k).wait_recv()
        for i in range(3): own[q,i]=(l_ref[(y*4+q)*3+i].astype(f32)+yb[q,i].astype(f32)).astype(bf)
        if k: z2(k).start()
    zb[z]=own[z]
    loop(lambda k: z2_arrive(k).wait_recv(),1,4)
    for i in range(3):
        late[t,(y*4+z)*3+i]=(zb[0,i].astype(f32)+zb[1,i].astype(f32)+zb[2,i].astype(f32)+zb[3,i].astype(f32)).astype(bf)
    def piece(tt,yy,zz): return late.at[tt,at(yy*4+zz)]
    def z3(k): return rcopy(piece(t,y,z),piece(t,y,z),z3s.at[k],z3r.at[k],dev((z+k)%4,y,x,c))
    def z3_arrive(k):
        q=(z-k+4)%4
        return rcopy(piece(t,y,q),piece(t,y,q),z3s.at[k],z3r.at[k],dev(q,y,x,c))
    def y4(q): return rcopy(piece(t,y,q),piece(t,y,q),y4s.at[q],y4r.at[q],beside)
    def y4_arrive(q): return rcopy(piece(t,1-y,q),piece(t,1-y,q),y4s.at[q],y4r.at[q],beside)
    far=(1-x)*2+c
    def x_copy(yy,q): return rcopy(piece(t,yy,q),piece(t,yy,q),xs.at[yy*4+q],xr.at[yy*4+q],across)
    def x_arrive(yy,q): return rcopy(piece(far,yy,q),piece(far,yy,q),xs.at[yy*4+q],xr.at[yy*4+q],across)
    def c_copy(yy,q): return rcopy(piece(t,yy,q),piece(t,yy,q),cs.at[yy*4+q],cr.at[yy*4+q],core)
    def c_arrive(yy,q): return rcopy(piece(x*2+1-c,yy,q),piece(x*2+1-c,yy,q),cs.at[yy*4+q],cr.at[yy*4+q],core)
    def f_copy(yy,q): return rcopy(piece(far,yy,q),piece(far,yy,q),fs.at[yy*4+q],fr.at[yy*4+q],core)
    def f_arrive(yy,q):
        r=piece((1-x)*2+1-c,yy,q)
        return rcopy(r,r,fs.at[yy*4+q],fr.at[yy*4+q],core)
    for k in (1,3,2): z3(k).start()
    y4(z).start(); x_copy(y,z).start(); c_copy(y,z).start()
    def passed_on(k):
        q=(z-k+4)%4
        if k:
            z3_arrive(k).wait_recv()
            y4(q).start(); x_copy(y,q).start(); c_copy(y,q).start()
        y4_arrive(q).wait_recv()
        x_copy(1-y,q).start(); c_copy(1-y,q).start()
    for k in (0,1,3,2): passed_on(k)
    loop(lambda k: d_arrive(k).wait_recv(),1,8)
    acc=vd[0]
    for i in range(1,8): acc=acc+vd[i]
    vo_ref[t]=acc
    loop(lambda k: t2(k).start(),1,4)
    for k in (0,1,3,2):
        q=(z-k+4)%4
        for yy in (y,1-y):
            x_arrive(yy,q).wait_recv(); f_copy(yy,q).start()
    def drain(q):
        for yy in range(2):
            c_arrive(yy,q).wait_recv(); f_arrive(yy,q).wait_recv()
            x_copy(yy,q).wait_send(); c_copy(yy,q).wait_send(); f_copy(yy,q).wait_send()
        y4(q).wait_send()
        y1(q).wait_send()
    loop(drain,0,4)
    def sent(k):
        t2_arrive(k).wait_recv()
        z2(k).wait_send(); z3(k).wait_send(); t1(k).wait_send(); t2(k).wait_send()
    loop(sent,1,4)
    loop(lambda k: d_copy(k).wait_send(),1,8)
    for p in range(2):
        for i in range(2):
            e_arrive(i,p).wait_recv(); e_copy(i,p).wait_send()

def last_sums(own,mine,over,v):
    DS=pltpu.SemaphoreType.DMA
    vm=pl.BlockSpec(memory_space=pltpu.VMEM)
    V=pltpu.VMEM
    S=jax.ShapeDtypeStruct
    rows=(3,v.shape[1])
    early,late,total=pl.pallas_call(last_sums_kernel,out_shape=[S((24,288,128),bf),S((4,24,144,128),bf),S((4,)+rows,f32)],in_specs=[vm]*4,out_specs=[vm]*3,
        scratch_shapes=[V((4,3,144,128),bf)]*3+[V((4,)+rows,f32),V((8,)+rows,f32)]+[DS((4,))]*8+[DS((8,))]*6+[DS((2,2))]*2+[DS((4,))]*2+[DS((8,))]*2+[DS((4,))]*2,
        cost_estimate=pl.CostEstimate(flops=10**7,bytes_accessed=150*10**6,transcendentals=0),
        compiler_params=pltpu.CompilerParams(has_side_effects=True,vmem_limit_bytes=60<<20),name="last_gradient_sums")(own.reshape(24,144,128),mine,over,v.reshape((4,)+rows))
    return early,late.reshape(48,288,128),total.reshape(v.shape)


H = 12
STEP = 10
EPS_NORM = 1e-06
BETA_ONE = 0.5
BETA_TWO = 0.5
ADAM_EPS = 1e-08
RATE_BLOCK = 0.3
RATE_VECTOR = 0.2
NEG_RAW = -8.0e9
HEAD = 64
SCALE = 1.0 / math.sqrt(HEAD)
EXP2 = SCALE * math.log2(math.e)
NN = (((1,), (0,)), ((), ()))
NT = (((1,), (1,)), ((), ()))
TN = (((0,), (0,)), ((), ()))


def mm(a, b, dims=NN):
    return lax.dot_general(a, b, dims, preferred_element_type=f32)


def column_sum(v):
    return jnp.sum(v, axis=0, keepdims=True)


def vmem_spec():
    return pl.BlockSpec(memory_space=pltpu.VMEM)


def smem_spec():
    return pl.BlockSpec(memory_space=pltpu.SMEM)


def any_spec():
    return pl.BlockSpec(memory_space=pl.ANY)


def params(mib=60):
    return pltpu.CompilerParams(vmem_limit_bytes=mib << 20)


def pack(block, odd):
    half = block.shape[0] // 2
    left, right = block[:, :64], block[:, 128:]
    even_tail = jnp.concatenate([right[:half], right[half:]], axis=1)
    odd_tail = jnp.concatenate([left[half:], left[:half]], axis=1)
    return jnp.where(odd, block[:, 64:], block[:, :128]), jnp.where(odd, odd_tail, even_tail)


def unpack(top, tail, odd):
    first, second = tail[:, :64], tail[:, 64:]
    even = jnp.concatenate([top, jnp.concatenate([first, second], axis=0)], axis=1)
    return jnp.where(odd, jnp.concatenate([jnp.concatenate([second, first], axis=0), top], axis=1), even)


def turn(v):
    return jnp.concatenate([v[:, 64:], v[:, :64]], axis=1)


def group_of(n):
    return 4 if n % 4 == 0 else 3 if n % 3 == 0 else 1


def pack_kernel(early, order_ref, odd_ref, *refs):
    g = len(refs) - 3
    p_ref, late_ref, s_ref = refs[g:]
    i = pl.program_id(0)
    for b in range(g):
        m = refs[b][0]
        top, tail = pack(m, odd_ref[i * g + b] == 1)
        for ref, here in ((p_ref, i < early), (late_ref, i >= early)):

            @pl.when(here)
            def _():
                ref[b, :192] = top.astype(bf)
                ref[b, 192:] = tail.astype(bf)

        s_ref[b] = jnp.full((8, 128), jnp.sum(m * m), f32)


def pack_master(order, odd, master, first):
    n = master.shape[0]
    g = group_of(first)
    early = first // g
    rest = max(n - first, g)
    spec = pltpu.PrefetchScalarGridSpec(
        num_scalar_prefetch=2,
        grid=(n // g,),
        in_specs=[pl.BlockSpec((1, 192, 192), lambda i, s, o, b=b: (s[i * g + b], 0, 0)) for b in range(g)],
        out_specs=[
            pl.BlockSpec((g, 288, 128), lambda i, s, o: (jnp.minimum(i, early - 1), 0, 0)),
            pl.BlockSpec((g, 288, 128), lambda i, s, o: (jnp.maximum(i - early, 0), 0, 0)),
            pl.BlockSpec((g, 8, 128), lambda i, s, o: (i, 0, 0)),
        ],
    )
    return pl.pallas_call(
        functools.partial(pack_kernel, early),
        grid_spec=spec,
        out_shape=[jax.ShapeDtypeStruct((first, 288, 128), bf), jax.ShapeDtypeStruct((rest, 288, 128), bf), jax.ShapeDtypeStruct((n, 8, 128), f32)],
        compiler_params=params(),
        name="pack_master",
    )(order, odd, *[master] * g)


def pick_kernel(at_ref, first_ref, rest_ref, o_ref, sems):
    split = first_ref.shape[0]
    for j in range(12):

        @pl.when(at_ref[j] < split)
        def _():
            pltpu.make_async_copy(first_ref.at[at_ref[j]], o_ref.at[j], sems.at[j]).start()

        @pl.when(at_ref[j] >= split)
        def _():
            pltpu.make_async_copy(rest_ref.at[at_ref[j] - split], o_ref.at[j], sems.at[j]).start()

    for j in range(12):
        pltpu.make_async_copy(first_ref.at[0], o_ref.at[j], sems.at[j]).wait()


def pick(at, first, rest):
    return pl.pallas_call(
        pick_kernel,
        in_specs=[smem_spec(), any_spec(), any_spec()],
        out_specs=vmem_spec(),
        out_shape=jax.ShapeDtypeStruct((12, 288, 128), bf),
        scratch_shapes=[pltpu.SemaphoreType.DMA((12,))],
        compiler_params=params(),
        name="pick_qkv_blocks",
    )(at, first, rest)


def qkv_kernel(src_ref, cnt_ref, at_ref, x0, x1, x2, x3, blk_ref, gain_ref, shift_ref, bq_ref, bv_ref, a_ref, q_ref, qt_ref, k_ref, kt_ref, v_ref, vt_ref, w_ref, st_ref):
    i = pl.program_id(0)

    @pl.when(i == 0)
    def _():
        odd = at_ref[0] == 1
        for r in range(4):
            parts = []
            for c in range(3):
                p = blk_ref[r * 3 + c].astype(f32)
                parts.append(unpack(p[:192], p[192:], odd))
            w_ref[r * 192 : (r + 1) * 192, :] = jnp.concatenate(parts, axis=1).astype(bf)

    x = jnp.concatenate([r[...] for r in (x0, x1, x2, x3)], axis=0).astype(f32)
    mean = jnp.mean(x, axis=-1, keepdims=True)
    cen = x - mean
    inv_std = lax.rsqrt(jnp.mean(cen * cen, axis=-1, keepdims=True) + EPS_NORM)
    a = (cen * inv_std * gain_ref[...] + shift_ref[...]).astype(bf)
    a_ref[...] = a
    qkv = mm(a, w_ref[...])
    q = (qkv[:, :192] + bq_ref[...]).astype(bf).astype(f32)
    k = qkv[:, 192:384].astype(bf).astype(f32)
    v = (qkv[:, 384:] + bv_ref[...]).astype(bf).astype(f32)
    row = lax.broadcasted_iota(jnp.int32, (128, 64), 0)
    lane = lax.broadcasted_iota(jnp.int32, (512, 64), 1)
    masked = jnp.concatenate(
        [jnp.where(row < cnt_ref[4 * i + b], 0.0, NEG_RAW) for b in range(4)], axis=0
    )
    ones = jnp.where(lane < 4, 1.0, 0.0)
    k_tail = jnp.where(lane == 0, masked, ones)
    v_tail = jnp.where(lane < 3, 1.0, 0.0)
    zero = jnp.zeros((512, 64), f32)
    sub = lax.broadcasted_iota(jnp.int32, (64, 512), 0)
    t_tail = jnp.where(sub < 1, 1.0, 0.0)
    qt, kt, vt = q.T, k.T, v.T
    longest = lambda a: jnp.max(jnp.concatenate([column_sum(a[h * 64 : (h + 1) * 64] ** 2) for h in range(3)], axis=0))
    st_ref[0] = jnp.where(lax.broadcasted_iota(jnp.int32, (8, 128), 0) == 0, longest(qt), longest(kt))
    for h in range(3):
        s = slice(h * 64, (h + 1) * 64)
        q_ref[h] = jnp.concatenate([q[:, s], zero], axis=1).astype(bf)
        k_ref[h] = jnp.concatenate([k[:, s], k_tail], axis=1).astype(bf)
        v_ref[h] = jnp.concatenate([v[:, s], v_tail], axis=1).astype(bf)
        qt_ref[h] = jnp.concatenate([qt[s], t_tail], axis=0).astype(bf)
        kt_ref[h] = kt[s].astype(bf)
        vt_ref[h] = jnp.concatenate([vt[s], t_tail[:16]], axis=0).astype(bf)


def qkv_forward(src, cnt, odd, tokens, blocks, gain, shift, bq, bv):
    n = tokens.shape[0]
    rows = [pl.BlockSpec((128, 768), lambda i, s, c, o, k=k: (s[4 * i + k], 0)) for k in range(4)]
    row = lambda i, s, c, o: (0, 0)
    spec = pltpu.PrefetchScalarGridSpec(
        num_scalar_prefetch=3,
        grid=(n // 512,),
        in_specs=rows
        + [pl.BlockSpec((12, 288, 128), lambda i, s, c, o: (0, 0, 0)), pl.BlockSpec((1, 768), row), pl.BlockSpec((1, 768), row), pl.BlockSpec((1, 192), row), pl.BlockSpec((1, 192), row)],
        out_specs=[
            pl.BlockSpec((512, 768), lambda i, s, c, o: (i, 0)),
            pl.BlockSpec((3, 512, 128), lambda i, s, c, o: (0, i, 0)),
            pl.BlockSpec((3, 128, 512), lambda i, s, c, o: (0, 0, i)),
            pl.BlockSpec((3, 512, 128), lambda i, s, c, o: (0, i, 0)),
            pl.BlockSpec((3, 64, 512), lambda i, s, c, o: (0, 0, i)),
            pl.BlockSpec((3, 512, 128), lambda i, s, c, o: (0, i, 0)),
            pl.BlockSpec((3, 80, 512), lambda i, s, c, o: (0, 0, i)),
            pl.BlockSpec((768, 576), row),
            pl.BlockSpec((1, 8, 128), lambda i, s, c, o: (i, 0, 0)),
        ],
    )
    shapes = [(n, 768), (3, n, 128), (3, 128, n), (3, n, 128), (3, 64, n), (3, n, 128), (3, 80, n), (768, 576)]
    return pl.pallas_call(
        qkv_kernel,
        grid_spec=spec,
        out_shape=[jax.ShapeDtypeStruct(s, bf) for s in shapes] + [jax.ShapeDtypeStruct((n // 512, 8, 128), f32)],
        compiler_params=params(),
        name="norm_and_qkv",
    )(src, cnt, odd, tokens, tokens, tokens, tokens, blocks, gain, shift, bq, bv)


def split3(v):
    a = v.astype(bf).astype(f32)
    b = (v - a).astype(bf).astype(f32)
    return a, b, v - a - b


def in_steps(units, sizes, body, carry):
    at = 0
    for size in sizes:
        count = (units - at) // size
        carry = lax.fori_loop(0, count, lambda i, c, at=at, size=size: body(at + i * size, size, c), carry)
        at = at + count * size
    return carry


def attend_kernel(bq, n_ref, k_ref, qt_ref, vt_ref, ot_ref, qb_ref, p_ref, rt_ref):
    live = n_ref[0]
    qi = pl.program_id(1)
    pairs = (live + 7) // 8 * 4

    def finish(top, acc):
        total = acc[64:65]
        ot_ref[0] = acc[:64] / total
        rt_ref[0] = 1.0 / total
        a, b, c = split3((top + jnp.log2(total)) * (-1.0 / EXP2))
        row = lax.broadcasted_iota(jnp.int32, (64, bq), 0)
        tail = jnp.where(row == 0, 1.0, jnp.where(row == 1, a, jnp.where(row == 2, b, jnp.where(row == 3, c, 0.0))))
        qb_ref[0, :64] = qt_ref[0, :64]
        qb_ref[0, 64:] = tail.astype(bf)

    def keys(u, size):
        return pl.ds(pl.multiple_of(u * 256, 256), size * 256)

    @pl.when(jnp.logical_and(qi * bq < live * 128, n_ref[1] == 1))
    def _():
        qt = qt_ref[0]

        def body(u, size, acc):
            step = min(size, 2)
            for part in range(0, size, step):
                at = keys(u + part, step)
                p = jnp.exp2(mm(k_ref[0, at, :], qt) * EXP2).astype(bf)
                p_ref[0, at, :] = p
                acc = acc + mm(vt_ref[0, :, at], p)
            return acc

        finish(0.0, in_steps(pairs, (16, 8, 4), body, jnp.zeros((80, bq), f32)))

    @pl.when(jnp.logical_and(qi * bq < live * 128, n_ref[1] == 0))
    def _():
        qt = qt_ref[0]

        def body(u, size, carry):
            top, acc = carry
            s = mm(k_ref[0, keys(u, size), :], qt) * EXP2
            new = jnp.maximum(top, jnp.max(s, axis=0, keepdims=True))
            p = jnp.exp2(s - new).astype(bf)
            return new, acc * jnp.exp2(top - new) + mm(vt_ref[0, :, keys(u, size)], p)

        finish(*in_steps(pairs, (4,), body, (jnp.full((1, bq), -3e38, f32), jnp.zeros((80, bq), f32))))


def attend(live, k, qt, vt, bq=1024):
    n = k.shape[1]
    spec = pltpu.PrefetchScalarGridSpec(
        num_scalar_prefetch=1,
        grid=(3, n // bq),
        in_specs=[
            pl.BlockSpec((1, n, 128), lambda h, i, s: (h, 0, 0)),
            pl.BlockSpec((1, 128, bq), lambda h, i, s: (h, 0, i)),
            pl.BlockSpec((1, 80, n), lambda h, i, s: (h, 0, 0)),
        ],
        out_specs=[
            pl.BlockSpec((1, 64, bq), lambda h, i, s: (h, 0, i)),
            pl.BlockSpec((1, 128, bq), lambda h, i, s: (h, 0, i)),
            pl.BlockSpec((1, n, bq), lambda h, i, s: (h, 0, i)),
            pl.BlockSpec((1, 1, bq), lambda h, i, s: (h, 0, i)),
        ],
    )
    return pl.pallas_call(
        functools.partial(attend_kernel, bq),
        grid_spec=spec,
        out_shape=[
            jax.ShapeDtypeStruct((3, 64, n), f32),
            jax.ShapeDtypeStruct((3, 128, n), bf),
            jax.ShapeDtypeStruct((3, n, n), bf),
            jax.ShapeDtypeStruct((3, 1, n), f32),
        ],
        compiler_params=params(),
        name="attention_forward",
    )(live, k, qt, vt)


def spread_kernel(src_ref, n_ref, t_ref, ot_ref, *o_refs):
    live, t, tiles = n_ref[0], t_ref[0], len(o_refs)
    per = o_refs[0].shape[1] // 128

    def step(b, _):
        g = src_ref[b]
        lanes = pl.ds(pl.multiple_of(b * 128, 128), 128)
        to = pl.ds(pl.multiple_of((g % per) * 128, 128), 128)
        for k in range(tiles):
            here = (g // per - t + tiles) % tiles == k

            @pl.when(jnp.logical_and(here, b < live))
            def _():
                for h in range(3):
                    o_refs[k][h * 64 : (h + 1) * 64, to] = ot_ref[h, :, lanes].astype(bf)

            @pl.when(jnp.logical_and(here, b >= live))
            def _():
                o_refs[k][:, to] = jnp.zeros((192, 128), bf)

        return 0

    lax.fori_loop(0, ot_ref.shape[2] // 128, step, 0)


def spread(src, live, tile, ot, tiles):
    n = ot.shape[2]
    return pl.pallas_call(
        spread_kernel,
        in_specs=[smem_spec()] * 3 + [vmem_spec()],
        out_specs=[vmem_spec()] * tiles,
        out_shape=[jax.ShapeDtypeStruct((192, n // tiles), bf)] * tiles,
        compiler_params=params(),
        name="spread_attended",
    )(src, live, tile, ot)


def collect_kernel(src_ref, n_ref, t_ref, ot_ref, rt_ref, *refs):
    g_refs, (dt_ref, d_ref) = refs[:-2], refs[-2:]
    live, t, tiles = n_ref[0], t_ref[0], len(g_refs)
    mild = n_ref[1] == 1
    per = g_refs[0].shape[1] // 128
    row = lax.broadcasted_iota(jnp.int32, (64, 128), 0)

    def step(b, _):
        g = src_ref[b]
        to = pl.ds(pl.multiple_of(b * 128, 128), 128)
        lanes = pl.ds(pl.multiple_of((g % per) * 128, 128), 128)
        for k in range(tiles):

            @pl.when(jnp.logical_and((t - g // per + tiles) % tiles == k, b < live))
            def _():
                for h in range(3):
                    scale = jnp.where(mild, rt_ref[h, :, to], 1.0)
                    d = (g_refs[k][h * 64 : (h + 1) * 64, lanes].astype(f32) * scale).astype(bf).astype(f32)
                    x, y, z = split3(-jnp.sum(d * ot_ref[h, :, to], axis=0, keepdims=True))
                    tail = jnp.where(row == 0, x, jnp.where(row == 1, y, jnp.where(row == 2, z, 0.0)))
                    dt_ref[h, :, to] = jnp.concatenate([d, tail], axis=0).astype(bf)
                    d_ref[h, to, :] = jnp.concatenate([d, jnp.zeros_like(d)], axis=0).T.astype(bf)

        @pl.when(b >= live)
        def _():
            dt_ref[:, :, to] = jnp.zeros((3, 128, 128), bf)
            d_ref[:, to, :] = jnp.zeros((3, 128, 128), bf)

        return 0

    lax.fori_loop(0, ot_ref.shape[2] // 128, step, 0)


def collect(src, live, tile, grads, ot, rt):
    n = ot.shape[2]
    return pl.pallas_call(
        collect_kernel,
        in_specs=[smem_spec()] * 3 + [vmem_spec()] * (2 + len(grads)),
        out_specs=[vmem_spec()] * 2,
        out_shape=[jax.ShapeDtypeStruct((3, 128, n), bf), jax.ShapeDtypeStruct((3, n, 128), bf)],
        compiler_params=params(),
        name="collect_attended_grad",
    )(src, live, tile, ot, rt, *grads)


def attend_back_kernel(bk, n_ref, p_ref, k_ref, kt_ref, v_ref, qb_ref, q_ref, dt_ref, d_ref, dq_ref, dk_ref, dv_ref):
    live = n_ref[0]
    j = pl.program_id(1)

    @pl.when(j == 0)
    def _():
        dq_ref[...] = jnp.zeros_like(dq_ref)

    def lanes(u):
        return pl.ds(pl.multiple_of(u * 256, 256), 256)

    pairs = (live + 1) // 2

    def over_queries(rows, sizes, body):
        zero = jnp.zeros((rows, 128), f32)
        dk, dv = in_steps((live + 7) // 8 * 4, sizes, body, (zero, zero))
        dk_ref[0, :rows] = (dk * SCALE).astype(bf)
        dv_ref[0, :rows] = dv.astype(bf)

    def with_kept(rows):
        k, v, kt = k_ref[0, :rows], v_ref[0, :rows], kt_ref[0, :, :rows]

        def body(u, size, carry):
            dk, dv = carry
            dp = mm(v, dt_ref[0, :, lanes(u)])
            for part in range(size):
                at = lanes(u + part)
                ahead = mm(v, dt_ref[0, :, lanes(u + part + 1)]) if part + 1 < size else None
                p = p_ref[0, :rows, at]
                ds = (p.astype(f32) * dp).astype(bf)
                dv = dv + mm(p, d_ref[0, at, :])
                dk = dk + mm(ds, q_ref[0, at, :])
                dq_ref[0, :, at] += mm(kt, ds)
                dp = dp if ahead is None else ahead
            return dk, dv

        over_queries(rows, (16, 8, 4), body)

    @pl.when(jnp.logical_and(n_ref[1] == 1, 2 * j + 2 <= pairs))
    def _():
        with_kept(bk)

    @pl.when(jnp.logical_and(n_ref[1] == 1, 2 * j + 1 == pairs))
    def _():
        dk_ref[0, bk // 2 :] = jnp.zeros((bk // 2, 128), bf)
        dv_ref[0, bk // 2 :] = jnp.zeros((bk // 2, 128), bf)
        with_kept(bk // 2)

    @pl.when(jnp.logical_and(n_ref[1] == 0, j * bk < live * 128))
    def _():
        k, v, kt = k_ref[0], v_ref[0], kt_ref[0]

        def body(u, size, carry):
            dk, dv = carry
            for part in range(size):
                at = lanes(u + part)
                p = jnp.exp2(mm(k, qb_ref[0, :, at]) * EXP2)
                ds = (p * mm(v, dt_ref[0, :, at])).astype(bf)
                dv = dv + mm(p.astype(bf), d_ref[0, at, :])
                dk = dk + mm(ds, q_ref[0, at, :])
                dq_ref[0, :, at] += mm(kt, ds)
            return dk, dv

        over_queries(bk, (4,), body)


def attend_back(first, heads, live, p, k, kt, v, qb, q, dt, d, bk=512):
    n = k.shape[1]
    whole_t = lambda h, j, s: (first + h, 0, 0)
    rows = lambda h, j, s: (first + h, j, 0)
    spec = pltpu.PrefetchScalarGridSpec(
        num_scalar_prefetch=1,
        grid=(heads, n // bk),
        in_specs=[
            pl.BlockSpec((1, bk, n), rows),
            pl.BlockSpec((1, bk, 128), rows),
            pl.BlockSpec((1, 64, bk), lambda h, j, s: (first + h, 0, j)),
            pl.BlockSpec((1, bk, 128), rows),
            pl.BlockSpec((1, 128, n), whole_t),
            pl.BlockSpec((1, n, 128), whole_t),
            pl.BlockSpec((1, 128, n), whole_t),
            pl.BlockSpec((1, n, 128), whole_t),
        ],
        out_specs=[
            pl.BlockSpec((1, 64, n), lambda h, j, s: (h, 0, 0)),
            pl.BlockSpec((1, bk, 128), lambda h, j, s: (h, j, 0)),
            pl.BlockSpec((1, bk, 128), lambda h, j, s: (h, j, 0)),
        ],
    )
    S = jax.ShapeDtypeStruct
    return pl.pallas_call(
        functools.partial(attend_back_kernel, bk),
        grid_spec=spec,
        out_shape=[S((heads, 64, n), f32), S((heads, n, 128), bf), S((heads, n, 128), bf)],
        cost_estimate=pl.CostEstimate(flops=heads * 4 * 10**10, bytes_accessed=heads * 50 * 10**6, transcendentals=0),
        compiler_params=params(),
        name="attention_backward",
    )(live, p, k, kt, v, qb, q, dt, d)


def qkv_back_kernel(given, src_ref, n_ref, odd_ref, x0, x1, x2, x3, gain_ref, a_ref, w_ref, *refs):
    grads, (ga_ref, gz_ref, gw_ref, gb_ref, vs_ref, acc, sums, rows, sems) = refs[:given], refs[given:]
    dqs, dks, dvs = [[(r, h) for r in grads[j::3] for h in range(r.shape[0])] for j in range(3)]
    early = ga_ref.shape[1] // 128
    i = pl.program_id(0)
    live = n_ref[0]

    @pl.when(i == 0)
    def _():
        acc[...] = jnp.zeros_like(acc)
        sums[...] = jnp.zeros_like(sums)
        vs_ref[...] = jnp.zeros_like(vs_ref)

    @pl.when(4 * i < live)
    def _():
        dq = jnp.concatenate([r[h] for r, h in dqs], axis=0).T * SCALE
        g = jnp.concatenate([dq] + [r[h][:, :64].astype(f32) for r, h in dks + dvs], axis=1).astype(bf)
        acc[...] += mm(a_ref[...], g, TN)
        sums[...] += jnp.broadcast_to(column_sum(g.astype(f32)), sums.shape)
        g1 = mm(g, w_ref[...], NT)
        rows[...] = g1.astype(bf)
        x = jnp.concatenate([r[...] for r in (x0, x1, x2, x3)], axis=0).astype(f32)
        cen = x - jnp.mean(x, axis=-1, keepdims=True)
        normed = cen * lax.rsqrt(jnp.mean(cen * cen, axis=-1, keepdims=True) + EPS_NORM)
        vs_ref[0:1, :] += column_sum(g1 * normed)
        vs_ref[1:2, :] += column_sum(g1)

    @pl.when(4 * i >= live)
    def _():
        rows[...] = jnp.zeros_like(rows)

    per = early + gz_ref.shape[1] // 128
    for b in range(4):
        block, at = rows.at[pl.ds(b * 128, 128)], src_ref[4 * i + b]
        t, j = at // per, at % per

        @pl.when(j < early)
        def _():
            pltpu.make_async_copy(block, ga_ref.at[t, pl.ds(pl.multiple_of(j * 128, 128), 128)], sems.at[b]).start()

        @pl.when(j >= early)
        def _():
            pltpu.make_async_copy(block, gz_ref.at[t, pl.ds(pl.multiple_of((j - early) * 128, 128), 128)], sems.at[b]).start()

    for b in range(4):
        pltpu.make_async_copy(rows.at[pl.ds(b * 128, 128)], ga_ref.at[0, pl.ds(0, 128)], sems.at[b]).wait()

    @pl.when(i == pl.num_programs(0) - 1)
    def _():
        for r in range(4):
            for c in range(3):
                top, tail = pack(acc[r * 192 : (r + 1) * 192, c * 192 : (c + 1) * 192], odd_ref[0] == 1)
                gw_ref[r * 3 + c, :192] = top.astype(bf)
                gw_ref[r * 3 + c, 192:] = tail.astype(bf)
        gb_ref[...] = sums[...]


def qkv_backward(src, live, odd, tokens, gain, a, w, grads, tiles, early):
    n = a.shape[0]
    per = n // tiles
    fixed = lambda i, s, c, o: (0, 0)
    row = lambda i, s, c, o: (0, i, 0)
    spec = pltpu.PrefetchScalarGridSpec(
        num_scalar_prefetch=3,
        grid=(n // 512,),
        in_specs=[pl.BlockSpec((128, 768), lambda i, s, c, o, k=k: (s[4 * i + k], 0)) for k in range(4)]
        + [pl.BlockSpec((1, 768), fixed), pl.BlockSpec((512, 768), lambda i, s, c, o: (i, 0)), pl.BlockSpec((768, 576), fixed)]
        + [
            pl.BlockSpec((g.shape[0], 64, 512), lambda i, s, c, o: (0, 0, i)) if g.shape[1] == 64 else pl.BlockSpec((g.shape[0], 512, 128), row)
            for g in grads
        ],
        out_specs=[any_spec(), any_spec(), pl.BlockSpec((12, 288, 128), lambda i, s, c, o: (0, 0, 0)), pl.BlockSpec((8, 576), fixed), pl.BlockSpec((8, 768), fixed)],
        scratch_shapes=[pltpu.VMEM((768, 576), f32), pltpu.VMEM((8, 576), f32), pltpu.VMEM((512, 768), bf), pltpu.SemaphoreType.DMA((4,))],
    )
    S = jax.ShapeDtypeStruct
    return pl.pallas_call(
        functools.partial(qkv_back_kernel, len(grads)),
        grid_spec=spec,
        out_shape=[S((tiles, early, 768), bf), S((tiles, per - early, 768), bf), S((12, 288, 128), bf), S((8, 576), f32), S((8, 768), f32)],
        cost_estimate=pl.CostEstimate(flops=3 * 10**10, bytes_accessed=40 * 10**6, transcendentals=0),
        compiler_params=params(),
        name="qkv_backward",
    )(src, live, odd, tokens, tokens, tokens, tokens, gain, a, w, *grads)


def gelu_parts(z):
    cdf = 0.5 + 0.5 * lax.erf(z * math.sqrt(0.5))
    return z * cdf, cdf + z * (jnp.exp2(z * z * (-0.5 * math.log2(math.e))) * (1.0 / math.sqrt(2.0 * math.pi)))


def middle_kernel(inv_ref, cnt_ref, t_ref, blk_ref, rest_ref, o0, o1, o2, o3, x_ref, c_ref, vp_ref, bu_ref, y_ref, gr_ref, g0, g1, g2_ref, g3,
                  u_s, gz_s, a2_s, gm_s, gb_s, o_s, vs_ref, us_ref, w_out, w_up, w_down, tails, tsem, isem):
    i = pl.program_id(0)
    rows = x_ref.shape[0]
    split = blk_ref.shape[0]
    r0 = i * rows
    kinds = ((w_out, 48, 2, 4), (w_up, 64, 8, 4), (w_down, 128, 2, 16))

    @pl.when(i == 0)
    def _():
        vs_ref[...] = jnp.zeros_like(vs_ref)
        us_ref[...] = jnp.zeros_like(us_ref)

        def pair(w, first, pairs):
            def parts(j, run):
                r = pl.multiple_of((j // pairs) * 192, 64)
                col = pl.multiple_of((j % pairs) * 384, 128)
                for b, off in ((0, 0), (1, 256)):
                    at = first + 2 * j + b
                    run(at, w.at[pl.ds(r, 192), pl.ds(col + off, 128)], tails.at[at - 48])
                return r, col

            def fetch(at, top, tail):
                for ref, here, slot in ((blk_ref, inv_ref[at] < split, inv_ref[at]), (rest_ref, inv_ref[at] >= split, inv_ref[at] - split)):

                    @pl.when(here)
                    def _():
                        pltpu.make_async_copy(ref.at[slot, pl.ds(0, 192)], top, tsem.at[at - 48]).start()
                        pltpu.make_async_copy(ref.at[slot, pl.ds(192, 96)], tail, isem.at[at - 48]).start()

            def fetched(at, top, tail):
                pltpu.make_async_copy(blk_ref.at[0, pl.ds(0, 192)], top, tsem.at[at - 48]).wait()
                pltpu.make_async_copy(blk_ref.at[0, pl.ds(192, 96)], tail, isem.at[at - 48]).wait()

            def start(j, _):
                parts(j, fetch)
                return 0

            def join(j, _):
                r, col = parts(j, fetched)
                even = tails[first + 2 * j - 48].astype(f32)
                odd = tails[first + 2 * j - 47].astype(f32)
                lane = lax.broadcasted_iota(jnp.int32, even.shape, 1) < 64
                w[pl.ds(r, 96), pl.ds(col + 128, 128)] = jnp.where(lane, even, odd).astype(bf)
                w[pl.ds(r + 96, 96), pl.ds(col + 128, 128)] = turn(jnp.where(lane, odd, even)).astype(bf)
                return 0

            return start, join

        todo = [(pair(w, first, pairs), pairs * high) for w, first, pairs, high in kinds]
        for (start, _), n in todo:
            lax.fori_loop(0, n, start, 0)

        for (_, join), n in todo:
            lax.fori_loop(0, n, join, 0)

    vp = vp_ref[...]
    row = r0 + lax.broadcasted_iota(jnp.int32, (rows, 1), 0)
    live = jnp.where(row < cnt_ref[0], 1.0, 0.0)
    t = t_ref[0]
    for k, ref in enumerate((o0, o1, o2, o3)):
        o_s[pl.ds(pl.multiple_of(((t - k + 4) % 4) * 192, 64), 192), :] = ref[...]
    o_t = o_s[...]
    res = x_ref[...].astype(f32) + mm(o_t, w_out[...], TN) + vp[6:7]
    cen = res - jnp.mean(res, axis=-1, keepdims=True)
    inv_std = lax.rsqrt(jnp.mean(cen * cen, axis=-1, keepdims=True) + EPS_NORM)
    normed = cen * inv_std
    a2 = (normed * vp[2:3] + vp[3:4]).astype(bf)
    gy = c_ref[...].astype(f32) * live
    gm = gy.astype(bf)
    a2_s[...] = a2
    gm_s[...] = gm
    branch = jnp.zeros((rows, 768), f32)
    g2 = jnp.zeros((rows, 768), f32)
    for j in range(4):
        cols = slice(j * 768, (j + 1) * 768)
        u, slope = gelu_parts(mm(a2, w_up[:, cols]) + bu_ref[:, cols])
        u = u.astype(bf)
        u_s[:, cols] = u
        branch = branch + mm(u, w_down[cols, :])
        gz = (mm(gm, w_down[cols, :], NT) * slope).astype(bf)
        gz_s[:, cols] = gz
        us_ref[:, cols] += jnp.broadcast_to(column_sum(gz.astype(f32)), (8, 768))
        g2 = g2 + mm(gz, w_up[:, cols], NT)
    y_ref[...] = (live * (res + branch + vp[7:8])).astype(bf)
    d2 = g2 * vp[2:3]
    gr = gy + inv_std * (d2 - jnp.mean(d2, axis=-1, keepdims=True) - normed * jnp.mean(d2 * normed, axis=-1, keepdims=True))
    gr_ref[...] = gr
    gb = gr.astype(bf)
    gb_s[...] = gb
    vs_ref[0:1, :] += column_sum(g2 * normed)
    vs_ref[1:2, :] += column_sum(g2)
    vs_ref[2:3, :] += column_sum(gb.astype(f32))
    vs_ref[3:4, :] += column_sum(gm.astype(f32))
    for k, ref in enumerate((g0, g1, g2_ref, g3)):
        ref[...] = mm(w_out[pl.ds(pl.multiple_of(((t + k) % 4) * 192, 64), 192), :], gb, NT).astype(bf)


def weight_grad_kernel(outs, pos_ref, o_in, gb_in, a2_in, gz_in, u_in, gm_in, *refs):
    s_refs, (o_s, gb_s, a2_s, gz_s, u_s, gm_s, ring, zero, lsem, osem, zsem) = refs[:outs], refs[outs:]
    each = s_refs[0].shape[0]

    def to_slot(block, at, sem):
        for o in range(outs):

            @pl.when(at // each == o)
            def _():
                pltpu.make_async_copy(block, s_refs[o].at[at % each], sem).start()

    def landed(block, sem):
        pltpu.make_async_copy(block, s_refs[0].at[0], sem).wait()

    loads = [pltpu.make_async_copy(a, b, lsem.at[j]) for j, (a, b) in enumerate(
        ((o_in, o_s), (gb_in, gb_s), (a2_in, a2_s), (gz_in, gz_s), (gm_in, gm_s), (u_in, u_s)))]
    for load in loads:
        load.start()
    zero[...] = jnp.zeros_like(zero)

    def clear(j, _):
        to_slot(zero, pos_ref[j], zsem.at[j])
        return 0

    lax.fori_loop(0, 48, clear, 0)
    def send(n, g, first, pairs, high, low):
        half = (n % 2) * 8

        def put(r, b):
            return first + (high + r) * 2 * pairs + 2 * low + b

        for r in range(4):
            part = g[r * 192 : (r + 1) * 192]
            mid = part[:, 128:256]
            upper, lower = mid[:96], turn(mid[96:])
            lane = lax.broadcasted_iota(jnp.int32, upper.shape, 1) < 64
            for b, top, tail in ((0, part[:, :128], jnp.where(lane, upper, lower)), (1, part[:, 256:], jnp.where(lane, lower, upper))):
                k = half + 2 * r + b

                @pl.when(n >= 2)
                def _():
                    landed(ring.at[k], osem.at[k])

                ring[k, :192] = top.astype(bf)
                ring[k, 192:] = tail.astype(bf)
                to_slot(ring.at[k], pos_ref[put(r, b)], osem.at[k])

    def lanes(j):
        return pl.ds(pl.multiple_of(j * 384, 128), 384)

    def grad_out(n, _):
        send(n, mm(o_s[...], gb_s[:, lanes(n)]), 48, 2, 0, n)
        return 0

    def grad_up(n, _):
        send(n, mm(a2_s[...], gz_s[:, lanes(n)], TN), 64, 8, 0, n)
        return 0

    def grad_down(n, _):
        high = n // 2
        send(n, mm(u_s[:, pl.ds(pl.multiple_of(high * 768, 128), 768)], gm_s[:, lanes(n % 2)], TN), 128, 2, high * 4, n % 2)
        return 0

    def drain():
        for k in range(16):
            landed(ring.at[k], osem.at[k])

    for f, n, first in ((grad_out, 2, 0), (grad_up, 8, 2), (grad_down, 8, 4)):
        loads[first].wait()
        loads[first + 1].wait()
        lax.fori_loop(0, n, f, 0)
        drain()

    def cleared(j, _):
        landed(zero, zsem.at[j])
        return 0

    lax.fori_loop(0, 48, cleared, 0)


def middle(inv, count, tile, blocks, rest, o_parts, tokens, cotangent, vec_params, bias_up, rows=256):
    n, width = tokens.shape
    hidden = bias_up.shape[1]
    row = lambda i, s, c, t: (i, 0)
    fixed = lambda i, s, c, t: (0, 0)
    col = lambda i, s, c, t: (0, i)
    V, DS = pltpu.VMEM, pltpu.SemaphoreType.DMA
    narrow, wide, part = pl.BlockSpec((rows, width), row), pl.BlockSpec((rows, hidden), row), pl.BlockSpec((192, rows), col)
    spec = pltpu.PrefetchScalarGridSpec(
        num_scalar_prefetch=3,
        grid=(n // rows,),
        in_specs=[any_spec()] * 2 + [part] * 4 + [narrow, narrow, pl.BlockSpec((12, width), fixed), pl.BlockSpec((1, hidden), fixed)],
        out_specs=[narrow, narrow] + [part] * 4 + [wide, wide, narrow, narrow, narrow, pl.BlockSpec((width, rows), col),
                   pl.BlockSpec((8, width), fixed), pl.BlockSpec((8, hidden), fixed)],
        scratch_shapes=[V((768, 768), bf), V((768, 3072), bf), V((3072, 768), bf), V((144, 96, 128), bf), DS((144,)), DS((144,))],
    )
    S = jax.ShapeDtypeStruct
    return pl.pallas_call(
        middle_kernel,
        grid_spec=spec,
        out_shape=[S((n, width), bf), S((n, width), f32)] + [S((192, n), bf)] * 4 + [S((n, hidden), bf)] * 2 + [S((n, width), bf)] * 3
        + [S((width, n), bf), S((8, width), f32), S((8, hidden), f32)],
        compiler_params=params(),
        name="projection_and_mlp",
    )(inv, count, tile, blocks, rest, *o_parts, tokens, cotangent, vec_params, bias_up)


def weight_grads_to_slots(pos, outs, block_count, o_t, gb, a2, gz, u, gm):
    V, DS = pltpu.VMEM, pltpu.SemaphoreType.DMA
    arrays = (o_t, gb, a2, gz, u, gm)
    return pl.pallas_call(
        functools.partial(weight_grad_kernel, outs),
        in_specs=[smem_spec()] + [any_spec()] * 6,
        out_specs=[any_spec()] * outs,
        out_shape=[jax.ShapeDtypeStruct((block_count // outs, 288, 128), bf)] * outs,
        scratch_shapes=[V(a.shape, bf) for a in arrays] + [V((16, 288, 128), bf), V((288, 128), bf), DS((6,)), DS((16,)), DS((48,))],
        cost_estimate=pl.CostEstimate(flops=6 * 10**10, bytes_accessed=32 * 10**6, transcendentals=0),
        compiler_params=params(),
        name="mlp_weight_gradients",
    )(pos, *arrays)


def quarters(b0, b1):
    return (b0 * 2 + b1, (1 - b0) * 2 + b1, b0 * 2 + 1 - b1, (1 - b0) * 2 + 1 - b1)


def add_pair_kernel(common, bits_ref, *refs):
    outs = list(refs[16:])
    for p in range(2):
        for side in range(4):
            j = 4 * p + side
            total = (refs[2 * j][...].astype(f32) + refs[2 * j + 1][...].astype(f32)).astype(bf)
            if side == common[p]:
                outs[6][p] = total
            else:
                outs[3 * p + side - (side > common[p])][...] = total


def add_pair(bits, common, keep, came):
    specs = []
    for p in range(2):
        for side in range(4):
            at = lambda i, b, p=p, side=side: (p * 12 + quarters(b[2 * p], b[2 * p + 1])[side] * 3 + i, 0, 0)
            specs += [pl.BlockSpec((4, 288, 128), at)] * 2
    S = jax.ShapeDtypeStruct
    return pl.pallas_call(
        functools.partial(add_pair_kernel, common),
        grid_spec=pltpu.PrefetchScalarGridSpec(
            num_scalar_prefetch=1,
            grid=(3,),
            in_specs=specs,
            out_specs=[pl.BlockSpec((4, 288, 128), lambda i, b: (i, 0, 0))] * 6 + [pl.BlockSpec((2, 4, 288, 128), lambda i, b: (0, i, 0, 0))],
        ),
        out_shape=[S((12, 288, 128), bf)] * 6 + [S((2, 12, 288, 128), bf)],
        compiler_params=params(),
        name="add_gradients_of_cores",
    )(bits, *[keep, came] * 8)


def add_four_kernel(common, bits_ref, *refs):
    outs = refs[7:]
    for p in range(2):
        parts = refs[3 * p : 3 * p + 3]
        for side, q in enumerate(quarters(bits_ref[2 * p], bits_ref[2 * p + 1])):
            for b in range(3):
                total = (sum(r[q * 3 + b].astype(f32) for r in parts) + refs[6][p, q * 3 + b].astype(f32)).astype(bf)
                if side == common[p]:
                    outs[6][p, b] = total
                else:
                    outs[3 * p + side - (side > common[p])][b] = total


def add_four(bits, common, parts):
    S = jax.ShapeDtypeStruct
    return pl.pallas_call(
        functools.partial(add_four_kernel, common),
        in_specs=[smem_spec()] + [vmem_spec()] * 7,
        out_specs=[vmem_spec()] * 7,
        out_shape=[S((3, 288, 128), bf)] * 6 + [S((2, 3, 288, 128), bf)],
        compiler_params=params(),
        name="add_gradients",
    )(bits, *parts)


def add_last_kernel(*refs):
    for p in range(2):
        for b in range(3):
            refs[7][3 * p + b] = (sum(r[b].astype(f32) for r in refs[3 * p : 3 * p + 3]) + refs[6][p, b].astype(f32)).astype(bf)


def add_last(parts):
    return pl.pallas_call(
        add_last_kernel,
        in_specs=[vmem_spec()] * 7,
        out_specs=vmem_spec(),
        out_shape=jax.ShapeDtypeStruct((6, 288, 128), bf),
        compiler_params=params(),
        name="add_last_gradients",
    )(*parts)


def split2(v):
    hi = v.astype(bf)
    return hi, (v - hi.astype(f32)).astype(bf)


def mm3(a, b, dims):
    return mm(a[0], b[0], dims) + (mm(a[0], b[1], dims) + mm(a[1], b[0], dims))


def adam_kernel(odd_ref, from_ref, g_ref, late_ref, m1_ref, m2_ref, l_ref, r_ref, g_out, m1_out, m2_out, u_out, s_out):
    for b in range(g_ref.shape[0]):
        slot = pl.program_id(0) * g_ref.shape[0] + b
        place = from_ref[slot]
        part = jnp.where(place >= 0, late_ref[jnp.maximum(place, 0)].astype(f32), g_ref[b].astype(f32))
        grad = unpack(part[:192], part[192:], odd_ref[slot] == 1)
        left, right = split2(l_ref[b]), split2(r_ref[b])
        low = grad.astype(bf)
        rot = mm3(split2(mm(left[0], low, TN) + mm(left[1], low, TN)), right, NN)
        first = BETA_ONE * m1_ref[b] + (1.0 - BETA_ONE) * rot
        second = BETA_TWO * m2_ref[b] + (1.0 - BETA_TWO) * rot * rot
        upd = (first / (1.0 - BETA_ONE**STEP)) / (jnp.sqrt(second / (1.0 - BETA_TWO**STEP)) + ADAM_EPS)
        upd = mm3(split2(mm3(left, split2(upd), NN)), right, NT)
        g_out[b] = grad
        m1_out[b] = first
        m2_out[b] = second
        u_out[b] = upd
        s_out[b] = jnp.full((8, 128), jnp.sum(upd * upd), f32)


def adam(odd, late_at, grads, late, first, second, left, right):
    n = grads.shape[0]
    g = group_of(n)
    at = lambda i, s, f: (i, 0, 0)
    big = pl.BlockSpec((g, 192, 192), at)
    spec = pltpu.PrefetchScalarGridSpec(
        num_scalar_prefetch=2,
        grid=(n // g,),
        in_specs=[pl.BlockSpec((g, 288, 128), at), pl.BlockSpec(late.shape, lambda i, s, f: (0, 0, 0))] + [big] * 4,
        out_specs=[big] * 4 + [pl.BlockSpec((g, 8, 128), at)],
    )
    return pl.pallas_call(
        adam_kernel,
        grid_spec=spec,
        out_shape=[jax.ShapeDtypeStruct((n, 192, 192), f32)] * 4 + [jax.ShapeDtypeStruct((n, 8, 128), f32)],
        compiler_params=params(),
        name="rotated_adam",
    )(odd, late_at, grads, late, first, second, left, right)


def update_kernel(rate_ref, m_ref, u_ref, mo_ref, mc_ref):
    g = m_ref.shape[0]
    for b in range(g):
        new = m_ref[b] - rate_ref[pl.program_id(0) * g + b] * u_ref[b]
        mo_ref[b] = new
        mc_ref[b] = new.astype(bf)


def new_weights(rate, master, update):
    n = master.shape[0]
    g = group_of(n)
    big = pl.BlockSpec((g, 192, 192), lambda i, r: (i, 0, 0))
    return pl.pallas_call(
        update_kernel,
        grid_spec=pltpu.PrefetchScalarGridSpec(num_scalar_prefetch=1, grid=(n // g,), in_specs=[big] * 2, out_specs=[big] * 2),
        out_shape=[jax.ShapeDtypeStruct(master.shape, f32), jax.ShapeDtypeStruct(master.shape, bf)],
        compiler_params=params(),
        name="new_weights",
    )(rate, master, update)


def halving_places(slot, core):
    dp, r = slot // 24, slot % 24
    y, z, far, x, s = dp % 2, dp // 2 % 2, dp // 4, r % 6 // 3, r % 3
    portion = r % 12 // 6
    inside = jnp.where(portion == 0, x * 8 + y * 4 + z * 2 + far, y * 8 + z * 4 + x * 2 + far)
    return jnp.where(r // 12 == core, 0, 96) + portion * 48 + inside * 3 + s


def norm_forward(row_data, gain_vec, shift_vec):
    row_mean = jnp.mean(row_data, axis=-1, keepdims=True)
    centred = row_data - row_mean
    inv_std = lax.rsqrt(jnp.mean(centred * centred, axis=-1, keepdims=True) + EPS_NORM)
    normed = centred * inv_std
    return (normed * gain_vec + shift_vec, normed, inv_std)


def norm_back(grad_out, normed, inv_std, gain_vec):
    grad_normed = grad_out * gain_vec
    return inv_std * (
        grad_normed
        - jnp.mean(grad_normed, axis=-1, keepdims=True)
        - normed * jnp.mean(grad_normed * normed, axis=-1, keepdims=True)
    )


def block_plan(counts, slot_count):
    tiles = counts.shape[0]
    per = slot_count // 128
    j = lax.broadcasted_iota(jnp.int32, (tiles, per), 1)
    kept = jnp.clip(counts[:, None] - j * 128, 0, 128).reshape(-1)
    full = (kept > 0).astype(jnp.int32)
    index = jnp.arange(tiles * per, dtype=jnp.int32)
    before = (index[None, :] < index[:, None]).astype(jnp.int32)
    ahead = jnp.sum(before * full[None, :], axis=1)
    live = jnp.sum(full)
    place = jnp.where(full > 0, ahead, live + index - ahead)
    hot = (place[None, :] == index[:, None]).astype(jnp.int32)
    return jnp.sum(hot * index[None, :], axis=1), jnp.sum(hot * kept[None, :], axis=1), live.reshape(1)


def make_body(tuned):
    def body(tokens, cotangent, counts, master, slot_block, groups, first_moment, second_moment, left_basis, right_basis, vec_params, vec_first, vec_second):
        slot_count, width = tokens.shape[1:]
        per_owner = master.shape[0]
        tile = lax.axis_index("tile")
        block_count = slot_block.shape[0]
        first = per_owner // 2 if tuned else per_owner
        index = jnp.arange(block_count, dtype=jnp.int32)
        owner = index // per_owner
        same = (owner[None, :] == owner[:, None]).astype(jnp.int32)
        is_qkv = (slot_block < 48).astype(jnp.int32)
        sooner = same * jnp.where(is_qkv[None, :] == is_qkv[:, None], (index[None, :] < index[:, None]).astype(jnp.int32), is_qkv[None, :])
        rank = jnp.sum(sooner, axis=1)
        place = jnp.where(rank < first, owner * first + rank, block_count // per_owner * first + owner * (per_owner - first) + rank - first)
        most = jnp.max(jnp.sum(same * is_qkv[None, :], axis=1))
        start = lax.axis_index("dp") * per_owner
        mine = lax.dynamic_slice(slot_block, (start,), (per_owner,))
        odd = mine % 2
        local = jnp.arange(per_owner, dtype=jnp.int32)
        at_rank = (lax.dynamic_slice(rank, (start,), (per_owner,))[None, :] == local[:, None]).astype(jnp.int32)
        order = jnp.sum(at_rank * local[None, :], axis=1)
        packed, packed_rest, weight_sq = pack_master(order, jnp.sum(at_rank * odd[None, :], axis=1), master, first)
        own_tokens = tokens.reshape(slot_count, width)
        count_tile = jnp.broadcast_to(counts.reshape(1, 1), (8, 128))
        if tuned:
            blocks, token_all, count_all = gather_all(packed, own_tokens, count_tile)
            packed_rest, blocks = lax.optimization_barrier((packed_rest, blocks))
            blocks_rest = lax.all_gather(packed_rest, "dp", axis=0, tiled=True)
        else:
            blocks = lax.all_gather(packed, "dp", axis=0, tiled=True)
            token_all = lax.all_gather(own_tokens, "tile", axis=0)
            count_all = lax.all_gather(count_tile, "tile", axis=0)
            blocks_rest = packed_rest
        tiles = token_all.shape[0]
        src, cnt, live = block_plan(count_all[:, 0, 0], slot_count)
        is_at = (slot_block[None, :] == index[:, None]).astype(jnp.int32)
        inverse = jnp.sum(is_at * index[None, :], axis=1)
        places = jnp.sum(is_at * place[None, :], axis=1)
        own_block = jnp.arange(12, dtype=jnp.int32) // 3 * 12 + jnp.arange(12, dtype=jnp.int32) % 3 * 4 + tile
        own_at = jnp.sum((slot_block[None, :] == own_block[:, None]).astype(jnp.int32) * place[None, :], axis=1)
        if tuned:
            qkv_blocks = lax.cond(
                most <= first,
                lambda: pick(own_at, blocks, packed_rest),
                lambda: pick(own_at, blocks, lax.all_gather(packed_rest, "dp", axis=0, tiled=True)),
            )
        else:
            qkv_blocks = pick(own_at, blocks, blocks_rest)
        tile_one = tile.astype(jnp.int32).reshape(1)
        own = width // tiles
        bias = lambda row: lax.dynamic_slice(vec_params[row : row + 1], (0, tile * own), (1, own))
        a1, q, qt, k, kt, v, vt, w_qkv, lengths = qkv_forward(
            src, cnt, tile_one % 2, token_all.reshape(-1, width), qkv_blocks, vec_params[0:1], vec_params[1:2], bias(4), bias(5)
        )
        mild = jnp.sqrt(jnp.max(lengths[:, 0, 0])) * jnp.sqrt(jnp.max(lengths[:, 1, 0])) * EXP2 <= 60.0
        live = jnp.concatenate([live, mild.astype(jnp.int32).reshape(1)])
        ot, qb, p, rt = attend(live, k, qt, vt)

        def shift(parts):
            return [parts[0]] + [lax.ppermute(parts[j], "tile", [(s, (s + j) % tiles) for s in range(tiles)]) for j in range(1, tiles)]

        o_parts = shift(spread(src, live, tile_one, ot, tiles))
        output, grad_resid, *rest = middle(
            places, counts.reshape(1), tile_one, blocks, blocks_rest, o_parts, own_tokens, cotangent.reshape(slot_count, width), vec_params, vec_params[8:].reshape(1, -1)
        )
        go_parts, (u, gz, a2, gm, gb, o_t, sums, up_sums) = rest[:tiles], rest[tiles:]
        go_parts = shift(go_parts)
        back = lambda first, heads, dt: list(attend_back(first, heads, live, p, k, kt, v, qb, q, dt, d))
        if tuned:
            dp = lax.axis_index("dp")
            bit = {"x": tile // 2, "y": dp % 2, "z": dp // 2 % 2, "far": dp // 4}
            mask = {"x": 2, "y": 4, "z": 8, "far": 16}

            def flip(array, *names):
                change = sum(mask[name] for name in names)
                return lax.ppermute(array, ("dp", "tile"), [(s, s ^ change) for s in range(32)])

            def three(sums, pairs, common):
                out = []
                for p, (a, b) in enumerate(pairs):
                    ways = [(), (a,), (b,), (a, b)]
                    del ways[common[p]]
                    out += [flip(sums[3 * p + j], *way) if way else sums[3 * p + j] for j, way in enumerate(ways)]
                return out + [flip(sums[6], pairs[0][common[0] - 1])]

            def bits_of(pairs):
                return jnp.stack([bit[name] for pair in pairs for name in pair]).astype(jnp.int32)

            first, second = [("x", "y"), ("y", "z")], [("z", "far"), ("x", "far")]
            keep, send = weight_grads_to_slots(halving_places(inverse, tile % 2), 2, block_count, o_t, gb, a2, gz, u, gm)
            send, go_parts = lax.optimization_barrier((send, go_parts))
            came = lax.ppermute(send, "tile", [(s, s ^ 1) for s in range(4)])
            dt, d = collect(src, live, tile_one, go_parts, ot, rt)
            dt, came = lax.optimization_barrier((dt, came))
            sums_one = add_pair(bits_of(first), (2, 1), keep, came)
            dt, sums_one = lax.optimization_barrier((dt, sums_one))
            parts = three(sums_one, first, (2, 1))
            head_grads = back(0, 2, dt)
            head_grads[0], parts = lax.optimization_barrier((head_grads[0], parts))
            sums_two = add_four(bits_of(second), (2, 2), parts)
            dt, sums_two = lax.optimization_barrier((dt, sums_two))
            parts = three(sums_two, second, (2, 2))
            head_grads += back(2, 1, dt)
            head_grads[3], parts = lax.optimization_barrier((head_grads[3], parts))
            mine_early = add_last(parts)
            head_grads[3], mine_early = lax.optimization_barrier((head_grads[3], mine_early))
            over_early = flip(mine_early, "x")
        else:
            slots = weight_grads_to_slots(inverse, 1, block_count, o_t, gb, a2, gz, u, gm)[0]
            dt, d = collect(src, live, tile_one, go_parts, ot, rt)
            head_grads = back(0, 3, dt)
        g_one, g_two, gw_qkv, qkv_sums, norm_sums = qkv_backward(
            src, live, tile_one % 2, token_all.reshape(-1, width), vec_params[0:1], a1, w_qkv, head_grads, tiles, slot_count * 3 // 8
        )
        if tuned:
            g_one, over_early = lax.optimization_barrier((g_one, over_early))
        zero = jnp.zeros((width,), f32)
        at_own = lambda s: lax.dynamic_update_slice(zero, s, (tile * own,))
        vector_part = jnp.concatenate(
            [norm_sums[0:2], sums[0:2], at_own(qkv_sums[0, :own])[None], at_own(qkv_sums[0, 2 * own :])[None], sums[2:4], up_sums[0].reshape(-1, width)], axis=0
        )
        if tuned:
            early, late, vector_grads = last_sums(gw_qkv, mine_early, over_early, vector_part)
            g_two, early = lax.optimization_barrier((g_two, early))
        else:
            early = lax.psum(lax.psum_scatter(slots.astype(f32), "dp", scatter_dimension=0, tiled=True), "tile").astype(bf)
            late = lax.all_gather(lax.psum(gw_qkv.astype(f32), "dp").astype(bf), "tile", axis=0, tiled=True)
            vector_grads = lax.psum(vector_part, ("dp", "tile"))
        g1 = jnp.concatenate([lax.psum_scatter(part, "tile", scatter_dimension=0, tiled=False) for part in (g_one, g_two)], axis=0)
        row_input = own_tokens.astype(f32)
        _, normed_one, inv_std_one = norm_forward(row_input, vec_params[0], vec_params[1])
        input_grad = grad_resid + norm_back(g1.astype(f32), normed_one, inv_std_one, vec_params[0])
        late_at = jnp.where(mine < 48, mine % 4 * 12 + mine // 12 * 3 + mine % 12 // 4, -1)
        weight_grads, first_out, second_out, update, update_sq = adam(odd, late_at, early, late, first_moment, second_moment, left_basis, right_basis)
        group_hot = (groups[:, None] == jnp.arange(128, dtype=jnp.int32)[None, :]).astype(f32)
        weight_part = jnp.sum(jnp.sum(at_rank.astype(f32)[:, :, None] * group_hot[None], axis=1) * weight_sq[:, 0], axis=0)
        group_part = jnp.pad(jnp.stack([weight_part, jnp.sum(group_hot * update_sq[:, 0], axis=0)]), ((0, 6), (0, 0)))
        group_both = group_sum(group_part, block_count // per_owner)
        own_both = jnp.sum(group_hot[None] * group_both[:2, None, :], axis=2)
        rate = RATE_BLOCK * jnp.sqrt(own_both[0]) / (jnp.sqrt(own_both[1]) + 1e-06)
        master_out, master_copy = new_weights(rate, master, update)
        vec_first_out = BETA_ONE * vec_first + (1.0 - BETA_ONE) * vector_grads
        vec_second_out = BETA_TWO * vec_second + (1.0 - BETA_TWO) * vector_grads * vector_grads
        vec_update = (vec_first_out / (1.0 - BETA_ONE**STEP)) / (jnp.sqrt(vec_second_out / (1.0 - BETA_TWO**STEP)) + ADAM_EPS)
        return (
            output.reshape(1, slot_count, width),
            input_grad.reshape(1, slot_count, width),
            weight_grads,
            first_out,
            second_out,
            master_out,
            master_copy,
            vector_grads,
            vec_first_out,
            vec_second_out,
            vec_params - RATE_VECTOR * vec_update,
        )

    return body


def solution(mesh):
    tuned = (mesh.shape["dp"], mesh.shape["tile"]) == (8, 4)
    rows, blocks = P("dp", "tile", None), P("dp", None, None)
    return jax.shard_map(
        make_body(tuned),
        mesh=mesh,
        in_specs=(rows, rows, P("dp", "tile"), blocks, P(), P("dp"), blocks, blocks, blocks, blocks, P(), P(), P()),
        out_specs=(rows, rows, blocks, blocks, blocks, blocks, blocks, P(), P(), P(), P()),
        check_vma=False,
    )
```

```python
import functools
import math

import jax
import jax.numpy as jnp
from jax import lax
from jax.experimental import pallas as pl
from jax.experimental.pallas import tpu as pltpu
from jax.sharding import PartitionSpec as P

f32 = jnp.float32
bf = jnp.bfloat16
MESH = pl.DeviceIdType.MESH

def where_am_i():
    dp=lax.axis_index("dp"); t=lax.axis_index("tile")
    return dp//2, dp%2, t//2, t%2

def dev(z,y,x,c):
    return (z*2+y, x*2+c)

def rcopy(src,dst,ss,rs,to):
    return pltpu.make_async_remote_copy(src_ref=src,dst_ref=dst,send_sem=ss,recv_sem=rs,device_id=to,device_id_type=MESH)

def gather_kernel(own_w,own_tok,own_cnt,all_w,all_tok,all_cnt,zs,zr,ys,yr,cs,cr,ts,tr,ns,nr,ls):
    z,y,x,c=where_am_i()
    per=own_w.shape[0]
    half=per//2
    def piece(shard,cc): return all_w.at[pl.ds(shard*per+cc*half,half)]
    own=own_w.at[pl.ds(c*half,half)]
    me=z*2+y
    core=dev(z,y,x,1-c); across=dev(z,y,1-x,c); beside=dev(z,1-y,x,c)
    up=dev(jnp.minimum(z+1,3),y,x,c); down=dev(jnp.maximum(z-1,0),y,x,c)
    def src(shard,first): return own if first else piece(shard,c)
    def z_copy(zz,first,go_up):
        shard=zz*2+y
        d=(z-zz) if go_up else (zz-z)
        k=0 if go_up else 1
        return rcopy(src(shard,first),piece(shard,c),zs.at[k,d],zr.at[k,d],up if go_up else down)
    def z_arrival(zz,k,dist):
        r=piece(zz*2+y,c)
        return rcopy(r,r,zs.at[k,dist-1],zr.at[k,dist-1],up)
    def y_copy(zz,first):
        shard=zz*2+y
        return rcopy(src(shard,first),piece(shard,c),ys.at[zz],yr.at[zz],beside)
    def y_arrival(zz):
        r=piece(zz*2+1-y,c)
        return rcopy(r,r,ys.at[zz],yr.at[zz],beside)
    def c_copy(shard): return rcopy(piece(shard,c),piece(shard,c),cs.at[shard],cr.at[shard],core)
    def c_arrival(shard): return rcopy(piece(shard,1-c),piece(shard,1-c),cs.at[shard],cr.at[shard],core)
    tile=x*2+c
    tok_x=rcopy(own_tok,all_tok.at[tile],ts.at[0],tr.at[0],across)
    tok_c=rcopy(own_tok,all_tok.at[tile],ts.at[1],tr.at[1],core)
    far=all_tok.at[(1-x)*2+c]
    tok_f=rcopy(far,far,ts.at[2],tr.at[2],core)
    near=all_tok.at[x*2+1-c]
    diag=all_tok.at[(1-x)*2+1-c]
    cnts=[rcopy(own_cnt,all_cnt.at[tile],ns.at[i],nr.at[i],to) for i,to in enumerate((across,core,dev(z,y,1-x,1-c)))]
    cnt_in=[rcopy(r,r,ns.at[i],nr.at[i],core) for i,r in enumerate((all_cnt.at[(1-x)*2+c],all_cnt.at[x*2+1-c],all_cnt.at[(1-x)*2+1-c]))]
    local=(pltpu.make_async_copy(own_w,all_w.at[pl.ds(me*per,per)],ls.at[0]),
           pltpu.make_async_copy(own_tok,all_tok.at[tile],ls.at[1]),pltpu.make_async_copy(own_cnt,all_cnt.at[tile],ls.at[2]))
    @pl.when(z<3)
    def _(): z_copy(z,True,True).start()
    @pl.when(z>0)
    def _(): z_copy(z,True,False).start()
    y_copy(z,True).start(); tok_x.start(); tok_c.start()
    for cp in cnts: cp.start()
    for cp in local: cp.start()
    def from_line(k,dist):
        zz=z-dist if k==0 else z+dist
        there=(zz>=0) if k==0 else (zz<=3)
        @pl.when(there)
        def _():
            z_arrival(zz,k,dist).wait_recv()
            @pl.when((z<3) if k==0 else (z>0))
            def _(): z_copy(zz,False,k==0).start()
            y_copy(zz,False).start(); c_copy(zz*2+y).start()
    def from_beside(zz):
        y_arrival(zz).wait_recv(); c_copy(zz*2+1-y).start()
    def guarded(f,dist):
        @pl.when(z-dist>=0)
        def _(): f(z-dist)
        @pl.when(z+dist<=3)
        def _(): f(z+dist)
    from_line(0,1); from_line(1,1)
    from_beside(z)
    from_line(0,2); from_line(1,2)
    guarded(from_beside,1)
    from_line(0,3); from_line(1,3)
    tok_x.wait_recv(); tok_f.start()
    guarded(from_beside,2)
    guarded(from_beside,3)
    def drain(s,_):
        @pl.when(s!=me)
        def _():
            c_arrival(s).wait_recv(); c_copy(s).wait_send()
        return 0
    lax.fori_loop(0,8,drain,0)
    def drain_y(zz,_):
        y_copy(zz,False).wait_send(); return 0
    lax.fori_loop(0,4,drain_y,0)
    for dist in range(4):
        @pl.when(jnp.logical_and(z<3,z-dist>=0))
        def _(): z_copy(z-dist,False,True).wait_send()
        @pl.when(jnp.logical_and(z>0,z+dist<=3))
        def _(): z_copy(z+dist,False,False).wait_send()
    rcopy(near,near,ts.at[1],tr.at[1],core).wait_recv()
    rcopy(diag,diag,ts.at[2],tr.at[2],core).wait_recv()
    tok_x.wait_send(); tok_c.wait_send(); tok_f.wait_send()
    for cp in cnts: cp.wait_send()
    for cp in cnt_in: cp.wait_recv()
    for cp in local: cp.wait()

def gather_all(own_w,own_tok,own_cnt):
    DS=pltpu.SemaphoreType.DMA
    hbm=pl.BlockSpec(memory_space=pl.ANY)
    return pl.pallas_call(gather_kernel,
        out_shape=[jax.ShapeDtypeStruct((8*own_w.shape[0],)+own_w.shape[1:],bf),jax.ShapeDtypeStruct((4,)+own_tok.shape,bf),jax.ShapeDtypeStruct((4,)+own_cnt.shape,own_cnt.dtype)],
        in_specs=[pl.BlockSpec(memory_space=pltpu.VMEM)]*3,out_specs=[hbm]*3,
        scratch_shapes=[DS((2,4)),DS((2,4)),DS((4,)),DS((4,)),DS((8,)),DS((8,)),DS((3,)),DS((3,)),DS((3,)),DS((3,)),DS((3,))],
        compiler_params=pltpu.CompilerParams(has_side_effects=True,vmem_limit_bytes=60<<20),name="gather_weights_tokens")(own_w,own_tok,own_cnt)

def group_sum_kernel(g_ref,o_ref,gd,gs,gr):
    dp=lax.axis_index("dp"); t=lax.axis_index("tile")
    nd=gd.shape[0]
    def copy(k):
        return rcopy(gd.at[dp],gd.at[dp],gs.at[k],gr.at[k],((dp+k)%nd,t))
    def arrive(k):
        q=(dp-k+nd)%nd
        return rcopy(gd.at[q],gd.at[q],gs.at[k],gr.at[k],(q,t))
    def loop(f):
        def s(k,_):
            f(k); return 0
        lax.fori_loop(1,nd,s,0)
    gd[dp]=g_ref[...]
    loop(lambda k: copy(k).start())
    loop(lambda k: arrive(k).wait_recv())
    acc=gd[0]
    for i in range(1,nd): acc=acc+gd[i]
    o_ref[...]=acc
    loop(lambda k: copy(k).wait_send())

def group_sum(g,nd):
    DS=pltpu.SemaphoreType.DMA
    vm=pl.BlockSpec(memory_space=pltpu.VMEM)
    return pl.pallas_call(group_sum_kernel,out_shape=jax.ShapeDtypeStruct(g.shape,f32),in_specs=[vm],out_specs=vm,
        scratch_shapes=[pltpu.VMEM((nd,)+g.shape,f32),DS((nd,)),DS((nd,))],
        compiler_params=pltpu.CompilerParams(has_side_effects=True,vmem_limit_bytes=60<<20),name="sum_groups")(g)

def last_sums_kernel(l_ref,mine,over,v_ref,early,late,vo_ref,yb,zb,own,vb,vd,y1s,y1r,z2s,z2r,z3s,z3r,y4s,y4r,xs,xr,cs,cr,fs,fr,es,er,ts,tr,ds,dr,us,ur):
    z,y,x,c=where_am_i()
    dp=lax.axis_index("dp"); t=lax.axis_index("tile")
    core=dev(z,y,x,1-c); across=dev(z,y,1-x,c); beside=dev(z,1-y,x,c)
    def loop(f,first,n):
        def s(k,_):
            f(k); return 0
        lax.fori_loop(first,n,s,0)
    at=lambda i: pl.ds(i*3,3)
    def y1(k):
        q=(z+k)%4
        return rcopy(l_ref.at[at((1-y)*4+q)],yb.at[q],y1s.at[q],y1r.at[q],beside)
    def z2(k):
        q=(z+k)%4
        return rcopy(own.at[q],zb.at[z],z2s.at[k],z2r.at[k],dev(q,y,x,c))
    def z2_arrive(k):
        q=(z-k+4)%4
        return rcopy(zb.at[q],zb.at[q],z2s.at[k],z2r.at[k],dev(q,y,x,c))
    for k in (2,1,3,0): y1(k).start()
    def t1(k): return rcopy(v_ref.at[(t+k)%4],vb.at[t],ts.at[k],tr.at[k],(dp,(t+k)%4))
    def t1_arrive(k):
        q=(t-k+4)%4
        return rcopy(vb.at[q],vb.at[q],ts.at[k],tr.at[k],(dp,q))
    def d_copy(k): return rcopy(vd.at[dp],vd.at[dp],ds.at[k],dr.at[k],((dp+k)%8,t))
    def d_arrive(k):
        q=(dp-k+8)%8
        return rcopy(vd.at[q],vd.at[q],ds.at[k],dr.at[k],(q,t))
    def t2(k): return rcopy(vo_ref.at[t],vo_ref.at[t],us.at[k],ur.at[k],(dp,(t+k)%4))
    def t2_arrive(k):
        q=(t-k+4)%4
        return rcopy(vo_ref.at[q],vo_ref.at[q],us.at[k],ur.at[k],(dp,q))
    loop(lambda k: t1(k).start(),1,4)
    vb[t]=v_ref[t]
    def place(xx,cc,p): return early.at[pl.ds(cc*12+p*6+xx*3,3)]
    for p in range(2):
        early[pl.ds(c*12+p*6+x*3,3)]=mine[pl.ds(p*3,3)]
        early[pl.ds(c*12+p*6+(1-x)*3,3)]=over[pl.ds(p*3,3)]
    def e_copy(i,p): return rcopy(place(i,c,p),place(i,c,p),es.at[i,p],er.at[i,p],core)
    def e_arrive(i,p): return rcopy(place(i,1-c,p),place(i,1-c,p),es.at[i,p],er.at[i,p],core)
    for p in range(2):
        e_copy(0,p).start(); e_copy(1,p).start()
    loop(lambda k: t1_arrive(k).wait_recv(),1,4)
    vd[dp]=vb[0]+vb[1]+vb[2]+vb[3]
    loop(lambda k: d_copy(k).start(),1,8)
    for k in (2,1,3,0):
        q=(z+k)%4
        y1(k).wait_recv()
        for i in range(3): own[q,i]=(l_ref[(y*4+q)*3+i].astype(f32)+yb[q,i].astype(f32)).astype(bf)
        if k: z2(k).start()
    zb[z]=own[z]
    loop(lambda k: z2_arrive(k).wait_recv(),1,4)
    for i in range(3):
        late[t,(y*4+z)*3+i]=(zb[0,i].astype(f32)+zb[1,i].astype(f32)+zb[2,i].astype(f32)+zb[3,i].astype(f32)).astype(bf)
    def piece(tt,yy,zz): return late.at[tt,at(yy*4+zz)]
    def z3(k): return rcopy(piece(t,y,z),piece(t,y,z),z3s.at[k],z3r.at[k],dev((z+k)%4,y,x,c))
    def z3_arrive(k):
        q=(z-k+4)%4
        return rcopy(piece(t,y,q),piece(t,y,q),z3s.at[k],z3r.at[k],dev(q,y,x,c))
    def y4(q): return rcopy(piece(t,y,q),piece(t,y,q),y4s.at[q],y4r.at[q],beside)
    def y4_arrive(q): return rcopy(piece(t,1-y,q),piece(t,1-y,q),y4s.at[q],y4r.at[q],beside)
    far=(1-x)*2+c
    def x_copy(yy,q): return rcopy(piece(t,yy,q),piece(t,yy,q),xs.at[yy*4+q],xr.at[yy*4+q],across)
    def x_arrive(yy,q): return rcopy(piece(far,yy,q),piece(far,yy,q),xs.at[yy*4+q],xr.at[yy*4+q],across)
    def c_copy(yy,q): return rcopy(piece(t,yy,q),piece(t,yy,q),cs.at[yy*4+q],cr.at[yy*4+q],core)
    def c_arrive(yy,q): return rcopy(piece(x*2+1-c,yy,q),piece(x*2+1-c,yy,q),cs.at[yy*4+q],cr.at[yy*4+q],core)
    def f_copy(yy,q): return rcopy(piece(far,yy,q),piece(far,yy,q),fs.at[yy*4+q],fr.at[yy*4+q],core)
    def f_arrive(yy,q):
        r=piece((1-x)*2+1-c,yy,q)
        return rcopy(r,r,fs.at[yy*4+q],fr.at[yy*4+q],core)
    for k in (1,3,2): z3(k).start()
    y4(z).start(); x_copy(y,z).start(); c_copy(y,z).start()
    def passed_on(k):
        q=(z-k+4)%4
        if k:
            z3_arrive(k).wait_recv()
            y4(q).start(); x_copy(y,q).start(); c_copy(y,q).start()
        y4_arrive(q).wait_recv()
        x_copy(1-y,q).start(); c_copy(1-y,q).start()
    for k in (0,1,3,2): passed_on(k)
    loop(lambda k: d_arrive(k).wait_recv(),1,8)
    acc=vd[0]
    for i in range(1,8): acc=acc+vd[i]
    vo_ref[t]=acc
    loop(lambda k: t2(k).start(),1,4)
    for k in (0,1,3,2):
        q=(z-k+4)%4
        for yy in (y,1-y):
            x_arrive(yy,q).wait_recv(); f_copy(yy,q).start()
    def drain(q):
        for yy in range(2):
            c_arrive(yy,q).wait_recv(); f_arrive(yy,q).wait_recv()
            x_copy(yy,q).wait_send(); c_copy(yy,q).wait_send(); f_copy(yy,q).wait_send()
        y4(q).wait_send()
        y1(q).wait_send()
    loop(drain,0,4)
    def sent(k):
        t2_arrive(k).wait_recv()
        z2(k).wait_send(); z3(k).wait_send(); t1(k).wait_send(); t2(k).wait_send()
    loop(sent,1,4)
    loop(lambda k: d_copy(k).wait_send(),1,8)
    for p in range(2):
        for i in range(2):
            e_arrive(i,p).wait_recv(); e_copy(i,p).wait_send()

def last_sums(own,mine,over,v):
    DS=pltpu.SemaphoreType.DMA
    vm=pl.BlockSpec(memory_space=pltpu.VMEM)
    V=pltpu.VMEM
    S=jax.ShapeDtypeStruct
    rows=(3,v.shape[1])
    early,late,total=pl.pallas_call(last_sums_kernel,out_shape=[S((24,288,128),bf),S((4,24,144,128),bf),S((4,)+rows,f32)],in_specs=[vm]*4,out_specs=[vm]*3,
        scratch_shapes=[V((4,3,144,128),bf)]*3+[V((4,)+rows,f32),V((8,)+rows,f32)]+[DS((4,))]*8+[DS((8,))]*6+[DS((2,2))]*2+[DS((4,))]*2+[DS((8,))]*2+[DS((4,))]*2,
        cost_estimate=pl.CostEstimate(flops=10**7,bytes_accessed=150*10**6,transcendentals=0),
        compiler_params=pltpu.CompilerParams(has_side_effects=True,vmem_limit_bytes=60<<20),name="last_gradient_sums")(own.reshape(24,144,128),mine,over,v.reshape((4,)+rows))
    return early,late.reshape(48,288,128),total.reshape(v.shape)


H = 12
STEP = 10
EPS_NORM = 1e-06
BETA_ONE = 0.5
BETA_TWO = 0.5
ADAM_EPS = 1e-08
RATE_BLOCK = 0.3
RATE_VECTOR = 0.2
NEG_RAW = -8.0e9
HEAD = 64
SCALE = 1.0 / math.sqrt(HEAD)
EXP2 = SCALE * math.log2(math.e)
NN = (((1,), (0,)), ((), ()))
NT = (((1,), (1,)), ((), ()))
TN = (((0,), (0,)), ((), ()))


def mm(a, b, dims=NN):
    return lax.dot_general(a, b, dims, preferred_element_type=f32)


def column_sum(v):
    return jnp.sum(v, axis=0, keepdims=True)


def vmem_spec():
    return pl.BlockSpec(memory_space=pltpu.VMEM)


def smem_spec():
    return pl.BlockSpec(memory_space=pltpu.SMEM)


def any_spec():
    return pl.BlockSpec(memory_space=pl.ANY)


def params(mib=60):
    return pltpu.CompilerParams(vmem_limit_bytes=mib << 20)


def pack(block, odd):
    half = block.shape[0] // 2
    if odd:
        return block[:, 64:], jnp.concatenate([block[half:, :64], block[:half, :64]], axis=1)
    return block[:, :128], jnp.concatenate([block[:half, 128:], block[half:, 128:]], axis=1)


def unpack(top, tail, odd):
    if odd:
        return jnp.concatenate([jnp.concatenate([tail[:, 64:], tail[:, :64]], axis=0), top], axis=1)
    return jnp.concatenate([top, jnp.concatenate([tail[:, :64], tail[:, 64:]], axis=0)], axis=1)


def by_parity(value, run):
    for odd in (0, 1):
        pl.when(value == odd)(functools.partial(run, odd))


def turn(v):
    return jnp.concatenate([v[:, 64:], v[:, :64]], axis=1)


def group_of(n):
    return 4 if n % 4 == 0 else 3 if n % 3 == 0 else 1


def pack_kernel(early, order_ref, odd_ref, *refs):
    g = len(refs) - 3
    p_ref, late_ref, s_ref = refs[g:]
    i = pl.program_id(0)
    for b in range(g):
        m = refs[b][0]

        def place(odd, m=m, b=b):
            top, tail = pack(m, odd)
            for ref, here in ((p_ref, i < early), (late_ref, i >= early)):

                @pl.when(here)
                def _():
                    ref[b, :192] = top.astype(bf)
                    ref[b, 192:] = tail.astype(bf)

        by_parity(odd_ref[i * g + b], place)
        s_ref[b] = jnp.full((8, 128), jnp.sum(m * m), f32)


def pack_master(order, odd, master, first):
    n = master.shape[0]
    g = group_of(first)
    early = first // g
    rest = max(n - first, g)
    spec = pltpu.PrefetchScalarGridSpec(
        num_scalar_prefetch=2,
        grid=(n // g,),
        in_specs=[pl.BlockSpec((1, 192, 192), lambda i, s, o, b=b: (s[i * g + b], 0, 0)) for b in range(g)],
        out_specs=[
            pl.BlockSpec((g, 288, 128), lambda i, s, o: (jnp.minimum(i, early - 1), 0, 0)),
            pl.BlockSpec((g, 288, 128), lambda i, s, o: (jnp.maximum(i - early, 0), 0, 0)),
            pl.BlockSpec((g, 8, 128), lambda i, s, o: (i, 0, 0)),
        ],
    )
    return pl.pallas_call(
        functools.partial(pack_kernel, early),
        grid_spec=spec,
        out_shape=[jax.ShapeDtypeStruct((first, 288, 128), bf), jax.ShapeDtypeStruct((rest, 288, 128), bf), jax.ShapeDtypeStruct((n, 8, 128), f32)],
        compiler_params=params(),
        name="pack_master",
    )(order, odd, *[master] * g)


def pick_kernel(at_ref, first_ref, rest_ref, o_ref, sems):
    split = first_ref.shape[0]
    for j in range(12):

        @pl.when(at_ref[j] < split)
        def _():
            pltpu.make_async_copy(first_ref.at[at_ref[j]], o_ref.at[j], sems.at[j]).start()

        @pl.when(at_ref[j] >= split)
        def _():
            pltpu.make_async_copy(rest_ref.at[at_ref[j] - split], o_ref.at[j], sems.at[j]).start()

    for j in range(12):
        pltpu.make_async_copy(first_ref.at[0], o_ref.at[j], sems.at[j]).wait()


def pick(at, first, rest):
    return pl.pallas_call(
        pick_kernel,
        in_specs=[smem_spec(), any_spec(), any_spec()],
        out_specs=vmem_spec(),
        out_shape=jax.ShapeDtypeStruct((12, 288, 128), bf),
        scratch_shapes=[pltpu.SemaphoreType.DMA((12,))],
        compiler_params=params(),
        name="pick_qkv_blocks",
    )(at, first, rest)


def qkv_kernel(src_ref, cnt_ref, at_ref, x0, x1, x2, x3, blk_ref, gain_ref, shift_ref, bq_ref, bv_ref, a_ref, qt_ref, k_ref, kt_ref, v_ref, vt_ref, w_ref, st_ref):
    i = pl.program_id(0)

    @pl.when(i == 0)
    def _():
        def join(odd):
            for r in range(4):
                parts = []
                for c in range(3):
                    p = blk_ref[r * 3 + c].astype(f32)
                    parts.append(unpack(p[:192], p[192:], odd))
                w_ref[r * 192 : (r + 1) * 192, :] = jnp.concatenate(parts, axis=1).astype(bf)

        by_parity(at_ref[0], join)

    x = jnp.concatenate([r[...] for r in (x0, x1, x2, x3)], axis=0).astype(f32)
    mean = jnp.mean(x, axis=-1, keepdims=True)
    cen = x - mean
    inv_std = lax.rsqrt(jnp.mean(cen * cen, axis=-1, keepdims=True) + EPS_NORM)
    a = (cen * inv_std * gain_ref[...] + shift_ref[...]).astype(bf)
    a_ref[...] = a
    qkv = mm(a, w_ref[...])
    q = (qkv[:, :192] + bq_ref[...]).astype(bf).astype(f32)
    k = qkv[:, 192:384].astype(bf).astype(f32)
    v = (qkv[:, 384:] + bv_ref[...]).astype(bf).astype(f32)
    row = lax.broadcasted_iota(jnp.int32, (128, 64), 0)
    lane = lax.broadcasted_iota(jnp.int32, (512, 64), 1)
    masked = jnp.concatenate(
        [jnp.where(row < cnt_ref[4 * i + b], 0.0, NEG_RAW) for b in range(4)], axis=0
    )
    ones = jnp.where(lane < 4, 1.0, 0.0)
    k_tail = jnp.where(lane == 0, masked, ones)
    v_tail = jnp.where(lane < 3, 1.0, 0.0)
    sub = lax.broadcasted_iota(jnp.int32, (64, 512), 0)
    t_tail = jnp.where(sub < 1, 1.0, 0.0)
    qt, kt, vt = q.T, k.T, v.T
    longest = lambda a: jnp.max(jnp.concatenate([column_sum(a[h * 64 : (h + 1) * 64] ** 2) for h in range(3)], axis=0))
    st_ref[0] = jnp.where(lax.broadcasted_iota(jnp.int32, (8, 128), 0) == 0, longest(qt), longest(kt))
    for h in range(3):
        s = slice(h * 64, (h + 1) * 64)
        k_ref[h] = jnp.concatenate([k[:, s], k_tail], axis=1).astype(bf)
        v_ref[h] = jnp.concatenate([v[:, s], v_tail], axis=1).astype(bf)
        qt_ref[h] = jnp.concatenate([qt[s], t_tail], axis=0).astype(bf)
        kt_ref[h] = kt[s].astype(bf)
        vt_ref[h] = jnp.concatenate([vt[s], t_tail[:16]], axis=0).astype(bf)


def qkv_forward(src, cnt, odd, tokens, blocks, gain, shift, bq, bv):
    n = tokens.shape[0]
    rows = [pl.BlockSpec((128, 768), lambda i, s, c, o, k=k: (s[4 * i + k], 0)) for k in range(4)]
    row = lambda i, s, c, o: (0, 0)
    spec = pltpu.PrefetchScalarGridSpec(
        num_scalar_prefetch=3,
        grid=(n // 512,),
        in_specs=rows
        + [pl.BlockSpec((12, 288, 128), lambda i, s, c, o: (0, 0, 0)), pl.BlockSpec((1, 768), row), pl.BlockSpec((1, 768), row), pl.BlockSpec((1, 192), row), pl.BlockSpec((1, 192), row)],
        out_specs=[
            pl.BlockSpec((512, 768), lambda i, s, c, o: (i, 0)),
            pl.BlockSpec((3, 128, 512), lambda i, s, c, o: (0, 0, i)),
            pl.BlockSpec((3, 512, 128), lambda i, s, c, o: (0, i, 0)),
            pl.BlockSpec((3, 64, 512), lambda i, s, c, o: (0, 0, i)),
            pl.BlockSpec((3, 512, 128), lambda i, s, c, o: (0, i, 0)),
            pl.BlockSpec((3, 80, 512), lambda i, s, c, o: (0, 0, i)),
            pl.BlockSpec((768, 576), row),
            pl.BlockSpec((1, 8, 128), lambda i, s, c, o: (i, 0, 0)),
        ],
    )
    shapes = [(n, 768), (3, 128, n), (3, n, 128), (3, 64, n), (3, n, 128), (3, 80, n), (768, 576)]
    return pl.pallas_call(
        qkv_kernel,
        grid_spec=spec,
        out_shape=[jax.ShapeDtypeStruct(s, bf) for s in shapes] + [jax.ShapeDtypeStruct((n // 512, 8, 128), f32)],
        compiler_params=params(),
        name="norm_and_qkv",
    )(src, cnt, odd, tokens, tokens, tokens, tokens, blocks, gain, shift, bq, bv)


def split3(v):
    a = v.astype(bf).astype(f32)
    b = (v - a).astype(bf).astype(f32)
    return a, b, v - a - b


def in_steps(units, sizes, body, carry):
    at = 0
    for size in sizes:
        count = (units - at) // size
        carry = lax.fori_loop(0, count, lambda i, c, at=at, size=size: body(at + i * size, size, c), carry)
        at = at + count * size
    return carry


def attend_kernel(bq, n_ref, k_ref, qt_ref, vt_ref, ot_ref, qb_ref, p_ref, rt_ref):
    live = n_ref[0]
    qi = pl.program_id(1)
    pairs = (live + 7) // 8 * 4

    def finish(top, acc):
        total = acc[64:65]
        ot_ref[0] = acc[:64] / total
        rt_ref[0] = 1.0 / total
        a, b, c = split3((top + jnp.log2(total)) * (-1.0 / EXP2))
        row = lax.broadcasted_iota(jnp.int32, (64, bq), 0)
        tail = jnp.where(row == 0, 1.0, jnp.where(row == 1, a, jnp.where(row == 2, b, jnp.where(row == 3, c, 0.0))))
        qb_ref[0, :64] = qt_ref[0, :64]
        qb_ref[0, 64:] = tail.astype(bf)

    def keys(u, size):
        return pl.ds(pl.multiple_of(u * 256, 256), size * 256)

    @pl.when(jnp.logical_and(qi * bq < live * 128, n_ref[1] == 1))
    def _():
        qt = qt_ref[0]

        def body(u, size, acc):
            step = min(size, 2)
            for part in range(0, size, step):
                at = keys(u + part, step)
                p = jnp.exp2(mm(k_ref[0, at, :], qt) * EXP2).astype(bf)
                p_ref[0, at, :] = p
                acc = acc + mm(vt_ref[0, :, at], p)
            return acc

        finish(0.0, in_steps(pairs, (16, 8, 4), body, jnp.zeros((80, bq), f32)))

    @pl.when(jnp.logical_and(qi * bq < live * 128, n_ref[1] == 0))
    def _():
        qt = qt_ref[0]

        def body(u, size, carry):
            top, acc = carry
            s = mm(k_ref[0, keys(u, size), :], qt) * EXP2
            new = jnp.maximum(top, jnp.max(s, axis=0, keepdims=True))
            p = jnp.exp2(s - new).astype(bf)
            return new, acc * jnp.exp2(top - new) + mm(vt_ref[0, :, keys(u, size)], p)

        finish(*in_steps(pairs, (4,), body, (jnp.full((1, bq), -3e38, f32), jnp.zeros((80, bq), f32))))


def attend(live, k, qt, vt, bq=1024):
    n = k.shape[1]
    spec = pltpu.PrefetchScalarGridSpec(
        num_scalar_prefetch=1,
        grid=(3, n // bq),
        in_specs=[
            pl.BlockSpec((1, n, 128), lambda h, i, s: (h, 0, 0)),
            pl.BlockSpec((1, 128, bq), lambda h, i, s: (h, 0, i)),
            pl.BlockSpec((1, 80, n), lambda h, i, s: (h, 0, 0)),
        ],
        out_specs=[
            pl.BlockSpec((1, 64, bq), lambda h, i, s: (h, 0, i)),
            pl.BlockSpec((1, 128, bq), lambda h, i, s: (h, 0, i)),
            pl.BlockSpec((1, n, bq), lambda h, i, s: (h, 0, i)),
            pl.BlockSpec((1, 1, bq), lambda h, i, s: (h, 0, i)),
        ],
    )
    return pl.pallas_call(
        functools.partial(attend_kernel, bq),
        grid_spec=spec,
        out_shape=[
            jax.ShapeDtypeStruct((3, 64, n), f32),
            jax.ShapeDtypeStruct((3, 128, n), bf),
            jax.ShapeDtypeStruct((3, n, n), bf),
            jax.ShapeDtypeStruct((3, 1, n), f32),
        ],
        compiler_params=params(),
        name="attention_forward",
    )(live, k, qt, vt)


def spread_kernel(src_ref, n_ref, t_ref, ot_ref, *o_refs):
    live, t, tiles = n_ref[0], t_ref[0], len(o_refs)
    per = o_refs[0].shape[1] // 128

    def step(b, _):
        g = src_ref[b]
        lanes = pl.ds(pl.multiple_of(b * 128, 128), 128)
        to = pl.ds(pl.multiple_of((g % per) * 128, 128), 128)
        for k in range(tiles):
            here = (g // per - t + tiles) % tiles == k

            @pl.when(jnp.logical_and(here, b < live))
            def _():
                for h in range(3):
                    o_refs[k][h * 64 : (h + 1) * 64, to] = ot_ref[h, :, lanes].astype(bf)

            @pl.when(jnp.logical_and(here, b >= live))
            def _():
                o_refs[k][:, to] = jnp.zeros((192, 128), bf)

        return 0

    lax.fori_loop(0, ot_ref.shape[2] // 128, step, 0)


def spread(src, live, tile, ot, tiles):
    n = ot.shape[2]
    return pl.pallas_call(
        spread_kernel,
        in_specs=[smem_spec()] * 3 + [vmem_spec()],
        out_specs=[vmem_spec()] * tiles,
        out_shape=[jax.ShapeDtypeStruct((192, n // tiles), bf)] * tiles,
        compiler_params=params(),
        name="spread_attended",
    )(src, live, tile, ot)


def collect_kernel(src_ref, n_ref, t_ref, ot_ref, rt_ref, *refs):
    g_refs, dt_ref = refs[:-1], refs[-1]
    live, t, tiles = n_ref[0], t_ref[0], len(g_refs)
    mild = n_ref[1] == 1
    per = g_refs[0].shape[1] // 128
    row = lax.broadcasted_iota(jnp.int32, (64, 128), 0)

    def step(b, _):
        g = src_ref[b]
        to = pl.ds(pl.multiple_of(b * 128, 128), 128)
        lanes = pl.ds(pl.multiple_of((g % per) * 128, 128), 128)
        for k in range(tiles):

            @pl.when(jnp.logical_and((t - g // per + tiles) % tiles == k, b < live))
            def _():
                for h in range(3):
                    scale = jnp.where(mild, rt_ref[h, :, to], 1.0)
                    d = (g_refs[k][h * 64 : (h + 1) * 64, lanes].astype(f32) * scale).astype(bf).astype(f32)
                    x, y, z = split3(-jnp.sum(d * ot_ref[h, :, to], axis=0, keepdims=True))
                    tail = jnp.where(row == 0, x, jnp.where(row == 1, y, jnp.where(row == 2, z, 0.0)))
                    dt_ref[h, :, to] = jnp.concatenate([d, tail], axis=0).astype(bf)

        @pl.when(b >= live)
        def _():
            dt_ref[:, :, to] = jnp.zeros((3, 128, 128), bf)

        return 0

    lax.fori_loop(0, ot_ref.shape[2] // 128, step, 0)


def collect(src, live, tile, grads, ot, rt):
    n = ot.shape[2]
    return pl.pallas_call(
        collect_kernel,
        in_specs=[smem_spec()] * 3 + [vmem_spec()] * (2 + len(grads)),
        out_specs=vmem_spec(),
        out_shape=jax.ShapeDtypeStruct((3, 128, n), bf),
        compiler_params=params(),
        name="collect_attended_grad",
    )(src, live, tile, ot, rt, *grads)


def attend_back_kernel(bk, n_ref, p_ref, k_ref, kt_ref, v_ref, qb_ref, dt_ref, dq_ref, dk_ref, dv_ref):
    live = n_ref[0]
    j = pl.program_id(1)

    @pl.when(j == 0)
    def _():
        dq_ref[...] = jnp.zeros_like(dq_ref)

    def lanes(u):
        return pl.ds(pl.multiple_of(u * 256, 256), 256)

    pairs = (live + 1) // 2

    def over_queries(rows, sizes, body):
        zero = jnp.zeros((rows, 64), f32)
        dk, dv = in_steps((live + 7) // 8 * 4, sizes, body, (zero, zero))
        dk_ref[0, :rows] = (dk * SCALE).astype(bf)
        dv_ref[0, :rows] = dv.astype(bf)

    def with_kept(rows):
        k, v, kt = k_ref[0, :rows], v_ref[0, :rows], kt_ref[0, :, :rows]

        def body(u, size, carry):
            dk, dv = carry
            dp = mm(v, dt_ref[0, :, lanes(u)])
            for part in range(size):
                at = lanes(u + part)
                ahead = mm(v, dt_ref[0, :, lanes(u + part + 1)]) if part + 1 < size else None
                p = p_ref[0, :rows, at]
                ds = (p.astype(f32) * dp).astype(bf)
                dv = dv + mm(p, dt_ref[0, :64, at], NT)
                dk = dk + mm(ds, qb_ref[0, :64, at], NT)
                dq_ref[0, :, at] += mm(kt, ds)
                dp = dp if ahead is None else ahead
            return dk, dv

        over_queries(rows, (16, 8, 4), body)

    @pl.when(jnp.logical_and(n_ref[1] == 1, 2 * j + 2 <= pairs))
    def _():
        with_kept(bk)

    @pl.when(jnp.logical_and(n_ref[1] == 1, 2 * j + 1 == pairs))
    def _():
        dk_ref[0, bk // 2 :] = jnp.zeros((bk // 2, 64), bf)
        dv_ref[0, bk // 2 :] = jnp.zeros((bk // 2, 64), bf)
        with_kept(bk // 2)

    @pl.when(jnp.logical_and(n_ref[1] == 0, j * bk < live * 128))
    def _():
        k, v, kt = k_ref[0], v_ref[0], kt_ref[0]

        def body(u, size, carry):
            dk, dv = carry
            for part in range(size):
                at = lanes(u + part)
                p = jnp.exp2(mm(k, qb_ref[0, :, at]) * EXP2)
                ds = (p * mm(v, dt_ref[0, :, at])).astype(bf)
                dv = dv + mm(p.astype(bf), dt_ref[0, :64, at], NT)
                dk = dk + mm(ds, qb_ref[0, :64, at], NT)
                dq_ref[0, :, at] += mm(kt, ds)
            return dk, dv

        over_queries(bk, (4,), body)


def attend_back(first, heads, live, p, k, kt, v, qb, dt, bk=512):
    n = k.shape[1]
    whole_t = lambda h, j, s: (first + h, 0, 0)
    rows = lambda h, j, s: (first + h, j, 0)
    spec = pltpu.PrefetchScalarGridSpec(
        num_scalar_prefetch=1,
        grid=(heads, n // bk),
        in_specs=[
            pl.BlockSpec((1, bk, n), rows),
            pl.BlockSpec((1, bk, 128), rows),
            pl.BlockSpec((1, 64, bk), lambda h, j, s: (first + h, 0, j)),
            pl.BlockSpec((1, bk, 128), rows),
            pl.BlockSpec((1, 128, n), whole_t),
            pl.BlockSpec((1, 128, n), whole_t),
        ],
        out_specs=[
            pl.BlockSpec((1, 64, n), lambda h, j, s: (h, 0, 0)),
            pl.BlockSpec((1, bk, 64), lambda h, j, s: (h, j, 0)),
            pl.BlockSpec((1, bk, 64), lambda h, j, s: (h, j, 0)),
        ],
    )
    S = jax.ShapeDtypeStruct
    return pl.pallas_call(
        functools.partial(attend_back_kernel, bk),
        grid_spec=spec,
        out_shape=[S((heads, 64, n), f32), S((heads, n, 64), bf), S((heads, n, 64), bf)],
        cost_estimate=pl.CostEstimate(flops=heads * 4 * 10**10, bytes_accessed=heads * 50 * 10**6, transcendentals=0),
        compiler_params=params(),
        name="attention_backward",
    )(live, p, k, kt, v, qb, dt)


def qkv_back_kernel(given, src_ref, n_ref, odd_ref, x0, x1, x2, x3, gain_ref, a_ref, w_ref, *refs):
    grads, (ga_ref, gz_ref, gw_ref, gb_ref, vs_ref, acc, sums, rows, sems) = refs[:given], refs[given:]
    dqs, dks, dvs = [[(r, h) for r in grads[j::3] for h in range(r.shape[0])] for j in range(3)]
    early = ga_ref.shape[1] // 128
    i = pl.program_id(0)
    live = n_ref[0]

    @pl.when(i == 0)
    def _():
        acc[...] = jnp.zeros_like(acc)
        sums[...] = jnp.zeros_like(sums)
        vs_ref[...] = jnp.zeros_like(vs_ref)

    @pl.when(4 * i < live)
    def _():
        dq = jnp.concatenate([r[h] for r, h in dqs], axis=0).T * SCALE
        g = jnp.concatenate([dq] + [r[h].astype(f32) for r, h in dks + dvs], axis=1).astype(bf)
        acc[...] += mm(a_ref[...], g, TN)
        sums[...] += jnp.broadcast_to(column_sum(g.astype(f32)), sums.shape)
        g1 = mm(g, w_ref[...], NT)
        rows[...] = g1.astype(bf)
        x = jnp.concatenate([r[...] for r in (x0, x1, x2, x3)], axis=0).astype(f32)
        cen = x - jnp.mean(x, axis=-1, keepdims=True)
        normed = cen * lax.rsqrt(jnp.mean(cen * cen, axis=-1, keepdims=True) + EPS_NORM)
        vs_ref[0:1, :] += column_sum(g1 * normed)
        vs_ref[1:2, :] += column_sum(g1)

    @pl.when(4 * i >= live)
    def _():
        rows[...] = jnp.zeros_like(rows)

    per = early + gz_ref.shape[1] // 128
    for b in range(4):
        block, at = rows.at[pl.ds(b * 128, 128)], src_ref[4 * i + b]
        t, j = at // per, at % per

        @pl.when(j < early)
        def _():
            pltpu.make_async_copy(block, ga_ref.at[t, pl.ds(pl.multiple_of(j * 128, 128), 128)], sems.at[b]).start()

        @pl.when(j >= early)
        def _():
            pltpu.make_async_copy(block, gz_ref.at[t, pl.ds(pl.multiple_of((j - early) * 128, 128), 128)], sems.at[b]).start()

    for b in range(4):
        pltpu.make_async_copy(rows.at[pl.ds(b * 128, 128)], ga_ref.at[0, pl.ds(0, 128)], sems.at[b]).wait()

    @pl.when(i == pl.num_programs(0) - 1)
    def _():
        def place(odd):
            for r in range(4):
                for c in range(3):
                    top, tail = pack(acc[r * 192 : (r + 1) * 192, c * 192 : (c + 1) * 192], odd)
                    gw_ref[r * 3 + c, :192] = top.astype(bf)
                    gw_ref[r * 3 + c, 192:] = tail.astype(bf)

        by_parity(odd_ref[0], place)
        gb_ref[...] = sums[...]


def qkv_backward(src, live, odd, tokens, gain, a, w, grads, tiles, early):
    n = a.shape[0]
    per = n // tiles
    fixed = lambda i, s, c, o: (0, 0)
    row = lambda i, s, c, o: (0, i, 0)
    spec = pltpu.PrefetchScalarGridSpec(
        num_scalar_prefetch=3,
        grid=(n // 512,),
        in_specs=[pl.BlockSpec((128, 768), lambda i, s, c, o, k=k: (s[4 * i + k], 0)) for k in range(4)]
        + [pl.BlockSpec((1, 768), fixed), pl.BlockSpec((512, 768), lambda i, s, c, o: (i, 0)), pl.BlockSpec((768, 576), fixed)]
        + [
            pl.BlockSpec((g.shape[0], 64, 512), lambda i, s, c, o: (0, 0, i)) if g.shape[1] == 64 else pl.BlockSpec((g.shape[0], 512, 64), row)
            for g in grads
        ],
        out_specs=[any_spec(), any_spec(), pl.BlockSpec((12, 288, 128), lambda i, s, c, o: (0, 0, 0)), pl.BlockSpec((8, 576), fixed), pl.BlockSpec((8, 768), fixed)],
        scratch_shapes=[pltpu.VMEM((768, 576), f32), pltpu.VMEM((8, 576), f32), pltpu.VMEM((512, 768), bf), pltpu.SemaphoreType.DMA((4,))],
    )
    S = jax.ShapeDtypeStruct
    return pl.pallas_call(
        functools.partial(qkv_back_kernel, len(grads)),
        grid_spec=spec,
        out_shape=[S((tiles, early, 768), bf), S((tiles, per - early, 768), bf), S((12, 288, 128), bf), S((8, 576), f32), S((8, 768), f32)],
        cost_estimate=pl.CostEstimate(flops=3 * 10**10, bytes_accessed=40 * 10**6, transcendentals=0),
        compiler_params=params(),
        name="qkv_backward",
    )(src, live, odd, tokens, tokens, tokens, tokens, gain, a, w, *grads)


def gelu_parts(z):
    cdf = 0.5 + 0.5 * lax.erf(z * math.sqrt(0.5))
    return z * cdf, cdf + z * (jnp.exp2(z * z * (-0.5 * math.log2(math.e))) * (1.0 / math.sqrt(2.0 * math.pi)))


def middle_kernel(inv_ref, cnt_ref, t_ref, blk_ref, rest_ref, o0, o1, o2, o3, x_ref, c_ref, vp_ref, bu_ref, y_ref, gr_ref, g0, g1, g2_ref, g3,
                  u_s, gz_s, a2_s, gm_s, gb_s, o_s, vs_ref, us_ref, w_out, w_up, w_down, tails, tsem, isem):
    i = pl.program_id(0)
    rows = x_ref.shape[0]
    split = blk_ref.shape[0]
    r0 = i * rows
    kinds = ((w_out, 48, 2, 4), (w_up, 64, 8, 4), (w_down, 128, 2, 16))

    @pl.when(i == 0)
    def _():
        vs_ref[...] = jnp.zeros_like(vs_ref)
        us_ref[...] = jnp.zeros_like(us_ref)

        def pair(w, first, pairs):
            def parts(j, run):
                r = pl.multiple_of((j // pairs) * 192, 64)
                col = pl.multiple_of((j % pairs) * 384, 128)
                for b, off in ((0, 0), (1, 256)):
                    at = first + 2 * j + b
                    run(at, w.at[pl.ds(r, 192), pl.ds(col + off, 128)], tails.at[at - 48])
                return r, col

            def fetch(at, top, tail):
                for ref, here, slot in ((blk_ref, inv_ref[at] < split, inv_ref[at]), (rest_ref, inv_ref[at] >= split, inv_ref[at] - split)):

                    @pl.when(here)
                    def _():
                        pltpu.make_async_copy(ref.at[slot, pl.ds(0, 192)], top, tsem.at[at - 48]).start()
                        pltpu.make_async_copy(ref.at[slot, pl.ds(192, 96)], tail, isem.at[at - 48]).start()

            def fetched(at, top, tail):
                pltpu.make_async_copy(blk_ref.at[0, pl.ds(0, 192)], top, tsem.at[at - 48]).wait()
                pltpu.make_async_copy(blk_ref.at[0, pl.ds(192, 96)], tail, isem.at[at - 48]).wait()

            def start(j, _):
                parts(j, fetch)
                return 0

            def join(j, _):
                r, col = parts(j, fetched)
                even = tails[first + 2 * j - 48].astype(f32)
                odd = tails[first + 2 * j - 47].astype(f32)
                lane = lax.broadcasted_iota(jnp.int32, even.shape, 1) < 64
                w[pl.ds(r, 96), pl.ds(col + 128, 128)] = jnp.where(lane, even, odd).astype(bf)
                w[pl.ds(r + 96, 96), pl.ds(col + 128, 128)] = turn(jnp.where(lane, odd, even)).astype(bf)
                return 0

            return start, join

        todo = [(pair(w, first, pairs), pairs * high) for w, first, pairs, high in kinds]
        for (start, _), n in todo:
            lax.fori_loop(0, n, start, 0)

        for (_, join), n in todo:
            lax.fori_loop(0, n, join, 0)

    vp = vp_ref[...]
    row = r0 + lax.broadcasted_iota(jnp.int32, (rows, 1), 0)
    live = jnp.where(row < cnt_ref[0], 1.0, 0.0)
    t = t_ref[0]
    for k, ref in enumerate((o0, o1, o2, o3)):
        o_s[pl.ds(pl.multiple_of(((t - k + 4) % 4) * 192, 64), 192), :] = ref[...]
    o_t = o_s[...]
    res = x_ref[...].astype(f32) + mm(o_t, w_out[...], TN) + vp[6:7]
    cen = res - jnp.mean(res, axis=-1, keepdims=True)
    inv_std = lax.rsqrt(jnp.mean(cen * cen, axis=-1, keepdims=True) + EPS_NORM)
    normed = cen * inv_std
    a2 = (normed * vp[2:3] + vp[3:4]).astype(bf)
    gy = c_ref[...].astype(f32) * live
    gm = gy.astype(bf)
    a2_s[...] = a2
    gm_s[...] = gm
    branch = jnp.zeros((rows, 768), f32)
    g2 = jnp.zeros((rows, 768), f32)
    for j in range(4):
        cols = slice(j * 768, (j + 1) * 768)
        u, slope = gelu_parts(mm(a2, w_up[:, cols]) + bu_ref[:, cols])
        u = u.astype(bf)
        u_s[:, cols] = u
        branch = branch + mm(u, w_down[cols, :])
        gz = (mm(gm, w_down[cols, :], NT) * slope).astype(bf)
        gz_s[:, cols] = gz
        us_ref[:, cols] += jnp.broadcast_to(column_sum(gz.astype(f32)), (8, 768))
        g2 = g2 + mm(gz, w_up[:, cols], NT)
    y_ref[...] = (live * (res + branch + vp[7:8])).astype(bf)
    d2 = g2 * vp[2:3]
    gr = gy + inv_std * (d2 - jnp.mean(d2, axis=-1, keepdims=True) - normed * jnp.mean(d2 * normed, axis=-1, keepdims=True))
    gr_ref[...] = gr
    gb = gr.astype(bf)
    gb_s[...] = gb
    vs_ref[0:1, :] += column_sum(g2 * normed)
    vs_ref[1:2, :] += column_sum(g2)
    vs_ref[2:3, :] += column_sum(gb.astype(f32))
    vs_ref[3:4, :] += column_sum(gm.astype(f32))
    for k, ref in enumerate((g0, g1, g2_ref, g3)):
        ref[...] = mm(w_out[pl.ds(pl.multiple_of(((t + k) % 4) * 192, 64), 192), :], gb, NT).astype(bf)


def weight_grad_kernel(outs, pos_ref, o_in, gb_in, a2_in, gz_in, u_in, gm_in, *refs):
    s_refs, (o_s, gb_s, a2_s, gz_s, u_s, gm_s, ring, zero, lsem, osem, zsem) = refs[:outs], refs[outs:]
    each = s_refs[0].shape[0]

    def to_slot(block, at, sem):
        for o in range(outs):

            @pl.when(at // each == o)
            def _():
                pltpu.make_async_copy(block, s_refs[o].at[at % each], sem).start()

    def landed(block, sem):
        pltpu.make_async_copy(block, s_refs[0].at[0], sem).wait()

    loads = [pltpu.make_async_copy(a, b, lsem.at[j]) for j, (a, b) in enumerate(
        ((o_in, o_s), (gb_in, gb_s), (a2_in, a2_s), (gz_in, gz_s), (gm_in, gm_s), (u_in, u_s)))]
    for load in loads:
        load.start()
    zero[...] = jnp.zeros_like(zero)

    def clear(j, _):
        to_slot(zero, pos_ref[j], zsem.at[j])
        return 0

    lax.fori_loop(0, 48, clear, 0)
    def send(n, g, first, pairs, high, low):
        half = (n % 2) * 8

        def put(r, b):
            return first + (high + r) * 2 * pairs + 2 * low + b

        for r in range(4):
            part = g[r * 192 : (r + 1) * 192]
            mid = part[:, 128:256]
            upper, lower = mid[:96], turn(mid[96:])
            lane = lax.broadcasted_iota(jnp.int32, upper.shape, 1) < 64
            for b, top, tail in ((0, part[:, :128], jnp.where(lane, upper, lower)), (1, part[:, 256:], jnp.where(lane, lower, upper))):
                k = half + 2 * r + b

                @pl.when(n >= 2)
                def _():
                    landed(ring.at[k], osem.at[k])

                ring[k, :192] = top.astype(bf)
                ring[k, 192:] = tail.astype(bf)
                to_slot(ring.at[k], pos_ref[put(r, b)], osem.at[k])

    def lanes(j):
        return pl.ds(pl.multiple_of(j * 384, 128), 384)

    def grad_out(n, _):
        send(n, mm(o_s[...], gb_s[:, lanes(n)]), 48, 2, 0, n)
        return 0

    def grad_up(n, _):
        send(n, mm(a2_s[...], gz_s[:, lanes(n)], TN), 64, 8, 0, n)
        return 0

    def grad_down(n, _):
        high = n // 2
        send(n, mm(u_s[:, pl.ds(pl.multiple_of(high * 768, 128), 768)], gm_s[:, lanes(n % 2)], TN), 128, 2, high * 4, n % 2)
        return 0

    def drain():
        for k in range(16):
            landed(ring.at[k], osem.at[k])

    for f, n, first in ((grad_out, 2, 0), (grad_up, 8, 2), (grad_down, 8, 4)):
        loads[first].wait()
        loads[first + 1].wait()
        lax.fori_loop(0, n, f, 0)
        drain()

    def cleared(j, _):
        landed(zero, zsem.at[j])
        return 0

    lax.fori_loop(0, 48, cleared, 0)


def middle(inv, count, tile, blocks, rest, o_parts, tokens, cotangent, vec_params, bias_up, rows=256):
    n, width = tokens.shape
    hidden = bias_up.shape[1]
    row = lambda i, s, c, t: (i, 0)
    fixed = lambda i, s, c, t: (0, 0)
    col = lambda i, s, c, t: (0, i)
    V, DS = pltpu.VMEM, pltpu.SemaphoreType.DMA
    narrow, wide, part = pl.BlockSpec((rows, width), row), pl.BlockSpec((rows, hidden), row), pl.BlockSpec((192, rows), col)
    spec = pltpu.PrefetchScalarGridSpec(
        num_scalar_prefetch=3,
        grid=(n // rows,),
        in_specs=[any_spec()] * 2 + [part] * 4 + [narrow, narrow, pl.BlockSpec((12, width), fixed), pl.BlockSpec((1, hidden), fixed)],
        out_specs=[narrow, narrow] + [part] * 4 + [wide, wide, narrow, narrow, narrow, pl.BlockSpec((width, rows), col),
                   pl.BlockSpec((8, width), fixed), pl.BlockSpec((8, hidden), fixed)],
        scratch_shapes=[V((768, 768), bf), V((768, 3072), bf), V((3072, 768), bf), V((144, 96, 128), bf), DS((144,)), DS((144,))],
    )
    S = jax.ShapeDtypeStruct
    return pl.pallas_call(
        middle_kernel,
        grid_spec=spec,
        out_shape=[S((n, width), bf), S((n, width), f32)] + [S((192, n), bf)] * 4 + [S((n, hidden), bf)] * 2 + [S((n, width), bf)] * 3
        + [S((width, n), bf), S((8, width), f32), S((8, hidden), f32)],
        compiler_params=params(),
        name="projection_and_mlp",
    )(inv, count, tile, blocks, rest, *o_parts, tokens, cotangent, vec_params, bias_up)


def weight_grads_to_slots(pos, outs, block_count, o_t, gb, a2, gz, u, gm):
    V, DS = pltpu.VMEM, pltpu.SemaphoreType.DMA
    arrays = (o_t, gb, a2, gz, u, gm)
    return pl.pallas_call(
        functools.partial(weight_grad_kernel, outs),
        in_specs=[smem_spec()] + [any_spec()] * 6,
        out_specs=[any_spec()] * outs,
        out_shape=[jax.ShapeDtypeStruct((block_count // outs, 288, 128), bf)] * outs,
        scratch_shapes=[V(a.shape, bf) for a in arrays] + [V((16, 288, 128), bf), V((288, 128), bf), DS((6,)), DS((16,)), DS((48,))],
        cost_estimate=pl.CostEstimate(flops=6 * 10**10, bytes_accessed=32 * 10**6, transcendentals=0),
        compiler_params=params(),
        name="mlp_weight_gradients",
    )(pos, *arrays)


def quarters(b0, b1):
    return (b0 * 2 + b1, (1 - b0) * 2 + b1, b0 * 2 + 1 - b1, (1 - b0) * 2 + 1 - b1)


def add_pair_kernel(common, bits_ref, *refs):
    outs = list(refs[16:])
    for p in range(2):
        for side in range(4):
            j = 4 * p + side
            total = (refs[2 * j][...].astype(f32) + refs[2 * j + 1][...].astype(f32)).astype(bf)
            if side == common[p]:
                outs[6][p] = total
            else:
                outs[3 * p + side - (side > common[p])][...] = total


def add_pair(bits, common, keep, came):
    specs = []
    for p in range(2):
        for side in range(4):
            at = lambda i, b, p=p, side=side: (p * 12 + quarters(b[2 * p], b[2 * p + 1])[side] * 3 + i, 0, 0)
            specs += [pl.BlockSpec((4, 288, 128), at)] * 2
    S = jax.ShapeDtypeStruct
    return pl.pallas_call(
        functools.partial(add_pair_kernel, common),
        grid_spec=pltpu.PrefetchScalarGridSpec(
            num_scalar_prefetch=1,
            grid=(3,),
            in_specs=specs,
            out_specs=[pl.BlockSpec((4, 288, 128), lambda i, b: (i, 0, 0))] * 6 + [pl.BlockSpec((2, 4, 288, 128), lambda i, b: (0, i, 0, 0))],
        ),
        out_shape=[S((12, 288, 128), bf)] * 6 + [S((2, 12, 288, 128), bf)],
        compiler_params=params(),
        name="add_gradients_of_cores",
    )(bits, *[keep, came] * 8)


def add_four_kernel(common, bits_ref, *refs):
    outs = refs[7:]
    for p in range(2):
        parts = refs[3 * p : 3 * p + 3]
        for side, q in enumerate(quarters(bits_ref[2 * p], bits_ref[2 * p + 1])):
            for b in range(3):
                total = (sum(r[q * 3 + b].astype(f32) for r in parts) + refs[6][p, q * 3 + b].astype(f32)).astype(bf)
                if side == common[p]:
                    outs[6][p, b] = total
                else:
                    outs[3 * p + side - (side > common[p])][b] = total


def add_four(bits, common, parts):
    S = jax.ShapeDtypeStruct
    return pl.pallas_call(
        functools.partial(add_four_kernel, common),
        in_specs=[smem_spec()] + [vmem_spec()] * 7,
        out_specs=[vmem_spec()] * 7,
        out_shape=[S((3, 288, 128), bf)] * 6 + [S((2, 3, 288, 128), bf)],
        compiler_params=params(),
        name="add_gradients",
    )(bits, *parts)


def add_last_kernel(*refs):
    for p in range(2):
        for b in range(3):
            refs[7][3 * p + b] = (sum(r[b].astype(f32) for r in refs[3 * p : 3 * p + 3]) + refs[6][p, b].astype(f32)).astype(bf)


def add_last(parts):
    return pl.pallas_call(
        add_last_kernel,
        in_specs=[vmem_spec()] * 7,
        out_specs=vmem_spec(),
        out_shape=jax.ShapeDtypeStruct((6, 288, 128), bf),
        compiler_params=params(),
        name="add_last_gradients",
    )(*parts)


def split2(v):
    hi = v.astype(bf)
    return hi, (v - hi.astype(f32)).astype(bf)


def mm3(a, b, dims):
    return mm(a[0], b[0], dims) + (mm(a[0], b[1], dims) + mm(a[1], b[0], dims))


def adam_kernel(odd_ref, from_ref, g_ref, late_ref, m1_ref, m2_ref, l_ref, r_ref, g_out, m1_out, m2_out, u_out, s_out, part):
    for b in range(g_ref.shape[0]):
        slot = pl.program_id(0) * g_ref.shape[0] + b
        place = from_ref[slot]

        @pl.when(place >= 0)
        def _():
            part[...] = late_ref[jnp.maximum(place, 0)]

        @pl.when(place < 0)
        def _():
            part[...] = g_ref[b]

        def whole(odd, b=b):
            g_out[b] = unpack(part[:192].astype(f32), part[192:].astype(f32), odd)

        by_parity(odd_ref[slot], whole)
        grad = g_out[b]
        left, right = split2(l_ref[b]), split2(r_ref[b])
        low = grad.astype(bf)
        rot = mm3(split2(mm(left[0], low, TN) + mm(left[1], low, TN)), right, NN)
        first = BETA_ONE * m1_ref[b] + (1.0 - BETA_ONE) * rot
        second = BETA_TWO * m2_ref[b] + (1.0 - BETA_TWO) * rot * rot
        upd = (first / (1.0 - BETA_ONE**STEP)) / (jnp.sqrt(second / (1.0 - BETA_TWO**STEP)) + ADAM_EPS)
        upd = mm3(split2(mm3(left, split2(upd), NN)), right, NT)
        m1_out[b] = first
        m2_out[b] = second
        u_out[b] = upd
        s_out[b] = jnp.full((8, 128), jnp.sum(upd * upd), f32)


def adam(odd, late_at, grads, late, first, second, left, right):
    n = grads.shape[0]
    g = group_of(n)
    at = lambda i, s, f: (i, 0, 0)
    big = pl.BlockSpec((g, 192, 192), at)
    spec = pltpu.PrefetchScalarGridSpec(
        num_scalar_prefetch=2,
        grid=(n // g,),
        in_specs=[pl.BlockSpec((g, 288, 128), at), pl.BlockSpec(late.shape, lambda i, s, f: (0, 0, 0))] + [big] * 4,
        out_specs=[big] * 4 + [pl.BlockSpec((g, 8, 128), at)],
        scratch_shapes=[pltpu.VMEM((288, 128), bf)],
    )
    return pl.pallas_call(
        adam_kernel,
        grid_spec=spec,
        out_shape=[jax.ShapeDtypeStruct((n, 192, 192), f32)] * 4 + [jax.ShapeDtypeStruct((n, 8, 128), f32)],
        compiler_params=params(),
        name="rotated_adam",
    )(odd, late_at, grads, late, first, second, left, right)


def update_kernel(rate_ref, m_ref, u_ref, mo_ref, mc_ref):
    g = m_ref.shape[0]
    for b in range(g):
        new = m_ref[b] - rate_ref[pl.program_id(0) * g + b] * u_ref[b]
        mo_ref[b] = new
        mc_ref[b] = new.astype(bf)


def new_weights(rate, master, update):
    n = master.shape[0]
    g = group_of(n)
    big = pl.BlockSpec((g, 192, 192), lambda i, r: (i, 0, 0))
    return pl.pallas_call(
        update_kernel,
        grid_spec=pltpu.PrefetchScalarGridSpec(num_scalar_prefetch=1, grid=(n // g,), in_specs=[big] * 2, out_specs=[big] * 2),
        out_shape=[jax.ShapeDtypeStruct(master.shape, f32), jax.ShapeDtypeStruct(master.shape, bf)],
        compiler_params=params(),
        name="new_weights",
    )(rate, master, update)


def halving_places(slot, core):
    dp, r = slot // 24, slot % 24
    y, z, far, x, s = dp % 2, dp // 2 % 2, dp // 4, r % 6 // 3, r % 3
    portion = r % 12 // 6
    inside = jnp.where(portion == 0, x * 8 + y * 4 + z * 2 + far, y * 8 + z * 4 + x * 2 + far)
    return jnp.where(r // 12 == core, 0, 96) + portion * 48 + inside * 3 + s


def input_grad_kernel(early, ga_ref, gz_ref, r_ref, x_ref, gain_ref, o_ref):
    x = x_ref[...].astype(f32)
    cen = x - jnp.mean(x, axis=-1, keepdims=True)
    inv_std = lax.rsqrt(jnp.mean(cen * cen, axis=-1, keepdims=True) + EPS_NORM)
    normed = cen * inv_std
    d = jnp.where(pl.program_id(0) < early, ga_ref[...], gz_ref[...]).astype(f32) * gain_ref[...]
    o_ref[...] = r_ref[...] + inv_std * (d - jnp.mean(d, axis=-1, keepdims=True) - normed * jnp.mean(d * normed, axis=-1, keepdims=True))


def input_gradient(g_one, g_two, grad_resid, tokens, gain):
    n, width = tokens.shape
    early = g_one.shape[0] // 128
    row = pl.BlockSpec((128, width), lambda i: (i, 0))
    return pl.pallas_call(
        functools.partial(input_grad_kernel, early),
        grid=(n // 128,),
        in_specs=[
            pl.BlockSpec((128, width), lambda i: (jnp.minimum(i, early - 1), 0)),
            pl.BlockSpec((128, width), lambda i: (jnp.maximum(i - early, 0), 0)),
            row,
            row,
            pl.BlockSpec((1, width), lambda i: (0, 0)),
        ],
        out_specs=row,
        out_shape=jax.ShapeDtypeStruct((n, width), f32),
        compiler_params=params(),
        name="input_gradient",
    )(g_one, g_two, grad_resid, tokens, gain)


def block_plan(counts, slot_count):
    tiles = counts.shape[0]
    per = slot_count // 128
    j = lax.broadcasted_iota(jnp.int32, (tiles, per), 1)
    kept = jnp.clip(counts[:, None] - j * 128, 0, 128).reshape(-1)
    full = (kept > 0).astype(jnp.int32)
    index = jnp.arange(tiles * per, dtype=jnp.int32)
    before = (index[None, :] < index[:, None]).astype(jnp.int32)
    ahead = jnp.sum(before * full[None, :], axis=1)
    live = jnp.sum(full)
    place = jnp.where(full > 0, ahead, live + index - ahead)
    hot = (place[None, :] == index[:, None]).astype(jnp.int32)
    return jnp.sum(hot * index[None, :], axis=1), jnp.sum(hot * kept[None, :], axis=1), live.reshape(1)


def make_body(tuned):
    def body(tokens, cotangent, counts, master, slot_block, groups, first_moment, second_moment, left_basis, right_basis, vec_params, vec_first, vec_second):
        slot_count, width = tokens.shape[1:]
        per_owner = master.shape[0]
        tile = lax.axis_index("tile")
        block_count = slot_block.shape[0]
        first = per_owner // 2 if tuned else per_owner
        index = jnp.arange(block_count, dtype=jnp.int32)
        owner = index // per_owner
        same = (owner[None, :] == owner[:, None]).astype(jnp.int32)
        is_qkv = (slot_block < 48).astype(jnp.int32)
        sooner = same * jnp.where(is_qkv[None, :] == is_qkv[:, None], (index[None, :] < index[:, None]).astype(jnp.int32), is_qkv[None, :])
        rank = jnp.sum(sooner, axis=1)
        place = jnp.where(rank < first, owner * first + rank, block_count // per_owner * first + owner * (per_owner - first) + rank - first)
        most = jnp.max(jnp.sum(same * is_qkv[None, :], axis=1))
        start = lax.axis_index("dp") * per_owner
        mine = lax.dynamic_slice(slot_block, (start,), (per_owner,))
        odd = mine % 2
        local = jnp.arange(per_owner, dtype=jnp.int32)
        at_rank = (lax.dynamic_slice(rank, (start,), (per_owner,))[None, :] == local[:, None]).astype(jnp.int32)
        order = jnp.sum(at_rank * local[None, :], axis=1)
        packed, packed_rest, weight_sq = pack_master(order, jnp.sum(at_rank * odd[None, :], axis=1), master, first)
        own_tokens = tokens.reshape(slot_count, width)
        count_tile = jnp.broadcast_to(counts.reshape(1, 1), (8, 128))
        if tuned:
            blocks, token_all, count_all = gather_all(packed, own_tokens, count_tile)
            packed_rest, blocks = lax.optimization_barrier((packed_rest, blocks))
            blocks_rest = lax.all_gather(packed_rest, "dp", axis=0, tiled=True)
        else:
            blocks = lax.all_gather(packed, "dp", axis=0, tiled=True)
            token_all = lax.all_gather(own_tokens, "tile", axis=0)
            count_all = lax.all_gather(count_tile, "tile", axis=0)
            blocks_rest = packed_rest
        tiles = token_all.shape[0]
        src, cnt, live = block_plan(count_all[:, 0, 0], slot_count)
        is_at = (slot_block[None, :] == index[:, None]).astype(jnp.int32)
        inverse = jnp.sum(is_at * index[None, :], axis=1)
        places = jnp.sum(is_at * place[None, :], axis=1)
        own_block = jnp.arange(12, dtype=jnp.int32) // 3 * 12 + jnp.arange(12, dtype=jnp.int32) % 3 * 4 + tile
        own_at = jnp.sum((slot_block[None, :] == own_block[:, None]).astype(jnp.int32) * place[None, :], axis=1)
        if tuned:
            qkv_blocks = lax.cond(
                most <= first,
                lambda: pick(own_at, blocks, packed_rest),
                lambda: pick(own_at, blocks, lax.all_gather(packed_rest, "dp", axis=0, tiled=True)),
            )
        else:
            qkv_blocks = pick(own_at, blocks, blocks_rest)
        tile_one = tile.astype(jnp.int32).reshape(1)
        own = width // tiles
        bias = lambda row: lax.dynamic_slice(vec_params[row : row + 1], (0, tile * own), (1, own))
        a1, qt, k, kt, v, vt, w_qkv, lengths = qkv_forward(
            src, cnt, tile_one % 2, token_all.reshape(-1, width), qkv_blocks, vec_params[0:1], vec_params[1:2], bias(4), bias(5)
        )
        mild = jnp.sqrt(jnp.max(lengths[:, 0, 0])) * jnp.sqrt(jnp.max(lengths[:, 1, 0])) * EXP2 <= 60.0
        live = jnp.concatenate([live, mild.astype(jnp.int32).reshape(1)])
        ot, qb, p, rt = attend(live, k, qt, vt)

        def shift(parts):
            return [parts[0]] + [lax.ppermute(parts[j], "tile", [(s, (s + j) % tiles) for s in range(tiles)]) for j in range(1, tiles)]

        o_parts = shift(spread(src, live, tile_one, ot, tiles))
        output, grad_resid, *rest = middle(
            places, counts.reshape(1), tile_one, blocks, blocks_rest, o_parts, own_tokens, cotangent.reshape(slot_count, width), vec_params, vec_params[8:].reshape(1, -1)
        )
        go_parts, (u, gz, a2, gm, gb, o_t, sums, up_sums) = rest[:tiles], rest[tiles:]
        go_parts = shift(go_parts)
        back = lambda first, heads, dt: list(attend_back(first, heads, live, p, k, kt, v, qb, dt))
        if tuned:
            dp = lax.axis_index("dp")
            bit = {"x": tile // 2, "y": dp % 2, "z": dp // 2 % 2, "far": dp // 4}
            mask = {"x": 2, "y": 4, "z": 8, "far": 16}

            def flip(array, *names):
                change = sum(mask[name] for name in names)
                return lax.ppermute(array, ("dp", "tile"), [(s, s ^ change) for s in range(32)])

            def three(sums, pairs, common):
                out = []
                for p, (a, b) in enumerate(pairs):
                    ways = [(), (a,), (b,), (a, b)]
                    del ways[common[p]]
                    out += [flip(sums[3 * p + j], *way) if way else sums[3 * p + j] for j, way in enumerate(ways)]
                return out + [flip(sums[6], pairs[0][common[0] - 1])]

            def bits_of(pairs):
                return jnp.stack([bit[name] for pair in pairs for name in pair]).astype(jnp.int32)

            first, second = [("x", "y"), ("y", "z")], [("z", "far"), ("x", "far")]
            keep, send = weight_grads_to_slots(halving_places(inverse, tile % 2), 2, block_count, o_t, gb, a2, gz, u, gm)
            send, go_parts = lax.optimization_barrier((send, go_parts))
            came = lax.ppermute(send, "tile", [(s, s ^ 1) for s in range(4)])
            dt = collect(src, live, tile_one, go_parts, ot, rt)
            dt, came = lax.optimization_barrier((dt, came))
            sums_one = add_pair(bits_of(first), (2, 1), keep, came)
            dt, sums_one = lax.optimization_barrier((dt, sums_one))
            parts = three(sums_one, first, (2, 1))
            head_grads = back(0, 2, dt)
            head_grads[0], parts = lax.optimization_barrier((head_grads[0], parts))
            sums_two = add_four(bits_of(second), (2, 2), parts)
            dt, sums_two = lax.optimization_barrier((dt, sums_two))
            parts = three(sums_two, second, (2, 2))
            head_grads += back(2, 1, dt)
            head_grads[3], parts = lax.optimization_barrier((head_grads[3], parts))
            mine_early = add_last(parts)
            head_grads[3], mine_early = lax.optimization_barrier((head_grads[3], mine_early))
            over_early = flip(mine_early, "x")
        else:
            slots = weight_grads_to_slots(inverse, 1, block_count, o_t, gb, a2, gz, u, gm)[0]
            dt = collect(src, live, tile_one, go_parts, ot, rt)
            head_grads = back(0, 3, dt)
        g_one, g_two, gw_qkv, qkv_sums, norm_sums = qkv_backward(
            src, live, tile_one % 2, token_all.reshape(-1, width), vec_params[0:1], a1, w_qkv, head_grads, tiles, slot_count * 3 // 8
        )
        if tuned:
            g_one, over_early = lax.optimization_barrier((g_one, over_early))
        zero = jnp.zeros((width,), f32)
        at_own = lambda s: lax.dynamic_update_slice(zero, s, (tile * own,))
        vector_part = jnp.concatenate(
            [norm_sums[0:2], sums[0:2], at_own(qkv_sums[0, :own])[None], at_own(qkv_sums[0, 2 * own :])[None], sums[2:4], up_sums[0].reshape(-1, width)], axis=0
        )
        if tuned:
            early, late, vector_grads = last_sums(gw_qkv, mine_early, over_early, vector_part)
            g_two, early = lax.optimization_barrier((g_two, early))
        else:
            early = lax.psum(lax.psum_scatter(slots.astype(f32), "dp", scatter_dimension=0, tiled=True), "tile").astype(bf)
            late = lax.all_gather(lax.psum(gw_qkv.astype(f32), "dp").astype(bf), "tile", axis=0, tiled=True)
            vector_grads = lax.psum(vector_part, ("dp", "tile"))
        g1 = [lax.psum_scatter(part, "tile", scatter_dimension=0, tiled=False) for part in (g_one, g_two)]
        input_grad = input_gradient(*g1, grad_resid, own_tokens, vec_params[0:1])
        late_at = jnp.where(mine < 48, mine % 4 * 12 + mine // 12 * 3 + mine % 12 // 4, -1)
        weight_grads, first_out, second_out, update, update_sq = adam(odd, late_at, early, late, first_moment, second_moment, left_basis, right_basis)
        group_hot = (groups[:, None] == jnp.arange(128, dtype=jnp.int32)[None, :]).astype(f32)
        weight_part = jnp.sum(jnp.sum(at_rank.astype(f32)[:, :, None] * group_hot[None], axis=1) * weight_sq[:, 0], axis=0)
        group_part = jnp.pad(jnp.stack([weight_part, jnp.sum(group_hot * update_sq[:, 0], axis=0)]), ((0, 6), (0, 0)))
        group_both = group_sum(group_part, block_count // per_owner)
        own_both = jnp.sum(group_hot[None] * group_both[:2, None, :], axis=2)
        rate = RATE_BLOCK * jnp.sqrt(own_both[0]) / (jnp.sqrt(own_both[1]) + 1e-06)
        master_out, master_copy = new_weights(rate, master, update)
        vec_first_out = BETA_ONE * vec_first + (1.0 - BETA_ONE) * vector_grads
        vec_second_out = BETA_TWO * vec_second + (1.0 - BETA_TWO) * vector_grads * vector_grads
        vec_update = (vec_first_out / (1.0 - BETA_ONE**STEP)) / (jnp.sqrt(vec_second_out / (1.0 - BETA_TWO**STEP)) + ADAM_EPS)
        return (
            output.reshape(1, slot_count, width),
            input_grad.reshape(1, slot_count, width),
            weight_grads,
            first_out,
            second_out,
            master_out,
            master_copy,
            vector_grads,
            vec_first_out,
            vec_second_out,
            vec_params - RATE_VECTOR * vec_update,
        )

    return body


def solution(mesh):
    tuned = (mesh.shape["dp"], mesh.shape["tile"]) == (8, 4)
    rows, blocks = P("dp", "tile", None), P("dp", None, None)
    return jax.shard_map(
        make_body(tuned),
        mesh=mesh,
        in_specs=(rows, rows, P("dp", "tile"), blocks, P(), P("dp"), blocks, blocks, blocks, blocks, P(), P(), P()),
        out_specs=(rows, rows, blocks, blocks, blocks, blocks, blocks, P(), P(), P(), P()),
        check_vma=False,
    )
```

```python
import functools
import math

import jax
import jax.numpy as jnp
from jax import lax
from jax.experimental import pallas as pl
from jax.experimental.pallas import tpu as pltpu
from jax.sharding import PartitionSpec as P

f32 = jnp.float32
bf = jnp.bfloat16
MESH = pl.DeviceIdType.MESH

def where_am_i():
    dp=lax.axis_index("dp"); t=lax.axis_index("tile")
    return dp//2, dp%2, t//2, t%2

def dev(z,y,x,c):
    return (z*2+y, x*2+c)

def rcopy(src,dst,ss,rs,to):
    return pltpu.make_async_remote_copy(src_ref=src,dst_ref=dst,send_sem=ss,recv_sem=rs,device_id=to,device_id_type=MESH)

def gather_kernel(own_w,own_tok,own_cnt,all_w,all_tok,all_cnt,zs,zr,ys,yr,cs,cr,ts,tr,ns,nr,ls):
    z,y,x,c=where_am_i()
    per=own_w.shape[0]
    half=per//2
    def piece(shard,cc): return all_w.at[pl.ds(shard*per+cc*half,half)]
    own=own_w.at[pl.ds(c*half,half)]
    me=z*2+y
    core=dev(z,y,x,1-c); across=dev(z,y,1-x,c); beside=dev(z,1-y,x,c)
    up=dev(jnp.minimum(z+1,3),y,x,c); down=dev(jnp.maximum(z-1,0),y,x,c)
    def src(shard,first): return own if first else piece(shard,c)
    def z_copy(zz,first,go_up):
        shard=zz*2+y
        d=(z-zz) if go_up else (zz-z)
        k=0 if go_up else 1
        return rcopy(src(shard,first),piece(shard,c),zs.at[k,d],zr.at[k,d],up if go_up else down)
    def z_arrival(zz,k,dist):
        r=piece(zz*2+y,c)
        return rcopy(r,r,zs.at[k,dist-1],zr.at[k,dist-1],up)
    def y_copy(zz,first):
        shard=zz*2+y
        return rcopy(src(shard,first),piece(shard,c),ys.at[zz],yr.at[zz],beside)
    def y_arrival(zz):
        r=piece(zz*2+1-y,c)
        return rcopy(r,r,ys.at[zz],yr.at[zz],beside)
    def c_copy(shard): return rcopy(piece(shard,c),piece(shard,c),cs.at[shard],cr.at[shard],core)
    def c_arrival(shard): return rcopy(piece(shard,1-c),piece(shard,1-c),cs.at[shard],cr.at[shard],core)
    tile=x*2+c
    tok_x=rcopy(own_tok,all_tok.at[tile],ts.at[0],tr.at[0],across)
    tok_c=rcopy(own_tok,all_tok.at[tile],ts.at[1],tr.at[1],core)
    far=all_tok.at[(1-x)*2+c]
    tok_f=rcopy(far,far,ts.at[2],tr.at[2],core)
    near=all_tok.at[x*2+1-c]
    diag=all_tok.at[(1-x)*2+1-c]
    cnts=[rcopy(own_cnt,all_cnt.at[tile],ns.at[i],nr.at[i],to) for i,to in enumerate((across,core,dev(z,y,1-x,1-c)))]
    cnt_in=[rcopy(r,r,ns.at[i],nr.at[i],core) for i,r in enumerate((all_cnt.at[(1-x)*2+c],all_cnt.at[x*2+1-c],all_cnt.at[(1-x)*2+1-c]))]
    local=(pltpu.make_async_copy(own_w,all_w.at[pl.ds(me*per,per)],ls.at[0]),
           pltpu.make_async_copy(own_tok,all_tok.at[tile],ls.at[1]),pltpu.make_async_copy(own_cnt,all_cnt.at[tile],ls.at[2]))
    @pl.when(z<3)
    def _(): z_copy(z,True,True).start()
    @pl.when(z>0)
    def _(): z_copy(z,True,False).start()
    y_copy(z,True).start(); tok_x.start(); tok_c.start()
    for cp in cnts: cp.start()
    for cp in local: cp.start()
    def from_line(k,dist):
        zz=z-dist if k==0 else z+dist
        there=(zz>=0) if k==0 else (zz<=3)
        @pl.when(there)
        def _():
            z_arrival(zz,k,dist).wait_recv()
            @pl.when((z<3) if k==0 else (z>0))
            def _(): z_copy(zz,False,k==0).start()
            y_copy(zz,False).start(); c_copy(zz*2+y).start()
    def from_beside(zz):
        y_arrival(zz).wait_recv(); c_copy(zz*2+1-y).start()
    def guarded(f,dist):
        @pl.when(z-dist>=0)
        def _(): f(z-dist)
        @pl.when(z+dist<=3)
        def _(): f(z+dist)
    from_line(0,1); from_line(1,1)
    from_beside(z)
    from_line(0,2); from_line(1,2)
    guarded(from_beside,1)
    from_line(0,3); from_line(1,3)
    tok_x.wait_recv(); tok_f.start()
    guarded(from_beside,2)
    guarded(from_beside,3)
    def drain(s,_):
        @pl.when(s!=me)
        def _():
            c_arrival(s).wait_recv(); c_copy(s).wait_send()
        return 0
    lax.fori_loop(0,8,drain,0)
    def drain_y(zz,_):
        y_copy(zz,False).wait_send(); return 0
    lax.fori_loop(0,4,drain_y,0)
    for dist in range(4):
        @pl.when(jnp.logical_and(z<3,z-dist>=0))
        def _(): z_copy(z-dist,False,True).wait_send()
        @pl.when(jnp.logical_and(z>0,z+dist<=3))
        def _(): z_copy(z+dist,False,False).wait_send()
    rcopy(near,near,ts.at[1],tr.at[1],core).wait_recv()
    rcopy(diag,diag,ts.at[2],tr.at[2],core).wait_recv()
    tok_x.wait_send(); tok_c.wait_send(); tok_f.wait_send()
    for cp in cnts: cp.wait_send()
    for cp in cnt_in: cp.wait_recv()
    for cp in local: cp.wait()

def gather_all(own_w,own_tok,own_cnt):
    DS=pltpu.SemaphoreType.DMA
    hbm=pl.BlockSpec(memory_space=pl.ANY)
    return pl.pallas_call(gather_kernel,
        out_shape=[jax.ShapeDtypeStruct((8*own_w.shape[0],)+own_w.shape[1:],bf),jax.ShapeDtypeStruct((4,)+own_tok.shape,bf),jax.ShapeDtypeStruct((4,)+own_cnt.shape,own_cnt.dtype)],
        in_specs=[pl.BlockSpec(memory_space=pltpu.VMEM)]*3,out_specs=[hbm]*3,
        scratch_shapes=[DS((2,4)),DS((2,4)),DS((4,)),DS((4,)),DS((8,)),DS((8,)),DS((3,)),DS((3,)),DS((3,)),DS((3,)),DS((3,))],
        compiler_params=pltpu.CompilerParams(has_side_effects=True,vmem_limit_bytes=60<<20),name="gather_weights_tokens")(own_w,own_tok,own_cnt)

def group_sum_kernel(g_ref,o_ref,gd,gs,gr):
    dp=lax.axis_index("dp"); t=lax.axis_index("tile")
    nd=gd.shape[0]
    def copy(k):
        return rcopy(gd.at[dp],gd.at[dp],gs.at[k],gr.at[k],((dp+k)%nd,t))
    def arrive(k):
        q=(dp-k+nd)%nd
        return rcopy(gd.at[q],gd.at[q],gs.at[k],gr.at[k],(q,t))
    def loop(f):
        def s(k,_):
            f(k); return 0
        lax.fori_loop(1,nd,s,0)
    gd[dp]=g_ref[...]
    loop(lambda k: copy(k).start())
    loop(lambda k: arrive(k).wait_recv())
    acc=gd[0]
    for i in range(1,nd): acc=acc+gd[i]
    o_ref[...]=acc
    loop(lambda k: copy(k).wait_send())

def group_sum(g,nd):
    DS=pltpu.SemaphoreType.DMA
    vm=pl.BlockSpec(memory_space=pltpu.VMEM)
    return pl.pallas_call(group_sum_kernel,out_shape=jax.ShapeDtypeStruct(g.shape,f32),in_specs=[vm],out_specs=vm,
        scratch_shapes=[pltpu.VMEM((nd,)+g.shape,f32),DS((nd,)),DS((nd,))],
        compiler_params=pltpu.CompilerParams(has_side_effects=True,vmem_limit_bytes=60<<20),name="sum_groups")(g)

def last_sums_kernel(l_ref,mine,over,v_ref,early,late,vo_ref,yb,zb,own,vb,vd,y1s,y1r,z2s,z2r,z3s,z3r,y4s,y4r,xs,xr,cs,cr,fs,fr,es,er,ts,tr,ds,dr,us,ur):
    z,y,x,c=where_am_i()
    dp=lax.axis_index("dp"); t=lax.axis_index("tile")
    core=dev(z,y,x,1-c); across=dev(z,y,1-x,c); beside=dev(z,1-y,x,c)
    def loop(f,first,n):
        def s(k,_):
            f(k); return 0
        lax.fori_loop(first,n,s,0)
    at=lambda i: pl.ds(i*3,3)
    def y1(k):
        q=(z+k)%4
        return rcopy(l_ref.at[at((1-y)*4+q)],yb.at[q],y1s.at[q],y1r.at[q],beside)
    def z2(k):
        q=(z+k)%4
        return rcopy(own.at[q],zb.at[z],z2s.at[k],z2r.at[k],dev(q,y,x,c))
    def z2_arrive(k):
        q=(z-k+4)%4
        return rcopy(zb.at[q],zb.at[q],z2s.at[k],z2r.at[k],dev(q,y,x,c))
    for k in (2,1,3,0): y1(k).start()
    def t1(k): return rcopy(v_ref.at[(t+k)%4],vb.at[t],ts.at[k],tr.at[k],(dp,(t+k)%4))
    def t1_arrive(k):
        q=(t-k+4)%4
        return rcopy(vb.at[q],vb.at[q],ts.at[k],tr.at[k],(dp,q))
    def d_copy(k): return rcopy(vd.at[dp],vd.at[dp],ds.at[k],dr.at[k],((dp+k)%8,t))
    def d_arrive(k):
        q=(dp-k+8)%8
        return rcopy(vd.at[q],vd.at[q],ds.at[k],dr.at[k],(q,t))
    def t2(k): return rcopy(vo_ref.at[t],vo_ref.at[t],us.at[k],ur.at[k],(dp,(t+k)%4))
    def t2_arrive(k):
        q=(t-k+4)%4
        return rcopy(vo_ref.at[q],vo_ref.at[q],us.at[k],ur.at[k],(dp,q))
    loop(lambda k: t1(k).start(),1,4)
    vb[t]=v_ref[t]
    def place(xx,cc,p): return early.at[pl.ds(cc*12+p*6+xx*3,3)]
    for p in range(2):
        early[pl.ds(c*12+p*6+x*3,3)]=mine[pl.ds(p*3,3)]
        early[pl.ds(c*12+p*6+(1-x)*3,3)]=over[pl.ds(p*3,3)]
    def e_copy(i,p): return rcopy(place(i,c,p),place(i,c,p),es.at[i,p],er.at[i,p],core)
    def e_arrive(i,p): return rcopy(place(i,1-c,p),place(i,1-c,p),es.at[i,p],er.at[i,p],core)
    for p in range(2):
        e_copy(0,p).start(); e_copy(1,p).start()
    loop(lambda k: t1_arrive(k).wait_recv(),1,4)
    vd[dp]=vb[0]+vb[1]+vb[2]+vb[3]
    loop(lambda k: d_copy(k).start(),1,8)
    for k in (2,1,3,0):
        q=(z+k)%4
        y1(k).wait_recv()
        for i in range(3): own[q,i]=(l_ref[(y*4+q)*3+i].astype(f32)+yb[q,i].astype(f32)).astype(bf)
        if k: z2(k).start()
    zb[z]=own[z]
    loop(lambda k: z2_arrive(k).wait_recv(),1,4)
    for i in range(3):
        late[t,(y*4+z)*3+i]=(zb[0,i].astype(f32)+zb[1,i].astype(f32)+zb[2,i].astype(f32)+zb[3,i].astype(f32)).astype(bf)
    def piece(tt,yy,zz): return late.at[tt,at(yy*4+zz)]
    def z3(k): return rcopy(piece(t,y,z),piece(t,y,z),z3s.at[k],z3r.at[k],dev((z+k)%4,y,x,c))
    def z3_arrive(k):
        q=(z-k+4)%4
        return rcopy(piece(t,y,q),piece(t,y,q),z3s.at[k],z3r.at[k],dev(q,y,x,c))
    def y4(q): return rcopy(piece(t,y,q),piece(t,y,q),y4s.at[q],y4r.at[q],beside)
    def y4_arrive(q): return rcopy(piece(t,1-y,q),piece(t,1-y,q),y4s.at[q],y4r.at[q],beside)
    far=(1-x)*2+c
    def x_copy(yy,q): return rcopy(piece(t,yy,q),piece(t,yy,q),xs.at[yy*4+q],xr.at[yy*4+q],across)
    def x_arrive(yy,q): return rcopy(piece(far,yy,q),piece(far,yy,q),xs.at[yy*4+q],xr.at[yy*4+q],across)
    def c_copy(yy,q): return rcopy(piece(t,yy,q),piece(t,yy,q),cs.at[yy*4+q],cr.at[yy*4+q],core)
    def c_arrive(yy,q): return rcopy(piece(x*2+1-c,yy,q),piece(x*2+1-c,yy,q),cs.at[yy*4+q],cr.at[yy*4+q],core)
    def f_copy(yy,q): return rcopy(piece(far,yy,q),piece(far,yy,q),fs.at[yy*4+q],fr.at[yy*4+q],core)
    def f_arrive(yy,q):
        r=piece((1-x)*2+1-c,yy,q)
        return rcopy(r,r,fs.at[yy*4+q],fr.at[yy*4+q],core)
    for k in (1,3,2): z3(k).start()
    y4(z).start(); x_copy(y,z).start(); c_copy(y,z).start()
    def passed_on(k):
        q=(z-k+4)%4
        if k:
            z3_arrive(k).wait_recv()
            y4(q).start(); x_copy(y,q).start(); c_copy(y,q).start()
        y4_arrive(q).wait_recv()
        x_copy(1-y,q).start(); c_copy(1-y,q).start()
    for k in (0,1,3,2): passed_on(k)
    loop(lambda k: d_arrive(k).wait_recv(),1,8)
    acc=vd[0]
    for i in range(1,8): acc=acc+vd[i]
    vo_ref[t]=acc
    loop(lambda k: t2(k).start(),1,4)
    for k in (0,1,3,2):
        q=(z-k+4)%4
        for yy in (y,1-y):
            x_arrive(yy,q).wait_recv(); f_copy(yy,q).start()
    def drain(q):
        for yy in range(2):
            c_arrive(yy,q).wait_recv(); f_arrive(yy,q).wait_recv()
            x_copy(yy,q).wait_send(); c_copy(yy,q).wait_send(); f_copy(yy,q).wait_send()
        y4(q).wait_send()
        y1(q).wait_send()
    loop(drain,0,4)
    def sent(k):
        t2_arrive(k).wait_recv()
        z2(k).wait_send(); z3(k).wait_send(); t1(k).wait_send(); t2(k).wait_send()
    loop(sent,1,4)
    loop(lambda k: d_copy(k).wait_send(),1,8)
    for p in range(2):
        for i in range(2):
            e_arrive(i,p).wait_recv(); e_copy(i,p).wait_send()

def last_sums(own,mine,over,v):
    DS=pltpu.SemaphoreType.DMA
    vm=pl.BlockSpec(memory_space=pltpu.VMEM)
    V=pltpu.VMEM
    S=jax.ShapeDtypeStruct
    rows=(3,v.shape[1])
    early,late,total=pl.pallas_call(last_sums_kernel,out_shape=[S((24,288,128),bf),S((4,24,144,128),bf),S((4,)+rows,f32)],in_specs=[vm]*4,out_specs=[vm]*3,
        scratch_shapes=[V((4,3,144,128),bf)]*3+[V((4,)+rows,f32),V((8,)+rows,f32)]+[DS((4,))]*8+[DS((8,))]*6+[DS((2,2))]*2+[DS((4,))]*2+[DS((8,))]*2+[DS((4,))]*2,
        cost_estimate=pl.CostEstimate(flops=10**7,bytes_accessed=150*10**6,transcendentals=0),
        compiler_params=pltpu.CompilerParams(has_side_effects=True,vmem_limit_bytes=60<<20),name="last_gradient_sums")(own.reshape(24,144,128),mine,over,v.reshape((4,)+rows))
    return early,late.reshape(48,288,128),total.reshape(v.shape)


H = 12
STEP = 10
EPS_NORM = 1e-06
BETA_ONE = 0.5
BETA_TWO = 0.5
ADAM_EPS = 1e-08
RATE_BLOCK = 0.3
RATE_VECTOR = 0.2
NEG_RAW = -8.0e9
HEAD = 64
SCALE = 1.0 / math.sqrt(HEAD)
EXP2 = SCALE * math.log2(math.e)
NN = (((1,), (0,)), ((), ()))
NT = (((1,), (1,)), ((), ()))
TN = (((0,), (0,)), ((), ()))


def mm(a, b, dims=NN):
    return lax.dot_general(a, b, dims, preferred_element_type=f32)


def column_sum(v):
    return jnp.sum(v, axis=0, keepdims=True)


def vmem_spec():
    return pl.BlockSpec(memory_space=pltpu.VMEM)


def smem_spec():
    return pl.BlockSpec(memory_space=pltpu.SMEM)


def any_spec():
    return pl.BlockSpec(memory_space=pl.ANY)


def params(mib=60):
    return pltpu.CompilerParams(vmem_limit_bytes=mib << 20)


def pack(block, odd):
    half = block.shape[0] // 2
    if odd:
        return block[:, 64:], jnp.concatenate([block[half:, :64], block[:half, :64]], axis=1)
    return block[:, :128], jnp.concatenate([block[:half, 128:], block[half:, 128:]], axis=1)


def unpack(top, tail, odd):
    if odd:
        return jnp.concatenate([jnp.concatenate([tail[:, 64:], tail[:, :64]], axis=0), top], axis=1)
    return jnp.concatenate([top, jnp.concatenate([tail[:, :64], tail[:, 64:]], axis=0)], axis=1)


def unpack_either(top, tail, odd):
    return jnp.where(odd, unpack(top, tail, 1), unpack(top, tail, 0))


def lane_sums(v):
    s = column_sum(v)
    return jnp.broadcast_to(s[:, :128] + jnp.concatenate([s[:, 128:], jnp.zeros((1, 64), f32)], axis=1), (8, 128))


def by_parity(value, run):
    for odd in (0, 1):
        pl.when(value == odd)(functools.partial(run, odd))


def turn(v):
    return jnp.concatenate([v[:, 64:], v[:, :64]], axis=1)


def group_of(n):
    return 4 if n % 4 == 0 else 3 if n % 3 == 0 else 1


def pack_kernel(early, order_ref, odd_ref, *refs):
    g = len(refs) - 3
    p_ref, late_ref, s_ref = refs[g:]
    i = pl.program_id(0)
    for b in range(g):
        m = refs[b][0]

        def place(odd, m=m, b=b):
            top, tail = pack(m, odd)
            for ref, here in ((p_ref, i < early), (late_ref, i >= early)):

                @pl.when(here)
                def _():
                    ref[b, :192] = top.astype(bf)
                    ref[b, 192:] = tail.astype(bf)

        by_parity(odd_ref[i * g + b], place)
        s_ref[b] = lane_sums(m * m)


def pack_master(order, odd, master, first):
    n = master.shape[0]
    g = group_of(first)
    early = first // g
    rest = max(n - first, g)
    spec = pltpu.PrefetchScalarGridSpec(
        num_scalar_prefetch=2,
        grid=(n // g,),
        in_specs=[pl.BlockSpec((1, 192, 192), lambda i, s, o, b=b: (s[i * g + b], 0, 0)) for b in range(g)],
        out_specs=[
            pl.BlockSpec((g, 288, 128), lambda i, s, o: (jnp.minimum(i, early - 1), 0, 0)),
            pl.BlockSpec((g, 288, 128), lambda i, s, o: (jnp.maximum(i - early, 0), 0, 0)),
            pl.BlockSpec((g, 8, 128), lambda i, s, o: (i, 0, 0)),
        ],
    )
    return pl.pallas_call(
        functools.partial(pack_kernel, early),
        grid_spec=spec,
        out_shape=[jax.ShapeDtypeStruct((first, 288, 128), bf), jax.ShapeDtypeStruct((rest, 288, 128), bf), jax.ShapeDtypeStruct((n, 8, 128), f32)],
        compiler_params=params(),
        name="pack_master",
    )(order, odd, *[master] * g)


def pick_kernel(at_ref, first_ref, rest_ref, o_ref, sems):
    split = first_ref.shape[0]
    for j in range(12):

        @pl.when(at_ref[j] < split)
        def _():
            pltpu.make_async_copy(first_ref.at[at_ref[j]], o_ref.at[j], sems.at[j]).start()

        @pl.when(at_ref[j] >= split)
        def _():
            pltpu.make_async_copy(rest_ref.at[at_ref[j] - split], o_ref.at[j], sems.at[j]).start()

    for j in range(12):
        pltpu.make_async_copy(first_ref.at[0], o_ref.at[j], sems.at[j]).wait()


def pick(at, first, rest):
    return pl.pallas_call(
        pick_kernel,
        in_specs=[smem_spec(), any_spec(), any_spec()],
        out_specs=vmem_spec(),
        out_shape=jax.ShapeDtypeStruct((12, 288, 128), bf),
        scratch_shapes=[pltpu.SemaphoreType.DMA((12,))],
        compiler_params=params(),
        name="pick_qkv_blocks",
    )(at, first, rest)


def qkv_kernel(src_ref, cnt_ref, at_ref, x0, x1, x2, x3, blk_ref, gain_ref, shift_ref, bq_ref, bv_ref, a_ref, qt_ref, k_ref, kt_ref, v_ref, vt_ref, w_ref, st_ref):
    i = pl.program_id(0)

    @pl.when(i == 0)
    def _():
        def join(odd):
            for r in range(4):
                parts = []
                for c in range(3):
                    p = blk_ref[r * 3 + c].astype(f32)
                    parts.append(unpack(p[:192], p[192:], odd))
                w_ref[r * 192 : (r + 1) * 192, :] = jnp.concatenate(parts, axis=1).astype(bf)

        by_parity(at_ref[0], join)

    x = jnp.concatenate([r[...] for r in (x0, x1, x2, x3)], axis=0).astype(f32)
    mean = jnp.mean(x, axis=-1, keepdims=True)
    cen = x - mean
    inv_std = lax.rsqrt(jnp.mean(cen * cen, axis=-1, keepdims=True) + EPS_NORM)
    a = (cen * inv_std * gain_ref[...] + shift_ref[...]).astype(bf)
    a_ref[...] = a
    qkv = mm(a, w_ref[...])
    q = (qkv[:, :192] + bq_ref[...]).astype(bf).astype(f32)
    k = qkv[:, 192:384].astype(bf).astype(f32)
    v = (qkv[:, 384:] + bv_ref[...]).astype(bf).astype(f32)
    row = lax.broadcasted_iota(jnp.int32, (128, 64), 0)
    lane = lax.broadcasted_iota(jnp.int32, (512, 64), 1)
    masked = jnp.concatenate(
        [jnp.where(row < cnt_ref[4 * i + b], 0.0, NEG_RAW) for b in range(4)], axis=0
    )
    ones = jnp.where(lane < 4, 1.0, 0.0)
    k_tail = jnp.where(lane == 0, masked, ones)
    v_tail = jnp.where(lane < 3, 1.0, 0.0)
    sub = lax.broadcasted_iota(jnp.int32, (64, 512), 0)
    t_tail = jnp.where(sub < 1, 1.0, 0.0)
    qt, kt, vt = q.T, k.T, v.T
    longest = lambda a: jnp.max(jnp.concatenate([column_sum(a[h * 64 : (h + 1) * 64] ** 2) for h in range(3)], axis=0))
    st_ref[0] = jnp.where(lax.broadcasted_iota(jnp.int32, (8, 128), 0) == 0, longest(qt), longest(kt))
    for h in range(3):
        s = slice(h * 64, (h + 1) * 64)
        k_ref[h] = jnp.concatenate([k[:, s], k_tail], axis=1).astype(bf)
        v_ref[h] = jnp.concatenate([v[:, s], v_tail], axis=1).astype(bf)
        qt_ref[h] = jnp.concatenate([qt[s], t_tail], axis=0).astype(bf)
        kt_ref[h] = kt[s].astype(bf)
        vt_ref[h] = jnp.concatenate([vt[s], t_tail[:16]], axis=0).astype(bf)


def qkv_forward(src, cnt, odd, tokens, blocks, gain, shift, bq, bv):
    n = tokens.shape[0]
    rows = [pl.BlockSpec((128, 768), lambda i, s, c, o, k=k: (s[4 * i + k], 0)) for k in range(4)]
    row = lambda i, s, c, o: (0, 0)
    spec = pltpu.PrefetchScalarGridSpec(
        num_scalar_prefetch=3,
        grid=(n // 512,),
        in_specs=rows
        + [pl.BlockSpec((12, 288, 128), lambda i, s, c, o: (0, 0, 0)), pl.BlockSpec((1, 768), row), pl.BlockSpec((1, 768), row), pl.BlockSpec((1, 192), row), pl.BlockSpec((1, 192), row)],
        out_specs=[
            pl.BlockSpec((512, 768), lambda i, s, c, o: (i, 0)),
            pl.BlockSpec((3, 128, 512), lambda i, s, c, o: (0, 0, i)),
            pl.BlockSpec((3, 512, 128), lambda i, s, c, o: (0, i, 0)),
            pl.BlockSpec((3, 64, 512), lambda i, s, c, o: (0, 0, i)),
            pl.BlockSpec((3, 512, 128), lambda i, s, c, o: (0, i, 0)),
            pl.BlockSpec((3, 80, 512), lambda i, s, c, o: (0, 0, i)),
            pl.BlockSpec((768, 576), row),
            pl.BlockSpec((1, 8, 128), lambda i, s, c, o: (i, 0, 0)),
        ],
    )
    shapes = [(n, 768), (3, 128, n), (3, n, 128), (3, 64, n), (3, n, 128), (3, 80, n), (768, 576)]
    return pl.pallas_call(
        qkv_kernel,
        grid_spec=spec,
        out_shape=[jax.ShapeDtypeStruct(s, bf) for s in shapes] + [jax.ShapeDtypeStruct((n // 512, 8, 128), f32)],
        compiler_params=params(),
        name="norm_and_qkv",
    )(src, cnt, odd, tokens, tokens, tokens, tokens, blocks, gain, shift, bq, bv)


def split3(v):
    a = v.astype(bf).astype(f32)
    b = (v - a).astype(bf).astype(f32)
    return a, b, v - a - b


def in_steps(units, sizes, body, carry):
    at = 0
    for size in sizes:
        count = (units - at) // size
        carry = lax.fori_loop(0, count, lambda i, c, at=at, size=size: body(at + i * size, size, c), carry)
        at = at + count * size
    return carry


def attend_kernel(bq, n_ref, k_ref, qt_ref, vt_ref, ot_ref, qb_ref, p_ref, rt_ref):
    live = n_ref[0]
    qi = pl.program_id(1)
    pairs = (live + 7) // 8 * 4

    def finish(top, acc):
        total = acc[64:65]
        ot_ref[0] = acc[:64] / total
        rt_ref[0] = 1.0 / total
        a, b, c = split3((top + jnp.log2(total)) * (-1.0 / EXP2))
        row = lax.broadcasted_iota(jnp.int32, (64, bq), 0)
        tail = jnp.where(row == 0, 1.0, jnp.where(row == 1, a, jnp.where(row == 2, b, jnp.where(row == 3, c, 0.0))))
        qb_ref[0, :64] = qt_ref[0, :64]
        qb_ref[0, 64:] = tail.astype(bf)

    def keys(u, size):
        return pl.ds(pl.multiple_of(u * 256, 256), size * 256)

    @pl.when(jnp.logical_and(qi * bq < live * 128, n_ref[1] == 1))
    def _():
        qt = qt_ref[0]

        def body(u, size, acc):
            step = min(size, 2)
            for part in range(0, size, step):
                at = keys(u + part, step)
                p = jnp.exp2(mm(k_ref[0, at, :], qt) * EXP2).astype(bf)
                p_ref[0, at, :] = p
                acc = acc + mm(vt_ref[0, :, at], p)
            return acc

        finish(0.0, in_steps(pairs, (16, 8, 4), body, jnp.zeros((80, bq), f32)))

    @pl.when(jnp.logical_and(qi * bq < live * 128, n_ref[1] == 0))
    def _():
        qt = qt_ref[0]

        def body(u, size, carry):
            top, acc = carry
            s = mm(k_ref[0, keys(u, size), :], qt) * EXP2
            new = jnp.maximum(top, jnp.max(s, axis=0, keepdims=True))
            p = jnp.exp2(s - new).astype(bf)
            return new, acc * jnp.exp2(top - new) + mm(vt_ref[0, :, keys(u, size)], p)

        finish(*in_steps(pairs, (4,), body, (jnp.full((1, bq), -3e38, f32), jnp.zeros((80, bq), f32))))


def attend(live, k, qt, vt, bq=1024):
    n = k.shape[1]
    spec = pltpu.PrefetchScalarGridSpec(
        num_scalar_prefetch=1,
        grid=(3, n // bq),
        in_specs=[
            pl.BlockSpec((1, n, 128), lambda h, i, s: (h, 0, 0)),
            pl.BlockSpec((1, 128, bq), lambda h, i, s: (h, 0, i)),
            pl.BlockSpec((1, 80, n), lambda h, i, s: (h, 0, 0)),
        ],
        out_specs=[
            pl.BlockSpec((1, 64, bq), lambda h, i, s: (h, 0, i)),
            pl.BlockSpec((1, 128, bq), lambda h, i, s: (h, 0, i)),
            pl.BlockSpec((1, n, bq), lambda h, i, s: (h, 0, i)),
            pl.BlockSpec((1, 1, bq), lambda h, i, s: (h, 0, i)),
        ],
    )
    return pl.pallas_call(
        functools.partial(attend_kernel, bq),
        grid_spec=spec,
        out_shape=[
            jax.ShapeDtypeStruct((3, 64, n), f32),
            jax.ShapeDtypeStruct((3, 128, n), bf),
            jax.ShapeDtypeStruct((3, n, n), bf),
            jax.ShapeDtypeStruct((3, 1, n), f32),
        ],
        compiler_params=params(),
        name="attention_forward",
    )(live, k, qt, vt)


def spread_kernel(src_ref, n_ref, t_ref, ot_ref, *o_refs):
    live, t, tiles = n_ref[0], t_ref[0], len(o_refs)
    per = o_refs[0].shape[1] // 128

    def step(b, _):
        g = src_ref[b]
        lanes = pl.ds(pl.multiple_of(b * 128, 128), 128)
        to = pl.ds(pl.multiple_of((g % per) * 128, 128), 128)
        for k in range(tiles):
            here = (g // per - t + tiles) % tiles == k

            @pl.when(jnp.logical_and(here, b < live))
            def _():
                for h in range(3):
                    o_refs[k][h * 64 : (h + 1) * 64, to] = ot_ref[h, :, lanes].astype(bf)

            @pl.when(jnp.logical_and(here, b >= live))
            def _():
                o_refs[k][:, to] = jnp.zeros((192, 128), bf)

        return 0

    lax.fori_loop(0, ot_ref.shape[2] // 128, step, 0)


def spread(src, live, tile, ot, tiles):
    n = ot.shape[2]
    return pl.pallas_call(
        spread_kernel,
        in_specs=[smem_spec()] * 3 + [vmem_spec()],
        out_specs=[vmem_spec()] * tiles,
        out_shape=[jax.ShapeDtypeStruct((192, n // tiles), bf)] * tiles,
        compiler_params=params(),
        name="spread_attended",
    )(src, live, tile, ot)


def collect_kernel(src_ref, n_ref, t_ref, ot_ref, rt_ref, *refs):
    g_refs, dt_ref = refs[:-1], refs[-1]
    live, t, tiles = n_ref[0], t_ref[0], len(g_refs)
    mild = n_ref[1] == 1
    per = g_refs[0].shape[1] // 128
    row = lax.broadcasted_iota(jnp.int32, (64, 128), 0)

    def step(b, _):
        g = src_ref[b]
        to = pl.ds(pl.multiple_of(b * 128, 128), 128)
        lanes = pl.ds(pl.multiple_of((g % per) * 128, 128), 128)
        for k in range(tiles):

            @pl.when(jnp.logical_and((t - g // per + tiles) % tiles == k, b < live))
            def _():
                for h in range(3):
                    scale = jnp.where(mild, rt_ref[h, :, to], 1.0)
                    d = (g_refs[k][h * 64 : (h + 1) * 64, lanes].astype(f32) * scale).astype(bf).astype(f32)
                    x, y, z = split3(-jnp.sum(d * ot_ref[h, :, to], axis=0, keepdims=True))
                    tail = jnp.where(row == 0, x, jnp.where(row == 1, y, jnp.where(row == 2, z, 0.0)))
                    dt_ref[h, :, to] = jnp.concatenate([d, tail], axis=0).astype(bf)

        @pl.when(b >= live)
        def _():
            dt_ref[:, :, to] = jnp.zeros((3, 128, 128), bf)

        return 0

    lax.fori_loop(0, ot_ref.shape[2] // 128, step, 0)


def collect(src, live, tile, grads, ot, rt):
    n = ot.shape[2]
    return pl.pallas_call(
        collect_kernel,
        in_specs=[smem_spec()] * 3 + [vmem_spec()] * (2 + len(grads)),
        out_specs=vmem_spec(),
        out_shape=jax.ShapeDtypeStruct((3, 128, n), bf),
        compiler_params=params(),
        name="collect_attended_grad",
    )(src, live, tile, ot, rt, *grads)


def attend_back_kernel(bk, n_ref, p_ref, k_ref, kt_ref, v_ref, qb_ref, dt_ref, dq_ref, dk_ref, dv_ref):
    live = n_ref[0]
    j = pl.program_id(1)

    @pl.when(j == 0)
    def _():
        dq_ref[...] = jnp.zeros_like(dq_ref)

    def lanes(u):
        return pl.ds(pl.multiple_of(u * 256, 256), 256)

    pairs = (live + 1) // 2

    def over_queries(rows, sizes, body):
        zero = jnp.zeros((rows, 64), f32)
        dk, dv = in_steps((live + 7) // 8 * 4, sizes, body, (zero, zero))
        dk_ref[0, :rows] = (dk * SCALE).astype(bf)
        dv_ref[0, :rows] = dv.astype(bf)

    def with_kept(rows):
        k, v, kt = k_ref[0, :rows], v_ref[0, :rows], kt_ref[0, :, :rows]

        def body(u, size, carry):
            dk, dv = carry
            dp = mm(v, dt_ref[0, :, lanes(u)])
            for part in range(size):
                at = lanes(u + part)
                ahead = mm(v, dt_ref[0, :, lanes(u + part + 1)]) if part + 1 < size else None
                p = p_ref[0, :rows, at]
                ds = (p.astype(f32) * dp).astype(bf)
                dv = dv + mm(p, dt_ref[0, :64, at], NT)
                dk = dk + mm(ds, qb_ref[0, :64, at], NT)
                dq_ref[0, :, at] += mm(kt, ds)
                dp = dp if ahead is None else ahead
            return dk, dv

        over_queries(rows, (16, 8, 4), body)

    @pl.when(jnp.logical_and(n_ref[1] == 1, 2 * j + 2 <= pairs))
    def _():
        with_kept(bk)

    @pl.when(jnp.logical_and(n_ref[1] == 1, 2 * j + 1 == pairs))
    def _():
        dk_ref[0, bk // 2 :] = jnp.zeros((bk // 2, 64), bf)
        dv_ref[0, bk // 2 :] = jnp.zeros((bk // 2, 64), bf)
        with_kept(bk // 2)

    @pl.when(jnp.logical_and(n_ref[1] == 0, j * bk < live * 128))
    def _():
        k, v, kt = k_ref[0], v_ref[0], kt_ref[0]

        def body(u, size, carry):
            dk, dv = carry
            for part in range(size):
                at = lanes(u + part)
                p = jnp.exp2(mm(k, qb_ref[0, :, at]) * EXP2)
                ds = (p * mm(v, dt_ref[0, :, at])).astype(bf)
                dv = dv + mm(p.astype(bf), dt_ref[0, :64, at], NT)
                dk = dk + mm(ds, qb_ref[0, :64, at], NT)
                dq_ref[0, :, at] += mm(kt, ds)
            return dk, dv

        over_queries(bk, (4,), body)


def attend_back(first, heads, live, p, k, kt, v, qb, dt, bk=512):
    n = k.shape[1]
    whole_t = lambda h, j, s: (first + h, 0, 0)
    rows = lambda h, j, s: (first + h, j, 0)
    spec = pltpu.PrefetchScalarGridSpec(
        num_scalar_prefetch=1,
        grid=(heads, n // bk),
        in_specs=[
            pl.BlockSpec((1, bk, n), rows),
            pl.BlockSpec((1, bk, 128), rows),
            pl.BlockSpec((1, 64, bk), lambda h, j, s: (first + h, 0, j)),
            pl.BlockSpec((1, bk, 128), rows),
            pl.BlockSpec((1, 128, n), whole_t),
            pl.BlockSpec((1, 128, n), whole_t),
        ],
        out_specs=[
            pl.BlockSpec((1, 64, n), lambda h, j, s: (h, 0, 0)),
            pl.BlockSpec((1, bk, 64), lambda h, j, s: (h, j, 0)),
            pl.BlockSpec((1, bk, 64), lambda h, j, s: (h, j, 0)),
        ],
    )
    S = jax.ShapeDtypeStruct
    return pl.pallas_call(
        functools.partial(attend_back_kernel, bk),
        grid_spec=spec,
        out_shape=[S((heads, 64, n), f32), S((heads, n, 64), bf), S((heads, n, 64), bf)],
        cost_estimate=pl.CostEstimate(flops=heads * 4 * 10**10, bytes_accessed=heads * 50 * 10**6, transcendentals=0),
        compiler_params=params(),
        name="attention_backward",
    )(live, p, k, kt, v, qb, dt)


def qkv_back_kernel(given, src_ref, n_ref, odd_ref, x0, x1, x2, x3, gain_ref, a_ref, w_ref, *refs):
    grads, (ga_ref, gz_ref, gw_ref, gb_ref, vs_ref, acc, sums, rows, sems) = refs[:given], refs[given:]
    dqs, dks, dvs = [[(r, h) for r in grads[j::3] for h in range(r.shape[0])] for j in range(3)]
    early = ga_ref.shape[1] // 128
    i = pl.program_id(0)
    live = n_ref[0]

    @pl.when(i == 0)
    def _():
        acc[...] = jnp.zeros_like(acc)
        sums[...] = jnp.zeros_like(sums)
        vs_ref[...] = jnp.zeros_like(vs_ref)

    @pl.when(4 * i < live)
    def _():
        dq = jnp.concatenate([r[h] for r, h in dqs], axis=0).T * SCALE
        g = jnp.concatenate([dq] + [r[h].astype(f32) for r, h in dks + dvs], axis=1).astype(bf)
        acc[...] += mm(a_ref[...], g, TN)
        sums[...] += jnp.broadcast_to(column_sum(g.astype(f32)), sums.shape)
        g1 = mm(g, w_ref[...], NT)
        rows[...] = g1.astype(bf)
        x = jnp.concatenate([r[...] for r in (x0, x1, x2, x3)], axis=0).astype(f32)
        cen = x - jnp.mean(x, axis=-1, keepdims=True)
        normed = cen * lax.rsqrt(jnp.mean(cen * cen, axis=-1, keepdims=True) + EPS_NORM)
        vs_ref[0:1, :] += column_sum(g1 * normed)
        vs_ref[1:2, :] += column_sum(g1)

    @pl.when(4 * i >= live)
    def _():
        rows[...] = jnp.zeros_like(rows)

    per = early + gz_ref.shape[1] // 128
    for b in range(4):
        block, at = rows.at[pl.ds(b * 128, 128)], src_ref[4 * i + b]
        t, j = at // per, at % per

        @pl.when(j < early)
        def _():
            pltpu.make_async_copy(block, ga_ref.at[t, pl.ds(pl.multiple_of(j * 128, 128), 128)], sems.at[b]).start()

        @pl.when(j >= early)
        def _():
            pltpu.make_async_copy(block, gz_ref.at[t, pl.ds(pl.multiple_of((j - early) * 128, 128), 128)], sems.at[b]).start()

    for b in range(4):
        pltpu.make_async_copy(rows.at[pl.ds(b * 128, 128)], ga_ref.at[0, pl.ds(0, 128)], sems.at[b]).wait()

    @pl.when(i == pl.num_programs(0) - 1)
    def _():
        def place(odd):
            for r in range(4):
                for c in range(3):
                    top, tail = pack(acc[r * 192 : (r + 1) * 192, c * 192 : (c + 1) * 192], odd)
                    gw_ref[r * 3 + c, :192] = top.astype(bf)
                    gw_ref[r * 3 + c, 192:] = tail.astype(bf)

        by_parity(odd_ref[0], place)
        gb_ref[...] = sums[...]


def qkv_backward(src, live, odd, tokens, gain, a, w, grads, tiles, early):
    n = a.shape[0]
    per = n // tiles
    fixed = lambda i, s, c, o: (0, 0)
    row = lambda i, s, c, o: (0, i, 0)
    spec = pltpu.PrefetchScalarGridSpec(
        num_scalar_prefetch=3,
        grid=(n // 512,),
        in_specs=[pl.BlockSpec((128, 768), lambda i, s, c, o, k=k: (s[4 * i + k], 0)) for k in range(4)]
        + [pl.BlockSpec((1, 768), fixed), pl.BlockSpec((512, 768), lambda i, s, c, o: (i, 0)), pl.BlockSpec((768, 576), fixed)]
        + [
            pl.BlockSpec((g.shape[0], 64, 512), lambda i, s, c, o: (0, 0, i)) if g.shape[1] == 64 else pl.BlockSpec((g.shape[0], 512, 64), row)
            for g in grads
        ],
        out_specs=[any_spec(), any_spec(), pl.BlockSpec((12, 288, 128), lambda i, s, c, o: (0, 0, 0)), pl.BlockSpec((8, 576), fixed), pl.BlockSpec((8, 768), fixed)],
        scratch_shapes=[pltpu.VMEM((768, 576), f32), pltpu.VMEM((8, 576), f32), pltpu.VMEM((512, 768), bf), pltpu.SemaphoreType.DMA((4,))],
    )
    S = jax.ShapeDtypeStruct
    return pl.pallas_call(
        functools.partial(qkv_back_kernel, len(grads)),
        grid_spec=spec,
        out_shape=[S((tiles, early, 768), bf), S((tiles, per - early, 768), bf), S((12, 288, 128), bf), S((8, 576), f32), S((8, 768), f32)],
        cost_estimate=pl.CostEstimate(flops=3 * 10**10, bytes_accessed=40 * 10**6, transcendentals=0),
        compiler_params=params(),
        name="qkv_backward",
    )(src, live, odd, tokens, tokens, tokens, tokens, gain, a, w, *grads)


def gelu_parts(z):
    cdf = 0.5 + 0.5 * lax.erf(z * math.sqrt(0.5))
    return z * cdf, cdf + z * (jnp.exp2(z * z * (-0.5 * math.log2(math.e))) * (1.0 / math.sqrt(2.0 * math.pi)))


def middle_kernel(inv_ref, cnt_ref, t_ref, blk_ref, rest_ref, o0, o1, o2, o3, x_ref, c_ref, vp_ref, bu_ref, y_ref, gr_ref, g0, g1, g2_ref, g3,
                  u_s, gz_s, a2_s, gm_s, gb_s, o_s, vs_ref, us_ref, w_out, w_up, w_down, tails, tsem, isem):
    i = pl.program_id(0)
    rows = x_ref.shape[0]
    split = blk_ref.shape[0]
    r0 = i * rows
    kinds = ((w_out, 48, 2, 4), (w_up, 64, 8, 4), (w_down, 128, 2, 16))

    @pl.when(i == 0)
    def _():
        vs_ref[...] = jnp.zeros_like(vs_ref)
        us_ref[...] = jnp.zeros_like(us_ref)

        def pair(w, first, pairs):
            def parts(j, run):
                r = pl.multiple_of((j // pairs) * 192, 64)
                col = pl.multiple_of((j % pairs) * 384, 128)
                for b, off in ((0, 0), (1, 256)):
                    at = first + 2 * j + b
                    run(at, w.at[pl.ds(r, 192), pl.ds(col + off, 128)], tails.at[at - 48])
                return r, col

            def fetch(at, top, tail):
                for ref, here, slot in ((blk_ref, inv_ref[at] < split, inv_ref[at]), (rest_ref, inv_ref[at] >= split, inv_ref[at] - split)):

                    @pl.when(here)
                    def _():
                        pltpu.make_async_copy(ref.at[slot, pl.ds(0, 192)], top, tsem.at[at - 48]).start()
                        pltpu.make_async_copy(ref.at[slot, pl.ds(192, 96)], tail, isem.at[at - 48]).start()

            def fetched(at, top, tail):
                pltpu.make_async_copy(blk_ref.at[0, pl.ds(0, 192)], top, tsem.at[at - 48]).wait()
                pltpu.make_async_copy(blk_ref.at[0, pl.ds(192, 96)], tail, isem.at[at - 48]).wait()

            def start(j, _):
                parts(j, fetch)
                return 0

            def join(j, _):
                r, col = parts(j, fetched)
                even = tails[first + 2 * j - 48].astype(f32)
                odd = tails[first + 2 * j - 47].astype(f32)
                lane = lax.broadcasted_iota(jnp.int32, even.shape, 1) < 64
                w[pl.ds(r, 96), pl.ds(col + 128, 128)] = jnp.where(lane, even, odd).astype(bf)
                w[pl.ds(r + 96, 96), pl.ds(col + 128, 128)] = turn(jnp.where(lane, odd, even)).astype(bf)
                return 0

            return start, join

        todo = [(pair(w, first, pairs), pairs * high) for w, first, pairs, high in kinds]
        for (start, _), n in todo:
            lax.fori_loop(0, n, start, 0)

        for (_, join), n in todo:
            lax.fori_loop(0, n, join, 0)

    vp = vp_ref[...]
    row = r0 + lax.broadcasted_iota(jnp.int32, (rows, 1), 0)
    live = jnp.where(row < cnt_ref[0], 1.0, 0.0)
    t = t_ref[0]
    for k, ref in enumerate((o0, o1, o2, o3)):
        o_s[pl.ds(pl.multiple_of(((t - k + 4) % 4) * 192, 64), 192), :] = ref[...]
    o_t = o_s[...]
    res = x_ref[...].astype(f32) + mm(o_t, w_out[...], TN) + vp[6:7]
    cen = res - jnp.mean(res, axis=-1, keepdims=True)
    inv_std = lax.rsqrt(jnp.mean(cen * cen, axis=-1, keepdims=True) + EPS_NORM)
    normed = cen * inv_std
    a2 = (normed * vp[2:3] + vp[3:4]).astype(bf)
    gy = c_ref[...].astype(f32) * live
    gm = gy.astype(bf)
    a2_s[...] = a2
    gm_s[...] = gm
    branch = jnp.zeros((rows, 768), f32)
    g2 = jnp.zeros((rows, 768), f32)
    for j in range(4):
        cols = slice(j * 768, (j + 1) * 768)
        u, slope = gelu_parts(mm(a2, w_up[:, cols]) + bu_ref[:, cols])
        u = u.astype(bf)
        u_s[:, cols] = u
        branch = branch + mm(u, w_down[cols, :])
        gz = (mm(gm, w_down[cols, :], NT) * slope).astype(bf)
        gz_s[:, cols] = gz
        us_ref[:, cols] += jnp.broadcast_to(column_sum(gz.astype(f32)), (8, 768))
        g2 = g2 + mm(gz, w_up[:, cols], NT)
    y_ref[...] = (live * (res + branch + vp[7:8])).astype(bf)
    d2 = g2 * vp[2:3]
    gr = gy + inv_std * (d2 - jnp.mean(d2, axis=-1, keepdims=True) - normed * jnp.mean(d2 * normed, axis=-1, keepdims=True))
    gr_ref[...] = gr
    gb = gr.astype(bf)
    gb_s[...] = gb
    vs_ref[0:1, :] += column_sum(g2 * normed)
    vs_ref[1:2, :] += column_sum(g2)
    vs_ref[2:3, :] += column_sum(gb.astype(f32))
    vs_ref[3:4, :] += column_sum(gm.astype(f32))
    for k, ref in enumerate((g0, g1, g2_ref, g3)):
        ref[...] = mm(w_out[pl.ds(pl.multiple_of(((t + k) % 4) * 192, 64), 192), :], gb, NT).astype(bf)


def weight_grad_kernel(outs, pos_ref, o_in, gb_in, a2_in, gz_in, u_in, gm_in, *refs):
    s_refs, (o_s, gb_s, a2_s, gz_s, u_s, gm_s, ring, zero, lsem, osem, zsem) = refs[:outs], refs[outs:]
    each = s_refs[0].shape[0]

    def to_slot(block, at, sem):
        for o in range(outs):

            @pl.when(at // each == o)
            def _():
                pltpu.make_async_copy(block, s_refs[o].at[at % each], sem).start()

    def landed(block, sem):
        pltpu.make_async_copy(block, s_refs[0].at[0], sem).wait()

    loads = [pltpu.make_async_copy(a, b, lsem.at[j]) for j, (a, b) in enumerate(
        ((o_in, o_s), (gb_in, gb_s), (a2_in, a2_s), (gz_in, gz_s), (gm_in, gm_s), (u_in, u_s)))]
    for load in loads:
        load.start()
    zero[...] = jnp.zeros_like(zero)

    def clear(j, _):
        to_slot(zero, pos_ref[j], zsem.at[j])
        return 0

    lax.fori_loop(0, 48, clear, 0)
    def send(n, g, first, pairs, high, low):
        half = (n % 2) * 8

        def put(r, b):
            return first + (high + r) * 2 * pairs + 2 * low + b

        for r in range(4):
            part = g[r * 192 : (r + 1) * 192]
            mid = part[:, 128:256]
            upper, lower = mid[:96], turn(mid[96:])
            lane = lax.broadcasted_iota(jnp.int32, upper.shape, 1) < 64
            for b, top, tail in ((0, part[:, :128], jnp.where(lane, upper, lower)), (1, part[:, 256:], jnp.where(lane, lower, upper))):
                k = half + 2 * r + b

                @pl.when(n >= 2)
                def _():
                    landed(ring.at[k], osem.at[k])

                ring[k, :192] = top.astype(bf)
                ring[k, 192:] = tail.astype(bf)
                to_slot(ring.at[k], pos_ref[put(r, b)], osem.at[k])

    def lanes(j):
        return pl.ds(pl.multiple_of(j * 384, 128), 384)

    def grad_out(n, _):
        send(n, mm(o_s[...], gb_s[:, lanes(n)]), 48, 2, 0, n)
        return 0

    def grad_up(n, _):
        send(n, mm(a2_s[...], gz_s[:, lanes(n)], TN), 64, 8, 0, n)
        return 0

    def grad_down(n, _):
        high = n // 2
        send(n, mm(u_s[:, pl.ds(pl.multiple_of(high * 768, 128), 768)], gm_s[:, lanes(n % 2)], TN), 128, 2, high * 4, n % 2)
        return 0

    def drain():
        for k in range(16):
            landed(ring.at[k], osem.at[k])

    for f, n, first in ((grad_out, 2, 0), (grad_up, 8, 2), (grad_down, 8, 4)):
        loads[first].wait()
        loads[first + 1].wait()
        lax.fori_loop(0, n, f, 0)
        drain()

    def cleared(j, _):
        landed(zero, zsem.at[j])
        return 0

    lax.fori_loop(0, 48, cleared, 0)


def middle(inv, count, tile, blocks, rest, o_parts, tokens, cotangent, vec_params, bias_up, rows=256):
    n, width = tokens.shape
    hidden = bias_up.shape[1]
    row = lambda i, s, c, t: (i, 0)
    fixed = lambda i, s, c, t: (0, 0)
    col = lambda i, s, c, t: (0, i)
    V, DS = pltpu.VMEM, pltpu.SemaphoreType.DMA
    narrow, wide, part = pl.BlockSpec((rows, width), row), pl.BlockSpec((rows, hidden), row), pl.BlockSpec((192, rows), col)
    spec = pltpu.PrefetchScalarGridSpec(
        num_scalar_prefetch=3,
        grid=(n // rows,),
        in_specs=[any_spec()] * 2 + [part] * 4 + [narrow, narrow, pl.BlockSpec((12, width), fixed), pl.BlockSpec((1, hidden), fixed)],
        out_specs=[narrow, narrow] + [part] * 4 + [wide, wide, narrow, narrow, narrow, pl.BlockSpec((width, rows), col),
                   pl.BlockSpec((8, width), fixed), pl.BlockSpec((8, hidden), fixed)],
        scratch_shapes=[V((768, 768), bf), V((768, 3072), bf), V((3072, 768), bf), V((144, 96, 128), bf), DS((144,)), DS((144,))],
    )
    S = jax.ShapeDtypeStruct
    return pl.pallas_call(
        middle_kernel,
        grid_spec=spec,
        out_shape=[S((n, width), bf), S((n, width), f32)] + [S((192, n), bf)] * 4 + [S((n, hidden), bf)] * 2 + [S((n, width), bf)] * 3
        + [S((width, n), bf), S((8, width), f32), S((8, hidden), f32)],
        compiler_params=params(),
        name="projection_and_mlp",
    )(inv, count, tile, blocks, rest, *o_parts, tokens, cotangent, vec_params, bias_up)


def weight_grads_to_slots(pos, outs, block_count, o_t, gb, a2, gz, u, gm):
    V, DS = pltpu.VMEM, pltpu.SemaphoreType.DMA
    arrays = (o_t, gb, a2, gz, u, gm)
    return pl.pallas_call(
        functools.partial(weight_grad_kernel, outs),
        in_specs=[smem_spec()] + [any_spec()] * 6,
        out_specs=[any_spec()] * outs,
        out_shape=[jax.ShapeDtypeStruct((block_count // outs, 288, 128), bf)] * outs,
        scratch_shapes=[V(a.shape, bf) for a in arrays] + [V((16, 288, 128), bf), V((288, 128), bf), DS((6,)), DS((16,)), DS((48,))],
        cost_estimate=pl.CostEstimate(flops=6 * 10**10, bytes_accessed=32 * 10**6, transcendentals=0),
        compiler_params=params(),
        name="mlp_weight_gradients",
    )(pos, *arrays)


def quarters(b0, b1):
    return (b0 * 2 + b1, (1 - b0) * 2 + b1, b0 * 2 + 1 - b1, (1 - b0) * 2 + 1 - b1)


def add_pair_kernel(common, bits_ref, *refs):
    outs = list(refs[16:])
    for p in range(2):
        for side in range(4):
            j = 4 * p + side
            total = (refs[2 * j][...].astype(f32) + refs[2 * j + 1][...].astype(f32)).astype(bf)
            if side == common[p]:
                outs[6][p] = total
            else:
                outs[3 * p + side - (side > common[p])][...] = total


def add_pair(bits, common, keep, came):
    specs = []
    for p in range(2):
        for side in range(4):
            at = lambda i, b, p=p, side=side: (p * 12 + quarters(b[2 * p], b[2 * p + 1])[side] * 3 + i, 0, 0)
            specs += [pl.BlockSpec((4, 288, 128), at)] * 2
    S = jax.ShapeDtypeStruct
    return pl.pallas_call(
        functools.partial(add_pair_kernel, common),
        grid_spec=pltpu.PrefetchScalarGridSpec(
            num_scalar_prefetch=1,
            grid=(3,),
            in_specs=specs,
            out_specs=[pl.BlockSpec((4, 288, 128), lambda i, b: (i, 0, 0))] * 6 + [pl.BlockSpec((2, 4, 288, 128), lambda i, b: (0, i, 0, 0))],
        ),
        out_shape=[S((12, 288, 128), bf)] * 6 + [S((2, 12, 288, 128), bf)],
        compiler_params=params(),
        name="add_gradients_of_cores",
    )(bits, *[keep, came] * 8)


def add_four_kernel(common, bits_ref, *refs):
    outs = refs[7:]
    for p in range(2):
        parts = refs[3 * p : 3 * p + 3]
        for side, q in enumerate(quarters(bits_ref[2 * p], bits_ref[2 * p + 1])):
            for b in range(3):
                total = (sum(r[q * 3 + b].astype(f32) for r in parts) + refs[6][p, q * 3 + b].astype(f32)).astype(bf)
                if side == common[p]:
                    outs[6][p, b] = total
                else:
                    outs[3 * p + side - (side > common[p])][b] = total


def add_four(bits, common, parts):
    S = jax.ShapeDtypeStruct
    return pl.pallas_call(
        functools.partial(add_four_kernel, common),
        in_specs=[smem_spec()] + [vmem_spec()] * 7,
        out_specs=[vmem_spec()] * 7,
        out_shape=[S((3, 288, 128), bf)] * 6 + [S((2, 3, 288, 128), bf)],
        compiler_params=params(),
        name="add_gradients",
    )(bits, *parts)


def add_last_kernel(*refs):
    for p in range(2):
        for b in range(3):
            refs[7][3 * p + b] = (sum(r[b].astype(f32) for r in refs[3 * p : 3 * p + 3]) + refs[6][p, b].astype(f32)).astype(bf)


def add_last(parts):
    return pl.pallas_call(
        add_last_kernel,
        in_specs=[vmem_spec()] * 7,
        out_specs=vmem_spec(),
        out_shape=jax.ShapeDtypeStruct((6, 288, 128), bf),
        compiler_params=params(),
        name="add_last_gradients",
    )(*parts)


def split2(v):
    hi = v.astype(bf)
    return hi, (v - hi.astype(f32)).astype(bf)


def mm3(a, b, dims):
    return mm(a[0], b[0], dims) + (mm(a[0], b[1], dims) + mm(a[1], b[0], dims))


def adam_kernel(odd_ref, from_ref, g_ref, late_ref, m1_ref, m2_ref, l_ref, r_ref, g_out, m1_out, m2_out, u_out, s_out):
    for b in range(g_ref.shape[0]):
        slot = pl.program_id(0) * g_ref.shape[0] + b
        place = from_ref[slot]
        part = jnp.where(place >= 0, late_ref[jnp.maximum(place, 0)].astype(f32), g_ref[b].astype(f32))
        grad = unpack_either(part[:192], part[192:], odd_ref[slot] == 1)
        left, right = split2(l_ref[b]), split2(r_ref[b])
        low = grad.astype(bf)
        rot = mm3(split2(mm(left[0], low, TN) + mm(left[1], low, TN)), right, NN)
        g_out[b] = grad
        first = BETA_ONE * m1_ref[b] + (1.0 - BETA_ONE) * rot
        second = BETA_TWO * m2_ref[b] + (1.0 - BETA_TWO) * rot * rot
        upd = (first / (1.0 - BETA_ONE**STEP)) / (jnp.sqrt(second / (1.0 - BETA_TWO**STEP)) + ADAM_EPS)
        upd = mm3(split2(mm3(left, split2(upd), NN)), right, NT)
        m1_out[b] = first
        m2_out[b] = second
        u_out[b] = upd
        s_out[b] = lane_sums(upd * upd)


def adam(odd, late_at, grads, late, first, second, left, right):
    n = grads.shape[0]
    g = group_of(n)
    at = lambda i, s, f: (i, 0, 0)
    big = pl.BlockSpec((g, 192, 192), at)
    spec = pltpu.PrefetchScalarGridSpec(
        num_scalar_prefetch=2,
        grid=(n // g,),
        in_specs=[pl.BlockSpec((g, 288, 128), at), pl.BlockSpec(late.shape, lambda i, s, f: (0, 0, 0))] + [big] * 4,
        out_specs=[big] * 4 + [pl.BlockSpec((g, 8, 128), at)],
    )
    return pl.pallas_call(
        adam_kernel,
        grid_spec=spec,
        out_shape=[jax.ShapeDtypeStruct((n, 192, 192), f32)] * 4 + [jax.ShapeDtypeStruct((n, 8, 128), f32)],
        compiler_params=params(),
        name="rotated_adam",
    )(odd, late_at, grads, late, first, second, left, right)


def update_kernel(rate_ref, m_ref, u_ref, mo_ref, mc_ref):
    g = m_ref.shape[0]
    for b in range(g):
        new = m_ref[b] - rate_ref[pl.program_id(0) * g + b] * u_ref[b]
        mo_ref[b] = new
        mc_ref[b] = new.astype(bf)


def new_weights(rate, master, update):
    n = master.shape[0]
    g = 8 if n % 8 == 0 else group_of(n)
    big = pl.BlockSpec((g, 192, 192), lambda i, r: (i, 0, 0))
    return pl.pallas_call(
        update_kernel,
        grid_spec=pltpu.PrefetchScalarGridSpec(num_scalar_prefetch=1, grid=(n // g,), in_specs=[big] * 2, out_specs=[big] * 2),
        out_shape=[jax.ShapeDtypeStruct(master.shape, f32), jax.ShapeDtypeStruct(master.shape, bf)],
        compiler_params=params(),
        name="new_weights",
    )(rate, master, update)


def halving_places(slot, core):
    dp, r = slot // 24, slot % 24
    y, z, far, x, s = dp % 2, dp // 2 % 2, dp // 4, r % 6 // 3, r % 3
    portion = r % 12 // 6
    inside = jnp.where(portion == 0, x * 8 + y * 4 + z * 2 + far, y * 8 + z * 4 + x * 2 + far)
    return jnp.where(r // 12 == core, 0, 96) + portion * 48 + inside * 3 + s


def norm_forward(row_data, gain_vec, shift_vec):
    row_mean = jnp.mean(row_data, axis=-1, keepdims=True)
    centred = row_data - row_mean
    inv_std = lax.rsqrt(jnp.mean(centred * centred, axis=-1, keepdims=True) + EPS_NORM)
    normed = centred * inv_std
    return (normed * gain_vec + shift_vec, normed, inv_std)


def norm_back(grad_out, normed, inv_std, gain_vec):
    grad_normed = grad_out * gain_vec
    return inv_std * (
        grad_normed
        - jnp.mean(grad_normed, axis=-1, keepdims=True)
        - normed * jnp.mean(grad_normed * normed, axis=-1, keepdims=True)
    )


def block_plan(counts, slot_count):
    tiles = counts.shape[0]
    per = slot_count // 128
    j = lax.broadcasted_iota(jnp.int32, (tiles, per), 1)
    kept = jnp.clip(counts[:, None] - j * 128, 0, 128).reshape(-1)
    full = (kept > 0).astype(jnp.int32)
    index = jnp.arange(tiles * per, dtype=jnp.int32)
    before = (index[None, :] < index[:, None]).astype(jnp.int32)
    ahead = jnp.sum(before * full[None, :], axis=1)
    live = jnp.sum(full)
    place = jnp.where(full > 0, ahead, live + index - ahead)
    hot = (place[None, :] == index[:, None]).astype(jnp.int32)
    return jnp.sum(hot * index[None, :], axis=1), jnp.sum(hot * kept[None, :], axis=1), live.reshape(1)


def make_body(tuned):
    def body(tokens, cotangent, counts, master, slot_block, groups, first_moment, second_moment, left_basis, right_basis, vec_params, vec_first, vec_second):
        slot_count, width = tokens.shape[1:]
        per_owner = master.shape[0]
        tile = lax.axis_index("tile")
        block_count = slot_block.shape[0]
        first = per_owner // 2 if tuned else per_owner
        index = jnp.arange(block_count, dtype=jnp.int32)
        owner = index // per_owner
        same = (owner[None, :] == owner[:, None]).astype(jnp.int32)
        is_qkv = (slot_block < 48).astype(jnp.int32)
        sooner = same * jnp.where(is_qkv[None, :] == is_qkv[:, None], (index[None, :] < index[:, None]).astype(jnp.int32), is_qkv[None, :])
        rank = jnp.sum(sooner, axis=1)
        place = jnp.where(rank < first, owner * first + rank, block_count // per_owner * first + owner * (per_owner - first) + rank - first)
        most = jnp.max(jnp.sum(same * is_qkv[None, :], axis=1))
        start = lax.axis_index("dp") * per_owner
        mine = lax.dynamic_slice(slot_block, (start,), (per_owner,))
        odd = mine % 2
        local = jnp.arange(per_owner, dtype=jnp.int32)
        at_rank = (lax.dynamic_slice(rank, (start,), (per_owner,))[None, :] == local[:, None]).astype(jnp.int32)
        order = jnp.sum(at_rank * local[None, :], axis=1)
        packed, packed_rest, weight_sq = pack_master(order, jnp.sum(at_rank * odd[None, :], axis=1), master, first)
        own_tokens = tokens.reshape(slot_count, width)
        count_tile = jnp.broadcast_to(counts.reshape(1, 1), (8, 128))
        if tuned:
            blocks, token_all, count_all = gather_all(packed, own_tokens, count_tile)
            packed_rest, blocks = lax.optimization_barrier((packed_rest, blocks))
            blocks_rest = lax.all_gather(packed_rest, "dp", axis=0, tiled=True)
        else:
            blocks = lax.all_gather(packed, "dp", axis=0, tiled=True)
            token_all = lax.all_gather(own_tokens, "tile", axis=0)
            count_all = lax.all_gather(count_tile, "tile", axis=0)
            blocks_rest = packed_rest
        tiles = token_all.shape[0]
        src, cnt, live = block_plan(count_all[:, 0, 0], slot_count)
        is_at = (slot_block[None, :] == index[:, None]).astype(jnp.int32)
        inverse = jnp.sum(is_at * index[None, :], axis=1)
        places = jnp.sum(is_at * place[None, :], axis=1)
        own_block = jnp.arange(12, dtype=jnp.int32) // 3 * 12 + jnp.arange(12, dtype=jnp.int32) % 3 * 4 + tile
        own_at = jnp.sum((slot_block[None, :] == own_block[:, None]).astype(jnp.int32) * place[None, :], axis=1)
        if tuned:
            qkv_blocks = lax.cond(
                most <= first,
                lambda: pick(own_at, blocks, packed_rest),
                lambda: pick(own_at, blocks, lax.all_gather(packed_rest, "dp", axis=0, tiled=True)),
            )
        else:
            qkv_blocks = pick(own_at, blocks, blocks_rest)
        tile_one = tile.astype(jnp.int32).reshape(1)
        own = width // tiles
        bias = lambda row: lax.dynamic_slice(vec_params[row : row + 1], (0, tile * own), (1, own))
        a1, qt, k, kt, v, vt, w_qkv, lengths = qkv_forward(
            src, cnt, tile_one % 2, token_all.reshape(-1, width), qkv_blocks, vec_params[0:1], vec_params[1:2], bias(4), bias(5)
        )
        mild = jnp.sqrt(jnp.max(lengths[:, 0, 0])) * jnp.sqrt(jnp.max(lengths[:, 1, 0])) * EXP2 <= 60.0
        live = jnp.concatenate([live, mild.astype(jnp.int32).reshape(1)])
        ot, qb, p, rt = attend(live, k, qt, vt)

        def shift(parts):
            return [parts[0]] + [lax.ppermute(parts[j], "tile", [(s, (s + j) % tiles) for s in range(tiles)]) for j in range(1, tiles)]

        o_parts = shift(spread(src, live, tile_one, ot, tiles))
        output, grad_resid, *rest = middle(
            places, counts.reshape(1), tile_one, blocks, blocks_rest, o_parts, own_tokens, cotangent.reshape(slot_count, width), vec_params, vec_params[8:].reshape(1, -1)
        )
        go_parts, (u, gz, a2, gm, gb, o_t, sums, up_sums) = rest[:tiles], rest[tiles:]
        go_parts = shift(go_parts)
        back = lambda first, heads, dt: list(attend_back(first, heads, live, p, k, kt, v, qb, dt))
        if tuned:
            dp = lax.axis_index("dp")
            bit = {"x": tile // 2, "y": dp % 2, "z": dp // 2 % 2, "far": dp // 4}
            mask = {"x": 2, "y": 4, "z": 8, "far": 16}

            def flip(array, *names):
                change = sum(mask[name] for name in names)
                return lax.ppermute(array, ("dp", "tile"), [(s, s ^ change) for s in range(32)])

            def three(sums, pairs, common):
                out = []
                for p, (a, b) in enumerate(pairs):
                    ways = [(), (a,), (b,), (a, b)]
                    del ways[common[p]]
                    out += [flip(sums[3 * p + j], *way) if way else sums[3 * p + j] for j, way in enumerate(ways)]
                return out + [flip(sums[6], pairs[0][common[0] - 1])]

            def bits_of(pairs):
                return jnp.stack([bit[name] for pair in pairs for name in pair]).astype(jnp.int32)

            first, second = [("x", "y"), ("y", "z")], [("z", "far"), ("x", "far")]
            keep, send = weight_grads_to_slots(halving_places(inverse, tile % 2), 2, block_count, o_t, gb, a2, gz, u, gm)
            send, go_parts = lax.optimization_barrier((send, go_parts))
            came = lax.ppermute(send, "tile", [(s, s ^ 1) for s in range(4)])
            dt = collect(src, live, tile_one, go_parts, ot, rt)
            dt, came = lax.optimization_barrier((dt, came))
            sums_one = add_pair(bits_of(first), (2, 1), keep, came)
            dt, sums_one = lax.optimization_barrier((dt, sums_one))
            parts = three(sums_one, first, (2, 1))
            head_grads = back(0, 2, dt)
            head_grads[0], parts = lax.optimization_barrier((head_grads[0], parts))
            sums_two = add_four(bits_of(second), (2, 2), parts)
            dt, sums_two = lax.optimization_barrier((dt, sums_two))
            parts = three(sums_two, second, (2, 2))
            head_grads += back(2, 1, dt)
            head_grads[3], parts = lax.optimization_barrier((head_grads[3], parts))
            mine_early = add_last(parts)
            head_grads[3], mine_early = lax.optimization_barrier((head_grads[3], mine_early))
            over_early = flip(mine_early, "x")
        else:
            slots = weight_grads_to_slots(inverse, 1, block_count, o_t, gb, a2, gz, u, gm)[0]
            dt = collect(src, live, tile_one, go_parts, ot, rt)
            head_grads = back(0, 3, dt)
        g_one, g_two, gw_qkv, qkv_sums, norm_sums = qkv_backward(
            src, live, tile_one % 2, token_all.reshape(-1, width), vec_params[0:1], a1, w_qkv, head_grads, tiles, slot_count * 3 // 8
        )
        if tuned:
            g_one, over_early = lax.optimization_barrier((g_one, over_early))
        zero = jnp.zeros((width,), f32)
        at_own = lambda s: lax.dynamic_update_slice(zero, s, (tile * own,))
        vector_part = jnp.concatenate(
            [norm_sums[0:2], sums[0:2], at_own(qkv_sums[0, :own])[None], at_own(qkv_sums[0, 2 * own :])[None], sums[2:4], up_sums[0].reshape(-1, width)], axis=0
        )
        if tuned:
            early, late, vector_grads = last_sums(gw_qkv, mine_early, over_early, vector_part)
            g_two, early = lax.optimization_barrier((g_two, early))
        else:
            early = lax.psum(lax.psum_scatter(slots.astype(f32), "dp", scatter_dimension=0, tiled=True), "tile").astype(bf)
            late = lax.all_gather(lax.psum(gw_qkv.astype(f32), "dp").astype(bf), "tile", axis=0, tiled=True)
            vector_grads = lax.psum(vector_part, ("dp", "tile"))
        g1 = jnp.concatenate([lax.psum_scatter(part, "tile", scatter_dimension=0, tiled=False) for part in (g_one, g_two)], axis=0)
        row_input = own_tokens.astype(f32)
        _, normed_one, inv_std_one = norm_forward(row_input, vec_params[0], vec_params[1])
        input_grad = grad_resid + norm_back(g1.astype(f32), normed_one, inv_std_one, vec_params[0])
        late_at = jnp.where(mine < 48, mine % 4 * 12 + mine // 12 * 3 + mine % 12 // 4, -1)
        weight_grads, first_out, second_out, update, update_sq = adam(odd, late_at, early, late, first_moment, second_moment, left_basis, right_basis)
        group_hot = (groups[:, None] == jnp.arange(128, dtype=jnp.int32)[None, :]).astype(f32)
        weight_part = jnp.sum(jnp.sum(at_rank.astype(f32)[:, :, None] * group_hot[None], axis=1) * jnp.sum(weight_sq[:, 0], axis=1)[:, None], axis=0)
        group_part = jnp.pad(jnp.stack([weight_part, jnp.sum(group_hot * jnp.sum(update_sq[:, 0], axis=1)[:, None], axis=0)]), ((0, 6), (0, 0)))
        group_both = group_sum(group_part, block_count // per_owner)
        own_both = jnp.sum(group_hot[None] * group_both[:2, None, :], axis=2)
        rate = RATE_BLOCK * jnp.sqrt(own_both[0]) / (jnp.sqrt(own_both[1]) + 1e-06)
        master_out, master_copy = new_weights(rate, master, update)
        vec_first_out = BETA_ONE * vec_first + (1.0 - BETA_ONE) * vector_grads
        vec_second_out = BETA_TWO * vec_second + (1.0 - BETA_TWO) * vector_grads * vector_grads
        vec_update = (vec_first_out / (1.0 - BETA_ONE**STEP)) / (jnp.sqrt(vec_second_out / (1.0 - BETA_TWO**STEP)) + ADAM_EPS)
        return (
            output.reshape(1, slot_count, width),
            input_grad.reshape(1, slot_count, width),
            weight_grads,
            first_out,
            second_out,
            master_out,
            master_copy,
            vector_grads,
            vec_first_out,
            vec_second_out,
            vec_params - RATE_VECTOR * vec_update,
        )

    return body


def solution(mesh):
    tuned = (mesh.shape["dp"], mesh.shape["tile"]) == (8, 4)
    rows, blocks = P("dp", "tile", None), P("dp", None, None)
    return jax.shard_map(
        make_body(tuned),
        mesh=mesh,
        in_specs=(rows, rows, P("dp", "tile"), blocks, P(), P("dp"), blocks, blocks, blocks, blocks, P(), P(), P()),
        out_specs=(rows, rows, blocks, blocks, blocks, blocks, blocks, P(), P(), P(), P()),
        check_vma=False,
    )
```

```python
import functools
import math

import jax
import jax.numpy as jnp
from jax import lax
from jax.experimental import pallas as pl
from jax.experimental.pallas import tpu as pltpu
from jax.sharding import PartitionSpec as P

f32 = jnp.float32
bf = jnp.bfloat16
MESH = pl.DeviceIdType.MESH

def where_am_i():
    dp=lax.axis_index("dp"); t=lax.axis_index("tile")
    return dp//2, dp%2, t//2, t%2

def dev(z,y,x,c):
    return (z*2+y, x*2+c)

def rcopy(src,dst,ss,rs,to):
    return pltpu.make_async_remote_copy(src_ref=src,dst_ref=dst,send_sem=ss,recv_sem=rs,device_id=to,device_id_type=MESH)

def gather_kernel(own_w,own_tok,own_cnt,all_w,all_tok,all_cnt,zs,zr,ys,yr,cs,cr,ts,tr,ns,nr,ls):
    z,y,x,c=where_am_i()
    per=own_w.shape[0]
    half=per//2
    def piece(shard,cc): return all_w.at[pl.ds(shard*per+cc*half,half)]
    own=own_w.at[pl.ds(c*half,half)]
    me=z*2+y
    core=dev(z,y,x,1-c); across=dev(z,y,1-x,c); beside=dev(z,1-y,x,c)
    up=dev(jnp.minimum(z+1,3),y,x,c); down=dev(jnp.maximum(z-1,0),y,x,c)
    def src(shard,first): return own if first else piece(shard,c)
    def z_copy(zz,first,go_up):
        shard=zz*2+y
        d=(z-zz) if go_up else (zz-z)
        k=0 if go_up else 1
        return rcopy(src(shard,first),piece(shard,c),zs.at[k,d],zr.at[k,d],up if go_up else down)
    def z_arrival(zz,k,dist):
        r=piece(zz*2+y,c)
        return rcopy(r,r,zs.at[k,dist-1],zr.at[k,dist-1],up)
    def y_copy(zz,first):
        shard=zz*2+y
        return rcopy(src(shard,first),piece(shard,c),ys.at[zz],yr.at[zz],beside)
    def y_arrival(zz):
        r=piece(zz*2+1-y,c)
        return rcopy(r,r,ys.at[zz],yr.at[zz],beside)
    def c_copy(shard): return rcopy(piece(shard,c),piece(shard,c),cs.at[shard],cr.at[shard],core)
    def c_arrival(shard): return rcopy(piece(shard,1-c),piece(shard,1-c),cs.at[shard],cr.at[shard],core)
    tile=x*2+c
    tok_x=rcopy(own_tok,all_tok.at[tile],ts.at[0],tr.at[0],across)
    tok_c=rcopy(own_tok,all_tok.at[tile],ts.at[1],tr.at[1],core)
    far=all_tok.at[(1-x)*2+c]
    tok_f=rcopy(far,far,ts.at[2],tr.at[2],core)
    near=all_tok.at[x*2+1-c]
    diag=all_tok.at[(1-x)*2+1-c]
    cnts=[rcopy(own_cnt,all_cnt.at[tile],ns.at[i],nr.at[i],to) for i,to in enumerate((across,core,dev(z,y,1-x,1-c)))]
    cnt_in=[rcopy(r,r,ns.at[i],nr.at[i],core) for i,r in enumerate((all_cnt.at[(1-x)*2+c],all_cnt.at[x*2+1-c],all_cnt.at[(1-x)*2+1-c]))]
    local=(pltpu.make_async_copy(own_w,all_w.at[pl.ds(me*per,per)],ls.at[0]),
           pltpu.make_async_copy(own_tok,all_tok.at[tile],ls.at[1]),pltpu.make_async_copy(own_cnt,all_cnt.at[tile],ls.at[2]))
    @pl.when(z<3)
    def _(): z_copy(z,True,True).start()
    @pl.when(z>0)
    def _(): z_copy(z,True,False).start()
    y_copy(z,True).start(); tok_x.start(); tok_c.start()
    for cp in cnts: cp.start()
    for cp in local: cp.start()
    def from_line(k,dist):
        zz=z-dist if k==0 else z+dist
        there=(zz>=0) if k==0 else (zz<=3)
        @pl.when(there)
        def _():
            z_arrival(zz,k,dist).wait_recv()
            @pl.when((z<3) if k==0 else (z>0))
            def _(): z_copy(zz,False,k==0).start()
            y_copy(zz,False).start(); c_copy(zz*2+y).start()
    def from_beside(zz):
        y_arrival(zz).wait_recv(); c_copy(zz*2+1-y).start()
    def guarded(f,dist):
        @pl.when(z-dist>=0)
        def _(): f(z-dist)
        @pl.when(z+dist<=3)
        def _(): f(z+dist)
    from_line(0,1); from_line(1,1)
    from_beside(z)
    from_line(0,2); from_line(1,2)
    guarded(from_beside,1)
    from_line(0,3); from_line(1,3)
    tok_x.wait_recv(); tok_f.start()
    guarded(from_beside,2)
    guarded(from_beside,3)
    def drain(s,_):
        @pl.when(s!=me)
        def _():
            c_arrival(s).wait_recv(); c_copy(s).wait_send()
        return 0
    lax.fori_loop(0,8,drain,0)
    def drain_y(zz,_):
        y_copy(zz,False).wait_send(); return 0
    lax.fori_loop(0,4,drain_y,0)
    for dist in range(4):
        @pl.when(jnp.logical_and(z<3,z-dist>=0))
        def _(): z_copy(z-dist,False,True).wait_send()
        @pl.when(jnp.logical_and(z>0,z+dist<=3))
        def _(): z_copy(z+dist,False,False).wait_send()
    rcopy(near,near,ts.at[1],tr.at[1],core).wait_recv()
    rcopy(diag,diag,ts.at[2],tr.at[2],core).wait_recv()
    tok_x.wait_send(); tok_c.wait_send(); tok_f.wait_send()
    for cp in cnts: cp.wait_send()
    for cp in cnt_in: cp.wait_recv()
    for cp in local: cp.wait()

def gather_all(own_w,own_tok,own_cnt):
    DS=pltpu.SemaphoreType.DMA
    hbm=pl.BlockSpec(memory_space=pl.ANY)
    return pl.pallas_call(gather_kernel,
        out_shape=[jax.ShapeDtypeStruct((8*own_w.shape[0],)+own_w.shape[1:],bf),jax.ShapeDtypeStruct((4,)+own_tok.shape,bf),jax.ShapeDtypeStruct((4,)+own_cnt.shape,own_cnt.dtype)],
        in_specs=[pl.BlockSpec(memory_space=pltpu.VMEM)]*3,out_specs=[hbm]*3,
        scratch_shapes=[DS((2,4)),DS((2,4)),DS((4,)),DS((4,)),DS((8,)),DS((8,)),DS((3,)),DS((3,)),DS((3,)),DS((3,)),DS((3,))],
        compiler_params=pltpu.CompilerParams(has_side_effects=True,vmem_limit_bytes=60<<20),name="gather_weights_tokens")(own_w,own_tok,own_cnt)

def group_sum_kernel(g_ref,o_ref,gd,gs,gr):
    dp=lax.axis_index("dp"); t=lax.axis_index("tile")
    nd=gd.shape[0]
    def copy(k):
        return rcopy(gd.at[dp],gd.at[dp],gs.at[k],gr.at[k],((dp+k)%nd,t))
    def arrive(k):
        q=(dp-k+nd)%nd
        return rcopy(gd.at[q],gd.at[q],gs.at[k],gr.at[k],(q,t))
    def loop(f):
        def s(k,_):
            f(k); return 0
        lax.fori_loop(1,nd,s,0)
    gd[dp]=g_ref[...]
    loop(lambda k: copy(k).start())
    loop(lambda k: arrive(k).wait_recv())
    acc=gd[0]
    for i in range(1,nd): acc=acc+gd[i]
    o_ref[...]=acc
    loop(lambda k: copy(k).wait_send())

def group_sum(g,nd):
    DS=pltpu.SemaphoreType.DMA
    vm=pl.BlockSpec(memory_space=pltpu.VMEM)
    return pl.pallas_call(group_sum_kernel,out_shape=jax.ShapeDtypeStruct(g.shape,f32),in_specs=[vm],out_specs=vm,
        scratch_shapes=[pltpu.VMEM((nd,)+g.shape,f32),DS((nd,)),DS((nd,))],
        compiler_params=pltpu.CompilerParams(has_side_effects=True,vmem_limit_bytes=60<<20),name="sum_groups")(g)

def last_sums_kernel(l_ref,mine,over,v_ref,early,late,vo_ref,yb,zb,own,vb,vd,y1s,y1r,z2s,z2r,z3s,z3r,y4s,y4r,xs,xr,cs,cr,fs,fr,es,er,ts,tr,ds,dr,us,ur):
    z,y,x,c=where_am_i()
    dp=lax.axis_index("dp"); t=lax.axis_index("tile")
    core=dev(z,y,x,1-c); across=dev(z,y,1-x,c); beside=dev(z,1-y,x,c)
    def loop(f,first,n):
        def s(k,_):
            f(k); return 0
        lax.fori_loop(first,n,s,0)
    at=lambda i: pl.ds(i*3,3)
    def y1(k):
        q=(z+k)%4
        return rcopy(l_ref.at[at((1-y)*4+q)],yb.at[q],y1s.at[q],y1r.at[q],beside)
    def z2(k):
        q=(z+k)%4
        return rcopy(own.at[q],zb.at[z],z2s.at[k],z2r.at[k],dev(q,y,x,c))
    def z2_arrive(k):
        q=(z-k+4)%4
        return rcopy(zb.at[q],zb.at[q],z2s.at[k],z2r.at[k],dev(q,y,x,c))
    for k in (2,1,3,0): y1(k).start()
    def t1(k): return rcopy(v_ref.at[(t+k)%4],vb.at[t],ts.at[k],tr.at[k],(dp,(t+k)%4))
    def t1_arrive(k):
        q=(t-k+4)%4
        return rcopy(vb.at[q],vb.at[q],ts.at[k],tr.at[k],(dp,q))
    def d_copy(k): return rcopy(vd.at[dp],vd.at[dp],ds.at[k],dr.at[k],((dp+k)%8,t))
    def d_arrive(k):
        q=(dp-k+8)%8
        return rcopy(vd.at[q],vd.at[q],ds.at[k],dr.at[k],(q,t))
    def t2(k): return rcopy(vo_ref.at[t],vo_ref.at[t],us.at[k],ur.at[k],(dp,(t+k)%4))
    def t2_arrive(k):
        q=(t-k+4)%4
        return rcopy(vo_ref.at[q],vo_ref.at[q],us.at[k],ur.at[k],(dp,q))
    loop(lambda k: t1(k).start(),1,4)
    vb[t]=v_ref[t]
    def place(xx,cc,p): return early.at[pl.ds(cc*12+p*6+xx*3,3)]
    for p in range(2):
        early[pl.ds(c*12+p*6+x*3,3)]=mine[pl.ds(p*3,3)]
        early[pl.ds(c*12+p*6+(1-x)*3,3)]=over[pl.ds(p*3,3)]
    def e_copy(i,p): return rcopy(place(i,c,p),place(i,c,p),es.at[i,p],er.at[i,p],core)
    def e_arrive(i,p): return rcopy(place(i,1-c,p),place(i,1-c,p),es.at[i,p],er.at[i,p],core)
    for p in range(2):
        e_copy(0,p).start(); e_copy(1,p).start()
    loop(lambda k: t1_arrive(k).wait_recv(),1,4)
    vd[dp]=vb[0]+vb[1]+vb[2]+vb[3]
    loop(lambda k: d_copy(k).start(),1,8)
    for k in (2,1,3,0):
        q=(z+k)%4
        y1(k).wait_recv()
        for i in range(3): own[q,i]=(l_ref[(y*4+q)*3+i].astype(f32)+yb[q,i].astype(f32)).astype(bf)
        if k: z2(k).start()
    zb[z]=own[z]
    loop(lambda k: z2_arrive(k).wait_recv(),1,4)
    for i in range(3):
        late[t,(y*4+z)*3+i]=(zb[0,i].astype(f32)+zb[1,i].astype(f32)+zb[2,i].astype(f32)+zb[3,i].astype(f32)).astype(bf)
    def piece(tt,yy,zz): return late.at[tt,at(yy*4+zz)]
    def z3(k): return rcopy(piece(t,y,z),piece(t,y,z),z3s.at[k],z3r.at[k],dev((z+k)%4,y,x,c))
    def z3_arrive(k):
        q=(z-k+4)%4
        return rcopy(piece(t,y,q),piece(t,y,q),z3s.at[k],z3r.at[k],dev(q,y,x,c))
    def y4(q): return rcopy(piece(t,y,q),piece(t,y,q),y4s.at[q],y4r.at[q],beside)
    def y4_arrive(q): return rcopy(piece(t,1-y,q),piece(t,1-y,q),y4s.at[q],y4r.at[q],beside)
    far=(1-x)*2+c
    def x_copy(yy,q): return rcopy(piece(t,yy,q),piece(t,yy,q),xs.at[yy*4+q],xr.at[yy*4+q],across)
    def x_arrive(yy,q): return rcopy(piece(far,yy,q),piece(far,yy,q),xs.at[yy*4+q],xr.at[yy*4+q],across)
    def c_copy(yy,q): return rcopy(piece(t,yy,q),piece(t,yy,q),cs.at[yy*4+q],cr.at[yy*4+q],core)
    def c_arrive(yy,q): return rcopy(piece(x*2+1-c,yy,q),piece(x*2+1-c,yy,q),cs.at[yy*4+q],cr.at[yy*4+q],core)
    def f_copy(yy,q): return rcopy(piece(far,yy,q),piece(far,yy,q),fs.at[yy*4+q],fr.at[yy*4+q],core)
    def f_arrive(yy,q):
        r=piece((1-x)*2+1-c,yy,q)
        return rcopy(r,r,fs.at[yy*4+q],fr.at[yy*4+q],core)
    for k in (1,3,2): z3(k).start()
    y4(z).start(); x_copy(y,z).start(); c_copy(y,z).start()
    def passed_on(k):
        q=(z-k+4)%4
        if k:
            z3_arrive(k).wait_recv()
            y4(q).start(); x_copy(y,q).start(); c_copy(y,q).start()
        y4_arrive(q).wait_recv()
        x_copy(1-y,q).start(); c_copy(1-y,q).start()
    for k in (0,1,3,2): passed_on(k)
    loop(lambda k: d_arrive(k).wait_recv(),1,8)
    acc=vd[0]
    for i in range(1,8): acc=acc+vd[i]
    vo_ref[t]=acc
    loop(lambda k: t2(k).start(),1,4)
    for k in (0,1,3,2):
        q=(z-k+4)%4
        for yy in (y,1-y):
            x_arrive(yy,q).wait_recv(); f_copy(yy,q).start()
    def drain(q):
        for yy in range(2):
            c_arrive(yy,q).wait_recv(); f_arrive(yy,q).wait_recv()
            x_copy(yy,q).wait_send(); c_copy(yy,q).wait_send(); f_copy(yy,q).wait_send()
        y4(q).wait_send()
        y1(q).wait_send()
    loop(drain,0,4)
    def sent(k):
        t2_arrive(k).wait_recv()
        z2(k).wait_send(); z3(k).wait_send(); t1(k).wait_send(); t2(k).wait_send()
    loop(sent,1,4)
    loop(lambda k: d_copy(k).wait_send(),1,8)
    for p in range(2):
        for i in range(2):
            e_arrive(i,p).wait_recv(); e_copy(i,p).wait_send()

def last_sums(own,mine,over,v):
    DS=pltpu.SemaphoreType.DMA
    vm=pl.BlockSpec(memory_space=pltpu.VMEM)
    V=pltpu.VMEM
    S=jax.ShapeDtypeStruct
    rows=(3,v.shape[1])
    early,late,total=pl.pallas_call(last_sums_kernel,out_shape=[S((24,288,128),bf),S((4,24,144,128),bf),S((4,)+rows,f32)],in_specs=[vm]*4,out_specs=[vm]*3,
        scratch_shapes=[V((4,3,144,128),bf)]*3+[V((4,)+rows,f32),V((8,)+rows,f32)]+[DS((4,))]*8+[DS((8,))]*6+[DS((2,2))]*2+[DS((4,))]*2+[DS((8,))]*2+[DS((4,))]*2,
        cost_estimate=pl.CostEstimate(flops=10**7,bytes_accessed=150*10**6,transcendentals=0),
        compiler_params=pltpu.CompilerParams(has_side_effects=True,vmem_limit_bytes=60<<20),name="last_gradient_sums")(own.reshape(24,144,128),mine,over,v.reshape((4,)+rows))
    return early,late.reshape(48,288,128),total.reshape(v.shape)


H = 12
STEP = 10
EPS_NORM = 1e-06
BETA_ONE = 0.5
BETA_TWO = 0.5
ADAM_EPS = 1e-08
RATE_BLOCK = 0.3
RATE_VECTOR = 0.2
NEG_RAW = -8.0e9
HEAD = 64
SCALE = 1.0 / math.sqrt(HEAD)
EXP2 = SCALE * math.log2(math.e)
NN = (((1,), (0,)), ((), ()))
NT = (((1,), (1,)), ((), ()))
TN = (((0,), (0,)), ((), ()))


def mm(a, b, dims=NN):
    return lax.dot_general(a, b, dims, preferred_element_type=f32)


def column_sum(v):
    return jnp.sum(v, axis=0, keepdims=True)


def vmem_spec():
    return pl.BlockSpec(memory_space=pltpu.VMEM)


def smem_spec():
    return pl.BlockSpec(memory_space=pltpu.SMEM)


def any_spec():
    return pl.BlockSpec(memory_space=pl.ANY)


def params(mib=60):
    return pltpu.CompilerParams(vmem_limit_bytes=mib << 20)


def pack(block, odd):
    half = block.shape[0] // 2
    if odd:
        return block[:, 64:], jnp.concatenate([block[half:, :64], block[:half, :64]], axis=1)
    return block[:, :128], jnp.concatenate([block[:half, 128:], block[half:, 128:]], axis=1)


def unpack(top, tail, odd):
    if odd:
        return jnp.concatenate([jnp.concatenate([tail[:, 64:], tail[:, :64]], axis=0), top], axis=1)
    return jnp.concatenate([top, jnp.concatenate([tail[:, :64], tail[:, 64:]], axis=0)], axis=1)


def unpack_either(top, tail, odd):
    return jnp.where(odd, unpack(top, tail, 1), unpack(top, tail, 0))


def lane_sums(v):
    s = column_sum(v)
    return jnp.broadcast_to(s[:, :128] + jnp.concatenate([s[:, 128:], jnp.zeros((1, 64), f32)], axis=1), (8, 128))


def by_parity(value, run):
    for odd in (0, 1):
        pl.when(value == odd)(functools.partial(run, odd))


def turn(v):
    return jnp.concatenate([v[:, 64:], v[:, :64]], axis=1)


def group_of(n):
    return 4 if n % 4 == 0 else 3 if n % 3 == 0 else 1


def pack_kernel(early, order_ref, odd_ref, *refs):
    g = len(refs) - 3
    p_ref, late_ref, s_ref = refs[g:]
    i = pl.program_id(0)
    for b in range(g):
        m = refs[b][0]

        def place(odd, m=m, b=b):
            top, tail = pack(m, odd)
            for ref, here in ((p_ref, i < early), (late_ref, i >= early)):

                @pl.when(here)
                def _():
                    ref[b, :192] = top.astype(bf)
                    ref[b, 192:] = tail.astype(bf)

        by_parity(odd_ref[i * g + b], place)
        s_ref[b] = lane_sums(m * m)


def pack_master(order, odd, master, first):
    n = master.shape[0]
    g = group_of(first)
    early = first // g
    rest = max(n - first, g)
    spec = pltpu.PrefetchScalarGridSpec(
        num_scalar_prefetch=2,
        grid=(n // g,),
        in_specs=[pl.BlockSpec((1, 192, 192), lambda i, s, o, b=b: (s[i * g + b], 0, 0)) for b in range(g)],
        out_specs=[
            pl.BlockSpec((g, 288, 128), lambda i, s, o: (jnp.minimum(i, early - 1), 0, 0)),
            pl.BlockSpec((g, 288, 128), lambda i, s, o: (jnp.maximum(i - early, 0), 0, 0)),
            pl.BlockSpec((g, 8, 128), lambda i, s, o: (i, 0, 0)),
        ],
    )
    return pl.pallas_call(
        functools.partial(pack_kernel, early),
        grid_spec=spec,
        out_shape=[jax.ShapeDtypeStruct((first, 288, 128), bf), jax.ShapeDtypeStruct((rest, 288, 128), bf), jax.ShapeDtypeStruct((n, 8, 128), f32)],
        compiler_params=params(),
        name="pack_master",
    )(order, odd, *[master] * g)


def pick_kernel(at_ref, first_ref, rest_ref, o_ref, sems):
    split = first_ref.shape[0]
    for j in range(12):

        @pl.when(at_ref[j] < split)
        def _():
            pltpu.make_async_copy(first_ref.at[at_ref[j]], o_ref.at[j], sems.at[j]).start()

        @pl.when(at_ref[j] >= split)
        def _():
            pltpu.make_async_copy(rest_ref.at[at_ref[j] - split], o_ref.at[j], sems.at[j]).start()

    for j in range(12):
        pltpu.make_async_copy(first_ref.at[0], o_ref.at[j], sems.at[j]).wait()


def pick(at, first, rest):
    return pl.pallas_call(
        pick_kernel,
        in_specs=[smem_spec(), any_spec(), any_spec()],
        out_specs=vmem_spec(),
        out_shape=jax.ShapeDtypeStruct((12, 288, 128), bf),
        scratch_shapes=[pltpu.SemaphoreType.DMA((12,))],
        compiler_params=params(),
        name="pick_qkv_blocks",
    )(at, first, rest)


def qkv_kernel(src_ref, cnt_ref, at_ref, x0, x1, x2, x3, blk_ref, gain_ref, shift_ref, bq_ref, bv_ref, a_ref, qt_ref, k_ref, kt_ref, v_ref, vt_ref, w_ref, st_ref):
    i = pl.program_id(0)

    @pl.when(i == 0)
    def _():
        def join(odd):
            for r in range(4):
                parts = []
                for c in range(3):
                    p = blk_ref[r * 3 + c].astype(f32)
                    parts.append(unpack(p[:192], p[192:], odd))
                w_ref[r * 192 : (r + 1) * 192, :] = jnp.concatenate(parts, axis=1).astype(bf)

        by_parity(at_ref[0], join)

    x = jnp.concatenate([r[...] for r in (x0, x1, x2, x3)], axis=0).astype(f32)
    mean = jnp.mean(x, axis=-1, keepdims=True)
    cen = x - mean
    inv_std = lax.rsqrt(jnp.mean(cen * cen, axis=-1, keepdims=True) + EPS_NORM)
    a = (cen * inv_std * gain_ref[...] + shift_ref[...]).astype(bf)
    a_ref[...] = a
    qkv = mm(a, w_ref[...])
    q = (qkv[:, :192] + bq_ref[...]).astype(bf).astype(f32)
    k = qkv[:, 192:384].astype(bf).astype(f32)
    v = (qkv[:, 384:] + bv_ref[...]).astype(bf).astype(f32)
    row = lax.broadcasted_iota(jnp.int32, (128, 64), 0)
    lane = lax.broadcasted_iota(jnp.int32, (512, 64), 1)
    masked = jnp.concatenate(
        [jnp.where(row < cnt_ref[4 * i + b], 0.0, NEG_RAW) for b in range(4)], axis=0
    )
    ones = jnp.where(lane < 4, 1.0, 0.0)
    k_tail = jnp.where(lane == 0, masked, ones)
    v_tail = jnp.where(lane < 3, 1.0, 0.0)
    sub = lax.broadcasted_iota(jnp.int32, (64, 512), 0)
    t_tail = jnp.where(sub < 1, 1.0, 0.0)
    qt, kt, vt = q.T, k.T, v.T
    longest = lambda a: jnp.max(jnp.concatenate([column_sum(a[h * 64 : (h + 1) * 64] ** 2) for h in range(3)], axis=0))
    st_ref[0] = jnp.where(lax.broadcasted_iota(jnp.int32, (8, 128), 0) == 0, longest(qt), longest(kt))
    for h in range(3):
        s = slice(h * 64, (h + 1) * 64)
        k_ref[h] = jnp.concatenate([k[:, s], k_tail], axis=1).astype(bf)
        v_ref[h] = jnp.concatenate([v[:, s], v_tail], axis=1).astype(bf)
        qt_ref[h] = jnp.concatenate([qt[s], t_tail], axis=0).astype(bf)
        kt_ref[h] = kt[s].astype(bf)
        vt_ref[h] = jnp.concatenate([vt[s], t_tail[:16]], axis=0).astype(bf)


def qkv_forward(src, cnt, odd, tokens, blocks, gain, shift, bq, bv):
    n = tokens.shape[0]
    rows = [pl.BlockSpec((128, 768), lambda i, s, c, o, k=k: (s[4 * i + k], 0)) for k in range(4)]
    row = lambda i, s, c, o: (0, 0)
    spec = pltpu.PrefetchScalarGridSpec(
        num_scalar_prefetch=3,
        grid=(n // 512,),
        in_specs=rows
        + [pl.BlockSpec((12, 288, 128), lambda i, s, c, o: (0, 0, 0)), pl.BlockSpec((1, 768), row), pl.BlockSpec((1, 768), row), pl.BlockSpec((1, 192), row), pl.BlockSpec((1, 192), row)],
        out_specs=[
            pl.BlockSpec((512, 768), lambda i, s, c, o: (i, 0)),
            pl.BlockSpec((3, 128, 512), lambda i, s, c, o: (0, 0, i)),
            pl.BlockSpec((3, 512, 128), lambda i, s, c, o: (0, i, 0)),
            pl.BlockSpec((3, 64, 512), lambda i, s, c, o: (0, 0, i)),
            pl.BlockSpec((3, 512, 128), lambda i, s, c, o: (0, i, 0)),
            pl.BlockSpec((3, 80, 512), lambda i, s, c, o: (0, 0, i)),
            pl.BlockSpec((768, 576), row),
            pl.BlockSpec((1, 8, 128), lambda i, s, c, o: (i, 0, 0)),
        ],
    )
    shapes = [(n, 768), (3, 128, n), (3, n, 128), (3, 64, n), (3, n, 128), (3, 80, n), (768, 576)]
    return pl.pallas_call(
        qkv_kernel,
        grid_spec=spec,
        out_shape=[jax.ShapeDtypeStruct(s, bf) for s in shapes] + [jax.ShapeDtypeStruct((n // 512, 8, 128), f32)],
        compiler_params=params(),
        name="norm_and_qkv",
    )(src, cnt, odd, tokens, tokens, tokens, tokens, blocks, gain, shift, bq, bv)


def split3(v):
    a = v.astype(bf).astype(f32)
    b = (v - a).astype(bf).astype(f32)
    return a, b, v - a - b


def in_steps(units, sizes, body, carry):
    at = 0
    for size in sizes:
        count = (units - at) // size
        carry = lax.fori_loop(0, count, lambda i, c, at=at, size=size: body(at + i * size, size, c), carry)
        at = at + count * size
    return carry


def attend_kernel(bq, n_ref, k_ref, qt_ref, vt_ref, ot_ref, qb_ref, p_ref, rt_ref):
    live = n_ref[0]
    qi = pl.program_id(1)
    pairs = (live + 7) // 8 * 4

    def finish(top, acc):
        total = acc[64:65]
        ot_ref[0] = acc[:64] / total
        rt_ref[0] = 1.0 / total
        a, b, c = split3((top + jnp.log2(total)) * (-1.0 / EXP2))
        row = lax.broadcasted_iota(jnp.int32, (64, bq), 0)
        tail = jnp.where(row == 0, 1.0, jnp.where(row == 1, a, jnp.where(row == 2, b, jnp.where(row == 3, c, 0.0))))
        qb_ref[0, :64] = qt_ref[0, :64]
        qb_ref[0, 64:] = tail.astype(bf)

    def keys(u, size):
        return pl.ds(pl.multiple_of(u * 256, 256), size * 256)

    @pl.when(jnp.logical_and(qi * bq < live * 128, n_ref[1] == 1))
    def _():
        qt = qt_ref[0]

        def body(u, size, acc):
            step = min(size, 2)
            for part in range(0, size, step):
                at = keys(u + part, step)
                p = jnp.exp2(mm(k_ref[0, at, :], qt) * EXP2).astype(bf)
                p_ref[0, at, :] = p
                acc = acc + mm(vt_ref[0, :, at], p)
            return acc

        finish(0.0, in_steps(pairs, (16, 8, 4), body, jnp.zeros((80, bq), f32)))

    @pl.when(jnp.logical_and(qi * bq < live * 128, n_ref[1] == 0))
    def _():
        qt = qt_ref[0]

        def body(u, size, carry):
            top, acc = carry
            s = mm(k_ref[0, keys(u, size), :], qt) * EXP2
            new = jnp.maximum(top, jnp.max(s, axis=0, keepdims=True))
            p = jnp.exp2(s - new).astype(bf)
            return new, acc * jnp.exp2(top - new) + mm(vt_ref[0, :, keys(u, size)], p)

        finish(*in_steps(pairs, (4,), body, (jnp.full((1, bq), -3e38, f32), jnp.zeros((80, bq), f32))))


def attend(live, k, qt, vt, bq=1024):
    n = k.shape[1]
    spec = pltpu.PrefetchScalarGridSpec(
        num_scalar_prefetch=1,
        grid=(3, n // bq),
        in_specs=[
            pl.BlockSpec((1, n, 128), lambda h, i, s: (h, 0, 0)),
            pl.BlockSpec((1, 128, bq), lambda h, i, s: (h, 0, i)),
            pl.BlockSpec((1, 80, n), lambda h, i, s: (h, 0, 0)),
        ],
        out_specs=[
            pl.BlockSpec((1, 64, bq), lambda h, i, s: (h, 0, i)),
            pl.BlockSpec((1, 128, bq), lambda h, i, s: (h, 0, i)),
            pl.BlockSpec((1, n, bq), lambda h, i, s: (h, 0, i)),
            pl.BlockSpec((1, 1, bq), lambda h, i, s: (h, 0, i)),
        ],
    )
    return pl.pallas_call(
        functools.partial(attend_kernel, bq),
        grid_spec=spec,
        out_shape=[
            jax.ShapeDtypeStruct((3, 64, n), f32),
            jax.ShapeDtypeStruct((3, 128, n), bf),
            jax.ShapeDtypeStruct((3, n, n), bf),
            jax.ShapeDtypeStruct((3, 1, n), f32),
        ],
        compiler_params=params(),
        name="attention_forward",
    )(live, k, qt, vt)


def spread_kernel(src_ref, n_ref, t_ref, ot_ref, *o_refs):
    live, t, tiles = n_ref[0], t_ref[0], len(o_refs)
    per = o_refs[0].shape[1] // 128

    def step(b, _):
        g = src_ref[b]
        lanes = pl.ds(pl.multiple_of(b * 128, 128), 128)
        to = pl.ds(pl.multiple_of((g % per) * 128, 128), 128)
        for k in range(tiles):
            here = (g // per - t + tiles) % tiles == k

            @pl.when(jnp.logical_and(here, b < live))
            def _():
                for h in range(3):
                    o_refs[k][h * 64 : (h + 1) * 64, to] = ot_ref[h, :, lanes].astype(bf)

            @pl.when(jnp.logical_and(here, b >= live))
            def _():
                o_refs[k][:, to] = jnp.zeros((192, 128), bf)

        return 0

    lax.fori_loop(0, ot_ref.shape[2] // 128, step, 0)


def spread(src, live, tile, ot, tiles):
    n = ot.shape[2]
    return pl.pallas_call(
        spread_kernel,
        in_specs=[smem_spec()] * 3 + [vmem_spec()],
        out_specs=[vmem_spec()] * tiles,
        out_shape=[jax.ShapeDtypeStruct((192, n // tiles), bf)] * tiles,
        compiler_params=params(),
        name="spread_attended",
    )(src, live, tile, ot)


def collect_kernel(src_ref, n_ref, t_ref, ot_ref, rt_ref, *refs):
    g_refs, dt_ref = refs[:-1], refs[-1]
    live, t, tiles = n_ref[0], t_ref[0], len(g_refs)
    mild = n_ref[1] == 1
    per = g_refs[0].shape[1] // 128
    row = lax.broadcasted_iota(jnp.int32, (64, 128), 0)

    def step(b, _):
        g = src_ref[b]
        to = pl.ds(pl.multiple_of(b * 128, 128), 128)
        lanes = pl.ds(pl.multiple_of((g % per) * 128, 128), 128)
        for k in range(tiles):

            @pl.when(jnp.logical_and((t - g // per + tiles) % tiles == k, b < live))
            def _():
                for h in range(3):
                    scale = jnp.where(mild, rt_ref[h, :, to], 1.0)
                    d = (g_refs[k][h * 64 : (h + 1) * 64, lanes].astype(f32) * scale).astype(bf).astype(f32)
                    x, y, z = split3(-jnp.sum(d * ot_ref[h, :, to], axis=0, keepdims=True))
                    tail = jnp.where(row == 0, x, jnp.where(row == 1, y, jnp.where(row == 2, z, 0.0)))
                    dt_ref[h, :, to] = jnp.concatenate([d, tail], axis=0).astype(bf)

        @pl.when(b >= live)
        def _():
            dt_ref[:, :, to] = jnp.zeros((3, 128, 128), bf)

        return 0

    lax.fori_loop(0, ot_ref.shape[2] // 128, step, 0)


def collect(src, live, tile, grads, ot, rt):
    n = ot.shape[2]
    return pl.pallas_call(
        collect_kernel,
        in_specs=[smem_spec()] * 3 + [vmem_spec()] * (2 + len(grads)),
        out_specs=vmem_spec(),
        out_shape=jax.ShapeDtypeStruct((3, 128, n), bf),
        compiler_params=params(),
        name="collect_attended_grad",
    )(src, live, tile, ot, rt, *grads)


def attend_back_kernel(bk, n_ref, p_ref, k_ref, kt_ref, v_ref, qb_ref, dt_ref, dq_ref, dk_ref, dv_ref):
    live = n_ref[0]
    j = pl.program_id(1)

    @pl.when(j == 0)
    def _():
        dq_ref[...] = jnp.zeros_like(dq_ref)

    def lanes(u):
        return pl.ds(pl.multiple_of(u * 256, 256), 256)

    pairs = (live + 1) // 2

    def over_queries(rows, sizes, body):
        zero = jnp.zeros((rows, 64), f32)
        dk, dv = in_steps((live + 7) // 8 * 4, sizes, body, (zero, zero))
        dk_ref[0, :rows] = (dk * SCALE).astype(bf)
        dv_ref[0, :rows] = dv.astype(bf)

    def with_kept(rows):
        k, v, kt = k_ref[0, :rows], v_ref[0, :rows], kt_ref[0, :, :rows]

        def body(u, size, carry):
            dk, dv = carry
            dp = mm(v, dt_ref[0, :, lanes(u)])
            for part in range(size):
                at = lanes(u + part)
                ahead = mm(v, dt_ref[0, :, lanes(u + part + 1)]) if part + 1 < size else None
                p = p_ref[0, :rows, at]
                ds = (p.astype(f32) * dp).astype(bf)
                dv = dv + mm(p, dt_ref[0, :64, at], NT)
                dk = dk + mm(ds, qb_ref[0, :64, at], NT)
                dq_ref[0, :, at] += mm(kt, ds)
                dp = dp if ahead is None else ahead
            return dk, dv

        over_queries(rows, (16, 8, 4), body)

    @pl.when(jnp.logical_and(n_ref[1] == 1, 2 * j + 2 <= pairs))
    def _():
        with_kept(bk)

    @pl.when(jnp.logical_and(n_ref[1] == 1, 2 * j + 1 == pairs))
    def _():
        dk_ref[0, bk // 2 :] = jnp.zeros((bk // 2, 64), bf)
        dv_ref[0, bk // 2 :] = jnp.zeros((bk // 2, 64), bf)
        with_kept(bk // 2)

    @pl.when(jnp.logical_and(n_ref[1] == 0, j * bk < live * 128))
    def _():
        k, v, kt = k_ref[0], v_ref[0], kt_ref[0]

        def body(u, size, carry):
            dk, dv = carry
            for part in range(size):
                at = lanes(u + part)
                p = jnp.exp2(mm(k, qb_ref[0, :, at]) * EXP2)
                ds = (p * mm(v, dt_ref[0, :, at])).astype(bf)
                dv = dv + mm(p.astype(bf), dt_ref[0, :64, at], NT)
                dk = dk + mm(ds, qb_ref[0, :64, at], NT)
                dq_ref[0, :, at] += mm(kt, ds)
            return dk, dv

        over_queries(bk, (4,), body)


def attend_back(first, heads, live, p, k, kt, v, qb, dt, bk=512):
    n = k.shape[1]
    whole_t = lambda h, j, s: (first + h, 0, 0)
    rows = lambda h, j, s: (first + h, j, 0)
    spec = pltpu.PrefetchScalarGridSpec(
        num_scalar_prefetch=1,
        grid=(heads, n // bk),
        in_specs=[
            pl.BlockSpec((1, bk, n), rows),
            pl.BlockSpec((1, bk, 128), rows),
            pl.BlockSpec((1, 64, bk), lambda h, j, s: (first + h, 0, j)),
            pl.BlockSpec((1, bk, 128), rows),
            pl.BlockSpec((1, 128, n), whole_t),
            pl.BlockSpec((1, 128, n), whole_t),
        ],
        out_specs=[
            pl.BlockSpec((1, 64, n), lambda h, j, s: (h, 0, 0)),
            pl.BlockSpec((1, bk, 64), lambda h, j, s: (h, j, 0)),
            pl.BlockSpec((1, bk, 64), lambda h, j, s: (h, j, 0)),
        ],
    )
    S = jax.ShapeDtypeStruct
    return pl.pallas_call(
        functools.partial(attend_back_kernel, bk),
        grid_spec=spec,
        out_shape=[S((heads, 64, n), f32), S((heads, n, 64), bf), S((heads, n, 64), bf)],
        cost_estimate=pl.CostEstimate(flops=heads * 4 * 10**10, bytes_accessed=heads * 50 * 10**6, transcendentals=0),
        compiler_params=params(),
        name="attention_backward",
    )(live, p, k, kt, v, qb, dt)


def qkv_back_kernel(given, src_ref, n_ref, odd_ref, x0, x1, x2, x3, gain_ref, a_ref, w_ref, *refs):
    grads, (ga_ref, gz_ref, gw_ref, gb_ref, vs_ref, acc, sums, rows, sems) = refs[:given], refs[given:]
    dqs, dks, dvs = [[(r, h) for r in grads[j::3] for h in range(r.shape[0])] for j in range(3)]
    early = ga_ref.shape[1] // 128
    i = pl.program_id(0)
    live = n_ref[0]
    slot = i % 2

    def wait_for(slot):
        for b in range(4):
            pltpu.make_async_copy(rows.at[slot, pl.ds(b * 128, 128)], ga_ref.at[0, pl.ds(0, 128)], sems.at[slot, b]).wait()

    @pl.when(i >= 2)
    def _():
        wait_for(slot)

    @pl.when(i == 0)
    def _():
        acc[...] = jnp.zeros_like(acc)
        sums[...] = jnp.zeros_like(sums)
        vs_ref[...] = jnp.zeros_like(vs_ref)

    @pl.when(4 * i < live)
    def _():
        dq = jnp.concatenate([r[h] for r, h in dqs], axis=0).T * SCALE
        g = jnp.concatenate([dq] + [r[h].astype(f32) for r, h in dks + dvs], axis=1).astype(bf)
        acc[...] += mm(a_ref[...], g, TN)
        sums[...] += jnp.broadcast_to(column_sum(g.astype(f32)), sums.shape)
        g1 = mm(g, w_ref[...], NT)
        rows[slot] = g1.astype(bf)
        x = jnp.concatenate([r[...] for r in (x0, x1, x2, x3)], axis=0).astype(f32)
        cen = x - jnp.mean(x, axis=-1, keepdims=True)
        normed = cen * lax.rsqrt(jnp.mean(cen * cen, axis=-1, keepdims=True) + EPS_NORM)
        vs_ref[0:1, :] += column_sum(g1 * normed)
        vs_ref[1:2, :] += column_sum(g1)

    @pl.when(4 * i >= live)
    def _():
        rows[slot] = jnp.zeros(rows.shape[1:], bf)

    per = early + gz_ref.shape[1] // 128
    for b in range(4):
        block, at = rows.at[slot, pl.ds(b * 128, 128)], src_ref[4 * i + b]
        t, j = at // per, at % per

        @pl.when(j < early)
        def _():
            pltpu.make_async_copy(block, ga_ref.at[t, pl.ds(pl.multiple_of(j * 128, 128), 128)], sems.at[slot, b]).start()

        @pl.when(j >= early)
        def _():
            pltpu.make_async_copy(block, gz_ref.at[t, pl.ds(pl.multiple_of((j - early) * 128, 128), 128)], sems.at[slot, b]).start()

    @pl.when(i == pl.num_programs(0) - 1)
    def _():
        wait_for(1 - slot)
        wait_for(slot)

        def place(odd):
            for r in range(4):
                for c in range(3):
                    top, tail = pack(acc[r * 192 : (r + 1) * 192, c * 192 : (c + 1) * 192], odd)
                    gw_ref[r * 3 + c, :192] = top.astype(bf)
                    gw_ref[r * 3 + c, 192:] = tail.astype(bf)

        by_parity(odd_ref[0], place)
        gb_ref[...] = sums[...]


def qkv_backward(src, live, odd, tokens, gain, a, w, grads, tiles, early):
    n = a.shape[0]
    per = n // tiles
    fixed = lambda i, s, c, o: (0, 0)
    row = lambda i, s, c, o: (0, i, 0)
    spec = pltpu.PrefetchScalarGridSpec(
        num_scalar_prefetch=3,
        grid=(n // 512,),
        in_specs=[pl.BlockSpec((128, 768), lambda i, s, c, o, k=k: (s[4 * i + k], 0)) for k in range(4)]
        + [pl.BlockSpec((1, 768), fixed), pl.BlockSpec((512, 768), lambda i, s, c, o: (i, 0)), pl.BlockSpec((768, 576), fixed)]
        + [
            pl.BlockSpec((g.shape[0], 64, 512), lambda i, s, c, o: (0, 0, i)) if g.shape[1] == 64 else pl.BlockSpec((g.shape[0], 512, 64), row)
            for g in grads
        ],
        out_specs=[any_spec(), any_spec(), pl.BlockSpec((12, 288, 128), lambda i, s, c, o: (0, 0, 0)), pl.BlockSpec((8, 576), fixed), pl.BlockSpec((8, 768), fixed)],
        scratch_shapes=[pltpu.VMEM((768, 576), f32), pltpu.VMEM((8, 576), f32), pltpu.VMEM((2, 512, 768), bf), pltpu.SemaphoreType.DMA((2, 4))],
    )
    S = jax.ShapeDtypeStruct
    return pl.pallas_call(
        functools.partial(qkv_back_kernel, len(grads)),
        grid_spec=spec,
        out_shape=[S((tiles, early, 768), bf), S((tiles, per - early, 768), bf), S((12, 288, 128), bf), S((8, 576), f32), S((8, 768), f32)],
        cost_estimate=pl.CostEstimate(flops=3 * 10**10, bytes_accessed=40 * 10**6, transcendentals=0),
        compiler_params=params(),
        name="qkv_backward",
    )(src, live, odd, tokens, tokens, tokens, tokens, gain, a, w, *grads)


def gelu_parts(z):
    cdf = 0.5 + 0.5 * lax.erf(z * math.sqrt(0.5))
    return z * cdf, cdf + z * (jnp.exp2(z * z * (-0.5 * math.log2(math.e))) * (1.0 / math.sqrt(2.0 * math.pi)))


def middle_kernel(inv_ref, cnt_ref, t_ref, blk_ref, rest_ref, o0, o1, o2, o3, x_ref, c_ref, vp_ref, bu_ref, y_ref, gr_ref, g0, g1, g2_ref, g3,
                  u_s, gz_s, a2_s, gm_s, gb_s, o_s, vs_ref, us_ref, w_out, w_up, w_down, tails, tsem, isem):
    i = pl.program_id(0)
    rows = x_ref.shape[0]
    split = blk_ref.shape[0]
    r0 = i * rows
    kinds = ((w_out, 48, 2, 4), (w_up, 64, 8, 4), (w_down, 128, 2, 16))

    @pl.when(i == 0)
    def _():
        vs_ref[...] = jnp.zeros_like(vs_ref)
        us_ref[...] = jnp.zeros_like(us_ref)

        def pair(w, first, pairs):
            def parts(j, run):
                r = pl.multiple_of((j // pairs) * 192, 64)
                col = pl.multiple_of((j % pairs) * 384, 128)
                for b, off in ((0, 0), (1, 256)):
                    at = first + 2 * j + b
                    run(at, w.at[pl.ds(r, 192), pl.ds(col + off, 128)], tails.at[at - 48])
                return r, col

            def fetch(at, top, tail):
                for ref, here, slot in ((blk_ref, inv_ref[at] < split, inv_ref[at]), (rest_ref, inv_ref[at] >= split, inv_ref[at] - split)):

                    @pl.when(here)
                    def _():
                        pltpu.make_async_copy(ref.at[slot, pl.ds(0, 192)], top, tsem.at[at - 48]).start()
                        pltpu.make_async_copy(ref.at[slot, pl.ds(192, 96)], tail, isem.at[at - 48]).start()

            def fetched(at, top, tail):
                pltpu.make_async_copy(blk_ref.at[0, pl.ds(0, 192)], top, tsem.at[at - 48]).wait()
                pltpu.make_async_copy(blk_ref.at[0, pl.ds(192, 96)], tail, isem.at[at - 48]).wait()

            def start(j, _):
                parts(j, fetch)
                return 0

            def join(j, _):
                r, col = parts(j, fetched)
                even = tails[first + 2 * j - 48].astype(f32)
                odd = tails[first + 2 * j - 47].astype(f32)
                lane = lax.broadcasted_iota(jnp.int32, even.shape, 1) < 64
                w[pl.ds(r, 96), pl.ds(col + 128, 128)] = jnp.where(lane, even, odd).astype(bf)
                w[pl.ds(r + 96, 96), pl.ds(col + 128, 128)] = turn(jnp.where(lane, odd, even)).astype(bf)
                return 0

            return start, join

        todo = [(pair(w, first, pairs), pairs * high) for w, first, pairs, high in kinds]
        for (start, _), n in todo:
            lax.fori_loop(0, n, start, 0)

        for (_, join), n in todo:
            lax.fori_loop(0, n, join, 0)

    vp = vp_ref[...]
    row = r0 + lax.broadcasted_iota(jnp.int32, (rows, 1), 0)
    live = jnp.where(row < cnt_ref[0], 1.0, 0.0)
    t = t_ref[0]
    for k, ref in enumerate((o0, o1, o2, o3)):
        o_s[pl.ds(pl.multiple_of(((t - k + 4) % 4) * 192, 64), 192), :] = ref[...]
    o_t = o_s[...]
    res = x_ref[...].astype(f32) + mm(o_t, w_out[...], TN) + vp[6:7]
    cen = res - jnp.mean(res, axis=-1, keepdims=True)
    inv_std = lax.rsqrt(jnp.mean(cen * cen, axis=-1, keepdims=True) + EPS_NORM)
    normed = cen * inv_std
    a2 = (normed * vp[2:3] + vp[3:4]).astype(bf)
    gy = c_ref[...].astype(f32) * live
    gm = gy.astype(bf)
    a2_s[...] = a2
    gm_s[...] = gm
    branch = jnp.zeros((rows, 768), f32)
    g2 = jnp.zeros((rows, 768), f32)
    for j in range(4):
        cols = slice(j * 768, (j + 1) * 768)
        u, slope = gelu_parts(mm(a2, w_up[:, cols]) + bu_ref[:, cols])
        u = u.astype(bf)
        u_s[:, cols] = u
        branch = branch + mm(u, w_down[cols, :])
        gz = (mm(gm, w_down[cols, :], NT) * slope).astype(bf)
        gz_s[:, cols] = gz
        us_ref[:, cols] += jnp.broadcast_to(column_sum(gz.astype(f32)), (8, 768))
        g2 = g2 + mm(gz, w_up[:, cols], NT)
    y_ref[...] = (live * (res + branch + vp[7:8])).astype(bf)
    d2 = g2 * vp[2:3]
    gr = gy + inv_std * (d2 - jnp.mean(d2, axis=-1, keepdims=True) - normed * jnp.mean(d2 * normed, axis=-1, keepdims=True))
    gr_ref[...] = gr
    gb = gr.astype(bf)
    gb_s[...] = gb
    vs_ref[0:1, :] += column_sum(g2 * normed)
    vs_ref[1:2, :] += column_sum(g2)
    vs_ref[2:3, :] += column_sum(gb.astype(f32))
    vs_ref[3:4, :] += column_sum(gm.astype(f32))
    for k, ref in enumerate((g0, g1, g2_ref, g3)):
        ref[...] = mm(w_out[pl.ds(pl.multiple_of(((t + k) % 4) * 192, 64), 192), :], gb, NT).astype(bf)


def weight_grad_kernel(outs, pos_ref, o_in, gb_in, a2_in, gz_in, u_in, gm_in, *refs):
    s_refs, (o_s, gb_s, a2_s, gz_s, u_s, gm_s, ring, zero, lsem, osem, zsem) = refs[:outs], refs[outs:]
    each = s_refs[0].shape[0]

    def to_slot(block, at, sem):
        for o in range(outs):

            @pl.when(at // each == o)
            def _():
                pltpu.make_async_copy(block, s_refs[o].at[at % each], sem).start()

    def landed(block, sem):
        pltpu.make_async_copy(block, s_refs[0].at[0], sem).wait()

    loads = [pltpu.make_async_copy(a, b, lsem.at[j]) for j, (a, b) in enumerate(
        ((o_in, o_s), (gb_in, gb_s), (a2_in, a2_s), (gz_in, gz_s), (gm_in, gm_s), (u_in, u_s)))]
    for load in loads:
        load.start()
    zero[...] = jnp.zeros_like(zero)

    def clear(j, _):
        to_slot(zero, pos_ref[j], zsem.at[j])
        return 0

    lax.fori_loop(0, 48, clear, 0)
    def send(n, g, first, pairs, high, low):
        half = (n % 2) * 8

        def put(r, b):
            return first + (high + r) * 2 * pairs + 2 * low + b

        for r in range(4):
            part = g[r * 192 : (r + 1) * 192]
            mid = part[:, 128:256]
            upper, lower = mid[:96], turn(mid[96:])
            lane = lax.broadcasted_iota(jnp.int32, upper.shape, 1) < 64
            for b, top, tail in ((0, part[:, :128], jnp.where(lane, upper, lower)), (1, part[:, 256:], jnp.where(lane, lower, upper))):
                k = half + 2 * r + b

                @pl.when(n >= 2)
                def _():
                    landed(ring.at[k], osem.at[k])

                ring[k, :192] = top.astype(bf)
                ring[k, 192:] = tail.astype(bf)
                to_slot(ring.at[k], pos_ref[put(r, b)], osem.at[k])

    def lanes(j):
        return pl.ds(pl.multiple_of(j * 384, 128), 384)

    def grad_out(n, _):
        send(n, mm(o_s[...], gb_s[:, lanes(n)]), 48, 2, 0, n)
        return 0

    def grad_up(n, _):
        send(n, mm(a2_s[...], gz_s[:, lanes(n)], TN), 64, 8, 0, n)
        return 0

    def grad_down(n, _):
        high = n // 2
        send(n, mm(u_s[:, pl.ds(pl.multiple_of(high * 768, 128), 768)], gm_s[:, lanes(n % 2)], TN), 128, 2, high * 4, n % 2)
        return 0

    def drain():
        for k in range(16):
            landed(ring.at[k], osem.at[k])

    for f, n, first in ((grad_out, 2, 0), (grad_up, 8, 2), (grad_down, 8, 4)):
        loads[first].wait()
        loads[first + 1].wait()
        lax.fori_loop(0, n, f, 0)
        drain()

    def cleared(j, _):
        landed(zero, zsem.at[j])
        return 0

    lax.fori_loop(0, 48, cleared, 0)


def middle(inv, count, tile, blocks, rest, o_parts, tokens, cotangent, vec_params, bias_up, rows=256):
    n, width = tokens.shape
    hidden = bias_up.shape[1]
    row = lambda i, s, c, t: (i, 0)
    fixed = lambda i, s, c, t: (0, 0)
    col = lambda i, s, c, t: (0, i)
    V, DS = pltpu.VMEM, pltpu.SemaphoreType.DMA
    narrow, wide, part = pl.BlockSpec((rows, width), row), pl.BlockSpec((rows, hidden), row), pl.BlockSpec((192, rows), col)
    spec = pltpu.PrefetchScalarGridSpec(
        num_scalar_prefetch=3,
        grid=(n // rows,),
        in_specs=[any_spec()] * 2 + [part] * 4 + [narrow, narrow, pl.BlockSpec((12, width), fixed), pl.BlockSpec((1, hidden), fixed)],
        out_specs=[narrow, narrow] + [part] * 4 + [wide, wide, narrow, narrow, narrow, pl.BlockSpec((width, rows), col),
                   pl.BlockSpec((8, width), fixed), pl.BlockSpec((8, hidden), fixed)],
        scratch_shapes=[V((768, 768), bf), V((768, 3072), bf), V((3072, 768), bf), V((144, 96, 128), bf), DS((144,)), DS((144,))],
    )
    S = jax.ShapeDtypeStruct
    return pl.pallas_call(
        middle_kernel,
        grid_spec=spec,
        out_shape=[S((n, width), bf), S((n, width), f32)] + [S((192, n), bf)] * 4 + [S((n, hidden), bf)] * 2 + [S((n, width), bf)] * 3
        + [S((width, n), bf), S((8, width), f32), S((8, hidden), f32)],
        compiler_params=params(),
        name="projection_and_mlp",
    )(inv, count, tile, blocks, rest, *o_parts, tokens, cotangent, vec_params, bias_up)


def weight_grads_to_slots(pos, outs, block_count, o_t, gb, a2, gz, u, gm):
    V, DS = pltpu.VMEM, pltpu.SemaphoreType.DMA
    arrays = (o_t, gb, a2, gz, u, gm)
    return pl.pallas_call(
        functools.partial(weight_grad_kernel, outs),
        in_specs=[smem_spec()] + [any_spec()] * 6,
        out_specs=[any_spec()] * outs,
        out_shape=[jax.ShapeDtypeStruct((block_count // outs, 288, 128), bf)] * outs,
        scratch_shapes=[V(a.shape, bf) for a in arrays] + [V((16, 288, 128), bf), V((288, 128), bf), DS((6,)), DS((16,)), DS((48,))],
        cost_estimate=pl.CostEstimate(flops=6 * 10**10, bytes_accessed=32 * 10**6, transcendentals=0),
        compiler_params=params(),
        name="mlp_weight_gradients",
    )(pos, *arrays)


def quarters(b0, b1):
    return (b0 * 2 + b1, (1 - b0) * 2 + b1, b0 * 2 + 1 - b1, (1 - b0) * 2 + 1 - b1)


def add_pair_kernel(common, bits_ref, *refs):
    outs = list(refs[16:])
    for p in range(2):
        for side in range(4):
            j = 4 * p + side
            total = (refs[2 * j][...].astype(f32) + refs[2 * j + 1][...].astype(f32)).astype(bf)
            if side == common[p]:
                outs[6][p] = total
            else:
                outs[3 * p + side - (side > common[p])][...] = total


def add_pair(bits, common, keep, came):
    specs = []
    for p in range(2):
        for side in range(4):
            at = lambda i, b, p=p, side=side: (p * 12 + quarters(b[2 * p], b[2 * p + 1])[side] * 3 + i, 0, 0)
            specs += [pl.BlockSpec((4, 288, 128), at)] * 2
    S = jax.ShapeDtypeStruct
    return pl.pallas_call(
        functools.partial(add_pair_kernel, common),
        grid_spec=pltpu.PrefetchScalarGridSpec(
            num_scalar_prefetch=1,
            grid=(3,),
            in_specs=specs,
            out_specs=[pl.BlockSpec((4, 288, 128), lambda i, b: (i, 0, 0))] * 6 + [pl.BlockSpec((2, 4, 288, 128), lambda i, b: (0, i, 0, 0))],
        ),
        out_shape=[S((12, 288, 128), bf)] * 6 + [S((2, 12, 288, 128), bf)],
        compiler_params=params(),
        name="add_gradients_of_cores",
    )(bits, *[keep, came] * 8)


def add_four_kernel(common, bits_ref, *refs):
    outs = refs[7:]
    for p in range(2):
        parts = refs[3 * p : 3 * p + 3]
        for side, q in enumerate(quarters(bits_ref[2 * p], bits_ref[2 * p + 1])):
            for b in range(3):
                total = (sum(r[q * 3 + b].astype(f32) for r in parts) + refs[6][p, q * 3 + b].astype(f32)).astype(bf)
                if side == common[p]:
                    outs[6][p, b] = total
                else:
                    outs[3 * p + side - (side > common[p])][b] = total


def add_four(bits, common, parts):
    S = jax.ShapeDtypeStruct
    return pl.pallas_call(
        functools.partial(add_four_kernel, common),
        in_specs=[smem_spec()] + [vmem_spec()] * 7,
        out_specs=[vmem_spec()] * 7,
        out_shape=[S((3, 288, 128), bf)] * 6 + [S((2, 3, 288, 128), bf)],
        compiler_params=params(),
        name="add_gradients",
    )(bits, *parts)


def add_last_kernel(*refs):
    for p in range(2):
        for b in range(3):
            refs[7][3 * p + b] = (sum(r[b].astype(f32) for r in refs[3 * p : 3 * p + 3]) + refs[6][p, b].astype(f32)).astype(bf)


def add_last(parts):
    return pl.pallas_call(
        add_last_kernel,
        in_specs=[vmem_spec()] * 7,
        out_specs=vmem_spec(),
        out_shape=jax.ShapeDtypeStruct((6, 288, 128), bf),
        compiler_params=params(),
        name="add_last_gradients",
    )(*parts)


def split2(v):
    hi = v.astype(bf)
    return hi, (v - hi.astype(f32)).astype(bf)


def mm3(a, b, dims):
    return mm(a[0], b[0], dims) + (mm(a[0], b[1], dims) + mm(a[1], b[0], dims))


def adam_kernel(odd_ref, from_ref, g_ref, late_ref, m1_ref, m2_ref, l_ref, r_ref, g_out, m1_out, m2_out, u_out, s_out):
    for b in range(g_ref.shape[0]):
        slot = pl.program_id(0) * g_ref.shape[0] + b
        place = from_ref[slot]
        part = jnp.where(place >= 0, late_ref[jnp.maximum(place, 0)].astype(f32), g_ref[b].astype(f32))
        grad = unpack_either(part[:192], part[192:], odd_ref[slot] == 1)
        left, right = split2(l_ref[b]), split2(r_ref[b])
        low = grad.astype(bf)
        rot = mm3(split2(mm(left[0], low, TN) + mm(left[1], low, TN)), right, NN)
        g_out[b] = grad
        first = BETA_ONE * m1_ref[b] + (1.0 - BETA_ONE) * rot
        second = BETA_TWO * m2_ref[b] + (1.0 - BETA_TWO) * rot * rot
        upd = (first * (1.0 / (1.0 - BETA_ONE**STEP))) / (jnp.sqrt(second * (1.0 / (1.0 - BETA_TWO**STEP))) + ADAM_EPS)
        upd = mm3(split2(mm3(left, split2(upd), NN)), right, NT)
        m1_out[b] = first
        m2_out[b] = second
        u_out[b] = upd.astype(bf)
        s_out[b] = lane_sums(upd * upd)


def adam(odd, late_at, grads, late, first, second, left, right):
    n = grads.shape[0]
    g = group_of(n)
    at = lambda i, s, f: (i, 0, 0)
    big = pl.BlockSpec((g, 192, 192), at)
    spec = pltpu.PrefetchScalarGridSpec(
        num_scalar_prefetch=2,
        grid=(n // g,),
        in_specs=[pl.BlockSpec((g, 288, 128), at), pl.BlockSpec(late.shape, lambda i, s, f: (0, 0, 0))] + [big] * 4,
        out_specs=[big] * 4 + [pl.BlockSpec((g, 8, 128), at)],
    )
    return pl.pallas_call(
        adam_kernel,
        grid_spec=spec,
        out_shape=[jax.ShapeDtypeStruct((n, 192, 192), f32)] * 3 + [jax.ShapeDtypeStruct((n, 192, 192), bf), jax.ShapeDtypeStruct((n, 8, 128), f32)],
        compiler_params=params(),
        name="rotated_adam",
    )(odd, late_at, grads, late, first, second, left, right)


def update_kernel(rate_ref, m_ref, u_ref, mo_ref, mc_ref):
    g = m_ref.shape[0]
    for b in range(g):
        new = m_ref[b] - rate_ref[pl.program_id(0) * g + b] * u_ref[b].astype(f32)
        mo_ref[b] = new
        mc_ref[b] = new.astype(bf)


def new_weights(rate, master, update):
    n = master.shape[0]
    g = 8 if n % 8 == 0 else group_of(n)
    big = pl.BlockSpec((g, 192, 192), lambda i, r: (i, 0, 0))
    return pl.pallas_call(
        update_kernel,
        grid_spec=pltpu.PrefetchScalarGridSpec(num_scalar_prefetch=1, grid=(n // g,), in_specs=[big] * 2, out_specs=[big] * 2),
        out_shape=[jax.ShapeDtypeStruct(master.shape, f32), jax.ShapeDtypeStruct(master.shape, bf)],
        compiler_params=params(),
        name="new_weights",
    )(rate, master, update)


def halving_places(slot, core):
    dp, r = slot // 24, slot % 24
    y, z, far, x, s = dp % 2, dp // 2 % 2, dp // 4, r % 6 // 3, r % 3
    portion = r % 12 // 6
    inside = jnp.where(portion == 0, x * 8 + y * 4 + z * 2 + far, y * 8 + z * 4 + x * 2 + far)
    return jnp.where(r // 12 == core, 0, 96) + portion * 48 + inside * 3 + s


def norm_forward(row_data, gain_vec, shift_vec):
    row_mean = jnp.mean(row_data, axis=-1, keepdims=True)
    centred = row_data - row_mean
    inv_std = lax.rsqrt(jnp.mean(centred * centred, axis=-1, keepdims=True) + EPS_NORM)
    normed = centred * inv_std
    return (normed * gain_vec + shift_vec, normed, inv_std)


def norm_back(grad_out, normed, inv_std, gain_vec):
    grad_normed = grad_out * gain_vec
    return inv_std * (
        grad_normed
        - jnp.mean(grad_normed, axis=-1, keepdims=True)
        - normed * jnp.mean(grad_normed * normed, axis=-1, keepdims=True)
    )


def block_plan(counts, slot_count):
    tiles = counts.shape[0]
    per = slot_count // 128
    j = lax.broadcasted_iota(jnp.int32, (tiles, per), 1)
    kept = jnp.clip(counts[:, None] - j * 128, 0, 128).reshape(-1)
    full = (kept > 0).astype(jnp.int32)
    index = jnp.arange(tiles * per, dtype=jnp.int32)
    before = (index[None, :] < index[:, None]).astype(jnp.int32)
    ahead = jnp.sum(before * full[None, :], axis=1)
    live = jnp.sum(full)
    place = jnp.where(full > 0, ahead, live + index - ahead)
    hot = (place[None, :] == index[:, None]).astype(jnp.int32)
    return jnp.sum(hot * index[None, :], axis=1), jnp.sum(hot * kept[None, :], axis=1), live.reshape(1)


def make_body(tuned):
    def body(tokens, cotangent, counts, master, slot_block, groups, first_moment, second_moment, left_basis, right_basis, vec_params, vec_first, vec_second):
        slot_count, width = tokens.shape[1:]
        per_owner = master.shape[0]
        tile = lax.axis_index("tile")
        block_count = slot_block.shape[0]
        first = per_owner // 2 if tuned else per_owner
        index = jnp.arange(block_count, dtype=jnp.int32)
        owner = index // per_owner
        same = (owner[None, :] == owner[:, None]).astype(jnp.int32)
        is_qkv = (slot_block < 48).astype(jnp.int32)
        sooner = same * jnp.where(is_qkv[None, :] == is_qkv[:, None], (index[None, :] < index[:, None]).astype(jnp.int32), is_qkv[None, :])
        rank = jnp.sum(sooner, axis=1)
        place = jnp.where(rank < first, owner * first + rank, block_count // per_owner * first + owner * (per_owner - first) + rank - first)
        most = jnp.max(jnp.sum(same * is_qkv[None, :], axis=1))
        start = lax.axis_index("dp") * per_owner
        mine = lax.dynamic_slice(slot_block, (start,), (per_owner,))
        odd = mine % 2
        local = jnp.arange(per_owner, dtype=jnp.int32)
        at_rank = (lax.dynamic_slice(rank, (start,), (per_owner,))[None, :] == local[:, None]).astype(jnp.int32)
        order = jnp.sum(at_rank * local[None, :], axis=1)
        packed, packed_rest, weight_sq = pack_master(order, jnp.sum(at_rank * odd[None, :], axis=1), master, first)
        own_tokens = tokens.reshape(slot_count, width)
        count_tile = jnp.broadcast_to(counts.reshape(1, 1), (8, 128))
        if tuned:
            blocks, token_all, count_all = gather_all(packed, own_tokens, count_tile)
            packed_rest, blocks = lax.optimization_barrier((packed_rest, blocks))
            blocks_rest = lax.all_gather(packed_rest, "dp", axis=0, tiled=True)
        else:
            blocks = lax.all_gather(packed, "dp", axis=0, tiled=True)
            token_all = lax.all_gather(own_tokens, "tile", axis=0)
            count_all = lax.all_gather(count_tile, "tile", axis=0)
            blocks_rest = packed_rest
        tiles = token_all.shape[0]
        src, cnt, live = block_plan(count_all[:, 0, 0], slot_count)
        is_at = (slot_block[None, :] == index[:, None]).astype(jnp.int32)
        inverse = jnp.sum(is_at * index[None, :], axis=1)
        places = jnp.sum(is_at * place[None, :], axis=1)
        own_block = jnp.arange(12, dtype=jnp.int32) // 3 * 12 + jnp.arange(12, dtype=jnp.int32) % 3 * 4 + tile
        own_at = jnp.sum((slot_block[None, :] == own_block[:, None]).astype(jnp.int32) * place[None, :], axis=1)
        if tuned:
            qkv_blocks = lax.cond(
                most <= first,
                lambda: pick(own_at, blocks, packed_rest),
                lambda: pick(own_at, blocks, lax.all_gather(packed_rest, "dp", axis=0, tiled=True)),
            )
        else:
            qkv_blocks = pick(own_at, blocks, blocks_rest)
        tile_one = tile.astype(jnp.int32).reshape(1)
        own = width // tiles
        bias = lambda row: lax.dynamic_slice(vec_params[row : row + 1], (0, tile * own), (1, own))
        a1, qt, k, kt, v, vt, w_qkv, lengths = qkv_forward(
            src, cnt, tile_one % 2, token_all.reshape(-1, width), qkv_blocks, vec_params[0:1], vec_params[1:2], bias(4), bias(5)
        )
        mild = jnp.sqrt(jnp.max(lengths[:, 0, 0])) * jnp.sqrt(jnp.max(lengths[:, 1, 0])) * EXP2 <= 60.0
        live = jnp.concatenate([live, mild.astype(jnp.int32).reshape(1)])
        ot, qb, p, rt = attend(live, k, qt, vt)

        def shift(parts):
            return [parts[0]] + [lax.ppermute(parts[j], "tile", [(s, (s + j) % tiles) for s in range(tiles)]) for j in range(1, tiles)]

        o_parts = shift(spread(src, live, tile_one, ot, tiles))
        output, grad_resid, *rest = middle(
            places, counts.reshape(1), tile_one, blocks, blocks_rest, o_parts, own_tokens, cotangent.reshape(slot_count, width), vec_params, vec_params[8:].reshape(1, -1)
        )
        go_parts, (u, gz, a2, gm, gb, o_t, sums, up_sums) = rest[:tiles], rest[tiles:]
        go_parts = shift(go_parts)
        back = lambda first, heads, dt: list(attend_back(first, heads, live, p, k, kt, v, qb, dt))
        if tuned:
            dp = lax.axis_index("dp")
            bit = {"x": tile // 2, "y": dp % 2, "z": dp // 2 % 2, "far": dp // 4}
            mask = {"x": 2, "y": 4, "z": 8, "far": 16}

            def flip(array, *names):
                change = sum(mask[name] for name in names)
                return lax.ppermute(array, ("dp", "tile"), [(s, s ^ change) for s in range(32)])

            def three(sums, pairs, common):
                out = []
                for p, (a, b) in enumerate(pairs):
                    ways = [(), (a,), (b,), (a, b)]
                    del ways[common[p]]
                    out += [flip(sums[3 * p + j], *way) if way else sums[3 * p + j] for j, way in enumerate(ways)]
                return out + [flip(sums[6], pairs[0][common[0] - 1])]

            def bits_of(pairs):
                return jnp.stack([bit[name] for pair in pairs for name in pair]).astype(jnp.int32)

            first, second = [("x", "y"), ("y", "z")], [("z", "far"), ("x", "far")]
            keep, send = weight_grads_to_slots(halving_places(inverse, tile % 2), 2, block_count, o_t, gb, a2, gz, u, gm)
            send, go_parts = lax.optimization_barrier((send, go_parts))
            came = lax.ppermute(send, "tile", [(s, s ^ 1) for s in range(4)])
            dt = collect(src, live, tile_one, go_parts, ot, rt)
            dt, came = lax.optimization_barrier((dt, came))
            sums_one = add_pair(bits_of(first), (2, 1), keep, came)
            dt, sums_one = lax.optimization_barrier((dt, sums_one))
            parts = three(sums_one, first, (2, 1))
            head_grads = back(0, 2, dt)
            head_grads[0], parts = lax.optimization_barrier((head_grads[0], parts))
            sums_two = add_four(bits_of(second), (2, 2), parts)
            dt, sums_two = lax.optimization_barrier((dt, sums_two))
            parts = three(sums_two, second, (2, 2))
            head_grads += back(2, 1, dt)
            head_grads[3], parts = lax.optimization_barrier((head_grads[3], parts))
            mine_early = add_last(parts)
            head_grads[3], mine_early = lax.optimization_barrier((head_grads[3], mine_early))
            over_early = flip(mine_early, "x")
        else:
            slots = weight_grads_to_slots(inverse, 1, block_count, o_t, gb, a2, gz, u, gm)[0]
            dt = collect(src, live, tile_one, go_parts, ot, rt)
            head_grads = back(0, 3, dt)
        g_one, g_two, gw_qkv, qkv_sums, norm_sums = qkv_backward(
            src, live, tile_one % 2, token_all.reshape(-1, width), vec_params[0:1], a1, w_qkv, head_grads, tiles, slot_count * 3 // 8
        )
        if tuned:
            g_one, over_early = lax.optimization_barrier((g_one, over_early))
        zero = jnp.zeros((width,), f32)
        at_own = lambda s: lax.dynamic_update_slice(zero, s, (tile * own,))
        vector_part = jnp.concatenate(
            [norm_sums[0:2], sums[0:2], at_own(qkv_sums[0, :own])[None], at_own(qkv_sums[0, 2 * own :])[None], sums[2:4], up_sums[0].reshape(-1, width)], axis=0
        )
        if tuned:
            early, late, vector_grads = last_sums(gw_qkv, mine_early, over_early, vector_part)
            g_two, early = lax.optimization_barrier((g_two, early))
        else:
            early = lax.psum(lax.psum_scatter(slots.astype(f32), "dp", scatter_dimension=0, tiled=True), "tile").astype(bf)
            late = lax.all_gather(lax.psum(gw_qkv.astype(f32), "dp").astype(bf), "tile", axis=0, tiled=True)
            vector_grads = lax.psum(vector_part, ("dp", "tile"))
        g1 = jnp.concatenate([lax.psum_scatter(part, "tile", scatter_dimension=0, tiled=False) for part in (g_one, g_two)], axis=0)
        row_input = own_tokens.astype(f32)
        _, normed_one, inv_std_one = norm_forward(row_input, vec_params[0], vec_params[1])
        input_grad = grad_resid + norm_back(g1.astype(f32), normed_one, inv_std_one, vec_params[0])
        late_at = jnp.where(mine < 48, mine % 4 * 12 + mine // 12 * 3 + mine % 12 // 4, -1)
        weight_grads, first_out, second_out, update, update_sq = adam(odd, late_at, early, late, first_moment, second_moment, left_basis, right_basis)
        group_hot = (groups[:, None] == jnp.arange(128, dtype=jnp.int32)[None, :]).astype(f32)
        weight_part = jnp.sum(jnp.sum(at_rank.astype(f32)[:, :, None] * group_hot[None], axis=1) * jnp.sum(weight_sq[:, 0], axis=1)[:, None], axis=0)
        group_part = jnp.pad(jnp.stack([weight_part, jnp.sum(group_hot * jnp.sum(update_sq[:, 0], axis=1)[:, None], axis=0)]), ((0, 6), (0, 0)))
        group_both = group_sum(group_part, block_count // per_owner)
        own_both = jnp.sum(group_hot[None] * group_both[:2, None, :], axis=2)
        rate = RATE_BLOCK * jnp.sqrt(own_both[0]) / (jnp.sqrt(own_both[1]) + 1e-06)
        master_out, master_copy = new_weights(rate, master, update)
        vec_first_out = BETA_ONE * vec_first + (1.0 - BETA_ONE) * vector_grads
        vec_second_out = BETA_TWO * vec_second + (1.0 - BETA_TWO) * vector_grads * vector_grads
        vec_update = (vec_first_out / (1.0 - BETA_ONE**STEP)) / (jnp.sqrt(vec_second_out / (1.0 - BETA_TWO**STEP)) + ADAM_EPS)
        return (
            output.reshape(1, slot_count, width),
            input_grad.reshape(1, slot_count, width),
            weight_grads,
            first_out,
            second_out,
            master_out,
            master_copy,
            vector_grads,
            vec_first_out,
            vec_second_out,
            vec_params - RATE_VECTOR * vec_update,
        )

    return body


def solution(mesh):
    tuned = (mesh.shape["dp"], mesh.shape["tile"]) == (8, 4)
    rows, blocks = P("dp", "tile", None), P("dp", None, None)
    return jax.shard_map(
        make_body(tuned),
        mesh=mesh,
        in_specs=(rows, rows, P("dp", "tile"), blocks, P(), P("dp"), blocks, blocks, blocks, blocks, P(), P(), P()),
        out_specs=(rows, rows, blocks, blocks, blocks, blocks, blocks, P(), P(), P(), P()),
        check_vma=False,
    )
```

```python
import functools
import math

import jax
import jax.numpy as jnp
from jax import lax
from jax.experimental import pallas as pl
from jax.experimental.pallas import tpu as pltpu
from jax.sharding import PartitionSpec as P

f32 = jnp.float32
bf = jnp.bfloat16
MESH = pl.DeviceIdType.MESH

def where_am_i():
    dp=lax.axis_index("dp"); t=lax.axis_index("tile")
    return dp//2, dp%2, t//2, t%2

def dev(z,y,x,c):
    return (z*2+y, x*2+c)

def rcopy(src,dst,ss,rs,to):
    return pltpu.make_async_remote_copy(src_ref=src,dst_ref=dst,send_sem=ss,recv_sem=rs,device_id=to,device_id_type=MESH)

def gather_kernel(own_w,own_tok,own_cnt,all_w,all_tok,all_cnt,zs,zr,gs,gr,ys,yr,cs,cr,hs,hr,ts,tr,ns,nr,ls):
    z,y,x,c=where_am_i()
    per=own_w.shape[0]
    half=per//2
    def piece(shard,cc): return all_w.at[pl.ds(shard*per+cc*half,half)]
    def main(shard,cc): return all_w.at[pl.ds(shard*per+cc*half,half-1)]
    def last(shard,cc): return all_w.at[pl.ds(shard*per+cc*half+half-1,1)]
    own=own_w.at[pl.ds(c*half,half)]
    me=z*2+y
    core=dev(z,y,x,1-c); across=dev(z,y,1-x,c); beside=dev(z,1-y,x,c)
    up=dev(jnp.minimum(z+1,3),y,x,c); down=dev(jnp.maximum(z-1,0),y,x,c)
    def src(shard,first): return own if first else piece(shard,c)
    def way(zz,go_up): return ((z-zz) if go_up else (zz-z),0 if go_up else 1,up if go_up else down)
    def z_copy(zz,first,go_up):
        d,k,to=way(zz,go_up)
        return rcopy(src(zz*2+y,first),piece(zz*2+y,c),zs.at[k,d],zr.at[k,d],to)
    def z_arrival(zz,k,dist):
        r=piece(zz*2+y,c)
        return rcopy(r,r,zs.at[k,dist-1],zr.at[k,dist-1],up)
    def e_copy(zz,go_up):
        d,k,to=way(zz,go_up)
        return rcopy(last(zz*2+1-y,c),last(zz*2+1-y,c),gs.at[k,d],gr.at[k,d],to)
    def e_arrival(zz,k,dist):
        r=last(zz*2+1-y,c)
        return rcopy(r,r,gs.at[k,dist-1],gr.at[k,dist-1],up)
    def y_own(): return rcopy(own,piece(me,c),ys.at[z],yr.at[z],beside)
    def y_copy(zz): return rcopy(main(zz*2+y,c),main(zz*2+y,c),ys.at[zz],yr.at[zz],beside)
    def y_arrival(zz,whole):
        r=(piece if whole else main)(zz*2+1-y,c)
        return rcopy(r,r,ys.at[zz],yr.at[zz],beside)
    def c_copy(shard,part): return rcopy(part(shard,c),part(shard,c),cs.at[shard],cr.at[shard],core)
    def c_arrival(shard,part): return rcopy(part(shard,1-c),part(shard,1-c),cs.at[shard],cr.at[shard],core)
    def d_copy(shard): return rcopy(last(shard,c),last(shard,c),hs.at[shard],hr.at[shard],core)
    def d_arrival(shard): return rcopy(last(shard,1-c),last(shard,1-c),hs.at[shard],hr.at[shard],core)
    tile=x*2+c
    tok_x=rcopy(own_tok,all_tok.at[tile],ts.at[0],tr.at[0],across)
    tok_c=rcopy(own_tok,all_tok.at[tile],ts.at[1],tr.at[1],core)
    far=all_tok.at[(1-x)*2+c]
    tok_f=rcopy(far,far,ts.at[2],tr.at[2],core)
    near=all_tok.at[x*2+1-c]
    diag=all_tok.at[(1-x)*2+1-c]
    cnts=[rcopy(own_cnt,all_cnt.at[tile],ns.at[i],nr.at[i],to) for i,to in enumerate((across,core,dev(z,y,1-x,1-c)))]
    cnt_in=[rcopy(r,r,ns.at[i],nr.at[i],core) for i,r in enumerate((all_cnt.at[(1-x)*2+c],all_cnt.at[x*2+1-c],all_cnt.at[(1-x)*2+1-c]))]
    local=(pltpu.make_async_copy(own_w,all_w.at[pl.ds(me*per,per)],ls.at[0]),
           pltpu.make_async_copy(own_tok,all_tok.at[tile],ls.at[1]),pltpu.make_async_copy(own_cnt,all_cnt.at[tile],ls.at[2]))
    @pl.when(z<3)
    def _(): z_copy(z,True,True).start()
    @pl.when(z>0)
    def _(): z_copy(z,True,False).start()
    y_own().start(); tok_x.start(); tok_c.start()
    for cp in cnts: cp.start()
    for cp in local: cp.start()
    def from_line(k,dist):
        zz=z-dist if k==0 else z+dist
        there=(zz>=0) if k==0 else (zz<=3)
        @pl.when(there)
        def _():
            z_arrival(zz,k,dist).wait_recv()
            @pl.when((z<3) if k==0 else (z>0))
            def _(): z_copy(zz,False,k==0).start()
            y_copy(zz).start(); c_copy(zz*2+y,piece).start()
    def last_from_line(k,dist):
        zz=z-dist if k==0 else z+dist
        there=(zz>=0) if k==0 else (zz<=3)
        @pl.when(there)
        def _():
            e_arrival(zz,k,dist).wait_recv()
            @pl.when((z<3) if k==0 else (z>0))
            def _(): e_copy(zz,k==0).start()
            d_copy(zz*2+1-y).start()
    def from_beside(zz):
        y_arrival(zz,False).wait_recv(); c_copy(zz*2+1-y,main).start()
    def guarded(f,dist):
        @pl.when(z-dist>=0)
        def _(): f(z-dist)
        @pl.when(z+dist<=3)
        def _(): f(z+dist)
    from_line(0,1); from_line(1,1)
    y_arrival(z,True).wait_recv(); c_copy(z*2+1-y,piece).start()
    @pl.when(z<3)
    def _(): e_copy(z,True).start()
    @pl.when(z>0)
    def _(): e_copy(z,False).start()
    from_line(0,2); from_line(1,2)
    guarded(from_beside,1)
    last_from_line(0,1); last_from_line(1,1)
    from_line(0,3); from_line(1,3)
    tok_x.wait_recv(); tok_f.start()
    last_from_line(0,2); last_from_line(1,2)
    guarded(from_beside,2)
    last_from_line(0,3); last_from_line(1,3)
    guarded(from_beside,3)
    def from_core(zz):
        c_arrival(zz*2+y,piece).wait_recv(); c_copy(zz*2+y,piece).wait_send()
        c_arrival(zz*2+1-y,main).wait_recv(); c_copy(zz*2+1-y,main).wait_send()
        d_arrival(zz*2+1-y).wait_recv(); d_copy(zz*2+1-y).wait_send()
        y_copy(zz).wait_send()
    for dist in (1,2,3): guarded(from_core,dist)
    c_arrival(z*2+1-y,piece).wait_recv(); c_copy(z*2+1-y,piece).wait_send()
    y_own().wait_send()
    for dist in range(4):
        @pl.when(jnp.logical_and(z<3,z-dist>=0))
        def _():
            z_copy(z-dist,False,True).wait_send(); e_copy(z-dist,True).wait_send()
        @pl.when(jnp.logical_and(z>0,z+dist<=3))
        def _():
            z_copy(z+dist,False,False).wait_send(); e_copy(z+dist,False).wait_send()
    rcopy(near,near,ts.at[1],tr.at[1],core).wait_recv()
    rcopy(diag,diag,ts.at[2],tr.at[2],core).wait_recv()
    tok_x.wait_send(); tok_c.wait_send(); tok_f.wait_send()
    for cp in cnts: cp.wait_send()
    for cp in cnt_in: cp.wait_recv()
    for cp in local: cp.wait()

def gather_all(own_w,own_tok,own_cnt):
    DS=pltpu.SemaphoreType.DMA
    hbm=pl.BlockSpec(memory_space=pl.ANY)
    return pl.pallas_call(gather_kernel,
        out_shape=[jax.ShapeDtypeStruct((8*own_w.shape[0],)+own_w.shape[1:],bf),jax.ShapeDtypeStruct((4,)+own_tok.shape,bf),jax.ShapeDtypeStruct((4,)+own_cnt.shape,own_cnt.dtype)],
        in_specs=[pl.BlockSpec(memory_space=pltpu.VMEM)]*3,out_specs=[hbm]*3,
        scratch_shapes=[DS((2,4)),DS((2,4)),DS((2,4)),DS((2,4)),DS((4,)),DS((4,)),DS((8,)),DS((8,)),DS((8,)),DS((8,)),DS((3,)),DS((3,)),DS((3,)),DS((3,)),DS((3,))],
        compiler_params=pltpu.CompilerParams(has_side_effects=True,vmem_limit_bytes=60<<20),name="gather_weights_tokens")(own_w,own_tok,own_cnt)

def group_sum_kernel(g_ref,o_ref,gd,gs,gr):
    dp=lax.axis_index("dp"); t=lax.axis_index("tile")
    nd=gd.shape[0]
    def copy(k):
        return rcopy(gd.at[dp],gd.at[dp],gs.at[k],gr.at[k],((dp+k)%nd,t))
    def arrive(k):
        q=(dp-k+nd)%nd
        return rcopy(gd.at[q],gd.at[q],gs.at[k],gr.at[k],(q,t))
    def loop(f):
        def s(k,_):
            f(k); return 0
        lax.fori_loop(1,nd,s,0)
    gd[dp]=g_ref[...]
    loop(lambda k: copy(k).start())
    loop(lambda k: arrive(k).wait_recv())
    acc=gd[0]
    for i in range(1,nd): acc=acc+gd[i]
    o_ref[...]=acc
    loop(lambda k: copy(k).wait_send())

def group_sum(g,nd):
    DS=pltpu.SemaphoreType.DMA
    vm=pl.BlockSpec(memory_space=pltpu.VMEM)
    return pl.pallas_call(group_sum_kernel,out_shape=jax.ShapeDtypeStruct(g.shape,f32),in_specs=[vm],out_specs=vm,
        scratch_shapes=[pltpu.VMEM((nd,)+g.shape,f32),DS((nd,)),DS((nd,))],
        compiler_params=pltpu.CompilerParams(has_side_effects=True,vmem_limit_bytes=60<<20),name="sum_groups")(g)

def last_sums_kernel(l_ref,mine,over,v_ref,early,late,vo_ref,yb,zb,own,vb,vd,y1s,y1r,z2s,z2r,z3s,z3r,y4s,y4r,xs,xr,cs,cr,fs,fr,es,er,ts,tr,ds,dr,us,ur):
    z,y,x,c=where_am_i()
    dp=lax.axis_index("dp"); t=lax.axis_index("tile")
    core=dev(z,y,x,1-c); across=dev(z,y,1-x,c); beside=dev(z,1-y,x,c)
    def loop(f,first,n):
        def s(k,_):
            f(k); return 0
        lax.fori_loop(first,n,s,0)
    at=lambda i: pl.ds(i*3,3)
    def y1(k):
        q=(z+k)%4
        return rcopy(l_ref.at[at((1-y)*4+q)],yb.at[q],y1s.at[q],y1r.at[q],beside)
    def z2(k):
        q=(z+k)%4
        return rcopy(own.at[q],zb.at[z],z2s.at[k],z2r.at[k],dev(q,y,x,c))
    def z2_arrive(k):
        q=(z-k+4)%4
        return rcopy(zb.at[q],zb.at[q],z2s.at[k],z2r.at[k],dev(q,y,x,c))
    for k in (2,1,3,0): y1(k).start()
    def t1(k): return rcopy(v_ref.at[(t+k)%4],vb.at[t],ts.at[k],tr.at[k],(dp,(t+k)%4))
    def t1_arrive(k):
        q=(t-k+4)%4
        return rcopy(vb.at[q],vb.at[q],ts.at[k],tr.at[k],(dp,q))
    def d_copy(k): return rcopy(vd.at[dp],vd.at[dp],ds.at[k],dr.at[k],((dp+k)%8,t))
    def d_arrive(k):
        q=(dp-k+8)%8
        return rcopy(vd.at[q],vd.at[q],ds.at[k],dr.at[k],(q,t))
    def t2(k): return rcopy(vo_ref.at[t],vo_ref.at[t],us.at[k],ur.at[k],(dp,(t+k)%4))
    def t2_arrive(k):
        q=(t-k+4)%4
        return rcopy(vo_ref.at[q],vo_ref.at[q],us.at[k],ur.at[k],(dp,q))
    loop(lambda k: t1(k).start(),1,4)
    vb[t]=v_ref[t]
    def place(xx,cc,p): return early.at[pl.ds(cc*12+p*6+xx*3,3)]
    for p in range(2):
        early[pl.ds(c*12+p*6+x*3,3)]=mine[pl.ds(p*3,3)]
        early[pl.ds(c*12+p*6+(1-x)*3,3)]=over[pl.ds(p*3,3)]
    def e_copy(i,p): return rcopy(place(i,c,p),place(i,c,p),es.at[i,p],er.at[i,p],core)
    def e_arrive(i,p): return rcopy(place(i,1-c,p),place(i,1-c,p),es.at[i,p],er.at[i,p],core)
    for p in range(2):
        e_copy(0,p).start(); e_copy(1,p).start()
    loop(lambda k: t1_arrive(k).wait_recv(),1,4)
    vd[dp]=vb[0]+vb[1]+vb[2]+vb[3]
    loop(lambda k: d_copy(k).start(),1,8)
    for k in (2,1,3,0):
        q=(z+k)%4
        y1(k).wait_recv()
        for i in range(3): own[q,i]=(l_ref[(y*4+q)*3+i].astype(f32)+yb[q,i].astype(f32)).astype(bf)
        if k: z2(k).start()
    zb[z]=own[z]
    loop(lambda k: z2_arrive(k).wait_recv(),1,4)
    for i in range(3):
        late[t,(y*4+z)*3+i]=(zb[0,i].astype(f32)+zb[1,i].astype(f32)+zb[2,i].astype(f32)+zb[3,i].astype(f32)).astype(bf)
    def piece(tt,yy,zz): return late.at[tt,at(yy*4+zz)]
    def z3(k): return rcopy(piece(t,y,z),piece(t,y,z),z3s.at[k],z3r.at[k],dev((z+k)%4,y,x,c))
    def z3_arrive(k):
        q=(z-k+4)%4
        return rcopy(piece(t,y,q),piece(t,y,q),z3s.at[k],z3r.at[k],dev(q,y,x,c))
    def y4(q): return rcopy(piece(t,y,q),piece(t,y,q),y4s.at[q],y4r.at[q],beside)
    def y4_arrive(q): return rcopy(piece(t,1-y,q),piece(t,1-y,q),y4s.at[q],y4r.at[q],beside)
    far=(1-x)*2+c
    def x_copy(yy,q): return rcopy(piece(t,yy,q),piece(t,yy,q),xs.at[yy*4+q],xr.at[yy*4+q],across)
    def x_arrive(yy,q): return rcopy(piece(far,yy,q),piece(far,yy,q),xs.at[yy*4+q],xr.at[yy*4+q],across)
    def c_copy(yy,q): return rcopy(piece(t,yy,q),piece(t,yy,q),cs.at[yy*4+q],cr.at[yy*4+q],core)
    def c_arrive(yy,q): return rcopy(piece(x*2+1-c,yy,q),piece(x*2+1-c,yy,q),cs.at[yy*4+q],cr.at[yy*4+q],core)
    def f_copy(yy,q): return rcopy(piece(far,yy,q),piece(far,yy,q),fs.at[yy*4+q],fr.at[yy*4+q],core)
    def f_arrive(yy,q):
        r=piece((1-x)*2+1-c,yy,q)
        return rcopy(r,r,fs.at[yy*4+q],fr.at[yy*4+q],core)
    for k in (1,3,2): z3(k).start()
    y4(z).start(); x_copy(y,z).start(); c_copy(y,z).start()
    def passed_on(k):
        q=(z-k+4)%4
        if k:
            z3_arrive(k).wait_recv()
            y4(q).start(); x_copy(y,q).start(); c_copy(y,q).start()
        y4_arrive(q).wait_recv()
        x_copy(1-y,q).start(); c_copy(1-y,q).start()
    for k in (0,1,3,2): passed_on(k)
    loop(lambda k: d_arrive(k).wait_recv(),1,8)
    acc=vd[0]
    for i in range(1,8): acc=acc+vd[i]
    vo_ref[t]=acc
    loop(lambda k: t2(k).start(),1,4)
    for k in (0,1,3,2):
        q=(z-k+4)%4
        for yy in (y,1-y):
            x_arrive(yy,q).wait_recv(); f_copy(yy,q).start()
    def drain(q):
        for yy in range(2):
            c_arrive(yy,q).wait_recv(); f_arrive(yy,q).wait_recv()
            x_copy(yy,q).wait_send(); c_copy(yy,q).wait_send(); f_copy(yy,q).wait_send()
        y4(q).wait_send()
        y1(q).wait_send()
    loop(drain,0,4)
    def sent(k):
        t2_arrive(k).wait_recv()
        z2(k).wait_send(); z3(k).wait_send(); t1(k).wait_send(); t2(k).wait_send()
    loop(sent,1,4)
    loop(lambda k: d_copy(k).wait_send(),1,8)
    for p in range(2):
        for i in range(2):
            e_arrive(i,p).wait_recv(); e_copy(i,p).wait_send()

def last_sums(own,mine,over,v):
    DS=pltpu.SemaphoreType.DMA
    vm=pl.BlockSpec(memory_space=pltpu.VMEM)
    V=pltpu.VMEM
    S=jax.ShapeDtypeStruct
    rows=(3,v.shape[1])
    early,late,total=pl.pallas_call(last_sums_kernel,out_shape=[S((24,288,128),bf),S((4,24,144,128),bf),S((4,)+rows,f32)],in_specs=[vm]*4,out_specs=[vm]*3,
        scratch_shapes=[V((4,3,144,128),bf)]*3+[V((4,)+rows,f32),V((8,)+rows,f32)]+[DS((4,))]*8+[DS((8,))]*6+[DS((2,2))]*2+[DS((4,))]*2+[DS((8,))]*2+[DS((4,))]*2,
        cost_estimate=pl.CostEstimate(flops=10**7,bytes_accessed=150*10**6,transcendentals=0),
        compiler_params=pltpu.CompilerParams(has_side_effects=True,vmem_limit_bytes=60<<20),name="last_gradient_sums")(own.reshape(24,144,128),mine,over,v.reshape((4,)+rows))
    return early,late.reshape(48,288,128),total.reshape(v.shape)


H = 12
STEP = 10
EPS_NORM = 1e-06
BETA_ONE = 0.5
BETA_TWO = 0.5
ADAM_EPS = 1e-08
RATE_BLOCK = 0.3
RATE_VECTOR = 0.2
NEG_RAW = -8.0e9
HEAD = 64
SCALE = 1.0 / math.sqrt(HEAD)
EXP2 = SCALE * math.log2(math.e)
NN = (((1,), (0,)), ((), ()))
NT = (((1,), (1,)), ((), ()))
TN = (((0,), (0,)), ((), ()))


def mm(a, b, dims=NN):
    return lax.dot_general(a, b, dims, preferred_element_type=f32)


def column_sum(v):
    return jnp.sum(v, axis=0, keepdims=True)


def vmem_spec():
    return pl.BlockSpec(memory_space=pltpu.VMEM)


def smem_spec():
    return pl.BlockSpec(memory_space=pltpu.SMEM)


def any_spec():
    return pl.BlockSpec(memory_space=pl.ANY)


def params(mib=60):
    return pltpu.CompilerParams(vmem_limit_bytes=mib << 20)


def pack(block, odd):
    half = block.shape[0] // 2
    if odd:
        return block[:, 64:], jnp.concatenate([block[half:, :64], block[:half, :64]], axis=1)
    return block[:, :128], jnp.concatenate([block[:half, 128:], block[half:, 128:]], axis=1)


def unpack(top, tail, odd):
    if odd:
        return jnp.concatenate([jnp.concatenate([tail[:, 64:], tail[:, :64]], axis=0), top], axis=1)
    return jnp.concatenate([top, jnp.concatenate([tail[:, :64], tail[:, 64:]], axis=0)], axis=1)


def unpack_either(top, tail, odd):
    return jnp.where(odd, unpack(top, tail, 1), unpack(top, tail, 0))


def lane_sums(v):
    s = column_sum(v)
    return jnp.broadcast_to(s[:, :128] + jnp.concatenate([s[:, 128:], jnp.zeros((1, 64), f32)], axis=1), (8, 128))


def by_parity(value, run):
    for odd in (0, 1):
        pl.when(value == odd)(functools.partial(run, odd))


def turn(v):
    return jnp.concatenate([v[:, 64:], v[:, :64]], axis=1)


def group_of(n):
    return 4 if n % 4 == 0 else 3 if n % 3 == 0 else 1


def pack_kernel(early, order_ref, odd_ref, *refs):
    g = len(refs) - 3
    p_ref, late_ref, s_ref = refs[g:]
    i = pl.program_id(0)
    for b in range(g):
        m = refs[b][0]

        def place(odd, m=m, b=b):
            top, tail = pack(m, odd)
            for ref, here in ((p_ref, i < early), (late_ref, i >= early)):

                @pl.when(here)
                def _():
                    ref[b, :192] = top.astype(bf)
                    ref[b, 192:] = tail.astype(bf)

        by_parity(odd_ref[i * g + b], place)
        s_ref[b] = lane_sums(m * m)


def pack_master(order, odd, master, first):
    n = master.shape[0]
    g = group_of(first)
    early = first // g
    rest = max(n - first, g)
    spec = pltpu.PrefetchScalarGridSpec(
        num_scalar_prefetch=2,
        grid=(n // g,),
        in_specs=[pl.BlockSpec((1, 192, 192), lambda i, s, o, b=b: (s[i * g + b], 0, 0)) for b in range(g)],
        out_specs=[
            pl.BlockSpec((g, 288, 128), lambda i, s, o: (jnp.minimum(i, early - 1), 0, 0)),
            pl.BlockSpec((g, 288, 128), lambda i, s, o: (jnp.maximum(i - early, 0), 0, 0)),
            pl.BlockSpec((g, 8, 128), lambda i, s, o: (i, 0, 0)),
        ],
    )
    return pl.pallas_call(
        functools.partial(pack_kernel, early),
        grid_spec=spec,
        out_shape=[jax.ShapeDtypeStruct((first, 288, 128), bf), jax.ShapeDtypeStruct((rest, 288, 128), bf), jax.ShapeDtypeStruct((n, 8, 128), f32)],
        compiler_params=params(),
        name="pack_master",
    )(order, odd, *[master] * g)


def pick_kernel(at_ref, first_ref, rest_ref, o_ref, sems):
    split = first_ref.shape[0]
    for j in range(12):

        @pl.when(at_ref[j] < split)
        def _():
            pltpu.make_async_copy(first_ref.at[at_ref[j]], o_ref.at[j], sems.at[j]).start()

        @pl.when(at_ref[j] >= split)
        def _():
            pltpu.make_async_copy(rest_ref.at[at_ref[j] - split], o_ref.at[j], sems.at[j]).start()

    for j in range(12):
        pltpu.make_async_copy(first_ref.at[0], o_ref.at[j], sems.at[j]).wait()


def pick(at, first, rest):
    return pl.pallas_call(
        pick_kernel,
        in_specs=[smem_spec(), any_spec(), any_spec()],
        out_specs=vmem_spec(),
        out_shape=jax.ShapeDtypeStruct((12, 288, 128), bf),
        scratch_shapes=[pltpu.SemaphoreType.DMA((12,))],
        compiler_params=params(),
        name="pick_qkv_blocks",
    )(at, first, rest)


def qkv_kernel(src_ref, cnt_ref, at_ref, x0, x1, x2, x3, blk_ref, gain_ref, shift_ref, bq_ref, bv_ref, a_ref, qt_ref, k_ref, kt_ref, v_ref, vt_ref, w_ref, st_ref):
    i = pl.program_id(0)

    @pl.when(i == 0)
    def _():
        def join(odd):
            for r in range(4):
                parts = []
                for c in range(3):
                    p = blk_ref[r * 3 + c].astype(f32)
                    parts.append(unpack(p[:192], p[192:], odd))
                w_ref[r * 192 : (r + 1) * 192, :] = jnp.concatenate(parts, axis=1).astype(bf)

        by_parity(at_ref[0], join)

    x = jnp.concatenate([r[...] for r in (x0, x1, x2, x3)], axis=0).astype(f32)
    mean = jnp.mean(x, axis=-1, keepdims=True)
    cen = x - mean
    inv_std = lax.rsqrt(jnp.mean(cen * cen, axis=-1, keepdims=True) + EPS_NORM)
    a = (cen * inv_std * gain_ref[...] + shift_ref[...]).astype(bf)
    a_ref[...] = a
    qkv = mm(a, w_ref[...])
    q = (qkv[:, :192] + bq_ref[...]).astype(bf).astype(f32)
    k = qkv[:, 192:384].astype(bf).astype(f32)
    v = (qkv[:, 384:] + bv_ref[...]).astype(bf).astype(f32)
    row = lax.broadcasted_iota(jnp.int32, (128, 64), 0)
    lane = lax.broadcasted_iota(jnp.int32, (512, 64), 1)
    masked = jnp.concatenate(
        [jnp.where(row < cnt_ref[4 * i + b], 0.0, NEG_RAW) for b in range(4)], axis=0
    )
    ones = jnp.where(lane < 4, 1.0, 0.0)
    k_tail = jnp.where(lane == 0, masked, ones)
    v_tail = jnp.where(lane < 3, 1.0, 0.0)
    sub = lax.broadcasted_iota(jnp.int32, (64, 512), 0)
    t_tail = jnp.where(sub < 1, 1.0, 0.0)
    qt, kt, vt = q.T, k.T, v.T
    longest = lambda a: jnp.max(jnp.concatenate([column_sum(a[h * 64 : (h + 1) * 64] ** 2) for h in range(3)], axis=0))
    st_ref[0] = jnp.where(lax.broadcasted_iota(jnp.int32, (8, 128), 0) == 0, longest(qt), longest(kt))
    for h in range(3):
        s = slice(h * 64, (h + 1) * 64)
        k_ref[h] = jnp.concatenate([k[:, s], k_tail], axis=1).astype(bf)
        v_ref[h] = jnp.concatenate([v[:, s], v_tail], axis=1).astype(bf)
        qt_ref[h] = jnp.concatenate([qt[s], t_tail], axis=0).astype(bf)
        kt_ref[h] = kt[s].astype(bf)
        vt_ref[h] = jnp.concatenate([vt[s], t_tail[:16]], axis=0).astype(bf)


def qkv_forward(src, cnt, odd, tokens, blocks, gain, shift, bq, bv):
    n = tokens.shape[0]
    rows = [pl.BlockSpec((128, 768), lambda i, s, c, o, k=k: (s[4 * i + k], 0)) for k in range(4)]
    row = lambda i, s, c, o: (0, 0)
    spec = pltpu.PrefetchScalarGridSpec(
        num_scalar_prefetch=3,
        grid=(n // 512,),
        in_specs=rows
        + [pl.BlockSpec((12, 288, 128), lambda i, s, c, o: (0, 0, 0)), pl.BlockSpec((1, 768), row), pl.BlockSpec((1, 768), row), pl.BlockSpec((1, 192), row), pl.BlockSpec((1, 192), row)],
        out_specs=[
            pl.BlockSpec((512, 768), lambda i, s, c, o: (i, 0)),
            pl.BlockSpec((3, 128, 512), lambda i, s, c, o: (0, 0, i)),
            pl.BlockSpec((3, 512, 128), lambda i, s, c, o: (0, i, 0)),
            pl.BlockSpec((3, 64, 512), lambda i, s, c, o: (0, 0, i)),
            pl.BlockSpec((3, 512, 128), lambda i, s, c, o: (0, i, 0)),
            pl.BlockSpec((3, 80, 512), lambda i, s, c, o: (0, 0, i)),
            pl.BlockSpec((768, 576), row),
            pl.BlockSpec((1, 8, 128), lambda i, s, c, o: (i, 0, 0)),
        ],
    )
    shapes = [(n, 768), (3, 128, n), (3, n, 128), (3, 64, n), (3, n, 128), (3, 80, n), (768, 576)]
    return pl.pallas_call(
        qkv_kernel,
        grid_spec=spec,
        out_shape=[jax.ShapeDtypeStruct(s, bf) for s in shapes] + [jax.ShapeDtypeStruct((n // 512, 8, 128), f32)],
        compiler_params=params(),
        name="norm_and_qkv",
    )(src, cnt, odd, tokens, tokens, tokens, tokens, blocks, gain, shift, bq, bv)


def split3(v):
    a = v.astype(bf).astype(f32)
    b = (v - a).astype(bf).astype(f32)
    return a, b, v - a - b


def in_steps(units, sizes, body, carry):
    at = 0
    for size in sizes:
        count = (units - at) // size
        carry = lax.fori_loop(0, count, lambda i, c, at=at, size=size: body(at + i * size, size, c), carry)
        at = at + count * size
    return carry


def attend_kernel(bq, n_ref, k_ref, qt_ref, vt_ref, ot_ref, qb_ref, p_ref, rt_ref):
    live = n_ref[0]
    qi = pl.program_id(1)
    pairs = (live + 7) // 8 * 4

    def finish(top, acc):
        total = acc[64:65]
        ot_ref[0] = acc[:64] / total
        rt_ref[0] = 1.0 / total
        a, b, c = split3((top + jnp.log2(total)) * (-1.0 / EXP2))
        row = lax.broadcasted_iota(jnp.int32, (64, bq), 0)
        tail = jnp.where(row == 0, 1.0, jnp.where(row == 1, a, jnp.where(row == 2, b, jnp.where(row == 3, c, 0.0))))
        qb_ref[0, :64] = qt_ref[0, :64]
        qb_ref[0, 64:] = tail.astype(bf)

    def keys(u, size):
        return pl.ds(pl.multiple_of(u * 256, 256), size * 256)

    @pl.when(jnp.logical_and(qi * bq < live * 128, n_ref[1] == 1))
    def _():
        qt = qt_ref[0]

        def body(u, size, acc):
            step = min(size, 2)
            for part in range(0, size, step):
                at = keys(u + part, step)
                p = jnp.exp2(mm(k_ref[0, at, :], qt) * EXP2).astype(bf)
                p_ref[0, at, :] = p
                acc = acc + mm(vt_ref[0, :, at], p)
            return acc

        finish(0.0, in_steps(pairs, (16, 8, 4), body, jnp.zeros((80, bq), f32)))

    @pl.when(jnp.logical_and(qi * bq < live * 128, n_ref[1] == 0))
    def _():
        qt = qt_ref[0]

        def body(u, size, carry):
            top, acc = carry
            s = mm(k_ref[0, keys(u, size), :], qt) * EXP2
            new = jnp.maximum(top, jnp.max(s, axis=0, keepdims=True))
            p = jnp.exp2(s - new).astype(bf)
            return new, acc * jnp.exp2(top - new) + mm(vt_ref[0, :, keys(u, size)], p)

        finish(*in_steps(pairs, (4,), body, (jnp.full((1, bq), -3e38, f32), jnp.zeros((80, bq), f32))))


def attend(live, k, qt, vt, bq=1024):
    n = k.shape[1]
    spec = pltpu.PrefetchScalarGridSpec(
        num_scalar_prefetch=1,
        grid=(3, n // bq),
        in_specs=[
            pl.BlockSpec((1, n, 128), lambda h, i, s: (h, 0, 0)),
            pl.BlockSpec((1, 128, bq), lambda h, i, s: (h, 0, i)),
            pl.BlockSpec((1, 80, n), lambda h, i, s: (h, 0, 0)),
        ],
        out_specs=[
            pl.BlockSpec((1, 64, bq), lambda h, i, s: (h, 0, i)),
            pl.BlockSpec((1, 128, bq), lambda h, i, s: (h, 0, i)),
            pl.BlockSpec((1, n, bq), lambda h, i, s: (h, 0, i)),
            pl.BlockSpec((1, 1, bq), lambda h, i, s: (h, 0, i)),
        ],
    )
    return pl.pallas_call(
        functools.partial(attend_kernel, bq),
        grid_spec=spec,
        out_shape=[
            jax.ShapeDtypeStruct((3, 64, n), f32),
            jax.ShapeDtypeStruct((3, 128, n), bf),
            jax.ShapeDtypeStruct((3, n, n), bf),
            jax.ShapeDtypeStruct((3, 1, n), f32),
        ],
        compiler_params=params(),
        name="attention_forward",
    )(live, k, qt, vt)


def spread_kernel(src_ref, n_ref, t_ref, ot_ref, *o_refs):
    live, t, tiles = n_ref[0], t_ref[0], len(o_refs)
    per = o_refs[0].shape[1] // 128

    def step(b, _):
        g = src_ref[b]
        lanes = pl.ds(pl.multiple_of(b * 128, 128), 128)
        to = pl.ds(pl.multiple_of((g % per) * 128, 128), 128)
        for k in range(tiles):
            here = (g // per - t + tiles) % tiles == k

            @pl.when(jnp.logical_and(here, b < live))
            def _():
                for h in range(3):
                    o_refs[k][h * 64 : (h + 1) * 64, to] = ot_ref[h, :, lanes].astype(bf)

            @pl.when(jnp.logical_and(here, b >= live))
            def _():
                o_refs[k][:, to] = jnp.zeros((192, 128), bf)

        return 0

    lax.fori_loop(0, ot_ref.shape[2] // 128, step, 0)


def spread(src, live, tile, ot, tiles):
    n = ot.shape[2]
    return pl.pallas_call(
        spread_kernel,
        in_specs=[smem_spec()] * 3 + [vmem_spec()],
        out_specs=[vmem_spec()] * tiles,
        out_shape=[jax.ShapeDtypeStruct((192, n // tiles), bf)] * tiles,
        compiler_params=params(),
        name="spread_attended",
    )(src, live, tile, ot)


def collect_kernel(src_ref, n_ref, t_ref, ot_ref, rt_ref, *refs):
    g_refs, dt_ref = refs[:-1], refs[-1]
    live, t, tiles = n_ref[0], t_ref[0], len(g_refs)
    mild = n_ref[1] == 1
    per = g_refs[0].shape[1] // 128
    row = lax.broadcasted_iota(jnp.int32, (64, 128), 0)

    def step(b, _):
        g = src_ref[b]
        to = pl.ds(pl.multiple_of(b * 128, 128), 128)
        lanes = pl.ds(pl.multiple_of((g % per) * 128, 128), 128)
        for k in range(tiles):

            @pl.when(jnp.logical_and((t - g // per + tiles) % tiles == k, b < live))
            def _():
                for h in range(3):
                    scale = jnp.where(mild, rt_ref[h, :, to], 1.0)
                    d = (g_refs[k][h * 64 : (h + 1) * 64, lanes].astype(f32) * scale).astype(bf).astype(f32)
                    x, y, z = split3(-jnp.sum(d * ot_ref[h, :, to], axis=0, keepdims=True))
                    tail = jnp.where(row == 0, x, jnp.where(row == 1, y, jnp.where(row == 2, z, 0.0)))
                    dt_ref[h, :, to] = jnp.concatenate([d, tail], axis=0).astype(bf)

        @pl.when(b >= live)
        def _():
            dt_ref[:, :, to] = jnp.zeros((3, 128, 128), bf)

        return 0

    lax.fori_loop(0, ot_ref.shape[2] // 128, step, 0)


def collect(src, live, tile, grads, ot, rt):
    n = ot.shape[2]
    return pl.pallas_call(
        collect_kernel,
        in_specs=[smem_spec()] * 3 + [vmem_spec()] * (2 + len(grads)),
        out_specs=vmem_spec(),
        out_shape=jax.ShapeDtypeStruct((3, 128, n), bf),
        compiler_params=params(),
        name="collect_attended_grad",
    )(src, live, tile, ot, rt, *grads)


def attend_back_kernel(bk, n_ref, p_ref, k_ref, kt_ref, v_ref, qb_ref, dt_ref, dq_ref, dk_ref, dv_ref):
    live = n_ref[0]
    j = pl.program_id(1)

    @pl.when(j == 0)
    def _():
        dq_ref[...] = jnp.zeros_like(dq_ref)

    def lanes(u):
        return pl.ds(pl.multiple_of(u * 256, 256), 256)

    pairs = (live + 1) // 2

    def over_queries(rows, sizes, body):
        zero = jnp.zeros((rows, 64), f32)
        dk, dv = in_steps((live + 7) // 8 * 4, sizes, body, (zero, zero))
        dk_ref[0, :rows] = (dk * SCALE).astype(bf)
        dv_ref[0, :rows] = dv.astype(bf)

    def with_kept(rows):
        k, v, kt = k_ref[0, :rows], v_ref[0, :rows], kt_ref[0, :, :rows]

        def body(u, size, carry):
            dk, dv = carry
            dp = mm(v, dt_ref[0, :, lanes(u)])
            for part in range(size):
                at = lanes(u + part)
                ahead = mm(v, dt_ref[0, :, lanes(u + part + 1)]) if part + 1 < size else None
                p = p_ref[0, :rows, at]
                ds = (p.astype(f32) * dp).astype(bf)
                dv = dv + mm(p, dt_ref[0, :64, at], NT)
                dk = dk + mm(ds, qb_ref[0, :64, at], NT)
                dq_ref[0, :, at] += mm(kt, ds)
                dp = dp if ahead is None else ahead
            return dk, dv

        over_queries(rows, (16, 8, 4), body)

    @pl.when(jnp.logical_and(n_ref[1] == 1, 2 * j + 2 <= pairs))
    def _():
        with_kept(bk)

    @pl.when(jnp.logical_and(n_ref[1] == 1, 2 * j + 1 == pairs))
    def _():
        dk_ref[0, bk // 2 :] = jnp.zeros((bk // 2, 64), bf)
        dv_ref[0, bk // 2 :] = jnp.zeros((bk // 2, 64), bf)
        with_kept(bk // 2)

    @pl.when(jnp.logical_and(n_ref[1] == 0, j * bk < live * 128))
    def _():
        k, v, kt = k_ref[0], v_ref[0], kt_ref[0]

        def body(u, size, carry):
            dk, dv = carry
            for part in range(size):
                at = lanes(u + part)
                p = jnp.exp2(mm(k, qb_ref[0, :, at]) * EXP2)
                ds = (p * mm(v, dt_ref[0, :, at])).astype(bf)
                dv = dv + mm(p.astype(bf), dt_ref[0, :64, at], NT)
                dk = dk + mm(ds, qb_ref[0, :64, at], NT)
                dq_ref[0, :, at] += mm(kt, ds)
            return dk, dv

        over_queries(bk, (4,), body)


def attend_back(first, heads, live, p, k, kt, v, qb, dt, bk=512):
    n = k.shape[1]
    whole_t = lambda h, j, s: (first + h, 0, 0)
    rows = lambda h, j, s: (first + h, j, 0)
    spec = pltpu.PrefetchScalarGridSpec(
        num_scalar_prefetch=1,
        grid=(heads, n // bk),
        in_specs=[
            pl.BlockSpec((1, bk, n), rows),
            pl.BlockSpec((1, bk, 128), rows),
            pl.BlockSpec((1, 64, bk), lambda h, j, s: (first + h, 0, j)),
            pl.BlockSpec((1, bk, 128), rows),
            pl.BlockSpec((1, 128, n), whole_t),
            pl.BlockSpec((1, 128, n), whole_t),
        ],
        out_specs=[
            pl.BlockSpec((1, 64, n), lambda h, j, s: (h, 0, 0)),
            pl.BlockSpec((1, bk, 64), lambda h, j, s: (h, j, 0)),
            pl.BlockSpec((1, bk, 64), lambda h, j, s: (h, j, 0)),
        ],
    )
    S = jax.ShapeDtypeStruct
    return pl.pallas_call(
        functools.partial(attend_back_kernel, bk),
        grid_spec=spec,
        out_shape=[S((heads, 64, n), f32), S((heads, n, 64), bf), S((heads, n, 64), bf)],
        cost_estimate=pl.CostEstimate(flops=heads * 4 * 10**10, bytes_accessed=heads * 50 * 10**6, transcendentals=0),
        compiler_params=params(),
        name="attention_backward",
    )(live, p, k, kt, v, qb, dt)


def qkv_back_kernel(given, src_ref, n_ref, odd_ref, x0, x1, x2, x3, gain_ref, a_ref, w_ref, *refs):
    grads, (ga_ref, gz_ref, gw_ref, gb_ref, vs_ref, acc, sums, rows, sems) = refs[:given], refs[given:]
    dqs, dks, dvs = [[(r, h) for r in grads[j::3] for h in range(r.shape[0])] for j in range(3)]
    early = ga_ref.shape[1] // 128
    i = pl.program_id(0)
    live = n_ref[0]
    slot = i % 2

    def wait_for(slot):
        for b in range(4):
            pltpu.make_async_copy(rows.at[slot, pl.ds(b * 128, 128)], ga_ref.at[0, pl.ds(0, 128)], sems.at[slot, b]).wait()

    @pl.when(i >= 2)
    def _():
        wait_for(slot)

    @pl.when(i == 0)
    def _():
        acc[...] = jnp.zeros_like(acc)
        sums[...] = jnp.zeros_like(sums)
        vs_ref[...] = jnp.zeros_like(vs_ref)

    @pl.when(4 * i < live)
    def _():
        dq = jnp.concatenate([r[h] for r, h in dqs], axis=0).T * SCALE
        g = jnp.concatenate([dq] + [r[h].astype(f32) for r, h in dks + dvs], axis=1).astype(bf)
        acc[...] += mm(a_ref[...], g, TN)
        sums[...] += jnp.broadcast_to(column_sum(g.astype(f32)), sums.shape)
        g1 = mm(g, w_ref[...], NT)
        rows[slot] = g1.astype(bf)
        x = jnp.concatenate([r[...] for r in (x0, x1, x2, x3)], axis=0).astype(f32)
        cen = x - jnp.mean(x, axis=-1, keepdims=True)
        normed = cen * lax.rsqrt(jnp.mean(cen * cen, axis=-1, keepdims=True) + EPS_NORM)
        vs_ref[0:1, :] += column_sum(g1 * normed)
        vs_ref[1:2, :] += column_sum(g1)

    @pl.when(4 * i >= live)
    def _():
        rows[slot] = jnp.zeros(rows.shape[1:], bf)

    per = early + gz_ref.shape[1] // 128
    for b in range(4):
        block, at = rows.at[slot, pl.ds(b * 128, 128)], src_ref[4 * i + b]
        t, j = at // per, at % per

        @pl.when(j < early)
        def _():
            pltpu.make_async_copy(block, ga_ref.at[t, pl.ds(pl.multiple_of(j * 128, 128), 128)], sems.at[slot, b]).start()

        @pl.when(j >= early)
        def _():
            pltpu.make_async_copy(block, gz_ref.at[t, pl.ds(pl.multiple_of((j - early) * 128, 128), 128)], sems.at[slot, b]).start()

    @pl.when(i == pl.num_programs(0) - 1)
    def _():
        wait_for(1 - slot)
        wait_for(slot)

        def place(odd):
            for r in range(4):
                for c in range(3):
                    top, tail = pack(acc[r * 192 : (r + 1) * 192, c * 192 : (c + 1) * 192], odd)
                    gw_ref[r * 3 + c, :192] = top.astype(bf)
                    gw_ref[r * 3 + c, 192:] = tail.astype(bf)

        by_parity(odd_ref[0], place)
        gb_ref[...] = sums[...]


def qkv_backward(src, live, odd, tokens, gain, a, w, grads, tiles, early):
    n = a.shape[0]
    per = n // tiles
    fixed = lambda i, s, c, o: (0, 0)
    row = lambda i, s, c, o: (0, i, 0)
    spec = pltpu.PrefetchScalarGridSpec(
        num_scalar_prefetch=3,
        grid=(n // 512,),
        in_specs=[pl.BlockSpec((128, 768), lambda i, s, c, o, k=k: (s[4 * i + k], 0)) for k in range(4)]
        + [pl.BlockSpec((1, 768), fixed), pl.BlockSpec((512, 768), lambda i, s, c, o: (i, 0)), pl.BlockSpec((768, 576), fixed)]
        + [
            pl.BlockSpec((g.shape[0], 64, 512), lambda i, s, c, o: (0, 0, i)) if g.shape[1] == 64 else pl.BlockSpec((g.shape[0], 512, 64), row)
            for g in grads
        ],
        out_specs=[any_spec(), any_spec(), pl.BlockSpec((12, 288, 128), lambda i, s, c, o: (0, 0, 0)), pl.BlockSpec((8, 576), fixed), pl.BlockSpec((8, 768), fixed)],
        scratch_shapes=[pltpu.VMEM((768, 576), f32), pltpu.VMEM((8, 576), f32), pltpu.VMEM((2, 512, 768), bf), pltpu.SemaphoreType.DMA((2, 4))],
    )
    S = jax.ShapeDtypeStruct
    return pl.pallas_call(
        functools.partial(qkv_back_kernel, len(grads)),
        grid_spec=spec,
        out_shape=[S((tiles, early, 768), bf), S((tiles, per - early, 768), bf), S((12, 288, 128), bf), S((8, 576), f32), S((8, 768), f32)],
        cost_estimate=pl.CostEstimate(flops=3 * 10**10, bytes_accessed=40 * 10**6, transcendentals=0),
        compiler_params=params(),
        name="qkv_backward",
    )(src, live, odd, tokens, tokens, tokens, tokens, gain, a, w, *grads)


def gelu_parts(z):
    cdf = 0.5 + 0.5 * lax.erf(z * math.sqrt(0.5))
    return z * cdf, cdf + z * (jnp.exp2(z * z * (-0.5 * math.log2(math.e))) * (1.0 / math.sqrt(2.0 * math.pi)))


def middle_kernel(inv_ref, cnt_ref, t_ref, blk_ref, rest_ref, o0, o1, o2, o3, x_ref, c_ref, vp_ref, bu_ref, y_ref, gr_ref, g0, g1, g2_ref, g3,
                  u_s, gz_s, a2_s, gm_s, gb_s, o_s, vs_ref, us_ref, w_out, w_up, w_down, tails, tsem, isem):
    i = pl.program_id(0)
    rows = x_ref.shape[0]
    split = blk_ref.shape[0]
    r0 = i * rows
    kinds = ((w_out, 48, 2, 4), (w_up, 64, 8, 4), (w_down, 128, 2, 16))

    @pl.when(i == 0)
    def _():
        vs_ref[...] = jnp.zeros_like(vs_ref)
        us_ref[...] = jnp.zeros_like(us_ref)

        def pair(w, first, pairs):
            def parts(j, run):
                r = pl.multiple_of((j // pairs) * 192, 64)
                col = pl.multiple_of((j % pairs) * 384, 128)
                for b, off in ((0, 0), (1, 256)):
                    at = first + 2 * j + b
                    run(at, w.at[pl.ds(r, 192), pl.ds(col + off, 128)], tails.at[at - 48])
                return r, col

            def fetch(at, top, tail):
                for ref, here, slot in ((blk_ref, inv_ref[at] < split, inv_ref[at]), (rest_ref, inv_ref[at] >= split, inv_ref[at] - split)):

                    @pl.when(here)
                    def _():
                        pltpu.make_async_copy(ref.at[slot, pl.ds(0, 192)], top, tsem.at[at - 48]).start()
                        pltpu.make_async_copy(ref.at[slot, pl.ds(192, 96)], tail, isem.at[at - 48]).start()

            def fetched(at, top, tail):
                pltpu.make_async_copy(blk_ref.at[0, pl.ds(0, 192)], top, tsem.at[at - 48]).wait()
                pltpu.make_async_copy(blk_ref.at[0, pl.ds(192, 96)], tail, isem.at[at - 48]).wait()

            def start(j, _):
                parts(j, fetch)
                return 0

            def join(j, _):
                r, col = parts(j, fetched)
                even = tails[first + 2 * j - 48].astype(f32)
                odd = tails[first + 2 * j - 47].astype(f32)
                lane = lax.broadcasted_iota(jnp.int32, even.shape, 1) < 64
                w[pl.ds(r, 96), pl.ds(col + 128, 128)] = jnp.where(lane, even, odd).astype(bf)
                w[pl.ds(r + 96, 96), pl.ds(col + 128, 128)] = turn(jnp.where(lane, odd, even)).astype(bf)
                return 0

            return start, join

        todo = [(pair(w, first, pairs), pairs * high) for w, first, pairs, high in kinds]
        for (start, _), n in todo:
            lax.fori_loop(0, n, start, 0)

        for (_, join), n in todo:
            lax.fori_loop(0, n, join, 0)

    vp = vp_ref[...]
    row = r0 + lax.broadcasted_iota(jnp.int32, (rows, 1), 0)
    live = jnp.where(row < cnt_ref[0], 1.0, 0.0)
    t = t_ref[0]
    for k, ref in enumerate((o0, o1, o2, o3)):
        o_s[pl.ds(pl.multiple_of(((t - k + 4) % 4) * 192, 64), 192), :] = ref[...]
    o_t = o_s[...]
    res = x_ref[...].astype(f32) + mm(o_t, w_out[...], TN) + vp[6:7]
    cen = res - jnp.mean(res, axis=-1, keepdims=True)
    inv_std = lax.rsqrt(jnp.mean(cen * cen, axis=-1, keepdims=True) + EPS_NORM)
    normed = cen * inv_std
    a2 = (normed * vp[2:3] + vp[3:4]).astype(bf)
    gy = c_ref[...].astype(f32) * live
    gm = gy.astype(bf)
    a2_s[...] = a2
    gm_s[...] = gm
    branch = jnp.zeros((rows, 768), f32)
    g2 = jnp.zeros((rows, 768), f32)
    for j in range(4):
        cols = slice(j * 768, (j + 1) * 768)
        u, slope = gelu_parts(mm(a2, w_up[:, cols]) + bu_ref[:, cols])
        u = u.astype(bf)
        u_s[:, cols] = u
        branch = branch + mm(u, w_down[cols, :])
        gz = (mm(gm, w_down[cols, :], NT) * slope).astype(bf)
        gz_s[:, cols] = gz
        us_ref[:, cols] += jnp.broadcast_to(column_sum(gz.astype(f32)), (8, 768))
        g2 = g2 + mm(gz, w_up[:, cols], NT)
    y_ref[...] = (live * (res + branch + vp[7:8])).astype(bf)
    d2 = g2 * vp[2:3]
    gr = gy + inv_std * (d2 - jnp.mean(d2, axis=-1, keepdims=True) - normed * jnp.mean(d2 * normed, axis=-1, keepdims=True))
    gr_ref[...] = gr
    gb = gr.astype(bf)
    gb_s[...] = gb
    vs_ref[0:1, :] += column_sum(g2 * normed)
    vs_ref[1:2, :] += column_sum(g2)
    vs_ref[2:3, :] += column_sum(gb.astype(f32))
    vs_ref[3:4, :] += column_sum(gm.astype(f32))
    for k, ref in enumerate((g0, g1, g2_ref, g3)):
        ref[...] = mm(w_out[pl.ds(pl.multiple_of(((t + k) % 4) * 192, 64), 192), :], gb, NT).astype(bf)


def weight_grad_kernel(outs, pos_ref, o_in, gb_in, a2_in, gz_in, u_in, gm_in, *refs):
    s_refs, (o_s, gb_s, a2_s, gz_s, u_s, gm_s, ring, zero, lsem, osem, zsem) = refs[:outs], refs[outs:]
    each = s_refs[0].shape[0]

    def to_slot(block, at, sem):
        for o in range(outs):

            @pl.when(at // each == o)
            def _():
                pltpu.make_async_copy(block, s_refs[o].at[at % each], sem).start()

    def landed(block, sem):
        pltpu.make_async_copy(block, s_refs[0].at[0], sem).wait()

    loads = [pltpu.make_async_copy(a, b, lsem.at[j]) for j, (a, b) in enumerate(
        ((o_in, o_s), (gb_in, gb_s), (a2_in, a2_s), (gz_in, gz_s), (gm_in, gm_s), (u_in, u_s)))]
    for load in loads:
        load.start()
    zero[...] = jnp.zeros_like(zero)

    def clear(j, _):
        to_slot(zero, pos_ref[j], zsem.at[j])
        return 0

    lax.fori_loop(0, 48, clear, 0)
    def send(n, g, first, pairs, high, low):
        half = (n % 2) * 8

        def put(r, b):
            return first + (high + r) * 2 * pairs + 2 * low + b

        for r in range(4):
            part = g[r * 192 : (r + 1) * 192]
            mid = part[:, 128:256]
            upper, lower = mid[:96], turn(mid[96:])
            lane = lax.broadcasted_iota(jnp.int32, upper.shape, 1) < 64
            for b, top, tail in ((0, part[:, :128], jnp.where(lane, upper, lower)), (1, part[:, 256:], jnp.where(lane, lower, upper))):
                k = half + 2 * r + b

                @pl.when(n >= 2)
                def _():
                    landed(ring.at[k], osem.at[k])

                ring[k, :192] = top.astype(bf)
                ring[k, 192:] = tail.astype(bf)
                to_slot(ring.at[k], pos_ref[put(r, b)], osem.at[k])

    def lanes(j):
        return pl.ds(pl.multiple_of(j * 384, 128), 384)

    def grad_out(n, _):
        send(n, mm(o_s[...], gb_s[:, lanes(n)]), 48, 2, 0, n)
        return 0

    def grad_up(n, _):
        send(n, mm(a2_s[...], gz_s[:, lanes(n)], TN), 64, 8, 0, n)
        return 0

    def grad_down(n, _):
        high = n // 2
        send(n, mm(u_s[:, pl.ds(pl.multiple_of(high * 768, 128), 768)], gm_s[:, lanes(n % 2)], TN), 128, 2, high * 4, n % 2)
        return 0

    def drain():
        for k in range(16):
            landed(ring.at[k], osem.at[k])

    for f, n, first in ((grad_out, 2, 0), (grad_up, 8, 2), (grad_down, 8, 4)):
        loads[first].wait()
        loads[first + 1].wait()
        lax.fori_loop(0, n, f, 0)
        drain()

    def cleared(j, _):
        landed(zero, zsem.at[j])
        return 0

    lax.fori_loop(0, 48, cleared, 0)


def middle(inv, count, tile, blocks, rest, o_parts, tokens, cotangent, vec_params, bias_up, rows=256):
    n, width = tokens.shape
    hidden = bias_up.shape[1]
    row = lambda i, s, c, t: (i, 0)
    fixed = lambda i, s, c, t: (0, 0)
    col = lambda i, s, c, t: (0, i)
    V, DS = pltpu.VMEM, pltpu.SemaphoreType.DMA
    narrow, wide, part = pl.BlockSpec((rows, width), row), pl.BlockSpec((rows, hidden), row), pl.BlockSpec((192, rows), col)
    spec = pltpu.PrefetchScalarGridSpec(
        num_scalar_prefetch=3,
        grid=(n // rows,),
        in_specs=[any_spec()] * 2 + [part] * 4 + [narrow, narrow, pl.BlockSpec((12, width), fixed), pl.BlockSpec((1, hidden), fixed)],
        out_specs=[narrow, narrow] + [part] * 4 + [wide, wide, narrow, narrow, narrow, pl.BlockSpec((width, rows), col),
                   pl.BlockSpec((8, width), fixed), pl.BlockSpec((8, hidden), fixed)],
        scratch_shapes=[V((768, 768), bf), V((768, 3072), bf), V((3072, 768), bf), V((144, 96, 128), bf), DS((144,)), DS((144,))],
    )
    S = jax.ShapeDtypeStruct
    return pl.pallas_call(
        middle_kernel,
        grid_spec=spec,
        out_shape=[S((n, width), bf), S((n, width), f32)] + [S((192, n), bf)] * 4 + [S((n, hidden), bf)] * 2 + [S((n, width), bf)] * 3
        + [S((width, n), bf), S((8, width), f32), S((8, hidden), f32)],
        compiler_params=params(),
        name="projection_and_mlp",
    )(inv, count, tile, blocks, rest, *o_parts, tokens, cotangent, vec_params, bias_up)


def weight_grads_to_slots(pos, outs, block_count, o_t, gb, a2, gz, u, gm):
    V, DS = pltpu.VMEM, pltpu.SemaphoreType.DMA
    arrays = (o_t, gb, a2, gz, u, gm)
    return pl.pallas_call(
        functools.partial(weight_grad_kernel, outs),
        in_specs=[smem_spec()] + [any_spec()] * 6,
        out_specs=[any_spec()] * outs,
        out_shape=[jax.ShapeDtypeStruct((block_count // outs, 288, 128), bf)] * outs,
        scratch_shapes=[V(a.shape, bf) for a in arrays] + [V((16, 288, 128), bf), V((288, 128), bf), DS((6,)), DS((16,)), DS((48,))],
        cost_estimate=pl.CostEstimate(flops=6 * 10**10, bytes_accessed=32 * 10**6, transcendentals=0),
        compiler_params=params(),
        name="mlp_weight_gradients",
    )(pos, *arrays)


def quarters(b0, b1):
    return (b0 * 2 + b1, (1 - b0) * 2 + b1, b0 * 2 + 1 - b1, (1 - b0) * 2 + 1 - b1)


def add_pair_kernel(common, bits_ref, *refs):
    outs = list(refs[16:])
    for p in range(2):
        for side in range(4):
            j = 4 * p + side
            total = (refs[2 * j][...].astype(f32) + refs[2 * j + 1][...].astype(f32)).astype(bf)
            if side == common[p]:
                outs[6][p] = total
            else:
                outs[3 * p + side - (side > common[p])][...] = total


def add_pair(bits, common, keep, came):
    specs = []
    for p in range(2):
        for side in range(4):
            at = lambda i, b, p=p, side=side: (p * 12 + quarters(b[2 * p], b[2 * p + 1])[side] * 3 + i, 0, 0)
            specs += [pl.BlockSpec((4, 288, 128), at)] * 2
    S = jax.ShapeDtypeStruct
    return pl.pallas_call(
        functools.partial(add_pair_kernel, common),
        grid_spec=pltpu.PrefetchScalarGridSpec(
            num_scalar_prefetch=1,
            grid=(3,),
            in_specs=specs,
            out_specs=[pl.BlockSpec((4, 288, 128), lambda i, b: (i, 0, 0))] * 6 + [pl.BlockSpec((2, 4, 288, 128), lambda i, b: (0, i, 0, 0))],
        ),
        out_shape=[S((12, 288, 128), bf)] * 6 + [S((2, 12, 288, 128), bf)],
        compiler_params=params(),
        name="add_gradients_of_cores",
    )(bits, *[keep, came] * 8)


def add_four_kernel(common, bits_ref, *refs):
    outs = refs[7:]
    for p in range(2):
        parts = refs[3 * p : 3 * p + 3]
        for side, q in enumerate(quarters(bits_ref[2 * p], bits_ref[2 * p + 1])):
            for b in range(3):
                total = (sum(r[q * 3 + b].astype(f32) for r in parts) + refs[6][p, q * 3 + b].astype(f32)).astype(bf)
                if side == common[p]:
                    outs[6][p, b] = total
                else:
                    outs[3 * p + side - (side > common[p])][b] = total


def add_four(bits, common, parts):
    S = jax.ShapeDtypeStruct
    return pl.pallas_call(
        functools.partial(add_four_kernel, common),
        in_specs=[smem_spec()] + [vmem_spec()] * 7,
        out_specs=[vmem_spec()] * 7,
        out_shape=[S((3, 288, 128), bf)] * 6 + [S((2, 3, 288, 128), bf)],
        compiler_params=params(),
        name="add_gradients",
    )(bits, *parts)


def add_last_kernel(*refs):
    for p in range(2):
        for b in range(3):
            refs[7][3 * p + b] = (sum(r[b].astype(f32) for r in refs[3 * p : 3 * p + 3]) + refs[6][p, b].astype(f32)).astype(bf)


def add_last(parts):
    return pl.pallas_call(
        add_last_kernel,
        in_specs=[vmem_spec()] * 7,
        out_specs=vmem_spec(),
        out_shape=jax.ShapeDtypeStruct((6, 288, 128), bf),
        compiler_params=params(),
        name="add_last_gradients",
    )(*parts)


def split2(v):
    hi = v.astype(bf)
    return hi, (v - hi.astype(f32)).astype(bf)


def mm3(a, b, dims):
    return mm(a[0], b[0], dims) + (mm(a[0], b[1], dims) + mm(a[1], b[0], dims))


def adam_kernel(odd_ref, from_ref, g_ref, late_ref, m1_ref, m2_ref, l_ref, r_ref, g_out, m1_out, m2_out, u_out, s_out):
    for b in range(g_ref.shape[0]):
        slot = pl.program_id(0) * g_ref.shape[0] + b
        place = from_ref[slot]
        part = jnp.where(place >= 0, late_ref[jnp.maximum(place, 0)].astype(f32), g_ref[b].astype(f32))
        grad = unpack_either(part[:192], part[192:], odd_ref[slot] == 1)
        left, right = split2(l_ref[b]), split2(r_ref[b])
        low = grad.astype(bf)
        rot = mm3(split2(mm(left[0], low, TN) + mm(left[1], low, TN)), right, NN)
        g_out[b] = grad
        first = BETA_ONE * m1_ref[b] + (1.0 - BETA_ONE) * rot
        second = BETA_TWO * m2_ref[b] + (1.0 - BETA_TWO) * rot * rot
        upd = (first * (1.0 / (1.0 - BETA_ONE**STEP))) / (jnp.sqrt(second * (1.0 / (1.0 - BETA_TWO**STEP))) + ADAM_EPS)
        upd = mm3(split2(mm3(left, split2(upd), NN)), right, NT)
        m1_out[b] = first
        m2_out[b] = second
        u_out[b] = upd.astype(bf)
        s_out[b] = lane_sums(upd * upd)


def adam(odd, late_at, grads, late, first, second, left, right):
    n = grads.shape[0]
    g = group_of(n)
    at = lambda i, s, f: (i, 0, 0)
    big = pl.BlockSpec((g, 192, 192), at)
    spec = pltpu.PrefetchScalarGridSpec(
        num_scalar_prefetch=2,
        grid=(n // g,),
        in_specs=[pl.BlockSpec((g, 288, 128), at), pl.BlockSpec(late.shape, lambda i, s, f: (0, 0, 0))] + [big] * 4,
        out_specs=[big] * 4 + [pl.BlockSpec((g, 8, 128), at)],
    )
    return pl.pallas_call(
        adam_kernel,
        grid_spec=spec,
        out_shape=[jax.ShapeDtypeStruct((n, 192, 192), f32)] * 3 + [jax.ShapeDtypeStruct((n, 192, 192), bf), jax.ShapeDtypeStruct((n, 8, 128), f32)],
        compiler_params=params(),
        name="rotated_adam",
    )(odd, late_at, grads, late, first, second, left, right)


def update_kernel(rate_ref, m_ref, u_ref, mo_ref, mc_ref):
    g = m_ref.shape[0]
    for b in range(g):
        new = m_ref[b] - rate_ref[pl.program_id(0) * g + b] * u_ref[b].astype(f32)
        mo_ref[b] = new
        mc_ref[b] = new.astype(bf)


def new_weights(rate, master, update):
    n = master.shape[0]
    g = 8 if n % 8 == 0 else group_of(n)
    big = pl.BlockSpec((g, 192, 192), lambda i, r: (i, 0, 0))
    return pl.pallas_call(
        update_kernel,
        grid_spec=pltpu.PrefetchScalarGridSpec(num_scalar_prefetch=1, grid=(n // g,), in_specs=[big] * 2, out_specs=[big] * 2),
        out_shape=[jax.ShapeDtypeStruct(master.shape, f32), jax.ShapeDtypeStruct(master.shape, bf)],
        compiler_params=params(),
        name="new_weights",
    )(rate, master, update)


def halving_places(slot, core):
    dp, r = slot // 24, slot % 24
    y, z, far, x, s = dp % 2, dp // 2 % 2, dp // 4, r % 6 // 3, r % 3
    portion = r % 12 // 6
    inside = jnp.where(portion == 0, x * 8 + y * 4 + z * 2 + far, y * 8 + z * 4 + x * 2 + far)
    return jnp.where(r // 12 == core, 0, 96) + portion * 48 + inside * 3 + s


def norm_forward(row_data, gain_vec, shift_vec):
    row_mean = jnp.mean(row_data, axis=-1, keepdims=True)
    centred = row_data - row_mean
    inv_std = lax.rsqrt(jnp.mean(centred * centred, axis=-1, keepdims=True) + EPS_NORM)
    normed = centred * inv_std
    return (normed * gain_vec + shift_vec, normed, inv_std)


def norm_back(grad_out, normed, inv_std, gain_vec):
    grad_normed = grad_out * gain_vec
    return inv_std * (
        grad_normed
        - jnp.mean(grad_normed, axis=-1, keepdims=True)
        - normed * jnp.mean(grad_normed * normed, axis=-1, keepdims=True)
    )


def block_plan(counts, slot_count):
    tiles = counts.shape[0]
    per = slot_count // 128
    j = lax.broadcasted_iota(jnp.int32, (tiles, per), 1)
    kept = jnp.clip(counts[:, None] - j * 128, 0, 128).reshape(-1)
    full = (kept > 0).astype(jnp.int32)
    index = jnp.arange(tiles * per, dtype=jnp.int32)
    before = (index[None, :] < index[:, None]).astype(jnp.int32)
    ahead = jnp.sum(before * full[None, :], axis=1)
    live = jnp.sum(full)
    place = jnp.where(full > 0, ahead, live + index - ahead)
    hot = (place[None, :] == index[:, None]).astype(jnp.int32)
    return jnp.sum(hot * index[None, :], axis=1), jnp.sum(hot * kept[None, :], axis=1), live.reshape(1)


def make_body(tuned):
    def body(tokens, cotangent, counts, master, slot_block, groups, first_moment, second_moment, left_basis, right_basis, vec_params, vec_first, vec_second):
        slot_count, width = tokens.shape[1:]
        per_owner = master.shape[0]
        tile = lax.axis_index("tile")
        block_count = slot_block.shape[0]
        first = per_owner // 2 if tuned else per_owner
        index = jnp.arange(block_count, dtype=jnp.int32)
        owner = index // per_owner
        same = (owner[None, :] == owner[:, None]).astype(jnp.int32)
        is_qkv = (slot_block < 48).astype(jnp.int32)
        sooner = same * jnp.where(is_qkv[None, :] == is_qkv[:, None], (index[None, :] < index[:, None]).astype(jnp.int32), is_qkv[None, :])
        rank = jnp.sum(sooner, axis=1)
        place = jnp.where(rank < first, owner * first + rank, block_count // per_owner * first + owner * (per_owner - first) + rank - first)
        most = jnp.max(jnp.sum(same * is_qkv[None, :], axis=1))
        start = lax.axis_index("dp") * per_owner
        mine = lax.dynamic_slice(slot_block, (start,), (per_owner,))
        odd = mine % 2
        local = jnp.arange(per_owner, dtype=jnp.int32)
        at_rank = (lax.dynamic_slice(rank, (start,), (per_owner,))[None, :] == local[:, None]).astype(jnp.int32)
        order = jnp.sum(at_rank * local[None, :], axis=1)
        packed, packed_rest, weight_sq = pack_master(order, jnp.sum(at_rank * odd[None, :], axis=1), master, first)
        own_tokens = tokens.reshape(slot_count, width)
        count_tile = jnp.broadcast_to(counts.reshape(1, 1), (8, 128))
        if tuned:
            blocks, token_all, count_all = gather_all(packed, own_tokens, count_tile)
            packed_rest, blocks = lax.optimization_barrier((packed_rest, blocks))
            blocks_rest = lax.all_gather(packed_rest, "dp", axis=0, tiled=True)
        else:
            blocks = lax.all_gather(packed, "dp", axis=0, tiled=True)
            token_all = lax.all_gather(own_tokens, "tile", axis=0)
            count_all = lax.all_gather(count_tile, "tile", axis=0)
            blocks_rest = packed_rest
        tiles = token_all.shape[0]
        src, cnt, live = block_plan(count_all[:, 0, 0], slot_count)
        is_at = (slot_block[None, :] == index[:, None]).astype(jnp.int32)
        inverse = jnp.sum(is_at * index[None, :], axis=1)
        places = jnp.sum(is_at * place[None, :], axis=1)
        own_block = jnp.arange(12, dtype=jnp.int32) // 3 * 12 + jnp.arange(12, dtype=jnp.int32) % 3 * 4 + tile
        own_at = jnp.sum((slot_block[None, :] == own_block[:, None]).astype(jnp.int32) * place[None, :], axis=1)
        if tuned:
            qkv_blocks = lax.cond(
                most <= first,
                lambda: pick(own_at, blocks, packed_rest),
                lambda: pick(own_at, blocks, lax.all_gather(packed_rest, "dp", axis=0, tiled=True)),
            )
        else:
            qkv_blocks = pick(own_at, blocks, blocks_rest)
        tile_one = tile.astype(jnp.int32).reshape(1)
        own = width // tiles
        bias = lambda row: lax.dynamic_slice(vec_params[row : row + 1], (0, tile * own), (1, own))
        a1, qt, k, kt, v, vt, w_qkv, lengths = qkv_forward(
            src, cnt, tile_one % 2, token_all.reshape(-1, width), qkv_blocks, vec_params[0:1], vec_params[1:2], bias(4), bias(5)
        )
        mild = jnp.sqrt(jnp.max(lengths[:, 0, 0])) * jnp.sqrt(jnp.max(lengths[:, 1, 0])) * EXP2 <= 60.0
        live = jnp.concatenate([live, mild.astype(jnp.int32).reshape(1)])
        ot, qb, p, rt = attend(live, k, qt, vt)

        def shift(parts):
            return [parts[0]] + [lax.ppermute(parts[j], "tile", [(s, (s + j) % tiles) for s in range(tiles)]) for j in range(1, tiles)]

        o_parts = shift(spread(src, live, tile_one, ot, tiles))
        output, grad_resid, *rest = middle(
            places, counts.reshape(1), tile_one, blocks, blocks_rest, o_parts, own_tokens, cotangent.reshape(slot_count, width), vec_params, vec_params[8:].reshape(1, -1)
        )
        go_parts, (u, gz, a2, gm, gb, o_t, sums, up_sums) = rest[:tiles], rest[tiles:]
        go_parts = shift(go_parts)
        back = lambda first, heads, dt: list(attend_back(first, heads, live, p, k, kt, v, qb, dt))
        if tuned:
            dp = lax.axis_index("dp")
            bit = {"x": tile // 2, "y": dp % 2, "z": dp // 2 % 2, "far": dp // 4}
            mask = {"x": 2, "y": 4, "z": 8, "far": 16}

            def flip(array, *names):
                change = sum(mask[name] for name in names)
                return lax.ppermute(array, ("dp", "tile"), [(s, s ^ change) for s in range(32)])

            def three(sums, pairs, common):
                out = []
                for p, (a, b) in enumerate(pairs):
                    ways = [(), (a,), (b,), (a, b)]
                    del ways[common[p]]
                    out += [flip(sums[3 * p + j], *way) if way else sums[3 * p + j] for j, way in enumerate(ways)]
                return out + [flip(sums[6], pairs[0][common[0] - 1])]

            def bits_of(pairs):
                return jnp.stack([bit[name] for pair in pairs for name in pair]).astype(jnp.int32)

            first, second = [("x", "y"), ("y", "z")], [("z", "far"), ("x", "far")]
            keep, send = weight_grads_to_slots(halving_places(inverse, tile % 2), 2, block_count, o_t, gb, a2, gz, u, gm)
            send, go_parts = lax.optimization_barrier((send, go_parts))
            came = lax.ppermute(send, "tile", [(s, s ^ 1) for s in range(4)])
            dt = collect(src, live, tile_one, go_parts, ot, rt)
            dt, came = lax.optimization_barrier((dt, came))
            sums_one = add_pair(bits_of(first), (2, 1), keep, came)
            dt, sums_one = lax.optimization_barrier((dt, sums_one))
            parts = three(sums_one, first, (2, 1))
            head_grads = back(0, 2, dt)
            head_grads[0], parts = lax.optimization_barrier((head_grads[0], parts))
            sums_two = add_four(bits_of(second), (2, 2), parts)
            dt, sums_two = lax.optimization_barrier((dt, sums_two))
            parts = three(sums_two, second, (2, 2))
            head_grads += back(2, 1, dt)
            head_grads[3], parts = lax.optimization_barrier((head_grads[3], parts))
            mine_early = add_last(parts)
            head_grads[3], mine_early = lax.optimization_barrier((head_grads[3], mine_early))
            over_early = flip(mine_early, "x")
        else:
            slots = weight_grads_to_slots(inverse, 1, block_count, o_t, gb, a2, gz, u, gm)[0]
            dt = collect(src, live, tile_one, go_parts, ot, rt)
            head_grads = back(0, 3, dt)
        g_one, g_two, gw_qkv, qkv_sums, norm_sums = qkv_backward(
            src, live, tile_one % 2, token_all.reshape(-1, width), vec_params[0:1], a1, w_qkv, head_grads, tiles, slot_count * 3 // 8
        )
        if tuned:
            g_one, over_early = lax.optimization_barrier((g_one, over_early))
        zero = jnp.zeros((width,), f32)
        at_own = lambda s: lax.dynamic_update_slice(zero, s, (tile * own,))
        vector_part = jnp.concatenate(
            [norm_sums[0:2], sums[0:2], at_own(qkv_sums[0, :own])[None], at_own(qkv_sums[0, 2 * own :])[None], sums[2:4], up_sums[0].reshape(-1, width)], axis=0
        )
        if tuned:
            early, late, vector_grads = last_sums(gw_qkv, mine_early, over_early, vector_part)
            g_two, early = lax.optimization_barrier((g_two, early))
        else:
            early = lax.psum(lax.psum_scatter(slots.astype(f32), "dp", scatter_dimension=0, tiled=True), "tile").astype(bf)
            late = lax.all_gather(lax.psum(gw_qkv.astype(f32), "dp").astype(bf), "tile", axis=0, tiled=True)
            vector_grads = lax.psum(vector_part, ("dp", "tile"))
        g1 = jnp.concatenate([lax.psum_scatter(part, "tile", scatter_dimension=0, tiled=False) for part in (g_one, g_two)], axis=0)
        row_input = own_tokens.astype(f32)
        _, normed_one, inv_std_one = norm_forward(row_input, vec_params[0], vec_params[1])
        input_grad = grad_resid + norm_back(g1.astype(f32), normed_one, inv_std_one, vec_params[0])
        late_at = jnp.where(mine < 48, mine % 4 * 12 + mine // 12 * 3 + mine % 12 // 4, -1)
        weight_grads, first_out, second_out, update, update_sq = adam(odd, late_at, early, late, first_moment, second_moment, left_basis, right_basis)
        group_hot = (groups[:, None] == jnp.arange(128, dtype=jnp.int32)[None, :]).astype(f32)
        weight_part = jnp.sum(jnp.sum(at_rank.astype(f32)[:, :, None] * group_hot[None], axis=1) * jnp.sum(weight_sq[:, 0], axis=1)[:, None], axis=0)
        group_part = jnp.pad(jnp.stack([weight_part, jnp.sum(group_hot * jnp.sum(update_sq[:, 0], axis=1)[:, None], axis=0)]), ((0, 6), (0, 0)))
        group_both = group_sum(group_part, block_count // per_owner)
        own_both = jnp.sum(group_hot[None] * group_both[:2, None, :], axis=2)
        rate = RATE_BLOCK * jnp.sqrt(own_both[0]) / (jnp.sqrt(own_both[1]) + 1e-06)
        master_out, master_copy = new_weights(rate, master, update)
        vec_first_out = BETA_ONE * vec_first + (1.0 - BETA_ONE) * vector_grads
        vec_second_out = BETA_TWO * vec_second + (1.0 - BETA_TWO) * vector_grads * vector_grads
        vec_update = (vec_first_out / (1.0 - BETA_ONE**STEP)) / (jnp.sqrt(vec_second_out / (1.0 - BETA_TWO**STEP)) + ADAM_EPS)
        return (
            output.reshape(1, slot_count, width),
            input_grad.reshape(1, slot_count, width),
            weight_grads,
            first_out,
            second_out,
            master_out,
            master_copy,
            vector_grads,
            vec_first_out,
            vec_second_out,
            vec_params - RATE_VECTOR * vec_update,
        )

    return body


def solution(mesh):
    tuned = (mesh.shape["dp"], mesh.shape["tile"]) == (8, 4)
    rows, blocks = P("dp", "tile", None), P("dp", None, None)
    return jax.shard_map(
        make_body(tuned),
        mesh=mesh,
        in_specs=(rows, rows, P("dp", "tile"), blocks, P(), P("dp"), blocks, blocks, blocks, blocks, P(), P(), P()),
        out_specs=(rows, rows, blocks, blocks, blocks, blocks, blocks, P(), P(), P(), P()),
        check_vma=False,
    )
```

```python
import functools
import math

import jax
import jax.numpy as jnp
from jax import lax
from jax.experimental import pallas as pl
from jax.experimental.pallas import tpu as pltpu
from jax.sharding import PartitionSpec as P

f32 = jnp.float32
bf = jnp.bfloat16
MESH = pl.DeviceIdType.MESH

def where_am_i():
    dp=lax.axis_index("dp"); t=lax.axis_index("tile")
    return dp//2, dp%2, t//2, t%2

def dev(z,y,x,c):
    return (z*2+y, x*2+c)

def rcopy(src,dst,ss,rs,to):
    return pltpu.make_async_remote_copy(src_ref=src,dst_ref=dst,send_sem=ss,recv_sem=rs,device_id=to,device_id_type=MESH)

def gather_kernel(own_w,own_tok,own_cnt,all_w,all_tok,all_cnt,zs,zr,ys,yr,cs,cr,ts,tr,ns,nr,ls):
    z,y,x,c=where_am_i()
    per=own_w.shape[0]
    half=per//2
    def piece(shard,cc): return all_w.at[pl.ds(shard*per+cc*half,half)]
    own=own_w.at[pl.ds(c*half,half)]
    me=z*2+y
    core=dev(z,y,x,1-c); across=dev(z,y,1-x,c); beside=dev(z,1-y,x,c)
    up=dev(jnp.minimum(z+1,3),y,x,c); down=dev(jnp.maximum(z-1,0),y,x,c)
    def src(shard,first): return own if first else piece(shard,c)
    def z_copy(zz,first,go_up):
        shard=zz*2+y
        d=(z-zz) if go_up else (zz-z)
        k=0 if go_up else 1
        return rcopy(src(shard,first),piece(shard,c),zs.at[k,d],zr.at[k,d],up if go_up else down)
    def z_arrival(zz,k,dist):
        r=piece(zz*2+y,c)
        return rcopy(r,r,zs.at[k,dist-1],zr.at[k,dist-1],up)
    def y_copy(zz,first):
        shard=zz*2+y
        return rcopy(src(shard,first),piece(shard,c),ys.at[zz],yr.at[zz],beside)
    def y_arrival(zz):
        r=piece(zz*2+1-y,c)
        return rcopy(r,r,ys.at[zz],yr.at[zz],beside)
    def c_copy(shard): return rcopy(piece(shard,c),piece(shard,c),cs.at[shard],cr.at[shard],core)
    def c_arrival(shard): return rcopy(piece(shard,1-c),piece(shard,1-c),cs.at[shard],cr.at[shard],core)
    tile=x*2+c
    tok_x=rcopy(own_tok,all_tok.at[tile],ts.at[0],tr.at[0],across)
    tok_c=rcopy(own_tok,all_tok.at[tile],ts.at[1],tr.at[1],core)
    far=all_tok.at[(1-x)*2+c]
    tok_f=rcopy(far,far,ts.at[2],tr.at[2],core)
    near=all_tok.at[x*2+1-c]
    diag=all_tok.at[(1-x)*2+1-c]
    cnts=[rcopy(own_cnt,all_cnt.at[tile],ns.at[i],nr.at[i],to) for i,to in enumerate((across,core,dev(z,y,1-x,1-c)))]
    cnt_in=[rcopy(r,r,ns.at[i],nr.at[i],core) for i,r in enumerate((all_cnt.at[(1-x)*2+c],all_cnt.at[x*2+1-c],all_cnt.at[(1-x)*2+1-c]))]
    local=(pltpu.make_async_copy(own_w,all_w.at[pl.ds(me*per,per)],ls.at[0]),
           pltpu.make_async_copy(own_tok,all_tok.at[tile],ls.at[1]),pltpu.make_async_copy(own_cnt,all_cnt.at[tile],ls.at[2]))
    @pl.when(z<3)
    def _(): z_copy(z,True,True).start()
    @pl.when(z>0)
    def _(): z_copy(z,True,False).start()
    y_copy(z,True).start(); tok_x.start(); tok_c.start()
    for cp in cnts: cp.start()
    for cp in local: cp.start()
    def from_line(k,dist):
        zz=z-dist if k==0 else z+dist
        there=(zz>=0) if k==0 else (zz<=3)
        @pl.when(there)
        def _():
            z_arrival(zz,k,dist).wait_recv()
            @pl.when((z<3) if k==0 else (z>0))
            def _(): z_copy(zz,False,k==0).start()
            y_copy(zz,False).start(); c_copy(zz*2+y).start()
    def from_beside(zz):
        y_arrival(zz).wait_recv(); c_copy(zz*2+1-y).start()
    def guarded(f,dist):
        @pl.when(z-dist>=0)
        def _(): f(z-dist)
        @pl.when(z+dist<=3)
        def _(): f(z+dist)
    from_line(0,1); from_line(1,1)
    from_beside(z)
    from_line(0,2); from_line(1,2)
    guarded(from_beside,1)
    from_line(0,3); from_line(1,3)
    tok_x.wait_recv(); tok_f.start()
    guarded(from_beside,2)
    guarded(from_beside,3)
    def drain(s,_):
        @pl.when(s!=me)
        def _():
            c_arrival(s).wait_recv(); c_copy(s).wait_send()
        return 0
    lax.fori_loop(0,8,drain,0)
    def drain_y(zz,_):
        y_copy(zz,False).wait_send(); return 0
    lax.fori_loop(0,4,drain_y,0)
    for dist in range(4):
        @pl.when(jnp.logical_and(z<3,z-dist>=0))
        def _(): z_copy(z-dist,False,True).wait_send()
        @pl.when(jnp.logical_and(z>0,z+dist<=3))
        def _(): z_copy(z+dist,False,False).wait_send()
    rcopy(near,near,ts.at[1],tr.at[1],core).wait_recv()
    rcopy(diag,diag,ts.at[2],tr.at[2],core).wait_recv()
    tok_x.wait_send(); tok_c.wait_send(); tok_f.wait_send()
    for cp in cnts: cp.wait_send()
    for cp in cnt_in: cp.wait_recv()
    for cp in local: cp.wait()

def gather_all(own_w,own_tok,own_cnt):
    DS=pltpu.SemaphoreType.DMA
    hbm=pl.BlockSpec(memory_space=pl.ANY)
    return pl.pallas_call(gather_kernel,
        out_shape=[jax.ShapeDtypeStruct((8*own_w.shape[0],)+own_w.shape[1:],bf),jax.ShapeDtypeStruct((4,)+own_tok.shape,bf),jax.ShapeDtypeStruct((4,)+own_cnt.shape,own_cnt.dtype)],
        in_specs=[pl.BlockSpec(memory_space=pltpu.VMEM)]*3,out_specs=[hbm]*3,
        scratch_shapes=[DS((2,4)),DS((2,4)),DS((4,)),DS((4,)),DS((8,)),DS((8,)),DS((3,)),DS((3,)),DS((3,)),DS((3,)),DS((3,))],
        compiler_params=pltpu.CompilerParams(has_side_effects=True,vmem_limit_bytes=60<<20),name="gather_weights_tokens")(own_w,own_tok,own_cnt)

def group_sum_kernel(g_ref,o_ref,gd,gs,gr):
    dp=lax.axis_index("dp"); t=lax.axis_index("tile")
    nd=gd.shape[0]
    def copy(k):
        return rcopy(gd.at[dp],gd.at[dp],gs.at[k],gr.at[k],((dp+k)%nd,t))
    def arrive(k):
        q=(dp-k+nd)%nd
        return rcopy(gd.at[q],gd.at[q],gs.at[k],gr.at[k],(q,t))
    def loop(f):
        def s(k,_):
            f(k); return 0
        lax.fori_loop(1,nd,s,0)
    gd[dp]=g_ref[...]
    loop(lambda k: copy(k).start())
    loop(lambda k: arrive(k).wait_recv())
    acc=gd[0]
    for i in range(1,nd): acc=acc+gd[i]
    o_ref[...]=acc
    loop(lambda k: copy(k).wait_send())

def group_sum(g,nd):
    DS=pltpu.SemaphoreType.DMA
    vm=pl.BlockSpec(memory_space=pltpu.VMEM)
    return pl.pallas_call(group_sum_kernel,out_shape=jax.ShapeDtypeStruct(g.shape,f32),in_specs=[vm],out_specs=vm,
        scratch_shapes=[pltpu.VMEM((nd,)+g.shape,f32),DS((nd,)),DS((nd,))],
        compiler_params=pltpu.CompilerParams(has_side_effects=True,vmem_limit_bytes=60<<20),name="sum_groups")(g)

def last_sums_kernel(l_ref,mine,over,v_ref,early,late,vo_ref,yb,zb,own,vb,vd,y1s,y1r,z2s,z2r,z3s,z3r,y4s,y4r,xs,xr,cs,cr,fs,fr,es,er,ts,tr,ds,dr,us,ur):
    z,y,x,c=where_am_i()
    dp=lax.axis_index("dp"); t=lax.axis_index("tile")
    core=dev(z,y,x,1-c); across=dev(z,y,1-x,c); beside=dev(z,1-y,x,c)
    def loop(f,first,n):
        def s(k,_):
            f(k); return 0
        lax.fori_loop(first,n,s,0)
    at=lambda i: pl.ds(i*3,3)
    def y1(k):
        q=(z+k)%4
        return rcopy(l_ref.at[at((1-y)*4+q)],yb.at[q],y1s.at[q],y1r.at[q],beside)
    def z2(k):
        q=(z+k)%4
        return rcopy(own.at[q],zb.at[z],z2s.at[k],z2r.at[k],dev(q,y,x,c))
    def z2_arrive(k):
        q=(z-k+4)%4
        return rcopy(zb.at[q],zb.at[q],z2s.at[k],z2r.at[k],dev(q,y,x,c))
    for k in (2,1,3,0): y1(k).start()
    def t1(k): return rcopy(v_ref.at[(t+k)%4],vb.at[t],ts.at[k],tr.at[k],(dp,(t+k)%4))
    def t1_arrive(k):
        q=(t-k+4)%4
        return rcopy(vb.at[q],vb.at[q],ts.at[k],tr.at[k],(dp,q))
    def d_copy(k): return rcopy(vd.at[dp],vd.at[dp],ds.at[k],dr.at[k],((dp+k)%8,t))
    def d_arrive(k):
        q=(dp-k+8)%8
        return rcopy(vd.at[q],vd.at[q],ds.at[k],dr.at[k],(q,t))
    def t2(k): return rcopy(vo_ref.at[t],vo_ref.at[t],us.at[k],ur.at[k],(dp,(t+k)%4))
    def t2_arrive(k):
        q=(t-k+4)%4
        return rcopy(vo_ref.at[q],vo_ref.at[q],us.at[k],ur.at[k],(dp,q))
    loop(lambda k: t1(k).start(),1,4)
    vb[t]=v_ref[t]
    def place(xx,cc,p): return early.at[pl.ds(cc*12+p*6+xx*3,3)]
    for p in range(2):
        early[pl.ds(c*12+p*6+x*3,3)]=mine[pl.ds(p*3,3)]
        early[pl.ds(c*12+p*6+(1-x)*3,3)]=over[pl.ds(p*3,3)]
    def e_copy(i,p): return rcopy(place(i,c,p),place(i,c,p),es.at[i,p],er.at[i,p],core)
    def e_arrive(i,p): return rcopy(place(i,1-c,p),place(i,1-c,p),es.at[i,p],er.at[i,p],core)
    for p in range(2):
        e_copy(0,p).start(); e_copy(1,p).start()
    loop(lambda k: t1_arrive(k).wait_recv(),1,4)
    vd[dp]=vb[0]+vb[1]+vb[2]+vb[3]
    loop(lambda k: d_copy(k).start(),1,8)
    for k in (2,1,3,0):
        q=(z+k)%4
        y1(k).wait_recv()
        for i in range(3): own[q,i]=(l_ref[(y*4+q)*3+i].astype(f32)+yb[q,i].astype(f32)).astype(bf)
        if k: z2(k).start()
    zb[z]=own[z]
    loop(lambda k: z2_arrive(k).wait_recv(),1,4)
    for i in range(3):
        late[t,(y*4+z)*3+i]=(zb[0,i].astype(f32)+zb[1,i].astype(f32)+zb[2,i].astype(f32)+zb[3,i].astype(f32)).astype(bf)
    def piece(tt,yy,zz): return late.at[tt,at(yy*4+zz)]
    def z3(k): return rcopy(piece(t,y,z),piece(t,y,z),z3s.at[k],z3r.at[k],dev((z+k)%4,y,x,c))
    def z3_arrive(k):
        q=(z-k+4)%4
        return rcopy(piece(t,y,q),piece(t,y,q),z3s.at[k],z3r.at[k],dev(q,y,x,c))
    def y4(q): return rcopy(piece(t,y,q),piece(t,y,q),y4s.at[q],y4r.at[q],beside)
    def y4_arrive(q): return rcopy(piece(t,1-y,q),piece(t,1-y,q),y4s.at[q],y4r.at[q],beside)
    far=(1-x)*2+c
    def x_copy(yy,q): return rcopy(piece(t,yy,q),piece(t,yy,q),xs.at[yy*4+q],xr.at[yy*4+q],across)
    def x_arrive(yy,q): return rcopy(piece(far,yy,q),piece(far,yy,q),xs.at[yy*4+q],xr.at[yy*4+q],across)
    def c_copy(yy,q): return rcopy(piece(t,yy,q),piece(t,yy,q),cs.at[yy*4+q],cr.at[yy*4+q],core)
    def c_arrive(yy,q): return rcopy(piece(x*2+1-c,yy,q),piece(x*2+1-c,yy,q),cs.at[yy*4+q],cr.at[yy*4+q],core)
    def f_copy(yy,q): return rcopy(piece(far,yy,q),piece(far,yy,q),fs.at[yy*4+q],fr.at[yy*4+q],core)
    def f_arrive(yy,q):
        r=piece((1-x)*2+1-c,yy,q)
        return rcopy(r,r,fs.at[yy*4+q],fr.at[yy*4+q],core)
    for k in (1,3,2): z3(k).start()
    y4(z).start(); x_copy(y,z).start(); c_copy(y,z).start()
    def passed_on(k):
        q=(z-k+4)%4
        if k:
            z3_arrive(k).wait_recv()
            y4(q).start(); x_copy(y,q).start(); c_copy(y,q).start()
        y4_arrive(q).wait_recv()
        x_copy(1-y,q).start(); c_copy(1-y,q).start()
    for k in (0,1,3,2): passed_on(k)
    loop(lambda k: d_arrive(k).wait_recv(),1,8)
    acc=vd[0]
    for i in range(1,8): acc=acc+vd[i]
    vo_ref[t]=acc
    loop(lambda k: t2(k).start(),1,4)
    for k in (0,1,3,2):
        q=(z-k+4)%4
        for yy in (y,1-y):
            x_arrive(yy,q).wait_recv(); f_copy(yy,q).start()
    def drain(q):
        for yy in range(2):
            c_arrive(yy,q).wait_recv(); f_arrive(yy,q).wait_recv()
            x_copy(yy,q).wait_send(); c_copy(yy,q).wait_send(); f_copy(yy,q).wait_send()
        y4(q).wait_send()
        y1(q).wait_send()
    loop(drain,0,4)
    def sent(k):
        t2_arrive(k).wait_recv()
        z2(k).wait_send(); z3(k).wait_send(); t1(k).wait_send(); t2(k).wait_send()
    loop(sent,1,4)
    loop(lambda k: d_copy(k).wait_send(),1,8)
    for p in range(2):
        for i in range(2):
            e_arrive(i,p).wait_recv(); e_copy(i,p).wait_send()

def last_sums(own,mine,over,v):
    DS=pltpu.SemaphoreType.DMA
    vm=pl.BlockSpec(memory_space=pltpu.VMEM)
    V=pltpu.VMEM
    S=jax.ShapeDtypeStruct
    rows=(3,v.shape[1])
    early,late,total=pl.pallas_call(last_sums_kernel,out_shape=[S((24,288,128),bf),S((4,24,144,128),bf),S((4,)+rows,f32)],in_specs=[vm]*4,out_specs=[vm]*3,
        scratch_shapes=[V((4,3,144,128),bf)]*3+[V((4,)+rows,f32),V((8,)+rows,f32)]+[DS((4,))]*8+[DS((8,))]*6+[DS((2,2))]*2+[DS((4,))]*2+[DS((8,))]*2+[DS((4,))]*2,
        cost_estimate=pl.CostEstimate(flops=10**7,bytes_accessed=150*10**6,transcendentals=0),
        compiler_params=pltpu.CompilerParams(has_side_effects=True,vmem_limit_bytes=60<<20),name="last_gradient_sums")(own.reshape(24,144,128),mine,over,v.reshape((4,)+rows))
    return early,late.reshape(48,288,128),total.reshape(v.shape)


H = 12
STEP = 10
EPS_NORM = 1e-06
BETA_ONE = 0.5
BETA_TWO = 0.5
ADAM_EPS = 1e-08
RATE_BLOCK = 0.3
RATE_VECTOR = 0.2
NEG_RAW = -8.0e9
HEAD = 64
SCALE = 1.0 / math.sqrt(HEAD)
EXP2 = SCALE * math.log2(math.e)
NN = (((1,), (0,)), ((), ()))
NT = (((1,), (1,)), ((), ()))
TN = (((0,), (0,)), ((), ()))


def mm(a, b, dims=NN):
    return lax.dot_general(a, b, dims, preferred_element_type=f32)


def column_sum(v):
    return jnp.sum(v, axis=0, keepdims=True)


def vmem_spec():
    return pl.BlockSpec(memory_space=pltpu.VMEM)


def smem_spec():
    return pl.BlockSpec(memory_space=pltpu.SMEM)


def any_spec():
    return pl.BlockSpec(memory_space=pl.ANY)


def params(mib=60):
    return pltpu.CompilerParams(vmem_limit_bytes=mib << 20)


def pack(block, odd):
    half = block.shape[0] // 2
    if odd:
        return block[:, 64:], jnp.concatenate([block[half:, :64], block[:half, :64]], axis=1)
    return block[:, :128], jnp.concatenate([block[:half, 128:], block[half:, 128:]], axis=1)


def unpack(top, tail, odd):
    if odd:
        return jnp.concatenate([jnp.concatenate([tail[:, 64:], tail[:, :64]], axis=0), top], axis=1)
    return jnp.concatenate([top, jnp.concatenate([tail[:, :64], tail[:, 64:]], axis=0)], axis=1)


def unpack_either(top, tail, odd):
    return jnp.where(odd, unpack(top, tail, 1), unpack(top, tail, 0))


def lane_sums(v):
    s = column_sum(v)
    return jnp.broadcast_to(s[:, :128] + jnp.concatenate([s[:, 128:], jnp.zeros((1, 64), f32)], axis=1), (8, 128))


def by_parity(value, run):
    for odd in (0, 1):
        pl.when(value == odd)(functools.partial(run, odd))


def turn(v):
    return jnp.concatenate([v[:, 64:], v[:, :64]], axis=1)


def group_of(n):
    return 4 if n % 4 == 0 else 3 if n % 3 == 0 else 1


def pack_kernel(early, order_ref, odd_ref, *refs):
    g = len(refs) - 3
    p_ref, late_ref, s_ref = refs[g:]
    i = pl.program_id(0)
    for b in range(g):
        m = refs[b][0]

        def place(odd, m=m, b=b):
            top, tail = pack(m, odd)
            for ref, here in ((p_ref, i < early), (late_ref, i >= early)):

                @pl.when(here)
                def _():
                    ref[b, :192] = top.astype(bf)
                    ref[b, 192:] = tail.astype(bf)

        by_parity(odd_ref[i * g + b], place)
        s_ref[b] = lane_sums(m * m)


def pack_master(order, odd, master, first):
    n = master.shape[0]
    g = 6 if first % 6 == 0 and n % 6 == 0 else group_of(first)
    early = first // g
    rest = max(n - first, g)
    spec = pltpu.PrefetchScalarGridSpec(
        num_scalar_prefetch=2,
        grid=(n // g,),
        in_specs=[pl.BlockSpec((1, 192, 192), lambda i, s, o, b=b: (s[i * g + b], 0, 0)) for b in range(g)],
        out_specs=[
            pl.BlockSpec((g, 288, 128), lambda i, s, o: (jnp.minimum(i, early - 1), 0, 0)),
            pl.BlockSpec((g, 288, 128), lambda i, s, o: (jnp.maximum(i - early, 0), 0, 0)),
            pl.BlockSpec((g, 8, 128), lambda i, s, o: (i, 0, 0)),
        ],
    )
    return pl.pallas_call(
        functools.partial(pack_kernel, early),
        grid_spec=spec,
        out_shape=[jax.ShapeDtypeStruct((first, 288, 128), bf), jax.ShapeDtypeStruct((rest, 288, 128), bf), jax.ShapeDtypeStruct((n, 8, 128), f32)],
        compiler_params=params(),
        name="pack_master",
    )(order, odd, *[master] * g)


def pick_kernel(at_ref, first_ref, rest_ref, o_ref, sems):
    split = first_ref.shape[0]
    for j in range(12):

        @pl.when(at_ref[j] < split)
        def _():
            pltpu.make_async_copy(first_ref.at[at_ref[j]], o_ref.at[j], sems.at[j]).start()

        @pl.when(at_ref[j] >= split)
        def _():
            pltpu.make_async_copy(rest_ref.at[at_ref[j] - split], o_ref.at[j], sems.at[j]).start()

    for j in range(12):
        pltpu.make_async_copy(first_ref.at[0], o_ref.at[j], sems.at[j]).wait()


def pick(at, first, rest):
    return pl.pallas_call(
        pick_kernel,
        in_specs=[smem_spec(), any_spec(), any_spec()],
        out_specs=vmem_spec(),
        out_shape=jax.ShapeDtypeStruct((12, 288, 128), bf),
        scratch_shapes=[pltpu.SemaphoreType.DMA((12,))],
        compiler_params=params(),
        name="pick_qkv_blocks",
    )(at, first, rest)


def qkv_kernel(src_ref, cnt_ref, at_ref, x0, x1, x2, x3, blk_ref, gain_ref, shift_ref, bq_ref, bv_ref, a_ref, qt_ref, k_ref, kt_ref, v_ref, vt_ref, w_ref, st_ref):
    i = pl.program_id(0)

    @pl.when(i == 0)
    def _():
        def join(odd):
            for r in range(4):
                parts = []
                for c in range(3):
                    p = blk_ref[r * 3 + c].astype(f32)
                    parts.append(unpack(p[:192], p[192:], odd))
                w_ref[r * 192 : (r + 1) * 192, :] = jnp.concatenate(parts, axis=1).astype(bf)

        by_parity(at_ref[0], join)

    x = jnp.concatenate([r[...] for r in (x0, x1, x2, x3)], axis=0).astype(f32)
    mean = jnp.mean(x, axis=-1, keepdims=True)
    cen = x - mean
    inv_std = lax.rsqrt(jnp.mean(cen * cen, axis=-1, keepdims=True) + EPS_NORM)
    a = (cen * inv_std * gain_ref[...] + shift_ref[...]).astype(bf)
    a_ref[...] = a
    qkv = mm(a, w_ref[...])
    q = (qkv[:, :192] + bq_ref[...]).astype(bf).astype(f32)
    k = qkv[:, 192:384].astype(bf).astype(f32)
    v = (qkv[:, 384:] + bv_ref[...]).astype(bf).astype(f32)
    row = lax.broadcasted_iota(jnp.int32, (128, 64), 0)
    lane = lax.broadcasted_iota(jnp.int32, (512, 64), 1)
    masked = jnp.concatenate(
        [jnp.where(row < cnt_ref[4 * i + b], 0.0, NEG_RAW) for b in range(4)], axis=0
    )
    ones = jnp.where(lane < 4, 1.0, 0.0)
    k_tail = jnp.where(lane == 0, masked, ones)
    v_tail = jnp.where(lane < 3, 1.0, 0.0)
    sub = lax.broadcasted_iota(jnp.int32, (64, 512), 0)
    t_tail = jnp.where(sub < 1, 1.0, 0.0)
    qt, kt, vt = q.T, k.T, v.T
    longest = lambda a: jnp.max(jnp.concatenate([column_sum(a[h * 64 : (h + 1) * 64] ** 2) for h in range(3)], axis=0))
    st_ref[0] = jnp.where(lax.broadcasted_iota(jnp.int32, (8, 128), 0) == 0, longest(qt), longest(kt))
    for h in range(3):
        s = slice(h * 64, (h + 1) * 64)
        k_ref[h] = jnp.concatenate([k[:, s], k_tail], axis=1).astype(bf)
        v_ref[h] = jnp.concatenate([v[:, s], v_tail], axis=1).astype(bf)
        qt_ref[h] = jnp.concatenate([qt[s], t_tail], axis=0).astype(bf)
        kt_ref[h] = kt[s].astype(bf)
        vt_ref[h] = jnp.concatenate([vt[s], t_tail[:16]], axis=0).astype(bf)


def qkv_forward(src, cnt, odd, tokens, blocks, gain, shift, bq, bv):
    n = tokens.shape[0]
    rows = [pl.BlockSpec((128, 768), lambda i, s, c, o, k=k: (s[4 * i + k], 0)) for k in range(4)]
    row = lambda i, s, c, o: (0, 0)
    spec = pltpu.PrefetchScalarGridSpec(
        num_scalar_prefetch=3,
        grid=(n // 512,),
        in_specs=rows
        + [pl.BlockSpec((12, 288, 128), lambda i, s, c, o: (0, 0, 0)), pl.BlockSpec((1, 768), row), pl.BlockSpec((1, 768), row), pl.BlockSpec((1, 192), row), pl.BlockSpec((1, 192), row)],
        out_specs=[
            pl.BlockSpec((512, 768), lambda i, s, c, o: (i, 0)),
            pl.BlockSpec((3, 128, 512), lambda i, s, c, o: (0, 0, i)),
            pl.BlockSpec((3, 512, 128), lambda i, s, c, o: (0, i, 0)),
            pl.BlockSpec((3, 64, 512), lambda i, s, c, o: (0, 0, i)),
            pl.BlockSpec((3, 512, 128), lambda i, s, c, o: (0, i, 0)),
            pl.BlockSpec((3, 80, 512), lambda i, s, c, o: (0, 0, i)),
            pl.BlockSpec((768, 576), row),
            pl.BlockSpec((1, 8, 128), lambda i, s, c, o: (i, 0, 0)),
        ],
    )
    shapes = [(n, 768), (3, 128, n), (3, n, 128), (3, 64, n), (3, n, 128), (3, 80, n), (768, 576)]
    return pl.pallas_call(
        qkv_kernel,
        grid_spec=spec,
        out_shape=[jax.ShapeDtypeStruct(s, bf) for s in shapes] + [jax.ShapeDtypeStruct((n // 512, 8, 128), f32)],
        compiler_params=params(),
        name="norm_and_qkv",
    )(src, cnt, odd, tokens, tokens, tokens, tokens, blocks, gain, shift, bq, bv)


def split3(v):
    a = v.astype(bf).astype(f32)
    b = (v - a).astype(bf).astype(f32)
    return a, b, v - a - b


def in_steps(units, sizes, body, carry):
    at = 0
    for size in sizes:
        count = (units - at) // size
        carry = lax.fori_loop(0, count, lambda i, c, at=at, size=size: body(at + i * size, size, c), carry)
        at = at + count * size
    return carry


def attend_kernel(bq, n_ref, k_ref, qt_ref, vt_ref, ot_ref, qb_ref, p_ref, rt_ref):
    live = n_ref[0]
    qi = pl.program_id(1)
    pairs = (live + 7) // 8 * 4

    def finish(top, acc):
        total = acc[64:65]
        ot_ref[0] = acc[:64] / total
        rt_ref[0] = 1.0 / total
        a, b, c = split3((top + jnp.log2(total)) * (-1.0 / EXP2))
        row = lax.broadcasted_iota(jnp.int32, (64, bq), 0)
        tail = jnp.where(row == 0, 1.0, jnp.where(row == 1, a, jnp.where(row == 2, b, jnp.where(row == 3, c, 0.0))))
        qb_ref[0, :64] = qt_ref[0, :64]
        qb_ref[0, 64:] = tail.astype(bf)

    def keys(u, size):
        return pl.ds(pl.multiple_of(u * 256, 256), size * 256)

    @pl.when(jnp.logical_and(qi * bq < live * 128, n_ref[1] == 1))
    def _():
        qt = qt_ref[0]

        def body(u, size, acc):
            step = min(size, 2)
            for part in range(0, size, step):
                at = keys(u + part, step)
                p = jnp.exp2(mm(k_ref[0, at, :], qt) * EXP2).astype(bf)
                p_ref[0, at, :] = p
                acc = acc + mm(vt_ref[0, :, at], p)
            return acc

        finish(0.0, in_steps(pairs, (16, 8, 4), body, jnp.zeros((80, bq), f32)))

    @pl.when(jnp.logical_and(qi * bq < live * 128, n_ref[1] == 0))
    def _():
        qt = qt_ref[0]

        def body(u, size, carry):
            top, acc = carry
            s = mm(k_ref[0, keys(u, size), :], qt) * EXP2
            new = jnp.maximum(top, jnp.max(s, axis=0, keepdims=True))
            p = jnp.exp2(s - new).astype(bf)
            return new, acc * jnp.exp2(top - new) + mm(vt_ref[0, :, keys(u, size)], p)

        finish(*in_steps(pairs, (4,), body, (jnp.full((1, bq), -3e38, f32), jnp.zeros((80, bq), f32))))


def attend(live, k, qt, vt, bq=1024):
    n = k.shape[1]
    spec = pltpu.PrefetchScalarGridSpec(
        num_scalar_prefetch=1,
        grid=(3, n // bq),
        in_specs=[
            pl.BlockSpec((1, n, 128), lambda h, i, s: (h, 0, 0)),
            pl.BlockSpec((1, 128, bq), lambda h, i, s: (h, 0, i)),
            pl.BlockSpec((1, 80, n), lambda h, i, s: (h, 0, 0)),
        ],
        out_specs=[
            pl.BlockSpec((1, 64, bq), lambda h, i, s: (h, 0, i)),
            pl.BlockSpec((1, 128, bq), lambda h, i, s: (h, 0, i)),
            pl.BlockSpec((1, n, bq), lambda h, i, s: (h, 0, i)),
            pl.BlockSpec((1, 1, bq), lambda h, i, s: (h, 0, i)),
        ],
    )
    return pl.pallas_call(
        functools.partial(attend_kernel, bq),
        grid_spec=spec,
        out_shape=[
            jax.ShapeDtypeStruct((3, 64, n), f32),
            jax.ShapeDtypeStruct((3, 128, n), bf),
            jax.ShapeDtypeStruct((3, n, n), bf),
            jax.ShapeDtypeStruct((3, 1, n), f32),
        ],
        compiler_params=params(),
        name="attention_forward",
    )(live, k, qt, vt)


def spread_kernel(src_ref, n_ref, t_ref, ot_ref, *o_refs):
    live, t, tiles = n_ref[0], t_ref[0], len(o_refs)
    per = o_refs[0].shape[1] // 128

    def step(b, _):
        g = src_ref[b]
        lanes = pl.ds(pl.multiple_of(b * 128, 128), 128)
        to = pl.ds(pl.multiple_of((g % per) * 128, 128), 128)
        for k in range(tiles):
            here = (g // per - t + tiles) % tiles == k

            @pl.when(jnp.logical_and(here, b < live))
            def _():
                for h in range(3):
                    o_refs[k][h * 64 : (h + 1) * 64, to] = ot_ref[h, :, lanes].astype(bf)

            @pl.when(jnp.logical_and(here, b >= live))
            def _():
                o_refs[k][:, to] = jnp.zeros((192, 128), bf)

        return 0

    lax.fori_loop(0, ot_ref.shape[2] // 128, step, 0)


def spread(src, live, tile, ot, tiles):
    n = ot.shape[2]
    return pl.pallas_call(
        spread_kernel,
        in_specs=[smem_spec()] * 3 + [vmem_spec()],
        out_specs=[vmem_spec()] * tiles,
        out_shape=[jax.ShapeDtypeStruct((192, n // tiles), bf)] * tiles,
        compiler_params=params(),
        name="spread_attended",
    )(src, live, tile, ot)


def collect_kernel(src_ref, n_ref, t_ref, ot_ref, rt_ref, *refs):
    g_refs, dt_ref = refs[:-1], refs[-1]
    live, t, tiles = n_ref[0], t_ref[0], len(g_refs)
    mild = n_ref[1] == 1
    per = g_refs[0].shape[1] // 128
    row = lax.broadcasted_iota(jnp.int32, (64, 128), 0)

    def step(b, _):
        g = src_ref[b]
        to = pl.ds(pl.multiple_of(b * 128, 128), 128)
        lanes = pl.ds(pl.multiple_of((g % per) * 128, 128), 128)
        for k in range(tiles):

            @pl.when(jnp.logical_and((t - g // per + tiles) % tiles == k, b < live))
            def _():
                for h in range(3):
                    scale = jnp.where(mild, rt_ref[h, :, to], 1.0)
                    d = (g_refs[k][h * 64 : (h + 1) * 64, lanes].astype(f32) * scale).astype(bf).astype(f32)
                    x, y, z = split3(-jnp.sum(d * ot_ref[h, :, to], axis=0, keepdims=True))
                    tail = jnp.where(row == 0, x, jnp.where(row == 1, y, jnp.where(row == 2, z, 0.0)))
                    dt_ref[h, :, to] = jnp.concatenate([d, tail], axis=0).astype(bf)

        @pl.when(b >= live)
        def _():
            dt_ref[:, :, to] = jnp.zeros((3, 128, 128), bf)

        return 0

    lax.fori_loop(0, ot_ref.shape[2] // 128, step, 0)


def collect(src, live, tile, grads, ot, rt):
    n = ot.shape[2]
    return pl.pallas_call(
        collect_kernel,
        in_specs=[smem_spec()] * 3 + [vmem_spec()] * (2 + len(grads)),
        out_specs=vmem_spec(),
        out_shape=jax.ShapeDtypeStruct((3, 128, n), bf),
        compiler_params=params(),
        name="collect_attended_grad",
    )(src, live, tile, ot, rt, *grads)


def attend_back_kernel(bk, n_ref, p_ref, k_ref, kt_ref, v_ref, qb_ref, dt_ref, dq_ref, dk_ref, dv_ref):
    live = n_ref[0]
    j = pl.program_id(1)

    @pl.when(j == 0)
    def _():
        dq_ref[...] = jnp.zeros_like(dq_ref)

    def lanes(u):
        return pl.ds(pl.multiple_of(u * 256, 256), 256)

    pairs = (live + 1) // 2

    def over_queries(rows, sizes, body):
        zero = jnp.zeros((rows, 64), f32)
        dk, dv = in_steps((live + 7) // 8 * 4, sizes, body, (zero, zero))
        dk_ref[0, :rows] = (dk * SCALE).astype(bf)
        dv_ref[0, :rows] = dv.astype(bf)

    def with_kept(rows):
        k, v, kt = k_ref[0, :rows], v_ref[0, :rows], kt_ref[0, :, :rows]

        def body(u, size, carry):
            dk, dv = carry
            dp = mm(v, dt_ref[0, :, lanes(u)])
            for part in range(size):
                at = lanes(u + part)
                ahead = mm(v, dt_ref[0, :, lanes(u + part + 1)]) if part + 1 < size else None
                p = p_ref[0, :rows, at]
                ds = (p.astype(f32) * dp).astype(bf)
                dv = dv + mm(p, dt_ref[0, :64, at], NT)
                dk = dk + mm(ds, qb_ref[0, :64, at], NT)
                dq_ref[0, :, at] += mm(kt, ds)
                dp = dp if ahead is None else ahead
            return dk, dv

        over_queries(rows, (16, 8, 4), body)

    @pl.when(jnp.logical_and(n_ref[1] == 1, 2 * j + 2 <= pairs))
    def _():
        with_kept(bk)

    @pl.when(jnp.logical_and(n_ref[1] == 1, 2 * j + 1 == pairs))
    def _():
        dk_ref[0, bk // 2 :] = jnp.zeros((bk // 2, 64), bf)
        dv_ref[0, bk // 2 :] = jnp.zeros((bk // 2, 64), bf)
        with_kept(bk // 2)

    @pl.when(jnp.logical_and(n_ref[1] == 0, j * bk < live * 128))
    def _():
        k, v, kt = k_ref[0], v_ref[0], kt_ref[0]

        def body(u, size, carry):
            dk, dv = carry
            for part in range(size):
                at = lanes(u + part)
                p = jnp.exp2(mm(k, qb_ref[0, :, at]) * EXP2)
                ds = (p * mm(v, dt_ref[0, :, at])).astype(bf)
                dv = dv + mm(p.astype(bf), dt_ref[0, :64, at], NT)
                dk = dk + mm(ds, qb_ref[0, :64, at], NT)
                dq_ref[0, :, at] += mm(kt, ds)
            return dk, dv

        over_queries(bk, (4,), body)


def attend_back(first, heads, live, p, k, kt, v, qb, dt, bk=512):
    n = k.shape[1]
    whole_t = lambda h, j, s: (first + h, 0, 0)
    rows = lambda h, j, s: (first + h, j, 0)
    spec = pltpu.PrefetchScalarGridSpec(
        num_scalar_prefetch=1,
        grid=(heads, n // bk),
        in_specs=[
            pl.BlockSpec((1, bk, n), rows),
            pl.BlockSpec((1, bk, 128), rows),
            pl.BlockSpec((1, 64, bk), lambda h, j, s: (first + h, 0, j)),
            pl.BlockSpec((1, bk, 128), rows),
            pl.BlockSpec((1, 128, n), whole_t),
            pl.BlockSpec((1, 128, n), whole_t),
        ],
        out_specs=[
            pl.BlockSpec((1, 64, n), lambda h, j, s: (h, 0, 0)),
            pl.BlockSpec((1, bk, 64), lambda h, j, s: (h, j, 0)),
            pl.BlockSpec((1, bk, 64), lambda h, j, s: (h, j, 0)),
        ],
    )
    S = jax.ShapeDtypeStruct
    return pl.pallas_call(
        functools.partial(attend_back_kernel, bk),
        grid_spec=spec,
        out_shape=[S((heads, 64, n), f32), S((heads, n, 64), bf), S((heads, n, 64), bf)],
        cost_estimate=pl.CostEstimate(flops=heads * 4 * 10**10, bytes_accessed=heads * 50 * 10**6, transcendentals=0),
        compiler_params=params(),
        name="attention_backward",
    )(live, p, k, kt, v, qb, dt)


def qkv_back_kernel(given, src_ref, n_ref, odd_ref, x0, x1, x2, x3, gain_ref, a_ref, w_ref, *refs):
    grads, (ga_ref, gz_ref, gw_ref, gb_ref, vs_ref, acc, sums, rows, sems) = refs[:given], refs[given:]
    dqs, dks, dvs = [[(r, h) for r in grads[j::3] for h in range(r.shape[0])] for j in range(3)]
    early = ga_ref.shape[1] // 128
    i = pl.program_id(0)
    live = n_ref[0]
    slot = i % 2

    def wait_for(slot):
        for b in range(4):
            pltpu.make_async_copy(rows.at[slot, pl.ds(b * 128, 128)], ga_ref.at[0, pl.ds(0, 128)], sems.at[slot, b]).wait()

    @pl.when(i >= 2)
    def _():
        wait_for(slot)

    @pl.when(i == 0)
    def _():
        acc[...] = jnp.zeros_like(acc)
        sums[...] = jnp.zeros_like(sums)
        vs_ref[...] = jnp.zeros_like(vs_ref)

    @pl.when(4 * i < live)
    def _():
        dq = jnp.concatenate([r[h] for r, h in dqs], axis=0).T * SCALE
        g = jnp.concatenate([dq] + [r[h].astype(f32) for r, h in dks + dvs], axis=1).astype(bf)
        acc[...] += mm(a_ref[...], g, TN)
        sums[...] += jnp.broadcast_to(column_sum(g.astype(f32)), sums.shape)
        g1 = mm(g, w_ref[...], NT)
        rows[slot] = g1.astype(bf)
        x = jnp.concatenate([r[...] for r in (x0, x1, x2, x3)], axis=0).astype(f32)
        cen = x - jnp.mean(x, axis=-1, keepdims=True)
        normed = cen * lax.rsqrt(jnp.mean(cen * cen, axis=-1, keepdims=True) + EPS_NORM)
        vs_ref[0:1, :] += column_sum(g1 * normed)
        vs_ref[1:2, :] += column_sum(g1)

    @pl.when(4 * i >= live)
    def _():
        rows[slot] = jnp.zeros(rows.shape[1:], bf)

    per = early + gz_ref.shape[1] // 128
    for b in range(4):
        block, at = rows.at[slot, pl.ds(b * 128, 128)], src_ref[4 * i + b]
        t, j = at // per, at % per

        @pl.when(j < early)
        def _():
            pltpu.make_async_copy(block, ga_ref.at[t, pl.ds(pl.multiple_of(j * 128, 128), 128)], sems.at[slot, b]).start()

        @pl.when(j >= early)
        def _():
            pltpu.make_async_copy(block, gz_ref.at[t, pl.ds(pl.multiple_of((j - early) * 128, 128), 128)], sems.at[slot, b]).start()

    @pl.when(i == pl.num_programs(0) - 1)
    def _():
        wait_for(1 - slot)
        wait_for(slot)

        def place(odd):
            for r in range(4):
                for c in range(3):
                    top, tail = pack(acc[r * 192 : (r + 1) * 192, c * 192 : (c + 1) * 192], odd)
                    gw_ref[r * 3 + c, :192] = top.astype(bf)
                    gw_ref[r * 3 + c, 192:] = tail.astype(bf)

        by_parity(odd_ref[0], place)
        gb_ref[...] = sums[...]


def qkv_backward(src, live, odd, tokens, gain, a, w, grads, tiles, early):
    n = a.shape[0]
    per = n // tiles
    fixed = lambda i, s, c, o: (0, 0)
    row = lambda i, s, c, o: (0, i, 0)
    spec = pltpu.PrefetchScalarGridSpec(
        num_scalar_prefetch=3,
        grid=(n // 512,),
        in_specs=[pl.BlockSpec((128, 768), lambda i, s, c, o, k=k: (s[4 * i + k], 0)) for k in range(4)]
        + [pl.BlockSpec((1, 768), fixed), pl.BlockSpec((512, 768), lambda i, s, c, o: (i, 0)), pl.BlockSpec((768, 576), fixed)]
        + [
            pl.BlockSpec((g.shape[0], 64, 512), lambda i, s, c, o: (0, 0, i)) if g.shape[1] == 64 else pl.BlockSpec((g.shape[0], 512, 64), row)
            for g in grads
        ],
        out_specs=[any_spec(), any_spec(), pl.BlockSpec((12, 288, 128), lambda i, s, c, o: (0, 0, 0)), pl.BlockSpec((8, 576), fixed), pl.BlockSpec((8, 768), fixed)],
        scratch_shapes=[pltpu.VMEM((768, 576), f32), pltpu.VMEM((8, 576), f32), pltpu.VMEM((2, 512, 768), bf), pltpu.SemaphoreType.DMA((2, 4))],
    )
    S = jax.ShapeDtypeStruct
    return pl.pallas_call(
        functools.partial(qkv_back_kernel, len(grads)),
        grid_spec=spec,
        out_shape=[S((tiles, early, 768), bf), S((tiles, per - early, 768), bf), S((12, 288, 128), bf), S((8, 576), f32), S((8, 768), f32)],
        cost_estimate=pl.CostEstimate(flops=3 * 10**10, bytes_accessed=40 * 10**6, transcendentals=0),
        compiler_params=params(),
        name="qkv_backward",
    )(src, live, odd, tokens, tokens, tokens, tokens, gain, a, w, *grads)


def gelu_parts(z):
    cdf = 0.5 + 0.5 * lax.erf(z * math.sqrt(0.5))
    return z * cdf, cdf + z * (jnp.exp2(z * z * (-0.5 * math.log2(math.e))) * (1.0 / math.sqrt(2.0 * math.pi)))


def middle_kernel(inv_ref, cnt_ref, t_ref, blk_ref, rest_ref, o0, o1, o2, o3, x_ref, c_ref, vp_ref, bu_ref, y_ref, gr_ref, g0, g1, g2_ref, g3,
                  u_s, gz_s, a2_s, gm_s, gb_s, o_s, vs_ref, us_ref, w_out, w_up, w_down, tails, tsem, isem):
    i = pl.program_id(0)
    rows = x_ref.shape[0]
    split = blk_ref.shape[0]
    r0 = i * rows
    kinds = ((w_out, 48, 2, 4), (w_up, 64, 8, 4), (w_down, 128, 2, 16))

    @pl.when(i == 0)
    def _():
        vs_ref[...] = jnp.zeros_like(vs_ref)
        us_ref[...] = jnp.zeros_like(us_ref)

        def pair(w, first, pairs):
            def parts(j, run):
                r = pl.multiple_of((j // pairs) * 192, 64)
                col = pl.multiple_of((j % pairs) * 384, 128)
                for b, off in ((0, 0), (1, 256)):
                    at = first + 2 * j + b
                    run(at, w.at[pl.ds(r, 192), pl.ds(col + off, 128)], tails.at[at - 48])
                return r, col

            def fetch(at, top, tail):
                for ref, here, slot in ((blk_ref, inv_ref[at] < split, inv_ref[at]), (rest_ref, inv_ref[at] >= split, inv_ref[at] - split)):

                    @pl.when(here)
                    def _():
                        pltpu.make_async_copy(ref.at[slot, pl.ds(0, 192)], top, tsem.at[at - 48]).start()
                        pltpu.make_async_copy(ref.at[slot, pl.ds(192, 96)], tail, isem.at[at - 48]).start()

            def fetched(at, top, tail):
                pltpu.make_async_copy(blk_ref.at[0, pl.ds(0, 192)], top, tsem.at[at - 48]).wait()
                pltpu.make_async_copy(blk_ref.at[0, pl.ds(192, 96)], tail, isem.at[at - 48]).wait()

            def start(j, _):
                parts(j, fetch)
                return 0

            def join(j, _):
                r, col = parts(j, fetched)
                even = tails[first + 2 * j - 48].astype(f32)
                odd = tails[first + 2 * j - 47].astype(f32)
                lane = lax.broadcasted_iota(jnp.int32, even.shape, 1) < 64
                w[pl.ds(r, 96), pl.ds(col + 128, 128)] = jnp.where(lane, even, odd).astype(bf)
                w[pl.ds(r + 96, 96), pl.ds(col + 128, 128)] = turn(jnp.where(lane, odd, even)).astype(bf)
                return 0

            return start, join

        todo = [(pair(w, first, pairs), pairs * high) for w, first, pairs, high in kinds]
        for (start, _), n in todo:
            lax.fori_loop(0, n, start, 0)

        for (_, join), n in todo:
            lax.fori_loop(0, n, join, 0)

    vp = vp_ref[...]
    row = r0 + lax.broadcasted_iota(jnp.int32, (rows, 1), 0)
    live = jnp.where(row < cnt_ref[0], 1.0, 0.0)
    t = t_ref[0]
    for k, ref in enumerate((o0, o1, o2, o3)):
        o_s[pl.ds(pl.multiple_of(((t - k + 4) % 4) * 192, 64), 192), :] = ref[...]
    o_t = o_s[...]
    res = x_ref[...].astype(f32) + mm(o_t, w_out[...], TN) + vp[6:7]
    cen = res - jnp.mean(res, axis=-1, keepdims=True)
    inv_std = lax.rsqrt(jnp.mean(cen * cen, axis=-1, keepdims=True) + EPS_NORM)
    normed = cen * inv_std
    a2 = (normed * vp[2:3] + vp[3:4]).astype(bf)
    gy = c_ref[...].astype(f32) * live
    gm = gy.astype(bf)
    a2_s[...] = a2
    gm_s[...] = gm
    branch = jnp.zeros((rows, 768), f32)
    g2 = jnp.zeros((rows, 768), f32)
    for j in range(4):
        cols = slice(j * 768, (j + 1) * 768)
        u, slope = gelu_parts(mm(a2, w_up[:, cols]) + bu_ref[:, cols])
        u = u.astype(bf)
        u_s[:, cols] = u
        branch = branch + mm(u, w_down[cols, :])
        gz = (mm(gm, w_down[cols, :], NT) * slope).astype(bf)
        gz_s[:, cols] = gz
        us_ref[:, cols] += jnp.broadcast_to(column_sum(gz.astype(f32)), (8, 768))
        g2 = g2 + mm(gz, w_up[:, cols], NT)
    y_ref[...] = (live * (res + branch + vp[7:8])).astype(bf)
    d2 = g2 * vp[2:3]
    gr = gy + inv_std * (d2 - jnp.mean(d2, axis=-1, keepdims=True) - normed * jnp.mean(d2 * normed, axis=-1, keepdims=True))
    gr_ref[...] = gr
    gb = gr.astype(bf)
    gb_s[...] = gb
    vs_ref[0:1, :] += column_sum(g2 * normed)
    vs_ref[1:2, :] += column_sum(g2)
    vs_ref[2:3, :] += column_sum(gb.astype(f32))
    vs_ref[3:4, :] += column_sum(gm.astype(f32))
    for k, ref in enumerate((g0, g1, g2_ref, g3)):
        ref[...] = mm(w_out[pl.ds(pl.multiple_of(((t + k) % 4) * 192, 64), 192), :], gb, NT).astype(bf)


def weight_grad_kernel(outs, pos_ref, o_in, gb_in, a2_in, gz_in, u_in, gm_in, *refs):
    s_refs, (o_s, gb_s, a2_s, gz_s, u_s, gm_s, ring, zero, lsem, osem, zsem) = refs[:outs], refs[outs:]
    each = s_refs[0].shape[0]

    def to_slot(block, at, sem):
        for o in range(outs):

            @pl.when(at // each == o)
            def _():
                pltpu.make_async_copy(block, s_refs[o].at[at % each], sem).start()

    def landed(block, sem):
        pltpu.make_async_copy(block, s_refs[0].at[0], sem).wait()

    loads = [pltpu.make_async_copy(a, b, lsem.at[j]) for j, (a, b) in enumerate(
        ((o_in, o_s), (gb_in, gb_s), (a2_in, a2_s), (gz_in, gz_s), (gm_in, gm_s), (u_in, u_s)))]
    for load in loads:
        load.start()
    zero[...] = jnp.zeros_like(zero)

    def clear(j, _):
        to_slot(zero, pos_ref[j], zsem.at[j])
        return 0

    lax.fori_loop(0, 48, clear, 0)
    def send(n, g, first, pairs, high, low):
        half = (n % 2) * 8

        def put(r, b):
            return first + (high + r) * 2 * pairs + 2 * low + b

        for r in range(4):
            part = g[r * 192 : (r + 1) * 192]
            mid = part[:, 128:256]
            upper, lower = mid[:96], turn(mid[96:])
            lane = lax.broadcasted_iota(jnp.int32, upper.shape, 1) < 64
            for b, top, tail in ((0, part[:, :128], jnp.where(lane, upper, lower)), (1, part[:, 256:], jnp.where(lane, lower, upper))):
                k = half + 2 * r + b

                @pl.when(n >= 2)
                def _():
                    landed(ring.at[k], osem.at[k])

                ring[k, :192] = top.astype(bf)
                ring[k, 192:] = tail.astype(bf)
                to_slot(ring.at[k], pos_ref[put(r, b)], osem.at[k])

    def lanes(j):
        return pl.ds(pl.multiple_of(j * 384, 128), 384)

    def grad_out(n, _):
        send(n, mm(o_s[...], gb_s[:, lanes(n)]), 48, 2, 0, n)
        return 0

    def grad_up(n, _):
        send(n, mm(a2_s[...], gz_s[:, lanes(n)], TN), 64, 8, 0, n)
        return 0

    def grad_down(n, _):
        high = n // 2
        send(n, mm(u_s[:, pl.ds(pl.multiple_of(high * 768, 128), 768)], gm_s[:, lanes(n % 2)], TN), 128, 2, high * 4, n % 2)
        return 0

    def drain():
        for k in range(16):
            landed(ring.at[k], osem.at[k])

    for f, n, first in ((grad_out, 2, 0), (grad_up, 8, 2), (grad_down, 8, 4)):
        loads[first].wait()
        loads[first + 1].wait()
        lax.fori_loop(0, n, f, 0)
        drain()

    def cleared(j, _):
        landed(zero, zsem.at[j])
        return 0

    lax.fori_loop(0, 48, cleared, 0)


def middle(inv, count, tile, blocks, rest, o_parts, tokens, cotangent, vec_params, bias_up, rows=256):
    n, width = tokens.shape
    hidden = bias_up.shape[1]
    row = lambda i, s, c, t: (i, 0)
    fixed = lambda i, s, c, t: (0, 0)
    col = lambda i, s, c, t: (0, i)
    V, DS = pltpu.VMEM, pltpu.SemaphoreType.DMA
    narrow, wide, part = pl.BlockSpec((rows, width), row), pl.BlockSpec((rows, hidden), row), pl.BlockSpec((192, rows), col)
    spec = pltpu.PrefetchScalarGridSpec(
        num_scalar_prefetch=3,
        grid=(n // rows,),
        in_specs=[any_spec()] * 2 + [part] * 4 + [narrow, narrow, pl.BlockSpec((12, width), fixed), pl.BlockSpec((1, hidden), fixed)],
        out_specs=[narrow, narrow] + [part] * 4 + [wide, wide, narrow, narrow, narrow, pl.BlockSpec((width, rows), col),
                   pl.BlockSpec((8, width), fixed), pl.BlockSpec((8, hidden), fixed)],
        scratch_shapes=[V((768, 768), bf), V((768, 3072), bf), V((3072, 768), bf), V((144, 96, 128), bf), DS((144,)), DS((144,))],
    )
    S = jax.ShapeDtypeStruct
    return pl.pallas_call(
        middle_kernel,
        grid_spec=spec,
        out_shape=[S((n, width), bf), S((n, width), f32)] + [S((192, n), bf)] * 4 + [S((n, hidden), bf)] * 2 + [S((n, width), bf)] * 3
        + [S((width, n), bf), S((8, width), f32), S((8, hidden), f32)],
        compiler_params=params(),
        name="projection_and_mlp",
    )(inv, count, tile, blocks, rest, *o_parts, tokens, cotangent, vec_params, bias_up)


def weight_grads_to_slots(pos, outs, block_count, o_t, gb, a2, gz, u, gm):
    V, DS = pltpu.VMEM, pltpu.SemaphoreType.DMA
    arrays = (o_t, gb, a2, gz, u, gm)
    return pl.pallas_call(
        functools.partial(weight_grad_kernel, outs),
        in_specs=[smem_spec()] + [any_spec()] * 6,
        out_specs=[any_spec()] * outs,
        out_shape=[jax.ShapeDtypeStruct((block_count // outs, 288, 128), bf)] * outs,
        scratch_shapes=[V(a.shape, bf) for a in arrays] + [V((16, 288, 128), bf), V((288, 128), bf), DS((6,)), DS((16,)), DS((48,))],
        cost_estimate=pl.CostEstimate(flops=6 * 10**10, bytes_accessed=32 * 10**6, transcendentals=0),
        compiler_params=params(),
        name="mlp_weight_gradients",
    )(pos, *arrays)


def quarters(b0, b1):
    return (b0 * 2 + b1, (1 - b0) * 2 + b1, b0 * 2 + 1 - b1, (1 - b0) * 2 + 1 - b1)


def add_pair_kernel(common, bits_ref, *refs):
    outs = list(refs[16:])
    for p in range(2):
        for side in range(4):
            j = 4 * p + side
            total = (refs[2 * j][...].astype(f32) + refs[2 * j + 1][...].astype(f32)).astype(bf)
            if side == common[p]:
                outs[6][p] = total
            else:
                outs[3 * p + side - (side > common[p])][...] = total


def add_pair(bits, common, keep, came):
    specs = []
    for p in range(2):
        for side in range(4):
            at = lambda i, b, p=p, side=side: (p * 8 + quarters(b[2 * p], b[2 * p + 1])[side] * 2 + i, 0, 0)
            specs += [pl.BlockSpec((6, 288, 128), at)] * 2
    S = jax.ShapeDtypeStruct
    return pl.pallas_call(
        functools.partial(add_pair_kernel, common),
        grid_spec=pltpu.PrefetchScalarGridSpec(
            num_scalar_prefetch=1,
            grid=(2,),
            in_specs=specs,
            out_specs=[pl.BlockSpec((6, 288, 128), lambda i, b: (i, 0, 0))] * 6 + [pl.BlockSpec((2, 6, 288, 128), lambda i, b: (0, i, 0, 0))],
        ),
        out_shape=[S((12, 288, 128), bf)] * 6 + [S((2, 12, 288, 128), bf)],
        compiler_params=params(),
        name="add_gradients_of_cores",
    )(bits, *[keep, came] * 8)


def add_four_kernel(common, bits_ref, *refs):
    outs = refs[7:]
    for p in range(2):
        parts = refs[3 * p : 3 * p + 3]
        for side, q in enumerate(quarters(bits_ref[2 * p], bits_ref[2 * p + 1])):
            for b in range(3):
                total = (sum(r[q * 3 + b].astype(f32) for r in parts) + refs[6][p, q * 3 + b].astype(f32)).astype(bf)
                if side == common[p]:
                    outs[6][p, b] = total
                else:
                    outs[3 * p + side - (side > common[p])][b] = total


def add_four(bits, common, parts):
    S = jax.ShapeDtypeStruct
    return pl.pallas_call(
        functools.partial(add_four_kernel, common),
        in_specs=[smem_spec()] + [vmem_spec()] * 7,
        out_specs=[vmem_spec()] * 7,
        out_shape=[S((3, 288, 128), bf)] * 6 + [S((2, 3, 288, 128), bf)],
        compiler_params=params(),
        name="add_gradients",
    )(bits, *parts)


def add_last_kernel(*refs):
    for p in range(2):
        for b in range(3):
            refs[7][3 * p + b] = (sum(r[b].astype(f32) for r in refs[3 * p : 3 * p + 3]) + refs[6][p, b].astype(f32)).astype(bf)


def add_last(parts):
    return pl.pallas_call(
        add_last_kernel,
        in_specs=[vmem_spec()] * 7,
        out_specs=vmem_spec(),
        out_shape=jax.ShapeDtypeStruct((6, 288, 128), bf),
        compiler_params=params(),
        name="add_last_gradients",
    )(*parts)


def split2(v):
    hi = v.astype(bf)
    return hi, (v - hi.astype(f32)).astype(bf)


def mm3(a, b, dims):
    return mm(a[0], b[0], dims) + (mm(a[0], b[1], dims) + mm(a[1], b[0], dims))


def adam_kernel(odd_ref, from_ref, g_ref, late_ref, m1_ref, m2_ref, l_ref, r_ref, g_out, m1_out, m2_out, u_out, s_out):
    for b in range(g_ref.shape[0]):
        slot = pl.program_id(0) * g_ref.shape[0] + b
        place = from_ref[slot]
        part = jnp.where(place >= 0, late_ref[jnp.maximum(place, 0)].astype(f32), g_ref[b].astype(f32))
        grad = unpack_either(part[:192], part[192:], odd_ref[slot] == 1)
        left, right = split2(l_ref[b]), split2(r_ref[b])
        low = grad.astype(bf)
        rot = mm3(split2(mm(left[0], low, TN) + mm(left[1], low, TN)), right, NN)
        g_out[b] = grad
        first = BETA_ONE * m1_ref[b] + (1.0 - BETA_ONE) * rot
        second = BETA_TWO * m2_ref[b] + (1.0 - BETA_TWO) * rot * rot
        upd = (first * (1.0 / (1.0 - BETA_ONE**STEP))) / (jnp.sqrt(second * (1.0 / (1.0 - BETA_TWO**STEP))) + ADAM_EPS)
        upd = mm3(split2(mm3(left, split2(upd), NN)), right, NT)
        m1_out[b] = first
        m2_out[b] = second
        u_out[b] = upd.astype(bf)
        s_out[b] = lane_sums(upd * upd)


def adam(odd, late_at, grads, late, first, second, left, right):
    n = grads.shape[0]
    g = group_of(n)
    at = lambda i, s, f: (i, 0, 0)
    big = pl.BlockSpec((g, 192, 192), at)
    spec = pltpu.PrefetchScalarGridSpec(
        num_scalar_prefetch=2,
        grid=(n // g,),
        in_specs=[pl.BlockSpec((g, 288, 128), at), pl.BlockSpec(late.shape, lambda i, s, f: (0, 0, 0))] + [big] * 4,
        out_specs=[big] * 4 + [pl.BlockSpec((g, 8, 128), at)],
    )
    return pl.pallas_call(
        adam_kernel,
        grid_spec=spec,
        out_shape=[jax.ShapeDtypeStruct((n, 192, 192), f32)] * 3 + [jax.ShapeDtypeStruct((n, 192, 192), bf), jax.ShapeDtypeStruct((n, 8, 128), f32)],
        compiler_params=params(),
        name="rotated_adam",
    )(odd, late_at, grads, late, first, second, left, right)


def update_kernel(rate_ref, m_ref, u_ref, mo_ref, mc_ref):
    g = m_ref.shape[0]
    for b in range(g):
        new = m_ref[b] - rate_ref[pl.program_id(0) * g + b] * u_ref[b].astype(f32)
        mo_ref[b] = new
        mc_ref[b] = new.astype(bf)


def new_weights(rate, master, update):
    n = master.shape[0]
    g = 8 if n % 8 == 0 else group_of(n)
    big = pl.BlockSpec((g, 192, 192), lambda i, r: (i, 0, 0))
    return pl.pallas_call(
        update_kernel,
        grid_spec=pltpu.PrefetchScalarGridSpec(num_scalar_prefetch=1, grid=(n // g,), in_specs=[big] * 2, out_specs=[big] * 2),
        out_shape=[jax.ShapeDtypeStruct(master.shape, f32), jax.ShapeDtypeStruct(master.shape, bf)],
        compiler_params=params(),
        name="new_weights",
    )(rate, master, update)


def halving_places(slot, core):
    dp, r = slot // 24, slot % 24
    y, z, far, x, s = dp % 2, dp // 2 % 2, dp // 4, r % 6 // 3, r % 3
    portion = r % 12 // 6
    inside = jnp.where(portion == 0, x * 8 + y * 4 + z * 2 + far, y * 8 + z * 4 + x * 2 + far)
    return jnp.where(r // 12 == core, 0, 96) + portion * 48 + inside * 3 + s


def norm_forward(row_data, gain_vec, shift_vec):
    row_mean = jnp.mean(row_data, axis=-1, keepdims=True)
    centred = row_data - row_mean
    inv_std = lax.rsqrt(jnp.mean(centred * centred, axis=-1, keepdims=True) + EPS_NORM)
    normed = centred * inv_std
    return (normed * gain_vec + shift_vec, normed, inv_std)


def norm_back(grad_out, normed, inv_std, gain_vec):
    grad_normed = grad_out * gain_vec
    return inv_std * (
        grad_normed
        - jnp.mean(grad_normed, axis=-1, keepdims=True)
        - normed * jnp.mean(grad_normed * normed, axis=-1, keepdims=True)
    )


def block_plan(counts, slot_count):
    tiles = counts.shape[0]
    per = slot_count // 128
    j = lax.broadcasted_iota(jnp.int32, (tiles, per), 1)
    kept = jnp.clip(counts[:, None] - j * 128, 0, 128).reshape(-1)
    full = (kept > 0).astype(jnp.int32)
    index = jnp.arange(tiles * per, dtype=jnp.int32)
    before = (index[None, :] < index[:, None]).astype(jnp.int32)
    ahead = jnp.sum(before * full[None, :], axis=1)
    live = jnp.sum(full)
    place = jnp.where(full > 0, ahead, live + index - ahead)
    hot = (place[None, :] == index[:, None]).astype(jnp.int32)
    return jnp.sum(hot * index[None, :], axis=1), jnp.sum(hot * kept[None, :], axis=1), live.reshape(1)


def make_body(tuned):
    def body(tokens, cotangent, counts, master, slot_block, groups, first_moment, second_moment, left_basis, right_basis, vec_params, vec_first, vec_second):
        slot_count, width = tokens.shape[1:]
        per_owner = master.shape[0]
        tile = lax.axis_index("tile")
        block_count = slot_block.shape[0]
        first = per_owner // 2 if tuned else per_owner
        index = jnp.arange(block_count, dtype=jnp.int32)
        owner = index // per_owner
        same = (owner[None, :] == owner[:, None]).astype(jnp.int32)
        is_qkv = (slot_block < 48).astype(jnp.int32)
        sooner = same * jnp.where(is_qkv[None, :] == is_qkv[:, None], (index[None, :] < index[:, None]).astype(jnp.int32), is_qkv[None, :])
        rank = jnp.sum(sooner, axis=1)
        place = jnp.where(rank < first, owner * first + rank, block_count // per_owner * first + owner * (per_owner - first) + rank - first)
        most = jnp.max(jnp.sum(same * is_qkv[None, :], axis=1))
        start = lax.axis_index("dp") * per_owner
        mine = lax.dynamic_slice(slot_block, (start,), (per_owner,))
        odd = mine % 2
        local = jnp.arange(per_owner, dtype=jnp.int32)
        at_rank = (lax.dynamic_slice(rank, (start,), (per_owner,))[None, :] == local[:, None]).astype(jnp.int32)
        order = jnp.sum(at_rank * local[None, :], axis=1)
        packed, packed_rest, weight_sq = pack_master(order, jnp.sum(at_rank * odd[None, :], axis=1), master, first)
        own_tokens = tokens.reshape(slot_count, width)
        count_tile = jnp.broadcast_to(counts.reshape(1, 1), (8, 128))
        if tuned:
            blocks, token_all, count_all = gather_all(packed, own_tokens, count_tile)
            packed_rest, blocks = lax.optimization_barrier((packed_rest, blocks))
            blocks_rest = lax.all_gather(packed_rest, "dp", axis=0, tiled=True)
        else:
            blocks = lax.all_gather(packed, "dp", axis=0, tiled=True)
            token_all = lax.all_gather(own_tokens, "tile", axis=0)
            count_all = lax.all_gather(count_tile, "tile", axis=0)
            blocks_rest = packed_rest
        tiles = token_all.shape[0]
        src, cnt, live = block_plan(count_all[:, 0, 0], slot_count)
        is_at = (slot_block[None, :] == index[:, None]).astype(jnp.int32)
        inverse = jnp.sum(is_at * index[None, :], axis=1)
        places = jnp.sum(is_at * place[None, :], axis=1)
        own_block = jnp.arange(12, dtype=jnp.int32) // 3 * 12 + jnp.arange(12, dtype=jnp.int32) % 3 * 4 + tile
        own_at = jnp.sum((slot_block[None, :] == own_block[:, None]).astype(jnp.int32) * place[None, :], axis=1)
        if tuned:
            qkv_blocks = lax.cond(
                most <= first,
                lambda: pick(own_at, blocks, packed_rest),
                lambda: pick(own_at, blocks, lax.all_gather(packed_rest, "dp", axis=0, tiled=True)),
            )
        else:
            qkv_blocks = pick(own_at, blocks, blocks_rest)
        tile_one = tile.astype(jnp.int32).reshape(1)
        own = width // tiles
        bias = lambda row: lax.dynamic_slice(vec_params[row : row + 1], (0, tile * own), (1, own))
        a1, qt, k, kt, v, vt, w_qkv, lengths = qkv_forward(
            src, cnt, tile_one % 2, token_all.reshape(-1, width), qkv_blocks, vec_params[0:1], vec_params[1:2], bias(4), bias(5)
        )
        mild = jnp.sqrt(jnp.max(lengths[:, 0, 0])) * jnp.sqrt(jnp.max(lengths[:, 1, 0])) * EXP2 <= 60.0
        live = jnp.concatenate([live, mild.astype(jnp.int32).reshape(1)])
        ot, qb, p, rt = attend(live, k, qt, vt)

        def shift(parts):
            return [parts[0]] + [lax.ppermute(parts[j], "tile", [(s, (s + j) % tiles) for s in range(tiles)]) for j in range(1, tiles)]

        o_parts = shift(spread(src, live, tile_one, ot, tiles))
        output, grad_resid, *rest = middle(
            places, counts.reshape(1), tile_one, blocks, blocks_rest, o_parts, own_tokens, cotangent.reshape(slot_count, width), vec_params, vec_params[8:].reshape(1, -1)
        )
        go_parts, (u, gz, a2, gm, gb, o_t, sums, up_sums) = rest[:tiles], rest[tiles:]
        go_parts = shift(go_parts)
        back = lambda first, heads, dt: list(attend_back(first, heads, live, p, k, kt, v, qb, dt))
        if tuned:
            dp = lax.axis_index("dp")
            bit = {"x": tile // 2, "y": dp % 2, "z": dp // 2 % 2, "far": dp // 4}
            mask = {"x": 2, "y": 4, "z": 8, "far": 16}

            def flip(array, *names):
                change = sum(mask[name] for name in names)
                return lax.ppermute(array, ("dp", "tile"), [(s, s ^ change) for s in range(32)])

            def three(sums, pairs, common):
                out = []
                for p, (a, b) in enumerate(pairs):
                    ways = [(), (a,), (b,), (a, b)]
                    del ways[common[p]]
                    out += [flip(sums[3 * p + j], *way) if way else sums[3 * p + j] for j, way in enumerate(ways)]
                return out + [flip(sums[6], pairs[0][common[0] - 1])]

            def bits_of(pairs):
                return jnp.stack([bit[name] for pair in pairs for name in pair]).astype(jnp.int32)

            first, second = [("x", "y"), ("y", "z")], [("z", "far"), ("x", "far")]
            keep, send = weight_grads_to_slots(halving_places(inverse, tile % 2), 2, block_count, o_t, gb, a2, gz, u, gm)
            send, go_parts = lax.optimization_barrier((send, go_parts))
            came = lax.ppermute(send, "tile", [(s, s ^ 1) for s in range(4)])
            dt = collect(src, live, tile_one, go_parts, ot, rt)
            dt, came = lax.optimization_barrier((dt, came))
            sums_one = add_pair(bits_of(first), (2, 1), keep, came)
            dt, sums_one = lax.optimization_barrier((dt, sums_one))
            parts = three(sums_one, first, (2, 1))
            head_grads = back(0, 2, dt)
            head_grads[0], parts = lax.optimization_barrier((head_grads[0], parts))
            sums_two = add_four(bits_of(second), (2, 2), parts)
            dt, sums_two = lax.optimization_barrier((dt, sums_two))
            parts = three(sums_two, second, (2, 2))
            head_grads += back(2, 1, dt)
            head_grads[3], parts = lax.optimization_barrier((head_grads[3], parts))
            mine_early = add_last(parts)
            head_grads[3], mine_early = lax.optimization_barrier((head_grads[3], mine_early))
            over_early = flip(mine_early, "x")
        else:
            slots = weight_grads_to_slots(inverse, 1, block_count, o_t, gb, a2, gz, u, gm)[0]
            dt = collect(src, live, tile_one, go_parts, ot, rt)
            head_grads = back(0, 3, dt)
        g_one, g_two, gw_qkv, qkv_sums, norm_sums = qkv_backward(
            src, live, tile_one % 2, token_all.reshape(-1, width), vec_params[0:1], a1, w_qkv, head_grads, tiles, slot_count * 3 // 8
        )
        if tuned:
            g_one, over_early = lax.optimization_barrier((g_one, over_early))
        zero = jnp.zeros((width,), f32)
        at_own = lambda s: lax.dynamic_update_slice(zero, s, (tile * own,))
        vector_part = jnp.concatenate(
            [norm_sums[0:2], sums[0:2], at_own(qkv_sums[0, :own])[None], at_own(qkv_sums[0, 2 * own :])[None], sums[2:4], up_sums[0].reshape(-1, width)], axis=0
        )
        if tuned:
            early, late, vector_grads = last_sums(gw_qkv, mine_early, over_early, vector_part)
            g_two, early = lax.optimization_barrier((g_two, early))
        else:
            early = lax.psum(lax.psum_scatter(slots.astype(f32), "dp", scatter_dimension=0, tiled=True), "tile").astype(bf)
            late = lax.all_gather(lax.psum(gw_qkv.astype(f32), "dp").astype(bf), "tile", axis=0, tiled=True)
            vector_grads = lax.psum(vector_part, ("dp", "tile"))
        g1 = jnp.concatenate([lax.psum_scatter(part, "tile", scatter_dimension=0, tiled=False) for part in (g_one, g_two)], axis=0)
        row_input = own_tokens.astype(f32)
        _, normed_one, inv_std_one = norm_forward(row_input, vec_params[0], vec_params[1])
        input_grad = grad_resid + norm_back(g1.astype(f32), normed_one, inv_std_one, vec_params[0])
        late_at = jnp.where(mine < 48, mine % 4 * 12 + mine // 12 * 3 + mine % 12 // 4, -1)
        weight_grads, first_out, second_out, update, update_sq = adam(odd, late_at, early, late, first_moment, second_moment, left_basis, right_basis)
        group_hot = (groups[:, None] == jnp.arange(128, dtype=jnp.int32)[None, :]).astype(f32)
        weight_part = jnp.sum(jnp.sum(at_rank.astype(f32)[:, :, None] * group_hot[None], axis=1) * jnp.sum(weight_sq[:, 0], axis=1)[:, None], axis=0)
        group_part = jnp.pad(jnp.stack([weight_part, jnp.sum(group_hot * jnp.sum(update_sq[:, 0], axis=1)[:, None], axis=0)]), ((0, 6), (0, 0)))
        group_both = group_sum(group_part, block_count // per_owner)
        own_both = jnp.sum(group_hot[None] * group_both[:2, None, :], axis=2)
        rate = RATE_BLOCK * jnp.sqrt(own_both[0]) / (jnp.sqrt(own_both[1]) + 1e-06)
        master_out, master_copy = new_weights(rate, master, update)
        vec_first_out = BETA_ONE * vec_first + (1.0 - BETA_ONE) * vector_grads
        vec_second_out = BETA_TWO * vec_second + (1.0 - BETA_TWO) * vector_grads * vector_grads
        vec_update = (vec_first_out / (1.0 - BETA_ONE**STEP)) / (jnp.sqrt(vec_second_out / (1.0 - BETA_TWO**STEP)) + ADAM_EPS)
        return (
            output.reshape(1, slot_count, width),
            input_grad.reshape(1, slot_count, width),
            weight_grads,
            first_out,
            second_out,
            master_out,
            master_copy,
            vector_grads,
            vec_first_out,
            vec_second_out,
            vec_params - RATE_VECTOR * vec_update,
        )

    return body


def solution(mesh):
    tuned = (mesh.shape["dp"], mesh.shape["tile"]) == (8, 4)
    rows, blocks = P("dp", "tile", None), P("dp", None, None)
    return jax.shard_map(
        make_body(tuned),
        mesh=mesh,
        in_specs=(rows, rows, P("dp", "tile"), blocks, P(), P("dp"), blocks, blocks, blocks, blocks, P(), P(), P()),
        out_specs=(rows, rows, blocks, blocks, blocks, blocks, blocks, P(), P(), P(), P()),
        check_vma=False,
    )
```
